32 devices in a mesh: batch: 4 (over x, core), head: 8 (over z, y).
Axes of the slice: x: 2, y: 2, z: 4, core: 2. Of those that a mesh axis runs over, the one named last changes fastest.
Arguments:
- tokens: bfloat16 [5120, 2048], P('batch'), may hold values from -6 to 6
- segment_ids: int32 [5120], P('batch'), may hold values from 0 to 6, as said below
- norm1_gain: bfloat16 [2048], P('batch'), may hold values from 0.25 to 1.75
- w_query: bfloat16 [2048, 1024], P('batch', 'head'), may hold values from -0.125 to 0.125
- w_key: bfloat16 [2048, 512], P('batch', 'head'), may hold values from -0.125 to 0.125
- w_value: bfloat16 [2048, 512], P('batch', 'head'), may hold values from -0.125 to 0.125
- w_gate: bfloat16 [2048, 1024], P('batch', 'head'), may hold values from -0.125 to 0.125
- w_out: bfloat16 [1024, 2048], P('head', 'batch'), may hold values from -4 to 4
- norm2_gain: bfloat16 [2048], P('batch'), may hold values from 0.25 to 1.75
- w_mlp_gate: bfloat16 [2048, 6144], P('batch', 'head'), may hold values from -0.125 to 0.125
- w_mlp_up: bfloat16 [2048, 6144], P('batch', 'head'), may hold values from -0.125 to 0.125
- w_down: bfloat16 [6144, 2048], P('head', 'batch'), may hold values from -0.078125 to 0.078125
- out_grad: bfloat16 [5120, 2048], P('batch'), may hold values from -6 to 6
Outputs:
- output: bfloat16 [5120, 2048], P('batch')
- d_tokens: bfloat16 [5120, 2048], P('batch')
- d_norm1_gain: float32 [2048], P('batch')
- d_w_query: float32 [2048, 1024], P('batch', 'head')
- d_w_key: float32 [2048, 512], P('batch', 'head')
- d_w_value: float32 [2048, 512], P('batch', 'head')
- d_w_gate: float32 [2048, 1024], P('batch', 'head')
- d_w_out: float32 [1024, 2048], P('head', 'batch')
- d_norm2_gain: float32 [2048], P('batch')
- d_w_mlp_gate: float32 [2048, 6144], P('batch', 'head')
- d_w_mlp_up: float32 [2048, 6144], P('batch', 'head')
- d_w_down: float32 [6144, 2048], P('head', 'batch')
The draws below stay inside these ranges and needn't reach their ends.
Inputs may be any that keep to these rules, and one draw needn't show every extreme that they name: `segment_ids`: segment ids never fall along the packed batch and every id from 0 to 6 occurs.
All inputs are finite; a program needn't handle non-finite values.
Results may differ from the reference program's by a relative error of at most 0.02.
Values may be sent and summed in bfloat16 or wider, within the bound.
A program may use at most 256 MiB of HBM per device.

```python
import math
import jax
import jax.numpy as jnp
from jax import lax

D = 2048
HD = 128
FF = 6144
TOK_DEV = 1280
HEADS = 8
KV_HEADS = 4
TOTAL_TOK = 5120


def draw_segment_ids(key, part):
    key_list = jax.random.split(key, 6)
    low_edge = TOK_DEV // 4
    high_edge = TOK_DEV // 2 + 1
    head_len = jax.random.randint(key_list[0], (), low_edge, high_edge)
    tail_len = jax.random.randint(key_list[1], (), low_edge, high_edge)
    first_cut = jax.random.randint(key_list[2], (), 1, head_len // 3 + 1)
    second_cut = first_cut + jax.random.randint(key_list[3], (), 1, head_len // 3 + 1)
    tail_start = TOTAL_TOK - tail_len
    third_cut = tail_start + jax.random.randint(key_list[4], (), 1, tail_len // 3 + 1)
    fourth_cut = third_cut + jax.random.randint(key_list[5], (), 1, tail_len // 3 + 1)
    bounds = jnp.stack([first_cut, second_cut, head_len, tail_start, third_cut, fourth_cut]).astype(jnp.int32)
    positions = jnp.arange(TOTAL_TOK, dtype=jnp.int32)
    return jnp.sum((positions[:, None] >= bounds[None, :]).astype(jnp.int32), axis=1).astype(jnp.int32)


def level_of(rng, dims, shards, smallest, top_value):
    def one(axis_at, parts):
        draws = jax.random.uniform(jax.random.fold_in(jax.random.fold_in(rng, 6), axis_at), (parts,), jnp.float32, smallest / len(shards), top_value / len(shards))
        return jnp.repeat(jnp.exp(draws), dims[axis_at] // parts).reshape((-1,) + (1,) * (len(dims) - axis_at - 1))

    factor_of = one(*shards[0])
    for cut in shards[1:]:
        factor_of = factor_of * one(*cut)
    return factor_of


def normal_values(own_key, extent, width, limit, cuts=(), kind=jnp.bfloat16):
    factor_of = level_of(own_key, extent, cuts, -0.22, 0.18) if cuts else 1.0
    array = jax.random.normal(own_key, extent, jnp.float32) * width * factor_of
    return jnp.minimum(jnp.maximum(array, -limit), limit).astype(kind)


def setup_inputs(seed: int = 0) -> dict:
    arg_keys = jax.random.split(jax.random.key(seed), 14)
    tokens = normal_values(arg_keys[0], (TOTAL_TOK, D), 1.0, 6.0, ((0, 4),))
    segment_ids = draw_segment_ids(jax.random.fold_in(arg_keys[13], 71), 0)
    norm1_gain = jnp.clip(1.0 + 0.15 * jax.random.normal(arg_keys[2], (D,), jnp.float32), 0.25, 1.75).astype(jnp.bfloat16)
    w_query = normal_values(arg_keys[3], (D, HEADS * HD), D ** -0.5, 0.125, ((0, 4), (1, 8)))
    w_key = normal_values(arg_keys[4], (D, KV_HEADS * HD), D ** -0.5, 0.125, ((0, 4), (1, 8)))
    w_value = normal_values(arg_keys[5], (D, KV_HEADS * HD), D ** -0.5, 0.125, ((0, 4), (1, 8)))
    w_gate = normal_values(arg_keys[6], (D, HEADS * HD), D ** -0.5, 0.125, ((0, 4), (1, 8)))
    w_out = normal_values(arg_keys[7], (HEADS * HD, D), 2 ** -0.5, 4.0, ((0, 8), (1, 4)))
    norm2_gain = jnp.clip(1.0 + 0.15 * jax.random.normal(arg_keys[8], (D,), jnp.float32), 0.25, 1.75).astype(jnp.bfloat16)
    w_mlp_gate = normal_values(arg_keys[9], (D, FF), D ** -0.5, 0.125, ((0, 4), (1, 8)))
    w_mlp_up = normal_values(arg_keys[10], (D, FF), D ** -0.5, 0.125, ((0, 4), (1, 8)))
    w_down = normal_values(arg_keys[11], (FF, D), FF ** -0.5, 0.078125, ((0, 8), (1, 4)))
    out_grad = normal_values(arg_keys[12], (TOTAL_TOK, D), 1.0, 6.0, ((0, 4),))
    return {"tokens": tokens, "segment_ids": segment_ids, "norm1_gain": norm1_gain, "w_query": w_query, "w_key": w_key, "w_value": w_value, "w_gate": w_gate, "w_out": w_out, "norm2_gain": norm2_gain, "w_mlp_gate": w_mlp_gate, "w_mlp_up": w_mlp_up, "w_down": w_down, "out_grad": out_grad}


EPSILON = 1e-06
MASKED = -1e+30

@jax.custom_vjp
def low(v):
    return lax.optimization_barrier(v.astype(jnp.bfloat16)).astype(jnp.float32)

@jax.custom_vjp
def low_back(v):
    return v

def low_keep(v):
    return (low(v), None)

def low_pass(kept, grad):
    return (grad,)

def back_keep(v):
    return (v, None)

def back_low(kept, grad):
    return (low(grad),)
low.defvjp(low_keep, low_pass)
low_back.defvjp(back_keep, back_low)

def both_ways(value):
    return low_back(low(value))

def matmul(left, right):
    return jnp.dot(left, right, precision=lax.Precision.HIGHEST)

def rms_scale(values):
    return lax.rsqrt(lax.optimization_barrier(jnp.mean(values * values, axis=-1, keepdims=True)) + EPSILON)

def attend(queries, keys, values, segment_ids):
    total_rows = queries.shape[0]
    query_heads = queries.reshape(total_rows, HEADS, HD)
    key_heads = jnp.repeat(keys.reshape(total_rows, KV_HEADS, HD), HEADS // KV_HEADS, axis=1)
    value_heads = jnp.repeat(values.reshape(total_rows, KV_HEADS, HD), HEADS // KV_HEADS, axis=1)
    positions = jnp.arange(total_rows, dtype=jnp.int32)
    block_width = math.gcd(total_rows, 256)
    block_count = total_rows // block_width
    scale_factor = 1.0 / math.sqrt(HD)

    @jax.checkpoint
    def one_block(pieces):
        query_block, query_pos, query_seg = pieces
        raw = low_back(jnp.einsum('ihd,jhd->hij', query_block, key_heads, precision=lax.Precision.HIGHEST))
        allowed = (query_seg[:, None] == segment_ids[None, :]) & (positions[None, :] <= query_pos[:, None])
        scores = jnp.where(allowed[None], raw * scale_factor, MASKED)
        weights = jax.nn.softmax(scores, axis=-1)
        return jnp.einsum('hij,jhd->ihd', low(weights), value_heads, precision=lax.Precision.HIGHEST)
    result = lax.map(one_block, (query_heads.reshape(block_count, block_width, HEADS, HD), positions.reshape(block_count, block_width), segment_ids.reshape(block_count, block_width)))
    return result.reshape(total_rows, HEADS * HD)

def layer(tokens_f, gain_one, w_query, w_key, w_value, w_gate, w_out, gain_two, w_mlp_gate, w_mlp_up, w_down, segment_ids):
    normed_one = low(tokens_f * rms_scale(tokens_f) * gain_one)
    queries = both_ways(matmul(normed_one, w_query))
    keys = both_ways(matmul(normed_one, w_key))
    values = both_ways(matmul(normed_one, w_value))
    gate_logit = low_back(matmul(normed_one, w_gate))
    attended = low_back(attend(queries, keys, values, segment_ids))
    mixed = low(attended * jax.nn.sigmoid(gate_logit))
    resid = tokens_f + low_back(matmul(mixed, w_out))
    normed_two = low(resid * rms_scale(resid) * gain_two)
    gate_pre = low_back(matmul(normed_two, w_mlp_gate))
    up_pre = low_back(matmul(normed_two, w_mlp_up))
    hidden = low(jax.nn.silu(gate_pre) * up_pre)
    return resid + low_back(matmul(hidden, w_down))

def reference(tokens, segment_ids, norm1_gain, w_query, w_key, w_value, w_gate, w_out, norm2_gain, w_mlp_gate, w_mlp_up, w_down, out_grad):
    floats = [member.astype(jnp.float32) for member in (tokens, norm1_gain, w_query, w_key, w_value, w_gate, w_out, norm2_gain, w_mlp_gate, w_mlp_up, w_down)]

    def forward(*arrays):
        return layer(*arrays, segment_ids)
    output, pullback = jax.vjp(forward, *floats)
    grads = pullback(out_grad.astype(jnp.float32))
    return (output.astype(jnp.bfloat16), grads[0].astype(jnp.bfloat16), grads[1], grads[2], grads[3], grads[4], grads[5], grads[6], grads[7], grads[8], grads[9], grads[10])
```

```python
import math

import jax
import jax.numpy as jnp
from jax import lax
from jax.sharding import PartitionSpec as P

EPSILON = 1e-06
MASKED = -1e30
BF = jnp.bfloat16
F32 = jnp.float32


def from_partner(block, axis):
    count = lax.axis_size(axis)
    route = [(at, at ^ 1) for at in range(count)]
    return lax.ppermute(block, axis, route)


def matmul(left, right):
    return jnp.dot(left, right, preferred_element_type=F32)


def rows_inner(left, right):
    return lax.dot_general(left, right, (((0,), (0,)), ((), ())), preferred_element_type=F32)


def cols_inner(left, right):
    return lax.dot_general(left, right, (((1,), (1,)), ((), ())), preferred_element_type=F32)


def rms_scale(values):
    return lax.rsqrt(jnp.mean(values * values, axis=1, keepdims=True) + EPSILON)


def keep_same(state):
    return state


def order_halves(own, mate, first):
    return jnp.where(first, jnp.concatenate([own, mate], 1), jnp.concatenate([mate, own], 1))


def per_device(
    tokens,
    segment_ids,
    norm1_gain,
    w_query,
    w_key,
    w_value,
    w_gate,
    w_out,
    norm2_gain,
    w_mlp_gate,
    w_mlp_up,
    w_down,
    out_grad,
):
    heads = lax.axis_size("head")
    batches = lax.axis_size("batch")
    row_count, width = tokens.shape
    head_size = w_query.shape[1]
    half = w_key.shape[1]
    chunk = row_count // heads
    me = lax.axis_index("head")
    first = me % 2 == 0
    scale_factor = 1.0 / math.sqrt(head_size)

    kv_shard = jnp.concatenate([w_key, w_value], axis=1)
    kv_mate = from_partner(kv_shard, "head")
    w_in = jnp.concatenate(
        [
            w_query,
            order_halves(w_key, kv_mate[:, :half], first),
            order_halves(w_value, kv_mate[:, half:], first),
            w_gate,
        ],
        axis=1,
    )
    w_in = lax.all_gather(w_in, "batch", axis=0, tiled=True)
    gains = lax.all_gather(jnp.stack([norm1_gain, norm2_gain]), "batch", axis=1, tiled=True)
    gain_one = gains[0].astype(F32)
    gain_two = gains[1].astype(F32)
    out_own = lax.all_gather(w_out, "batch", axis=1, tiled=True)
    out_full = lax.all_gather(out_own, "head", axis=0, tiled=True)
    mgate_full = lax.all_gather(w_mlp_gate, "batch", axis=0, tiled=True)
    mup_full = lax.all_gather(w_mlp_up, "batch", axis=0, tiled=True)
    down_full = lax.all_gather(w_down, "batch", axis=1, tiled=True)

    positions = lax.axis_index("batch") * row_count + jnp.arange(row_count, dtype=jnp.int32)
    inputs = tokens.astype(F32)
    recip_one = rms_scale(inputs)
    normed_one = (inputs * recip_one * gain_one).astype(BF)
    projected = matmul(normed_one, w_in)
    queries = projected[:, :head_size].astype(BF)
    kv_local = projected[:, head_size : 3 * head_size].astype(BF)
    gate_vals = jax.nn.sigmoid(projected[:, 3 * head_size :])
    kv_all = lax.all_gather(kv_local, "batch", axis=0, tiled=True)
    seg_all = lax.all_gather(segment_ids, "batch", axis=0, tiled=True)
    block_rows = row_count
    block_total = batches

    def block_parts(block_index):
        first_row = block_index * block_rows
        key_block = kv_all[first_row : first_row + block_rows, :head_size]
        value_block = kv_all[first_row : first_row + block_rows, head_size:]
        seg_block = seg_all[first_row : first_row + block_rows]
        key_pos = first_row + jnp.arange(block_rows, dtype=jnp.int32)
        allowed = (segment_ids[:, None] == seg_block[None, :]) & (
            key_pos[None, :] <= positions[:, None]
        )
        scores = cols_inner(queries, key_block) * scale_factor
        return (scores, allowed, key_block, value_block)

    def is_live(block_index):
        first_row = block_index * block_rows
        return (first_row <= positions[-1]) & (
            seg_all[first_row + block_rows - 1] >= segment_ids[0]
        )

    run_max = jnp.full((row_count,), MASKED, F32)
    run_sum = jnp.zeros((row_count,), F32)
    for block_index in range(block_total):

        def grow(state, block_index=block_index):
            old_max, old_sum = state
            scores, allowed, key_block, value_block = block_parts(block_index)
            new_max = jnp.maximum(old_max, jnp.max(jnp.where(allowed, scores, MASKED), axis=1))
            weights = jnp.where(allowed, jnp.exp(scores - new_max[:, None]), 0.0)
            return (new_max, old_sum * jnp.exp(old_max - new_max) + jnp.sum(weights, axis=1))

        run_max, run_sum = lax.cond(is_live(block_index), grow, keep_same, (run_max, run_sum))
    log_total = run_max + jnp.log(run_sum)

    def probs_of(block_index):
        scores, allowed, key_block, value_block = block_parts(block_index)
        return (
            jnp.where(allowed, jnp.exp(scores - log_total[:, None]), 0.0),
            key_block,
            value_block,
        )

    attended = jnp.zeros((row_count, head_size), F32)
    for block_index in range(block_total):

        def accumulate(running, block_index=block_index):
            probs, key_block, value_block = probs_of(block_index)
            return running + matmul(probs.astype(BF), value_block)

        attended = lax.cond(is_live(block_index), accumulate, keep_same, attended)

    mixed = (attended * gate_vals).astype(BF)
    mixed_all = lax.all_gather(mixed, "head", axis=1, tiled=True)
    resid = inputs + matmul(mixed_all, out_full)
    recip_two = rms_scale(resid)
    normed_two = (resid * recip_two * gain_two).astype(BF)
    resid_own = lax.dynamic_slice_in_dim(resid, me * chunk, chunk, 0)
    recip_own = lax.dynamic_slice_in_dim(recip_two, me * chunk, chunk, 0)
    mixed_own = lax.dynamic_slice_in_dim(mixed_all, me * chunk, chunk, 0)
    dy_own = lax.dynamic_slice_in_dim(out_grad, me * chunk, chunk, 0).astype(F32)

    gate_pre = matmul(normed_two, mgate_full)
    up_pre = matmul(normed_two, mup_full)
    sig_gate = jax.nn.sigmoid(gate_pre)
    silu_gate = gate_pre * sig_gate
    hidden = (silu_gate * up_pre).astype(BF)
    d_hidden = cols_inner(out_grad, down_full)
    d_gate_pre = (d_hidden * up_pre * sig_gate * (1.0 + gate_pre * (1.0 - sig_gate))).astype(BF)
    d_up_pre = (d_hidden * silu_gate).astype(BF)
    dn2_part = cols_inner(d_gate_pre, mgate_full) + cols_inner(d_up_pre, mup_full)
    dn2 = lax.psum_scatter(dn2_part.astype(BF), "head", scatter_dimension=0, tiled=True).astype(F32)
    mlp_part = matmul(hidden, down_full).astype(BF)
    mlp_own = lax.psum_scatter(mlp_part, "head", scatter_dimension=0, tiled=True).astype(F32)
    output = lax.all_gather((resid_own + mlp_own).astype(BF), "head", axis=0, tiled=True)

    d_gain_two = jnp.sum(dn2 * resid_own * recip_own, axis=0)
    weighted_two = gain_two * dn2
    d_resid = (
        dy_own
        + recip_own * weighted_two
        - resid_own * recip_own**3 * jnp.mean(weighted_two * resid_own, axis=1, keepdims=True)
    )
    d_resid_low = d_resid.astype(BF)
    d_mixed_all = cols_inner(d_resid_low, out_full).astype(BF)
    d_mixed = lax.all_to_all(d_mixed_all, "head", split_axis=1, concat_axis=0, tiled=True).astype(F32)
    d_out_part = rows_inner(mixed_own, d_resid_low).astype(BF)
    d_out_head = lax.psum_scatter(d_out_part, "head", scatter_dimension=0, tiled=True)

    d_attended = (d_mixed * gate_vals).astype(BF)
    d_gate_logit = (d_mixed * attended * gate_vals * (1.0 - gate_vals)).astype(BF)
    delta = jnp.zeros((row_count,), F32)
    for block_index in range(block_total):

        def delta_add(running, block_index=block_index):
            probs, key_block, value_block = probs_of(block_index)
            return running + jnp.sum(probs * cols_inner(d_attended, value_block), axis=1)

        delta = lax.cond(is_live(block_index), delta_add, keep_same, delta)
    d_queries = jnp.zeros((row_count, head_size), F32)
    grad_pieces = []
    for block_index in range(block_total):

        def block_grads(running, block_index=block_index):
            probs, key_block, value_block = probs_of(block_index)
            d_probs = cols_inner(d_attended, value_block)
            d_scores = (probs * (d_probs - delta[:, None]) * scale_factor).astype(BF)
            d_key_block = rows_inner(d_scores, queries)
            d_value_block = rows_inner(probs.astype(BF), d_attended)
            return (
                running + matmul(d_scores, key_block),
                jnp.concatenate([d_key_block, d_value_block], axis=1).astype(BF),
            )

        def block_empty(running):
            return (running, jnp.zeros((block_rows, 2 * head_size), BF))

        d_queries, grad_piece = lax.cond(is_live(block_index), block_grads, block_empty, d_queries)
        grad_pieces.append(grad_piece)
    d_kv_all = jnp.concatenate(grad_pieces, axis=0)
    d_kv_own = lax.psum_scatter(d_kv_all, "batch", scatter_dimension=0, tiled=True)
    d_kv_mate = from_partner(d_kv_own, "head")
    d_kv = (d_kv_own.astype(F32) + d_kv_mate.astype(F32)).astype(BF)
    d_cat = jnp.concatenate(
        [
            d_queries.astype(BF),
            jnp.where(first, d_kv[:, :half], d_kv[:, half:head_size]),
            jnp.where(first, d_kv[:, head_size : head_size + half], d_kv[:, head_size + half :]),
            d_gate_logit,
        ],
        axis=1,
    )
    w_key_own = jnp.where(
        first, w_in[:, head_size : head_size + half], w_in[:, head_size + half : 2 * head_size]
    )
    w_value_own = jnp.where(
        first, w_in[:, 2 * head_size : 2 * head_size + half], w_in[:, 2 * head_size + half : 3 * head_size]
    )
    w_cat = jnp.concatenate(
        [w_in[:, :head_size], w_key_own, w_value_own, w_in[:, 3 * head_size :]], axis=1
    )
    dn1_part = cols_inner(d_cat, w_cat).astype(BF)
    dn1 = lax.psum_scatter(dn1_part, "head", scatter_dimension=0, tiled=True).astype(F32)
    inputs_own = lax.dynamic_slice_in_dim(inputs, me * chunk, chunk, 0)
    recip_in = lax.dynamic_slice_in_dim(recip_one, me * chunk, chunk, 0)
    d_gain_one = jnp.sum(dn1 * inputs_own * recip_in, axis=0)
    weighted_one = gain_one * dn1
    d_tokens = (
        d_resid
        + recip_in * weighted_one
        - inputs_own * recip_in**3 * jnp.mean(weighted_one * inputs_own, axis=1, keepdims=True)
    ).astype(BF)
    d_tokens = lax.all_gather(d_tokens, "head", axis=0, tiled=True)

    d_mlp = jnp.concatenate(
        [rows_inner(normed_two, d_gate_pre).astype(BF), rows_inner(normed_two, d_up_pre).astype(BF)], 1
    )
    d_mlp = lax.psum_scatter(d_mlp, "batch", scatter_dimension=0, tiled=True).astype(F32)
    d_down = rows_inner(hidden, out_grad).astype(BF)
    d_down = lax.psum_scatter(d_down, "batch", scatter_dimension=1, tiled=True).astype(F32)
    d_in = rows_inner(normed_one, d_cat).astype(BF)
    d_in = lax.psum_scatter(d_in, "batch", scatter_dimension=0, tiled=True).astype(F32)
    d_out = lax.psum_scatter(d_out_head, "batch", scatter_dimension=1, tiled=True).astype(F32)
    d_gains = lax.psum(jnp.stack([d_gain_one, d_gain_two]), ("batch", "head"))
    d_gains = lax.dynamic_slice_in_dim(
        d_gains, lax.axis_index("batch") * norm1_gain.shape[0], norm1_gain.shape[0], 1
    )
    hidden_own = w_mlp_gate.shape[1]
    return (
        output,
        d_tokens,
        d_gains[0],
        d_in[:, :head_size],
        d_in[:, head_size : head_size + half],
        d_in[:, head_size + half : 2 * head_size],
        d_in[:, 2 * head_size :],
        d_out,
        d_gains[1],
        d_mlp[:, :hidden_own],
        d_mlp[:, hidden_own:],
        d_down,
    )


def solution(mesh):
    return jax.shard_map(
        per_device,
        mesh=mesh,
        in_specs=(
            P("batch", None),
            P("batch"),
            P("batch"),
            P("batch", "head"),
            P("batch", "head"),
            P("batch", "head"),
            P("batch", "head"),
            P("head", "batch"),
            P("batch"),
            P("batch", "head"),
            P("batch", "head"),
            P("head", "batch"),
            P("batch", None),
        ),
        out_specs=(
            P("batch", None),
            P("batch", None),
            P("batch"),
            P("batch", "head"),
            P("batch", "head"),
            P("batch", "head"),
            P("batch", "head"),
            P("head", "batch"),
            P("batch"),
            P("batch", "head"),
            P("batch", "head"),
            P("head", "batch"),
        ),
        check_vma=False,
    )
```

```python
import functools
import math

import jax
import jax.numpy as jnp
from jax import lax
from jax.experimental import pallas as pl
from jax.experimental.pallas import tpu as pltpu
from jax.sharding import PartitionSpec as P

EPSILON = 1e-06
MASKED = -1e30
BF = jnp.bfloat16
F32 = jnp.float32


MESH = pl.DeviceIdType.MESH
VMEM_LIMIT = 60 << 20


def ring_place(head, count):
    high, low = head // 2, head % 2
    return (1 - low) * high + low * (count - 1 - high)


def ring_head(place, count):
    low = place // (count // 2)
    high = (1 - low) * place + low * (count - 1 - place)
    return 2 * high + low


def ring_setup(count):
    batch = lax.axis_index("batch")
    place = ring_place(lax.axis_index("head"), count)
    right = (batch, ring_head(lax.rem(place + 1, count), count))
    left = (batch, ring_head(lax.rem(place + count - 1, count), count))
    return place, right, left


def greet(devices):
    barrier = pltpu.get_barrier_semaphore()
    for device in devices:
        pl.semaphore_signal(barrier, inc=1, device_id=device, device_id_type=MESH)
    pl.semaphore_wait(barrier, len(devices))


def send(source, target, sems, slot, device):
    copy = pltpu.make_async_remote_copy(
        src_ref=source,
        dst_ref=target,
        send_sem=sems[0].at[slot],
        recv_sem=sems[1].at[slot],
        device_id=device,
        device_id_type=MESH,
    )
    copy.start()
    return copy


def sum_kernel(count, part_ref, own_ref, from_left, from_right, send_sem, recv_sem):
    steps = count // 2
    rows = part_ref.shape[0] // count
    width = part_ref.shape[1]
    side = width // 2
    place, right, left = ring_setup(count)
    greet((right, left))
    sems = (send_sem, recv_sem)

    def part(owner):
        return part_ref.at[pl.ds(pl.multiple_of(lax.rem(owner + count, count) * rows, rows), rows)]

    far = part(place + steps)
    copies = [
        send(far.at[:, pl.ds(0, side)], from_left.at[0, :, pl.ds(0, side)], sems, 0, right),
        send(far.at[:, pl.ds(side, side)], from_right.at[0, :, pl.ds(side, side)], sems, steps, left),
    ]
    for step in range(1, steps):
        for flow, held, owner, device in (
            (0, from_left, place + steps - step, right),
            (1, from_right, place - steps + step, left),
        ):
            copies[2 * step - 2 + flow].wait_recv()
            mine = part(owner)
            if step == 1:
                have = pl.ds(flow * side, side)
                lack = pl.ds((1 - flow) * side, side)
                held[0, :, have] = (held[0, :, have].astype(F32) + mine[:, have].astype(F32)).astype(BF)
                held[0, :, lack] = mine[:, lack]
            else:
                held[step - 1] = (held[step - 1].astype(F32) + mine[...].astype(F32)).astype(BF)
            copies.append(
                send(held.at[step - 1], held.at[step], sems, flow * steps + step, device)
            )
    copies[-2].wait_recv()
    copies[-1].wait_recv()
    own_ref[...] = (
        part(place)[...].astype(F32)
        + from_left[steps - 1].astype(F32)
        + from_right[steps - 1].astype(F32)
    )
    for copy in copies:
        copy.wait_send()


def sum_own(part, collective_id):
    count = lax.axis_size("head")
    rows, width = part.shape[0] // count, part.shape[1]
    vmem = pl.BlockSpec(memory_space=pltpu.VMEM)
    return pl.pallas_call(
        functools.partial(sum_kernel, count),
        out_shape=jax.ShapeDtypeStruct((rows, width), F32),
        in_specs=[vmem],
        out_specs=vmem,
        scratch_shapes=[
            pltpu.VMEM((count // 2, rows, width), BF),
            pltpu.VMEM((count // 2, rows, width), BF),
            pltpu.SemaphoreType.DMA((count,)),
            pltpu.SemaphoreType.DMA((count,)),
        ],
        compiler_params=pltpu.CompilerParams(
            collective_id=collective_id, has_side_effects=True, vmem_limit_bytes=VMEM_LIMIT
        ),
        name=f"sum_own_{collective_id}",
    )(part)


def half_of(extent, flow):
    if extent[1] % 256:
        return (pl.ds(flow * (extent[0] // 2), extent[0] // 2), slice(None))
    return (slice(None), pl.ds(flow * (extent[1] // 2), extent[1] // 2))


def spread_kernel(count, arrays, *refs):
    steps = count // 2
    own_refs, all_refs = refs[:arrays], refs[arrays : 2 * arrays]
    send_sem, recv_sem, local_sem = refs[2 * arrays :]
    place, right, left = ring_setup(count)
    greet((right, left))
    sems = (send_sem, recv_sem)
    local = []
    for index in range(arrays):
        copy = pltpu.make_async_copy(own_refs[index], all_refs[index].at[place], local_sem.at[index])
        copy.start()
        local.append(copy)
    waiting = []
    copies = [None] * (2 * arrays)
    for step in range(steps):
        for index in range(arrays):
            extent = own_refs[index].shape
            for flow, chunk, device in (
                (0, place - step, right),
                (1, place + step, left),
            ):
                at = 2 * index + flow
                if step:
                    copies[at].wait_recv()
                chunk = lax.rem(chunk + count, count)
                target = all_refs[index].at[chunk]
                source = target if step else own_refs[index]
                if step == steps - 1:
                    part = half_of(extent, flow)
                    source = source.at[part]
                    target = target.at[part]
                copies[at] = send(source, target, sems, at * steps + step, device)
                waiting.append(copies[at])
    for copy in copies:
        copy.wait_recv()
    for copy in waiting:
        copy.wait_send()
    for copy in local:
        copy.wait()


def spread(arrays, collective_id, space=pl.ANY):
    count = lax.axis_size("head")
    slots = len(arrays) * count
    return pl.pallas_call(
        functools.partial(spread_kernel, count, len(arrays)),
        out_shape=[jax.ShapeDtypeStruct((count, *a.shape), a.dtype) for a in arrays],
        in_specs=[pl.BlockSpec(memory_space=space)] * len(arrays),
        out_specs=[pl.BlockSpec(memory_space=space)] * len(arrays),
        scratch_shapes=[
            pltpu.SemaphoreType.DMA((slots,)),
            pltpu.SemaphoreType.DMA((slots,)),
            pltpu.SemaphoreType.DMA((len(arrays),)),
        ],
        compiler_params=pltpu.CompilerParams(
            collective_id=collective_id, has_side_effects=True, vmem_limit_bytes=VMEM_LIMIT
        ),
        name=f"spread_{collective_id}",
    )(*arrays)


def from_partner(block, axis):
    count = lax.axis_size(axis)
    route = [(at, at ^ 1) for at in range(count)]
    return lax.ppermute(block, axis, route)


def matmul(left, right):
    return jnp.dot(left, right, preferred_element_type=F32)


def rows_inner(left, right):
    return lax.dot_general(left, right, (((0,), (0,)), ((), ())), preferred_element_type=F32)


def cols_inner(left, right):
    return lax.dot_general(left, right, (((1,), (1,)), ((), ())), preferred_element_type=F32)


def rms_scale(values):
    return lax.rsqrt(jnp.mean(values * values, axis=1, keepdims=True) + EPSILON)


def keep_same(state):
    return state


def order_halves(own, mate, first):
    return jnp.where(first, jnp.concatenate([own, mate], 1), jnp.concatenate([mate, own], 1))


def per_device(
    tokens,
    segment_ids,
    norm1_gain,
    w_query,
    w_key,
    w_value,
    w_gate,
    w_out,
    norm2_gain,
    w_mlp_gate,
    w_mlp_up,
    w_down,
    out_grad,
):
    heads = lax.axis_size("head")
    batches = lax.axis_size("batch")
    row_count, width = tokens.shape
    head_size = w_query.shape[1]
    half = w_key.shape[1]
    chunk = row_count // heads
    first = lax.axis_index("head") % 2 == 0
    me = ring_place(lax.axis_index("head"), heads)
    scale_factor = 1.0 / math.sqrt(head_size)

    kv_shard = jnp.concatenate([w_key, w_value], axis=1)
    kv_mate = from_partner(kv_shard, "head")
    w_in = jnp.concatenate(
        [
            w_query,
            order_halves(w_key, kv_mate[:, :half], first),
            order_halves(w_value, kv_mate[:, half:], first),
            w_gate,
        ],
        axis=1,
    )
    w_in = lax.all_gather(w_in, "batch", axis=0, tiled=True)
    gains = lax.all_gather(jnp.stack([norm1_gain, norm2_gain]), "batch", axis=1, tiled=True)
    gain_one = gains[0].astype(F32)
    gain_two = gains[1].astype(F32)
    (out_rows,) = spread([w_out], 1)
    out_full = lax.all_gather(out_rows.reshape(heads * head_size, -1), "batch", axis=1, tiled=True)
    mgate_full = lax.all_gather(w_mlp_gate, "batch", axis=0, tiled=True)
    mup_full = lax.all_gather(w_mlp_up, "batch", axis=0, tiled=True)
    down_full = lax.all_gather(w_down, "batch", axis=1, tiled=True)

    positions = lax.axis_index("batch") * row_count + jnp.arange(row_count, dtype=jnp.int32)
    inputs = tokens.astype(F32)
    recip_one = rms_scale(inputs)
    normed_one = (inputs * recip_one * gain_one).astype(BF)
    projected = matmul(normed_one, w_in)
    queries = projected[:, :head_size].astype(BF)
    kv_local = projected[:, head_size : 3 * head_size].astype(BF)
    gate_vals = jax.nn.sigmoid(projected[:, 3 * head_size :])
    kv_all = lax.all_gather(kv_local, "batch", axis=0, tiled=True)
    seg_all = lax.all_gather(segment_ids, "batch", axis=0, tiled=True)
    block_rows = row_count
    block_total = batches

    def block_parts(block_index):
        first_row = block_index * block_rows
        key_block = kv_all[first_row : first_row + block_rows, :head_size]
        value_block = kv_all[first_row : first_row + block_rows, head_size:]
        seg_block = seg_all[first_row : first_row + block_rows]
        key_pos = first_row + jnp.arange(block_rows, dtype=jnp.int32)
        allowed = (segment_ids[:, None] == seg_block[None, :]) & (
            key_pos[None, :] <= positions[:, None]
        )
        scores = cols_inner(queries, key_block) * scale_factor
        return (scores, allowed, key_block, value_block)

    def is_live(block_index):
        first_row = block_index * block_rows
        return (first_row <= positions[-1]) & (
            seg_all[first_row + block_rows - 1] >= segment_ids[0]
        )

    run_max = jnp.full((row_count,), MASKED, F32)
    run_sum = jnp.zeros((row_count,), F32)
    for block_index in range(block_total):

        def grow(state, block_index=block_index):
            old_max, old_sum = state
            scores, allowed, key_block, value_block = block_parts(block_index)
            new_max = jnp.maximum(old_max, jnp.max(jnp.where(allowed, scores, MASKED), axis=1))
            weights = jnp.where(allowed, jnp.exp(scores - new_max[:, None]), 0.0)
            return (new_max, old_sum * jnp.exp(old_max - new_max) + jnp.sum(weights, axis=1))

        run_max, run_sum = lax.cond(is_live(block_index), grow, keep_same, (run_max, run_sum))
    log_total = run_max + jnp.log(run_sum)

    def probs_of(block_index):
        scores, allowed, key_block, value_block = block_parts(block_index)
        return (
            jnp.where(allowed, jnp.exp(scores - log_total[:, None]), 0.0),
            key_block,
            value_block,
        )

    attended = jnp.zeros((row_count, head_size), F32)
    for block_index in range(block_total):

        def accumulate(running, block_index=block_index):
            probs, key_block, value_block = probs_of(block_index)
            return running + matmul(probs.astype(BF), value_block)

        attended = lax.cond(is_live(block_index), accumulate, keep_same, attended)

    mixed = (attended * gate_vals).astype(BF)
    (mixed_all,) = spread([mixed], 2)
    mixed_all = mixed_all.transpose(1, 0, 2).reshape(row_count, -1)
    resid = inputs + matmul(mixed_all, out_full)
    recip_two = rms_scale(resid)
    normed_two = (resid * recip_two * gain_two).astype(BF)
    resid_own = lax.dynamic_slice_in_dim(resid, me * chunk, chunk, 0)
    recip_own = lax.dynamic_slice_in_dim(recip_two, me * chunk, chunk, 0)
    mixed_own = lax.dynamic_slice_in_dim(mixed_all, me * chunk, chunk, 0)
    dy_own = lax.dynamic_slice_in_dim(out_grad, me * chunk, chunk, 0).astype(F32)

    gate_pre = matmul(normed_two, mgate_full)
    up_pre = matmul(normed_two, mup_full)
    sig_gate = jax.nn.sigmoid(gate_pre)
    silu_gate = gate_pre * sig_gate
    hidden = (silu_gate * up_pre).astype(BF)
    d_hidden = cols_inner(out_grad, down_full)
    d_gate_pre = (d_hidden * up_pre * sig_gate * (1.0 + gate_pre * (1.0 - sig_gate))).astype(BF)
    d_up_pre = (d_hidden * silu_gate).astype(BF)
    dn2_part = cols_inner(d_gate_pre, mgate_full) + cols_inner(d_up_pre, mup_full)
    dn2 = sum_own(dn2_part.astype(BF), 3)
    mlp_part = matmul(hidden, down_full).astype(BF)
    output = (resid_own + sum_own(mlp_part, 4)).astype(BF)

    d_gain_two = jnp.sum(dn2 * resid_own * recip_own, axis=0)
    weighted_two = gain_two * dn2
    d_resid = (
        dy_own
        + recip_own * weighted_two
        - resid_own * recip_own**3 * jnp.mean(weighted_two * resid_own, axis=1, keepdims=True)
    )
    d_resid_low = d_resid.astype(BF)
    d_mixed_all = cols_inner(d_resid_low, out_full).astype(BF)
    d_mixed_all = d_mixed_all.reshape(chunk, heads, head_size)
    places = [ring_place(at, heads) for at in range(heads)]
    d_mixed_all = jnp.stack([d_mixed_all[:, at] for at in places], axis=0)
    d_mixed = lax.all_to_all(d_mixed_all, "head", split_axis=0, concat_axis=0, tiled=True)
    d_mixed = jnp.concatenate([d_mixed[ring_head(at, heads)] for at in range(heads)], axis=0)
    d_mixed = d_mixed.astype(F32)
    d_out_part = rows_inner(mixed_own, d_resid_low).astype(BF)
    d_out_part = lax.psum_scatter(d_out_part, "batch", scatter_dimension=1, tiled=True)
    d_out = sum_own(d_out_part, 7)

    d_attended = (d_mixed * gate_vals).astype(BF)
    d_gate_logit = (d_mixed * attended * gate_vals * (1.0 - gate_vals)).astype(BF)
    delta = jnp.zeros((row_count,), F32)
    for block_index in range(block_total):

        def delta_add(running, block_index=block_index):
            probs, key_block, value_block = probs_of(block_index)
            return running + jnp.sum(probs * cols_inner(d_attended, value_block), axis=1)

        delta = lax.cond(is_live(block_index), delta_add, keep_same, delta)
    d_queries = jnp.zeros((row_count, head_size), F32)
    grad_pieces = []
    for block_index in range(block_total):

        def block_grads(running, block_index=block_index):
            probs, key_block, value_block = probs_of(block_index)
            d_probs = cols_inner(d_attended, value_block)
            d_scores = (probs * (d_probs - delta[:, None]) * scale_factor).astype(BF)
            d_key_block = rows_inner(d_scores, queries)
            d_value_block = rows_inner(probs.astype(BF), d_attended)
            return (
                running + matmul(d_scores, key_block),
                jnp.concatenate([d_key_block, d_value_block], axis=1).astype(BF),
            )

        def block_empty(running):
            return (running, jnp.zeros((block_rows, 2 * head_size), BF))

        d_queries, grad_piece = lax.cond(is_live(block_index), block_grads, block_empty, d_queries)
        grad_pieces.append(grad_piece)
    d_kv_all = jnp.concatenate(grad_pieces, axis=0)
    d_kv_own = lax.psum_scatter(d_kv_all, "batch", scatter_dimension=0, tiled=True)
    d_kv_mate = from_partner(d_kv_own, "head")
    d_kv = (d_kv_own.astype(F32) + d_kv_mate.astype(F32)).astype(BF)
    d_cat = jnp.concatenate(
        [
            d_queries.astype(BF),
            jnp.where(first, d_kv[:, :half], d_kv[:, half:head_size]),
            jnp.where(first, d_kv[:, head_size : head_size + half], d_kv[:, head_size + half :]),
            d_gate_logit,
        ],
        axis=1,
    )
    w_key_own = jnp.where(
        first, w_in[:, head_size : head_size + half], w_in[:, head_size + half : 2 * head_size]
    )
    w_value_own = jnp.where(
        first, w_in[:, 2 * head_size : 2 * head_size + half], w_in[:, 2 * head_size + half : 3 * head_size]
    )
    w_cat = jnp.concatenate(
        [w_in[:, :head_size], w_key_own, w_value_own, w_in[:, 3 * head_size :]], axis=1
    )
    dn1_part = cols_inner(d_cat, w_cat).astype(BF)
    dn1 = sum_own(dn1_part, 5)
    inputs_own = lax.dynamic_slice_in_dim(inputs, me * chunk, chunk, 0)
    recip_in = lax.dynamic_slice_in_dim(recip_one, me * chunk, chunk, 0)
    d_gain_one = jnp.sum(dn1 * inputs_own * recip_in, axis=0)
    weighted_one = gain_one * dn1
    d_tokens = (
        d_resid
        + recip_in * weighted_one
        - inputs_own * recip_in**3 * jnp.mean(weighted_one * inputs_own, axis=1, keepdims=True)
    ).astype(BF)
    output, d_tokens = spread([output, d_tokens], 6)
    output = output.reshape(row_count, width)
    d_tokens = d_tokens.reshape(row_count, width)

    d_mlp = jnp.concatenate(
        [rows_inner(normed_two, d_gate_pre).astype(BF), rows_inner(normed_two, d_up_pre).astype(BF)], 1
    )
    d_mlp = lax.psum_scatter(d_mlp, "batch", scatter_dimension=0, tiled=True).astype(F32)
    d_down = rows_inner(hidden, out_grad).astype(BF)
    d_down = lax.psum_scatter(d_down, "batch", scatter_dimension=1, tiled=True).astype(F32)
    d_in = rows_inner(normed_one, d_cat).astype(BF)
    d_in = lax.psum_scatter(d_in, "batch", scatter_dimension=0, tiled=True).astype(F32)
    d_gains = lax.psum(jnp.stack([d_gain_one, d_gain_two]), ("batch", "head"))
    d_gains = lax.dynamic_slice_in_dim(
        d_gains, lax.axis_index("batch") * norm1_gain.shape[0], norm1_gain.shape[0], 1
    )
    hidden_own = w_mlp_gate.shape[1]
    return (
        output,
        d_tokens,
        d_gains[0],
        d_in[:, :head_size],
        d_in[:, head_size : head_size + half],
        d_in[:, head_size + half : 2 * head_size],
        d_in[:, 2 * head_size :],
        d_out,
        d_gains[1],
        d_mlp[:, :hidden_own],
        d_mlp[:, hidden_own:],
        d_down,
    )


def solution(mesh):
    return jax.shard_map(
        per_device,
        mesh=mesh,
        in_specs=(
            P("batch", None),
            P("batch"),
            P("batch"),
            P("batch", "head"),
            P("batch", "head"),
            P("batch", "head"),
            P("batch", "head"),
            P("head", "batch"),
            P("batch"),
            P("batch", "head"),
            P("batch", "head"),
            P("head", "batch"),
            P("batch", None),
        ),
        out_specs=(
            P("batch", None),
            P("batch", None),
            P("batch"),
            P("batch", "head"),
            P("batch", "head"),
            P("batch", "head"),
            P("batch", "head"),
            P("head", "batch"),
            P("batch"),
            P("batch", "head"),
            P("batch", "head"),
            P("head", "batch"),
        ),
        check_vma=False,
    )
```

```python
import functools
import math

import jax
import jax.numpy as jnp
from jax import lax
from jax.experimental import pallas as pl
from jax.experimental.pallas import tpu as pltpu
from jax.sharding import PartitionSpec as P

EPSILON = 1e-06
MASKED = -1e30
DOCUMENTS = 7
BF = jnp.bfloat16
F32 = jnp.float32


MESH = pl.DeviceIdType.MESH
VMEM_LIMIT = 60 << 20


def ring_place(head, count):
    high, low = head // 2, head % 2
    return (1 - low) * high + low * (count - 1 - high)


def ring_head(place, count):
    low = place // (count // 2)
    high = (1 - low) * place + low * (count - 1 - place)
    return 2 * high + low


def ring_setup(count):
    batch = lax.axis_index("batch")
    place = ring_place(lax.axis_index("head"), count)
    right = (batch, ring_head(lax.rem(place + 1, count), count))
    left = (batch, ring_head(lax.rem(place + count - 1, count), count))
    return place, right, left


def greet(devices):
    barrier = pltpu.get_barrier_semaphore()
    for device in devices:
        pl.semaphore_signal(barrier, inc=1, device_id=device, device_id_type=MESH)
    pl.semaphore_wait(barrier, len(devices))


def send(source, target, sems, slot, device):
    copy = pltpu.make_async_remote_copy(
        src_ref=source,
        dst_ref=target,
        send_sem=sems[0].at[slot],
        recv_sem=sems[1].at[slot],
        device_id=device,
        device_id_type=MESH,
    )
    copy.start()
    return copy


def sum_kernel(count, part_ref, own_ref, from_left, from_right, send_sem, recv_sem):
    steps = count // 2
    rows = part_ref.shape[0] // count
    width = part_ref.shape[1]
    side = width // 2
    place, right, left = ring_setup(count)
    greet((right, left))
    sems = (send_sem, recv_sem)

    def part(owner):
        return part_ref.at[pl.ds(pl.multiple_of(lax.rem(owner + count, count) * rows, rows), rows)]

    far = part(place + steps)
    copies = [
        send(far.at[:, pl.ds(0, side)], from_left.at[0, :, pl.ds(0, side)], sems, 0, right),
        send(far.at[:, pl.ds(side, side)], from_right.at[0, :, pl.ds(side, side)], sems, steps, left),
    ]
    for step in range(1, steps):
        for flow, held, owner, device in (
            (0, from_left, place + steps - step, right),
            (1, from_right, place - steps + step, left),
        ):
            copies[2 * step - 2 + flow].wait_recv()
            mine = part(owner)
            if step == 1:
                have = pl.ds(flow * side, side)
                lack = pl.ds((1 - flow) * side, side)
                held[0, :, have] = (held[0, :, have].astype(F32) + mine[:, have].astype(F32)).astype(BF)
                held[0, :, lack] = mine[:, lack]
            else:
                held[step - 1] = (held[step - 1].astype(F32) + mine[...].astype(F32)).astype(BF)
            copies.append(
                send(held.at[step - 1], held.at[step], sems, flow * steps + step, device)
            )
    copies[-2].wait_recv()
    copies[-1].wait_recv()
    own_ref[...] = (
        part(place)[...].astype(F32)
        + from_left[steps - 1].astype(F32)
        + from_right[steps - 1].astype(F32)
    )
    for copy in copies:
        copy.wait_send()


def sum_own(part, collective_id):
    count = lax.axis_size("head")
    rows, width = part.shape[0] // count, part.shape[1]
    vmem = pl.BlockSpec(memory_space=pltpu.VMEM)
    return pl.pallas_call(
        functools.partial(sum_kernel, count),
        out_shape=jax.ShapeDtypeStruct((rows, width), F32),
        in_specs=[vmem],
        out_specs=vmem,
        scratch_shapes=[
            pltpu.VMEM((count // 2, rows, width), BF),
            pltpu.VMEM((count // 2, rows, width), BF),
            pltpu.SemaphoreType.DMA((count,)),
            pltpu.SemaphoreType.DMA((count,)),
        ],
        compiler_params=pltpu.CompilerParams(
            collective_id=collective_id, has_side_effects=True, vmem_limit_bytes=VMEM_LIMIT
        ),
        name=f"sum_own_{collective_id}",
    )(part)


def half_of(extent, flow):
    if extent[1] % 256:
        return (pl.ds(flow * (extent[0] // 2), extent[0] // 2), slice(None))
    return (slice(None), pl.ds(flow * (extent[1] // 2), extent[1] // 2))


def spread_kernel(count, arrays, *refs):
    steps = count // 2
    own_refs, all_refs = refs[:arrays], refs[arrays : 2 * arrays]
    send_sem, recv_sem, local_sem = refs[2 * arrays :]
    place, right, left = ring_setup(count)
    greet((right, left))
    sems = (send_sem, recv_sem)
    local = []
    for index in range(arrays):
        copy = pltpu.make_async_copy(own_refs[index], all_refs[index].at[place], local_sem.at[index])
        copy.start()
        local.append(copy)
    waiting = []
    copies = [None] * (2 * arrays)
    for step in range(steps):
        for index in range(arrays):
            extent = own_refs[index].shape
            for flow, chunk, device in (
                (0, place - step, right),
                (1, place + step, left),
            ):
                at = 2 * index + flow
                if step:
                    copies[at].wait_recv()
                chunk = lax.rem(chunk + count, count)
                target = all_refs[index].at[chunk]
                source = target if step else own_refs[index]
                if step == steps - 1:
                    part = half_of(extent, flow)
                    source = source.at[part]
                    target = target.at[part]
                copies[at] = send(source, target, sems, at * steps + step, device)
                waiting.append(copies[at])
    for copy in copies:
        copy.wait_recv()
    for copy in waiting:
        copy.wait_send()
    for copy in local:
        copy.wait()


def spread(arrays, collective_id, space=pl.ANY):
    count = lax.axis_size("head")
    slots = len(arrays) * count
    return pl.pallas_call(
        functools.partial(spread_kernel, count, len(arrays)),
        out_shape=[jax.ShapeDtypeStruct((count, *a.shape), a.dtype) for a in arrays],
        in_specs=[pl.BlockSpec(memory_space=space)] * len(arrays),
        out_specs=[pl.BlockSpec(memory_space=space)] * len(arrays),
        scratch_shapes=[
            pltpu.SemaphoreType.DMA((slots,)),
            pltpu.SemaphoreType.DMA((slots,)),
            pltpu.SemaphoreType.DMA((len(arrays),)),
        ],
        compiler_params=pltpu.CompilerParams(
            collective_id=collective_id, has_side_effects=True, vmem_limit_bytes=VMEM_LIMIT
        ),
        name=f"spread_{collective_id}",
    )(*arrays)


KEY_BLOCK = 512
QUERY_BLOCK = 256


def key_range(start_ref, base, query_block):
    first = query_block * QUERY_BLOCK
    lowest = start_ref[first]
    highest = start_ref[first + QUERY_BLOCK - 1]
    begin = lowest // KEY_BLOCK
    end = (base + first + QUERY_BLOCK - 1) // KEY_BLOCK + 1
    full_begin = jnp.minimum((highest + KEY_BLOCK - 1) // KEY_BLOCK, end)
    full_end = jnp.maximum((base + first + 1) // KEY_BLOCK, full_begin)
    return begin, full_begin, full_end, end


def allowed_pairs(key_block, start_row, base_row):
    shape = (KEY_BLOCK, QUERY_BLOCK)
    key_pos = key_block * KEY_BLOCK + lax.broadcasted_iota(jnp.int32, shape, 0)
    query_pos = base_row + lax.broadcasted_iota(jnp.int32, shape, 1)
    return (key_pos >= start_row) & (key_pos <= query_pos)


def attend_kernel(
    scale, start_sm, base_sm, q_ref, kv_ref, start_ref, logit_ref, o_ref, a_ref, lse_ref
):
    base = base_sm[0]
    size = q_ref.shape[1]
    factor = scale * math.log2(math.e)

    @pl.loop(0, q_ref.shape[0] // QUERY_BLOCK)
    def _(block):
        rows = pl.ds(pl.multiple_of(block * QUERY_BLOCK, QUERY_BLOCK), QUERY_BLOCK)
        queries = q_ref[rows]
        start_row = start_ref[:, rows]
        begin, full_begin, full_end, end = key_range(start_sm, base, block)

        def step(masked, at, state):
            old_max, old_sum, total = state
            keys = pl.ds(pl.multiple_of(at * KEY_BLOCK, KEY_BLOCK), KEY_BLOCK)
            scores = cols_inner(kv_ref[keys, :size], queries)
            if masked:
                allowed = allowed_pairs(at, start_row, base + block * QUERY_BLOCK)
                scores = jnp.where(allowed, scores, MASKED)
            new_max = jnp.maximum(old_max, jnp.max(scores, axis=0, keepdims=True))
            keep = jnp.exp2((old_max - new_max) * factor)
            weights = jnp.exp2(scores * factor - new_max * factor)
            new_sum = old_sum * keep + jnp.sum(weights, axis=0, keepdims=True)
            total = total * keep + rows_inner(kv_ref[keys, size:], weights.astype(BF))
            return new_max, new_sum, total

        state = (
            jnp.full((1, QUERY_BLOCK), MASKED, F32),
            jnp.zeros((1, QUERY_BLOCK), F32),
            jnp.zeros((size, QUERY_BLOCK), F32),
        )
        state = lax.fori_loop(begin, full_begin, functools.partial(step, True), state)
        state = lax.fori_loop(full_begin, full_end, functools.partial(step, False), state)
        state = lax.fori_loop(full_end, end, functools.partial(step, True), state)
        run_max, run_sum, total = state
        lse_ref[:, rows] = run_max * factor + jnp.log2(run_sum)
        attended = (total / run_sum).T
        o_ref[rows] = attended
        a_ref[rows] = (attended * jax.nn.sigmoid(logit_ref[rows])).astype(BF)


def attend_back_kernel(
    scale, start_sm, base_sm, q_ref, kv_ref, start_ref, logit_ref, o_ref, da_ref, lse_ref,
    dq_ref, dg_ref, dkv_ref, dk_acc, dv_acc,
):
    base = base_sm[0]
    size = q_ref.shape[1]
    factor = scale * math.log2(math.e)
    dk_acc[...] = jnp.zeros_like(dk_acc)
    dv_acc[...] = jnp.zeros_like(dv_acc)

    @pl.loop(0, q_ref.shape[0] // QUERY_BLOCK)
    def _(block):
        rows = pl.ds(pl.multiple_of(block * QUERY_BLOCK, QUERY_BLOCK), QUERY_BLOCK)
        queries = q_ref[rows]
        start_row = start_ref[:, rows]
        lse = lse_ref[:, rows]
        gate = jax.nn.sigmoid(logit_ref[rows])
        attended = o_ref[rows]
        d_mixed = da_ref[rows].astype(F32)
        d_attended = (d_mixed * gate).astype(BF)
        dg_ref[rows] = (d_mixed * attended * gate * (1.0 - gate)).astype(BF)
        delta = jnp.sum((d_attended.astype(F32) * attended).T, axis=0, keepdims=True)
        begin, full_begin, full_end, end = key_range(start_sm, base, block)

        def step(masked, at, d_queries):
            keys = pl.ds(pl.multiple_of(at * KEY_BLOCK, KEY_BLOCK), KEY_BLOCK)
            key_block = kv_ref[keys, :size]
            probs = jnp.exp2(cols_inner(key_block, queries) * factor - lse)
            if masked:
                allowed = allowed_pairs(at, start_row, base + block * QUERY_BLOCK)
                probs = jnp.where(allowed, probs, 0.0)
            d_probs = cols_inner(kv_ref[keys, size:], d_attended)
            d_scores = (probs * (d_probs - delta) * scale).astype(BF)
            dv_acc[keys] += matmul(probs.astype(BF), d_attended)
            dk_acc[keys] += matmul(d_scores, queries)
            return d_queries + rows_inner(key_block, d_scores)

        d_queries = jnp.zeros((size, QUERY_BLOCK), F32)
        d_queries = lax.fori_loop(begin, full_begin, functools.partial(step, True), d_queries)
        d_queries = lax.fori_loop(full_begin, full_end, functools.partial(step, False), d_queries)
        d_queries = lax.fori_loop(full_end, end, functools.partial(step, True), d_queries)
        dq_ref[rows] = d_queries.T.astype(BF)

    @pl.loop(0, kv_ref.shape[0] // KEY_BLOCK)
    def _(at):
        keys = pl.ds(pl.multiple_of(at * KEY_BLOCK, KEY_BLOCK), KEY_BLOCK)
        dkv_ref[keys, :size] = dk_acc[keys].astype(BF)
        dkv_ref[keys, size:] = dv_acc[keys].astype(BF)


def local_call(kernel, scalars, arrays, outs, scratch, flops, name):
    vmem = pl.BlockSpec(memory_space=pltpu.VMEM)
    smem = pl.BlockSpec(memory_space=pltpu.SMEM)
    return pl.pallas_call(
        kernel,
        out_shape=outs,
        in_specs=[smem] * len(scalars) + [vmem] * len(arrays),
        out_specs=[vmem] * len(outs),
        scratch_shapes=scratch,
        compiler_params=pltpu.CompilerParams(vmem_limit_bytes=VMEM_LIMIT),
        cost_estimate=pl.CostEstimate(flops=flops, bytes_accessed=8 << 20, transcendentals=0),
        name=name,
    )(*scalars, *arrays)


def from_partner(block, axis):
    count = lax.axis_size(axis)
    route = [(at, at ^ 1) for at in range(count)]
    return lax.ppermute(block, axis, route)


def matmul(left, right):
    return jnp.dot(left, right, preferred_element_type=F32)


def rows_inner(left, right):
    return lax.dot_general(left, right, (((0,), (0,)), ((), ())), preferred_element_type=F32)


def cols_inner(left, right):
    return lax.dot_general(left, right, (((1,), (1,)), ((), ())), preferred_element_type=F32)


def rms_scale(values):
    return lax.rsqrt(jnp.mean(values * values, axis=1, keepdims=True) + EPSILON)


def order_halves(own, mate, first):
    return jnp.where(first, jnp.concatenate([own, mate], 1), jnp.concatenate([mate, own], 1))


def per_device(
    tokens,
    segment_ids,
    norm1_gain,
    w_query,
    w_key,
    w_value,
    w_gate,
    w_out,
    norm2_gain,
    w_mlp_gate,
    w_mlp_up,
    w_down,
    out_grad,
):
    heads = lax.axis_size("head")
    batches = lax.axis_size("batch")
    row_count, width = tokens.shape
    head_size = w_query.shape[1]
    half = w_key.shape[1]
    chunk = row_count // heads
    first = lax.axis_index("head") % 2 == 0
    me = ring_place(lax.axis_index("head"), heads)
    scale_factor = 1.0 / math.sqrt(head_size)

    kv_shard = jnp.concatenate([w_key, w_value], axis=1)
    kv_mate = from_partner(kv_shard, "head")
    w_in = jnp.concatenate(
        [
            w_query,
            order_halves(w_key, kv_mate[:, :half], first),
            order_halves(w_value, kv_mate[:, half:], first),
            w_gate,
        ],
        axis=1,
    )
    w_in = lax.all_gather(w_in, "batch", axis=0, tiled=True)
    gains = lax.all_gather(jnp.stack([norm1_gain, norm2_gain]), "batch", axis=1, tiled=True)
    gain_one = gains[0].astype(F32)
    gain_two = gains[1].astype(F32)
    (out_rows,) = spread([w_out], 1)
    out_full = lax.all_gather(out_rows.reshape(heads * head_size, -1), "batch", axis=1, tiled=True)
    mgate_full = lax.all_gather(w_mlp_gate, "batch", axis=0, tiled=True)
    mup_full = lax.all_gather(w_mlp_up, "batch", axis=0, tiled=True)
    down_full = lax.all_gather(w_down, "batch", axis=1, tiled=True)

    inputs = tokens.astype(F32)
    recip_one = rms_scale(inputs)
    normed_one = (inputs * recip_one * gain_one).astype(BF)
    projected = matmul(normed_one, w_in)
    queries = projected[:, :head_size].astype(BF)
    kv_local = projected[:, head_size : 3 * head_size].astype(BF)
    gate_logit = projected[:, 3 * head_size :]
    kv_all = lax.all_gather(kv_local, "batch", axis=0, tiled=True)
    seg_all = lax.all_gather(segment_ids, "batch", axis=0, tiled=True)
    base = lax.axis_index("batch") * row_count
    ids = jnp.arange(DOCUMENTS, dtype=jnp.int32)
    below = jnp.sum((seg_all[None, :] < ids[:, None]).astype(jnp.int32), axis=1)
    starts = jnp.sum(jnp.where(segment_ids[None, :] == ids[:, None], below[:, None], 0), axis=0)
    scalars = (starts, base.reshape(1))
    pair_flops = 4 * row_count * kv_all.shape[0] * head_size
    attended, mixed, lse = local_call(
        functools.partial(attend_kernel, scale_factor),
        scalars,
        (queries, kv_all, starts[None], gate_logit),
        [
            jax.ShapeDtypeStruct((row_count, head_size), F32),
            jax.ShapeDtypeStruct((row_count, head_size), BF),
            jax.ShapeDtypeStruct((1, row_count), F32),
        ],
        [],
        pair_flops,
        "attend",
    )
    (mixed_all,) = spread([mixed], 2)
    mixed_all = mixed_all.transpose(1, 0, 2).reshape(row_count, -1)
    resid = inputs + matmul(mixed_all, out_full)
    recip_two = rms_scale(resid)
    normed_two = (resid * recip_two * gain_two).astype(BF)
    resid_own = lax.dynamic_slice_in_dim(resid, me * chunk, chunk, 0)
    recip_own = lax.dynamic_slice_in_dim(recip_two, me * chunk, chunk, 0)
    mixed_own = lax.dynamic_slice_in_dim(mixed_all, me * chunk, chunk, 0)
    dy_own = lax.dynamic_slice_in_dim(out_grad, me * chunk, chunk, 0).astype(F32)

    gate_pre = matmul(normed_two, mgate_full)
    up_pre = matmul(normed_two, mup_full)
    sig_gate = jax.nn.sigmoid(gate_pre)
    silu_gate = gate_pre * sig_gate
    hidden = (silu_gate * up_pre).astype(BF)
    d_hidden = cols_inner(out_grad, down_full)
    d_gate_pre = (d_hidden * up_pre * sig_gate * (1.0 + gate_pre * (1.0 - sig_gate))).astype(BF)
    d_up_pre = (d_hidden * silu_gate).astype(BF)
    dn2_part = cols_inner(d_gate_pre, mgate_full) + cols_inner(d_up_pre, mup_full)
    dn2 = sum_own(dn2_part.astype(BF), 3)
    mlp_part = matmul(hidden, down_full).astype(BF)
    output = (resid_own + sum_own(mlp_part, 4)).astype(BF)

    d_gain_two = jnp.sum(dn2 * resid_own * recip_own, axis=0)
    weighted_two = gain_two * dn2
    d_resid = (
        dy_own
        + recip_own * weighted_two
        - resid_own * recip_own**3 * jnp.mean(weighted_two * resid_own, axis=1, keepdims=True)
    )
    d_resid_low = d_resid.astype(BF)
    d_mixed_all = cols_inner(d_resid_low, out_full).astype(BF)
    d_mixed_all = d_mixed_all.reshape(chunk, heads, head_size)
    places = [ring_place(at, heads) for at in range(heads)]
    d_mixed_all = jnp.stack([d_mixed_all[:, at] for at in places], axis=0)
    d_mixed = lax.all_to_all(d_mixed_all, "head", split_axis=0, concat_axis=0, tiled=True)
    d_mixed = jnp.concatenate([d_mixed[ring_head(at, heads)] for at in range(heads)], axis=0)
    d_out_part = rows_inner(mixed_own, d_resid_low).astype(BF)
    d_out_part = lax.psum_scatter(d_out_part, "batch", scatter_dimension=1, tiled=True)
    d_out = sum_own(d_out_part, 7)

    d_queries, d_gate_logit, d_kv_all = local_call(
        functools.partial(attend_back_kernel, scale_factor),
        scalars,
        (queries, kv_all, starts[None], gate_logit, attended, d_mixed, lse),
        [
            jax.ShapeDtypeStruct((row_count, head_size), BF),
            jax.ShapeDtypeStruct((row_count, head_size), BF),
            jax.ShapeDtypeStruct(kv_all.shape, BF),
        ],
        [pltpu.VMEM((kv_all.shape[0], head_size), F32)] * 2,
        5 * pair_flops // 2,
        "attend_back",
    )
    d_kv_own = lax.psum_scatter(d_kv_all, "batch", scatter_dimension=0, tiled=True)
    d_kv_mate = from_partner(d_kv_own, "head")
    d_kv = (d_kv_own.astype(F32) + d_kv_mate.astype(F32)).astype(BF)
    d_cat = jnp.concatenate(
        [
            d_queries,
            jnp.where(first, d_kv[:, :half], d_kv[:, half:head_size]),
            jnp.where(first, d_kv[:, head_size : head_size + half], d_kv[:, head_size + half :]),
            d_gate_logit,
        ],
        axis=1,
    )
    w_key_own = jnp.where(
        first, w_in[:, head_size : head_size + half], w_in[:, head_size + half : 2 * head_size]
    )
    w_value_own = jnp.where(
        first, w_in[:, 2 * head_size : 2 * head_size + half], w_in[:, 2 * head_size + half : 3 * head_size]
    )
    w_cat = jnp.concatenate(
        [w_in[:, :head_size], w_key_own, w_value_own, w_in[:, 3 * head_size :]], axis=1
    )
    dn1_part = cols_inner(d_cat, w_cat).astype(BF)
    dn1 = sum_own(dn1_part, 5)
    inputs_own = lax.dynamic_slice_in_dim(inputs, me * chunk, chunk, 0)
    recip_in = lax.dynamic_slice_in_dim(recip_one, me * chunk, chunk, 0)
    d_gain_one = jnp.sum(dn1 * inputs_own * recip_in, axis=0)
    weighted_one = gain_one * dn1
    d_tokens = (
        d_resid
        + recip_in * weighted_one
        - inputs_own * recip_in**3 * jnp.mean(weighted_one * inputs_own, axis=1, keepdims=True)
    ).astype(BF)
    output, d_tokens = spread([output, d_tokens], 6)
    output = output.reshape(row_count, width)
    d_tokens = d_tokens.reshape(row_count, width)

    d_mlp = jnp.concatenate(
        [rows_inner(normed_two, d_gate_pre).astype(BF), rows_inner(normed_two, d_up_pre).astype(BF)], 1
    )
    d_mlp = lax.psum_scatter(d_mlp, "batch", scatter_dimension=0, tiled=True).astype(F32)
    d_down = rows_inner(hidden, out_grad).astype(BF)
    d_down = lax.psum_scatter(d_down, "batch", scatter_dimension=1, tiled=True).astype(F32)
    d_in = rows_inner(normed_one, d_cat).astype(BF)
    d_in = lax.psum_scatter(d_in, "batch", scatter_dimension=0, tiled=True).astype(F32)
    d_gains = jnp.concatenate([d_gain_one, d_gain_two])
    d_gains = lax.all_gather(d_gains, "head", axis=0)
    d_gains = jnp.sum(d_gains, axis=0).reshape(2, batches, -1)
    d_gains = lax.all_to_all(d_gains, "batch", split_axis=1, concat_axis=1, tiled=True)
    d_gains = jnp.sum(d_gains, axis=1)
    hidden_own = w_mlp_gate.shape[1]
    return (
        output,
        d_tokens,
        d_gains[0],
        d_in[:, :head_size],
        d_in[:, head_size : head_size + half],
        d_in[:, head_size + half : 2 * head_size],
        d_in[:, 2 * head_size :],
        d_out,
        d_gains[1],
        d_mlp[:, :hidden_own],
        d_mlp[:, hidden_own:],
        d_down,
    )


def solution(mesh):
    return jax.shard_map(
        per_device,
        mesh=mesh,
        in_specs=(
            P("batch", None),
            P("batch"),
            P("batch"),
            P("batch", "head"),
            P("batch", "head"),
            P("batch", "head"),
            P("batch", "head"),
            P("head", "batch"),
            P("batch"),
            P("batch", "head"),
            P("batch", "head"),
            P("head", "batch"),
            P("batch", None),
        ),
        out_specs=(
            P("batch", None),
            P("batch", None),
            P("batch"),
            P("batch", "head"),
            P("batch", "head"),
            P("batch", "head"),
            P("batch", "head"),
            P("head", "batch"),
            P("batch"),
            P("batch", "head"),
            P("batch", "head"),
            P("head", "batch"),
        ),
        check_vma=False,
    )
```

```python
import functools
import math

import jax
import jax.numpy as jnp
from jax import lax
from jax.experimental import pallas as pl
from jax.experimental.pallas import tpu as pltpu
from jax.sharding import PartitionSpec as P

EPSILON = 1e-06
MASKED = -1e30
DOCUMENTS = 7
BF = jnp.bfloat16
F32 = jnp.float32


MESH = pl.DeviceIdType.MESH
VMEM_LIMIT = 60 << 20


def ring_place(head, count):
    high, low = head // 2, head % 2
    return (1 - low) * high + low * (count - 1 - high)


def ring_head(place, count):
    low = place // (count // 2)
    high = (1 - low) * place + low * (count - 1 - place)
    return 2 * high + low


def ring_setup(count):
    batch = lax.axis_index("batch")
    place = ring_place(lax.axis_index("head"), count)
    right = (batch, ring_head(lax.rem(place + 1, count), count))
    left = (batch, ring_head(lax.rem(place + count - 1, count), count))
    return place, right, left


def greet(devices):
    barrier = pltpu.get_barrier_semaphore()
    for device in devices:
        pl.semaphore_signal(barrier, inc=1, device_id=device, device_id_type=MESH)
    pl.semaphore_wait(barrier, len(devices))


def send(source, target, sems, slot, device):
    copy = pltpu.make_async_remote_copy(
        src_ref=source,
        dst_ref=target,
        send_sem=sems[0].at[slot],
        recv_sem=sems[1].at[slot],
        device_id=device,
        device_id_type=MESH,
    )
    copy.start()
    return copy


def sum_kernel(count, part_ref, own_ref, from_left, from_right, send_sem, recv_sem):
    steps = count // 2
    rows = part_ref.shape[0] // count
    width = part_ref.shape[1]
    side = width // 2
    place, right, left = ring_setup(count)
    greet((right, left))
    sems = (send_sem, recv_sem)

    def part(owner):
        return part_ref.at[pl.ds(pl.multiple_of(lax.rem(owner + count, count) * rows, rows), rows)]

    far = part(place + steps)
    copies = [
        send(far.at[:, pl.ds(0, side)], from_left.at[0, :, pl.ds(0, side)], sems, 0, right),
        send(far.at[:, pl.ds(side, side)], from_right.at[0, :, pl.ds(side, side)], sems, steps, left),
    ]
    for step in range(1, steps):
        for flow, held, owner, device in (
            (0, from_left, place + steps - step, right),
            (1, from_right, place - steps + step, left),
        ):
            copies[2 * step - 2 + flow].wait_recv()
            mine = part(owner)
            if step == 1:
                have = pl.ds(flow * side, side)
                lack = pl.ds((1 - flow) * side, side)
                held[0, :, have] = (held[0, :, have].astype(F32) + mine[:, have].astype(F32)).astype(BF)
                held[0, :, lack] = mine[:, lack]
            else:
                held[step - 1] = (held[step - 1].astype(F32) + mine[...].astype(F32)).astype(BF)
            copies.append(
                send(held.at[step - 1], held.at[step], sems, flow * steps + step, device)
            )
    copies[-2].wait_recv()
    copies[-1].wait_recv()
    own_ref[...] = (
        part(place)[...].astype(F32)
        + from_left[steps - 1].astype(F32)
        + from_right[steps - 1].astype(F32)
    )
    for copy in copies:
        copy.wait_send()


def sum_own(part, collective_id):
    count = lax.axis_size("head")
    rows, width = part.shape[0] // count, part.shape[1]
    vmem = pl.BlockSpec(memory_space=pltpu.VMEM)
    return pl.pallas_call(
        functools.partial(sum_kernel, count),
        out_shape=jax.ShapeDtypeStruct((rows, width), F32),
        in_specs=[vmem],
        out_specs=vmem,
        scratch_shapes=[
            pltpu.VMEM((count // 2, rows, width), BF),
            pltpu.VMEM((count // 2, rows, width), BF),
            pltpu.SemaphoreType.DMA((count,)),
            pltpu.SemaphoreType.DMA((count,)),
        ],
        compiler_params=pltpu.CompilerParams(
            collective_id=collective_id, has_side_effects=True, vmem_limit_bytes=VMEM_LIMIT
        ),
        name=f"sum_own_{collective_id}",
    )(part)


def half_of(extent, flow):
    if extent[1] % 256:
        return (pl.ds(flow * (extent[0] // 2), extent[0] // 2), slice(None))
    return (slice(None), pl.ds(flow * (extent[1] // 2), extent[1] // 2))


def spread_kernel(count, arrays, *refs):
    steps = count // 2
    own_refs, all_refs = refs[:arrays], refs[arrays : 2 * arrays]
    send_sem, recv_sem, local_sem = refs[2 * arrays :]
    place, right, left = ring_setup(count)
    greet((right, left))
    sems = (send_sem, recv_sem)
    local = []
    for index in range(arrays):
        copy = pltpu.make_async_copy(own_refs[index], all_refs[index].at[place], local_sem.at[index])
        copy.start()
        local.append(copy)
    waiting = []
    copies = [None] * (2 * arrays)
    for step in range(steps):
        for index in range(arrays):
            extent = own_refs[index].shape
            for flow, chunk, device in (
                (0, place - step, right),
                (1, place + step, left),
            ):
                at = 2 * index + flow
                if step:
                    copies[at].wait_recv()
                chunk = lax.rem(chunk + count, count)
                target = all_refs[index].at[chunk]
                source = target if step else own_refs[index]
                if step == steps - 1:
                    part = half_of(extent, flow)
                    source = source.at[part]
                    target = target.at[part]
                copies[at] = send(source, target, sems, at * steps + step, device)
                waiting.append(copies[at])
    for copy in copies:
        copy.wait_recv()
    for copy in waiting:
        copy.wait_send()
    for copy in local:
        copy.wait()


def spread(arrays, collective_id, space=pl.ANY):
    count = lax.axis_size("head")
    slots = len(arrays) * count
    return pl.pallas_call(
        functools.partial(spread_kernel, count, len(arrays)),
        out_shape=[jax.ShapeDtypeStruct((count, *a.shape), a.dtype) for a in arrays],
        in_specs=[pl.BlockSpec(memory_space=space)] * len(arrays),
        out_specs=[pl.BlockSpec(memory_space=space)] * len(arrays),
        scratch_shapes=[
            pltpu.SemaphoreType.DMA((slots,)),
            pltpu.SemaphoreType.DMA((slots,)),
            pltpu.SemaphoreType.DMA((len(arrays),)),
        ],
        compiler_params=pltpu.CompilerParams(
            collective_id=collective_id, has_side_effects=True, vmem_limit_bytes=VMEM_LIMIT
        ),
        name=f"spread_{collective_id}",
    )(*arrays)


KEY_BLOCK = 512
QUERY_BLOCK = 256


def key_range(start_ref, base, query_block):
    first = query_block * QUERY_BLOCK
    lowest = start_ref[first]
    highest = start_ref[first + QUERY_BLOCK - 1]
    begin = lowest // KEY_BLOCK
    end = (base + first + QUERY_BLOCK - 1) // KEY_BLOCK + 1
    full_begin = jnp.minimum((highest + KEY_BLOCK - 1) // KEY_BLOCK, end)
    full_end = jnp.maximum((base + first + 1) // KEY_BLOCK, full_begin)
    return begin, full_begin, full_end, end


def allowed_pairs(key_block, start_row, base_row):
    shape = (KEY_BLOCK, QUERY_BLOCK)
    key_pos = key_block * KEY_BLOCK + lax.broadcasted_iota(jnp.int32, shape, 0)
    query_pos = base_row + lax.broadcasted_iota(jnp.int32, shape, 1)
    return (key_pos >= start_row) & (key_pos <= query_pos)


def attend_kernel(
    scale, start_sm, base_sm, q_ref, kv_ref, start_ref, logit_ref, o_ref, a_ref, lse_ref
):
    base = base_sm[0]
    size = q_ref.shape[1]
    factor = scale * math.log2(math.e)

    @pl.loop(0, q_ref.shape[0] // QUERY_BLOCK)
    def _(block):
        rows = pl.ds(pl.multiple_of(block * QUERY_BLOCK, QUERY_BLOCK), QUERY_BLOCK)
        queries = q_ref[rows]
        start_row = start_ref[:, rows]
        begin, full_begin, full_end, end = key_range(start_sm, base, block)

        def step(masked, at, state):
            old_max, old_sum, total = state
            keys = pl.ds(pl.multiple_of(at * KEY_BLOCK, KEY_BLOCK), KEY_BLOCK)
            scores = cols_inner(kv_ref[keys, :size], queries)
            if masked:
                allowed = allowed_pairs(at, start_row, base + block * QUERY_BLOCK)
                scores = jnp.where(allowed, scores, MASKED)
            new_max = jnp.maximum(old_max, jnp.max(scores, axis=0, keepdims=True))
            keep = jnp.exp2((old_max - new_max) * factor)
            weights = jnp.exp2(scores * factor - new_max * factor)
            new_sum = old_sum * keep + jnp.sum(weights, axis=0, keepdims=True)
            total = total * keep + rows_inner(kv_ref[keys, size:], weights.astype(BF))
            return new_max, new_sum, total

        state = (
            jnp.full((1, QUERY_BLOCK), MASKED, F32),
            jnp.zeros((1, QUERY_BLOCK), F32),
            jnp.zeros((size, QUERY_BLOCK), F32),
        )
        state = lax.fori_loop(begin, full_begin, functools.partial(step, True), state)
        state = lax.fori_loop(full_begin, full_end, functools.partial(step, False), state)
        state = lax.fori_loop(full_end, end, functools.partial(step, True), state)
        run_max, run_sum, total = state
        lse_ref[:, rows] = run_max * factor + jnp.log2(run_sum)
        attended = (total / run_sum).T
        o_ref[rows] = attended
        a_ref[rows] = (attended * jax.nn.sigmoid(logit_ref[rows])).astype(BF)


def attend_back_kernel(
    scale, start_sm, base_sm, q_ref, kv_ref, start_ref, logit_ref, o_ref, da_ref, lse_ref,
    dq_ref, dg_ref, dkv_ref, dk_acc, dv_acc,
):
    base = base_sm[0]
    size = q_ref.shape[1]
    factor = scale * math.log2(math.e)
    dk_acc[...] = jnp.zeros_like(dk_acc)
    dv_acc[...] = jnp.zeros_like(dv_acc)

    @pl.loop(0, q_ref.shape[0] // QUERY_BLOCK)
    def _(block):
        rows = pl.ds(pl.multiple_of(block * QUERY_BLOCK, QUERY_BLOCK), QUERY_BLOCK)
        queries = q_ref[rows]
        start_row = start_ref[:, rows]
        lse = lse_ref[:, rows]
        gate = jax.nn.sigmoid(logit_ref[rows])
        attended = o_ref[rows]
        d_mixed = da_ref[rows].astype(F32)
        d_attended = (d_mixed * gate).astype(BF)
        dg_ref[rows] = (d_mixed * attended * gate * (1.0 - gate)).astype(BF)
        delta = jnp.sum((d_attended.astype(F32) * attended).T, axis=0, keepdims=True)
        begin, full_begin, full_end, end = key_range(start_sm, base, block)

        def step(masked, at, d_queries):
            keys = pl.ds(pl.multiple_of(at * KEY_BLOCK, KEY_BLOCK), KEY_BLOCK)
            key_block = kv_ref[keys, :size]
            probs = jnp.exp2(cols_inner(key_block, queries) * factor - lse)
            if masked:
                allowed = allowed_pairs(at, start_row, base + block * QUERY_BLOCK)
                probs = jnp.where(allowed, probs, 0.0)
            d_probs = cols_inner(kv_ref[keys, size:], d_attended)
            d_scores = (probs * (d_probs - delta) * scale).astype(BF)
            dv_acc[keys] += matmul(probs.astype(BF), d_attended)
            dk_acc[keys] += matmul(d_scores, queries)
            return d_queries + rows_inner(key_block, d_scores)

        d_queries = jnp.zeros((size, QUERY_BLOCK), F32)
        d_queries = lax.fori_loop(begin, full_begin, functools.partial(step, True), d_queries)
        d_queries = lax.fori_loop(full_begin, full_end, functools.partial(step, False), d_queries)
        d_queries = lax.fori_loop(full_end, end, functools.partial(step, True), d_queries)
        dq_ref[rows] = d_queries.T.astype(BF)

    @pl.loop(0, kv_ref.shape[0] // KEY_BLOCK)
    def _(at):
        keys = pl.ds(pl.multiple_of(at * KEY_BLOCK, KEY_BLOCK), KEY_BLOCK)
        dkv_ref[keys, :size] = dk_acc[keys].astype(BF)
        dkv_ref[keys, size:] = dv_acc[keys].astype(BF)


def local_call(kernel, scalars, arrays, outs, scratch, flops, name):
    vmem = pl.BlockSpec(memory_space=pltpu.VMEM)
    smem = pl.BlockSpec(memory_space=pltpu.SMEM)
    return pl.pallas_call(
        kernel,
        out_shape=outs,
        in_specs=[smem] * len(scalars) + [vmem] * len(arrays),
        out_specs=[vmem] * len(outs),
        scratch_shapes=scratch,
        compiler_params=pltpu.CompilerParams(vmem_limit_bytes=VMEM_LIMIT),
        cost_estimate=pl.CostEstimate(flops=flops, bytes_accessed=8 << 20, transcendentals=0),
        name=name,
    )(*scalars, *arrays)


def ring_routes(count):
    spots = [ring_head(at, count) for at in range(count)]
    right = [(spots[at], spots[(at + 1) % count]) for at in range(count)]
    left = [(spots[at], spots[at - 1]) for at in range(count)]
    return right, left


def add_low(one, other):
    return (one.astype(F32) + other.astype(F32)).astype(BF)


def flow_sum(part):
    count = lax.axis_size("head")
    place = ring_place(lax.axis_index("head"), count)
    right, left = ring_routes(count)
    rows, side = part.shape[0] // count, part.shape[1] // 2
    steps = count // 2

    def mine(owner):
        return lax.dynamic_slice_in_dim(part, lax.rem(owner + count, count) * rows, rows, 0)

    far = mine(place + steps)
    for step in range(steps):
        if step == 0:
            going, coming = far[:, :side], far[:, side:]
        from_left = lax.ppermute(going, "head", right)
        from_right = lax.ppermute(coming, "head", left)
        if step == steps - 1:
            break
        one, two = mine(place + steps - 1 - step), mine(place - steps + 1 + step)
        if step == 0:
            going = jnp.concatenate([add_low(from_left, one[:, :side]), one[:, side:]], 1)
            coming = jnp.concatenate([two[:, :side], add_low(from_right, two[:, side:])], 1)
        else:
            going, coming = add_low(from_left, one), add_low(from_right, two)
    return mine(place).astype(F32) + from_left.astype(F32) + from_right.astype(F32)


def flow_spread(own):
    count = lax.axis_size("head")
    place = ring_place(lax.axis_index("head"), count)
    right, left = ring_routes(count)
    side = own.shape[1] // 2
    going = coming = own
    pieces = [(0, own)]
    for step in range(1, count // 2):
        going = lax.ppermute(going, "head", right)
        coming = lax.ppermute(coming, "head", left)
        pieces += [(-step, going), (step, coming)]
    one = lax.ppermute(going[:, :side], "head", right)
    two = lax.ppermute(coming[:, side:], "head", left)
    pieces.append((count // 2, jnp.concatenate([one, two], 1)))
    whole = jnp.zeros((count * own.shape[0], own.shape[1]), own.dtype)
    for shift, piece in pieces:
        at = lax.rem(place + shift + count, count) * own.shape[0]
        whole = lax.dynamic_update_slice_in_dim(whole, piece, at, 0)
    return whole


def swap(block, axis, stride):
    return lax.ppermute(block, axis, [(at, at ^ stride) for at in range(lax.axis_size(axis))])


def halve_batch(block, rows):
    me = lax.axis_index("batch")
    stride = 1
    while stride < lax.axis_size("batch"):
        block = block.reshape(-1, 2, rows, block.shape[-1])
        bit = (me // stride) % 2
        keep = lax.dynamic_index_in_dim(block, bit, 1, keepdims=False)
        give = lax.dynamic_index_in_dim(block, 1 - bit, 1, keepdims=False)
        got = swap(give, "batch", stride)
        block = (keep.astype(F32) + got.astype(F32)).astype(block.dtype)
        stride *= 2
    return block.reshape(rows, -1)


def sum_heads(block):
    stride = 1
    while stride < lax.axis_size("head"):
        block = block + swap(block, "head", stride)
        stride *= 2
    return block


def from_partner(block, axis):
    count = lax.axis_size(axis)
    route = [(at, at ^ 1) for at in range(count)]
    return lax.ppermute(block, axis, route)


def matmul(left, right):
    return jnp.dot(left, right, preferred_element_type=F32)


def rows_inner(left, right):
    return lax.dot_general(left, right, (((0,), (0,)), ((), ())), preferred_element_type=F32)


def cols_inner(left, right):
    return lax.dot_general(left, right, (((1,), (1,)), ((), ())), preferred_element_type=F32)


def rms_scale(values):
    return lax.rsqrt(jnp.mean(values * values, axis=1, keepdims=True) + EPSILON)


def order_halves(own, mate, first):
    return jnp.where(first, jnp.concatenate([own, mate], 1), jnp.concatenate([mate, own], 1))


def per_device(
    tokens,
    segment_ids,
    norm1_gain,
    w_query,
    w_key,
    w_value,
    w_gate,
    w_out,
    norm2_gain,
    w_mlp_gate,
    w_mlp_up,
    w_down,
    out_grad,
):
    heads = lax.axis_size("head")
    batches = lax.axis_size("batch")
    row_count, width = tokens.shape
    head_size = w_query.shape[1]
    half = w_key.shape[1]
    chunk = row_count // heads
    first = lax.axis_index("head") % 2 == 0
    me = ring_place(lax.axis_index("head"), heads)
    scale_factor = 1.0 / math.sqrt(head_size)

    kv_shard = jnp.concatenate([w_key, w_value], axis=1)
    kv_mate = from_partner(kv_shard, "head")
    w_in = jnp.concatenate(
        [
            w_query,
            order_halves(w_key, kv_mate[:, :half], first),
            order_halves(w_value, kv_mate[:, half:], first),
            w_gate,
        ],
        axis=1,
    )
    w_in = lax.all_gather(w_in, "batch", axis=0, tiled=True)
    gains = lax.all_gather(jnp.stack([norm1_gain, norm2_gain]), "batch", axis=1, tiled=True)
    gain_one = gains[0].astype(F32)
    gain_two = gains[1].astype(F32)
    (out_rows,) = spread([w_out], 1)
    out_full = lax.all_gather(out_rows.reshape(heads * head_size, -1), "batch", axis=1, tiled=True)
    mgate_full = lax.all_gather(w_mlp_gate, "batch", axis=0, tiled=True)
    mup_full = lax.all_gather(w_mlp_up, "batch", axis=0, tiled=True)
    down_full = lax.all_gather(w_down, "batch", axis=1, tiled=True)

    inputs = tokens.astype(F32)
    recip_one = rms_scale(inputs)
    normed_one = (inputs * recip_one * gain_one).astype(BF)
    projected = matmul(normed_one, w_in)
    queries = projected[:, :head_size].astype(BF)
    kv_local = projected[:, head_size : 3 * head_size].astype(BF)
    gate_logit = projected[:, 3 * head_size :]
    kv_all = lax.all_gather(kv_local, "batch", axis=0, tiled=True)
    seg_all = lax.all_gather(segment_ids, "batch", axis=0, tiled=True)
    base = lax.axis_index("batch") * row_count
    ids = jnp.arange(DOCUMENTS, dtype=jnp.int32)
    below = jnp.sum((seg_all[None, :] < ids[:, None]).astype(jnp.int32), axis=1)
    starts = jnp.sum(jnp.where(segment_ids[None, :] == ids[:, None], below[:, None], 0), axis=0)
    scalars = (starts, base.reshape(1))
    pair_flops = 4 * row_count * kv_all.shape[0] * head_size
    attended, mixed, lse = local_call(
        functools.partial(attend_kernel, scale_factor),
        scalars,
        (queries, kv_all, starts[None], gate_logit),
        [
            jax.ShapeDtypeStruct((row_count, head_size), F32),
            jax.ShapeDtypeStruct((row_count, head_size), BF),
            jax.ShapeDtypeStruct((1, row_count), F32),
        ],
        [],
        pair_flops,
        "attend",
    )
    (mixed_all,) = spread([mixed], 2)
    mixed_all = mixed_all.transpose(1, 0, 2).reshape(row_count, -1)
    resid = inputs + matmul(mixed_all, out_full)
    recip_two = rms_scale(resid)
    normed_two = (resid * recip_two * gain_two).astype(BF)
    resid_own = lax.dynamic_slice_in_dim(resid, me * chunk, chunk, 0)
    recip_own = lax.dynamic_slice_in_dim(recip_two, me * chunk, chunk, 0)
    mixed_own = lax.dynamic_slice_in_dim(mixed_all, me * chunk, chunk, 0)
    dy_own = lax.dynamic_slice_in_dim(out_grad, me * chunk, chunk, 0).astype(F32)

    gate_pre = matmul(normed_two, mgate_full)
    up_pre = matmul(normed_two, mup_full)
    sig_gate = jax.nn.sigmoid(gate_pre)
    silu_gate = gate_pre * sig_gate
    hidden = (silu_gate * up_pre).astype(BF)
    d_hidden = cols_inner(out_grad, down_full)
    d_gate_pre = (d_hidden * up_pre * sig_gate * (1.0 + gate_pre * (1.0 - sig_gate))).astype(BF)
    d_up_pre = (d_hidden * silu_gate).astype(BF)
    dn2_part = cols_inner(d_gate_pre, mgate_full) + cols_inner(d_up_pre, mup_full)
    dn2 = sum_own(dn2_part.astype(BF), 3)
    hidden_late, dn2 = lax.optimization_barrier((hidden, dn2))
    mlp_part = matmul(hidden_late, down_full).astype(BF)
    output = flow_spread((resid_own + flow_sum(mlp_part)).astype(BF))

    d_gain_two = jnp.sum(dn2 * resid_own * recip_own, axis=0)
    weighted_two = gain_two * dn2
    d_resid = (
        dy_own
        + recip_own * weighted_two
        - resid_own * recip_own**3 * jnp.mean(weighted_two * resid_own, axis=1, keepdims=True)
    )
    d_resid_low = d_resid.astype(BF)
    d_mixed_all = cols_inner(d_resid_low, out_full).astype(BF)
    d_mixed_all = d_mixed_all.reshape(chunk, heads, head_size)
    places = [ring_place(at, heads) for at in range(heads)]
    d_mixed_all = jnp.stack([d_mixed_all[:, at] for at in places], axis=0)
    d_mixed = lax.all_to_all(d_mixed_all, "head", split_axis=0, concat_axis=0, tiled=True)
    d_mixed = jnp.concatenate([d_mixed[ring_head(at, heads)] for at in range(heads)], axis=0)
    d_out_part = rows_inner(mixed_own, d_resid_low).astype(BF)
    d_out_part = lax.psum_scatter(d_out_part, "batch", scatter_dimension=1, tiled=True)
    d_out = flow_sum(d_out_part)

    d_queries, d_gate_logit, d_kv_all = local_call(
        functools.partial(attend_back_kernel, scale_factor),
        scalars,
        (queries, kv_all, starts[None], gate_logit, attended, d_mixed, lse),
        [
            jax.ShapeDtypeStruct((row_count, head_size), BF),
            jax.ShapeDtypeStruct((row_count, head_size), BF),
            jax.ShapeDtypeStruct(kv_all.shape, BF),
        ],
        [pltpu.VMEM((kv_all.shape[0], head_size), F32)] * 2,
        5 * pair_flops // 2,
        "attend_back",
    )
    d_kv_own = halve_batch(d_kv_all, row_count)
    d_kv_mate = from_partner(d_kv_own, "head")
    d_kv = (d_kv_own.astype(F32) + d_kv_mate.astype(F32)).astype(BF)
    d_cat = jnp.concatenate(
        [
            d_queries,
            jnp.where(first, d_kv[:, :half], d_kv[:, half:head_size]),
            jnp.where(first, d_kv[:, head_size : head_size + half], d_kv[:, head_size + half :]),
            d_gate_logit,
        ],
        axis=1,
    )
    w_key_own = jnp.where(
        first, w_in[:, head_size : head_size + half], w_in[:, head_size + half : 2 * head_size]
    )
    w_value_own = jnp.where(
        first, w_in[:, 2 * head_size : 2 * head_size + half], w_in[:, 2 * head_size + half : 3 * head_size]
    )
    w_cat = jnp.concatenate(
        [w_in[:, :head_size], w_key_own, w_value_own, w_in[:, 3 * head_size :]], axis=1
    )
    dn1_part = cols_inner(d_cat, w_cat).astype(BF)
    dn1 = flow_sum(dn1_part)
    inputs_own = lax.dynamic_slice_in_dim(inputs, me * chunk, chunk, 0)
    recip_in = lax.dynamic_slice_in_dim(recip_one, me * chunk, chunk, 0)
    d_gain_one = jnp.sum(dn1 * inputs_own * recip_in, axis=0)
    weighted_one = gain_one * dn1
    d_tokens = (
        d_resid
        + recip_in * weighted_one
        - inputs_own * recip_in**3 * jnp.mean(weighted_one * inputs_own, axis=1, keepdims=True)
    ).astype(BF)
    d_tokens = flow_spread(d_tokens)

    d_mlp = jnp.concatenate(
        [rows_inner(normed_two, d_gate_pre).astype(BF), rows_inner(normed_two, d_up_pre).astype(BF)], 1
    )
    d_mlp = lax.psum_scatter(d_mlp, "batch", scatter_dimension=0, tiled=True).astype(F32)
    d_down = rows_inner(hidden, out_grad).astype(BF)
    d_down = lax.psum_scatter(d_down, "batch", scatter_dimension=1, tiled=True).astype(F32)
    d_in = rows_inner(normed_one, d_cat).astype(BF)
    d_in = lax.psum_scatter(d_in, "batch", scatter_dimension=0, tiled=True).astype(F32)
    d_gains = jnp.stack([d_gain_one, d_gain_two]).reshape(2, batches, -1).transpose(1, 0, 2)
    d_gains = sum_heads(halve_batch(d_gains.reshape(2 * batches, -1), 2))
    hidden_own = w_mlp_gate.shape[1]
    return (
        output,
        d_tokens,
        d_gains[0],
        d_in[:, :head_size],
        d_in[:, head_size : head_size + half],
        d_in[:, head_size + half : 2 * head_size],
        d_in[:, 2 * head_size :],
        d_out,
        d_gains[1],
        d_mlp[:, :hidden_own],
        d_mlp[:, hidden_own:],
        d_down,
    )


def solution(mesh):
    return jax.shard_map(
        per_device,
        mesh=mesh,
        in_specs=(
            P("batch", None),
            P("batch"),
            P("batch"),
            P("batch", "head"),
            P("batch", "head"),
            P("batch", "head"),
            P("batch", "head"),
            P("head", "batch"),
            P("batch"),
            P("batch", "head"),
            P("batch", "head"),
            P("head", "batch"),
            P("batch", None),
        ),
        out_specs=(
            P("batch", None),
            P("batch", None),
            P("batch"),
            P("batch", "head"),
            P("batch", "head"),
            P("batch", "head"),
            P("batch", "head"),
            P("head", "batch"),
            P("batch"),
            P("batch", "head"),
            P("batch", "head"),
            P("head", "batch"),
        ),
        check_vma=False,
    )
```

```python
import functools
import math

import jax
import jax.numpy as jnp
from jax import lax
from jax.experimental import pallas as pl
from jax.experimental.pallas import tpu as pltpu
from jax.sharding import PartitionSpec as P

EPSILON = 1e-06
MASKED = -1e30
DOCUMENTS = 7
BF = jnp.bfloat16
F32 = jnp.float32


MESH = pl.DeviceIdType.MESH
VMEM_LIMIT = 60 << 20


def ring_place(head, count):
    high, low = head // 2, head % 2
    return (1 - low) * high + low * (count - 1 - high)


def ring_head(place, count):
    low = place // (count // 2)
    high = (1 - low) * place + low * (count - 1 - place)
    return 2 * high + low


def ring_setup(count):
    batch = lax.axis_index("batch")
    place = ring_place(lax.axis_index("head"), count)
    right = (batch, ring_head(lax.rem(place + 1, count), count))
    left = (batch, ring_head(lax.rem(place + count - 1, count), count))
    return place, right, left


def greet(devices):
    barrier = pltpu.get_barrier_semaphore()
    for device in devices:
        pl.semaphore_signal(barrier, inc=1, device_id=device, device_id_type=MESH)
    pl.semaphore_wait(barrier, len(devices))


def send(source, target, sems, slot, device):
    copy = pltpu.make_async_remote_copy(
        src_ref=source,
        dst_ref=target,
        send_sem=sems[0].at[slot],
        recv_sem=sems[1].at[slot],
        device_id=device,
        device_id_type=MESH,
    )
    copy.start()
    return copy


def half_of(extent, flow):
    if extent[1] % 256:
        return (pl.ds(flow * (extent[0] // 2), extent[0] // 2), slice(None))
    return (slice(None), pl.ds(flow * (extent[1] // 2), extent[1] // 2))


def place_of(whole, own, chunk):
    if len(whole.shape) == 3:
        return whole.at[chunk]
    wide = own.shape[1]
    return whole.at[:, pl.ds(pl.multiple_of(chunk * wide, wide), wide)]


def spread_kernel(count, arrays, *refs):
    steps = count // 2
    own_refs, all_refs = refs[:arrays], refs[arrays : 2 * arrays]
    send_sem, recv_sem, local_sem = refs[2 * arrays :]
    place, right, left = ring_setup(count)
    greet((right, left))
    sems = (send_sem, recv_sem)
    local = []
    for index in range(arrays):
        copy = pltpu.make_async_copy(
            own_refs[index], place_of(all_refs[index], own_refs[index], place), local_sem.at[index]
        )
        copy.start()
        local.append(copy)
    waiting = []
    copies = [None] * (2 * arrays)
    for step in range(steps):
        for index in range(arrays):
            extent = own_refs[index].shape
            for flow, chunk, device in (
                (0, place - step, right),
                (1, place + step, left),
            ):
                at = 2 * index + flow
                if step:
                    copies[at].wait_recv()
                chunk = lax.rem(chunk + count, count)
                target = place_of(all_refs[index], own_refs[index], chunk)
                source = target if step else own_refs[index]
                if step == steps - 1:
                    part = half_of(extent, flow)
                    source = source.at[part]
                    target = target.at[part]
                copies[at] = send(source, target, sems, at * steps + step, device)
                waiting.append(copies[at])
    for copy in copies:
        copy.wait_recv()
    for copy in waiting:
        copy.wait_send()
    for copy in local:
        copy.wait()


def spread(arrays, collective_id, columns=False, space=pl.ANY):
    count = lax.axis_size("head")
    shapes = [(a.shape[0], count * a.shape[1]) if columns else (count, *a.shape) for a in arrays]
    slots = len(arrays) * count
    return pl.pallas_call(
        functools.partial(spread_kernel, count, len(arrays)),
        out_shape=[jax.ShapeDtypeStruct(shape, a.dtype) for shape, a in zip(shapes, arrays)],
        in_specs=[pl.BlockSpec(memory_space=space)] * len(arrays),
        out_specs=[pl.BlockSpec(memory_space=space)] * len(arrays),
        scratch_shapes=[
            pltpu.SemaphoreType.DMA((slots,)),
            pltpu.SemaphoreType.DMA((slots,)),
            pltpu.SemaphoreType.DMA((len(arrays),)),
        ],
        compiler_params=pltpu.CompilerParams(
            collective_id=collective_id, has_side_effects=True, vmem_limit_bytes=VMEM_LIMIT
        ),
        name=f"spread_{collective_id}",
    )(*arrays)


def mlp_kernel(
    count, x_hbm, a_hbm, dy_hbm, gain_ref, out_w, gate_w, up_w, down_w,
    n2_hbm, hid_hbm, grad_hbm, mlp_hbm, dn2_ref, h1_ref,
    x_s, a_s, dy_s, n2_s, hid_s, grad_s, mlp_s, h1_s,
    right_part, left_part, right_got, left_got,
    in_sem, out_sem, send_sem, recv_sem,
):
    steps = count // 2
    rows = x_hbm.shape[0] // count
    width = x_hbm.shape[1]
    hidden = gate_w.shape[1]
    side = width // 2
    tile = 256
    inner = 256 if hidden % 256 == 0 else 128
    place, right, left = ring_setup(count)
    greet((right, left))

    def owners(group):
        first = jnp.where(group == 0, 1, 0)
        one = lax.rem(place + steps - group, count)
        two = lax.rem(place - steps + group + first * steps + count, count)
        return one, two

    def span(owner):
        return pl.ds(pl.multiple_of(owner * rows, rows), rows)

    def loads(group, slot):
        return [
            pltpu.make_async_copy(
                source.at[span(owner)],
                target.at[slot, pl.ds(at * rows, rows)],
                in_sem.at[slot, 2 * index + at],
            )
            for index, (source, target) in enumerate(((x_hbm, x_s), (a_hbm, a_s), (dy_hbm, dy_s)))
            for at, owner in enumerate(owners(group))
        ]

    def stores(group, slot):
        return [
            pltpu.make_async_copy(
                source.at[slot, pl.ds(at * rows, rows)],
                target.at[span(owner)],
                out_sem.at[slot, 2 * index + at],
            )
            for index, (source, target) in enumerate(
                ((n2_s, n2_hbm), (hid_s, hid_hbm), (grad_s, grad_hbm), (mlp_s, mlp_hbm))
            )
            for at, owner in enumerate(owners(group))
        ]

    def passing(source, target, flow, step, device):
        return pltpu.make_async_remote_copy(
            src_ref=source,
            dst_ref=target,
            send_sem=send_sem.at[flow * steps + step],
            recv_sem=recv_sem.at[flow * steps + step],
            device_id=device,
            device_id_type=MESH,
        )

    def first_copies():
        ahead, behind = pl.ds(0, side), pl.ds(side, side)
        return (
            passing(right_part.at[0, :, ahead], right_got.at[0, :, ahead], 0, 0, right),
            passing(right_part.at[0, :, behind], left_got.at[0, :, behind], 1, 0, left),
        )

    def later_copies(step):
        return (
            passing(right_part.at[step], right_got.at[step], 0, step, right),
            passing(left_part.at[step], left_got.at[step], 1, step, left),
        )

    for copy in loads(0, 0):
        copy.start()

    @pl.loop(0, steps)
    def _(group):
        slot = lax.rem(group, 2)
        for copy in loads(group, slot):
            copy.wait()

        @pl.when(group + 1 < steps)
        def _():
            for copy in loads(group + 1, 1 - slot):
                copy.start()

        @pl.when(group >= 2)
        def _():
            for copy in stores(group - 2, slot):
                copy.wait()

        mixed = a_s[slot]

        def residual(at, total):
            cols = pl.ds(pl.multiple_of(at * tile, tile), tile)
            values = x_s[slot, :, cols].astype(F32) + matmul(mixed, out_w[:, cols])
            h1_s[:, cols] = values
            return total + jnp.sum(values * values, axis=1, keepdims=True)

        total = lax.fori_loop(0, width // tile, residual, jnp.zeros((2 * rows, 1), F32))
        scale = lax.rsqrt(total / width + EPSILON)

        @pl.when(group == 0)
        def _():
            h1_ref[...] = h1_s[pl.ds(rows, rows)]

        @pl.loop(0, width // tile)
        def _(at):
            cols = pl.ds(pl.multiple_of(at * tile, tile), tile)
            n2_s[slot, :, cols] = (h1_s[:, cols] * scale * gain_ref[:, cols]).astype(BF)

        normed = n2_s[slot]
        dy = dy_s[slot]

        @pl.loop(0, hidden // inner)
        def _(at):
            cols = pl.ds(pl.multiple_of(at * inner, inner), inner)
            cols_up = pl.ds(pl.multiple_of(hidden + at * inner, inner), inner)
            gate = matmul(normed, gate_w[:, cols])
            up = matmul(normed, up_w[:, cols])
            d_hidden = cols_inner(dy, down_w[cols])
            sig = jax.nn.sigmoid(gate)
            silu = gate * sig
            hid_s[slot, :, cols] = (silu * up).astype(BF)
            grad_s[slot, :, cols] = (d_hidden * up * sig * (1.0 + gate * (1.0 - sig))).astype(BF)
            grad_s[slot, :, cols_up] = (d_hidden * silu).astype(BF)

        hid = hid_s[slot]
        d_gate = grad_s[slot, :, :hidden]
        d_up = grad_s[slot, :, hidden:]

        @pl.loop(0, width // tile)
        def _(at):
            cols = pl.ds(pl.multiple_of(at * tile, tile), tile)
            part = (cols_inner(d_gate, gate_w[cols]) + cols_inner(d_up, up_w[cols])).astype(BF)
            right_part[group, :, cols] = part[:rows]
            left_part[group, :, cols] = part[rows:]
            mlp_s[slot, :, cols] = matmul(hid, down_w[:, cols]).astype(BF)

        for copy in stores(group, slot):
            copy.start()

        @pl.when(group == 0)
        def _():
            for copy in first_copies():
                copy.start()

        @pl.when(group == 1)
        def _():
            one, two = first_copies()
            one.wait_recv()
            two.wait_recv()
            ahead, behind = pl.ds(0, side), pl.ds(side, side)
            right_part[1, :, ahead] = add_low(right_part[1, :, ahead], right_got[0, :, ahead])
            left_part[1, :, behind] = add_low(left_part[1, :, behind], left_got[0, :, behind])

        @pl.when(group >= 2)
        def _():
            one, two = later_copies(group - 1)
            one.wait_recv()
            right_part[group] = add_low(right_part[group], right_got[group - 1])
            two.wait_recv()
            left_part[group] = add_low(left_part[group], left_got[group - 1])

        @pl.when(group >= 1)
        def _():
            for copy in later_copies(group):
                copy.start()

    for copy in later_copies(steps - 1):
        copy.wait_recv()
    dn2_ref[...] = (
        left_part[0].astype(F32) + right_got[steps - 1].astype(F32) + left_got[steps - 1].astype(F32)
    )
    for copy in first_copies():
        copy.wait_send()
    for step in range(1, steps):
        for copy in later_copies(step):
            copy.wait_send()
    for group in range(max(steps - 2, 0), steps):
        for copy in stores(group, group % 2):
            copy.wait()


def mlp_back(tokens, mixed, dy, gain, out_w, gate_w, up_w, down_w, collective_id):
    count = lax.axis_size("head")
    total, width = tokens.shape
    hidden = gate_w.shape[1]
    rows, steps = total // count, count // 2
    vmem = pl.BlockSpec(memory_space=pltpu.VMEM)
    hbm = pl.BlockSpec(memory_space=pl.ANY)

    def slots(wide, dtype=BF):
        return pltpu.VMEM((2, 2 * rows, wide), dtype)

    part = pltpu.VMEM((steps, rows, width), BF)
    flops = 2 * total * width * (mixed.shape[1] + 6 * hidden)
    return pl.pallas_call(
        functools.partial(mlp_kernel, count),
        out_shape=[
            jax.ShapeDtypeStruct((total, width), BF),
            jax.ShapeDtypeStruct((total, hidden), BF),
            jax.ShapeDtypeStruct((total, 2 * hidden), BF),
            jax.ShapeDtypeStruct((total, width), BF),
            jax.ShapeDtypeStruct((rows, width), F32),
            jax.ShapeDtypeStruct((rows, width), F32),
        ],
        in_specs=[hbm] * 3 + [vmem] * 5,
        out_specs=[hbm] * 4 + [vmem] * 2,
        scratch_shapes=[
            slots(width), slots(mixed.shape[1]), slots(width), slots(width), slots(hidden),
            slots(2 * hidden), slots(width), pltpu.VMEM((2 * rows, width), F32),
            part, part, part, part,
            pltpu.SemaphoreType.DMA((2, 6)), pltpu.SemaphoreType.DMA((2, 8)),
            pltpu.SemaphoreType.DMA((count,)), pltpu.SemaphoreType.DMA((count,)),
        ],
        compiler_params=pltpu.CompilerParams(
            collective_id=collective_id, has_side_effects=True, vmem_limit_bytes=VMEM_LIMIT
        ),
        cost_estimate=pl.CostEstimate(flops=flops, bytes_accessed=40 << 20, transcendentals=0),
        name="mlp_back",
    )(tokens, mixed, dy, gain, out_w, gate_w, up_w, down_w)


KEY_BLOCK = 512
QUERY_BLOCK = 256


def key_range(start_ref, base, query_block):
    first = query_block * QUERY_BLOCK
    lowest = start_ref[first]
    highest = start_ref[first + QUERY_BLOCK - 1]
    begin = lowest // KEY_BLOCK
    end = (base + first + QUERY_BLOCK - 1) // KEY_BLOCK + 1
    full_begin = jnp.minimum((highest + KEY_BLOCK - 1) // KEY_BLOCK, end)
    full_end = jnp.maximum((base + first + 1) // KEY_BLOCK, full_begin)
    return begin, full_begin, full_end, end


def allowed_pairs(key_block, start_row, base_row):
    shape = (KEY_BLOCK, QUERY_BLOCK)
    key_pos = key_block * KEY_BLOCK + lax.broadcasted_iota(jnp.int32, shape, 0)
    query_pos = base_row + lax.broadcasted_iota(jnp.int32, shape, 1)
    return (key_pos >= start_row) & (key_pos <= query_pos)


def attend_kernel(
    scale, start_sm, base_sm, q_ref, kv_ref, start_ref, logit_ref, o_ref, a_ref, lse_ref
):
    base = base_sm[0]
    size = q_ref.shape[1]
    factor = scale * math.log2(math.e)

    @pl.loop(0, q_ref.shape[0] // QUERY_BLOCK)
    def _(block):
        rows = pl.ds(pl.multiple_of(block * QUERY_BLOCK, QUERY_BLOCK), QUERY_BLOCK)
        queries = q_ref[rows]
        start_row = start_ref[:, rows]
        begin, full_begin, full_end, end = key_range(start_sm, base, block)

        def step(masked, at, state):
            old_max, old_sum, total = state
            keys = pl.ds(pl.multiple_of(at * KEY_BLOCK, KEY_BLOCK), KEY_BLOCK)
            scores = cols_inner(kv_ref[keys, :size], queries)
            if masked:
                allowed = allowed_pairs(at, start_row, base + block * QUERY_BLOCK)
                scores = jnp.where(allowed, scores, MASKED)
            new_max = jnp.maximum(old_max, jnp.max(scores, axis=0, keepdims=True))
            keep = jnp.exp2((old_max - new_max) * factor)
            weights = jnp.exp2(scores * factor - new_max * factor)
            new_sum = old_sum * keep + jnp.sum(weights, axis=0, keepdims=True)
            total = total * keep + rows_inner(kv_ref[keys, size:], weights.astype(BF))
            return new_max, new_sum, total

        state = (
            jnp.full((1, QUERY_BLOCK), MASKED, F32),
            jnp.zeros((1, QUERY_BLOCK), F32),
            jnp.zeros((size, QUERY_BLOCK), F32),
        )
        state = lax.fori_loop(begin, full_begin, functools.partial(step, True), state)
        state = lax.fori_loop(full_begin, full_end, functools.partial(step, False), state)
        state = lax.fori_loop(full_end, end, functools.partial(step, True), state)
        run_max, run_sum, total = state
        lse_ref[:, rows] = run_max * factor + jnp.log2(run_sum)
        attended = (total / run_sum).T
        o_ref[rows] = attended
        a_ref[rows] = (attended * jax.nn.sigmoid(logit_ref[rows])).astype(BF)


def attend_back_kernel(
    scale, start_sm, base_sm, q_ref, kv_ref, start_ref, logit_ref, o_ref, da_ref, lse_ref,
    dq_ref, dg_ref, dkv_ref, dk_acc, dv_acc,
):
    base = base_sm[0]
    size = q_ref.shape[1]
    factor = scale * math.log2(math.e)
    dk_acc[...] = jnp.zeros_like(dk_acc)
    dv_acc[...] = jnp.zeros_like(dv_acc)

    @pl.loop(0, q_ref.shape[0] // QUERY_BLOCK)
    def _(block):
        rows = pl.ds(pl.multiple_of(block * QUERY_BLOCK, QUERY_BLOCK), QUERY_BLOCK)
        queries = q_ref[rows]
        start_row = start_ref[:, rows]
        lse = lse_ref[:, rows]
        gate = jax.nn.sigmoid(logit_ref[rows])
        attended = o_ref[rows]
        d_mixed = da_ref[rows].astype(F32)
        d_attended = (d_mixed * gate).astype(BF)
        dg_ref[rows] = (d_mixed * attended * gate * (1.0 - gate)).astype(BF)
        delta = jnp.sum((d_attended.astype(F32) * attended).T, axis=0, keepdims=True)
        begin, full_begin, full_end, end = key_range(start_sm, base, block)

        def step(masked, at, d_queries):
            keys = pl.ds(pl.multiple_of(at * KEY_BLOCK, KEY_BLOCK), KEY_BLOCK)
            key_block = kv_ref[keys, :size]
            probs = jnp.exp2(cols_inner(key_block, queries) * factor - lse)
            if masked:
                allowed = allowed_pairs(at, start_row, base + block * QUERY_BLOCK)
                probs = jnp.where(allowed, probs, 0.0)
            d_probs = cols_inner(kv_ref[keys, size:], d_attended)
            d_scores = (probs * (d_probs - delta) * scale).astype(BF)
            dv_acc[keys] += matmul(probs.astype(BF), d_attended)
            dk_acc[keys] += matmul(d_scores, queries)
            return d_queries + rows_inner(key_block, d_scores)

        d_queries = jnp.zeros((size, QUERY_BLOCK), F32)
        d_queries = lax.fori_loop(begin, full_begin, functools.partial(step, True), d_queries)
        d_queries = lax.fori_loop(full_begin, full_end, functools.partial(step, False), d_queries)
        d_queries = lax.fori_loop(full_end, end, functools.partial(step, True), d_queries)
        dq_ref[rows] = d_queries.T.astype(BF)

    @pl.loop(0, kv_ref.shape[0] // KEY_BLOCK)
    def _(at):
        keys = pl.ds(pl.multiple_of(at * KEY_BLOCK, KEY_BLOCK), KEY_BLOCK)
        dkv_ref[keys, :size] = dk_acc[keys].astype(BF)
        dkv_ref[keys, size:] = dv_acc[keys].astype(BF)


def local_call(kernel, scalars, arrays, outs, scratch, flops, name):
    vmem = pl.BlockSpec(memory_space=pltpu.VMEM)
    smem = pl.BlockSpec(memory_space=pltpu.SMEM)
    return pl.pallas_call(
        kernel,
        out_shape=outs,
        in_specs=[smem] * len(scalars) + [vmem] * len(arrays),
        out_specs=[vmem] * len(outs),
        scratch_shapes=scratch,
        compiler_params=pltpu.CompilerParams(vmem_limit_bytes=VMEM_LIMIT),
        cost_estimate=pl.CostEstimate(flops=flops, bytes_accessed=8 << 20, transcendentals=0),
        name=name,
    )(*scalars, *arrays)


def ring_routes(count):
    spots = [ring_head(at, count) for at in range(count)]
    right = [(spots[at], spots[(at + 1) % count]) for at in range(count)]
    left = [(spots[at], spots[at - 1]) for at in range(count)]
    return right, left


def add_low(one, other):
    return (one.astype(F32) + other.astype(F32)).astype(BF)


def flow_sum(part):
    count = lax.axis_size("head")
    place = ring_place(lax.axis_index("head"), count)
    right, left = ring_routes(count)
    rows, side = part.shape[0] // count, part.shape[1] // 2
    steps = count // 2

    def mine(owner):
        return lax.dynamic_slice_in_dim(part, lax.rem(owner + count, count) * rows, rows, 0)

    far = mine(place + steps)
    for step in range(steps):
        if step == 0:
            going, coming = far[:, :side], far[:, side:]
        from_left = lax.ppermute(going, "head", right)
        from_right = lax.ppermute(coming, "head", left)
        if step == steps - 1:
            break
        one, two = mine(place + steps - 1 - step), mine(place - steps + 1 + step)
        if step == 0:
            going = jnp.concatenate([add_low(from_left, one[:, :side]), one[:, side:]], 1)
            coming = jnp.concatenate([two[:, :side], add_low(from_right, two[:, side:])], 1)
        else:
            going, coming = add_low(from_left, one), add_low(from_right, two)
    return mine(place).astype(F32) + from_left.astype(F32) + from_right.astype(F32)


def flow_spread(own):
    count = lax.axis_size("head")
    place = ring_place(lax.axis_index("head"), count)
    right, left = ring_routes(count)
    side = own.shape[1] // 2
    going = coming = own
    pieces = [(0, own)]
    for step in range(1, count // 2):
        going = lax.ppermute(going, "head", right)
        coming = lax.ppermute(coming, "head", left)
        pieces += [(-step, going), (step, coming)]
    one = lax.ppermute(going[:, :side], "head", right)
    two = lax.ppermute(coming[:, side:], "head", left)
    pieces.append((count // 2, jnp.concatenate([one, two], 1)))
    whole = jnp.zeros((count * own.shape[0], own.shape[1]), own.dtype)
    for shift, piece in pieces:
        at = lax.rem(place + shift + count, count) * own.shape[0]
        whole = lax.dynamic_update_slice_in_dim(whole, piece, at, 0)
    return whole


def swap(block, axis, stride):
    return lax.ppermute(block, axis, [(at, at ^ stride) for at in range(lax.axis_size(axis))])


def halve_batch(block, rows):
    me = lax.axis_index("batch")
    stride = 1
    while stride < lax.axis_size("batch"):
        block = block.reshape(-1, 2, rows, block.shape[-1])
        bit = (me // stride) % 2
        keep = lax.dynamic_index_in_dim(block, bit, 1, keepdims=False)
        give = lax.dynamic_index_in_dim(block, 1 - bit, 1, keepdims=False)
        got = swap(give, "batch", stride)
        block = (keep.astype(F32) + got.astype(F32)).astype(block.dtype)
        stride *= 2
    return block.reshape(rows, -1)


def sum_heads(block):
    stride = 1
    while stride < lax.axis_size("head"):
        block = block + swap(block, "head", stride)
        stride *= 2
    return block


def from_partner(block, axis):
    count = lax.axis_size(axis)
    route = [(at, at ^ 1) for at in range(count)]
    return lax.ppermute(block, axis, route)


def matmul(left, right):
    return jnp.dot(left, right, preferred_element_type=F32)


def rows_inner(left, right):
    return lax.dot_general(left, right, (((0,), (0,)), ((), ())), preferred_element_type=F32)


def cols_inner(left, right):
    return lax.dot_general(left, right, (((1,), (1,)), ((), ())), preferred_element_type=F32)


def rms_scale(values):
    return lax.rsqrt(jnp.mean(values * values, axis=1, keepdims=True) + EPSILON)


def order_halves(own, mate, first):
    return jnp.where(first, jnp.concatenate([own, mate], 1), jnp.concatenate([mate, own], 1))


def per_device(
    tokens,
    segment_ids,
    norm1_gain,
    w_query,
    w_key,
    w_value,
    w_gate,
    w_out,
    norm2_gain,
    w_mlp_gate,
    w_mlp_up,
    w_down,
    out_grad,
):
    heads = lax.axis_size("head")
    batches = lax.axis_size("batch")
    row_count, width = tokens.shape
    head_size = w_query.shape[1]
    half = w_key.shape[1]
    chunk = row_count // heads
    first = lax.axis_index("head") % 2 == 0
    me = ring_place(lax.axis_index("head"), heads)
    scale_factor = 1.0 / math.sqrt(head_size)

    kv_shard = jnp.concatenate([w_key, w_value], axis=1)
    kv_mate = from_partner(kv_shard, "head")
    w_in = jnp.concatenate(
        [
            w_query,
            order_halves(w_key, kv_mate[:, :half], first),
            order_halves(w_value, kv_mate[:, half:], first),
            w_gate,
        ],
        axis=1,
    )
    w_in = lax.all_gather(w_in, "batch", axis=0, tiled=True)
    gains = lax.all_gather(jnp.stack([norm1_gain, norm2_gain]), "batch", axis=1, tiled=True)
    gain_one = gains[0].astype(F32)
    gain_two = gains[1].astype(F32)
    (out_rows,) = spread([w_out], 1)
    out_full = lax.all_gather(out_rows.reshape(heads * head_size, -1), "batch", axis=1, tiled=True)
    mgate_full = lax.all_gather(w_mlp_gate, "batch", axis=0, tiled=True)
    mup_full = lax.all_gather(w_mlp_up, "batch", axis=0, tiled=True)
    down_full = lax.all_gather(w_down, "batch", axis=1, tiled=True)

    inputs = tokens.astype(F32)
    recip_one = rms_scale(inputs)
    normed_one = (inputs * recip_one * gain_one).astype(BF)
    projected = matmul(normed_one, w_in)
    queries = projected[:, :head_size].astype(BF)
    kv_local = projected[:, head_size : 3 * head_size].astype(BF)
    gate_logit = projected[:, 3 * head_size :]
    kv_all = lax.all_gather(kv_local, "batch", axis=0, tiled=True)
    seg_all = lax.all_gather(segment_ids, "batch", axis=0, tiled=True)
    base = lax.axis_index("batch") * row_count
    ids = jnp.arange(DOCUMENTS, dtype=jnp.int32)
    below = jnp.sum((seg_all[None, :] < ids[:, None]).astype(jnp.int32), axis=1)
    starts = jnp.sum(jnp.where(segment_ids[None, :] == ids[:, None], below[:, None], 0), axis=0)
    scalars = (starts, base.reshape(1))
    pair_flops = 4 * row_count * kv_all.shape[0] * head_size
    attended, mixed, lse = local_call(
        functools.partial(attend_kernel, scale_factor),
        scalars,
        (queries, kv_all, starts[None], gate_logit),
        [
            jax.ShapeDtypeStruct((row_count, head_size), F32),
            jax.ShapeDtypeStruct((row_count, head_size), BF),
            jax.ShapeDtypeStruct((1, row_count), F32),
        ],
        [],
        pair_flops,
        "attend",
    )
    (mixed_all,) = spread([mixed], 2, columns=True)
    normed_two, hidden, d_pre, mlp_part, dn2, resid_own = mlp_back(
        tokens, mixed_all, out_grad, gain_two[None], out_full, mgate_full, mup_full, down_full, 3
    )
    recip_own = rms_scale(resid_own)
    mixed_own = lax.dynamic_slice_in_dim(mixed_all, me * chunk, chunk, 0)
    dy_own = lax.dynamic_slice_in_dim(out_grad, me * chunk, chunk, 0).astype(F32)
    output = flow_spread((resid_own + flow_sum(mlp_part)).astype(BF))

    d_gain_two = jnp.sum(dn2 * resid_own * recip_own, axis=0)
    weighted_two = gain_two * dn2
    d_resid = (
        dy_own
        + recip_own * weighted_two
        - resid_own * recip_own**3 * jnp.mean(weighted_two * resid_own, axis=1, keepdims=True)
    )
    d_resid_low = d_resid.astype(BF)
    d_mixed_all = cols_inner(d_resid_low, out_full).astype(BF)
    d_mixed_all = d_mixed_all.reshape(chunk, heads, head_size)
    places = [ring_place(at, heads) for at in range(heads)]
    d_mixed_all = jnp.stack([d_mixed_all[:, at] for at in places], axis=0)
    d_mixed = lax.all_to_all(d_mixed_all, "head", split_axis=0, concat_axis=0, tiled=True)
    d_mixed = jnp.concatenate([d_mixed[ring_head(at, heads)] for at in range(heads)], axis=0)
    d_out_part = rows_inner(mixed_own, d_resid_low).astype(BF)
    d_out_part = lax.psum_scatter(d_out_part, "batch", scatter_dimension=1, tiled=True)
    d_out = flow_sum(d_out_part)

    d_queries, d_gate_logit, d_kv_all = local_call(
        functools.partial(attend_back_kernel, scale_factor),
        scalars,
        (queries, kv_all, starts[None], gate_logit, attended, d_mixed, lse),
        [
            jax.ShapeDtypeStruct((row_count, head_size), BF),
            jax.ShapeDtypeStruct((row_count, head_size), BF),
            jax.ShapeDtypeStruct(kv_all.shape, BF),
        ],
        [pltpu.VMEM((kv_all.shape[0], head_size), F32)] * 2,
        5 * pair_flops // 2,
        "attend_back",
    )
    d_kv_own = halve_batch(d_kv_all, row_count)
    d_kv_mate = from_partner(d_kv_own, "head")
    d_kv = (d_kv_own.astype(F32) + d_kv_mate.astype(F32)).astype(BF)
    d_cat = jnp.concatenate(
        [
            d_queries,
            jnp.where(first, d_kv[:, :half], d_kv[:, half:head_size]),
            jnp.where(first, d_kv[:, head_size : head_size + half], d_kv[:, head_size + half :]),
            d_gate_logit,
        ],
        axis=1,
    )
    w_key_own = jnp.where(
        first, w_in[:, head_size : head_size + half], w_in[:, head_size + half : 2 * head_size]
    )
    w_value_own = jnp.where(
        first, w_in[:, 2 * head_size : 2 * head_size + half], w_in[:, 2 * head_size + half : 3 * head_size]
    )
    w_cat = jnp.concatenate(
        [w_in[:, :head_size], w_key_own, w_value_own, w_in[:, 3 * head_size :]], axis=1
    )
    dn1_part = cols_inner(d_cat, w_cat).astype(BF)
    dn1 = flow_sum(dn1_part)
    inputs_own = lax.dynamic_slice_in_dim(inputs, me * chunk, chunk, 0)
    recip_in = lax.dynamic_slice_in_dim(recip_one, me * chunk, chunk, 0)
    d_gain_one = jnp.sum(dn1 * inputs_own * recip_in, axis=0)
    weighted_one = gain_one * dn1
    d_tokens = (
        d_resid
        + recip_in * weighted_one
        - inputs_own * recip_in**3 * jnp.mean(weighted_one * inputs_own, axis=1, keepdims=True)
    ).astype(BF)
    d_tokens = flow_spread(d_tokens)

    d_mlp = rows_inner(normed_two, d_pre).astype(BF)
    d_mlp = lax.psum_scatter(d_mlp, "batch", scatter_dimension=0, tiled=True).astype(F32)
    d_down = rows_inner(hidden, out_grad).astype(BF)
    d_down = lax.psum_scatter(d_down, "batch", scatter_dimension=1, tiled=True).astype(F32)
    d_in = rows_inner(normed_one, d_cat).astype(BF)
    d_in = lax.psum_scatter(d_in, "batch", scatter_dimension=0, tiled=True).astype(F32)
    d_gains = jnp.stack([d_gain_one, d_gain_two]).reshape(2, batches, -1).transpose(1, 0, 2)
    d_gains = sum_heads(halve_batch(d_gains.reshape(2 * batches, -1), 2))
    hidden_own = w_mlp_gate.shape[1]
    return (
        output,
        d_tokens,
        d_gains[0],
        d_in[:, :head_size],
        d_in[:, head_size : head_size + half],
        d_in[:, head_size + half : 2 * head_size],
        d_in[:, 2 * head_size :],
        d_out,
        d_gains[1],
        d_mlp[:, :hidden_own],
        d_mlp[:, hidden_own:],
        d_down,
    )


def solution(mesh):
    return jax.shard_map(
        per_device,
        mesh=mesh,
        in_specs=(
            P("batch", None),
            P("batch"),
            P("batch"),
            P("batch", "head"),
            P("batch", "head"),
            P("batch", "head"),
            P("batch", "head"),
            P("head", "batch"),
            P("batch"),
            P("batch", "head"),
            P("batch", "head"),
            P("head", "batch"),
            P("batch", None),
        ),
        out_specs=(
            P("batch", None),
            P("batch", None),
            P("batch"),
            P("batch", "head"),
            P("batch", "head"),
            P("batch", "head"),
            P("batch", "head"),
            P("head", "batch"),
            P("batch"),
            P("batch", "head"),
            P("batch", "head"),
            P("head", "batch"),
        ),
        check_vma=False,
    )
```

```python
import functools
import math

import jax
import jax.numpy as jnp
from jax import lax
from jax.experimental import pallas as pl
from jax.experimental.pallas import tpu as pltpu
from jax.sharding import PartitionSpec as P

EPSILON = 1e-06
MASKED = -1e30
DOCUMENTS = 7
BF = jnp.bfloat16
F32 = jnp.float32


MESH = pl.DeviceIdType.MESH
VMEM_LIMIT = 60 << 20


def ring_place(head, count):
    high, low = head // 2, head % 2
    return (1 - low) * high + low * (count - 1 - high)


def ring_head(place, count):
    low = place // (count // 2)
    high = (1 - low) * place + low * (count - 1 - place)
    return 2 * high + low


def ring_setup(count):
    batch = lax.axis_index("batch")
    place = ring_place(lax.axis_index("head"), count)
    right = (batch, ring_head(lax.rem(place + 1, count), count))
    left = (batch, ring_head(lax.rem(place + count - 1, count), count))
    return place, right, left


def greet(devices):
    barrier = pltpu.get_barrier_semaphore()
    for device in devices:
        pl.semaphore_signal(barrier, inc=1, device_id=device, device_id_type=MESH)
    pl.semaphore_wait(barrier, len(devices))


def send(source, target, sems, slot, device):
    copy = pltpu.make_async_remote_copy(
        src_ref=source,
        dst_ref=target,
        send_sem=sems[0].at[slot],
        recv_sem=sems[1].at[slot],
        device_id=device,
        device_id_type=MESH,
    )
    copy.start()
    return copy


def half_of(extent, flow):
    if extent[1] % 256:
        return (pl.ds(flow * (extent[0] // 2), extent[0] // 2), slice(None))
    return (slice(None), pl.ds(flow * (extent[1] // 2), extent[1] // 2))


def place_of(whole, own, chunk, form):
    rows, wide = own.shape[-2:]
    if form == "lead":
        return whole.at[chunk]
    if form == "rows":
        return whole.at[pl.ds(pl.multiple_of(chunk * rows, rows), rows)]
    return whole.at[:, pl.ds(pl.multiple_of(chunk * wide, wide), wide)]


def spread_kernel(count, batches, plans, *refs):
    steps = count // 2
    arrays = len(plans)
    own_refs, all_refs = refs[:arrays], refs[arrays : 2 * arrays]
    send_sem, recv_sem, local_sem = refs[2 * arrays :]
    place, right, left = ring_setup(count)
    head = lax.axis_index("head")
    batch = lax.axis_index("batch")
    across, core = batch // 2, lax.rem(batch, 2)
    others = batches // 2
    twin = (across * 2 + 1 - core, head)
    peers = [(lax.rem(across + hop, others) * 2 + core, head) for hop in range(1, others)]
    ring = any(axis == "head" for axis, _ in plans)
    grid = any(axis == "batch" for axis, _ in plans)
    greet((right, left) * ring + (twin, *peers) * grid)
    sems = (send_sem, recv_sem)
    slot = 0
    waiting, arriving, local = [], [], []

    def go(source, target, device):
        nonlocal slot
        copy = send(source, target, sems, slot, device)
        slot += 1
        waiting.append(copy)
        return copy

    onward = []
    for index, (axis, form) in enumerate(plans):
        own, whole = own_refs[index], all_refs[index]
        spot = place if axis == "head" else batch
        mine = place_of(whole, own, spot, form)
        copy = pltpu.make_async_copy(own, mine, local_sem.at[index])
        copy.start()
        local.append(copy)
        if axis == "batch":
            for hop, peer in enumerate(peers, 1):
                source = lax.rem(across + others - hop, others) * 2 + core
                onward.append((go(own, mine, peer), place_of(whole, own, source, form)))
            arriving.append(go(own, mine, twin))
    copies = [None] * (2 * arrays)
    for step in range(steps):
        for index, (axis, form) in enumerate(plans):
            if axis != "head":
                continue
            own = own_refs[index]
            for flow, chunk, device in ((0, place - step, right), (1, place + step, left)):
                at = 2 * index + flow
                if step:
                    copies[at].wait_recv()
                chunk = lax.rem(chunk + count, count)
                target = place_of(all_refs[index], own, chunk, form)
                source = target if step else own
                if step == steps - 1:
                    part = half_of(own.shape, flow)
                    source = source.at[part]
                    target = target.at[part]
                copies[at] = go(source, target, device)
        if step == 0 or not ring:
            for copy, block in onward:
                copy.wait_recv()
                arriving.append(go(block, block, twin))
            onward = []
    for copy in copies:
        if copy is not None:
            arriving.append(copy)
    for copy in arriving:
        copy.wait_recv()
    for copy in waiting:
        copy.wait_send()
    for copy in local:
        copy.wait()


def spread(arrays, plans, collective_id):
    count = lax.axis_size("head")
    batches = lax.axis_size("batch")
    shapes = []
    slots = 0
    for array, (axis, form) in zip(arrays, plans):
        many = count if axis == "head" else batches
        slots += count if axis == "head" else batches - 1
        if form == "lead":
            shapes.append((many, *array.shape))
        elif form == "rows":
            shapes.append((many * array.shape[0], array.shape[1]))
        else:
            shapes.append((array.shape[0], many * array.shape[1]))
    hbm = pl.BlockSpec(memory_space=pl.ANY)
    return pl.pallas_call(
        functools.partial(spread_kernel, count, batches, plans),
        out_shape=[jax.ShapeDtypeStruct(shape, a.dtype) for shape, a in zip(shapes, arrays)],
        in_specs=[hbm] * len(arrays),
        out_specs=[hbm] * len(arrays),
        scratch_shapes=[
            pltpu.SemaphoreType.DMA((slots,)),
            pltpu.SemaphoreType.DMA((slots,)),
            pltpu.SemaphoreType.DMA((len(arrays),)),
        ],
        compiler_params=pltpu.CompilerParams(
            collective_id=collective_id, has_side_effects=True, vmem_limit_bytes=VMEM_LIMIT
        ),
        name=f"spread_{collective_id}",
    )(*arrays)


def mlp_kernel(
    count, x_hbm, a_hbm, dy_hbm, gain_ref, out_w, gate_w, up_w, down_w,
    n2_hbm, hid_hbm, grad_hbm, mlp_hbm, dn2_ref, h1_ref,
    x_s, a_s, dy_s, n2_s, hid_s, grad_s, mlp_s, h1_s,
    right_part, left_part, right_got, left_got,
    in_sem, out_sem, send_sem, recv_sem,
):
    steps = count // 2
    rows = x_hbm.shape[0] // count
    width = x_hbm.shape[1]
    hidden = gate_w.shape[1]
    side = width // 2
    tile = 256
    inner = 256 if hidden % 256 == 0 else 128
    place, right, left = ring_setup(count)
    greet((right, left))

    def owners(group):
        first = jnp.where(group == 0, 1, 0)
        one = lax.rem(place + steps - group, count)
        two = lax.rem(place - steps + group + first * steps + count, count)
        return one, two

    def span(owner):
        return pl.ds(pl.multiple_of(owner * rows, rows), rows)

    def loads(group, slot):
        return [
            pltpu.make_async_copy(
                source.at[span(owner)],
                target.at[slot, pl.ds(at * rows, rows)],
                in_sem.at[slot, 2 * index + at],
            )
            for index, (source, target) in enumerate(((x_hbm, x_s), (a_hbm, a_s), (dy_hbm, dy_s)))
            for at, owner in enumerate(owners(group))
        ]

    def stores(group, slot):
        return [
            pltpu.make_async_copy(
                source.at[slot, pl.ds(at * rows, rows)],
                target.at[span(owner)],
                out_sem.at[slot, 2 * index + at],
            )
            for index, (source, target) in enumerate(
                ((n2_s, n2_hbm), (hid_s, hid_hbm), (grad_s, grad_hbm), (mlp_s, mlp_hbm))
            )
            for at, owner in enumerate(owners(group))
        ]

    def passing(source, target, flow, step, device):
        return pltpu.make_async_remote_copy(
            src_ref=source,
            dst_ref=target,
            send_sem=send_sem.at[flow * steps + step],
            recv_sem=recv_sem.at[flow * steps + step],
            device_id=device,
            device_id_type=MESH,
        )

    def first_copies():
        ahead, behind = pl.ds(0, side), pl.ds(side, side)
        return (
            passing(right_part.at[0, :, ahead], right_got.at[0, :, ahead], 0, 0, right),
            passing(right_part.at[0, :, behind], left_got.at[0, :, behind], 1, 0, left),
        )

    def later_copies(step):
        return (
            passing(right_part.at[step], right_got.at[step], 0, step, right),
            passing(left_part.at[step], left_got.at[step], 1, step, left),
        )

    for copy in loads(0, 0):
        copy.start()

    @pl.loop(0, steps)
    def _(group):
        slot = lax.rem(group, 2)
        for copy in loads(group, slot):
            copy.wait()

        @pl.when(group + 1 < steps)
        def _():
            for copy in loads(group + 1, 1 - slot):
                copy.start()

        @pl.when(group >= 2)
        def _():
            for copy in stores(group - 2, slot):
                copy.wait()

        mixed = a_s[slot]

        def residual(at, total):
            cols = pl.ds(pl.multiple_of(at * tile, tile), tile)
            values = x_s[slot, :, cols].astype(F32) + matmul(mixed, out_w[:, cols])
            h1_s[:, cols] = values
            return total + jnp.sum(values * values, axis=1, keepdims=True)

        total = lax.fori_loop(0, width // tile, residual, jnp.zeros((2 * rows, 1), F32))
        scale = lax.rsqrt(total / width + EPSILON)

        @pl.when(group == 0)
        def _():
            h1_ref[...] = h1_s[pl.ds(rows, rows)]

        @pl.loop(0, width // tile)
        def _(at):
            cols = pl.ds(pl.multiple_of(at * tile, tile), tile)
            n2_s[slot, :, cols] = (h1_s[:, cols] * scale * gain_ref[:, cols]).astype(BF)

        normed = n2_s[slot]
        dy = dy_s[slot]

        @pl.loop(0, hidden // inner)
        def _(at):
            cols = pl.ds(pl.multiple_of(at * inner, inner), inner)
            cols_up = pl.ds(pl.multiple_of(hidden + at * inner, inner), inner)
            gate = matmul(normed, gate_w[:, cols])
            up = matmul(normed, up_w[:, cols])
            d_hidden = cols_inner(dy, down_w[cols])
            sig = jax.nn.sigmoid(gate)
            silu = gate * sig
            hid_s[slot, :, cols] = (silu * up).astype(BF)
            grad_s[slot, :, cols] = (d_hidden * up * sig * (1.0 + gate * (1.0 - sig))).astype(BF)
            grad_s[slot, :, cols_up] = (d_hidden * silu).astype(BF)

        hid = hid_s[slot]
        d_gate = grad_s[slot, :, :hidden]
        d_up = grad_s[slot, :, hidden:]

        @pl.loop(0, width // tile)
        def _(at):
            cols = pl.ds(pl.multiple_of(at * tile, tile), tile)
            part = (cols_inner(d_gate, gate_w[cols]) + cols_inner(d_up, up_w[cols])).astype(BF)
            right_part[group, :, cols] = part[:rows]
            left_part[group, :, cols] = part[rows:]
            mlp_s[slot, :, cols] = matmul(hid, down_w[:, cols]).astype(BF)

        for copy in stores(group, slot):
            copy.start()

        @pl.when(group == 0)
        def _():
            for copy in first_copies():
                copy.start()

        @pl.when(group == 1)
        def _():
            one, two = first_copies()
            one.wait_recv()
            two.wait_recv()
            ahead, behind = pl.ds(0, side), pl.ds(side, side)
            right_part[1, :, ahead] = add_low(right_part[1, :, ahead], right_got[0, :, ahead])
            left_part[1, :, behind] = add_low(left_part[1, :, behind], left_got[0, :, behind])

        @pl.when(group >= 2)
        def _():
            one, two = later_copies(group - 1)
            one.wait_recv()
            right_part[group] = add_low(right_part[group], right_got[group - 1])
            two.wait_recv()
            left_part[group] = add_low(left_part[group], left_got[group - 1])

        @pl.when(group >= 1)
        def _():
            for copy in later_copies(group):
                copy.start()

    for copy in later_copies(steps - 1):
        copy.wait_recv()
    dn2_ref[...] = (
        left_part[0].astype(F32) + right_got[steps - 1].astype(F32) + left_got[steps - 1].astype(F32)
    )
    for copy in first_copies():
        copy.wait_send()
    for step in range(1, steps):
        for copy in later_copies(step):
            copy.wait_send()
    for group in range(max(steps - 2, 0), steps):
        for copy in stores(group, group % 2):
            copy.wait()


def mlp_back(tokens, mixed, dy, gain, out_w, gate_w, up_w, down_w, collective_id):
    count = lax.axis_size("head")
    total, width = tokens.shape
    hidden = gate_w.shape[1]
    rows, steps = total // count, count // 2
    vmem = pl.BlockSpec(memory_space=pltpu.VMEM)
    hbm = pl.BlockSpec(memory_space=pl.ANY)

    def slots(wide, dtype=BF):
        return pltpu.VMEM((2, 2 * rows, wide), dtype)

    part = pltpu.VMEM((steps, rows, width), BF)
    flops = 2 * total * width * (mixed.shape[1] + 6 * hidden)
    return pl.pallas_call(
        functools.partial(mlp_kernel, count),
        out_shape=[
            jax.ShapeDtypeStruct((total, width), BF),
            jax.ShapeDtypeStruct((total, hidden), BF),
            jax.ShapeDtypeStruct((total, 2 * hidden), BF),
            jax.ShapeDtypeStruct((total, width), BF),
            jax.ShapeDtypeStruct((rows, width), F32),
            jax.ShapeDtypeStruct((rows, width), F32),
        ],
        in_specs=[hbm] * 3 + [vmem] * 5,
        out_specs=[hbm] * 4 + [vmem] * 2,
        scratch_shapes=[
            slots(width), slots(mixed.shape[1]), slots(width), slots(width), slots(hidden),
            slots(2 * hidden), slots(width), pltpu.VMEM((2 * rows, width), F32),
            part, part, part, part,
            pltpu.SemaphoreType.DMA((2, 6)), pltpu.SemaphoreType.DMA((2, 8)),
            pltpu.SemaphoreType.DMA((count,)), pltpu.SemaphoreType.DMA((count,)),
        ],
        compiler_params=pltpu.CompilerParams(
            collective_id=collective_id, has_side_effects=True, vmem_limit_bytes=VMEM_LIMIT
        ),
        cost_estimate=pl.CostEstimate(flops=flops, bytes_accessed=40 << 20, transcendentals=0),
        name="mlp_back",
    )(tokens, mixed, dy, gain, out_w, gate_w, up_w, down_w)


KEY_BLOCK = 512
QUERY_BLOCK = 256


def key_range(start_ref, base, query_block):
    first = query_block * QUERY_BLOCK
    lowest = start_ref[first]
    highest = start_ref[first + QUERY_BLOCK - 1]
    begin = lowest // KEY_BLOCK
    end = (base + first + QUERY_BLOCK - 1) // KEY_BLOCK + 1
    full_begin = jnp.minimum((highest + KEY_BLOCK - 1) // KEY_BLOCK, end)
    full_end = jnp.maximum((base + first + 1) // KEY_BLOCK, full_begin)
    return begin, full_begin, full_end, end


def allowed_pairs(key_block, start_row, base_row):
    shape = (KEY_BLOCK, QUERY_BLOCK)
    key_pos = key_block * KEY_BLOCK + lax.broadcasted_iota(jnp.int32, shape, 0)
    query_pos = base_row + lax.broadcasted_iota(jnp.int32, shape, 1)
    return (key_pos >= start_row) & (key_pos <= query_pos)


def attend_kernel(
    scale, start_sm, base_sm, q_ref, kv_ref, start_ref, logit_ref, o_ref, a_ref, lse_ref
):
    base = base_sm[0]
    size = q_ref.shape[1]
    factor = scale * math.log2(math.e)

    @pl.loop(0, q_ref.shape[0] // QUERY_BLOCK)
    def _(block):
        rows = pl.ds(pl.multiple_of(block * QUERY_BLOCK, QUERY_BLOCK), QUERY_BLOCK)
        queries = q_ref[rows]
        start_row = start_ref[:, rows]
        begin, full_begin, full_end, end = key_range(start_sm, base, block)

        def step(masked, at, state):
            old_max, old_sum, total = state
            keys = pl.ds(pl.multiple_of(at * KEY_BLOCK, KEY_BLOCK), KEY_BLOCK)
            scores = cols_inner(kv_ref[keys, :size], queries)
            if masked:
                allowed = allowed_pairs(at, start_row, base + block * QUERY_BLOCK)
                scores = jnp.where(allowed, scores, MASKED)
            new_max = jnp.maximum(old_max, jnp.max(scores, axis=0, keepdims=True))
            keep = jnp.exp2((old_max - new_max) * factor)
            weights = jnp.exp2(scores * factor - new_max * factor)
            new_sum = old_sum * keep + jnp.sum(weights, axis=0, keepdims=True)
            total = total * keep + rows_inner(kv_ref[keys, size:], weights.astype(BF))
            return new_max, new_sum, total

        state = (
            jnp.full((1, QUERY_BLOCK), MASKED, F32),
            jnp.zeros((1, QUERY_BLOCK), F32),
            jnp.zeros((size, QUERY_BLOCK), F32),
        )
        state = lax.fori_loop(begin, full_begin, functools.partial(step, True), state)
        state = lax.fori_loop(full_begin, full_end, functools.partial(step, False), state)
        state = lax.fori_loop(full_end, end, functools.partial(step, True), state)
        run_max, run_sum, total = state
        lse_ref[:, rows] = run_max * factor + jnp.log2(run_sum)
        attended = (total / run_sum).T
        o_ref[rows] = attended
        a_ref[rows] = (attended * jax.nn.sigmoid(logit_ref[rows])).astype(BF)


def attend_back_kernel(
    scale, start_sm, base_sm, q_ref, kv_ref, start_ref, logit_ref, o_ref, da_ref, lse_ref,
    dq_ref, dg_ref, dkv_ref, dk_acc, dv_acc,
):
    base = base_sm[0]
    size = q_ref.shape[1]
    factor = scale * math.log2(math.e)
    dk_acc[...] = jnp.zeros_like(dk_acc)
    dv_acc[...] = jnp.zeros_like(dv_acc)

    @pl.loop(0, q_ref.shape[0] // QUERY_BLOCK)
    def _(block):
        rows = pl.ds(pl.multiple_of(block * QUERY_BLOCK, QUERY_BLOCK), QUERY_BLOCK)
        queries = q_ref[rows]
        start_row = start_ref[:, rows]
        lse = lse_ref[:, rows]
        gate = jax.nn.sigmoid(logit_ref[rows])
        attended = o_ref[rows]
        d_mixed = da_ref[rows].astype(F32)
        d_attended = (d_mixed * gate).astype(BF)
        dg_ref[rows] = (d_mixed * attended * gate * (1.0 - gate)).astype(BF)
        delta = jnp.sum((d_attended.astype(F32) * attended).T, axis=0, keepdims=True)
        begin, full_begin, full_end, end = key_range(start_sm, base, block)

        def step(masked, at, d_queries):
            keys = pl.ds(pl.multiple_of(at * KEY_BLOCK, KEY_BLOCK), KEY_BLOCK)
            key_block = kv_ref[keys, :size]
            probs = jnp.exp2(cols_inner(key_block, queries) * factor - lse)
            if masked:
                allowed = allowed_pairs(at, start_row, base + block * QUERY_BLOCK)
                probs = jnp.where(allowed, probs, 0.0)
            d_probs = cols_inner(kv_ref[keys, size:], d_attended)
            d_scores = (probs * (d_probs - delta) * scale).astype(BF)
            dv_acc[keys] += matmul(probs.astype(BF), d_attended)
            dk_acc[keys] += matmul(d_scores, queries)
            return d_queries + rows_inner(key_block, d_scores)

        d_queries = jnp.zeros((size, QUERY_BLOCK), F32)
        d_queries = lax.fori_loop(begin, full_begin, functools.partial(step, True), d_queries)
        d_queries = lax.fori_loop(full_begin, full_end, functools.partial(step, False), d_queries)
        d_queries = lax.fori_loop(full_end, end, functools.partial(step, True), d_queries)
        dq_ref[rows] = d_queries.T.astype(BF)

    @pl.loop(0, kv_ref.shape[0] // KEY_BLOCK)
    def _(at):
        keys = pl.ds(pl.multiple_of(at * KEY_BLOCK, KEY_BLOCK), KEY_BLOCK)
        dkv_ref[keys, :size] = dk_acc[keys].astype(BF)
        dkv_ref[keys, size:] = dv_acc[keys].astype(BF)


def local_call(kernel, scalars, arrays, outs, scratch, flops, name):
    vmem = pl.BlockSpec(memory_space=pltpu.VMEM)
    smem = pl.BlockSpec(memory_space=pltpu.SMEM)
    return pl.pallas_call(
        kernel,
        out_shape=outs,
        in_specs=[smem] * len(scalars) + [vmem] * len(arrays),
        out_specs=[vmem] * len(outs),
        scratch_shapes=scratch,
        compiler_params=pltpu.CompilerParams(vmem_limit_bytes=VMEM_LIMIT),
        cost_estimate=pl.CostEstimate(flops=flops, bytes_accessed=8 << 20, transcendentals=0),
        name=name,
    )(*scalars, *arrays)


def ring_routes(count):
    spots = [ring_head(at, count) for at in range(count)]
    right = [(spots[at], spots[(at + 1) % count]) for at in range(count)]
    left = [(spots[at], spots[at - 1]) for at in range(count)]
    return right, left


def add_low(one, other):
    return (one.astype(F32) + other.astype(F32)).astype(BF)


def flow_steps(part):
    count = lax.axis_size("head")
    place = ring_place(lax.axis_index("head"), count)
    right, left = ring_routes(count)
    rows, side = part.shape[0] // count, part.shape[1] // 2
    steps = count // 2

    def mine(owner):
        return lax.dynamic_slice_in_dim(part, lax.rem(owner + count, count) * rows, rows, 0)

    far = mine(place + steps)
    going, coming = far[:, :side], far[:, side:]
    for step in range(steps - 1):
        from_left = lax.ppermute(going, "head", right)
        from_right = lax.ppermute(coming, "head", left)
        one, two = mine(place + steps - 1 - step), mine(place - steps + 1 + step)
        if step == 0:
            going = jnp.concatenate([add_low(from_left, one[:, :side]), one[:, side:]], 1)
            coming = jnp.concatenate([two[:, :side], add_low(from_right, two[:, side:])], 1)
        else:
            going, coming = add_low(from_left, one), add_low(from_right, two)
        going, coming = yield going, coming
    from_left = lax.ppermute(going, "head", right)
    from_right = lax.ppermute(coming, "head", left)
    yield mine(place).astype(F32) + from_left.astype(F32) + from_right.astype(F32)


def flow_sum(part):
    flow = flow_steps(part)
    state = next(flow)
    while isinstance(state, tuple):
        state = flow.send(state)
    return state


def after(flow, state, array):
    array, going, coming = lax.optimization_barrier((array, *state))
    return array, flow.send((going, coming))


def flow_spread(own):
    count = lax.axis_size("head")
    place = ring_place(lax.axis_index("head"), count)
    right, left = ring_routes(count)
    side = own.shape[1] // 2
    going = coming = own
    pieces = [(0, own)]
    for step in range(1, count // 2):
        going = lax.ppermute(going, "head", right)
        coming = lax.ppermute(coming, "head", left)
        pieces += [(-step, going), (step, coming)]
    one = lax.ppermute(going[:, :side], "head", right)
    two = lax.ppermute(coming[:, side:], "head", left)
    pieces.append((count // 2, jnp.concatenate([one, two], 1)))
    whole = jnp.zeros((count * own.shape[0], own.shape[1]), own.dtype)
    for shift, piece in pieces:
        at = lax.rem(place + shift + count, count) * own.shape[0]
        whole = lax.dynamic_update_slice_in_dim(whole, piece, at, 0)
    return whole


def swap(block, axis, stride):
    return lax.ppermute(block, axis, [(at, at ^ stride) for at in range(lax.axis_size(axis))])


def halve_batch(block, rows):
    me = lax.axis_index("batch")
    stride = 1
    while stride < lax.axis_size("batch"):
        block = block.reshape(-1, 2, rows, block.shape[-1])
        bit = (me // stride) % 2
        keep = lax.dynamic_index_in_dim(block, bit, 1, keepdims=False)
        give = lax.dynamic_index_in_dim(block, 1 - bit, 1, keepdims=False)
        got = swap(give, "batch", stride)
        block = (keep.astype(F32) + got.astype(F32)).astype(block.dtype)
        stride *= 2
    return block.reshape(rows, -1)


def sum_heads(block):
    stride = 1
    while stride < lax.axis_size("head"):
        block = block + swap(block, "head", stride)
        stride *= 2
    return block


def from_partner(block, axis):
    count = lax.axis_size(axis)
    route = [(at, at ^ 1) for at in range(count)]
    return lax.ppermute(block, axis, route)


def matmul(left, right):
    return jnp.dot(left, right, preferred_element_type=F32)


def rows_inner(left, right):
    return lax.dot_general(left, right, (((0,), (0,)), ((), ())), preferred_element_type=F32)


def cols_inner(left, right):
    return lax.dot_general(left, right, (((1,), (1,)), ((), ())), preferred_element_type=F32)


def rms_scale(values):
    return lax.rsqrt(jnp.mean(values * values, axis=1, keepdims=True) + EPSILON)


def order_halves(own, mate, first):
    return jnp.where(first, jnp.concatenate([own, mate], 1), jnp.concatenate([mate, own], 1))


def per_device(
    tokens,
    segment_ids,
    norm1_gain,
    w_query,
    w_key,
    w_value,
    w_gate,
    w_out,
    norm2_gain,
    w_mlp_gate,
    w_mlp_up,
    w_down,
    out_grad,
):
    heads = lax.axis_size("head")
    batches = lax.axis_size("batch")
    row_count, width = tokens.shape
    head_size = w_query.shape[1]
    half = w_key.shape[1]
    chunk = row_count // heads
    first = lax.axis_index("head") % 2 == 0
    me = ring_place(lax.axis_index("head"), heads)
    scale_factor = 1.0 / math.sqrt(head_size)

    kv_shard = jnp.concatenate([w_key, w_value], axis=1)
    kv_mate = from_partner(kv_shard, "head")
    w_in = jnp.concatenate(
        [
            w_query,
            order_halves(w_key, kv_mate[:, :half], first),
            order_halves(w_value, kv_mate[:, half:], first),
            w_gate,
        ],
        axis=1,
    )
    w_in = lax.all_gather(w_in, "batch", axis=0, tiled=True)
    gains = lax.all_gather(jnp.stack([norm1_gain, norm2_gain]), "batch", axis=1, tiled=True)
    gain_one = gains[0].astype(F32)
    gain_two = gains[1].astype(F32)
    mgate_full = lax.all_gather(w_mlp_gate, "batch", axis=0, tiled=True)
    mup_full = lax.all_gather(w_mlp_up, "batch", axis=0, tiled=True)
    down_full = lax.all_gather(w_down, "batch", axis=1, tiled=True)

    inputs = tokens.astype(F32)
    recip_one = rms_scale(inputs)
    normed_one = (inputs * recip_one * gain_one).astype(BF)
    projected = matmul(normed_one, w_in)
    queries = projected[:, :head_size].astype(BF)
    kv_local = projected[:, head_size : 3 * head_size].astype(BF)
    gate_logit = projected[:, 3 * head_size :]
    out_rows, kv_all, seg_all = spread(
        [w_out, kv_local, segment_ids.reshape(-1, 128)],
        (("head", "rows"), ("batch", "rows"), ("batch", "lead")),
        1,
    )
    seg_all = seg_all.reshape(-1)
    base = lax.axis_index("batch") * row_count
    ids = jnp.arange(DOCUMENTS, dtype=jnp.int32)
    below = jnp.sum((seg_all[None, :] < ids[:, None]).astype(jnp.int32), axis=1)
    starts = jnp.sum(jnp.where(segment_ids[None, :] == ids[:, None], below[:, None], 0), axis=0)
    scalars = (starts, base.reshape(1))
    pair_flops = 4 * row_count * kv_all.shape[0] * head_size
    attended, mixed, lse = local_call(
        functools.partial(attend_kernel, scale_factor),
        scalars,
        (queries, kv_all, starts[None], gate_logit),
        [
            jax.ShapeDtypeStruct((row_count, head_size), F32),
            jax.ShapeDtypeStruct((row_count, head_size), BF),
            jax.ShapeDtypeStruct((1, row_count), F32),
        ],
        [],
        pair_flops,
        "attend",
    )
    mixed_all, out_full = spread([mixed, out_rows], (("head", "cols"), ("batch", "cols")), 2)
    normed_two, hidden, d_pre, mlp_part, dn2, resid_own = mlp_back(
        tokens, mixed_all, out_grad, gain_two[None], out_full, mgate_full, mup_full, down_full, 3
    )
    recip_own = rms_scale(resid_own)
    mixed_own = lax.dynamic_slice_in_dim(mixed_all, me * chunk, chunk, 0)
    dy_own = lax.dynamic_slice_in_dim(out_grad, me * chunk, chunk, 0).astype(F32)
    out_flow = flow_steps(mlp_part)
    out_state = next(out_flow)

    d_gain_two = jnp.sum(dn2 * resid_own * recip_own, axis=0)
    weighted_two = gain_two * dn2
    d_resid = (
        dy_own
        + recip_own * weighted_two
        - resid_own * recip_own**3 * jnp.mean(weighted_two * resid_own, axis=1, keepdims=True)
    )
    d_resid_low = d_resid.astype(BF)
    d_mixed_all = cols_inner(d_resid_low, out_full).astype(BF)
    d_mixed_all = d_mixed_all.reshape(chunk, heads, head_size)
    places = [ring_place(at, heads) for at in range(heads)]
    d_mixed_all = jnp.stack([d_mixed_all[:, at] for at in places], axis=0)
    d_mixed = lax.all_to_all(d_mixed_all, "head", split_axis=0, concat_axis=0, tiled=True)
    d_mixed = jnp.concatenate([d_mixed[ring_head(at, heads)] for at in range(heads)], axis=0)
    d_out_part = rows_inner(mixed_own, d_resid_low).astype(BF)
    d_out_part = lax.psum_scatter(d_out_part, "batch", scatter_dimension=1, tiled=True)
    d_out = flow_sum(d_out_part)

    d_mixed, out_state = after(out_flow, out_state, d_mixed)
    d_queries, d_gate_logit, d_kv_all = local_call(
        functools.partial(attend_back_kernel, scale_factor),
        scalars,
        (queries, kv_all, starts[None], gate_logit, attended, d_mixed, lse),
        [
            jax.ShapeDtypeStruct((row_count, head_size), BF),
            jax.ShapeDtypeStruct((row_count, head_size), BF),
            jax.ShapeDtypeStruct(kv_all.shape, BF),
        ],
        [pltpu.VMEM((kv_all.shape[0], head_size), F32)] * 2,
        5 * pair_flops // 2,
        "attend_back",
    )
    d_kv_all, out_state = after(out_flow, out_state, d_kv_all)
    d_kv_own = halve_batch(d_kv_all, row_count)
    d_kv_own, out_state = after(out_flow, out_state, d_kv_own)
    while isinstance(out_state, tuple):
        out_state = out_flow.send(out_state)
    output = flow_spread((resid_own + out_state).astype(BF))
    d_kv_mate = from_partner(d_kv_own, "head")
    d_kv = (d_kv_own.astype(F32) + d_kv_mate.astype(F32)).astype(BF)
    d_cat = jnp.concatenate(
        [
            d_queries,
            jnp.where(first, d_kv[:, :half], d_kv[:, half:head_size]),
            jnp.where(first, d_kv[:, head_size : head_size + half], d_kv[:, head_size + half :]),
            d_gate_logit,
        ],
        axis=1,
    )
    w_key_own = jnp.where(
        first, w_in[:, head_size : head_size + half], w_in[:, head_size + half : 2 * head_size]
    )
    w_value_own = jnp.where(
        first, w_in[:, 2 * head_size : 2 * head_size + half], w_in[:, 2 * head_size + half : 3 * head_size]
    )
    w_cat = jnp.concatenate(
        [w_in[:, :head_size], w_key_own, w_value_own, w_in[:, 3 * head_size :]], axis=1
    )
    dn1_part = cols_inner(d_cat, w_cat).astype(BF)
    dn1 = flow_sum(dn1_part)
    inputs_own = lax.dynamic_slice_in_dim(inputs, me * chunk, chunk, 0)
    recip_in = lax.dynamic_slice_in_dim(recip_one, me * chunk, chunk, 0)
    d_gain_one = jnp.sum(dn1 * inputs_own * recip_in, axis=0)
    weighted_one = gain_one * dn1
    d_tokens = (
        d_resid
        + recip_in * weighted_one
        - inputs_own * recip_in**3 * jnp.mean(weighted_one * inputs_own, axis=1, keepdims=True)
    ).astype(BF)
    d_tokens = flow_spread(d_tokens)

    d_mlp = rows_inner(normed_two, d_pre).astype(BF)
    d_mlp = lax.psum_scatter(d_mlp, "batch", scatter_dimension=0, tiled=True).astype(F32)
    d_down = rows_inner(hidden, out_grad).astype(BF)
    d_down = lax.psum_scatter(d_down, "batch", scatter_dimension=1, tiled=True).astype(F32)
    d_in = rows_inner(normed_one, d_cat).astype(BF)
    d_in = lax.psum_scatter(d_in, "batch", scatter_dimension=0, tiled=True).astype(F32)
    d_gains = jnp.stack([d_gain_one, d_gain_two]).reshape(2, batches, -1).transpose(1, 0, 2)
    d_gains = sum_heads(halve_batch(d_gains.reshape(2 * batches, -1), 2))
    hidden_own = w_mlp_gate.shape[1]
    return (
        output,
        d_tokens,
        d_gains[0],
        d_in[:, :head_size],
        d_in[:, head_size : head_size + half],
        d_in[:, head_size + half : 2 * head_size],
        d_in[:, 2 * head_size :],
        d_out,
        d_gains[1],
        d_mlp[:, :hidden_own],
        d_mlp[:, hidden_own:],
        d_down,
    )


def solution(mesh):
    return jax.shard_map(
        per_device,
        mesh=mesh,
        in_specs=(
            P("batch", None),
            P("batch"),
            P("batch"),
            P("batch", "head"),
            P("batch", "head"),
            P("batch", "head"),
            P("batch", "head"),
            P("head", "batch"),
            P("batch"),
            P("batch", "head"),
            P("batch", "head"),
            P("head", "batch"),
            P("batch", None),
        ),
        out_specs=(
            P("batch", None),
            P("batch", None),
            P("batch"),
            P("batch", "head"),
            P("batch", "head"),
            P("batch", "head"),
            P("batch", "head"),
            P("head", "batch"),
            P("batch"),
            P("batch", "head"),
            P("batch", "head"),
            P("head", "batch"),
        ),
        check_vma=False,
    )
```

```python
import functools
import math

import jax
import jax.numpy as jnp
from jax import lax
from jax.experimental import pallas as pl
from jax.experimental.pallas import tpu as pltpu
from jax.sharding import PartitionSpec as P

EPSILON = 1e-06
MASKED = -1e30
DOCUMENTS = 7
BF = jnp.bfloat16
F32 = jnp.float32


MESH = pl.DeviceIdType.MESH
VMEM_LIMIT = 60 << 20


def ring_place(head, count):
    high, low = head // 2, head % 2
    return (1 - low) * high + low * (count - 1 - high)


def ring_head(place, count):
    low = place // (count // 2)
    high = (1 - low) * place + low * (count - 1 - place)
    return 2 * high + low


def ring_setup(count):
    batch = lax.axis_index("batch")
    place = ring_place(lax.axis_index("head"), count)
    right = (batch, ring_head(lax.rem(place + 1, count), count))
    left = (batch, ring_head(lax.rem(place + count - 1, count), count))
    return place, right, left


def greet(devices):
    barrier = pltpu.get_barrier_semaphore()
    for device in devices:
        pl.semaphore_signal(barrier, inc=1, device_id=device, device_id_type=MESH)
    pl.semaphore_wait(barrier, len(devices))


def send(source, target, sems, slot, device):
    copy = pltpu.make_async_remote_copy(
        src_ref=source,
        dst_ref=target,
        send_sem=sems[0].at[slot],
        recv_sem=sems[1].at[slot],
        device_id=device,
        device_id_type=MESH,
    )
    copy.start()
    return copy


def half_of(extent, flow):
    if extent[1] % 256:
        return (pl.ds(flow * (extent[0] // 2), extent[0] // 2), slice(None))
    return (slice(None), pl.ds(flow * (extent[1] // 2), extent[1] // 2))


def place_of(whole, own, chunk, form):
    rows, wide = own.shape[-2:]
    if form == "lead":
        return whole.at[chunk]
    if form == "rows":
        return whole.at[pl.ds(pl.multiple_of(chunk * rows, rows), rows)]
    return whole.at[:, pl.ds(pl.multiple_of(chunk * wide, wide), wide)]


def spread_kernel(count, batches, plans, *refs):
    steps = count // 2
    arrays = len(plans)
    own_refs, all_refs = refs[:arrays], refs[arrays : 2 * arrays]
    send_sem, recv_sem, local_sem = refs[2 * arrays :]
    place, right, left = ring_setup(count)
    head = lax.axis_index("head")
    batch = lax.axis_index("batch")
    across, core = batch // 2, lax.rem(batch, 2)
    others = batches // 2
    twin = (across * 2 + 1 - core, head)
    peers = [(lax.rem(across + hop, others) * 2 + core, head) for hop in range(1, others)]
    ring = any(axis == "head" for axis, _ in plans)
    grid = any(axis == "batch" for axis, _ in plans)
    greet((right, left) * ring + (twin, *peers) * grid)
    sems = (send_sem, recv_sem)
    slot = 0
    waiting, arriving, local = [], [], []

    def go(source, target, device):
        nonlocal slot
        copy = send(source, target, sems, slot, device)
        slot += 1
        waiting.append(copy)
        return copy

    onward = []
    for index, (axis, form) in enumerate(plans):
        own, whole = own_refs[index], all_refs[index]
        spot = place if axis == "head" else batch
        mine = place_of(whole, own, spot, form)
        copy = pltpu.make_async_copy(own, mine, local_sem.at[index])
        copy.start()
        local.append(copy)
        if axis == "batch":
            for hop, peer in enumerate(peers, 1):
                source = lax.rem(across + others - hop, others) * 2 + core
                onward.append((go(own, mine, peer), place_of(whole, own, source, form)))
            arriving.append(go(own, mine, twin))
    copies = [None] * (2 * arrays)
    for step in range(steps):
        for index, (axis, form) in enumerate(plans):
            if axis != "head":
                continue
            own = own_refs[index]
            for flow, chunk, device in ((0, place - step, right), (1, place + step, left)):
                at = 2 * index + flow
                if step:
                    copies[at].wait_recv()
                chunk = lax.rem(chunk + count, count)
                target = place_of(all_refs[index], own, chunk, form)
                source = target if step else own
                if step == steps - 1:
                    part = half_of(own.shape, flow)
                    source = source.at[part]
                    target = target.at[part]
                copies[at] = go(source, target, device)
        if step == 0 or not ring:
            for copy, block in onward:
                copy.wait_recv()
                arriving.append(go(block, block, twin))
            onward = []
    for copy in copies:
        if copy is not None:
            arriving.append(copy)
    for copy in arriving:
        copy.wait_recv()
    for copy in waiting:
        copy.wait_send()
    for copy in local:
        copy.wait()


def spread(arrays, plans, collective_id):
    count = lax.axis_size("head")
    batches = lax.axis_size("batch")
    shapes = []
    slots = 0
    for array, (axis, form) in zip(arrays, plans):
        many = count if axis == "head" else batches
        slots += count if axis == "head" else batches - 1
        if form == "lead":
            shapes.append((many, *array.shape))
        elif form == "rows":
            shapes.append((many * array.shape[0], array.shape[1]))
        else:
            shapes.append((array.shape[0], many * array.shape[1]))
    hbm = pl.BlockSpec(memory_space=pl.ANY)
    return pl.pallas_call(
        functools.partial(spread_kernel, count, batches, plans),
        out_shape=[jax.ShapeDtypeStruct(shape, a.dtype) for shape, a in zip(shapes, arrays)],
        in_specs=[hbm] * len(arrays),
        out_specs=[hbm] * len(arrays),
        scratch_shapes=[
            pltpu.SemaphoreType.DMA((slots,)),
            pltpu.SemaphoreType.DMA((slots,)),
            pltpu.SemaphoreType.DMA((len(arrays),)),
        ],
        compiler_params=pltpu.CompilerParams(
            collective_id=collective_id, has_side_effects=True, vmem_limit_bytes=VMEM_LIMIT
        ),
        name=f"spread_{collective_id}",
    )(*arrays)


def mlp_kernel(
    count, x_hbm, a_hbm, dy_hbm, gain_ref, out_w, gate_w, up_w, down_w,
    n2_hbm, hid_hbm, grad_hbm, mlp_hbm, h1_ref, dh1_ref, low_ref, dgain_ref, da_ref,
    x_s, a_s, dy_s, n2_s, hid_s, grad_s, mlp_s, h1_s, dy_own, da_part,
    right_part, left_part, right_got, left_got,
    in_sem, out_sem, send_sem, recv_sem, da_send, da_recv,
):
    steps = count // 2
    rows = x_hbm.shape[0] // count
    width = x_hbm.shape[1]
    hidden = gate_w.shape[1]
    side = width // 2
    tile = 256
    inner = 256 if hidden % 256 == 0 else 128
    size = da_ref.shape[1]
    place, right, left = ring_setup(count)

    def member(hop):
        spot = lax.rem(place + hop, count)
        return spot, (lax.axis_index("batch"), ring_head(spot, count))

    greet([member(hop)[1] for hop in range(1, count)])

    def owners(group):
        first = jnp.where(group == 0, 1, 0)
        one = lax.rem(place + steps - group, count)
        two = lax.rem(place - steps + group + first * steps + count, count)
        return one, two

    def span(owner):
        return pl.ds(pl.multiple_of(owner * rows, rows), rows)

    def loads(group, slot):
        return [
            pltpu.make_async_copy(
                source.at[span(owner)],
                target.at[slot, pl.ds(at * rows, rows)],
                in_sem.at[slot, 2 * index + at],
            )
            for index, (source, target) in enumerate(((x_hbm, x_s), (a_hbm, a_s), (dy_hbm, dy_s)))
            for at, owner in enumerate(owners(group))
        ]

    def stores(group, slot):
        return [
            pltpu.make_async_copy(
                source.at[slot, pl.ds(at * rows, rows)],
                target.at[span(owner)],
                out_sem.at[slot, 2 * index + at],
            )
            for index, (source, target) in enumerate(
                ((n2_s, n2_hbm), (hid_s, hid_hbm), (grad_s, grad_hbm), (mlp_s, mlp_hbm))
            )
            for at, owner in enumerate(owners(group))
        ]

    def passing(source, target, flow, step, device):
        return pltpu.make_async_remote_copy(
            src_ref=source,
            dst_ref=target,
            send_sem=send_sem.at[flow * steps + step],
            recv_sem=recv_sem.at[flow * steps + step],
            device_id=device,
            device_id_type=MESH,
        )

    def first_copies():
        ahead, behind = pl.ds(0, side), pl.ds(side, side)
        return (
            passing(right_part.at[0, :, ahead], right_got.at[0, :, ahead], 0, 0, right),
            passing(right_part.at[0, :, behind], left_got.at[0, :, behind], 1, 0, left),
        )

    def later_copies(step):
        return (
            passing(right_part.at[step], right_got.at[step], 0, step, right),
            passing(left_part.at[step], left_got.at[step], 1, step, left),
        )

    for copy in loads(0, 0):
        copy.start()

    @pl.loop(0, steps)
    def _(group):
        slot = lax.rem(group, 2)
        for copy in loads(group, slot):
            copy.wait()

        @pl.when(group + 1 < steps)
        def _():
            for copy in loads(group + 1, 1 - slot):
                copy.start()

        @pl.when(group >= 2)
        def _():
            for copy in stores(group - 2, slot):
                copy.wait()

        mixed = a_s[slot]

        def residual(at, total):
            cols = pl.ds(pl.multiple_of(at * tile, tile), tile)
            values = x_s[slot, :, cols].astype(F32) + matmul(mixed, out_w[:, cols])
            h1_s[:, cols] = values
            return total + jnp.sum(values * values, axis=1, keepdims=True)

        total = lax.fori_loop(0, width // tile, residual, jnp.zeros((2 * rows, 1), F32))
        scale = lax.rsqrt(total / width + EPSILON)

        @pl.when(group == 0)
        def _():
            h1_ref[...] = h1_s[pl.ds(rows, rows)]
            dy_own[...] = dy_s[slot, pl.ds(rows, rows)]

        @pl.loop(0, width // tile)
        def _(at):
            cols = pl.ds(pl.multiple_of(at * tile, tile), tile)
            n2_s[slot, :, cols] = (h1_s[:, cols] * scale * gain_ref[:, cols]).astype(BF)

        normed = n2_s[slot]
        dy = dy_s[slot]

        @pl.loop(0, hidden // inner)
        def _(at):
            cols = pl.ds(pl.multiple_of(at * inner, inner), inner)
            cols_up = pl.ds(pl.multiple_of(hidden + at * inner, inner), inner)
            gate = matmul(normed, gate_w[:, cols])
            up = matmul(normed, up_w[:, cols])
            d_hidden = cols_inner(dy, down_w[cols])
            sig = jax.nn.sigmoid(gate)
            silu = gate * sig
            hid_s[slot, :, cols] = (silu * up).astype(BF)
            grad_s[slot, :, cols] = (d_hidden * up * sig * (1.0 + gate * (1.0 - sig))).astype(BF)
            grad_s[slot, :, cols_up] = (d_hidden * silu).astype(BF)

        hid = hid_s[slot]
        d_gate = grad_s[slot, :, :hidden]
        d_up = grad_s[slot, :, hidden:]

        @pl.loop(0, width // tile)
        def _(at):
            cols = pl.ds(pl.multiple_of(at * tile, tile), tile)
            part = (cols_inner(d_gate, gate_w[cols]) + cols_inner(d_up, up_w[cols])).astype(BF)
            right_part[group, :, cols] = part[:rows]
            left_part[group, :, cols] = part[rows:]
            mlp_s[slot, :, cols] = matmul(hid, down_w[:, cols]).astype(BF)

        for copy in stores(group, slot):
            copy.start()

        @pl.when(group == 0)
        def _():
            for copy in first_copies():
                copy.start()

        @pl.when(group == 1)
        def _():
            one, two = first_copies()
            one.wait_recv()
            two.wait_recv()
            ahead, behind = pl.ds(0, side), pl.ds(side, side)
            right_part[1, :, ahead] = add_low(right_part[1, :, ahead], right_got[0, :, ahead])
            left_part[1, :, behind] = add_low(left_part[1, :, behind], left_got[0, :, behind])

        @pl.when(group >= 2)
        def _():
            one, two = later_copies(group - 1)
            one.wait_recv()
            right_part[group] = add_low(right_part[group], right_got[group - 1])
            two.wait_recv()
            left_part[group] = add_low(left_part[group], left_got[group - 1])

        @pl.when(group >= 1)
        def _():
            for copy in later_copies(group):
                copy.start()

    for copy in later_copies(steps - 1):
        copy.wait_recv()

    def tile_of(at):
        return pl.ds(pl.multiple_of(at * tile, tile), tile)

    def collect(at, state):
        squares, mean = state
        cols = tile_of(at)
        dn2 = (
            left_part[0, :, cols].astype(F32)
            + right_got[steps - 1, :, cols].astype(F32)
            + left_got[steps - 1, :, cols].astype(F32)
        )
        dh1_ref[:, cols] = dn2
        h1 = h1_ref[:, cols]
        squares = squares + jnp.sum(h1 * h1, axis=1, keepdims=True)
        return squares, mean + jnp.sum(gain_ref[:, cols] * dn2 * h1, axis=1, keepdims=True)

    zero = jnp.zeros((rows, 1), F32)
    squares, mean = lax.fori_loop(0, width // tile, collect, (zero, zero))
    scale_own = lax.rsqrt(squares / width + EPSILON)
    pull = scale_own * scale_own * scale_own * (mean / width)

    @pl.loop(0, width // tile)
    def _(at):
        cols = tile_of(at)
        dn2, h1 = dh1_ref[:, cols], h1_ref[:, cols]
        dgain_ref[:, cols] = jnp.sum(dn2 * h1 * scale_own, axis=0, keepdims=True)
        d_resid = dy_own[:, cols].astype(F32) + scale_own * (gain_ref[:, cols] * dn2) - h1 * pull
        dh1_ref[:, cols] = d_resid
        low_ref[:, cols] = d_resid.astype(BF)

    def da_copy(hop):
        return pltpu.make_async_remote_copy(
            src_ref=da_part.at[hop],
            dst_ref=da_ref.at[span(place)],
            send_sem=da_send.at[hop],
            recv_sem=da_recv.at[hop],
            device_id=member(hop)[1],
            device_id_type=MESH,
        )

    low = low_ref[...]

    @pl.loop(1, count)
    def _(hop):
        spot = member(hop)[0]
        part = cols_inner(low, out_w[pl.ds(pl.multiple_of(spot * size, size), size)])
        da_part[hop] = part.astype(BF)
        da_copy(hop).start()

    own_w = out_w[pl.ds(pl.multiple_of(place * size, size), size)]
    da_ref[span(place)] = cols_inner(low, own_w).astype(BF)

    @pl.loop(1, count)
    def _(hop):
        da_copy(hop).wait_recv()
        da_copy(hop).wait_send()

    for copy in first_copies():
        copy.wait_send()
    for step in range(1, steps):
        for copy in later_copies(step):
            copy.wait_send()
    for group in range(max(steps - 2, 0), steps):
        for copy in stores(group, group % 2):
            copy.wait()


def mlp_back(tokens, mixed, dy, gain, out_w, gate_w, up_w, down_w, collective_id):
    count = lax.axis_size("head")
    total, width = tokens.shape
    hidden = gate_w.shape[1]
    rows, steps = total // count, count // 2
    size = mixed.shape[1] // count
    vmem = pl.BlockSpec(memory_space=pltpu.VMEM)
    hbm = pl.BlockSpec(memory_space=pl.ANY)

    def slots(wide, dtype=BF):
        return pltpu.VMEM((2, 2 * rows, wide), dtype)

    part = pltpu.VMEM((steps, rows, width), BF)
    flops = 2 * total * width * (mixed.shape[1] + 6 * hidden)
    return pl.pallas_call(
        functools.partial(mlp_kernel, count),
        out_shape=[
            jax.ShapeDtypeStruct((total, width), BF),
            jax.ShapeDtypeStruct((total, hidden), BF),
            jax.ShapeDtypeStruct((total, 2 * hidden), BF),
            jax.ShapeDtypeStruct((total, width), BF),
            jax.ShapeDtypeStruct((rows, width), F32),
            jax.ShapeDtypeStruct((rows, width), F32),
            jax.ShapeDtypeStruct((rows, width), BF),
            jax.ShapeDtypeStruct((1, width), F32),
            jax.ShapeDtypeStruct((total, size), BF),
        ],
        in_specs=[hbm] * 3 + [vmem] * 5,
        out_specs=[hbm] * 4 + [vmem] * 5,
        scratch_shapes=[
            slots(width), slots(mixed.shape[1]), slots(width), slots(width), slots(hidden),
            slots(2 * hidden), slots(width), pltpu.VMEM((2 * rows, width), F32),
            pltpu.VMEM((rows, width), BF), pltpu.VMEM((count, rows, size), BF),
            part, part, part, part,
            pltpu.SemaphoreType.DMA((2, 6)), pltpu.SemaphoreType.DMA((2, 8)),
            pltpu.SemaphoreType.DMA((count,)), pltpu.SemaphoreType.DMA((count,)),
            pltpu.SemaphoreType.DMA((count,)), pltpu.SemaphoreType.DMA((count,)),
        ],
        compiler_params=pltpu.CompilerParams(
            collective_id=collective_id, has_side_effects=True, vmem_limit_bytes=VMEM_LIMIT
        ),
        cost_estimate=pl.CostEstimate(flops=flops, bytes_accessed=40 << 20, transcendentals=0),
        name="mlp_back",
    )(tokens, mixed, dy, gain, out_w, gate_w, up_w, down_w)


KEY_BLOCK = 512
QUERY_BLOCK = 256


def key_range(start_ref, base, query_block):
    first = query_block * QUERY_BLOCK
    lowest = start_ref[first]
    highest = start_ref[first + QUERY_BLOCK - 1]
    begin = lowest // KEY_BLOCK
    end = (base + first + QUERY_BLOCK - 1) // KEY_BLOCK + 1
    full_begin = jnp.minimum((highest + KEY_BLOCK - 1) // KEY_BLOCK, end)
    full_end = jnp.maximum((base + first + 1) // KEY_BLOCK, full_begin)
    return begin, full_begin, full_end, end


def allowed_pairs(key_block, start_row, base_row):
    shape = (KEY_BLOCK, QUERY_BLOCK)
    key_pos = key_block * KEY_BLOCK + lax.broadcasted_iota(jnp.int32, shape, 0)
    query_pos = base_row + lax.broadcasted_iota(jnp.int32, shape, 1)
    return (key_pos >= start_row) & (key_pos <= query_pos)


def attend_kernel(
    scale, start_sm, base_sm, q_ref, kv_ref, start_ref, logit_ref, o_ref, a_ref, lse_ref
):
    base = base_sm[0]
    size = q_ref.shape[1]
    factor = scale * math.log2(math.e)

    @pl.loop(0, q_ref.shape[0] // QUERY_BLOCK)
    def _(block):
        rows = pl.ds(pl.multiple_of(block * QUERY_BLOCK, QUERY_BLOCK), QUERY_BLOCK)
        queries = q_ref[rows]
        start_row = start_ref[:, rows]
        begin, full_begin, full_end, end = key_range(start_sm, base, block)

        def step(masked, at, state):
            old_max, old_sum, total = state
            keys = pl.ds(pl.multiple_of(at * KEY_BLOCK, KEY_BLOCK), KEY_BLOCK)
            scores = cols_inner(kv_ref[keys, :size], queries)
            if masked:
                allowed = allowed_pairs(at, start_row, base + block * QUERY_BLOCK)
                scores = jnp.where(allowed, scores, MASKED)
            new_max = jnp.maximum(old_max, jnp.max(scores, axis=0, keepdims=True))
            keep = jnp.exp2((old_max - new_max) * factor)
            weights = jnp.exp2(scores * factor - new_max * factor)
            new_sum = old_sum * keep + jnp.sum(weights, axis=0, keepdims=True)
            total = total * keep + rows_inner(kv_ref[keys, size:], weights.astype(BF))
            return new_max, new_sum, total

        state = (
            jnp.full((1, QUERY_BLOCK), MASKED, F32),
            jnp.zeros((1, QUERY_BLOCK), F32),
            jnp.zeros((size, QUERY_BLOCK), F32),
        )
        state = lax.fori_loop(begin, full_begin, functools.partial(step, True), state)
        state = lax.fori_loop(full_begin, full_end, functools.partial(step, False), state)
        state = lax.fori_loop(full_end, end, functools.partial(step, True), state)
        run_max, run_sum, total = state
        lse_ref[:, rows] = run_max * factor + jnp.log2(run_sum)
        attended = (total / run_sum).T
        o_ref[rows] = attended
        a_ref[rows] = (attended * jax.nn.sigmoid(logit_ref[rows])).astype(BF)


def attend_back_kernel(
    scale, start_sm, base_sm, q_ref, kv_ref, start_ref, logit_ref, o_ref, da_ref, lse_ref,
    dq_ref, dg_ref, dkv_ref, dk_acc, dv_acc,
):
    base = base_sm[0]
    size = q_ref.shape[1]
    factor = scale * math.log2(math.e)
    dk_acc[...] = jnp.zeros_like(dk_acc)
    dv_acc[...] = jnp.zeros_like(dv_acc)

    @pl.loop(0, q_ref.shape[0] // QUERY_BLOCK)
    def _(block):
        rows = pl.ds(pl.multiple_of(block * QUERY_BLOCK, QUERY_BLOCK), QUERY_BLOCK)
        queries = q_ref[rows]
        start_row = start_ref[:, rows]
        lse = lse_ref[:, rows]
        gate = jax.nn.sigmoid(logit_ref[rows])
        attended = o_ref[rows]
        d_mixed = da_ref[rows].astype(F32)
        d_attended = (d_mixed * gate).astype(BF)
        dg_ref[rows] = (d_mixed * attended * gate * (1.0 - gate)).astype(BF)
        delta = jnp.sum((d_attended.astype(F32) * attended).T, axis=0, keepdims=True)
        begin, full_begin, full_end, end = key_range(start_sm, base, block)

        def step(masked, at, d_queries):
            keys = pl.ds(pl.multiple_of(at * KEY_BLOCK, KEY_BLOCK), KEY_BLOCK)
            key_block = kv_ref[keys, :size]
            probs = jnp.exp2(cols_inner(key_block, queries) * factor - lse)
            if masked:
                allowed = allowed_pairs(at, start_row, base + block * QUERY_BLOCK)
                probs = jnp.where(allowed, probs, 0.0)
            d_probs = cols_inner(kv_ref[keys, size:], d_attended)
            d_scores = (probs * (d_probs - delta) * scale).astype(BF)
            dv_acc[keys] += matmul(probs.astype(BF), d_attended)
            dk_acc[keys] += matmul(d_scores, queries)
            return d_queries + rows_inner(key_block, d_scores)

        d_queries = jnp.zeros((size, QUERY_BLOCK), F32)
        d_queries = lax.fori_loop(begin, full_begin, functools.partial(step, True), d_queries)
        d_queries = lax.fori_loop(full_begin, full_end, functools.partial(step, False), d_queries)
        d_queries = lax.fori_loop(full_end, end, functools.partial(step, True), d_queries)
        dq_ref[rows] = d_queries.T.astype(BF)

    @pl.loop(0, kv_ref.shape[0] // KEY_BLOCK)
    def _(at):
        keys = pl.ds(pl.multiple_of(at * KEY_BLOCK, KEY_BLOCK), KEY_BLOCK)
        dk, dv = dk_acc[keys].astype(BF), dv_acc[keys].astype(BF)
        half = size // 2
        dkv_ref[keys, :size] = jnp.concatenate([dk[:, :half], dv[:, :half]], axis=1)
        dkv_ref[keys, size:] = jnp.concatenate([dk[:, half:], dv[:, half:]], axis=1)


def fold_kernel(
    batches, part_ref, own_ref, core_got, x_first, x_second, y_first, y_second, held, send_sem, recv_sem
):
    rows, size = own_ref.shape
    half = rows // 2
    others = batches // 2
    head = lax.axis_index("head")
    batch = lax.axis_index("batch")
    across, core, low = batch // 2, lax.rem(batch, 2), lax.rem(head, 2)
    twin = (across * 2 + 1 - core, head)
    mate = (batch, head + 1 - 2 * low)
    spots = [lax.rem(across + hop, others) for hop in range(others)]
    peers = [(spot * 2 + core, head) for spot in spots]
    greet((twin, mate, *peers[1:]))
    sems = (send_sem, recv_sem)
    slot = 0
    copies = []
    mine = pl.ds(pl.multiple_of(low * size, size), size)
    given = pl.ds(pl.multiple_of((1 - low) * size, size), size)
    top, bottom = pl.ds(0, half), pl.ds(half, half)

    def block(at, side):
        return pl.ds(pl.multiple_of((2 * at + side) * rows, rows), rows)

    def go(source, target, device):
        nonlocal slot
        copy = send(source, target, sems, slot, device)
        slot += 1
        copies.append(copy)
        return copy

    order = list(range(1, others)) + [0]
    first = [go(part_ref.at[block(spots[hop], 1 - core)], core_got.at[spots[hop]], twin) for hop in order]
    tops, bottoms = [], []
    for copy, hop in zip(first, order):
        copy.wait_recv()
        spot = spots[hop]
        core_got[spot] = add_low(core_got[spot], part_ref[block(spot, core)])
        bottoms.append(go(core_got.at[spot, bottom, given], y_first.at[spot], mate))
        if hop:
            tops.append(go(core_got.at[spot, top], x_first.at[hop - 1], peers[hop]))
    total = core_got[across, top].astype(F32)
    for hop in range(1, others):
        tops[hop - 1].wait_recv()
        total = total + x_first[hop - 1].astype(F32)
    held[...] = total.astype(BF)
    last = go(held.at[:, given], y_second, mate)
    ends = []
    for copy, hop in zip(bottoms, order):
        copy.wait_recv()
        spot = spots[hop]
        y_first[spot] = add_low(y_first[spot], core_got[spot, bottom, mine])
        if hop:
            ends.append(go(y_first.at[spot], x_second.at[hop - 1], peers[hop]))
    last.wait_recv()
    own_ref[top] = add_low(held[:, mine], y_second[...])
    total = y_first[across].astype(F32)
    for hop in range(1, others):
        ends[hop - 1].wait_recv()
        total = total + x_second[hop - 1].astype(F32)
    own_ref[bottom] = total.astype(BF)
    for copy in copies:
        copy.wait_send()


def fold(part, rows, collective_id):
    batches = lax.axis_size("batch")
    others = batches // 2
    size = part.shape[1] // 2
    half = rows // 2
    vmem = pl.BlockSpec(memory_space=pltpu.VMEM)
    sems = pltpu.SemaphoreType.DMA((4 * others,))
    return pl.pallas_call(
        functools.partial(fold_kernel, batches),
        out_shape=jax.ShapeDtypeStruct((rows, size), BF),
        in_specs=[vmem],
        out_specs=vmem,
        scratch_shapes=[
            pltpu.VMEM((others, rows, 2 * size), BF),
            pltpu.VMEM((others - 1, half, 2 * size), BF),
            pltpu.VMEM((others - 1, half, size), BF),
            pltpu.VMEM((others, half, size), BF),
            pltpu.VMEM((half, size), BF),
            pltpu.VMEM((half, 2 * size), BF),
            sems,
            sems,
        ],
        compiler_params=pltpu.CompilerParams(
            collective_id=collective_id, has_side_effects=True, vmem_limit_bytes=VMEM_LIMIT
        ),
        name="fold",
    )(part)


def local_call(kernel, scalars, arrays, outs, scratch, flops, name):
    vmem = pl.BlockSpec(memory_space=pltpu.VMEM)
    smem = pl.BlockSpec(memory_space=pltpu.SMEM)
    return pl.pallas_call(
        kernel,
        out_shape=outs,
        in_specs=[smem] * len(scalars) + [vmem] * len(arrays),
        out_specs=[vmem] * len(outs),
        scratch_shapes=scratch,
        compiler_params=pltpu.CompilerParams(vmem_limit_bytes=VMEM_LIMIT),
        cost_estimate=pl.CostEstimate(flops=flops, bytes_accessed=8 << 20, transcendentals=0),
        name=name,
    )(*scalars, *arrays)


def ring_routes(count):
    spots = [ring_head(at, count) for at in range(count)]
    right = [(spots[at], spots[(at + 1) % count]) for at in range(count)]
    left = [(spots[at], spots[at - 1]) for at in range(count)]
    return right, left


def add_low(one, other):
    return (one.astype(F32) + other.astype(F32)).astype(BF)


def flow_steps(part):
    count = lax.axis_size("head")
    place = ring_place(lax.axis_index("head"), count)
    right, left = ring_routes(count)
    rows, side = part.shape[0] // count, part.shape[1] // 2
    steps = count // 2

    def mine(owner):
        return lax.dynamic_slice_in_dim(part, lax.rem(owner + count, count) * rows, rows, 0)

    far = mine(place + steps)
    going, coming = far[:, :side], far[:, side:]
    for step in range(steps - 1):
        from_left = lax.ppermute(going, "head", right)
        from_right = lax.ppermute(coming, "head", left)
        one, two = mine(place + steps - 1 - step), mine(place - steps + 1 + step)
        if step == 0:
            going = jnp.concatenate([add_low(from_left, one[:, :side]), one[:, side:]], 1)
            coming = jnp.concatenate([two[:, :side], add_low(from_right, two[:, side:])], 1)
        else:
            going, coming = add_low(from_left, one), add_low(from_right, two)
        going, coming = yield going, coming
    from_left = lax.ppermute(going, "head", right)
    from_right = lax.ppermute(coming, "head", left)
    yield mine(place).astype(F32) + from_left.astype(F32) + from_right.astype(F32)


def flow_sum(part):
    flow = flow_steps(part)
    state = next(flow)
    while isinstance(state, tuple):
        state = flow.send(state)
    return state


def after(flow, state, array):
    array, going, coming = lax.optimization_barrier((array, *state))
    return array, flow.send((going, coming))


def flow_spread(own):
    count = lax.axis_size("head")
    place = ring_place(lax.axis_index("head"), count)
    right, left = ring_routes(count)
    side = own.shape[1] // 2
    going = coming = own
    pieces = [(0, own)]
    for step in range(1, count // 2):
        going = lax.ppermute(going, "head", right)
        coming = lax.ppermute(coming, "head", left)
        pieces += [(-step, going), (step, coming)]
    one = lax.ppermute(going[:, :side], "head", right)
    two = lax.ppermute(coming[:, side:], "head", left)
    pieces.append((count // 2, jnp.concatenate([one, two], 1)))
    whole = jnp.zeros((count * own.shape[0], own.shape[1]), own.dtype)
    for shift, piece in pieces:
        at = lax.rem(place + shift + count, count) * own.shape[0]
        whole = lax.dynamic_update_slice_in_dim(whole, piece, at, 0)
    return whole


def swap(block, axis, stride):
    return lax.ppermute(block, axis, [(at, at ^ stride) for at in range(lax.axis_size(axis))])


def halve_batch(block, rows):
    me = lax.axis_index("batch")
    stride = 1
    while stride < lax.axis_size("batch"):
        block = block.reshape(-1, 2, rows, block.shape[-1])
        bit = (me // stride) % 2
        keep = lax.dynamic_index_in_dim(block, bit, 1, keepdims=False)
        give = lax.dynamic_index_in_dim(block, 1 - bit, 1, keepdims=False)
        got = swap(give, "batch", stride)
        block = (keep.astype(F32) + got.astype(F32)).astype(block.dtype)
        stride *= 2
    return block.reshape(rows, -1)


def sum_heads(block):
    stride = 1
    while stride < lax.axis_size("head"):
        block = block + swap(block, "head", stride)
        stride *= 2
    return block


def from_partner(block, axis):
    count = lax.axis_size(axis)
    route = [(at, at ^ 1) for at in range(count)]
    return lax.ppermute(block, axis, route)


def matmul(left, right):
    return jnp.dot(left, right, preferred_element_type=F32)


def rows_inner(left, right):
    return lax.dot_general(left, right, (((0,), (0,)), ((), ())), preferred_element_type=F32)


def cols_inner(left, right):
    return lax.dot_general(left, right, (((1,), (1,)), ((), ())), preferred_element_type=F32)


def rms_scale(values):
    return lax.rsqrt(jnp.mean(values * values, axis=1, keepdims=True) + EPSILON)


def order_halves(own, mate, first):
    return jnp.where(first, jnp.concatenate([own, mate], 1), jnp.concatenate([mate, own], 1))


def per_device(
    tokens,
    segment_ids,
    norm1_gain,
    w_query,
    w_key,
    w_value,
    w_gate,
    w_out,
    norm2_gain,
    w_mlp_gate,
    w_mlp_up,
    w_down,
    out_grad,
):
    heads = lax.axis_size("head")
    batches = lax.axis_size("batch")
    row_count, width = tokens.shape
    head_size = w_query.shape[1]
    half = w_key.shape[1]
    chunk = row_count // heads
    first = lax.axis_index("head") % 2 == 0
    me = ring_place(lax.axis_index("head"), heads)
    scale_factor = 1.0 / math.sqrt(head_size)

    kv_shard = jnp.concatenate([w_key, w_value], axis=1)
    kv_mate = from_partner(kv_shard, "head")
    w_in = jnp.concatenate(
        [
            w_query,
            order_halves(w_key, kv_mate[:, :half], first),
            order_halves(w_value, kv_mate[:, half:], first),
            w_gate,
        ],
        axis=1,
    )
    w_in = lax.all_gather(w_in, "batch", axis=0, tiled=True)
    gains = lax.all_gather(jnp.stack([norm1_gain, norm2_gain]), "batch", axis=1, tiled=True)
    gain_one = gains[0].astype(F32)
    gain_two = gains[1].astype(F32)
    mgate_full = lax.all_gather(w_mlp_gate, "batch", axis=0, tiled=True)
    mup_full = lax.all_gather(w_mlp_up, "batch", axis=0, tiled=True)
    down_full = lax.all_gather(w_down, "batch", axis=1, tiled=True)

    inputs = tokens.astype(F32)
    recip_one = rms_scale(inputs)
    normed_one = (inputs * recip_one * gain_one).astype(BF)
    projected = matmul(normed_one, w_in)
    queries = projected[:, :head_size].astype(BF)
    kv_local = projected[:, head_size : 3 * head_size].astype(BF)
    gate_logit = projected[:, 3 * head_size :]
    out_rows, kv_all, seg_all = spread(
        [w_out, kv_local, segment_ids.reshape(-1, 128)],
        (("head", "rows"), ("batch", "rows"), ("batch", "lead")),
        1,
    )
    seg_all = seg_all.reshape(-1)
    base = lax.axis_index("batch") * row_count
    ids = jnp.arange(DOCUMENTS, dtype=jnp.int32)
    below = jnp.sum((seg_all[None, :] < ids[:, None]).astype(jnp.int32), axis=1)
    starts = jnp.sum(jnp.where(segment_ids[None, :] == ids[:, None], below[:, None], 0), axis=0)
    scalars = (starts, base.reshape(1))
    pair_flops = 4 * row_count * kv_all.shape[0] * head_size
    attended, mixed, lse = local_call(
        functools.partial(attend_kernel, scale_factor),
        scalars,
        (queries, kv_all, starts[None], gate_logit),
        [
            jax.ShapeDtypeStruct((row_count, head_size), F32),
            jax.ShapeDtypeStruct((row_count, head_size), BF),
            jax.ShapeDtypeStruct((1, row_count), F32),
        ],
        [],
        pair_flops,
        "attend",
    )
    mixed_all, out_full = spread([mixed, out_rows], (("head", "cols"), ("batch", "cols")), 2)
    normed_two, hidden, d_pre, mlp_part, resid_own, d_resid, d_resid_low, d_gain_two, d_mixed = mlp_back(
        tokens, mixed_all, out_grad, gain_two[None], out_full, mgate_full, mup_full, down_full, 3
    )
    mixed_own = lax.dynamic_slice_in_dim(mixed_all, me * chunk, chunk, 0)
    out_flow = flow_steps(mlp_part)
    out_state = next(out_flow)
    d_down = rows_inner(hidden, out_grad).astype(BF)
    normed_late, d_down, *out_state = lax.optimization_barrier((normed_two, d_down, *out_state))
    out_state = out_flow.send(tuple(out_state))
    d_mlp = rows_inner(normed_late, d_pre).astype(BF)
    d_mixed, d_mlp, *out_state = lax.optimization_barrier((d_mixed, d_mlp, *out_state))
    out_state = tuple(out_state)
    d_down = lax.psum_scatter(d_down, "batch", scatter_dimension=1, tiled=True).astype(F32)
    d_mlp = lax.psum_scatter(d_mlp, "batch", scatter_dimension=0, tiled=True).astype(F32)

    d_mixed, out_state = after(out_flow, out_state, d_mixed)
    d_queries, d_gate_logit, d_kv_all = local_call(
        functools.partial(attend_back_kernel, scale_factor),
        scalars,
        (queries, kv_all, starts[None], gate_logit, attended, d_mixed, lse),
        [
            jax.ShapeDtypeStruct((row_count, head_size), BF),
            jax.ShapeDtypeStruct((row_count, head_size), BF),
            jax.ShapeDtypeStruct(kv_all.shape, BF),
        ],
        [pltpu.VMEM((kv_all.shape[0], head_size), F32)] * 2,
        5 * pair_flops // 2,
        "attend_back",
    )
    d_kv_all, out_state = after(out_flow, out_state, d_kv_all)
    d_kv = fold(d_kv_all, row_count, 4)
    while isinstance(out_state, tuple):
        out_state = out_flow.send(out_state)
    out_total = out_state
    d_kv, out_total = lax.optimization_barrier((d_kv, out_total))
    output = flow_spread((resid_own + out_total).astype(BF))
    d_cat = jnp.concatenate([d_queries, d_kv, d_gate_logit], axis=1)
    d_out_part = rows_inner(mixed_own, d_resid_low).astype(BF)
    d_out_part = lax.psum_scatter(d_out_part, "batch", scatter_dimension=1, tiled=True)
    d_out = flow_sum(d_out_part)
    w_key_own = jnp.where(
        first, w_in[:, head_size : head_size + half], w_in[:, head_size + half : 2 * head_size]
    )
    w_value_own = jnp.where(
        first, w_in[:, 2 * head_size : 2 * head_size + half], w_in[:, 2 * head_size + half : 3 * head_size]
    )
    w_cat = jnp.concatenate(
        [w_in[:, :head_size], w_key_own, w_value_own, w_in[:, 3 * head_size :]], axis=1
    )
    dn1_part = cols_inner(d_cat, w_cat).astype(BF)
    dn1 = flow_sum(dn1_part)
    inputs_own = lax.dynamic_slice_in_dim(inputs, me * chunk, chunk, 0)
    recip_in = lax.dynamic_slice_in_dim(recip_one, me * chunk, chunk, 0)
    d_gain_one = jnp.sum(dn1 * inputs_own * recip_in, axis=0)
    weighted_one = gain_one * dn1
    d_tokens = (
        d_resid
        + recip_in * weighted_one
        - inputs_own * recip_in**3 * jnp.mean(weighted_one * inputs_own, axis=1, keepdims=True)
    ).astype(BF)
    d_tokens = flow_spread(d_tokens)

    d_in = rows_inner(normed_one, d_cat).astype(BF)
    d_in = lax.psum_scatter(d_in, "batch", scatter_dimension=0, tiled=True).astype(F32)
    d_gains = jnp.stack([d_gain_one, d_gain_two[0]]).reshape(2, batches, -1).transpose(1, 0, 2)
    d_gains = sum_heads(halve_batch(d_gains.reshape(2 * batches, -1), 2))
    hidden_own = w_mlp_gate.shape[1]
    return (
        output,
        d_tokens,
        d_gains[0],
        d_in[:, :head_size],
        d_in[:, head_size : head_size + half],
        d_in[:, head_size + half : 2 * head_size],
        d_in[:, 2 * head_size :],
        d_out,
        d_gains[1],
        d_mlp[:, :hidden_own],
        d_mlp[:, hidden_own:],
        d_down,
    )


def solution(mesh):
    return jax.shard_map(
        per_device,
        mesh=mesh,
        in_specs=(
            P("batch", None),
            P("batch"),
            P("batch"),
            P("batch", "head"),
            P("batch", "head"),
            P("batch", "head"),
            P("batch", "head"),
            P("head", "batch"),
            P("batch"),
            P("batch", "head"),
            P("batch", "head"),
            P("head", "batch"),
            P("batch", None),
        ),
        out_specs=(
            P("batch", None),
            P("batch", None),
            P("batch"),
            P("batch", "head"),
            P("batch", "head"),
            P("batch", "head"),
            P("batch", "head"),
            P("head", "batch"),
            P("batch"),
            P("batch", "head"),
            P("batch", "head"),
            P("head", "batch"),
        ),
        check_vma=False,
    )
```

```python
import functools
import math

import jax
import jax.numpy as jnp
from jax import lax
from jax.experimental import pallas as pl
from jax.experimental.pallas import tpu as pltpu
from jax.sharding import PartitionSpec as P

EPSILON = 1e-06
MASKED = -1e30
DOCUMENTS = 7
BF = jnp.bfloat16
F32 = jnp.float32


MESH = pl.DeviceIdType.MESH
VMEM_LIMIT = 60 << 20


def ring_place(head, count):
    high, low = head // 2, head % 2
    return (1 - low) * high + low * (count - 1 - high)


def ring_head(place, count):
    low = place // (count // 2)
    high = (1 - low) * place + low * (count - 1 - place)
    return 2 * high + low


def ring_setup(count):
    batch = lax.axis_index("batch")
    place = ring_place(lax.axis_index("head"), count)
    right = (batch, ring_head(lax.rem(place + 1, count), count))
    left = (batch, ring_head(lax.rem(place + count - 1, count), count))
    return place, right, left


def greet(devices):
    barrier = pltpu.get_barrier_semaphore()
    for device in devices:
        pl.semaphore_signal(barrier, inc=1, device_id=device, device_id_type=MESH)
    pl.semaphore_wait(barrier, len(devices))


def send(source, target, sems, slot, device):
    copy = pltpu.make_async_remote_copy(
        src_ref=source,
        dst_ref=target,
        send_sem=sems[0].at[slot],
        recv_sem=sems[1].at[slot],
        device_id=device,
        device_id_type=MESH,
    )
    copy.start()
    return copy


def half_of(extent, flow):
    if extent[1] % 256:
        return (pl.ds(flow * (extent[0] // 2), extent[0] // 2), slice(None))
    return (slice(None), pl.ds(flow * (extent[1] // 2), extent[1] // 2))


def place_of(whole, own, chunk, form):
    rows, wide = own.shape[-2:]
    if form == "lead":
        return whole.at[chunk]
    if form == "rows":
        return whole.at[pl.ds(pl.multiple_of(chunk * rows, rows), rows)]
    return whole.at[:, pl.ds(pl.multiple_of(chunk * wide, wide), wide)]


def spread_kernel(count, batches, plans, *refs):
    steps = count // 2
    arrays = len(plans)
    own_refs, all_refs = refs[:arrays], refs[arrays : 2 * arrays]
    send_sem, recv_sem, local_sem = refs[2 * arrays :]
    place, right, left = ring_setup(count)
    head = lax.axis_index("head")
    batch = lax.axis_index("batch")
    across, core = batch // 2, lax.rem(batch, 2)
    others = batches // 2
    twin = (across * 2 + 1 - core, head)
    peers = [(lax.rem(across + hop, others) * 2 + core, head) for hop in range(1, others)]
    ring = any(axis == "head" for axis, _ in plans)
    grid = any(axis == "batch" for axis, _ in plans)
    greet((right, left) * ring + (twin, *peers) * grid)
    sems = (send_sem, recv_sem)
    slot = 0
    waiting, arriving, local = [], [], []

    def go(source, target, device):
        nonlocal slot
        copy = send(source, target, sems, slot, device)
        slot += 1
        waiting.append(copy)
        return copy

    onward = []
    for index, (axis, form) in enumerate(plans):
        own, whole = own_refs[index], all_refs[index]
        spot = place if axis == "head" else batch
        mine = place_of(whole, own, spot, form)
        copy = pltpu.make_async_copy(own, mine, local_sem.at[index])
        copy.start()
        local.append(copy)
        if axis == "batch":
            for hop, peer in enumerate(peers, 1):
                source = lax.rem(across + others - hop, others) * 2 + core
                onward.append((go(own, mine, peer), place_of(whole, own, source, form)))
            arriving.append(go(own, mine, twin))
    copies = [None] * (2 * arrays)
    for step in range(steps):
        for index, (axis, form) in enumerate(plans):
            if axis != "head":
                continue
            own = own_refs[index]
            for flow, chunk, device in ((0, place - step, right), (1, place + step, left)):
                at = 2 * index + flow
                if step:
                    copies[at].wait_recv()
                chunk = lax.rem(chunk + count, count)
                target = place_of(all_refs[index], own, chunk, form)
                source = target if step else own
                if step == steps - 1:
                    part = half_of(own.shape, flow)
                    source = source.at[part]
                    target = target.at[part]
                copies[at] = go(source, target, device)
        if step == 0 or not ring:
            for copy, block in onward:
                copy.wait_recv()
                arriving.append(go(block, block, twin))
            onward = []
    for copy in copies:
        if copy is not None:
            arriving.append(copy)
    for copy in arriving:
        copy.wait_recv()
    for copy in waiting:
        copy.wait_send()
    for copy in local:
        copy.wait()


def spread(arrays, plans, collective_id):
    count = lax.axis_size("head")
    batches = lax.axis_size("batch")
    shapes = []
    slots = 0
    for array, (axis, form) in zip(arrays, plans):
        many = count if axis == "head" else batches
        slots += count if axis == "head" else batches - 1
        if form == "lead":
            shapes.append((many, *array.shape))
        elif form == "rows":
            shapes.append((many * array.shape[0], array.shape[1]))
        else:
            shapes.append((array.shape[0], many * array.shape[1]))
    hbm = pl.BlockSpec(memory_space=pl.ANY)
    return pl.pallas_call(
        functools.partial(spread_kernel, count, batches, plans),
        out_shape=[jax.ShapeDtypeStruct(shape, a.dtype) for shape, a in zip(shapes, arrays)],
        in_specs=[hbm] * len(arrays),
        out_specs=[hbm] * len(arrays),
        scratch_shapes=[
            pltpu.SemaphoreType.DMA((slots,)),
            pltpu.SemaphoreType.DMA((slots,)),
            pltpu.SemaphoreType.DMA((len(arrays),)),
        ],
        compiler_params=pltpu.CompilerParams(
            collective_id=collective_id, has_side_effects=True, vmem_limit_bytes=VMEM_LIMIT
        ),
        name=f"spread_{collective_id}",
    )(*arrays)


def mlp_kernel(
    count, x_hbm, a_hbm, dy_hbm, gain_ref, out_w, gate_w, up_w, down_w,
    n2_hbm, hid_hbm, grad_hbm, mlp_hbm, h1_ref, dh1_ref, low_ref, dgain_ref, da_ref,
    x_s, a_s, dy_s, n2_s, hid_s, grad_s, mlp_s, h1_s, dy_own, da_part,
    right_part, left_part, right_got, left_got,
    in_sem, out_sem, send_sem, recv_sem, da_send, da_recv,
):
    steps = count // 2
    rows = x_hbm.shape[0] // count
    width = x_hbm.shape[1]
    hidden = gate_w.shape[1]
    side = width // 2
    tile = 256
    inner = 256 if hidden % 256 == 0 else 128
    size = da_ref.shape[1]
    place, right, left = ring_setup(count)

    def member(hop):
        spot = lax.rem(place + hop, count)
        return spot, (lax.axis_index("batch"), ring_head(spot, count))

    greet([member(hop)[1] for hop in range(1, count)])

    def owners(group):
        first = jnp.where(group == 0, 1, 0)
        one = lax.rem(place + steps - group, count)
        two = lax.rem(place - steps + group + first * steps + count, count)
        return one, two

    def span(owner):
        return pl.ds(pl.multiple_of(owner * rows, rows), rows)

    def loads(group, slot):
        return [
            pltpu.make_async_copy(
                source.at[span(owner)],
                target.at[slot, pl.ds(at * rows, rows)],
                in_sem.at[slot, 2 * index + at],
            )
            for index, (source, target) in enumerate(((x_hbm, x_s), (a_hbm, a_s), (dy_hbm, dy_s)))
            for at, owner in enumerate(owners(group))
        ]

    def stores(group, slot):
        return [
            pltpu.make_async_copy(
                source.at[slot, pl.ds(at * rows, rows)],
                target.at[span(owner)],
                out_sem.at[slot, 2 * index + at],
            )
            for index, (source, target) in enumerate(
                ((n2_s, n2_hbm), (hid_s, hid_hbm), (grad_s, grad_hbm), (mlp_s, mlp_hbm))
            )
            for at, owner in enumerate(owners(group))
        ]

    def passing(source, target, flow, step, device):
        return pltpu.make_async_remote_copy(
            src_ref=source,
            dst_ref=target,
            send_sem=send_sem.at[flow * steps + step],
            recv_sem=recv_sem.at[flow * steps + step],
            device_id=device,
            device_id_type=MESH,
        )

    def first_copies():
        ahead, behind = pl.ds(0, side), pl.ds(side, side)
        return (
            passing(right_part.at[0, :, ahead], right_got.at[0, :, ahead], 0, 0, right),
            passing(right_part.at[0, :, behind], left_got.at[0, :, behind], 1, 0, left),
        )

    def later_copies(step):
        return (
            passing(right_part.at[step], right_got.at[step], 0, step, right),
            passing(left_part.at[step], left_got.at[step], 1, step, left),
        )

    for copy in loads(0, 0):
        copy.start()

    @pl.loop(0, steps)
    def _(group):
        slot = lax.rem(group, 2)
        for copy in loads(group, slot):
            copy.wait()

        @pl.when(group + 1 < steps)
        def _():
            for copy in loads(group + 1, 1 - slot):
                copy.start()

        @pl.when(group >= 2)
        def _():
            for copy in stores(group - 2, slot):
                copy.wait()

        mixed = a_s[slot]

        def residual(at, total):
            cols = pl.ds(pl.multiple_of(at * tile, tile), tile)
            values = x_s[slot, :, cols].astype(F32) + matmul(mixed, out_w[:, cols])
            h1_s[:, cols] = values
            return total + jnp.sum(values * values, axis=1, keepdims=True)

        total = lax.fori_loop(0, width // tile, residual, jnp.zeros((2 * rows, 1), F32))
        scale = lax.rsqrt(total / width + EPSILON)

        @pl.when(group == 0)
        def _():
            h1_ref[...] = h1_s[pl.ds(rows, rows)]
            dy_own[...] = dy_s[slot, pl.ds(rows, rows)]

        @pl.loop(0, width // tile)
        def _(at):
            cols = pl.ds(pl.multiple_of(at * tile, tile), tile)
            n2_s[slot, :, cols] = (h1_s[:, cols] * scale * gain_ref[:, cols]).astype(BF)

        normed = n2_s[slot]
        dy = dy_s[slot]

        @pl.loop(0, hidden // inner)
        def _(at):
            cols = pl.ds(pl.multiple_of(at * inner, inner), inner)
            cols_up = pl.ds(pl.multiple_of(hidden + at * inner, inner), inner)
            gate = matmul(normed, gate_w[:, cols])
            up = matmul(normed, up_w[:, cols])
            d_hidden = cols_inner(dy, down_w[cols])
            sig = jax.nn.sigmoid(gate)
            silu = gate * sig
            hid_s[slot, :, cols] = (silu * up).astype(BF)
            grad_s[slot, :, cols] = (d_hidden * up * sig * (1.0 + gate * (1.0 - sig))).astype(BF)
            grad_s[slot, :, cols_up] = (d_hidden * silu).astype(BF)

        hid = hid_s[slot]
        d_gate = grad_s[slot, :, :hidden]
        d_up = grad_s[slot, :, hidden:]

        @pl.loop(0, width // tile)
        def _(at):
            cols = pl.ds(pl.multiple_of(at * tile, tile), tile)
            part = (cols_inner(d_gate, gate_w[cols]) + cols_inner(d_up, up_w[cols])).astype(BF)
            right_part[group, :, cols] = part[:rows]
            left_part[group, :, cols] = part[rows:]
            mlp_s[slot, :, cols] = matmul(hid, down_w[:, cols]).astype(BF)

        for copy in stores(group, slot):
            copy.start()

        @pl.when(group == 0)
        def _():
            for copy in first_copies():
                copy.start()

        @pl.when(group == 1)
        def _():
            one, two = first_copies()
            one.wait_recv()
            two.wait_recv()
            ahead, behind = pl.ds(0, side), pl.ds(side, side)
            right_part[1, :, ahead] = add_low(right_part[1, :, ahead], right_got[0, :, ahead])
            left_part[1, :, behind] = add_low(left_part[1, :, behind], left_got[0, :, behind])

        @pl.when(group >= 2)
        def _():
            one, two = later_copies(group - 1)
            one.wait_recv()
            right_part[group] = add_low(right_part[group], right_got[group - 1])
            two.wait_recv()
            left_part[group] = add_low(left_part[group], left_got[group - 1])

        @pl.when(group >= 1)
        def _():
            for copy in later_copies(group):
                copy.start()

    for copy in later_copies(steps - 1):
        copy.wait_recv()

    def tile_of(at):
        return pl.ds(pl.multiple_of(at * tile, tile), tile)

    def collect(at, state):
        squares, mean = state
        cols = tile_of(at)
        dn2 = (
            left_part[0, :, cols].astype(F32)
            + right_got[steps - 1, :, cols].astype(F32)
            + left_got[steps - 1, :, cols].astype(F32)
        )
        dh1_ref[:, cols] = dn2
        h1 = h1_ref[:, cols]
        squares = squares + jnp.sum(h1 * h1, axis=1, keepdims=True)
        return squares, mean + jnp.sum(gain_ref[:, cols] * dn2 * h1, axis=1, keepdims=True)

    zero = jnp.zeros((rows, 1), F32)
    squares, mean = lax.fori_loop(0, width // tile, collect, (zero, zero))
    scale_own = lax.rsqrt(squares / width + EPSILON)
    pull = scale_own * scale_own * scale_own * (mean / width)

    @pl.loop(0, width // tile)
    def _(at):
        cols = tile_of(at)
        dn2, h1 = dh1_ref[:, cols], h1_ref[:, cols]
        dgain_ref[:, cols] = jnp.sum(dn2 * h1 * scale_own, axis=0, keepdims=True)
        d_resid = dy_own[:, cols].astype(F32) + scale_own * (gain_ref[:, cols] * dn2) - h1 * pull
        dh1_ref[:, cols] = d_resid
        low_ref[:, cols] = d_resid.astype(BF)

    def da_copy(hop):
        return pltpu.make_async_remote_copy(
            src_ref=da_part.at[hop],
            dst_ref=da_ref.at[span(place)],
            send_sem=da_send.at[hop],
            recv_sem=da_recv.at[hop],
            device_id=member(hop)[1],
            device_id_type=MESH,
        )

    low = low_ref[...]

    @pl.loop(1, count)
    def _(hop):
        spot = member(hop)[0]
        part = cols_inner(low, out_w[pl.ds(pl.multiple_of(spot * size, size), size)])
        da_part[hop] = part.astype(BF)
        da_copy(hop).start()

    own_w = out_w[pl.ds(pl.multiple_of(place * size, size), size)]
    da_ref[span(place)] = cols_inner(low, own_w).astype(BF)

    @pl.loop(1, count)
    def _(hop):
        da_copy(hop).wait_recv()
        da_copy(hop).wait_send()

    for copy in first_copies():
        copy.wait_send()
    for step in range(1, steps):
        for copy in later_copies(step):
            copy.wait_send()
    for group in range(max(steps - 2, 0), steps):
        for copy in stores(group, group % 2):
            copy.wait()


def mlp_back(tokens, mixed, dy, gain, out_w, gate_w, up_w, down_w, collective_id):
    count = lax.axis_size("head")
    total, width = tokens.shape
    hidden = gate_w.shape[1]
    rows, steps = total // count, count // 2
    size = mixed.shape[1] // count
    vmem = pl.BlockSpec(memory_space=pltpu.VMEM)
    hbm = pl.BlockSpec(memory_space=pl.ANY)

    def slots(wide, dtype=BF):
        return pltpu.VMEM((2, 2 * rows, wide), dtype)

    part = pltpu.VMEM((steps, rows, width), BF)
    flops = 2 * total * width * (mixed.shape[1] + 6 * hidden)
    return pl.pallas_call(
        functools.partial(mlp_kernel, count),
        out_shape=[
            jax.ShapeDtypeStruct((total, width), BF),
            jax.ShapeDtypeStruct((total, hidden), BF),
            jax.ShapeDtypeStruct((total, 2 * hidden), BF),
            jax.ShapeDtypeStruct((total, width), BF),
            jax.ShapeDtypeStruct((rows, width), F32),
            jax.ShapeDtypeStruct((rows, width), F32),
            jax.ShapeDtypeStruct((rows, width), BF),
            jax.ShapeDtypeStruct((1, width), F32),
            jax.ShapeDtypeStruct((total, size), BF),
        ],
        in_specs=[hbm] * 3 + [vmem] * 5,
        out_specs=[hbm] * 4 + [vmem] * 5,
        scratch_shapes=[
            slots(width), slots(mixed.shape[1]), slots(width), slots(width), slots(hidden),
            slots(2 * hidden), slots(width), pltpu.VMEM((2 * rows, width), F32),
            pltpu.VMEM((rows, width), BF), pltpu.VMEM((count, rows, size), BF),
            part, part, part, part,
            pltpu.SemaphoreType.DMA((2, 6)), pltpu.SemaphoreType.DMA((2, 8)),
            pltpu.SemaphoreType.DMA((count,)), pltpu.SemaphoreType.DMA((count,)),
            pltpu.SemaphoreType.DMA((count,)), pltpu.SemaphoreType.DMA((count,)),
        ],
        compiler_params=pltpu.CompilerParams(
            collective_id=collective_id, has_side_effects=True, vmem_limit_bytes=VMEM_LIMIT
        ),
        cost_estimate=pl.CostEstimate(flops=flops, bytes_accessed=40 << 20, transcendentals=0),
        name="mlp_back",
    )(tokens, mixed, dy, gain, out_w, gate_w, up_w, down_w)


def entry_kernel(
    count, batches, x_ref, w_ref, out_ref, gain_ref, seg_ref,
    n1_ref, q_ref, logit_ref, kv_ref, w_all, out_all, gain_all, seg_all,
    send_sem, recv_sem, local_sem,
):
    steps = count // 2
    others = batches // 2
    rows, width = x_ref.shape
    depth = w_ref.shape[0]
    size, wide = out_ref.shape
    block = 256
    place, right, left = ring_setup(count)
    head = lax.axis_index("head")
    batch = lax.axis_index("batch")
    across, core, low = batch // 2, lax.rem(batch, 2), lax.rem(head, 2)
    twin = (across * 2 + 1 - core, head)
    mate = (batch, head + 1 - 2 * low)
    spots = [lax.rem(across + hop, others) for hop in range(others)]
    backs = [lax.rem(across + others - hop, others) for hop in range(others)]
    peers = [(spot * 2 + core, head) for spot in spots]
    far_peers = [(spot * 2 + 1 - core, head) for spot in spots]
    greet((twin, mate, right, left, *peers[1:], *far_peers[1:]))
    sems = (send_sem, recv_sem)
    slot = 0
    copies = []

    def go(source, target, device):
        nonlocal slot
        copy = send(source, target, sems, slot, device)
        slot += 1
        copies.append(copy)
        return copy

    def part(at, extent):
        return pl.ds(pl.multiple_of(at * extent, extent), extent)

    def both(view, own):
        out = [go(own, view(batch), peers[hop]) for hop in range(1, others)]
        return out, [go(own, view(batch), twin)]

    def pass_on(view, arrived):
        out = []
        for hop in range(1, others):
            arrived[hop - 1].wait_recv()
            there = view(backs[hop] * 2 + core)
            out.append(go(there, there, twin))
        return out

    local = []

    def stay(source, target):
        copy = pltpu.make_async_copy(source, target, local_sem.at[len(local)])
        copy.start()
        local.append(copy)

    def main_view(at):
        return w_all.at[part(at, depth), pl.ds(0, 3 * size)]

    def mate_view(at):
        return w_all.at[part(at, depth), pl.ds(3 * size, size)]

    def out_view(chunk, at):
        return out_all.at[part(chunk, size), part(at, wide)]

    small = []
    for own, whole in ((gain_ref, gain_all), (seg_ref, seg_all)):
        for device in (twin, *peers[1:], *far_peers[1:]):
            small.append(go(own, whole.at[batch], device))
        stay(own, whole.at[batch])
    from_mate = go(w_ref.at[:, pl.ds(2 * size, size)], mate_view(batch), mate)
    main_out, main_twin = both(main_view, w_ref)
    stay(w_ref, main_view(batch))
    out_peers = [go(out_ref, out_view(place, batch), peers[hop]) for hop in range(1, others)]
    stay(out_ref, out_view(place, batch))
    flows = [[None, None] for _ in range(others)]

    def ring(step):
        for hop in range(others):
            lane = spots[0] if hop == 0 else backs[hop]
            at = lane * 2 + core
            if step == 0 and hop:
                out_peers[hop - 1].wait_recv()
            for flow, chunk, device in ((0, place - step, right), (1, place + step, left)):
                if step:
                    flows[hop][flow].wait_recv()
                target = out_view(lax.rem(chunk + count, count), at)
                source = out_ref if step == 0 and hop == 0 else target
                if step == steps - 1:
                    cut = (pl.ds(flow * (size // 2), size // 2), slice(None))
                    source, target = source.at[cut], target.at[cut]
                flows[hop][flow] = go(source, target, device)

    for copy in small:
        copy.wait_recv()
    for copy in local[:2]:
        copy.wait()

    def normalize(at):
        here = part(at, block)

        def squares(tile, total):
            values = x_ref[here, part(tile, 256)].astype(F32)
            return total + jnp.sum(values * values, axis=1, keepdims=True)

        total = lax.fori_loop(0, width // 256, squares, jnp.zeros((block, 1), F32))
        scale = lax.rsqrt(total / width + EPSILON)

        @pl.loop(0, batches)
        def _(owner):
            for tile in range(depth // 128):
                cols = pl.ds(pl.multiple_of(owner * depth + tile * 128, 128), 128)
                values = x_ref[here, cols].astype(F32) * scale
                n1_ref[here, cols] = (values * gain_all[owner, pl.ds(tile, 1)]).astype(BF)

    blocks = rows // block
    middle = blocks // 2

    @pl.loop(0, middle)
    def _(at):
        normalize(at)

    from_mate.wait_recv()
    mate_out, mate_twin = both(mate_view, mate_view(batch))
    ring(0)

    @pl.loop(middle, blocks)
    def _(at):
        normalize(at)

    main_passed = pass_on(main_view, main_out)
    mate_passed = pass_on(mate_view, mate_out)
    for copy in (*main_twin, *mate_twin, *main_passed, *mate_passed):
        copy.wait_recv()
    for copy in local[2:]:
        copy.wait()

    def kv_view(at):
        return kv_ref.at[part(at, rows)]

    @pl.loop(0, blocks)
    def _(at):
        here = part(at, block)
        values = matmul(n1_ref[here], w_all[:, pl.ds(2 * size, 2 * size)])
        one, two = values[:, :size], values[:, size:]
        first = jnp.where(low == 0, one, two).astype(BF)
        second = jnp.where(low == 0, two, one).astype(BF)
        half = size // 2
        there = pl.ds(pl.multiple_of(batch * rows + at * block, block), block)
        kv_ref[there, pl.ds(0, size)] = jnp.concatenate([first[:, :half], second[:, :half]], 1)
        kv_ref[there, pl.ds(size, size)] = jnp.concatenate([first[:, half:], second[:, half:]], 1)

    kv_out, kv_twin = both(kv_view, kv_view(batch))
    ring(1)

    @pl.loop(0, blocks)
    def _(at):
        here = part(at, block)
        values = matmul(n1_ref[here], w_all[:, pl.ds(0, 2 * size)])
        q_ref[here] = values[:, :size].astype(BF)
        logit_ref[here] = values[:, size:]

    for step in range(2, steps):
        ring(step)
    kv_passed = pass_on(kv_view, kv_out)
    for pair in flows:
        for copy in pair:
            copy.wait_recv()
    swaps = []
    for hop in range(others):
        there = out_all.at[:, part(spots[hop] * 2 + core, wide)]
        swaps.append(go(there, there, twin))
    for copy in (*kv_twin, *kv_passed, *swaps):
        copy.wait_recv()
    for copy in copies:
        copy.wait_send()


def entry(tokens, w_shard, w_out, gains, segments, collective_id):
    count = lax.axis_size("head")
    batches = lax.axis_size("batch")
    others = batches // 2
    rows, width = tokens.shape
    size, wide = w_out.shape
    vmem = pl.BlockSpec(memory_space=pltpu.VMEM)
    slots = 4 * (batches - 1) + 2 * (batches - 1) + others * (count + 3)
    sems = pltpu.SemaphoreType.DMA((slots,))
    return pl.pallas_call(
        functools.partial(entry_kernel, count, batches),
        out_shape=[
            jax.ShapeDtypeStruct((rows, width), BF),
            jax.ShapeDtypeStruct((rows, size), BF),
            jax.ShapeDtypeStruct((rows, size), F32),
            jax.ShapeDtypeStruct((batches * rows, 2 * size), BF),
            jax.ShapeDtypeStruct((width, 4 * size), BF),
            jax.ShapeDtypeStruct((count * size, batches * wide), BF),
            jax.ShapeDtypeStruct((batches, *gains.shape), F32),
            jax.ShapeDtypeStruct((batches, *segments.shape), jnp.int32),
        ],
        in_specs=[vmem] * 5,
        out_specs=[vmem] * 8,
        scratch_shapes=[sems, sems, pltpu.SemaphoreType.DMA((4,))],
        compiler_params=pltpu.CompilerParams(
            collective_id=collective_id, has_side_effects=True, vmem_limit_bytes=VMEM_LIMIT
        ),
        name="entry",
    )(tokens, w_shard, w_out, gains, segments)


KEY_BLOCK = 512
QUERY_BLOCK = 256


def key_range(start_ref, base, query_block):
    first = query_block * QUERY_BLOCK
    lowest = start_ref[first]
    highest = start_ref[first + QUERY_BLOCK - 1]
    begin = lowest // KEY_BLOCK
    end = (base + first + QUERY_BLOCK - 1) // KEY_BLOCK + 1
    full_begin = jnp.minimum((highest + KEY_BLOCK - 1) // KEY_BLOCK, end)
    full_end = jnp.maximum((base + first + 1) // KEY_BLOCK, full_begin)
    return begin, full_begin, full_end, end


def allowed_pairs(key_block, start_row, base_row):
    shape = (KEY_BLOCK, QUERY_BLOCK)
    key_pos = key_block * KEY_BLOCK + lax.broadcasted_iota(jnp.int32, shape, 0)
    query_pos = base_row + lax.broadcasted_iota(jnp.int32, shape, 1)
    return (key_pos >= start_row) & (key_pos <= query_pos)


def attend_kernel(
    scale, start_sm, base_sm, q_ref, kv_ref, start_ref, logit_ref, o_ref, a_ref, lse_ref
):
    base = base_sm[0]
    size = q_ref.shape[1]
    factor = scale * math.log2(math.e)

    @pl.loop(0, q_ref.shape[0] // QUERY_BLOCK)
    def _(block):
        rows = pl.ds(pl.multiple_of(block * QUERY_BLOCK, QUERY_BLOCK), QUERY_BLOCK)
        queries = q_ref[rows]
        start_row = start_ref[:, rows]
        begin, full_begin, full_end, end = key_range(start_sm, base, block)

        def step(masked, at, state):
            old_max, old_sum, total = state
            keys = pl.ds(pl.multiple_of(at * KEY_BLOCK, KEY_BLOCK), KEY_BLOCK)
            scores = cols_inner(kv_ref[keys, :size], queries)
            if masked:
                allowed = allowed_pairs(at, start_row, base + block * QUERY_BLOCK)
                scores = jnp.where(allowed, scores, MASKED)
            new_max = jnp.maximum(old_max, jnp.max(scores, axis=0, keepdims=True))
            keep = jnp.exp2((old_max - new_max) * factor)
            weights = jnp.exp2(scores * factor - new_max * factor)
            new_sum = old_sum * keep + jnp.sum(weights, axis=0, keepdims=True)
            total = total * keep + rows_inner(kv_ref[keys, size:], weights.astype(BF))
            return new_max, new_sum, total

        state = (
            jnp.full((1, QUERY_BLOCK), MASKED, F32),
            jnp.zeros((1, QUERY_BLOCK), F32),
            jnp.zeros((size, QUERY_BLOCK), F32),
        )
        state = lax.fori_loop(begin, full_begin, functools.partial(step, True), state)
        state = lax.fori_loop(full_begin, full_end, functools.partial(step, False), state)
        state = lax.fori_loop(full_end, end, functools.partial(step, True), state)
        run_max, run_sum, total = state
        lse_ref[:, rows] = run_max * factor + jnp.log2(run_sum)
        attended = (total / run_sum).T
        o_ref[rows] = attended
        a_ref[rows] = (attended * jax.nn.sigmoid(logit_ref[rows])).astype(BF)


def attend_back_kernel(
    scale, start_sm, base_sm, q_ref, kv_ref, start_ref, logit_ref, o_ref, da_ref, lse_ref,
    dq_ref, dg_ref, dkv_ref, dk_acc, dv_acc,
):
    base = base_sm[0]
    size = q_ref.shape[1]
    factor = scale * math.log2(math.e)
    dk_acc[...] = jnp.zeros_like(dk_acc)
    dv_acc[...] = jnp.zeros_like(dv_acc)

    @pl.loop(0, q_ref.shape[0] // QUERY_BLOCK)
    def _(block):
        rows = pl.ds(pl.multiple_of(block * QUERY_BLOCK, QUERY_BLOCK), QUERY_BLOCK)
        queries = q_ref[rows]
        start_row = start_ref[:, rows]
        lse = lse_ref[:, rows]
        gate = jax.nn.sigmoid(logit_ref[rows])
        attended = o_ref[rows]
        d_mixed = da_ref[rows].astype(F32)
        d_attended = (d_mixed * gate).astype(BF)
        dg_ref[rows] = (d_mixed * attended * gate * (1.0 - gate)).astype(BF)
        delta = jnp.sum((d_attended.astype(F32) * attended).T, axis=0, keepdims=True)
        begin, full_begin, full_end, end = key_range(start_sm, base, block)

        def step(masked, at, d_queries):
            keys = pl.ds(pl.multiple_of(at * KEY_BLOCK, KEY_BLOCK), KEY_BLOCK)
            key_block = kv_ref[keys, :size]
            probs = jnp.exp2(cols_inner(key_block, queries) * factor - lse)
            if masked:
                allowed = allowed_pairs(at, start_row, base + block * QUERY_BLOCK)
                probs = jnp.where(allowed, probs, 0.0)
            d_probs = cols_inner(kv_ref[keys, size:], d_attended)
            d_scores = (probs * (d_probs - delta) * scale).astype(BF)
            dv_acc[keys] += matmul(probs.astype(BF), d_attended)
            dk_acc[keys] += matmul(d_scores, queries)
            return d_queries + rows_inner(key_block, d_scores)

        d_queries = jnp.zeros((size, QUERY_BLOCK), F32)
        d_queries = lax.fori_loop(begin, full_begin, functools.partial(step, True), d_queries)
        d_queries = lax.fori_loop(full_begin, full_end, functools.partial(step, False), d_queries)
        d_queries = lax.fori_loop(full_end, end, functools.partial(step, True), d_queries)
        dq_ref[rows] = d_queries.T.astype(BF)

    @pl.loop(0, kv_ref.shape[0] // KEY_BLOCK)
    def _(at):
        keys = pl.ds(pl.multiple_of(at * KEY_BLOCK, KEY_BLOCK), KEY_BLOCK)
        dk, dv = dk_acc[keys].astype(BF), dv_acc[keys].astype(BF)
        half = size // 2
        dkv_ref[keys, :size] = jnp.concatenate([dk[:, :half], dv[:, :half]], axis=1)
        dkv_ref[keys, size:] = jnp.concatenate([dk[:, half:], dv[:, half:]], axis=1)


def fold_kernel(
    batches, part_ref, own_ref, core_got, x_first, x_second, y_first, y_second, held, send_sem, recv_sem
):
    rows, size = own_ref.shape
    half = rows // 2
    others = batches // 2
    head = lax.axis_index("head")
    batch = lax.axis_index("batch")
    across, core, low = batch // 2, lax.rem(batch, 2), lax.rem(head, 2)
    twin = (across * 2 + 1 - core, head)
    mate = (batch, head + 1 - 2 * low)
    spots = [lax.rem(across + hop, others) for hop in range(others)]
    peers = [(spot * 2 + core, head) for spot in spots]
    greet((twin, mate, *peers[1:]))
    sems = (send_sem, recv_sem)
    slot = 0
    copies = []
    mine = pl.ds(pl.multiple_of(low * size, size), size)
    given = pl.ds(pl.multiple_of((1 - low) * size, size), size)
    top, bottom = pl.ds(0, half), pl.ds(half, half)

    def block(at, side):
        return pl.ds(pl.multiple_of((2 * at + side) * rows, rows), rows)

    def go(source, target, device):
        nonlocal slot
        copy = send(source, target, sems, slot, device)
        slot += 1
        copies.append(copy)
        return copy

    order = list(range(1, others)) + [0]
    first = [go(part_ref.at[block(spots[hop], 1 - core)], core_got.at[spots[hop]], twin) for hop in order]
    tops, bottoms = [], []
    for copy, hop in zip(first, order):
        copy.wait_recv()
        spot = spots[hop]
        core_got[spot] = add_low(core_got[spot], part_ref[block(spot, core)])
        bottoms.append(go(core_got.at[spot, bottom, given], y_first.at[spot], mate))
        if hop:
            tops.append(go(core_got.at[spot, top], x_first.at[hop - 1], peers[hop]))
    total = core_got[across, top].astype(F32)
    for hop in range(1, others):
        tops[hop - 1].wait_recv()
        total = total + x_first[hop - 1].astype(F32)
    held[...] = total.astype(BF)
    last = go(held.at[:, given], y_second, mate)
    ends = []
    for copy, hop in zip(bottoms, order):
        copy.wait_recv()
        spot = spots[hop]
        y_first[spot] = add_low(y_first[spot], core_got[spot, bottom, mine])
        if hop:
            ends.append(go(y_first.at[spot], x_second.at[hop - 1], peers[hop]))
    last.wait_recv()
    own_ref[top] = add_low(held[:, mine], y_second[...])
    total = y_first[across].astype(F32)
    for hop in range(1, others):
        ends[hop - 1].wait_recv()
        total = total + x_second[hop - 1].astype(F32)
    own_ref[bottom] = total.astype(BF)
    for copy in copies:
        copy.wait_send()


def fold(part, rows, collective_id):
    batches = lax.axis_size("batch")
    others = batches // 2
    size = part.shape[1] // 2
    half = rows // 2
    vmem = pl.BlockSpec(memory_space=pltpu.VMEM)
    sems = pltpu.SemaphoreType.DMA((4 * others,))
    return pl.pallas_call(
        functools.partial(fold_kernel, batches),
        out_shape=jax.ShapeDtypeStruct((rows, size), BF),
        in_specs=[vmem],
        out_specs=vmem,
        scratch_shapes=[
            pltpu.VMEM((others, rows, 2 * size), BF),
            pltpu.VMEM((others - 1, half, 2 * size), BF),
            pltpu.VMEM((others - 1, half, size), BF),
            pltpu.VMEM((others, half, size), BF),
            pltpu.VMEM((half, size), BF),
            pltpu.VMEM((half, 2 * size), BF),
            sems,
            sems,
        ],
        compiler_params=pltpu.CompilerParams(
            collective_id=collective_id, has_side_effects=True, vmem_limit_bytes=VMEM_LIMIT
        ),
        name="fold",
    )(part)


def local_call(kernel, scalars, arrays, outs, scratch, flops, name):
    vmem = pl.BlockSpec(memory_space=pltpu.VMEM)
    smem = pl.BlockSpec(memory_space=pltpu.SMEM)
    return pl.pallas_call(
        kernel,
        out_shape=outs,
        in_specs=[smem] * len(scalars) + [vmem] * len(arrays),
        out_specs=[vmem] * len(outs),
        scratch_shapes=scratch,
        compiler_params=pltpu.CompilerParams(vmem_limit_bytes=VMEM_LIMIT),
        cost_estimate=pl.CostEstimate(flops=flops, bytes_accessed=8 << 20, transcendentals=0),
        name=name,
    )(*scalars, *arrays)


def ring_routes(count):
    spots = [ring_head(at, count) for at in range(count)]
    right = [(spots[at], spots[(at + 1) % count]) for at in range(count)]
    left = [(spots[at], spots[at - 1]) for at in range(count)]
    return right, left


def add_low(one, other):
    return (one.astype(F32) + other.astype(F32)).astype(BF)


def flow_steps(part):
    count = lax.axis_size("head")
    place = ring_place(lax.axis_index("head"), count)
    right, left = ring_routes(count)
    rows, side = part.shape[0] // count, part.shape[1] // 2
    steps = count // 2

    def mine(owner):
        return lax.dynamic_slice_in_dim(part, lax.rem(owner + count, count) * rows, rows, 0)

    far = mine(place + steps)
    going, coming = far[:, :side], far[:, side:]
    for step in range(steps - 1):
        from_left = lax.ppermute(going, "head", right)
        from_right = lax.ppermute(coming, "head", left)
        one, two = mine(place + steps - 1 - step), mine(place - steps + 1 + step)
        if step == 0:
            going = jnp.concatenate([add_low(from_left, one[:, :side]), one[:, side:]], 1)
            coming = jnp.concatenate([two[:, :side], add_low(from_right, two[:, side:])], 1)
        else:
            going, coming = add_low(from_left, one), add_low(from_right, two)
        going, coming = yield going, coming
    from_left = lax.ppermute(going, "head", right)
    from_right = lax.ppermute(coming, "head", left)
    yield mine(place).astype(F32) + from_left.astype(F32) + from_right.astype(F32)


def flow_sum(part):
    flow = flow_steps(part)
    state = next(flow)
    while isinstance(state, tuple):
        state = flow.send(state)
    return state


def after(flow, state, array):
    array, going, coming = lax.optimization_barrier((array, *state))
    return array, flow.send((going, coming))


def flow_spread(own):
    count = lax.axis_size("head")
    place = ring_place(lax.axis_index("head"), count)
    right, left = ring_routes(count)
    side = own.shape[1] // 2
    going = coming = own
    pieces = [(0, own)]
    for step in range(1, count // 2):
        going = lax.ppermute(going, "head", right)
        coming = lax.ppermute(coming, "head", left)
        pieces += [(-step, going), (step, coming)]
    one = lax.ppermute(going[:, :side], "head", right)
    two = lax.ppermute(coming[:, side:], "head", left)
    pieces.append((count // 2, jnp.concatenate([one, two], 1)))
    whole = jnp.zeros((count * own.shape[0], own.shape[1]), own.dtype)
    for shift, piece in pieces:
        at = lax.rem(place + shift + count, count) * own.shape[0]
        whole = lax.dynamic_update_slice_in_dim(whole, piece, at, 0)
    return whole


def swap(block, axis, stride):
    return lax.ppermute(block, axis, [(at, at ^ stride) for at in range(lax.axis_size(axis))])


def halve_batch(block, rows):
    me = lax.axis_index("batch")
    stride = 1
    while stride < lax.axis_size("batch"):
        block = block.reshape(-1, 2, rows, block.shape[-1])
        bit = (me // stride) % 2
        keep = lax.dynamic_index_in_dim(block, bit, 1, keepdims=False)
        give = lax.dynamic_index_in_dim(block, 1 - bit, 1, keepdims=False)
        got = swap(give, "batch", stride)
        block = (keep.astype(F32) + got.astype(F32)).astype(block.dtype)
        stride *= 2
    return block.reshape(rows, -1)


def sum_heads(block):
    stride = 1
    while stride < lax.axis_size("head"):
        block = block + swap(block, "head", stride)
        stride *= 2
    return block


def matmul(left, right):
    return jnp.dot(left, right, preferred_element_type=F32)


def rows_inner(left, right):
    return lax.dot_general(left, right, (((0,), (0,)), ((), ())), preferred_element_type=F32)


def cols_inner(left, right):
    return lax.dot_general(left, right, (((1,), (1,)), ((), ())), preferred_element_type=F32)


def rms_scale(values):
    return lax.rsqrt(jnp.mean(values * values, axis=1, keepdims=True) + EPSILON)


def per_device(
    tokens,
    segment_ids,
    norm1_gain,
    w_query,
    w_key,
    w_value,
    w_gate,
    w_out,
    norm2_gain,
    w_mlp_gate,
    w_mlp_up,
    w_down,
    out_grad,
):
    heads = lax.axis_size("head")
    batches = lax.axis_size("batch")
    row_count, width = tokens.shape
    head_size = w_query.shape[1]
    half = w_key.shape[1]
    chunk = row_count // heads
    me = ring_place(lax.axis_index("head"), heads)
    scale_factor = 1.0 / math.sqrt(head_size)

    w_shard = jnp.concatenate([w_query, w_gate, w_key, w_value], axis=1)
    gains = jnp.concatenate([norm1_gain, norm2_gain]).reshape(-1, 128).astype(F32)
    normed_one, queries, gate_logit, kv_all, w_in, out_full, gains, seg_all = entry(
        tokens, w_shard, w_out, gains, segment_ids.reshape(-1, 128), 1
    )
    seg_all = seg_all.reshape(-1)
    gains = gains.reshape(batches, 2, -1).transpose(1, 0, 2).reshape(2, width)
    gain_one, gain_two = gains[0], gains[1]
    mgate_full = lax.all_gather(w_mlp_gate, "batch", axis=0, tiled=True)
    mup_full = lax.all_gather(w_mlp_up, "batch", axis=0, tiled=True)

    base = lax.axis_index("batch") * row_count
    ids = jnp.arange(DOCUMENTS, dtype=jnp.int32)
    below = jnp.sum((seg_all[None, :] < ids[:, None]).astype(jnp.int32), axis=1)
    starts = jnp.sum(jnp.where(segment_ids[None, :] == ids[:, None], below[:, None], 0), axis=0)
    scalars = (starts, base.reshape(1))
    pair_flops = 4 * row_count * kv_all.shape[0] * head_size
    attended, mixed, lse = local_call(
        functools.partial(attend_kernel, scale_factor),
        scalars,
        (queries, kv_all, starts[None], gate_logit),
        [
            jax.ShapeDtypeStruct((row_count, head_size), F32),
            jax.ShapeDtypeStruct((row_count, head_size), BF),
            jax.ShapeDtypeStruct((1, row_count), F32),
        ],
        [],
        pair_flops,
        "attend",
    )
    mixed_all, down_full = spread([mixed, w_down], (("head", "cols"), ("batch", "cols")), 2)
    normed_two, hidden, d_pre, mlp_part, resid_own, d_resid, d_resid_low, d_gain_two, d_mixed = mlp_back(
        tokens, mixed_all, out_grad, gain_two[None], out_full, mgate_full, mup_full, down_full, 3
    )
    mixed_own = lax.dynamic_slice_in_dim(mixed_all, me * chunk, chunk, 0)
    out_flow = flow_steps(mlp_part)
    out_state = next(out_flow)
    d_down = rows_inner(hidden, out_grad).astype(BF)
    normed_late, d_down, *out_state = lax.optimization_barrier((normed_two, d_down, *out_state))
    out_state = out_flow.send(tuple(out_state))
    d_mlp = rows_inner(normed_late, d_pre).astype(BF)
    d_mixed, d_mlp, *out_state = lax.optimization_barrier((d_mixed, d_mlp, *out_state))
    out_state = tuple(out_state)
    d_down = lax.psum_scatter(d_down, "batch", scatter_dimension=1, tiled=True).astype(F32)
    d_mlp = lax.psum_scatter(d_mlp, "batch", scatter_dimension=0, tiled=True).astype(F32)

    d_mixed, out_state = after(out_flow, out_state, d_mixed)
    d_queries, d_gate_logit, d_kv_all = local_call(
        functools.partial(attend_back_kernel, scale_factor),
        scalars,
        (queries, kv_all, starts[None], gate_logit, attended, d_mixed, lse),
        [
            jax.ShapeDtypeStruct((row_count, head_size), BF),
            jax.ShapeDtypeStruct((row_count, head_size), BF),
            jax.ShapeDtypeStruct(kv_all.shape, BF),
        ],
        [pltpu.VMEM((kv_all.shape[0], head_size), F32)] * 2,
        5 * pair_flops // 2,
        "attend_back",
    )
    d_kv_all, out_state = after(out_flow, out_state, d_kv_all)
    d_kv = fold(d_kv_all, row_count, 4)
    while isinstance(out_state, tuple):
        out_state = out_flow.send(out_state)
    out_total = out_state
    d_kv, out_total = lax.optimization_barrier((d_kv, out_total))
    output = flow_spread((resid_own + out_total).astype(BF))
    d_cat = jnp.concatenate([d_queries, d_gate_logit, d_kv], axis=1)
    d_out_part = rows_inner(mixed_own, d_resid_low).astype(BF)
    d_out_part = lax.psum_scatter(d_out_part, "batch", scatter_dimension=1, tiled=True)
    d_out = flow_sum(d_out_part)
    w_cat = w_in[:, : 3 * head_size]
    dn1_part = cols_inner(d_cat, w_cat).astype(BF)
    dn1 = flow_sum(dn1_part)
    inputs_own = lax.dynamic_slice_in_dim(tokens, me * chunk, chunk, 0).astype(F32)
    recip_in = rms_scale(inputs_own)
    d_gain_one = jnp.sum(dn1 * inputs_own * recip_in, axis=0)
    weighted_one = gain_one * dn1
    d_tokens = (
        d_resid
        + recip_in * weighted_one
        - inputs_own * recip_in**3 * jnp.mean(weighted_one * inputs_own, axis=1, keepdims=True)
    ).astype(BF)
    d_tokens = flow_spread(d_tokens)

    d_in = rows_inner(normed_one, d_cat).astype(BF)
    d_in = lax.psum_scatter(d_in, "batch", scatter_dimension=0, tiled=True).astype(F32)
    d_gains = jnp.stack([d_gain_one, d_gain_two[0]]).reshape(2, batches, -1).transpose(1, 0, 2)
    d_gains = sum_heads(halve_batch(d_gains.reshape(2 * batches, -1), 2))
    hidden_own = w_mlp_gate.shape[1]
    return (
        output,
        d_tokens,
        d_gains[0],
        d_in[:, :head_size],
        d_in[:, 2 * head_size : 2 * head_size + half],
        d_in[:, 2 * head_size + half :],
        d_in[:, head_size : 2 * head_size],
        d_out,
        d_gains[1],
        d_mlp[:, :hidden_own],
        d_mlp[:, hidden_own:],
        d_down,
    )


def solution(mesh):
    return jax.shard_map(
        per_device,
        mesh=mesh,
        in_specs=(
            P("batch", None),
            P("batch"),
            P("batch"),
            P("batch", "head"),
            P("batch", "head"),
            P("batch", "head"),
            P("batch", "head"),
            P("head", "batch"),
            P("batch"),
            P("batch", "head"),
            P("batch", "head"),
            P("head", "batch"),
            P("batch", None),
        ),
        out_specs=(
            P("batch", None),
            P("batch", None),
            P("batch"),
            P("batch", "head"),
            P("batch", "head"),
            P("batch", "head"),
            P("batch", "head"),
            P("head", "batch"),
            P("batch"),
            P("batch", "head"),
            P("batch", "head"),
            P("head", "batch"),
        ),
        check_vma=False,
    )
```

```python
import functools
import math

import jax
import jax.numpy as jnp
from jax import lax
from jax.experimental import pallas as pl
from jax.experimental.pallas import tpu as pltpu
from jax.sharding import PartitionSpec as P

EPSILON = 1e-06
MASKED = -1e30
DOCUMENTS = 7
BF = jnp.bfloat16
F32 = jnp.float32


MESH = pl.DeviceIdType.MESH
VMEM_LIMIT = 60 << 20


def ring_place(head, count):
    high, low = head // 2, head % 2
    return (1 - low) * high + low * (count - 1 - high)


def ring_head(place, count):
    low = place // (count // 2)
    high = (1 - low) * place + low * (count - 1 - place)
    return 2 * high + low


def ring_setup(count):
    batch = lax.axis_index("batch")
    place = ring_place(lax.axis_index("head"), count)
    right = (batch, ring_head(lax.rem(place + 1, count), count))
    left = (batch, ring_head(lax.rem(place + count - 1, count), count))
    return place, right, left


def greet(devices):
    barrier = pltpu.get_barrier_semaphore()
    for device in devices:
        pl.semaphore_signal(barrier, inc=1, device_id=device, device_id_type=MESH)
    pl.semaphore_wait(barrier, len(devices))


def send(source, target, sems, slot, device):
    copy = pltpu.make_async_remote_copy(
        src_ref=source,
        dst_ref=target,
        send_sem=sems[0].at[slot],
        recv_sem=sems[1].at[slot],
        device_id=device,
        device_id_type=MESH,
    )
    copy.start()
    return copy


def half_of(extent, flow):
    if extent[1] % 256:
        return (pl.ds(flow * (extent[0] // 2), extent[0] // 2), slice(None))
    return (slice(None), pl.ds(flow * (extent[1] // 2), extent[1] // 2))


def place_of(whole, own, chunk, form):
    rows, wide = own.shape[-2:]
    if form == "lead":
        return whole.at[chunk]
    if form == "rows":
        return whole.at[pl.ds(pl.multiple_of(chunk * rows, rows), rows)]
    return whole.at[:, pl.ds(pl.multiple_of(chunk * wide, wide), wide)]


def spread_kernel(count, batches, plans, *refs):
    steps = count // 2
    arrays = len(plans)
    own_refs, all_refs = refs[:arrays], refs[arrays : 2 * arrays]
    send_sem, recv_sem, local_sem = refs[2 * arrays :]
    place, right, left = ring_setup(count)
    head = lax.axis_index("head")
    batch = lax.axis_index("batch")
    across, core = batch // 2, lax.rem(batch, 2)
    others = batches // 2
    twin = (across * 2 + 1 - core, head)
    peers = [(lax.rem(across + hop, others) * 2 + core, head) for hop in range(1, others)]
    ring = any(axis == "head" for axis, _ in plans)
    grid = any(axis == "batch" for axis, _ in plans)
    greet((right, left) * ring + (twin, *peers) * grid)
    sems = (send_sem, recv_sem)
    slot = 0
    waiting, arriving, local = [], [], []

    def go(source, target, device):
        nonlocal slot
        copy = send(source, target, sems, slot, device)
        slot += 1
        waiting.append(copy)
        return copy

    onward = []
    for index, (axis, form) in enumerate(plans):
        own, whole = own_refs[index], all_refs[index]
        spot = place if axis == "head" else batch
        mine = place_of(whole, own, spot, form)
        copy = pltpu.make_async_copy(own, mine, local_sem.at[index])
        copy.start()
        local.append(copy)
        if axis == "batch":
            for hop, peer in enumerate(peers, 1):
                source = lax.rem(across + others - hop, others) * 2 + core
                onward.append((go(own, mine, peer), place_of(whole, own, source, form)))
            arriving.append(go(own, mine, twin))
    copies = [None] * (2 * arrays)
    for step in range(steps):
        for index, (axis, form) in enumerate(plans):
            if axis != "head":
                continue
            own = own_refs[index]
            for flow, chunk, device in ((0, place - step, right), (1, place + step, left)):
                at = 2 * index + flow
                if step:
                    copies[at].wait_recv()
                chunk = lax.rem(chunk + count, count)
                target = place_of(all_refs[index], own, chunk, form)
                source = target if step else own
                if step == steps - 1:
                    part = half_of(own.shape, flow)
                    source = source.at[part]
                    target = target.at[part]
                copies[at] = go(source, target, device)
        if step == 0 or not ring:
            for copy, block in onward:
                copy.wait_recv()
                arriving.append(go(block, block, twin))
            onward = []
    for copy in copies:
        if copy is not None:
            arriving.append(copy)
    for copy in arriving:
        copy.wait_recv()
    for copy in waiting:
        copy.wait_send()
    for copy in local:
        copy.wait()


def spread(arrays, plans, collective_id):
    count = lax.axis_size("head")
    batches = lax.axis_size("batch")
    shapes = []
    slots = 0
    for array, (axis, form) in zip(arrays, plans):
        many = count if axis == "head" else batches
        slots += count if axis == "head" else batches - 1
        if form == "lead":
            shapes.append((many, *array.shape))
        elif form == "rows":
            shapes.append((many * array.shape[0], array.shape[1]))
        else:
            shapes.append((array.shape[0], many * array.shape[1]))
    hbm = pl.BlockSpec(memory_space=pl.ANY)
    return pl.pallas_call(
        functools.partial(spread_kernel, count, batches, plans),
        out_shape=[jax.ShapeDtypeStruct(shape, a.dtype) for shape, a in zip(shapes, arrays)],
        in_specs=[hbm] * len(arrays),
        out_specs=[hbm] * len(arrays),
        scratch_shapes=[
            pltpu.SemaphoreType.DMA((slots,)),
            pltpu.SemaphoreType.DMA((slots,)),
            pltpu.SemaphoreType.DMA((len(arrays),)),
        ],
        compiler_params=pltpu.CompilerParams(
            collective_id=collective_id, has_side_effects=True, vmem_limit_bytes=VMEM_LIMIT
        ),
        name=f"spread_{collective_id}",
    )(*arrays)


def mlp_kernel(
    count, x_hbm, a_hbm, dy_hbm, gain_ref, out_w, gate_w, up_w, down_w,
    n2_hbm, hid_hbm, grad_hbm, mlp_hbm, h1_ref, dh1_ref, low_ref, dgain_ref, da_ref,
    x_s, a_s, dy_s, n2_s, hid_s, grad_s, mlp_s, h1_s, dy_own, da_part,
    right_part, left_part, right_got, left_got,
    in_sem, out_sem, send_sem, recv_sem, da_send, da_recv,
):
    steps = count // 2
    rows = x_hbm.shape[0] // count
    width = x_hbm.shape[1]
    hidden = gate_w.shape[1]
    side = width // 2
    tile = 256
    inner = 256 if hidden % 256 == 0 else 128
    size = da_ref.shape[1]
    place, right, left = ring_setup(count)

    def member(hop):
        spot = lax.rem(place + hop, count)
        return spot, (lax.axis_index("batch"), ring_head(spot, count))

    greet([member(hop)[1] for hop in range(1, count)])

    def owners(group):
        first = jnp.where(group == 0, 1, 0)
        one = lax.rem(place + steps - group, count)
        two = lax.rem(place - steps + group + first * steps + count, count)
        return one, two

    def span(owner):
        return pl.ds(pl.multiple_of(owner * rows, rows), rows)

    def loads(group, slot):
        return [
            pltpu.make_async_copy(
                source.at[span(owner)],
                target.at[slot, pl.ds(at * rows, rows)],
                in_sem.at[slot, 2 * index + at],
            )
            for index, (source, target) in enumerate(((x_hbm, x_s), (a_hbm, a_s), (dy_hbm, dy_s)))
            for at, owner in enumerate(owners(group))
        ]

    def stores(group, slot):
        return [
            pltpu.make_async_copy(
                source.at[slot, pl.ds(at * rows, rows)],
                target.at[span(owner)],
                out_sem.at[slot, 2 * index + at],
            )
            for index, (source, target) in enumerate(
                ((n2_s, n2_hbm), (hid_s, hid_hbm), (grad_s, grad_hbm), (mlp_s, mlp_hbm))
            )
            for at, owner in enumerate(owners(group))
        ]

    def passing(source, target, flow, step, device):
        return pltpu.make_async_remote_copy(
            src_ref=source,
            dst_ref=target,
            send_sem=send_sem.at[flow * steps + step],
            recv_sem=recv_sem.at[flow * steps + step],
            device_id=device,
            device_id_type=MESH,
        )

    def first_copies():
        ahead, behind = pl.ds(0, side), pl.ds(side, side)
        return (
            passing(right_part.at[0, :, ahead], right_got.at[0, :, ahead], 0, 0, right),
            passing(right_part.at[0, :, behind], left_got.at[0, :, behind], 1, 0, left),
        )

    def later_copies(step):
        return (
            passing(right_part.at[step], right_got.at[step], 0, step, right),
            passing(left_part.at[step], left_got.at[step], 1, step, left),
        )

    for copy in loads(0, 0):
        copy.start()

    @pl.loop(0, steps)
    def _(group):
        slot = lax.rem(group, 2)
        for copy in loads(group, slot):
            copy.wait()

        @pl.when(group + 1 < steps)
        def _():
            for copy in loads(group + 1, 1 - slot):
                copy.start()

        @pl.when(group >= 2)
        def _():
            for copy in stores(group - 2, slot):
                copy.wait()

        mixed = a_s[slot]

        def residual(at, total):
            cols = pl.ds(pl.multiple_of(at * tile, tile), tile)
            values = x_s[slot, :, cols].astype(F32) + matmul(mixed, out_w[:, cols])
            h1_s[:, cols] = values
            return total + jnp.sum(values * values, axis=1, keepdims=True)

        total = lax.fori_loop(0, width // tile, residual, jnp.zeros((2 * rows, 1), F32))
        scale = lax.rsqrt(total / width + EPSILON)

        @pl.when(group == 0)
        def _():
            h1_ref[...] = h1_s[pl.ds(rows, rows)]
            dy_own[...] = dy_s[slot, pl.ds(rows, rows)]

        @pl.loop(0, width // tile)
        def _(at):
            cols = pl.ds(pl.multiple_of(at * tile, tile), tile)
            n2_s[slot, :, cols] = (h1_s[:, cols] * scale * gain_ref[:, cols]).astype(BF)

        normed = n2_s[slot]
        dy = dy_s[slot]

        @pl.loop(0, hidden // inner)
        def _(at):
            cols = pl.ds(pl.multiple_of(at * inner, inner), inner)
            cols_up = pl.ds(pl.multiple_of(hidden + at * inner, inner), inner)
            gate = matmul(normed, gate_w[:, cols])
            up = matmul(normed, up_w[:, cols])
            d_hidden = cols_inner(dy, down_w[cols])
            sig = jax.nn.sigmoid(gate)
            silu = gate * sig
            hid_s[slot, :, cols] = (silu * up).astype(BF)
            grad_s[slot, :, cols] = (d_hidden * up * sig * (1.0 + gate * (1.0 - sig))).astype(BF)
            grad_s[slot, :, cols_up] = (d_hidden * silu).astype(BF)

        hid = hid_s[slot]
        d_gate = grad_s[slot, :, :hidden]
        d_up = grad_s[slot, :, hidden:]

        @pl.loop(0, width // tile)
        def _(at):
            cols = pl.ds(pl.multiple_of(at * tile, tile), tile)
            part = (cols_inner(d_gate, gate_w[cols]) + cols_inner(d_up, up_w[cols])).astype(BF)
            right_part[group, :, cols] = part[:rows]
            left_part[group, :, cols] = part[rows:]
            mlp_s[slot, :, cols] = matmul(hid, down_w[:, cols]).astype(BF)

        for copy in stores(group, slot):
            copy.start()

        @pl.when(group == 0)
        def _():
            for copy in first_copies():
                copy.start()

        @pl.when(group == 1)
        def _():
            one, two = first_copies()
            one.wait_recv()
            two.wait_recv()
            ahead, behind = pl.ds(0, side), pl.ds(side, side)
            right_part[1, :, ahead] = add_low(right_part[1, :, ahead], right_got[0, :, ahead])
            left_part[1, :, behind] = add_low(left_part[1, :, behind], left_got[0, :, behind])

        @pl.when(group >= 2)
        def _():
            one, two = later_copies(group - 1)
            one.wait_recv()
            right_part[group] = add_low(right_part[group], right_got[group - 1])
            two.wait_recv()
            left_part[group] = add_low(left_part[group], left_got[group - 1])

        @pl.when(group >= 1)
        def _():
            for copy in later_copies(group):
                copy.start()

    for copy in later_copies(steps - 1):
        copy.wait_recv()

    def tile_of(at):
        return pl.ds(pl.multiple_of(at * tile, tile), tile)

    def collect(at, state):
        squares, mean = state
        cols = tile_of(at)
        dn2 = (
            left_part[0, :, cols].astype(F32)
            + right_got[steps - 1, :, cols].astype(F32)
            + left_got[steps - 1, :, cols].astype(F32)
        )
        dh1_ref[:, cols] = dn2
        h1 = h1_ref[:, cols]
        squares = squares + jnp.sum(h1 * h1, axis=1, keepdims=True)
        return squares, mean + jnp.sum(gain_ref[:, cols] * dn2 * h1, axis=1, keepdims=True)

    zero = jnp.zeros((rows, 1), F32)
    squares, mean = lax.fori_loop(0, width // tile, collect, (zero, zero))
    scale_own = lax.rsqrt(squares / width + EPSILON)
    pull = scale_own * scale_own * scale_own * (mean / width)

    @pl.loop(0, width // tile)
    def _(at):
        cols = tile_of(at)
        dn2, h1 = dh1_ref[:, cols], h1_ref[:, cols]
        dgain_ref[:, cols] = jnp.sum(dn2 * h1 * scale_own, axis=0, keepdims=True)
        d_resid = dy_own[:, cols].astype(F32) + scale_own * (gain_ref[:, cols] * dn2) - h1 * pull
        dh1_ref[:, cols] = d_resid
        low_ref[:, cols] = d_resid.astype(BF)

    def da_copy(hop):
        return pltpu.make_async_remote_copy(
            src_ref=da_part.at[hop],
            dst_ref=da_ref.at[span(place)],
            send_sem=da_send.at[hop],
            recv_sem=da_recv.at[hop],
            device_id=member(hop)[1],
            device_id_type=MESH,
        )

    low = low_ref[...]

    @pl.loop(1, count)
    def _(hop):
        spot = member(hop)[0]
        part = cols_inner(low, out_w[pl.ds(pl.multiple_of(spot * size, size), size)])
        da_part[hop] = part.astype(BF)
        da_copy(hop).start()

    own_w = out_w[pl.ds(pl.multiple_of(place * size, size), size)]
    da_ref[span(place)] = cols_inner(low, own_w).astype(BF)

    @pl.loop(1, count)
    def _(hop):
        da_copy(hop).wait_recv()
        da_copy(hop).wait_send()

    for copy in first_copies():
        copy.wait_send()
    for step in range(1, steps):
        for copy in later_copies(step):
            copy.wait_send()
    for group in range(max(steps - 2, 0), steps):
        for copy in stores(group, group % 2):
            copy.wait()


def mlp_back(tokens, mixed, dy, gain, out_w, gate_w, up_w, down_w, collective_id):
    count = lax.axis_size("head")
    total, width = tokens.shape
    hidden = gate_w.shape[1]
    rows, steps = total // count, count // 2
    size = mixed.shape[1] // count
    vmem = pl.BlockSpec(memory_space=pltpu.VMEM)
    hbm = pl.BlockSpec(memory_space=pl.ANY)

    def slots(wide, dtype=BF):
        return pltpu.VMEM((2, 2 * rows, wide), dtype)

    part = pltpu.VMEM((steps, rows, width), BF)
    flops = 2 * total * width * (mixed.shape[1] + 6 * hidden)
    return pl.pallas_call(
        functools.partial(mlp_kernel, count),
        out_shape=[
            jax.ShapeDtypeStruct((total, width), BF),
            jax.ShapeDtypeStruct((total, hidden), BF),
            jax.ShapeDtypeStruct((total, 2 * hidden), BF),
            jax.ShapeDtypeStruct((total, width), BF),
            jax.ShapeDtypeStruct((rows, width), F32),
            jax.ShapeDtypeStruct((rows, width), F32),
            jax.ShapeDtypeStruct((rows, width), BF),
            jax.ShapeDtypeStruct((1, width), F32),
            jax.ShapeDtypeStruct((total, size), BF),
        ],
        in_specs=[hbm] * 3 + [vmem] * 5,
        out_specs=[hbm] * 4 + [vmem] * 5,
        scratch_shapes=[
            slots(width), slots(mixed.shape[1]), slots(width), slots(width), slots(hidden),
            slots(2 * hidden), slots(width), pltpu.VMEM((2 * rows, width), F32),
            pltpu.VMEM((rows, width), BF), pltpu.VMEM((count, rows, size), BF),
            part, part, part, part,
            pltpu.SemaphoreType.DMA((2, 6)), pltpu.SemaphoreType.DMA((2, 8)),
            pltpu.SemaphoreType.DMA((count,)), pltpu.SemaphoreType.DMA((count,)),
            pltpu.SemaphoreType.DMA((count,)), pltpu.SemaphoreType.DMA((count,)),
        ],
        compiler_params=pltpu.CompilerParams(
            collective_id=collective_id, has_side_effects=True, vmem_limit_bytes=VMEM_LIMIT
        ),
        cost_estimate=pl.CostEstimate(flops=flops, bytes_accessed=40 << 20, transcendentals=0),
        name="mlp_back",
    )(tokens, mixed, dy, gain, out_w, gate_w, up_w, down_w)


def entry_kernel(
    count, batches, x_ref, w_ref, out_ref, gain_ref, seg_ref, down_ref,
    n1_ref, q_ref, logit_ref, kv_ref, w_all, out_all, gain_all, seg_all, down_all,
    send_sem, recv_sem, local_sem,
):
    steps = count // 2
    others = batches // 2
    rows, width = x_ref.shape
    depth = w_ref.shape[0]
    size, wide = out_ref.shape
    block = 256
    place, right, left = ring_setup(count)
    head = lax.axis_index("head")
    batch = lax.axis_index("batch")
    across, core, low = batch // 2, lax.rem(batch, 2), lax.rem(head, 2)
    twin = (across * 2 + 1 - core, head)
    mate = (batch, head + 1 - 2 * low)
    spots = [lax.rem(across + hop, others) for hop in range(others)]
    backs = [lax.rem(across + others - hop, others) for hop in range(others)]
    peers = [(spot * 2 + core, head) for spot in spots]
    far_peers = [(spot * 2 + 1 - core, head) for spot in spots]
    greet((twin, mate, right, left, *peers[1:], *far_peers[1:]))
    sems = (send_sem, recv_sem)
    slot = 0
    copies = []

    def go(source, target, device):
        nonlocal slot
        copy = send(source, target, sems, slot, device)
        slot += 1
        copies.append(copy)
        return copy

    def part(at, extent):
        return pl.ds(pl.multiple_of(at * extent, extent), extent)

    def both(view, own):
        out = [go(own, view(batch), peers[hop]) for hop in range(1, others)]
        return out, [go(own, view(batch), twin)]

    def pass_on(view, arrived):
        out = []
        for hop in range(1, others):
            arrived[hop - 1].wait_recv()
            there = view(backs[hop] * 2 + core)
            out.append(go(there, there, twin))
        return out

    local = []

    def stay(source, target):
        copy = pltpu.make_async_copy(source, target, local_sem.at[len(local)])
        copy.start()
        local.append(copy)

    def main_view(at):
        return w_all.at[part(at, depth), pl.ds(0, 3 * size)]

    def mate_view(at):
        return w_all.at[part(at, depth), pl.ds(3 * size, size)]

    def out_view(chunk, at):
        return out_all.at[part(chunk, size), part(at, wide)]

    small = []
    for own, whole in ((gain_ref, gain_all), (seg_ref, seg_all)):
        for device in (twin, *peers[1:], *far_peers[1:]):
            small.append(go(own, whole.at[batch], device))
        stay(own, whole.at[batch])
    from_mate = go(w_ref.at[:, pl.ds(2 * size, size)], mate_view(batch), mate)
    main_out, main_twin = both(main_view, w_ref)
    stay(w_ref, main_view(batch))
    out_peers = [go(out_ref, out_view(place, batch), peers[hop]) for hop in range(1, others)]
    stay(out_ref, out_view(place, batch))
    flows = [[None, None] for _ in range(others)]

    def ring(step):
        for hop in range(others):
            lane = spots[0] if hop == 0 else backs[hop]
            at = lane * 2 + core
            if step == 0 and hop:
                out_peers[hop - 1].wait_recv()
            for flow, chunk, device in ((0, place - step, right), (1, place + step, left)):
                if step:
                    flows[hop][flow].wait_recv()
                target = out_view(lax.rem(chunk + count, count), at)
                source = out_ref if step == 0 and hop == 0 else target
                if step == steps - 1:
                    cut = (pl.ds(flow * (size // 2), size // 2), slice(None))
                    source, target = source.at[cut], target.at[cut]
                flows[hop][flow] = go(source, target, device)

    for copy in small:
        copy.wait_recv()
    for copy in local[:2]:
        copy.wait()

    def normalize(at):
        here = part(at, block)

        def squares(tile, total):
            values = x_ref[here, part(tile, 256)].astype(F32)
            return total + jnp.sum(values * values, axis=1, keepdims=True)

        total = lax.fori_loop(0, width // 256, squares, jnp.zeros((block, 1), F32))
        scale = lax.rsqrt(total / width + EPSILON)

        @pl.loop(0, batches)
        def _(owner):
            for tile in range(depth // 128):
                cols = pl.ds(pl.multiple_of(owner * depth + tile * 128, 128), 128)
                values = x_ref[here, cols].astype(F32) * scale
                n1_ref[here, cols] = (values * gain_all[owner, pl.ds(tile, 1)]).astype(BF)

    blocks = rows // block
    middle = blocks // 2

    @pl.loop(0, middle)
    def _(at):
        normalize(at)

    from_mate.wait_recv()
    mate_out, mate_twin = both(mate_view, mate_view(batch))
    ring(0)

    @pl.loop(middle, blocks)
    def _(at):
        normalize(at)

    main_passed = pass_on(main_view, main_out)
    mate_passed = pass_on(mate_view, mate_out)
    for copy in (*main_twin, *mate_twin, *main_passed, *mate_passed):
        copy.wait_recv()
    for copy in local[2:]:
        copy.wait()

    def kv_view(at):
        return kv_ref.at[part(at, rows)]

    def down_view(at):
        return down_all.at[:, part(at, down_ref.shape[1])]

    down_out, down_twin = both(down_view, down_ref)
    stay(down_ref, down_view(batch))

    @pl.loop(0, blocks)
    def _(at):
        here = part(at, block)
        values = matmul(n1_ref[here], w_all[:, pl.ds(2 * size, 2 * size)])
        one, two = values[:, :size], values[:, size:]
        first = jnp.where(low == 0, one, two).astype(BF)
        second = jnp.where(low == 0, two, one).astype(BF)
        half = size // 2
        there = pl.ds(pl.multiple_of(batch * rows + at * block, block), block)
        kv_ref[there, pl.ds(0, size)] = jnp.concatenate([first[:, :half], second[:, :half]], 1)
        kv_ref[there, pl.ds(size, size)] = jnp.concatenate([first[:, half:], second[:, half:]], 1)

    kv_out, kv_twin = both(kv_view, kv_view(batch))
    ring(1)

    @pl.loop(0, blocks)
    def _(at):
        here = part(at, block)
        values = matmul(n1_ref[here], w_all[:, pl.ds(0, 2 * size)])
        q_ref[here] = values[:, :size].astype(BF)
        logit_ref[here] = values[:, size:]

    for step in range(2, steps):
        ring(step)
    kv_passed = pass_on(kv_view, kv_out)
    down_passed = pass_on(down_view, down_out)
    local[-1].wait()
    for pair in flows:
        for copy in pair:
            copy.wait_recv()
    swaps = []
    for hop in range(others):
        there = out_all.at[:, part(spots[hop] * 2 + core, wide)]
        swaps.append(go(there, there, twin))
    for copy in (*kv_twin, *kv_passed, *swaps, *down_twin, *down_passed):
        copy.wait_recv()
    for copy in copies:
        copy.wait_send()


def entry(tokens, w_shard, w_out, gains, segments, w_down, collective_id):
    count = lax.axis_size("head")
    batches = lax.axis_size("batch")
    others = batches // 2
    rows, width = tokens.shape
    size, wide = w_out.shape
    vmem = pl.BlockSpec(memory_space=pltpu.VMEM)
    hbm = pl.BlockSpec(memory_space=pl.ANY)
    slots = 6 * batches + others * (count + 3)
    sems = pltpu.SemaphoreType.DMA((slots,))
    return pl.pallas_call(
        functools.partial(entry_kernel, count, batches),
        out_shape=[
            jax.ShapeDtypeStruct((rows, width), BF),
            jax.ShapeDtypeStruct((rows, size), BF),
            jax.ShapeDtypeStruct((rows, size), F32),
            jax.ShapeDtypeStruct((batches * rows, 2 * size), BF),
            jax.ShapeDtypeStruct((width, 4 * size), BF),
            jax.ShapeDtypeStruct((count * size, batches * wide), BF),
            jax.ShapeDtypeStruct((batches, *gains.shape), F32),
            jax.ShapeDtypeStruct((batches, *segments.shape), jnp.int32),
            jax.ShapeDtypeStruct((w_down.shape[0], batches * w_down.shape[1]), BF),
        ],
        in_specs=[vmem] * 5 + [hbm],
        out_specs=[vmem] * 8 + [hbm],
        scratch_shapes=[sems, sems, pltpu.SemaphoreType.DMA((5,))],
        compiler_params=pltpu.CompilerParams(
            collective_id=collective_id, has_side_effects=True, vmem_limit_bytes=VMEM_LIMIT
        ),
        name="entry",
    )(tokens, w_shard, w_out, gains, segments, w_down)


KEY_BLOCK = 512
QUERY_BLOCK = 256


def key_range(start_ref, base, query_block):
    first = query_block * QUERY_BLOCK
    lowest = start_ref[first]
    highest = start_ref[first + QUERY_BLOCK - 1]
    begin = lowest // KEY_BLOCK
    end = (base + first + QUERY_BLOCK - 1) // KEY_BLOCK + 1
    full_begin = jnp.minimum((highest + KEY_BLOCK - 1) // KEY_BLOCK, end)
    full_end = jnp.maximum((base + first + 1) // KEY_BLOCK, full_begin)
    return begin, full_begin, full_end, end


def allowed_pairs(key_block, start_row, base_row):
    shape = (KEY_BLOCK, QUERY_BLOCK)
    key_pos = key_block * KEY_BLOCK + lax.broadcasted_iota(jnp.int32, shape, 0)
    query_pos = base_row + lax.broadcasted_iota(jnp.int32, shape, 1)
    return (key_pos >= start_row) & (key_pos <= query_pos)


def attend_kernel(
    scale, start_sm, base_sm, q_ref, kv_ref, start_ref, logit_ref, o_ref, a_ref, lse_ref
):
    base = base_sm[0]
    size = q_ref.shape[1]
    factor = scale * math.log2(math.e)

    @pl.loop(0, q_ref.shape[0] // QUERY_BLOCK)
    def _(block):
        rows = pl.ds(pl.multiple_of(block * QUERY_BLOCK, QUERY_BLOCK), QUERY_BLOCK)
        queries = q_ref[rows]
        start_row = start_ref[:, rows]
        begin, full_begin, full_end, end = key_range(start_sm, base, block)

        def step(masked, at, state):
            old_max, old_sum, total = state
            keys = pl.ds(pl.multiple_of(at * KEY_BLOCK, KEY_BLOCK), KEY_BLOCK)
            scores = cols_inner(kv_ref[keys, :size], queries)
            if masked:
                allowed = allowed_pairs(at, start_row, base + block * QUERY_BLOCK)
                scores = jnp.where(allowed, scores, MASKED)
            new_max = jnp.maximum(old_max, jnp.max(scores, axis=0, keepdims=True))
            keep = jnp.exp2((old_max - new_max) * factor)
            weights = jnp.exp2(scores * factor - new_max * factor)
            new_sum = old_sum * keep + jnp.sum(weights, axis=0, keepdims=True)
            total = total * keep + rows_inner(kv_ref[keys, size:], weights.astype(BF))
            return new_max, new_sum, total

        state = (
            jnp.full((1, QUERY_BLOCK), MASKED, F32),
            jnp.zeros((1, QUERY_BLOCK), F32),
            jnp.zeros((size, QUERY_BLOCK), F32),
        )
        state = lax.fori_loop(begin, full_begin, functools.partial(step, True), state)
        state = lax.fori_loop(full_begin, full_end, functools.partial(step, False), state)
        state = lax.fori_loop(full_end, end, functools.partial(step, True), state)
        run_max, run_sum, total = state
        lse_ref[:, rows] = run_max * factor + jnp.log2(run_sum)
        attended = (total / run_sum).T
        o_ref[rows] = attended
        a_ref[rows] = (attended * jax.nn.sigmoid(logit_ref[rows])).astype(BF)


def attend_back_kernel(
    scale, start_sm, base_sm, q_ref, kv_ref, start_ref, logit_ref, o_ref, da_ref, lse_ref,
    dq_ref, dg_ref, dkv_ref, dk_acc, dv_acc,
):
    base = base_sm[0]
    size = q_ref.shape[1]
    factor = scale * math.log2(math.e)
    dk_acc[...] = jnp.zeros_like(dk_acc)
    dv_acc[...] = jnp.zeros_like(dv_acc)

    @pl.loop(0, q_ref.shape[0] // QUERY_BLOCK)
    def _(block):
        rows = pl.ds(pl.multiple_of(block * QUERY_BLOCK, QUERY_BLOCK), QUERY_BLOCK)
        queries = q_ref[rows]
        start_row = start_ref[:, rows]
        lse = lse_ref[:, rows]
        gate = jax.nn.sigmoid(logit_ref[rows])
        attended = o_ref[rows]
        d_mixed = da_ref[rows].astype(F32)
        d_attended = (d_mixed * gate).astype(BF)
        dg_ref[rows] = (d_mixed * attended * gate * (1.0 - gate)).astype(BF)
        delta = jnp.sum((d_attended.astype(F32) * attended).T, axis=0, keepdims=True)
        begin, full_begin, full_end, end = key_range(start_sm, base, block)

        def step(masked, at, d_queries):
            keys = pl.ds(pl.multiple_of(at * KEY_BLOCK, KEY_BLOCK), KEY_BLOCK)
            key_block = kv_ref[keys, :size]
            probs = jnp.exp2(cols_inner(key_block, queries) * factor - lse)
            if masked:
                allowed = allowed_pairs(at, start_row, base + block * QUERY_BLOCK)
                probs = jnp.where(allowed, probs, 0.0)
            d_probs = cols_inner(kv_ref[keys, size:], d_attended)
            d_scores = (probs * (d_probs - delta) * scale).astype(BF)
            dv_acc[keys] += matmul(probs.astype(BF), d_attended)
            dk_acc[keys] += matmul(d_scores, queries)
            return d_queries + rows_inner(key_block, d_scores)

        d_queries = jnp.zeros((size, QUERY_BLOCK), F32)
        d_queries = lax.fori_loop(begin, full_begin, functools.partial(step, True), d_queries)
        d_queries = lax.fori_loop(full_begin, full_end, functools.partial(step, False), d_queries)
        d_queries = lax.fori_loop(full_end, end, functools.partial(step, True), d_queries)
        dq_ref[rows] = d_queries.T.astype(BF)

    @pl.loop(0, kv_ref.shape[0] // KEY_BLOCK)
    def _(at):
        keys = pl.ds(pl.multiple_of(at * KEY_BLOCK, KEY_BLOCK), KEY_BLOCK)
        dk, dv = dk_acc[keys].astype(BF), dv_acc[keys].astype(BF)
        half = size // 2
        dkv_ref[keys, :size] = jnp.concatenate([dk[:, :half], dv[:, :half]], axis=1)
        dkv_ref[keys, size:] = jnp.concatenate([dk[:, half:], dv[:, half:]], axis=1)


def fold_kernel(
    batches, part_ref, own_ref, core_got, x_first, x_second, y_first, y_second, held, send_sem, recv_sem
):
    rows, size = own_ref.shape
    half = rows // 2
    others = batches // 2
    head = lax.axis_index("head")
    batch = lax.axis_index("batch")
    across, core, low = batch // 2, lax.rem(batch, 2), lax.rem(head, 2)
    twin = (across * 2 + 1 - core, head)
    mate = (batch, head + 1 - 2 * low)
    spots = [lax.rem(across + hop, others) for hop in range(others)]
    peers = [(spot * 2 + core, head) for spot in spots]
    greet((twin, mate, *peers[1:]))
    sems = (send_sem, recv_sem)
    slot = 0
    copies = []
    mine = pl.ds(pl.multiple_of(low * size, size), size)
    given = pl.ds(pl.multiple_of((1 - low) * size, size), size)
    top, bottom = pl.ds(0, half), pl.ds(half, half)

    def block(at, side):
        return pl.ds(pl.multiple_of((2 * at + side) * rows, rows), rows)

    def go(source, target, device):
        nonlocal slot
        copy = send(source, target, sems, slot, device)
        slot += 1
        copies.append(copy)
        return copy

    order = list(range(1, others)) + [0]
    first = [go(part_ref.at[block(spots[hop], 1 - core)], core_got.at[spots[hop]], twin) for hop in order]
    tops, bottoms = [], []
    for copy, hop in zip(first, order):
        copy.wait_recv()
        spot = spots[hop]
        core_got[spot] = add_low(core_got[spot], part_ref[block(spot, core)])
        bottoms.append(go(core_got.at[spot, bottom, given], y_first.at[spot], mate))
        if hop:
            tops.append(go(core_got.at[spot, top], x_first.at[hop - 1], peers[hop]))
    total = core_got[across, top].astype(F32)
    for hop in range(1, others):
        tops[hop - 1].wait_recv()
        total = total + x_first[hop - 1].astype(F32)
    held[...] = total.astype(BF)
    last = go(held.at[:, given], y_second, mate)
    ends = []
    for copy, hop in zip(bottoms, order):
        copy.wait_recv()
        spot = spots[hop]
        y_first[spot] = add_low(y_first[spot], core_got[spot, bottom, mine])
        if hop:
            ends.append(go(y_first.at[spot], x_second.at[hop - 1], peers[hop]))
    last.wait_recv()
    own_ref[top] = add_low(held[:, mine], y_second[...])
    total = y_first[across].astype(F32)
    for hop in range(1, others):
        ends[hop - 1].wait_recv()
        total = total + x_second[hop - 1].astype(F32)
    own_ref[bottom] = total.astype(BF)
    for copy in copies:
        copy.wait_send()


def fold(part, rows, collective_id):
    batches = lax.axis_size("batch")
    others = batches // 2
    size = part.shape[1] // 2
    half = rows // 2
    vmem = pl.BlockSpec(memory_space=pltpu.VMEM)
    sems = pltpu.SemaphoreType.DMA((4 * others,))
    return pl.pallas_call(
        functools.partial(fold_kernel, batches),
        out_shape=jax.ShapeDtypeStruct((rows, size), BF),
        in_specs=[vmem],
        out_specs=vmem,
        scratch_shapes=[
            pltpu.VMEM((others, rows, 2 * size), BF),
            pltpu.VMEM((others - 1, half, 2 * size), BF),
            pltpu.VMEM((others - 1, half, size), BF),
            pltpu.VMEM((others, half, size), BF),
            pltpu.VMEM((half, size), BF),
            pltpu.VMEM((half, 2 * size), BF),
            sems,
            sems,
        ],
        compiler_params=pltpu.CompilerParams(
            collective_id=collective_id, has_side_effects=True, vmem_limit_bytes=VMEM_LIMIT
        ),
        name="fold",
    )(part)


def local_call(kernel, scalars, arrays, outs, scratch, flops, name):
    vmem = pl.BlockSpec(memory_space=pltpu.VMEM)
    smem = pl.BlockSpec(memory_space=pltpu.SMEM)
    return pl.pallas_call(
        kernel,
        out_shape=outs,
        in_specs=[smem] * len(scalars) + [vmem] * len(arrays),
        out_specs=[vmem] * len(outs),
        scratch_shapes=scratch,
        compiler_params=pltpu.CompilerParams(vmem_limit_bytes=VMEM_LIMIT),
        cost_estimate=pl.CostEstimate(flops=flops, bytes_accessed=8 << 20, transcendentals=0),
        name=name,
    )(*scalars, *arrays)


def ring_routes(count):
    spots = [ring_head(at, count) for at in range(count)]
    right = [(spots[at], spots[(at + 1) % count]) for at in range(count)]
    left = [(spots[at], spots[at - 1]) for at in range(count)]
    return right, left


def add_low(one, other):
    return (one.astype(F32) + other.astype(F32)).astype(BF)


def flow_steps(part):
    count = lax.axis_size("head")
    place = ring_place(lax.axis_index("head"), count)
    right, left = ring_routes(count)
    rows, side = part.shape[0] // count, part.shape[1] // 2
    steps = count // 2

    def mine(owner):
        return lax.dynamic_slice_in_dim(part, lax.rem(owner + count, count) * rows, rows, 0)

    far = mine(place + steps)
    going, coming = far[:, :side], far[:, side:]
    for step in range(steps - 1):
        from_left = lax.ppermute(going, "head", right)
        from_right = lax.ppermute(coming, "head", left)
        one, two = mine(place + steps - 1 - step), mine(place - steps + 1 + step)
        if step == 0:
            going = jnp.concatenate([add_low(from_left, one[:, :side]), one[:, side:]], 1)
            coming = jnp.concatenate([two[:, :side], add_low(from_right, two[:, side:])], 1)
        else:
            going, coming = add_low(from_left, one), add_low(from_right, two)
        going, coming = yield going, coming
    from_left = lax.ppermute(going, "head", right)
    from_right = lax.ppermute(coming, "head", left)
    yield mine(place).astype(F32) + from_left.astype(F32) + from_right.astype(F32)


def flow_sum(part):
    flow = flow_steps(part)
    state = next(flow)
    while isinstance(state, tuple):
        state = flow.send(state)
    return state


def after(flow, state, array):
    array, going, coming = lax.optimization_barrier((array, *state))
    return array, flow.send((going, coming))


def flow_spread(own):
    count = lax.axis_size("head")
    place = ring_place(lax.axis_index("head"), count)
    right, left = ring_routes(count)
    side = own.shape[1] // 2
    going = coming = own
    pieces = [(0, own)]
    for step in range(1, count // 2):
        going = lax.ppermute(going, "head", right)
        coming = lax.ppermute(coming, "head", left)
        pieces += [(-step, going), (step, coming)]
    one = lax.ppermute(going[:, :side], "head", right)
    two = lax.ppermute(coming[:, side:], "head", left)
    pieces.append((count // 2, jnp.concatenate([one, two], 1)))
    whole = jnp.zeros((count * own.shape[0], own.shape[1]), own.dtype)
    for shift, piece in pieces:
        at = lax.rem(place + shift + count, count) * own.shape[0]
        whole = lax.dynamic_update_slice_in_dim(whole, piece, at, 0)
    return whole


def swap(block, axis, stride):
    return lax.ppermute(block, axis, [(at, at ^ stride) for at in range(lax.axis_size(axis))])


def halve_batch(block, rows):
    me = lax.axis_index("batch")
    stride = 1
    while stride < lax.axis_size("batch"):
        block = block.reshape(-1, 2, rows, block.shape[-1])
        bit = (me // stride) % 2
        keep = lax.dynamic_index_in_dim(block, bit, 1, keepdims=False)
        give = lax.dynamic_index_in_dim(block, 1 - bit, 1, keepdims=False)
        got = swap(give, "batch", stride)
        block = (keep.astype(F32) + got.astype(F32)).astype(block.dtype)
        stride *= 2
    return block.reshape(rows, -1)


def sum_heads(block):
    stride = 1
    while stride < lax.axis_size("head"):
        block = block + swap(block, "head", stride)
        stride *= 2
    return block


def matmul(left, right):
    return jnp.dot(left, right, preferred_element_type=F32)


def rows_inner(left, right):
    return lax.dot_general(left, right, (((0,), (0,)), ((), ())), preferred_element_type=F32)


def cols_inner(left, right):
    return lax.dot_general(left, right, (((1,), (1,)), ((), ())), preferred_element_type=F32)


def rms_scale(values):
    return lax.rsqrt(jnp.mean(values * values, axis=1, keepdims=True) + EPSILON)


def per_device(
    tokens,
    segment_ids,
    norm1_gain,
    w_query,
    w_key,
    w_value,
    w_gate,
    w_out,
    norm2_gain,
    w_mlp_gate,
    w_mlp_up,
    w_down,
    out_grad,
):
    heads = lax.axis_size("head")
    batches = lax.axis_size("batch")
    row_count, width = tokens.shape
    head_size = w_query.shape[1]
    half = w_key.shape[1]
    chunk = row_count // heads
    me = ring_place(lax.axis_index("head"), heads)
    scale_factor = 1.0 / math.sqrt(head_size)

    w_shard = jnp.concatenate([w_query, w_gate, w_key, w_value], axis=1)
    gains = jnp.concatenate([norm1_gain, norm2_gain]).reshape(-1, 128).astype(F32)
    normed_one, queries, gate_logit, kv_all, w_in, out_full, gains, seg_all, down_full = entry(
        tokens, w_shard, w_out, gains, segment_ids.reshape(-1, 128), w_down, 1
    )
    gains, w_mlp_gate, w_mlp_up = lax.optimization_barrier((gains, w_mlp_gate, w_mlp_up))
    seg_all = seg_all.reshape(-1)
    gains = gains.reshape(batches, 2, -1).transpose(1, 0, 2).reshape(2, width)
    gain_one, gain_two = gains[0], gains[1]
    mgate_full = lax.all_gather(w_mlp_gate, "batch", axis=0, tiled=True)
    mup_full = lax.all_gather(w_mlp_up, "batch", axis=0, tiled=True)

    base = lax.axis_index("batch") * row_count
    ids = jnp.arange(DOCUMENTS, dtype=jnp.int32)
    below = jnp.sum((seg_all[None, :] < ids[:, None]).astype(jnp.int32), axis=1)
    starts = jnp.sum(jnp.where(segment_ids[None, :] == ids[:, None], below[:, None], 0), axis=0)
    scalars = (starts, base.reshape(1))
    pair_flops = 4 * row_count * kv_all.shape[0] * head_size
    attended, mixed, lse = local_call(
        functools.partial(attend_kernel, scale_factor),
        scalars,
        (queries, kv_all, starts[None], gate_logit),
        [
            jax.ShapeDtypeStruct((row_count, head_size), F32),
            jax.ShapeDtypeStruct((row_count, head_size), BF),
            jax.ShapeDtypeStruct((1, row_count), F32),
        ],
        [],
        pair_flops,
        "attend",
    )
    (mixed_all,) = spread([mixed], (("head", "cols"),), 2)
    normed_two, hidden, d_pre, mlp_part, resid_own, d_resid, d_resid_low, d_gain_two, d_mixed = mlp_back(
        tokens, mixed_all, out_grad, gain_two[None], out_full, mgate_full, mup_full, down_full, 3
    )
    mixed_own = lax.dynamic_slice_in_dim(mixed_all, me * chunk, chunk, 0)
    out_flow = flow_steps(mlp_part)
    out_state = next(out_flow)
    d_down = rows_inner(hidden, out_grad).astype(BF)
    normed_late, d_down, *out_state = lax.optimization_barrier((normed_two, d_down, *out_state))
    out_state = out_flow.send(tuple(out_state))
    d_mlp = rows_inner(normed_late, d_pre).astype(BF)
    d_mixed, d_mlp, *out_state = lax.optimization_barrier((d_mixed, d_mlp, *out_state))
    out_state = tuple(out_state)
    d_down = lax.psum_scatter(d_down, "batch", scatter_dimension=1, tiled=True).astype(F32)
    d_mlp = lax.psum_scatter(d_mlp, "batch", scatter_dimension=0, tiled=True).astype(F32)

    d_mixed, out_state = after(out_flow, out_state, d_mixed)
    d_queries, d_gate_logit, d_kv_all = local_call(
        functools.partial(attend_back_kernel, scale_factor),
        scalars,
        (queries, kv_all, starts[None], gate_logit, attended, d_mixed, lse),
        [
            jax.ShapeDtypeStruct((row_count, head_size), BF),
            jax.ShapeDtypeStruct((row_count, head_size), BF),
            jax.ShapeDtypeStruct(kv_all.shape, BF),
        ],
        [pltpu.VMEM((kv_all.shape[0], head_size), F32)] * 2,
        5 * pair_flops // 2,
        "attend_back",
    )
    d_kv_all, out_state = after(out_flow, out_state, d_kv_all)
    d_kv = fold(d_kv_all, row_count, 4)
    while isinstance(out_state, tuple):
        out_state = out_flow.send(out_state)
    out_total = out_state
    d_kv, out_total = lax.optimization_barrier((d_kv, out_total))
    output = flow_spread((resid_own + out_total).astype(BF))
    d_cat = jnp.concatenate([d_queries, d_gate_logit, d_kv], axis=1)
    d_out_part = rows_inner(mixed_own, d_resid_low).astype(BF)
    d_out_part = lax.psum_scatter(d_out_part, "batch", scatter_dimension=1, tiled=True)
    d_out = flow_sum(d_out_part)
    w_cat = w_in[:, : 3 * head_size]
    dn1_part = cols_inner(d_cat, w_cat).astype(BF)
    dn1 = flow_sum(dn1_part)
    inputs_own = lax.dynamic_slice_in_dim(tokens, me * chunk, chunk, 0).astype(F32)
    recip_in = rms_scale(inputs_own)
    d_gain_one = jnp.sum(dn1 * inputs_own * recip_in, axis=0)
    weighted_one = gain_one * dn1
    d_tokens = (
        d_resid
        + recip_in * weighted_one
        - inputs_own * recip_in**3 * jnp.mean(weighted_one * inputs_own, axis=1, keepdims=True)
    ).astype(BF)
    d_tokens = flow_spread(d_tokens)

    d_in = rows_inner(normed_one, d_cat).astype(BF)
    d_in = lax.psum_scatter(d_in, "batch", scatter_dimension=0, tiled=True).astype(F32)
    d_gains = jnp.stack([d_gain_one, d_gain_two[0]]).reshape(2, batches, -1).transpose(1, 0, 2)
    d_gains = sum_heads(halve_batch(d_gains.reshape(2 * batches, -1), 2))
    hidden_own = w_mlp_gate.shape[1]
    return (
        output,
        d_tokens,
        d_gains[0],
        d_in[:, :head_size],
        d_in[:, 2 * head_size : 2 * head_size + half],
        d_in[:, 2 * head_size + half :],
        d_in[:, head_size : 2 * head_size],
        d_out,
        d_gains[1],
        d_mlp[:, :hidden_own],
        d_mlp[:, hidden_own:],
        d_down,
    )


def solution(mesh):
    return jax.shard_map(
        per_device,
        mesh=mesh,
        in_specs=(
            P("batch", None),
            P("batch"),
            P("batch"),
            P("batch", "head"),
            P("batch", "head"),
            P("batch", "head"),
            P("batch", "head"),
            P("head", "batch"),
            P("batch"),
            P("batch", "head"),
            P("batch", "head"),
            P("head", "batch"),
            P("batch", None),
        ),
        out_specs=(
            P("batch", None),
            P("batch", None),
            P("batch"),
            P("batch", "head"),
            P("batch", "head"),
            P("batch", "head"),
            P("batch", "head"),
            P("head", "batch"),
            P("batch"),
            P("batch", "head"),
            P("batch", "head"),
            P("head", "batch"),
        ),
        check_vma=False,
    )
```

```python
import functools
import math

import jax
import jax.numpy as jnp
from jax import lax
from jax.experimental import pallas as pl
from jax.experimental.pallas import tpu as pltpu
from jax.sharding import PartitionSpec as P

EPSILON = 1e-06
MASKED = -1e30
DOCUMENTS = 7
BF = jnp.bfloat16
F32 = jnp.float32


MESH = pl.DeviceIdType.MESH
VMEM_LIMIT = 60 << 20


def ring_place(head, count):
    high, low = head // 2, head % 2
    return (1 - low) * high + low * (count - 1 - high)


def ring_head(place, count):
    low = place // (count // 2)
    high = (1 - low) * place + low * (count - 1 - place)
    return 2 * high + low


def ring_setup(count):
    batch = lax.axis_index("batch")
    place = ring_place(lax.axis_index("head"), count)
    right = (batch, ring_head(lax.rem(place + 1, count), count))
    left = (batch, ring_head(lax.rem(place + count - 1, count), count))
    return place, right, left


def greet(devices):
    barrier = pltpu.get_barrier_semaphore()
    for device in devices:
        pl.semaphore_signal(barrier, inc=1, device_id=device, device_id_type=MESH)
    pl.semaphore_wait(barrier, len(devices))


def send(source, target, sems, slot, device):
    copy = pltpu.make_async_remote_copy(
        src_ref=source,
        dst_ref=target,
        send_sem=sems[0].at[slot],
        recv_sem=sems[1].at[slot],
        device_id=device,
        device_id_type=MESH,
    )
    copy.start()
    return copy


def half_of(extent, flow):
    if extent[1] % 256:
        return (pl.ds(flow * (extent[0] // 2), extent[0] // 2), slice(None))
    return (slice(None), pl.ds(flow * (extent[1] // 2), extent[1] // 2))


def place_of(whole, own, chunk, form):
    rows, wide = own.shape[-2:]
    if form == "lead":
        return whole.at[chunk]
    if form == "rows":
        return whole.at[pl.ds(pl.multiple_of(chunk * rows, rows), rows)]
    return whole.at[:, pl.ds(pl.multiple_of(chunk * wide, wide), wide)]


def spread_kernel(count, batches, plans, *refs):
    steps = count // 2
    arrays = len(plans)
    own_refs, all_refs = refs[:arrays], refs[arrays : 2 * arrays]
    send_sem, recv_sem, local_sem = refs[2 * arrays :]
    place, right, left = ring_setup(count)
    head = lax.axis_index("head")
    batch = lax.axis_index("batch")
    across, core = batch // 2, lax.rem(batch, 2)
    others = batches // 2
    twin = (across * 2 + 1 - core, head)
    peers = [(lax.rem(across + hop, others) * 2 + core, head) for hop in range(1, others)]
    ring = any(axis == "head" for axis, _ in plans)
    grid = any(axis == "batch" for axis, _ in plans)
    greet((right, left) * ring + (twin, *peers) * grid)
    sems = (send_sem, recv_sem)
    slot = 0
    waiting, arriving, local = [], [], []

    def go(source, target, device):
        nonlocal slot
        copy = send(source, target, sems, slot, device)
        slot += 1
        waiting.append(copy)
        return copy

    onward = []
    for index, (axis, form) in enumerate(plans):
        own, whole = own_refs[index], all_refs[index]
        spot = place if axis == "head" else batch
        mine = place_of(whole, own, spot, form)
        copy = pltpu.make_async_copy(own, mine, local_sem.at[index])
        copy.start()
        local.append(copy)
        if axis == "batch":
            for hop, peer in enumerate(peers, 1):
                source = lax.rem(across + others - hop, others) * 2 + core
                onward.append((go(own, mine, peer), place_of(whole, own, source, form)))
            arriving.append(go(own, mine, twin))
    copies = [None] * (2 * arrays)
    for step in range(steps):
        for index, (axis, form) in enumerate(plans):
            if axis != "head":
                continue
            own = own_refs[index]
            for flow, chunk, device in ((0, place - step, right), (1, place + step, left)):
                at = 2 * index + flow
                if step:
                    copies[at].wait_recv()
                chunk = lax.rem(chunk + count, count)
                target = place_of(all_refs[index], own, chunk, form)
                source = target if step else own
                if step == steps - 1:
                    part = half_of(own.shape, flow)
                    source = source.at[part]
                    target = target.at[part]
                copies[at] = go(source, target, device)
        if step == 0 or not ring:
            for copy, block in onward:
                copy.wait_recv()
                arriving.append(go(block, block, twin))
            onward = []
    for copy in copies:
        if copy is not None:
            arriving.append(copy)
    for copy in arriving:
        copy.wait_recv()
    for copy in waiting:
        copy.wait_send()
    for copy in local:
        copy.wait()


def spread(arrays, plans, collective_id):
    count = lax.axis_size("head")
    batches = lax.axis_size("batch")
    shapes = []
    slots = 0
    for array, (axis, form) in zip(arrays, plans):
        many = count if axis == "head" else batches
        slots += count if axis == "head" else batches - 1
        if form == "lead":
            shapes.append((many, *array.shape))
        elif form == "rows":
            shapes.append((many * array.shape[0], array.shape[1]))
        else:
            shapes.append((array.shape[0], many * array.shape[1]))
    hbm = pl.BlockSpec(memory_space=pl.ANY)
    return pl.pallas_call(
        functools.partial(spread_kernel, count, batches, plans),
        out_shape=[jax.ShapeDtypeStruct(shape, a.dtype) for shape, a in zip(shapes, arrays)],
        in_specs=[hbm] * len(arrays),
        out_specs=[hbm] * len(arrays),
        scratch_shapes=[
            pltpu.SemaphoreType.DMA((slots,)),
            pltpu.SemaphoreType.DMA((slots,)),
            pltpu.SemaphoreType.DMA((len(arrays),)),
        ],
        compiler_params=pltpu.CompilerParams(
            collective_id=collective_id, has_side_effects=True, vmem_limit_bytes=VMEM_LIMIT
        ),
        name=f"spread_{collective_id}",
    )(*arrays)


def mlp_kernel(
    count, x_hbm, a_hbm, dy_hbm, gain_ref, out_w, gate_w, up_w, down_w,
    n2_hbm, hid_hbm, grad_hbm, mlp_hbm, h1_ref, dh1_ref, low_ref, dgain_ref, da_ref, ahead_ref, behind_ref,
    x_s, a_s, dy_s, n2_s, hid_s, grad_s, mlp_s, h1_s, dy_own, da_part, mlp_far, mlp_got,
    right_part, left_part, right_got, left_got,
    in_sem, out_sem, send_sem, recv_sem, da_send, da_recv, far_send, far_recv,
):
    steps = count // 2
    rows = x_hbm.shape[0] // count
    width = x_hbm.shape[1]
    hidden = gate_w.shape[1]
    side = width // 2
    tile = 256
    inner = 256 if hidden % 256 == 0 else 128
    size = da_ref.shape[1]
    place, right, left = ring_setup(count)

    def member(hop):
        spot = lax.rem(place + hop, count)
        return spot, (lax.axis_index("batch"), ring_head(spot, count))

    greet([member(hop)[1] for hop in range(1, count)])

    def owners(group):
        first = jnp.where(group == 0, 1, 0)
        one = lax.rem(place + steps - group, count)
        two = lax.rem(place - steps + group + first * steps + count, count)
        return one, two

    def span(owner):
        return pl.ds(pl.multiple_of(owner * rows, rows), rows)

    def loads(group, slot):
        return [
            pltpu.make_async_copy(
                source.at[span(owner)],
                target.at[slot, pl.ds(at * rows, rows)],
                in_sem.at[slot, 2 * index + at],
            )
            for index, (source, target) in enumerate(((x_hbm, x_s), (a_hbm, a_s), (dy_hbm, dy_s)))
            for at, owner in enumerate(owners(group))
        ]

    def stores(group, slot):
        return [
            pltpu.make_async_copy(
                source.at[slot, pl.ds(at * rows, rows)],
                target.at[span(owner)],
                out_sem.at[slot, 2 * index + at],
            )
            for index, (source, target) in enumerate(
                ((n2_s, n2_hbm), (hid_s, hid_hbm), (grad_s, grad_hbm), (mlp_s, mlp_hbm))
            )
            for at, owner in enumerate(owners(group))
        ]

    def passing(source, target, flow, step, device):
        return pltpu.make_async_remote_copy(
            src_ref=source,
            dst_ref=target,
            send_sem=send_sem.at[flow * steps + step],
            recv_sem=recv_sem.at[flow * steps + step],
            device_id=device,
            device_id_type=MESH,
        )

    def first_copies():
        ahead, behind = pl.ds(0, side), pl.ds(side, side)
        return (
            passing(right_part.at[0, :, ahead], right_got.at[0, :, ahead], 0, 0, right),
            passing(right_part.at[0, :, behind], left_got.at[0, :, behind], 1, 0, left),
        )

    def later_copies(step):
        return (
            passing(right_part.at[step], right_got.at[step], 0, step, right),
            passing(left_part.at[step], left_got.at[step], 1, step, left),
        )

    for copy in loads(0, 0):
        copy.start()

    @pl.loop(0, steps)
    def _(group):
        slot = lax.rem(group, 2)
        for copy in loads(group, slot):
            copy.wait()

        @pl.when(group + 1 < steps)
        def _():
            for copy in loads(group + 1, 1 - slot):
                copy.start()

        @pl.when(group >= 2)
        def _():
            for copy in stores(group - 2, slot):
                copy.wait()

        mixed = a_s[slot]

        def residual(at, total):
            cols = pl.ds(pl.multiple_of(at * tile, tile), tile)
            values = x_s[slot, :, cols].astype(F32) + matmul(mixed, out_w[:, cols])
            h1_s[:, cols] = values
            return total + jnp.sum(values * values, axis=1, keepdims=True)

        total = lax.fori_loop(0, width // tile, residual, jnp.zeros((2 * rows, 1), F32))
        scale = lax.rsqrt(total / width + EPSILON)

        @pl.when(group == 0)
        def _():
            h1_ref[...] = h1_s[pl.ds(rows, rows)]
            dy_own[...] = dy_s[slot, pl.ds(rows, rows)]

        @pl.loop(0, width // tile)
        def _(at):
            cols = pl.ds(pl.multiple_of(at * tile, tile), tile)
            n2_s[slot, :, cols] = (h1_s[:, cols] * scale * gain_ref[:, cols]).astype(BF)

        normed = n2_s[slot]
        dy = dy_s[slot]

        @pl.loop(0, hidden // inner)
        def _(at):
            cols = pl.ds(pl.multiple_of(at * inner, inner), inner)
            cols_up = pl.ds(pl.multiple_of(hidden + at * inner, inner), inner)
            gate = matmul(normed, gate_w[:, cols])
            up = matmul(normed, up_w[:, cols])
            d_hidden = cols_inner(dy, down_w[cols])
            sig = jax.nn.sigmoid(gate)
            silu = gate * sig
            hid_s[slot, :, cols] = (silu * up).astype(BF)
            grad_s[slot, :, cols] = (d_hidden * up * sig * (1.0 + gate * (1.0 - sig))).astype(BF)
            grad_s[slot, :, cols_up] = (d_hidden * silu).astype(BF)

        hid = hid_s[slot]
        d_gate = grad_s[slot, :, :hidden]
        d_up = grad_s[slot, :, hidden:]

        @pl.loop(0, width // tile)
        def _(at):
            cols = pl.ds(pl.multiple_of(at * tile, tile), tile)
            part = (cols_inner(d_gate, gate_w[cols]) + cols_inner(d_up, up_w[cols])).astype(BF)
            right_part[group, :, cols] = part[:rows]
            left_part[group, :, cols] = part[rows:]
            mlp_s[slot, :, cols] = matmul(hid, down_w[:, cols]).astype(BF)

        for copy in stores(group, slot):
            copy.start()

        @pl.when(group == 0)
        def _():
            mlp_far[...] = mlp_s[slot, pl.ds(0, rows)]

        @pl.when(group == 1)
        def _():
            ahead_ref[...] = mlp_s[slot, pl.ds(0, rows)]
            behind_ref[...] = mlp_s[slot, pl.ds(rows, rows)]

        @pl.when(group == 0)
        def _():
            for copy in first_copies():
                copy.start()

        @pl.when(group == 1)
        def _():
            one, two = first_copies()
            one.wait_recv()
            two.wait_recv()
            ahead, behind = pl.ds(0, side), pl.ds(side, side)
            right_part[1, :, ahead] = add_low(right_part[1, :, ahead], right_got[0, :, ahead])
            left_part[1, :, behind] = add_low(left_part[1, :, behind], left_got[0, :, behind])

        @pl.when(group >= 2)
        def _():
            one, two = later_copies(group - 1)
            one.wait_recv()
            right_part[group] = add_low(right_part[group], right_got[group - 1])
            two.wait_recv()
            left_part[group] = add_low(left_part[group], left_got[group - 1])

        @pl.when(group >= 1)
        def _():
            for copy in later_copies(group):
                copy.start()

    for copy in later_copies(steps - 1):
        copy.wait_recv()
    far_copies = [
        pltpu.make_async_remote_copy(
            src_ref=mlp_far.at[:, pl.ds(flow * side, side)],
            dst_ref=mlp_got.at[flow],
            send_sem=far_send.at[flow],
            recv_sem=far_recv.at[flow],
            device_id=device,
            device_id_type=MESH,
        )
        for flow, device in ((0, right), (1, left))
    ]
    for copy in far_copies:
        copy.start()

    def tile_of(at):
        return pl.ds(pl.multiple_of(at * tile, tile), tile)

    def collect(at, state):
        squares, mean = state
        cols = tile_of(at)
        dn2 = (
            left_part[0, :, cols].astype(F32)
            + right_got[steps - 1, :, cols].astype(F32)
            + left_got[steps - 1, :, cols].astype(F32)
        )
        dh1_ref[:, cols] = dn2
        h1 = h1_ref[:, cols]
        squares = squares + jnp.sum(h1 * h1, axis=1, keepdims=True)
        return squares, mean + jnp.sum(gain_ref[:, cols] * dn2 * h1, axis=1, keepdims=True)

    zero = jnp.zeros((rows, 1), F32)
    squares, mean = lax.fori_loop(0, width // tile, collect, (zero, zero))
    scale_own = lax.rsqrt(squares / width + EPSILON)
    pull = scale_own * scale_own * scale_own * (mean / width)

    @pl.loop(0, width // tile)
    def _(at):
        cols = tile_of(at)
        dn2, h1 = dh1_ref[:, cols], h1_ref[:, cols]
        dgain_ref[:, cols] = jnp.sum(dn2 * h1 * scale_own, axis=0, keepdims=True)
        d_resid = dy_own[:, cols].astype(F32) + scale_own * (gain_ref[:, cols] * dn2) - h1 * pull
        dh1_ref[:, cols] = d_resid
        low_ref[:, cols] = d_resid.astype(BF)

    def da_copy(hop):
        return pltpu.make_async_remote_copy(
            src_ref=da_part.at[hop],
            dst_ref=da_ref.at[span(place)],
            send_sem=da_send.at[hop],
            recv_sem=da_recv.at[hop],
            device_id=member(hop)[1],
            device_id_type=MESH,
        )

    low = low_ref[...]

    @pl.loop(1, count)
    def _(hop):
        spot = member(hop)[0]
        part = cols_inner(low, out_w[pl.ds(pl.multiple_of(spot * size, size), size)])
        da_part[hop] = part.astype(BF)
        da_copy(hop).start()

    own_w = out_w[pl.ds(pl.multiple_of(place * size, size), size)]
    da_ref[span(place)] = cols_inner(low, own_w).astype(BF)

    @pl.loop(1, count)
    def _(hop):
        da_copy(hop).wait_recv()
        da_copy(hop).wait_send()

    for flow, held in ((0, ahead_ref), (1, behind_ref)):
        far_copies[flow].wait_recv()
        cols = pl.ds(flow * side, side)
        held[:, cols] = add_low(held[:, cols], mlp_got[flow])
        far_copies[flow].wait_send()

    for copy in first_copies():
        copy.wait_send()
    for step in range(1, steps):
        for copy in later_copies(step):
            copy.wait_send()
    for group in range(max(steps - 2, 0), steps):
        for copy in stores(group, group % 2):
            copy.wait()


def mlp_back(tokens, mixed, dy, gain, out_w, gate_w, up_w, down_w, collective_id):
    count = lax.axis_size("head")
    total, width = tokens.shape
    hidden = gate_w.shape[1]
    rows, steps = total // count, count // 2
    size = mixed.shape[1] // count
    vmem = pl.BlockSpec(memory_space=pltpu.VMEM)
    hbm = pl.BlockSpec(memory_space=pl.ANY)

    def slots(wide, dtype=BF):
        return pltpu.VMEM((2, 2 * rows, wide), dtype)

    part = pltpu.VMEM((steps, rows, width), BF)
    flops = 2 * total * width * (mixed.shape[1] + 6 * hidden)
    return pl.pallas_call(
        functools.partial(mlp_kernel, count),
        out_shape=[
            jax.ShapeDtypeStruct((total, width), BF),
            jax.ShapeDtypeStruct((total, hidden), BF),
            jax.ShapeDtypeStruct((total, 2 * hidden), BF),
            jax.ShapeDtypeStruct((total, width), BF),
            jax.ShapeDtypeStruct((rows, width), F32),
            jax.ShapeDtypeStruct((rows, width), F32),
            jax.ShapeDtypeStruct((rows, width), BF),
            jax.ShapeDtypeStruct((1, width), F32),
            jax.ShapeDtypeStruct((total, size), BF),
            jax.ShapeDtypeStruct((rows, width), BF),
            jax.ShapeDtypeStruct((rows, width), BF),
        ],
        in_specs=[hbm] * 3 + [vmem] * 5,
        out_specs=[hbm] * 4 + [vmem] * 7,
        scratch_shapes=[
            slots(width), slots(mixed.shape[1]), slots(width), slots(width), slots(hidden),
            slots(2 * hidden), slots(width), pltpu.VMEM((2 * rows, width), F32),
            pltpu.VMEM((rows, width), BF), pltpu.VMEM((count, rows, size), BF),
            pltpu.VMEM((rows, width), BF), pltpu.VMEM((2, rows, width // 2), BF),
            part, part, part, part,
            pltpu.SemaphoreType.DMA((2, 6)), pltpu.SemaphoreType.DMA((2, 8)),
            pltpu.SemaphoreType.DMA((count,)), pltpu.SemaphoreType.DMA((count,)),
            pltpu.SemaphoreType.DMA((count,)), pltpu.SemaphoreType.DMA((count,)),
            pltpu.SemaphoreType.DMA((2,)), pltpu.SemaphoreType.DMA((2,)),
        ],
        compiler_params=pltpu.CompilerParams(
            collective_id=collective_id, has_side_effects=True, vmem_limit_bytes=VMEM_LIMIT
        ),
        cost_estimate=pl.CostEstimate(flops=flops, bytes_accessed=40 << 20, transcendentals=0),
        name="mlp_back",
    )(tokens, mixed, dy, gain, out_w, gate_w, up_w, down_w)


def entry_kernel(
    count, batches, x_ref, w_ref, out_ref, gain_ref, seg_ref, down_ref,
    n1_ref, q_ref, logit_ref, kv_ref, w_all, out_all, gain_all, seg_all, down_all,
    send_sem, recv_sem, local_sem,
):
    steps = count // 2
    others = batches // 2
    rows, width = x_ref.shape
    depth = w_ref.shape[0]
    size, wide = out_ref.shape
    block = 256
    place, right, left = ring_setup(count)
    head = lax.axis_index("head")
    batch = lax.axis_index("batch")
    across, core, low = batch // 2, lax.rem(batch, 2), lax.rem(head, 2)
    twin = (across * 2 + 1 - core, head)
    mate = (batch, head + 1 - 2 * low)
    spots = [lax.rem(across + hop, others) for hop in range(others)]
    backs = [lax.rem(across + others - hop, others) for hop in range(others)]
    peers = [(spot * 2 + core, head) for spot in spots]
    far_peers = [(spot * 2 + 1 - core, head) for spot in spots]
    greet((twin, mate, right, left, *peers[1:], *far_peers[1:]))
    sems = (send_sem, recv_sem)
    slot = 0
    copies = []

    def go(source, target, device):
        nonlocal slot
        copy = send(source, target, sems, slot, device)
        slot += 1
        copies.append(copy)
        return copy

    def part(at, extent):
        return pl.ds(pl.multiple_of(at * extent, extent), extent)

    def both(view, own):
        out = [go(own, view(batch), peers[hop]) for hop in range(1, others)]
        return out, [go(own, view(batch), twin)]

    def pass_on(view, arrived):
        out = []
        for hop in range(1, others):
            arrived[hop - 1].wait_recv()
            there = view(backs[hop] * 2 + core)
            out.append(go(there, there, twin))
        return out

    local = []

    def stay(source, target):
        copy = pltpu.make_async_copy(source, target, local_sem.at[len(local)])
        copy.start()
        local.append(copy)

    def main_view(at):
        return w_all.at[part(at, depth), pl.ds(0, 3 * size)]

    def mate_view(at):
        return w_all.at[part(at, depth), pl.ds(3 * size, size)]

    def out_view(chunk, at):
        return out_all.at[part(chunk, size), part(at, wide)]

    small = []
    for own, whole in ((gain_ref, gain_all), (seg_ref, seg_all)):
        for device in (twin, *peers[1:], *far_peers[1:]):
            small.append(go(own, whole.at[batch], device))
        stay(own, whole.at[batch])
    from_mate = go(w_ref.at[:, pl.ds(2 * size, size)], mate_view(batch), mate)
    main_out, main_twin = both(main_view, w_ref)
    stay(w_ref, main_view(batch))
    out_peers = [go(out_ref, out_view(place, batch), peers[hop]) for hop in range(1, others)]
    stay(out_ref, out_view(place, batch))
    flows = [[None, None] for _ in range(others)]

    def ring(step):
        for hop in range(others):
            lane = spots[0] if hop == 0 else backs[hop]
            at = lane * 2 + core
            if step == 0 and hop:
                out_peers[hop - 1].wait_recv()
            for flow, chunk, device in ((0, place - step, right), (1, place + step, left)):
                if step:
                    flows[hop][flow].wait_recv()
                target = out_view(lax.rem(chunk + count, count), at)
                source = out_ref if step == 0 and hop == 0 else target
                if step == steps - 1:
                    cut = (pl.ds(flow * (size // 2), size // 2), slice(None))
                    source, target = source.at[cut], target.at[cut]
                flows[hop][flow] = go(source, target, device)

    for copy in small:
        copy.wait_recv()
    for copy in local[:2]:
        copy.wait()

    def normalize(at):
        here = part(at, block)

        def squares(tile, total):
            values = x_ref[here, part(tile, 256)].astype(F32)
            return total + jnp.sum(values * values, axis=1, keepdims=True)

        total = lax.fori_loop(0, width // 256, squares, jnp.zeros((block, 1), F32))
        scale = lax.rsqrt(total / width + EPSILON)

        @pl.loop(0, batches)
        def _(owner):
            for tile in range(depth // 128):
                cols = pl.ds(pl.multiple_of(owner * depth + tile * 128, 128), 128)
                values = x_ref[here, cols].astype(F32) * scale
                n1_ref[here, cols] = (values * gain_all[owner, pl.ds(tile, 1)]).astype(BF)

    blocks = rows // block
    middle = blocks // 2

    @pl.loop(0, middle)
    def _(at):
        normalize(at)

    from_mate.wait_recv()
    mate_out, mate_twin = both(mate_view, mate_view(batch))
    ring(0)

    @pl.loop(middle, blocks)
    def _(at):
        normalize(at)

    main_passed = pass_on(main_view, main_out)
    mate_passed = pass_on(mate_view, mate_out)
    for copy in (*main_twin, *mate_twin, *main_passed, *mate_passed):
        copy.wait_recv()
    for copy in local[2:]:
        copy.wait()

    def kv_view(at):
        return kv_ref.at[part(at, rows)]

    def down_view(at):
        return down_all.at[:, part(at, down_ref.shape[1])]

    down_out, down_twin = both(down_view, down_ref)
    stay(down_ref, down_view(batch))

    @pl.loop(0, blocks)
    def _(at):
        here = part(at, block)
        values = matmul(n1_ref[here], w_all[:, pl.ds(2 * size, 2 * size)])
        one, two = values[:, :size], values[:, size:]
        first = jnp.where(low == 0, one, two).astype(BF)
        second = jnp.where(low == 0, two, one).astype(BF)
        half = size // 2
        there = pl.ds(pl.multiple_of(batch * rows + at * block, block), block)
        kv_ref[there, pl.ds(0, size)] = jnp.concatenate([first[:, :half], second[:, :half]], 1)
        kv_ref[there, pl.ds(size, size)] = jnp.concatenate([first[:, half:], second[:, half:]], 1)

    kv_out, kv_twin = both(kv_view, kv_view(batch))
    ring(1)

    @pl.loop(0, blocks)
    def _(at):
        here = part(at, block)
        values = matmul(n1_ref[here], w_all[:, pl.ds(0, 2 * size)])
        q_ref[here] = values[:, :size].astype(BF)
        logit_ref[here] = values[:, size:]

    for step in range(2, steps):
        ring(step)
    kv_passed = pass_on(kv_view, kv_out)
    down_passed = pass_on(down_view, down_out)
    local[-1].wait()
    for pair in flows:
        for copy in pair:
            copy.wait_recv()
    swaps = []
    for hop in range(others):
        there = out_all.at[:, part(spots[hop] * 2 + core, wide)]
        swaps.append(go(there, there, twin))
    for copy in (*kv_twin, *kv_passed, *swaps, *down_twin, *down_passed):
        copy.wait_recv()
    for copy in copies:
        copy.wait_send()


def entry(tokens, w_shard, w_out, gains, segments, w_down, collective_id):
    count = lax.axis_size("head")
    batches = lax.axis_size("batch")
    others = batches // 2
    rows, width = tokens.shape
    size, wide = w_out.shape
    vmem = pl.BlockSpec(memory_space=pltpu.VMEM)
    slots = 6 * batches + others * (count + 3)
    sems = pltpu.SemaphoreType.DMA((slots,))
    return pl.pallas_call(
        functools.partial(entry_kernel, count, batches),
        out_shape=[
            jax.ShapeDtypeStruct((rows, width), BF),
            jax.ShapeDtypeStruct((rows, size), BF),
            jax.ShapeDtypeStruct((rows, size), F32),
            jax.ShapeDtypeStruct((batches * rows, 2 * size), BF),
            jax.ShapeDtypeStruct((width, 4 * size), BF),
            jax.ShapeDtypeStruct((count * size, batches * wide), BF),
            jax.ShapeDtypeStruct((batches, *gains.shape), F32),
            jax.ShapeDtypeStruct((batches, *segments.shape), jnp.int32),
            jax.ShapeDtypeStruct((w_down.shape[0], batches * w_down.shape[1]), BF),
        ],
        in_specs=[vmem] * 6,
        out_specs=[vmem] * 9,
        scratch_shapes=[sems, sems, pltpu.SemaphoreType.DMA((5,))],
        compiler_params=pltpu.CompilerParams(
            collective_id=collective_id, has_side_effects=True, vmem_limit_bytes=VMEM_LIMIT
        ),
        name="entry",
    )(tokens, w_shard, w_out, gains, segments, w_down)


KEY_BLOCK = 512
QUERY_BLOCK = 256


def key_range(start_ref, base, query_block):
    first = query_block * QUERY_BLOCK
    lowest = start_ref[first]
    highest = start_ref[first + QUERY_BLOCK - 1]
    begin = lowest // KEY_BLOCK
    end = (base + first + QUERY_BLOCK - 1) // KEY_BLOCK + 1
    full_begin = jnp.minimum((highest + KEY_BLOCK - 1) // KEY_BLOCK, end)
    full_end = jnp.maximum((base + first + 1) // KEY_BLOCK, full_begin)
    return begin, full_begin, full_end, end


def allowed_pairs(key_block, start_row, base_row):
    shape = (KEY_BLOCK, QUERY_BLOCK)
    key_pos = key_block * KEY_BLOCK + lax.broadcasted_iota(jnp.int32, shape, 0)
    query_pos = base_row + lax.broadcasted_iota(jnp.int32, shape, 1)
    return (key_pos >= start_row) & (key_pos <= query_pos)


def attend_kernel(
    scale, start_sm, base_sm, q_ref, kv_ref, start_ref, logit_ref, o_ref, a_ref, lse_ref
):
    base = base_sm[0]
    size = q_ref.shape[1]
    factor = scale * math.log2(math.e)

    @pl.loop(0, q_ref.shape[0] // QUERY_BLOCK)
    def _(block):
        rows = pl.ds(pl.multiple_of(block * QUERY_BLOCK, QUERY_BLOCK), QUERY_BLOCK)
        queries = q_ref[rows]
        start_row = start_ref[:, rows]
        begin, full_begin, full_end, end = key_range(start_sm, base, block)

        def step(masked, at, state):
            old_max, old_sum, total = state
            keys = pl.ds(pl.multiple_of(at * KEY_BLOCK, KEY_BLOCK), KEY_BLOCK)
            scores = cols_inner(kv_ref[keys, :size], queries)
            if masked:
                allowed = allowed_pairs(at, start_row, base + block * QUERY_BLOCK)
                scores = jnp.where(allowed, scores, MASKED)
            new_max = jnp.maximum(old_max, jnp.max(scores, axis=0, keepdims=True))
            keep = jnp.exp2((old_max - new_max) * factor)
            weights = jnp.exp2(scores * factor - new_max * factor)
            new_sum = old_sum * keep + jnp.sum(weights, axis=0, keepdims=True)
            total = total * keep + rows_inner(kv_ref[keys, size:], weights.astype(BF))
            return new_max, new_sum, total

        state = (
            jnp.full((1, QUERY_BLOCK), MASKED, F32),
            jnp.zeros((1, QUERY_BLOCK), F32),
            jnp.zeros((size, QUERY_BLOCK), F32),
        )
        state = lax.fori_loop(begin, full_begin, functools.partial(step, True), state)
        state = lax.fori_loop(full_begin, full_end, functools.partial(step, False), state)
        state = lax.fori_loop(full_end, end, functools.partial(step, True), state)
        run_max, run_sum, total = state
        lse_ref[:, rows] = run_max * factor + jnp.log2(run_sum)
        attended = (total / run_sum).T
        o_ref[rows] = attended
        a_ref[rows] = (attended * jax.nn.sigmoid(logit_ref[rows])).astype(BF)


def attend_back_kernel(
    scale, start_sm, base_sm, q_ref, kv_ref, start_ref, logit_ref, o_ref, da_ref, lse_ref,
    dq_ref, dg_ref, dkv_ref, dk_acc, dv_acc,
):
    base = base_sm[0]
    size = q_ref.shape[1]
    factor = scale * math.log2(math.e)
    dk_acc[...] = jnp.zeros_like(dk_acc)
    dv_acc[...] = jnp.zeros_like(dv_acc)

    @pl.loop(0, q_ref.shape[0] // QUERY_BLOCK)
    def _(block):
        rows = pl.ds(pl.multiple_of(block * QUERY_BLOCK, QUERY_BLOCK), QUERY_BLOCK)
        queries = q_ref[rows]
        start_row = start_ref[:, rows]
        lse = lse_ref[:, rows]
        gate = jax.nn.sigmoid(logit_ref[rows])
        attended = o_ref[rows]
        d_mixed = da_ref[rows].astype(F32)
        d_attended = (d_mixed * gate).astype(BF)
        dg_ref[rows] = (d_mixed * attended * gate * (1.0 - gate)).astype(BF)
        delta = jnp.sum((d_attended.astype(F32) * attended).T, axis=0, keepdims=True)
        begin, full_begin, full_end, end = key_range(start_sm, base, block)

        def step(masked, at, d_queries):
            keys = pl.ds(pl.multiple_of(at * KEY_BLOCK, KEY_BLOCK), KEY_BLOCK)
            key_block = kv_ref[keys, :size]
            probs = jnp.exp2(cols_inner(key_block, queries) * factor - lse)
            if masked:
                allowed = allowed_pairs(at, start_row, base + block * QUERY_BLOCK)
                probs = jnp.where(allowed, probs, 0.0)
            d_probs = cols_inner(kv_ref[keys, size:], d_attended)
            d_scores = (probs * (d_probs - delta) * scale).astype(BF)
            dv_acc[keys] += matmul(probs.astype(BF), d_attended)
            dk_acc[keys] += matmul(d_scores, queries)
            return d_queries + rows_inner(key_block, d_scores)

        d_queries = jnp.zeros((size, QUERY_BLOCK), F32)
        d_queries = lax.fori_loop(begin, full_begin, functools.partial(step, True), d_queries)
        d_queries = lax.fori_loop(full_begin, full_end, functools.partial(step, False), d_queries)
        d_queries = lax.fori_loop(full_end, end, functools.partial(step, True), d_queries)
        dq_ref[rows] = d_queries.T.astype(BF)

    @pl.loop(0, kv_ref.shape[0] // KEY_BLOCK)
    def _(at):
        keys = pl.ds(pl.multiple_of(at * KEY_BLOCK, KEY_BLOCK), KEY_BLOCK)
        dk, dv = dk_acc[keys].astype(BF), dv_acc[keys].astype(BF)
        half = size // 2
        dkv_ref[keys, :size] = jnp.concatenate([dk[:, :half], dv[:, :half]], axis=1)
        dkv_ref[keys, size:] = jnp.concatenate([dk[:, half:], dv[:, half:]], axis=1)


def fold_kernel(
    batches, part_ref, own_ref, core_got, x_first, x_second, y_first, y_second, held, send_sem, recv_sem
):
    rows, size = own_ref.shape
    half = rows // 2
    others = batches // 2
    head = lax.axis_index("head")
    batch = lax.axis_index("batch")
    across, core, low = batch // 2, lax.rem(batch, 2), lax.rem(head, 2)
    twin = (across * 2 + 1 - core, head)
    mate = (batch, head + 1 - 2 * low)
    spots = [lax.rem(across + hop, others) for hop in range(others)]
    peers = [(spot * 2 + core, head) for spot in spots]
    greet((twin, mate, *peers[1:]))
    sems = (send_sem, recv_sem)
    slot = 0
    copies = []
    mine = pl.ds(pl.multiple_of(low * size, size), size)
    given = pl.ds(pl.multiple_of((1 - low) * size, size), size)
    top, bottom = pl.ds(0, half), pl.ds(half, half)

    def block(at, side):
        return pl.ds(pl.multiple_of((2 * at + side) * rows, rows), rows)

    def go(source, target, device):
        nonlocal slot
        copy = send(source, target, sems, slot, device)
        slot += 1
        copies.append(copy)
        return copy

    order = list(range(1, others)) + [0]
    first = [go(part_ref.at[block(spots[hop], 1 - core)], core_got.at[spots[hop]], twin) for hop in order]
    tops, bottoms = [], []
    for copy, hop in zip(first, order):
        copy.wait_recv()
        spot = spots[hop]
        core_got[spot] = add_low(core_got[spot], part_ref[block(spot, core)])
        bottoms.append(go(core_got.at[spot, bottom, given], y_first.at[spot], mate))
        if hop:
            tops.append(go(core_got.at[spot, top], x_first.at[hop - 1], peers[hop]))
    total = core_got[across, top].astype(F32)
    for hop in range(1, others):
        tops[hop - 1].wait_recv()
        total = total + x_first[hop - 1].astype(F32)
    held[...] = total.astype(BF)
    last = go(held.at[:, given], y_second, mate)
    ends = []
    for copy, hop in zip(bottoms, order):
        copy.wait_recv()
        spot = spots[hop]
        y_first[spot] = add_low(y_first[spot], core_got[spot, bottom, mine])
        if hop:
            ends.append(go(y_first.at[spot], x_second.at[hop - 1], peers[hop]))
    last.wait_recv()
    own_ref[top] = add_low(held[:, mine], y_second[...])
    total = y_first[across].astype(F32)
    for hop in range(1, others):
        ends[hop - 1].wait_recv()
        total = total + x_second[hop - 1].astype(F32)
    own_ref[bottom] = total.astype(BF)
    for copy in copies:
        copy.wait_send()


def fold(part, rows, collective_id):
    batches = lax.axis_size("batch")
    others = batches // 2
    size = part.shape[1] // 2
    half = rows // 2
    vmem = pl.BlockSpec(memory_space=pltpu.VMEM)
    sems = pltpu.SemaphoreType.DMA((4 * others,))
    return pl.pallas_call(
        functools.partial(fold_kernel, batches),
        out_shape=jax.ShapeDtypeStruct((rows, size), BF),
        in_specs=[vmem],
        out_specs=vmem,
        scratch_shapes=[
            pltpu.VMEM((others, rows, 2 * size), BF),
            pltpu.VMEM((others - 1, half, 2 * size), BF),
            pltpu.VMEM((others - 1, half, size), BF),
            pltpu.VMEM((others, half, size), BF),
            pltpu.VMEM((half, size), BF),
            pltpu.VMEM((half, 2 * size), BF),
            sems,
            sems,
        ],
        compiler_params=pltpu.CompilerParams(
            collective_id=collective_id, has_side_effects=True, vmem_limit_bytes=VMEM_LIMIT
        ),
        name="fold",
    )(part)


def tail_kernel(
    count, batches, cat_ref, w_ref, x_ref, gain_ref, dh1_ref, out_ref, wout_ref, second_ref,
    out_all, tok_all, gains_ref, wout_own,
    part_ref, tok_ref, got, wout_got, gain_own, gain_got, gain_mid, gain_heads,
    send_sem, recv_sem, local_sem,
):
    steps = count // 2
    rows, width = x_ref.shape
    depth = cat_ref.shape[1]
    tile = 256
    place, right, left = ring_setup(count)
    batch, head = lax.axis_index("batch"), lax.axis_index("head")
    others = [lax.rem(batch + hop, batches) for hop in range(1, batches)]
    members = [(batch, ring_head(lax.rem(place + hop, count), count)) for hop in range(1, count)]
    greet((*members, *[(other, head) for other in others]))
    sems = (send_sem, recv_sem)
    slot = 0
    copies = []

    def go(source, target, device):
        nonlocal slot
        copy = send(source, target, sems, slot, device)
        slot += 1
        copies.append(copy)
        return copy

    def span(owner, extent):
        return pl.ds(pl.multiple_of(lax.rem(owner + count, count) * extent, extent), extent)

    def compute(owner):
        here = span(owner, rows)
        values = cat_ref[here]

        @pl.loop(0, width // tile)
        def _(at):
            cols = pl.ds(pl.multiple_of(at * tile, tile), tile)
            part_ref[here, cols] = cols_inner(values, w_ref[cols, pl.ds(0, depth)]).astype(BF)

    def gather(own, whole, step, last):
        out = []
        for flow, chunk, device in ((0, place - step, right), (1, place + step, left)):
            if step:
                last[flow].wait_recv()
            target = whole.at[lax.rem(chunk + count, count)]
            source = target if step else own
            if step == steps - 1:
                cut = (slice(None), pl.ds(flow * (width // 2), width // 2))
                source, target = source.at[cut], target.at[cut]
            out.append(go(source, target, device))
        return out

    def reduce(parts, held, step, last):
        extent, side = held.shape[2], held.shape[3] // 2
        out = []
        for flow, owner, device in (
            (0, place + steps - step, right),
            (1, place - steps + step, left),
        ):
            have = pl.ds(flow * side, side)
            lack = pl.ds((1 - flow) * side, side)
            mine = parts.at[span(owner, extent)]
            if step == 0:
                out.append(go(mine.at[:, have], held.at[flow, 0, :, have], device))
                continue
            last[flow].wait_recv()
            if step == 1:
                held[flow, 0, :, have] = add_low(held[flow, 0, :, have], mine[:, have])
                held[flow, 0, :, lack] = mine[:, lack]
            else:
                held[flow, step - 1] = add_low(held[flow, step - 1], mine[...])
            out.append(go(held.at[flow, step - 1], held.at[flow, step], device))
        return out

    keep_out = pltpu.make_async_copy(out_ref, out_all.at[place], local_sem.at[0])
    keep_out.start()
    compute(place + steps)
    sums = reduce(part_ref, got, 0, None)
    outs = gather(out_ref, out_all, 0, None)
    wsums = reduce(wout_ref, wout_got, 0, None)

    @pl.loop(1, count)
    def _(hop):
        compute(place + steps + hop)

    for step in range(1, steps):
        sums = reduce(part_ref, got, step, sums)
        wsums = reduce(wout_ref, wout_got, step, wsums)
        outs = gather(out_ref, out_all, step, outs)
    for copy in sums:
        copy.wait_recv()

    def tile_of(at):
        return pl.ds(pl.multiple_of(at * tile, tile), tile)

    def total(cols):
        return (
            part_ref[span(place, rows), cols].astype(F32)
            + got[0, steps - 1, :, cols].astype(F32)
            + got[1, steps - 1, :, cols].astype(F32)
        )

    def collect(at, state):
        squares, mean = state
        cols = tile_of(at)
        x = x_ref[:, cols].astype(F32)
        squares = squares + jnp.sum(x * x, axis=1, keepdims=True)
        return squares, mean + jnp.sum(gain_ref[:, cols] * total(cols) * x, axis=1, keepdims=True)

    zero = jnp.zeros((rows, 1), F32)
    squares, mean = lax.fori_loop(0, width // tile, collect, (zero, zero))
    scale = lax.rsqrt(squares / width + EPSILON)
    pull = scale * scale * scale * (mean / width)

    @pl.loop(0, width // tile)
    def _(at):
        cols = tile_of(at)
        x, dn1 = x_ref[:, cols].astype(F32), total(cols)
        gain_own[pl.ds(0, 1), cols] = jnp.sum(dn1 * x * scale, axis=0, keepdims=True)
        gain_own[pl.ds(1, 1), cols] = second_ref[:, cols]
        tok_ref[:, cols] = (dh1_ref[:, cols] + scale * (gain_ref[:, cols] * dn1) - x * pull).astype(BF)

    keep_tok = pltpu.make_async_copy(tok_ref, tok_all.at[place], local_sem.at[1])
    keep_tok.start()
    toks = gather(tok_ref, tok_all, 0, None)
    wide = width // batches

    def slice_of(at):
        return pl.ds(pl.multiple_of(at * wide, wide), wide)

    gains = [
        go(gain_own.at[:, slice_of(other)], gain_got.at[hop], (other, head))
        for hop, other in enumerate(others)
    ]
    toks = gather(tok_ref, tok_all, 1, toks)
    middle = gain_own[:, slice_of(batch)]
    for hop, copy in enumerate(gains):
        copy.wait_recv()
        middle = middle + gain_got[hop]
    gain_mid[...] = middle
    gain_heads[place] = middle
    gains = [go(gain_mid, gain_heads.at[place], member) for member in members]
    for step in range(2, steps):
        toks = gather(tok_ref, tok_all, step, toks)
    for copy in gains:
        copy.wait_recv()
    middle = gain_heads[0]
    for at in range(1, count):
        middle = middle + gain_heads[at]
    gains_ref[...] = middle
    for copy in (*wsums, *outs):
        copy.wait_recv()
    wout_own[...] = (
        wout_ref[span(place, wout_own.shape[0])].astype(F32)
        + wout_got[0, steps - 1].astype(F32)
        + wout_got[1, steps - 1].astype(F32)
    )
    for copy in toks:
        copy.wait_recv()
    for copy in copies:
        copy.wait_send()
    keep_out.wait()
    keep_tok.wait()


def tail(d_cat, w_in, x_own, gain, d_resid, out_own, wout_part, second, collective_id):
    count = lax.axis_size("head")
    batches = lax.axis_size("batch")
    steps = count // 2
    rows, width = x_own.shape
    size, wide = wout_part.shape[0] // count, wout_part.shape[1]
    vmem = pl.BlockSpec(memory_space=pltpu.VMEM)
    hbm = pl.BlockSpec(memory_space=pl.ANY)
    whole = jax.ShapeDtypeStruct((count, rows, width), BF)
    sems = pltpu.SemaphoreType.DMA((5 * count + batches,))
    gains = (2, width // batches)
    return pl.pallas_call(
        functools.partial(tail_kernel, count, batches),
        out_shape=[
            whole,
            whole,
            jax.ShapeDtypeStruct(gains, F32),
            jax.ShapeDtypeStruct((size, wide), F32),
        ],
        in_specs=[vmem] * 8,
        out_specs=[hbm, hbm, vmem, vmem],
        scratch_shapes=[
            pltpu.VMEM((count * rows, width), BF),
            pltpu.VMEM((rows, width), BF),
            pltpu.VMEM((2, steps, rows, width), BF),
            pltpu.VMEM((2, steps, size, wide), BF),
            pltpu.VMEM((2, width), F32),
            pltpu.VMEM((batches - 1, *gains), F32),
            pltpu.VMEM(gains, F32),
            pltpu.VMEM((count, *gains), F32),
            sems,
            sems,
            pltpu.SemaphoreType.DMA((2,)),
        ],
        compiler_params=pltpu.CompilerParams(
            collective_id=collective_id, has_side_effects=True, vmem_limit_bytes=VMEM_LIMIT
        ),
        cost_estimate=pl.CostEstimate(
            flops=2 * count * rows * width * d_cat.shape[1], bytes_accessed=400 << 20, transcendentals=0
        ),
        name="tail",
    )(d_cat, w_in, x_own, gain, d_resid, out_own, wout_part, second)


def local_call(kernel, scalars, arrays, outs, scratch, flops, name):
    vmem = pl.BlockSpec(memory_space=pltpu.VMEM)
    smem = pl.BlockSpec(memory_space=pltpu.SMEM)
    return pl.pallas_call(
        kernel,
        out_shape=outs,
        in_specs=[smem] * len(scalars) + [vmem] * len(arrays),
        out_specs=[vmem] * len(outs),
        scratch_shapes=scratch,
        compiler_params=pltpu.CompilerParams(vmem_limit_bytes=VMEM_LIMIT),
        cost_estimate=pl.CostEstimate(flops=flops, bytes_accessed=8 << 20, transcendentals=0),
        name=name,
    )(*scalars, *arrays)


def ring_routes(count):
    spots = [ring_head(at, count) for at in range(count)]
    right = [(spots[at], spots[(at + 1) % count]) for at in range(count)]
    left = [(spots[at], spots[at - 1]) for at in range(count)]
    return right, left


def add_low(one, other):
    return (one.astype(F32) + other.astype(F32)).astype(BF)


def flow_steps(part, going, coming):
    count = lax.axis_size("head")
    place = ring_place(lax.axis_index("head"), count)
    right, left = ring_routes(count)
    rows = part.shape[0] // count
    steps = count // 2

    def mine(owner):
        return lax.dynamic_slice_in_dim(part, lax.rem(owner + count, count) * rows, rows, 0)

    for step in range(1, steps - 1):
        from_left = lax.ppermute(going, "head", right)
        from_right = lax.ppermute(coming, "head", left)
        going = add_low(from_left, mine(place + steps - 1 - step))
        coming = add_low(from_right, mine(place - steps + 1 + step))
        going, coming = yield going, coming
    from_left = lax.ppermute(going, "head", right)
    from_right = lax.ppermute(coming, "head", left)
    yield mine(place).astype(F32) + from_left.astype(F32) + from_right.astype(F32)


def matmul(left, right):
    return jnp.dot(left, right, preferred_element_type=F32)


def rows_inner(left, right):
    return lax.dot_general(left, right, (((0,), (0,)), ((), ())), preferred_element_type=F32)


def cols_inner(left, right):
    return lax.dot_general(left, right, (((1,), (1,)), ((), ())), preferred_element_type=F32)


def rms_scale(values):
    return lax.rsqrt(jnp.mean(values * values, axis=1, keepdims=True) + EPSILON)


def per_device(
    tokens,
    segment_ids,
    norm1_gain,
    w_query,
    w_key,
    w_value,
    w_gate,
    w_out,
    norm2_gain,
    w_mlp_gate,
    w_mlp_up,
    w_down,
    out_grad,
):
    heads = lax.axis_size("head")
    batches = lax.axis_size("batch")
    row_count, width = tokens.shape
    head_size = w_query.shape[1]
    half = w_key.shape[1]
    chunk = row_count // heads
    me = ring_place(lax.axis_index("head"), heads)
    scale_factor = 1.0 / math.sqrt(head_size)

    w_shard = jnp.concatenate([w_query, w_gate, w_key, w_value], axis=1)
    gains = jnp.concatenate([norm1_gain, norm2_gain]).reshape(-1, 128).astype(F32)
    normed_one, queries, gate_logit, kv_all, w_in, out_full, gains, seg_all, down_full = entry(
        tokens, w_shard, w_out, gains, segment_ids.reshape(-1, 128), w_down, 1
    )
    gains, w_mlp_gate, w_mlp_up = lax.optimization_barrier((gains, w_mlp_gate, w_mlp_up))
    seg_all = seg_all.reshape(-1)
    gains = gains.reshape(batches, 2, -1).transpose(1, 0, 2).reshape(2, width)
    gain_one, gain_two = gains[0], gains[1]
    mgate_full = lax.all_gather(w_mlp_gate, "batch", axis=0, tiled=True)
    mup_full = lax.all_gather(w_mlp_up, "batch", axis=0, tiled=True)

    base = lax.axis_index("batch") * row_count
    ids = jnp.arange(DOCUMENTS, dtype=jnp.int32)
    below = jnp.sum((seg_all[None, :] < ids[:, None]).astype(jnp.int32), axis=1)
    starts = jnp.sum(jnp.where(segment_ids[None, :] == ids[:, None], below[:, None], 0), axis=0)
    scalars = (starts, base.reshape(1))
    pair_flops = 4 * row_count * kv_all.shape[0] * head_size
    attended, mixed, lse = local_call(
        functools.partial(attend_kernel, scale_factor),
        scalars,
        (queries, kv_all, starts[None], gate_logit),
        [
            jax.ShapeDtypeStruct((row_count, head_size), F32),
            jax.ShapeDtypeStruct((row_count, head_size), BF),
            jax.ShapeDtypeStruct((1, row_count), F32),
        ],
        [],
        pair_flops,
        "attend",
    )
    (mixed_all,) = spread([mixed], (("head", "cols"),), 2)
    (
        normed_two, hidden, d_pre, mlp_part, resid_own, d_resid, d_resid_low, d_gain_two, d_mixed,
        going, coming,
    ) = mlp_back(
        tokens, mixed_all, out_grad, gain_two[None], out_full, mgate_full, mup_full, down_full, 3
    )
    hold = lax.optimization_barrier
    mixed_own = lax.dynamic_slice_in_dim(mixed_all, me * chunk, chunk, 0)
    flow = flow_steps(mlp_part, going, coming)
    state = next(flow)
    d_out_part = rows_inner(mixed_own, d_resid_low).astype(BF)
    hidden, d_out_part = hold((hidden, d_out_part))
    d_out_part = lax.psum_scatter(d_out_part, "batch", scatter_dimension=1, tiled=True)
    d_down = rows_inner(hidden, out_grad).astype(BF)
    normed_two, d_down, state = hold((normed_two, d_down, state))
    d_down = lax.psum_scatter(d_down, "batch", scatter_dimension=1, tiled=True).astype(F32)
    state = flow.send(state)
    d_mlp = rows_inner(normed_two, d_pre).astype(BF)
    d_mixed, d_mlp, state = hold((d_mixed, d_mlp, state))
    d_mlp = lax.psum_scatter(d_mlp, "batch", scatter_dimension=0, tiled=True).astype(F32)
    while isinstance(state, tuple):
        state = flow.send(state)

    d_queries, d_gate_logit, d_kv_all = local_call(
        functools.partial(attend_back_kernel, scale_factor),
        scalars,
        (queries, kv_all, starts[None], gate_logit, attended, d_mixed, lse),
        [
            jax.ShapeDtypeStruct((row_count, head_size), BF),
            jax.ShapeDtypeStruct((row_count, head_size), BF),
            jax.ShapeDtypeStruct(kv_all.shape, BF),
        ],
        [pltpu.VMEM((kv_all.shape[0], head_size), F32)] * 2,
        5 * pair_flops // 2,
        "attend_back",
    )
    d_kv_all, state, d_out_part = hold((d_kv_all, state, d_out_part))
    out_own = (resid_own + state).astype(BF)
    d_kv = fold(d_kv_all, row_count, 4)
    d_cat = jnp.concatenate([d_queries, d_gate_logit, d_kv], axis=1)
    d_cat, d_down = hold((d_cat, d_down))
    d_in = rows_inner(normed_one, d_cat).astype(BF)
    d_cat, d_in = hold((d_cat, d_in))
    d_in = lax.psum_scatter(d_in, "batch", scatter_dimension=0, tiled=True).astype(F32)
    inputs_own = lax.dynamic_slice_in_dim(tokens, me * chunk, chunk, 0)
    output, d_tokens, d_gains, d_out = tail(
        d_cat, w_in, inputs_own, gain_one[None], d_resid, out_own, d_out_part, d_gain_two, 5
    )
    output = output.reshape(row_count, width)
    d_tokens = d_tokens.reshape(row_count, width)
    hidden_own = w_mlp_gate.shape[1]
    return (
        output,
        d_tokens,
        d_gains[0],
        d_in[:, :head_size],
        d_in[:, 2 * head_size : 2 * head_size + half],
        d_in[:, 2 * head_size + half :],
        d_in[:, head_size : 2 * head_size],
        d_out,
        d_gains[1],
        d_mlp[:, :hidden_own],
        d_mlp[:, hidden_own:],
        d_down,
    )


def solution(mesh):
    return jax.shard_map(
        per_device,
        mesh=mesh,
        in_specs=(
            P("batch", None),
            P("batch"),
            P("batch"),
            P("batch", "head"),
            P("batch", "head"),
            P("batch", "head"),
            P("batch", "head"),
            P("head", "batch"),
            P("batch"),
            P("batch", "head"),
            P("batch", "head"),
            P("head", "batch"),
            P("batch", None),
        ),
        out_specs=(
            P("batch", None),
            P("batch", None),
            P("batch"),
            P("batch", "head"),
            P("batch", "head"),
            P("batch", "head"),
            P("batch", "head"),
            P("head", "batch"),
            P("batch"),
            P("batch", "head"),
            P("batch", "head"),
            P("head", "batch"),
        ),
        check_vma=False,
    )
```

```python
import functools
import math

import jax
import jax.numpy as jnp
from jax import lax
from jax.experimental import pallas as pl
from jax.experimental.pallas import tpu as pltpu
from jax.sharding import PartitionSpec as P

EPSILON = 1e-06
MASKED = -1e30
DOCUMENTS = 7
BF = jnp.bfloat16
F32 = jnp.float32


MESH = pl.DeviceIdType.MESH
VMEM_LIMIT = 60 << 20


def ring_place(head, count):
    high, low = head // 2, head % 2
    return (1 - low) * high + low * (count - 1 - high)


def ring_head(place, count):
    low = place // (count // 2)
    high = (1 - low) * place + low * (count - 1 - place)
    return 2 * high + low


def ring_setup(count):
    batch = lax.axis_index("batch")
    place = ring_place(lax.axis_index("head"), count)
    right = (batch, ring_head(lax.rem(place + 1, count), count))
    left = (batch, ring_head(lax.rem(place + count - 1, count), count))
    return place, right, left


def greet(devices):
    barrier = pltpu.get_barrier_semaphore()
    for device in devices:
        pl.semaphore_signal(barrier, inc=1, device_id=device, device_id_type=MESH)
    pl.semaphore_wait(barrier, len(devices))


def send(source, target, sems, slot, device):
    copy = pltpu.make_async_remote_copy(
        src_ref=source,
        dst_ref=target,
        send_sem=sems[0].at[slot],
        recv_sem=sems[1].at[slot],
        device_id=device,
        device_id_type=MESH,
    )
    copy.start()
    return copy


def half_of(extent, flow):
    if extent[1] % 256:
        return (pl.ds(flow * (extent[0] // 2), extent[0] // 2), slice(None))
    return (slice(None), pl.ds(flow * (extent[1] // 2), extent[1] // 2))


def place_of(whole, own, chunk, form):
    rows, wide = own.shape[-2:]
    if form == "lead":
        return whole.at[chunk]
    if form == "rows":
        return whole.at[pl.ds(pl.multiple_of(chunk * rows, rows), rows)]
    return whole.at[:, pl.ds(pl.multiple_of(chunk * wide, wide), wide)]


def spread_kernel(count, batches, plans, *refs):
    steps = count // 2
    arrays = len(plans)
    own_refs, all_refs = refs[:arrays], refs[arrays : 2 * arrays]
    send_sem, recv_sem, local_sem = refs[2 * arrays :]
    place, right, left = ring_setup(count)
    head = lax.axis_index("head")
    batch = lax.axis_index("batch")
    across, core = batch // 2, lax.rem(batch, 2)
    others = batches // 2
    twin = (across * 2 + 1 - core, head)
    peers = [(lax.rem(across + hop, others) * 2 + core, head) for hop in range(1, others)]
    ring = any(axis == "head" for axis, _ in plans)
    grid = any(axis == "batch" for axis, _ in plans)
    greet((right, left) * ring + (twin, *peers) * grid)
    sems = (send_sem, recv_sem)
    slot = 0
    waiting, arriving, local = [], [], []

    def go(source, target, device):
        nonlocal slot
        copy = send(source, target, sems, slot, device)
        slot += 1
        waiting.append(copy)
        return copy

    onward = []
    for index, (axis, form) in enumerate(plans):
        own, whole = own_refs[index], all_refs[index]
        spot = place if axis == "head" else batch
        mine = place_of(whole, own, spot, form)
        copy = pltpu.make_async_copy(own, mine, local_sem.at[index])
        copy.start()
        local.append(copy)
        if axis == "batch":
            for hop, peer in enumerate(peers, 1):
                source = lax.rem(across + others - hop, others) * 2 + core
                onward.append((go(own, mine, peer), place_of(whole, own, source, form)))
            arriving.append(go(own, mine, twin))
    copies = [None] * (2 * arrays)
    for step in range(steps):
        for index, (axis, form) in enumerate(plans):
            if axis != "head":
                continue
            own = own_refs[index]
            for flow, chunk, device in ((0, place - step, right), (1, place + step, left)):
                at = 2 * index + flow
                if step:
                    copies[at].wait_recv()
                chunk = lax.rem(chunk + count, count)
                target = place_of(all_refs[index], own, chunk, form)
                source = target if step else own
                if step == steps - 1:
                    part = half_of(own.shape, flow)
                    source = source.at[part]
                    target = target.at[part]
                copies[at] = go(source, target, device)
        if step == 0 or not ring:
            for copy, block in onward:
                copy.wait_recv()
                arriving.append(go(block, block, twin))
            onward = []
    for copy in copies:
        if copy is not None:
            arriving.append(copy)
    for copy in arriving:
        copy.wait_recv()
    for copy in waiting:
        copy.wait_send()
    for copy in local:
        copy.wait()


def spread(arrays, plans, collective_id):
    count = lax.axis_size("head")
    batches = lax.axis_size("batch")
    shapes = []
    slots = 0
    for array, (axis, form) in zip(arrays, plans):
        many = count if axis == "head" else batches
        slots += count if axis == "head" else batches - 1
        if form == "lead":
            shapes.append((many, *array.shape))
        elif form == "rows":
            shapes.append((many * array.shape[0], array.shape[1]))
        else:
            shapes.append((array.shape[0], many * array.shape[1]))
    hbm = pl.BlockSpec(memory_space=pl.ANY)
    return pl.pallas_call(
        functools.partial(spread_kernel, count, batches, plans),
        out_shape=[jax.ShapeDtypeStruct(shape, a.dtype) for shape, a in zip(shapes, arrays)],
        in_specs=[pl.BlockSpec(memory_space=pltpu.VMEM)] * len(arrays),
        out_specs=[hbm] * len(arrays),
        scratch_shapes=[
            pltpu.SemaphoreType.DMA((slots,)),
            pltpu.SemaphoreType.DMA((slots,)),
            pltpu.SemaphoreType.DMA((len(arrays),)),
        ],
        compiler_params=pltpu.CompilerParams(
            collective_id=collective_id, has_side_effects=True, vmem_limit_bytes=VMEM_LIMIT
        ),
        name=f"spread_{collective_id}",
    )(*arrays)


def mlp_kernel(
    count, x_hbm, a_hbm, dy_hbm, gain_ref, out_w, gate_w, up_w, down_w,
    n2_hbm, hid_hbm, grad_hbm, mlp_hbm, h1_ref, dh1_ref, low_ref, dgain_ref, da_ref, ahead_ref, behind_ref,
    x_s, a_s, dy_s, n2_s, hid_s, grad_s, mlp_s, h1_s, dy_own, da_part, mlp_far, mlp_got,
    right_part, left_part, right_got, left_got,
    in_sem, out_sem, send_sem, recv_sem, da_send, da_recv, far_send, far_recv,
):
    steps = count // 2
    rows = x_hbm.shape[0] // count
    width = x_hbm.shape[1]
    hidden = gate_w.shape[1]
    side = width // 2
    tile = 256
    inner = 256 if hidden % 256 == 0 else 128
    size = da_ref.shape[1]
    place, right, left = ring_setup(count)

    def member(hop):
        spot = lax.rem(place + hop, count)
        return spot, (lax.axis_index("batch"), ring_head(spot, count))

    greet([member(hop)[1] for hop in range(1, count)])

    def owners(group):
        first = jnp.where(group == 0, 1, 0)
        one = lax.rem(place + steps - group, count)
        two = lax.rem(place - steps + group + first * steps + count, count)
        return one, two

    def span(owner):
        return pl.ds(pl.multiple_of(owner * rows, rows), rows)

    def loads(group, slot):
        return [
            pltpu.make_async_copy(
                source.at[span(owner)],
                target.at[slot, pl.ds(at * rows, rows)],
                in_sem.at[slot, 2 * index + at],
            )
            for index, (source, target) in enumerate(((x_hbm, x_s), (a_hbm, a_s), (dy_hbm, dy_s)))
            for at, owner in enumerate(owners(group))
        ]

    def stores(group, slot):
        return [
            pltpu.make_async_copy(
                source.at[slot, pl.ds(at * rows, rows)],
                target.at[span(owner)],
                out_sem.at[slot, 2 * index + at],
            )
            for index, (source, target) in enumerate(
                ((n2_s, n2_hbm), (hid_s, hid_hbm), (grad_s, grad_hbm), (mlp_s, mlp_hbm))
            )
            for at, owner in enumerate(owners(group))
        ]

    def passing(source, target, flow, step, device):
        return pltpu.make_async_remote_copy(
            src_ref=source,
            dst_ref=target,
            send_sem=send_sem.at[flow * steps + step],
            recv_sem=recv_sem.at[flow * steps + step],
            device_id=device,
            device_id_type=MESH,
        )

    def first_copies():
        ahead, behind = pl.ds(0, side), pl.ds(side, side)
        return (
            passing(right_part.at[0, :, ahead], right_got.at[0, :, ahead], 0, 0, right),
            passing(right_part.at[0, :, behind], left_got.at[0, :, behind], 1, 0, left),
        )

    def later_copies(step):
        return (
            passing(right_part.at[step], right_got.at[step], 0, step, right),
            passing(left_part.at[step], left_got.at[step], 1, step, left),
        )

    for copy in loads(0, 0):
        copy.start()

    @pl.loop(0, steps)
    def _(group):
        slot = lax.rem(group, 2)
        for copy in loads(group, slot):
            copy.wait()

        @pl.when(group + 1 < steps)
        def _():
            for copy in loads(group + 1, 1 - slot):
                copy.start()

        @pl.when(group >= 2)
        def _():
            for copy in stores(group - 2, slot):
                copy.wait()

        mixed = a_s[slot]

        def residual(at, total):
            cols = pl.ds(pl.multiple_of(at * tile, tile), tile)
            values = x_s[slot, :, cols].astype(F32) + matmul(mixed, out_w[:, cols])
            h1_s[:, cols] = values
            return total + jnp.sum(values * values, axis=1, keepdims=True)

        total = lax.fori_loop(0, width // tile, residual, jnp.zeros((2 * rows, 1), F32))
        scale = lax.rsqrt(total / width + EPSILON)

        @pl.when(group == 0)
        def _():
            h1_ref[...] = h1_s[pl.ds(rows, rows)]
            dy_own[...] = dy_s[slot, pl.ds(rows, rows)]

        @pl.loop(0, width // tile)
        def _(at):
            cols = pl.ds(pl.multiple_of(at * tile, tile), tile)
            n2_s[slot, :, cols] = (h1_s[:, cols] * scale * gain_ref[:, cols]).astype(BF)

        normed = n2_s[slot]
        dy = dy_s[slot]

        @pl.loop(0, hidden // inner)
        def _(at):
            cols = pl.ds(pl.multiple_of(at * inner, inner), inner)
            cols_up = pl.ds(pl.multiple_of(hidden + at * inner, inner), inner)
            gate = matmul(normed, gate_w[:, cols])
            up = matmul(normed, up_w[:, cols])
            d_hidden = cols_inner(dy, down_w[cols])
            sig = jax.nn.sigmoid(gate)
            silu = gate * sig
            hid_s[slot, :, cols] = (silu * up).astype(BF)
            grad_s[slot, :, cols] = (d_hidden * up * sig * (1.0 + gate * (1.0 - sig))).astype(BF)
            grad_s[slot, :, cols_up] = (d_hidden * silu).astype(BF)

        hid = hid_s[slot]
        d_gate = grad_s[slot, :, :hidden]
        d_up = grad_s[slot, :, hidden:]

        @pl.loop(0, width // tile)
        def _(at):
            cols = pl.ds(pl.multiple_of(at * tile, tile), tile)
            part = (cols_inner(d_gate, gate_w[cols]) + cols_inner(d_up, up_w[cols])).astype(BF)
            right_part[group, :, cols] = part[:rows]
            left_part[group, :, cols] = part[rows:]
            mlp_s[slot, :, cols] = matmul(hid, down_w[:, cols]).astype(BF)

        for copy in stores(group, slot):
            copy.start()

        @pl.when(group == 0)
        def _():
            mlp_far[...] = mlp_s[slot, pl.ds(0, rows)]

        @pl.when(group == 1)
        def _():
            ahead_ref[...] = mlp_s[slot, pl.ds(0, rows)]
            behind_ref[...] = mlp_s[slot, pl.ds(rows, rows)]

        @pl.when(group == 0)
        def _():
            for copy in first_copies():
                copy.start()

        @pl.when(group == 1)
        def _():
            one, two = first_copies()
            one.wait_recv()
            two.wait_recv()
            ahead, behind = pl.ds(0, side), pl.ds(side, side)
            right_part[1, :, ahead] = add_low(right_part[1, :, ahead], right_got[0, :, ahead])
            left_part[1, :, behind] = add_low(left_part[1, :, behind], left_got[0, :, behind])

        @pl.when(group >= 2)
        def _():
            one, two = later_copies(group - 1)
            one.wait_recv()
            right_part[group] = add_low(right_part[group], right_got[group - 1])
            two.wait_recv()
            left_part[group] = add_low(left_part[group], left_got[group - 1])

        @pl.when(group >= 1)
        def _():
            for copy in later_copies(group):
                copy.start()

    for copy in later_copies(steps - 1):
        copy.wait_recv()
    far_copies = [
        pltpu.make_async_remote_copy(
            src_ref=mlp_far.at[:, pl.ds(flow * side, side)],
            dst_ref=mlp_got.at[flow],
            send_sem=far_send.at[flow],
            recv_sem=far_recv.at[flow],
            device_id=device,
            device_id_type=MESH,
        )
        for flow, device in ((0, right), (1, left))
    ]
    for copy in far_copies:
        copy.start()

    def tile_of(at):
        return pl.ds(pl.multiple_of(at * tile, tile), tile)

    def collect(at, state):
        squares, mean = state
        cols = tile_of(at)
        dn2 = (
            left_part[0, :, cols].astype(F32)
            + right_got[steps - 1, :, cols].astype(F32)
            + left_got[steps - 1, :, cols].astype(F32)
        )
        dh1_ref[:, cols] = dn2
        h1 = h1_ref[:, cols]
        squares = squares + jnp.sum(h1 * h1, axis=1, keepdims=True)
        return squares, mean + jnp.sum(gain_ref[:, cols] * dn2 * h1, axis=1, keepdims=True)

    zero = jnp.zeros((rows, 1), F32)
    squares, mean = lax.fori_loop(0, width // tile, collect, (zero, zero))
    scale_own = lax.rsqrt(squares / width + EPSILON)
    pull = scale_own * scale_own * scale_own * (mean / width)

    @pl.loop(0, width // tile)
    def _(at):
        cols = tile_of(at)
        dn2, h1 = dh1_ref[:, cols], h1_ref[:, cols]
        dgain_ref[:, cols] = jnp.sum(dn2 * h1 * scale_own, axis=0, keepdims=True)
        d_resid = dy_own[:, cols].astype(F32) + scale_own * (gain_ref[:, cols] * dn2) - h1 * pull
        dh1_ref[:, cols] = d_resid
        low_ref[:, cols] = d_resid.astype(BF)

    def da_copy(hop):
        return pltpu.make_async_remote_copy(
            src_ref=da_part.at[hop],
            dst_ref=da_ref.at[span(place)],
            send_sem=da_send.at[hop],
            recv_sem=da_recv.at[hop],
            device_id=member(hop)[1],
            device_id_type=MESH,
        )

    low = low_ref[...]

    @pl.loop(1, count)
    def _(hop):
        spot = member(hop)[0]
        part = cols_inner(low, out_w[pl.ds(pl.multiple_of(spot * size, size), size)])
        da_part[hop] = part.astype(BF)
        da_copy(hop).start()

    own_w = out_w[pl.ds(pl.multiple_of(place * size, size), size)]
    da_ref[span(place)] = cols_inner(low, own_w).astype(BF)

    @pl.loop(1, count)
    def _(hop):
        da_copy(hop).wait_recv()
        da_copy(hop).wait_send()

    for flow, held in ((0, ahead_ref), (1, behind_ref)):
        far_copies[flow].wait_recv()
        cols = pl.ds(flow * side, side)
        held[:, cols] = add_low(held[:, cols], mlp_got[flow])
        far_copies[flow].wait_send()

    for copy in first_copies():
        copy.wait_send()
    for step in range(1, steps):
        for copy in later_copies(step):
            copy.wait_send()
    for group in range(max(steps - 2, 0), steps):
        for copy in stores(group, group % 2):
            copy.wait()


def mlp_back(tokens, mixed, dy, gain, out_w, gate_w, up_w, down_w, collective_id):
    count = lax.axis_size("head")
    total, width = tokens.shape
    hidden = gate_w.shape[1]
    rows, steps = total // count, count // 2
    size = mixed.shape[1] // count
    vmem = pl.BlockSpec(memory_space=pltpu.VMEM)
    hbm = pl.BlockSpec(memory_space=pl.ANY)

    def slots(wide, dtype=BF):
        return pltpu.VMEM((2, 2 * rows, wide), dtype)

    part = pltpu.VMEM((steps, rows, width), BF)
    flops = 2 * total * width * (mixed.shape[1] + 6 * hidden)
    return pl.pallas_call(
        functools.partial(mlp_kernel, count),
        out_shape=[
            jax.ShapeDtypeStruct((total, width), BF),
            jax.ShapeDtypeStruct((total, hidden), BF),
            jax.ShapeDtypeStruct((total, 2 * hidden), BF),
            jax.ShapeDtypeStruct((total, width), BF),
            jax.ShapeDtypeStruct((rows, width), F32),
            jax.ShapeDtypeStruct((rows, width), F32),
            jax.ShapeDtypeStruct((rows, width), BF),
            jax.ShapeDtypeStruct((1, width), F32),
            jax.ShapeDtypeStruct((total, size), BF),
            jax.ShapeDtypeStruct((rows, width), BF),
            jax.ShapeDtypeStruct((rows, width), BF),
        ],
        in_specs=[hbm] * 3 + [vmem] * 5,
        out_specs=[hbm] * 4 + [vmem] * 7,
        scratch_shapes=[
            slots(width), slots(mixed.shape[1]), slots(width), slots(width), slots(hidden),
            slots(2 * hidden), slots(width), pltpu.VMEM((2 * rows, width), F32),
            pltpu.VMEM((rows, width), BF), pltpu.VMEM((count, rows, size), BF),
            pltpu.VMEM((rows, width), BF), pltpu.VMEM((2, rows, width // 2), BF),
            part, part, part, part,
            pltpu.SemaphoreType.DMA((2, 6)), pltpu.SemaphoreType.DMA((2, 8)),
            pltpu.SemaphoreType.DMA((count,)), pltpu.SemaphoreType.DMA((count,)),
            pltpu.SemaphoreType.DMA((count,)), pltpu.SemaphoreType.DMA((count,)),
            pltpu.SemaphoreType.DMA((2,)), pltpu.SemaphoreType.DMA((2,)),
        ],
        compiler_params=pltpu.CompilerParams(
            collective_id=collective_id, has_side_effects=True, vmem_limit_bytes=VMEM_LIMIT
        ),
        cost_estimate=pl.CostEstimate(flops=flops, bytes_accessed=40 << 20, transcendentals=0),
        name="mlp_back",
    )(tokens, mixed, dy, gain, out_w, gate_w, up_w, down_w)


def entry_kernel(
    count, batches, x_ref, w_ref, out_ref, gain_ref, seg_ref,
    n1_ref, q_ref, logit_ref, kv_ref, w_all, out_all, gain_all, seg_all,
    send_sem, recv_sem, local_sem,
):
    steps = count // 2
    others = batches // 2
    rows, width = x_ref.shape
    depth = w_ref.shape[0]
    size, wide = out_ref.shape
    block = 256
    place, right, left = ring_setup(count)
    head = lax.axis_index("head")
    batch = lax.axis_index("batch")
    across, core, low = batch // 2, lax.rem(batch, 2), lax.rem(head, 2)
    twin = (across * 2 + 1 - core, head)
    mate = (batch, head + 1 - 2 * low)
    spots = [lax.rem(across + hop, others) for hop in range(others)]
    backs = [lax.rem(across + others - hop, others) for hop in range(others)]
    peers = [(spot * 2 + core, head) for spot in spots]
    far_peers = [(spot * 2 + 1 - core, head) for spot in spots]
    greet((twin, mate, right, left, *peers[1:], *far_peers[1:]))
    sems = (send_sem, recv_sem)
    slot = 0
    copies = []

    def go(source, target, device):
        nonlocal slot
        copy = send(source, target, sems, slot, device)
        slot += 1
        copies.append(copy)
        return copy

    def part(at, extent):
        return pl.ds(pl.multiple_of(at * extent, extent), extent)

    def both(view, own):
        out = [go(own, view(batch), peers[hop]) for hop in range(1, others)]
        return out, [go(own, view(batch), twin)]

    def pass_on(view, arrived):
        out = []
        for hop in range(1, others):
            arrived[hop - 1].wait_recv()
            there = view(backs[hop] * 2 + core)
            out.append(go(there, there, twin))
        return out

    local = []

    def stay(source, target):
        copy = pltpu.make_async_copy(source, target, local_sem.at[len(local)])
        copy.start()
        local.append(copy)

    def main_view(at):
        return w_all.at[part(at, depth), pl.ds(0, 3 * size)]

    def mate_view(at):
        return w_all.at[part(at, depth), pl.ds(3 * size, size)]

    def out_view(chunk, at):
        return out_all.at[part(chunk, size), part(at, wide)]

    small = []
    for own, whole in ((gain_ref, gain_all), (seg_ref, seg_all)):
        for device in (twin, *peers[1:], *far_peers[1:]):
            small.append(go(own, whole.at[batch], device))
        stay(own, whole.at[batch])
    from_mate = go(w_ref.at[:, pl.ds(2 * size, size)], mate_view(batch), mate)
    main_out, main_twin = both(main_view, w_ref)
    stay(w_ref, main_view(batch))
    out_peers = [go(out_ref, out_view(place, batch), peers[hop]) for hop in range(1, others)]
    stay(out_ref, out_view(place, batch))
    flows = [[None, None] for _ in range(others)]

    def ring(step):
        for hop in range(others):
            lane = spots[0] if hop == 0 else backs[hop]
            at = lane * 2 + core
            if step == 0 and hop:
                out_peers[hop - 1].wait_recv()
            for flow, chunk, device in ((0, place - step, right), (1, place + step, left)):
                if step:
                    flows[hop][flow].wait_recv()
                target = out_view(lax.rem(chunk + count, count), at)
                source = out_ref if step == 0 and hop == 0 else target
                if step == steps - 1:
                    cut = (pl.ds(flow * (size // 2), size // 2), slice(None))
                    source, target = source.at[cut], target.at[cut]
                flows[hop][flow] = go(source, target, device)

    for copy in small:
        copy.wait_recv()
    for copy in local[:2]:
        copy.wait()

    def normalize(at):
        here = part(at, block)

        def squares(tile, total):
            values = x_ref[here, part(tile, 256)].astype(F32)
            return total + jnp.sum(values * values, axis=1, keepdims=True)

        total = lax.fori_loop(0, width // 256, squares, jnp.zeros((block, 1), F32))
        scale = lax.rsqrt(total / width + EPSILON)

        @pl.loop(0, batches)
        def _(owner):
            for tile in range(depth // 128):
                cols = pl.ds(pl.multiple_of(owner * depth + tile * 128, 128), 128)
                values = x_ref[here, cols].astype(F32) * scale
                n1_ref[here, cols] = (values * gain_all[owner, pl.ds(tile, 1)]).astype(BF)

    blocks = rows // block
    middle = blocks // 2

    @pl.loop(0, middle)
    def _(at):
        normalize(at)

    from_mate.wait_recv()
    mate_out, mate_twin = both(mate_view, mate_view(batch))
    ring(0)

    @pl.loop(middle, blocks)
    def _(at):
        normalize(at)

    main_passed = pass_on(main_view, main_out)
    mate_passed = pass_on(mate_view, mate_out)
    for copy in (*main_twin, *mate_twin, *main_passed, *mate_passed):
        copy.wait_recv()
    for copy in local[2:]:
        copy.wait()

    def kv_view(at):
        return kv_ref.at[part(at, rows)]

    @pl.loop(0, blocks)
    def _(at):
        here = part(at, block)
        values = matmul(n1_ref[here], w_all[:, pl.ds(2 * size, 2 * size)])
        one, two = values[:, :size], values[:, size:]
        first = jnp.where(low == 0, one, two).astype(BF)
        second = jnp.where(low == 0, two, one).astype(BF)
        half = size // 2
        there = pl.ds(pl.multiple_of(batch * rows + at * block, block), block)
        kv_ref[there, pl.ds(0, size)] = jnp.concatenate([first[:, :half], second[:, :half]], 1)
        kv_ref[there, pl.ds(size, size)] = jnp.concatenate([first[:, half:], second[:, half:]], 1)

    kv_out, kv_twin = both(kv_view, kv_view(batch))
    ring(1)

    @pl.loop(0, blocks)
    def _(at):
        here = part(at, block)
        values = matmul(n1_ref[here], w_all[:, pl.ds(0, 2 * size)])
        q_ref[here] = values[:, :size].astype(BF)
        logit_ref[here] = values[:, size:]

    for step in range(2, steps):
        ring(step)
    kv_passed = pass_on(kv_view, kv_out)
    for pair in flows:
        for copy in pair:
            copy.wait_recv()
    swaps = []
    for hop in range(others):
        there = out_all.at[:, part(spots[hop] * 2 + core, wide)]
        swaps.append(go(there, there, twin))
    for copy in (*kv_twin, *kv_passed, *swaps):
        copy.wait_recv()
    for copy in copies:
        copy.wait_send()


def entry(tokens, w_shard, w_out, gains, segments, collective_id):
    count = lax.axis_size("head")
    batches = lax.axis_size("batch")
    others = batches // 2
    rows, width = tokens.shape
    size, wide = w_out.shape
    vmem = pl.BlockSpec(memory_space=pltpu.VMEM)
    slots = 6 * batches + others * (count + 3)
    sems = pltpu.SemaphoreType.DMA((slots,))
    return pl.pallas_call(
        functools.partial(entry_kernel, count, batches),
        out_shape=[
            jax.ShapeDtypeStruct((rows, width), BF),
            jax.ShapeDtypeStruct((rows, size), BF),
            jax.ShapeDtypeStruct((rows, size), F32),
            jax.ShapeDtypeStruct((batches * rows, 2 * size), BF),
            jax.ShapeDtypeStruct((width, 4 * size), BF),
            jax.ShapeDtypeStruct((count * size, batches * wide), BF),
            jax.ShapeDtypeStruct((batches, *gains.shape), F32),
            jax.ShapeDtypeStruct((batches, *segments.shape), jnp.int32),
        ],
        in_specs=[vmem] * 5,
        out_specs=[vmem] * 8,
        scratch_shapes=[sems, sems, pltpu.SemaphoreType.DMA((5,))],
        compiler_params=pltpu.CompilerParams(
            collective_id=collective_id, has_side_effects=True, vmem_limit_bytes=VMEM_LIMIT
        ),
        name="entry",
    )(tokens, w_shard, w_out, gains, segments)


KEY_BLOCK = 512
QUERY_BLOCK = 256


def key_range(start_ref, base, query_block):
    first = query_block * QUERY_BLOCK
    lowest = start_ref[first]
    highest = start_ref[first + QUERY_BLOCK - 1]
    begin = lowest // KEY_BLOCK
    end = (base + first + QUERY_BLOCK - 1) // KEY_BLOCK + 1
    full_begin = jnp.minimum((highest + KEY_BLOCK - 1) // KEY_BLOCK, end)
    full_end = jnp.maximum((base + first + 1) // KEY_BLOCK, full_begin)
    return begin, full_begin, full_end, end


def allowed_pairs(key_block, start_row, base_row):
    shape = (KEY_BLOCK, QUERY_BLOCK)
    key_pos = key_block * KEY_BLOCK + lax.broadcasted_iota(jnp.int32, shape, 0)
    query_pos = base_row + lax.broadcasted_iota(jnp.int32, shape, 1)
    return (key_pos >= start_row) & (key_pos <= query_pos)


def attend_kernel(
    scale, start_sm, base_sm, q_ref, kv_ref, start_ref, logit_ref, o_ref, a_ref, lse_ref
):
    base = base_sm[0]
    size = q_ref.shape[1]
    factor = scale * math.log2(math.e)

    @pl.loop(0, q_ref.shape[0] // QUERY_BLOCK)
    def _(block):
        rows = pl.ds(pl.multiple_of(block * QUERY_BLOCK, QUERY_BLOCK), QUERY_BLOCK)
        queries = q_ref[rows]
        start_row = start_ref[:, rows]
        begin, full_begin, full_end, end = key_range(start_sm, base, block)

        def step(masked, at, state):
            old_max, old_sum, total = state
            keys = pl.ds(pl.multiple_of(at * KEY_BLOCK, KEY_BLOCK), KEY_BLOCK)
            scores = cols_inner(kv_ref[keys, :size], queries)
            if masked:
                allowed = allowed_pairs(at, start_row, base + block * QUERY_BLOCK)
                scores = jnp.where(allowed, scores, MASKED)
            new_max = jnp.maximum(old_max, jnp.max(scores, axis=0, keepdims=True))
            keep = jnp.exp2((old_max - new_max) * factor)
            weights = jnp.exp2(scores * factor - new_max * factor)
            new_sum = old_sum * keep + jnp.sum(weights, axis=0, keepdims=True)
            total = total * keep + rows_inner(kv_ref[keys, size:], weights.astype(BF))
            return new_max, new_sum, total

        state = (
            jnp.full((1, QUERY_BLOCK), MASKED, F32),
            jnp.zeros((1, QUERY_BLOCK), F32),
            jnp.zeros((size, QUERY_BLOCK), F32),
        )
        state = lax.fori_loop(begin, full_begin, functools.partial(step, True), state)
        state = lax.fori_loop(full_begin, full_end, functools.partial(step, False), state)
        state = lax.fori_loop(full_end, end, functools.partial(step, True), state)
        run_max, run_sum, total = state
        lse_ref[:, rows] = run_max * factor + jnp.log2(run_sum)
        attended = (total / run_sum).T
        o_ref[rows] = attended
        a_ref[rows] = (attended * jax.nn.sigmoid(logit_ref[rows])).astype(BF)


def attend_back_kernel(
    scale, start_sm, base_sm, q_ref, kv_ref, start_ref, logit_ref, o_ref, da_ref, lse_ref,
    dq_ref, dg_ref, dkv_ref, dk_acc, dv_acc,
):
    base = base_sm[0]
    size = q_ref.shape[1]
    factor = scale * math.log2(math.e)
    dk_acc[...] = jnp.zeros_like(dk_acc)
    dv_acc[...] = jnp.zeros_like(dv_acc)

    @pl.loop(0, q_ref.shape[0] // QUERY_BLOCK)
    def _(block):
        rows = pl.ds(pl.multiple_of(block * QUERY_BLOCK, QUERY_BLOCK), QUERY_BLOCK)
        queries = q_ref[rows]
        start_row = start_ref[:, rows]
        lse = lse_ref[:, rows]
        gate = jax.nn.sigmoid(logit_ref[rows])
        attended = o_ref[rows]
        d_mixed = da_ref[rows].astype(F32)
        d_attended = (d_mixed * gate).astype(BF)
        dg_ref[rows] = (d_mixed * attended * gate * (1.0 - gate)).astype(BF)
        delta = jnp.sum((d_attended.astype(F32) * attended).T, axis=0, keepdims=True)
        begin, full_begin, full_end, end = key_range(start_sm, base, block)

        def step(masked, at, d_queries):
            keys = pl.ds(pl.multiple_of(at * KEY_BLOCK, KEY_BLOCK), KEY_BLOCK)
            key_block = kv_ref[keys, :size]
            probs = jnp.exp2(cols_inner(key_block, queries) * factor - lse)
            if masked:
                allowed = allowed_pairs(at, start_row, base + block * QUERY_BLOCK)
                probs = jnp.where(allowed, probs, 0.0)
            d_probs = cols_inner(kv_ref[keys, size:], d_attended)
            d_scores = (probs * (d_probs - delta) * scale).astype(BF)
            dv_acc[keys] += matmul(probs.astype(BF), d_attended)
            dk_acc[keys] += matmul(d_scores, queries)
            return d_queries + rows_inner(key_block, d_scores)

        d_queries = jnp.zeros((size, QUERY_BLOCK), F32)
        d_queries = lax.fori_loop(begin, full_begin, functools.partial(step, True), d_queries)
        d_queries = lax.fori_loop(full_begin, full_end, functools.partial(step, False), d_queries)
        d_queries = lax.fori_loop(full_end, end, functools.partial(step, True), d_queries)
        dq_ref[rows] = d_queries.T.astype(BF)

    @pl.loop(0, kv_ref.shape[0] // KEY_BLOCK)
    def _(at):
        keys = pl.ds(pl.multiple_of(at * KEY_BLOCK, KEY_BLOCK), KEY_BLOCK)
        dk, dv = dk_acc[keys].astype(BF), dv_acc[keys].astype(BF)
        half = size // 2
        dkv_ref[keys, :size] = jnp.concatenate([dk[:, :half], dv[:, :half]], axis=1)
        dkv_ref[keys, size:] = jnp.concatenate([dk[:, half:], dv[:, half:]], axis=1)


def fold_kernel(
    batches, part_ref, own_ref, core_got, x_first, x_second, y_first, y_second, held, send_sem, recv_sem
):
    rows, size = own_ref.shape
    half = rows // 2
    others = batches // 2
    head = lax.axis_index("head")
    batch = lax.axis_index("batch")
    across, core, low = batch // 2, lax.rem(batch, 2), lax.rem(head, 2)
    twin = (across * 2 + 1 - core, head)
    mate = (batch, head + 1 - 2 * low)
    spots = [lax.rem(across + hop, others) for hop in range(others)]
    peers = [(spot * 2 + core, head) for spot in spots]
    greet((twin, mate, *peers[1:]))
    sems = (send_sem, recv_sem)
    slot = 0
    copies = []
    mine = pl.ds(pl.multiple_of(low * size, size), size)
    given = pl.ds(pl.multiple_of((1 - low) * size, size), size)
    top, bottom = pl.ds(0, half), pl.ds(half, half)

    def block(at, side):
        return pl.ds(pl.multiple_of((2 * at + side) * rows, rows), rows)

    def go(source, target, device):
        nonlocal slot
        copy = send(source, target, sems, slot, device)
        slot += 1
        copies.append(copy)
        return copy

    order = list(range(1, others)) + [0]
    first = [go(part_ref.at[block(spots[hop], 1 - core)], core_got.at[spots[hop]], twin) for hop in order]
    tops, bottoms = [], []
    for copy, hop in zip(first, order):
        copy.wait_recv()
        spot = spots[hop]
        core_got[spot] = add_low(core_got[spot], part_ref[block(spot, core)])
        bottoms.append(go(core_got.at[spot, bottom, given], y_first.at[spot], mate))
        if hop:
            tops.append(go(core_got.at[spot, top], x_first.at[hop - 1], peers[hop]))
    total = core_got[across, top].astype(F32)
    for hop in range(1, others):
        tops[hop - 1].wait_recv()
        total = total + x_first[hop - 1].astype(F32)
    held[...] = total.astype(BF)
    last = go(held.at[:, given], y_second, mate)
    ends = []
    for copy, hop in zip(bottoms, order):
        copy.wait_recv()
        spot = spots[hop]
        y_first[spot] = add_low(y_first[spot], core_got[spot, bottom, mine])
        if hop:
            ends.append(go(y_first.at[spot], x_second.at[hop - 1], peers[hop]))
    last.wait_recv()
    own_ref[top] = add_low(held[:, mine], y_second[...])
    total = y_first[across].astype(F32)
    for hop in range(1, others):
        ends[hop - 1].wait_recv()
        total = total + x_second[hop - 1].astype(F32)
    own_ref[bottom] = total.astype(BF)
    for copy in copies:
        copy.wait_send()


def fold(part, rows, collective_id):
    batches = lax.axis_size("batch")
    others = batches // 2
    size = part.shape[1] // 2
    half = rows // 2
    vmem = pl.BlockSpec(memory_space=pltpu.VMEM)
    sems = pltpu.SemaphoreType.DMA((4 * others,))
    return pl.pallas_call(
        functools.partial(fold_kernel, batches),
        out_shape=jax.ShapeDtypeStruct((rows, size), BF),
        in_specs=[vmem],
        out_specs=vmem,
        scratch_shapes=[
            pltpu.VMEM((others, rows, 2 * size), BF),
            pltpu.VMEM((others - 1, half, 2 * size), BF),
            pltpu.VMEM((others - 1, half, size), BF),
            pltpu.VMEM((others, half, size), BF),
            pltpu.VMEM((half, size), BF),
            pltpu.VMEM((half, 2 * size), BF),
            sems,
            sems,
        ],
        compiler_params=pltpu.CompilerParams(
            collective_id=collective_id, has_side_effects=True, vmem_limit_bytes=VMEM_LIMIT
        ),
        name="fold",
    )(part)


def tail_kernel(
    count, batches, cat_ref, w_ref, x_ref, gain_ref, dh1_ref, wout_ref, second_ref,
    out_0, out_r1, out_l1, out_all, tok_all, gains_ref, wout_own,
    part_ref, tok_ref, got, wout_got, gain_own, gain_got, gain_mid, gain_heads,
    send_sem, recv_sem, local_sem,
):
    steps = count // 2
    rows, width = x_ref.shape
    depth = cat_ref.shape[1]
    tile = 256
    place, right, left = ring_setup(count)
    batch, head = lax.axis_index("batch"), lax.axis_index("head")
    others = [lax.rem(batch + hop, batches) for hop in range(1, batches)]
    members = [(batch, ring_head(lax.rem(place + hop, count), count)) for hop in range(1, count)]
    greet((*members, *[(other, head) for other in others]))
    sems = (send_sem, recv_sem)
    slot = 0
    copies = []

    def go(source, target, device):
        nonlocal slot
        copy = send(source, target, sems, slot, device)
        slot += 1
        copies.append(copy)
        return copy

    def span(owner, extent):
        return pl.ds(pl.multiple_of(lax.rem(owner + count, count) * extent, extent), extent)

    def compute(owner):
        here = span(owner, rows)
        values = cat_ref[here]

        @pl.loop(0, width // tile)
        def _(at):
            cols = pl.ds(pl.multiple_of(at * tile, tile), tile)
            part_ref[here, cols] = cols_inner(values, w_ref[cols, pl.ds(0, depth)]).astype(BF)

    def gather(own, whole, step, last):
        out = []
        for flow, chunk, device in ((0, place - step, right), (1, place + step, left)):
            if last:
                last[flow].wait_recv()
            target = whole.at[lax.rem(chunk + count, count)]
            source = target if step else own
            if step == steps - 1:
                cut = (slice(None), pl.ds(flow * (width // 2), width // 2))
                source, target = source.at[cut], target.at[cut]
            out.append(go(source, target, device))
        return out

    def reduce(parts, held, step, last):
        extent, side = held.shape[2], held.shape[3] // 2
        out = []
        for flow, owner, device in (
            (0, place + steps - step, right),
            (1, place - steps + step, left),
        ):
            have = pl.ds(flow * side, side)
            lack = pl.ds((1 - flow) * side, side)
            mine = parts.at[span(owner, extent)]
            if step == 0:
                out.append(go(mine.at[:, have], held.at[flow, 0, :, have], device))
                continue
            last[flow].wait_recv()
            if step == 1:
                held[flow, 0, :, have] = add_low(held[flow, 0, :, have], mine[:, have])
                held[flow, 0, :, lack] = mine[:, lack]
            else:
                held[flow, step - 1] = add_low(held[flow, step - 1], mine[...])
            out.append(go(held.at[flow, step - 1], held.at[flow, step], device))
        return out

    keep = []
    for index, (piece, shift) in enumerate(
        ((out_0, 0), (out_r1, -1), (out_l1, 1))
    ):
        target = out_all.at[lax.rem(place + shift + count, count)]
        keep.append(pltpu.make_async_copy(piece, target, local_sem.at[index]))
        keep[-1].start()
    compute(place + steps)
    sums = reduce(part_ref, got, 0, None)
    wsums = reduce(wout_ref, wout_got, 0, None)
    outs = []

    @pl.loop(1, count)
    def _(hop):
        compute(place + steps + hop)

    for step in range(1, steps):
        sums = reduce(part_ref, got, step, sums)
        wsums = reduce(wout_ref, wout_got, step, wsums)
        if step == 1:
            for copy in keep:
                copy.wait()
        outs = gather(None, out_all, step, outs)
    for copy in sums:
        copy.wait_recv()

    def tile_of(at):
        return pl.ds(pl.multiple_of(at * tile, tile), tile)

    def total(cols):
        return (
            part_ref[span(place, rows), cols].astype(F32)
            + got[0, steps - 1, :, cols].astype(F32)
            + got[1, steps - 1, :, cols].astype(F32)
        )

    def collect(at, state):
        squares, mean = state
        cols = tile_of(at)
        x = x_ref[:, cols].astype(F32)
        squares = squares + jnp.sum(x * x, axis=1, keepdims=True)
        return squares, mean + jnp.sum(gain_ref[:, cols] * total(cols) * x, axis=1, keepdims=True)

    zero = jnp.zeros((rows, 1), F32)
    squares, mean = lax.fori_loop(0, width // tile, collect, (zero, zero))
    scale = lax.rsqrt(squares / width + EPSILON)
    pull = scale * scale * scale * (mean / width)

    @pl.loop(0, width // tile)
    def _(at):
        cols = tile_of(at)
        x, dn1 = x_ref[:, cols].astype(F32), total(cols)
        gain_own[pl.ds(0, 1), cols] = jnp.sum(dn1 * x * scale, axis=0, keepdims=True)
        gain_own[pl.ds(1, 1), cols] = second_ref[:, cols]
        tok_ref[:, cols] = (dh1_ref[:, cols] + scale * (gain_ref[:, cols] * dn1) - x * pull).astype(BF)

    keep_tok = pltpu.make_async_copy(tok_ref, tok_all.at[place], local_sem.at[3])
    keep_tok.start()
    toks = gather(tok_ref, tok_all, 0, None)
    wide = width // batches

    def slice_of(at):
        return pl.ds(pl.multiple_of(at * wide, wide), wide)

    gains = [
        go(gain_own.at[:, slice_of(other)], gain_got.at[hop], (other, head))
        for hop, other in enumerate(others)
    ]
    toks = gather(tok_ref, tok_all, 1, toks)
    middle = gain_own[:, slice_of(batch)]
    for hop, copy in enumerate(gains):
        copy.wait_recv()
        middle = middle + gain_got[hop]
    gain_mid[...] = middle
    gain_heads[place] = middle
    gains = [go(gain_mid, gain_heads.at[place], member) for member in members]
    for step in range(2, steps):
        toks = gather(tok_ref, tok_all, step, toks)
    for copy in gains:
        copy.wait_recv()
    middle = gain_heads[0]
    for at in range(1, count):
        middle = middle + gain_heads[at]
    gains_ref[...] = middle
    for copy in (*wsums, *outs):
        copy.wait_recv()
    wout_own[...] = (
        wout_ref[span(place, wout_own.shape[0])].astype(F32)
        + wout_got[0, steps - 1].astype(F32)
        + wout_got[1, steps - 1].astype(F32)
    )
    for copy in toks:
        copy.wait_recv()
    for copy in copies:
        copy.wait_send()
    keep_tok.wait()


def tail(d_cat, w_in, x_own, gain, d_resid, wout_part, second, pieces, collective_id):
    count = lax.axis_size("head")
    batches = lax.axis_size("batch")
    steps = count // 2
    rows, width = x_own.shape
    size, wide = wout_part.shape[0] // count, wout_part.shape[1]
    vmem = pl.BlockSpec(memory_space=pltpu.VMEM)
    whole = jax.ShapeDtypeStruct((count, rows, width), BF)
    sems = pltpu.SemaphoreType.DMA((5 * count + batches,))
    gains = (2, width // batches)
    return pl.pallas_call(
        functools.partial(tail_kernel, count, batches),
        out_shape=[
            whole,
            whole,
            jax.ShapeDtypeStruct(gains, F32),
            jax.ShapeDtypeStruct((size, wide), F32),
        ],
        in_specs=[vmem] * 10,
        out_specs=[vmem] * 4,
        scratch_shapes=[
            pltpu.VMEM((count * rows, width), BF),
            pltpu.VMEM((rows, width), BF),
            pltpu.VMEM((2, steps, rows, width), BF),
            pltpu.VMEM((2, steps, size, wide), BF),
            pltpu.VMEM((2, width), F32),
            pltpu.VMEM((batches - 1, *gains), F32),
            pltpu.VMEM(gains, F32),
            pltpu.VMEM((count, *gains), F32),
            sems,
            sems,
            pltpu.SemaphoreType.DMA((4,)),
        ],
        compiler_params=pltpu.CompilerParams(
            collective_id=collective_id, has_side_effects=True, vmem_limit_bytes=VMEM_LIMIT
        ),
        cost_estimate=pl.CostEstimate(
            flops=2 * count * rows * width * d_cat.shape[1], bytes_accessed=400 << 20, transcendentals=0
        ),
        name="tail",
    )(d_cat, w_in, x_own, gain, d_resid, wout_part, second, *pieces)


def local_call(kernel, scalars, arrays, outs, scratch, flops, name):
    vmem = pl.BlockSpec(memory_space=pltpu.VMEM)
    smem = pl.BlockSpec(memory_space=pltpu.SMEM)
    return pl.pallas_call(
        kernel,
        out_shape=outs,
        in_specs=[smem] * len(scalars) + [vmem] * len(arrays),
        out_specs=[vmem] * len(outs),
        scratch_shapes=scratch,
        compiler_params=pltpu.CompilerParams(vmem_limit_bytes=VMEM_LIMIT),
        cost_estimate=pl.CostEstimate(flops=flops, bytes_accessed=8 << 20, transcendentals=0),
        name=name,
    )(*scalars, *arrays)


def ring_routes(count):
    spots = [ring_head(at, count) for at in range(count)]
    right = [(spots[at], spots[(at + 1) % count]) for at in range(count)]
    left = [(spots[at], spots[at - 1]) for at in range(count)]
    return right, left


def add_low(one, other):
    return (one.astype(F32) + other.astype(F32)).astype(BF)


def flow_steps(part, going, coming):
    count = lax.axis_size("head")
    place = ring_place(lax.axis_index("head"), count)
    right, left = ring_routes(count)
    rows = part.shape[0] // count
    steps = count // 2

    def mine(owner):
        return lax.dynamic_slice_in_dim(part, lax.rem(owner + count, count) * rows, rows, 0)

    for step in range(1, steps - 1):
        from_left = lax.ppermute(going, "head", right)
        from_right = lax.ppermute(coming, "head", left)
        going = add_low(from_left, mine(place + steps - 1 - step))
        coming = add_low(from_right, mine(place - steps + 1 + step))
        going, coming = yield going, coming
    from_left = lax.ppermute(going, "head", right)
    from_right = lax.ppermute(coming, "head", left)
    yield mine(place).astype(F32) + from_left.astype(F32) + from_right.astype(F32)


def matmul(left, right):
    return jnp.dot(left, right, preferred_element_type=F32)


def rows_inner(left, right):
    return lax.dot_general(left, right, (((0,), (0,)), ((), ())), preferred_element_type=F32)


def cols_inner(left, right):
    return lax.dot_general(left, right, (((1,), (1,)), ((), ())), preferred_element_type=F32)


def rms_scale(values):
    return lax.rsqrt(jnp.mean(values * values, axis=1, keepdims=True) + EPSILON)


def per_device(
    tokens,
    segment_ids,
    norm1_gain,
    w_query,
    w_key,
    w_value,
    w_gate,
    w_out,
    norm2_gain,
    w_mlp_gate,
    w_mlp_up,
    w_down,
    out_grad,
):
    heads = lax.axis_size("head")
    batches = lax.axis_size("batch")
    row_count, width = tokens.shape
    head_size = w_query.shape[1]
    half = w_key.shape[1]
    chunk = row_count // heads
    me = ring_place(lax.axis_index("head"), heads)
    scale_factor = 1.0 / math.sqrt(head_size)

    w_shard = jnp.concatenate([w_query, w_gate, w_key, w_value], axis=1)
    gains = jnp.concatenate([norm1_gain, norm2_gain]).reshape(-1, 128).astype(F32)
    normed_one, queries, gate_logit, kv_all, w_in, out_full, gains, seg_all = entry(
        tokens, w_shard, w_out, gains, segment_ids.reshape(-1, 128), 1
    )
    gains, w_mlp_gate, w_mlp_up = lax.optimization_barrier((gains, w_mlp_gate, w_mlp_up))
    seg_all = seg_all.reshape(-1)
    gains = gains.reshape(batches, 2, -1).transpose(1, 0, 2).reshape(2, width)
    gain_one, gain_two = gains[0], gains[1]
    mgate_full = lax.all_gather(w_mlp_gate, "batch", axis=0, tiled=True)
    mup_full = lax.all_gather(w_mlp_up, "batch", axis=0, tiled=True)

    base = lax.axis_index("batch") * row_count
    ids = jnp.arange(DOCUMENTS, dtype=jnp.int32)
    below = jnp.sum((seg_all[None, :] < ids[:, None]).astype(jnp.int32), axis=1)
    starts = jnp.sum(jnp.where(segment_ids[None, :] == ids[:, None], below[:, None], 0), axis=0)
    scalars = (starts, base.reshape(1))
    pair_flops = 4 * row_count * kv_all.shape[0] * head_size
    attended, mixed, lse = local_call(
        functools.partial(attend_kernel, scale_factor),
        scalars,
        (queries, kv_all, starts[None], gate_logit),
        [
            jax.ShapeDtypeStruct((row_count, head_size), F32),
            jax.ShapeDtypeStruct((row_count, head_size), BF),
            jax.ShapeDtypeStruct((1, row_count), F32),
        ],
        [],
        pair_flops,
        "attend",
    )
    mixed_all, down_full = spread([mixed, w_down], (("head", "cols"), ("batch", "cols")), 2)
    (
        normed_two, hidden, d_pre, mlp_part, resid_own, d_resid, d_resid_low, d_gain_two, d_mixed,
        going, coming,
    ) = mlp_back(
        tokens, mixed_all, out_grad, gain_two[None], out_full, mgate_full, mup_full, down_full, 3
    )
    hold = lax.optimization_barrier
    mixed_own = lax.dynamic_slice_in_dim(mixed_all, me * chunk, chunk, 0)
    flow = flow_steps(mlp_part, going, coming)
    state = next(flow)
    d_out_part = rows_inner(mixed_own, d_resid_low).astype(BF)
    hidden, d_out_part = hold((hidden, d_out_part))
    d_out_part = lax.psum_scatter(d_out_part, "batch", scatter_dimension=1, tiled=True)
    d_down = rows_inner(hidden, out_grad).astype(BF)
    normed_two, d_down, state = hold((normed_two, d_down, state))
    state = flow.send(state)
    d_mlp = rows_inner(normed_two, d_pre).astype(BF)
    d_mixed, d_mlp, state = hold((d_mixed, d_mlp, state))
    d_mlp = lax.psum_scatter(d_mlp, "batch", scatter_dimension=0, tiled=True).astype(F32)
    while isinstance(state, tuple):
        state = flow.send(state)

    d_queries, d_gate_logit, d_kv_all = local_call(
        functools.partial(attend_back_kernel, scale_factor),
        scalars,
        (queries, kv_all, starts[None], gate_logit, attended, d_mixed, lse),
        [
            jax.ShapeDtypeStruct((row_count, head_size), BF),
            jax.ShapeDtypeStruct((row_count, head_size), BF),
            jax.ShapeDtypeStruct(kv_all.shape, BF),
        ],
        [pltpu.VMEM((kv_all.shape[0], head_size), F32)] * 2,
        5 * pair_flops // 2,
        "attend_back",
    )
    d_kv_all, state, d_down, d_out_part = hold((d_kv_all, state, d_down, d_out_part))
    d_down = lax.psum_scatter(d_down, "batch", scatter_dimension=1, tiled=True).astype(F32)
    right, left = ring_routes(heads)
    pieces = [(resid_own + state).astype(BF)]
    pieces += [lax.ppermute(pieces[0], "head", right), lax.ppermute(pieces[0], "head", left)]
    d_kv = fold(d_kv_all, row_count, 4)
    d_kv, *pieces = hold((d_kv, *pieces))
    d_cat = jnp.concatenate([d_queries, d_gate_logit, d_kv], axis=1)
    d_in = rows_inner(normed_one, d_cat).astype(BF)
    d_cat, d_in, d_down = hold((d_cat, d_in, d_down))
    d_in = lax.psum_scatter(d_in, "batch", scatter_dimension=0, tiled=True).astype(F32)
    inputs_own = lax.dynamic_slice_in_dim(tokens, me * chunk, chunk, 0)
    output, d_tokens, d_gains, d_out = tail(
        d_cat, w_in, inputs_own, gain_one[None], d_resid, d_out_part, d_gain_two, pieces, 5
    )
    output = output.reshape(row_count, width)
    d_tokens = d_tokens.reshape(row_count, width)
    hidden_own = w_mlp_gate.shape[1]
    return (
        output,
        d_tokens,
        d_gains[0],
        d_in[:, :head_size],
        d_in[:, 2 * head_size : 2 * head_size + half],
        d_in[:, 2 * head_size + half :],
        d_in[:, head_size : 2 * head_size],
        d_out,
        d_gains[1],
        d_mlp[:, :hidden_own],
        d_mlp[:, hidden_own:],
        d_down,
    )


def solution(mesh):
    return jax.shard_map(
        per_device,
        mesh=mesh,
        in_specs=(
            P("batch", None),
            P("batch"),
            P("batch"),
            P("batch", "head"),
            P("batch", "head"),
            P("batch", "head"),
            P("batch", "head"),
            P("head", "batch"),
            P("batch"),
            P("batch", "head"),
            P("batch", "head"),
            P("head", "batch"),
            P("batch", None),
        ),
        out_specs=(
            P("batch", None),
            P("batch", None),
            P("batch"),
            P("batch", "head"),
            P("batch", "head"),
            P("batch", "head"),
            P("batch", "head"),
            P("head", "batch"),
            P("batch"),
            P("batch", "head"),
            P("batch", "head"),
            P("head", "batch"),
        ),
        check_vma=False,
    )
```

```python
import functools
import math

import jax
import jax.numpy as jnp
from jax import lax
from jax.experimental import pallas as pl
from jax.experimental.pallas import tpu as pltpu
from jax.sharding import PartitionSpec as P

EPSILON = 1e-06
MASKED = -1e30
DOCUMENTS = 7
BF = jnp.bfloat16
F32 = jnp.float32


MESH = pl.DeviceIdType.MESH
VMEM_LIMIT = 60 << 20


def ring_place(head, count):
    high, low = head // 2, head % 2
    return (1 - low) * high + low * (count - 1 - high)


def ring_head(place, count):
    low = place // (count // 2)
    high = (1 - low) * place + low * (count - 1 - place)
    return 2 * high + low


def ring_setup(count):
    batch = lax.axis_index("batch")
    place = ring_place(lax.axis_index("head"), count)
    right = (batch, ring_head(lax.rem(place + 1, count), count))
    left = (batch, ring_head(lax.rem(place + count - 1, count), count))
    return place, right, left


def greet(devices):
    barrier = pltpu.get_barrier_semaphore()
    for device in devices:
        pl.semaphore_signal(barrier, inc=1, device_id=device, device_id_type=MESH)
    pl.semaphore_wait(barrier, len(devices))


def send(source, target, sems, slot, device):
    copy = pltpu.make_async_remote_copy(
        src_ref=source,
        dst_ref=target,
        send_sem=sems[0].at[slot],
        recv_sem=sems[1].at[slot],
        device_id=device,
        device_id_type=MESH,
    )
    copy.start()
    return copy


def half_of(extent, flow):
    if extent[1] % 256:
        return (pl.ds(flow * (extent[0] // 2), extent[0] // 2), slice(None))
    return (slice(None), pl.ds(flow * (extent[1] // 2), extent[1] // 2))


def place_of(whole, own, chunk, form):
    rows, wide = own.shape[-2:]
    if form == "lead":
        return whole.at[chunk]
    if form == "rows":
        return whole.at[pl.ds(pl.multiple_of(chunk * rows, rows), rows)]
    return whole.at[:, pl.ds(pl.multiple_of(chunk * wide, wide), wide)]


def spread_kernel(count, batches, plans, *refs):
    steps = count // 2
    arrays = len(plans)
    own_refs, all_refs = refs[:arrays], refs[arrays : 2 * arrays]
    send_sem, recv_sem, local_sem = refs[2 * arrays :]
    place, right, left = ring_setup(count)
    head = lax.axis_index("head")
    batch = lax.axis_index("batch")
    across, core = batch // 2, lax.rem(batch, 2)
    others = batches // 2
    twin = (across * 2 + 1 - core, head)
    peers = [(lax.rem(across + hop, others) * 2 + core, head) for hop in range(1, others)]
    ring = any(axis == "head" for axis, _ in plans)
    grid = any(axis == "batch" for axis, _ in plans)
    greet((right, left) * ring + (twin, *peers) * grid)
    sems = (send_sem, recv_sem)
    slot = 0
    waiting, arriving, local = [], [], []

    def go(source, target, device):
        nonlocal slot
        copy = send(source, target, sems, slot, device)
        slot += 1
        waiting.append(copy)
        return copy

    onward = []
    for index, (axis, form) in enumerate(plans):
        own, whole = own_refs[index], all_refs[index]
        spot = place if axis == "head" else batch
        mine = place_of(whole, own, spot, form)
        copy = pltpu.make_async_copy(own, mine, local_sem.at[index])
        copy.start()
        local.append(copy)
        if axis == "batch":
            for hop, peer in enumerate(peers, 1):
                source = lax.rem(across + others - hop, others) * 2 + core
                onward.append((go(own, mine, peer), place_of(whole, own, source, form)))
            arriving.append(go(own, mine, twin))
    copies = [None] * (2 * arrays)
    for step in range(steps):
        for index, (axis, form) in enumerate(plans):
            if axis != "head":
                continue
            own = own_refs[index]
            for flow, chunk, device in ((0, place - step, right), (1, place + step, left)):
                at = 2 * index + flow
                if step:
                    copies[at].wait_recv()
                chunk = lax.rem(chunk + count, count)
                target = place_of(all_refs[index], own, chunk, form)
                source = target if step else own
                if step == steps - 1:
                    part = half_of(own.shape, flow)
                    source = source.at[part]
                    target = target.at[part]
                copies[at] = go(source, target, device)
        if step == 0 or not ring:
            for copy, block in onward:
                copy.wait_recv()
                arriving.append(go(block, block, twin))
            onward = []
    for copy in copies:
        if copy is not None:
            arriving.append(copy)
    for copy in arriving:
        copy.wait_recv()
    for copy in waiting:
        copy.wait_send()
    for copy in local:
        copy.wait()


def spread(arrays, plans, collective_id):
    count = lax.axis_size("head")
    batches = lax.axis_size("batch")
    shapes = []
    slots = 0
    for array, (axis, form) in zip(arrays, plans):
        many = count if axis == "head" else batches
        slots += count if axis == "head" else batches - 1
        if form == "lead":
            shapes.append((many, *array.shape))
        elif form == "rows":
            shapes.append((many * array.shape[0], array.shape[1]))
        else:
            shapes.append((array.shape[0], many * array.shape[1]))
    hbm = pl.BlockSpec(memory_space=pl.ANY)
    return pl.pallas_call(
        functools.partial(spread_kernel, count, batches, plans),
        out_shape=[jax.ShapeDtypeStruct(shape, a.dtype) for shape, a in zip(shapes, arrays)],
        in_specs=[pl.BlockSpec(memory_space=pltpu.VMEM)] * len(arrays),
        out_specs=[hbm] * len(arrays),
        scratch_shapes=[
            pltpu.SemaphoreType.DMA((slots,)),
            pltpu.SemaphoreType.DMA((slots,)),
            pltpu.SemaphoreType.DMA((len(arrays),)),
        ],
        compiler_params=pltpu.CompilerParams(
            collective_id=collective_id, has_side_effects=True, vmem_limit_bytes=VMEM_LIMIT
        ),
        name=f"spread_{collective_id}",
    )(*arrays)


def mlp_kernel(
    count, x_hbm, a_hbm, dy_hbm, gain_ref, out_w, gate_w, up_w, down_w,
    mlp_hbm, dmlp_hbm, ddown_hbm, h1_ref, dh1_ref, low_ref, dgain_ref, da_ref, ahead_ref, behind_ref,
    x_s, a_s, mlp_s, h1_s, dy_all, n2_all, hid_all, grad_all, dmlp_s, ddown_s, da_part,
    mlp_far, mlp_next, mlp_got, right_part, left_part, right_got, left_got,
    in_sem, out_sem, grad_sem, send_sem, recv_sem, da_send, da_recv, far_send, far_recv,
):
    steps = count // 2
    rows = x_hbm.shape[0] // count
    width = x_hbm.shape[1]
    hidden = gate_w.shape[1]
    side = width // 2
    tile = 256
    inner = 256 if hidden % 256 == 0 else 128
    size = da_ref.shape[1]
    place, right, left = ring_setup(count)

    def member(hop):
        spot = lax.rem(place + hop, count)
        return spot, (lax.axis_index("batch"), ring_head(spot, count))

    greet([member(hop)[1] for hop in range(1, count)])

    def owners(group):
        first = jnp.where(group == 0, 1, 0)
        one = lax.rem(place + steps - group, count)
        two = lax.rem(place - steps + group + first * steps + count, count)
        return one, two

    def span(owner):
        return pl.ds(pl.multiple_of(owner * rows, rows), rows)

    def tile_of(at, extent=tile):
        return pl.ds(pl.multiple_of(at * extent, extent), extent)

    def loads(group, slot):
        return [
            pltpu.make_async_copy(
                source.at[span(owner)],
                target.at[pl.ds(at * rows, rows)],
                in_sem.at[slot, 2 * index + at],
            )
            for index, (source, target) in enumerate(
                ((x_hbm, x_s.at[slot]), (a_hbm, a_s.at[slot]), (dy_hbm, dy_all.at[group]))
            )
            for at, owner in enumerate(owners(group))
        ]

    def stores(group, slot):
        return [
            pltpu.make_async_copy(
                mlp_s.at[slot, pl.ds(at * rows, rows)], mlp_hbm.at[span(owner)], out_sem.at[slot, at]
            )
            for at, owner in enumerate(owners(group))
        ]

    def passing(source, target, sems, slot, device):
        return pltpu.make_async_remote_copy(
            src_ref=source,
            dst_ref=target,
            send_sem=sems[0].at[slot],
            recv_sem=sems[1].at[slot],
            device_id=device,
            device_id_type=MESH,
        )

    ring_sems, far_sems = (send_sem, recv_sem), (far_send, far_recv)
    ahead, behind = pl.ds(0, side), pl.ds(side, side)

    def first_copies():
        return (
            passing(right_part.at[0, :, ahead], right_got.at[0, :, ahead], ring_sems, 0, right),
            passing(right_part.at[0, :, behind], left_got.at[0, :, behind], ring_sems, steps, left),
        )

    def later_copies(step):
        return (
            passing(right_got.at[step - 1], right_got.at[step], ring_sems, step, right),
            passing(left_got.at[step - 1], left_got.at[step], ring_sems, steps + step, left),
        )

    for copy in loads(0, 0):
        copy.start()

    @pl.loop(0, steps)
    def _(group):
        slot = lax.rem(group, 2)
        for copy in loads(group, slot):
            copy.wait()

        @pl.when(group + 1 < steps)
        def _():
            for copy in loads(group + 1, 1 - slot):
                copy.start()

        @pl.when(group >= 2)
        def _():
            for copy in stores(group - 2, slot):
                copy.wait()

        mixed = a_s[slot]

        def residual(at, total):
            cols = tile_of(at)
            values = x_s[slot, :, cols].astype(F32) + matmul(mixed, out_w[:, cols])
            h1_s[:, cols] = values
            return total + jnp.sum(values * values, axis=1, keepdims=True)

        total = lax.fori_loop(0, width // tile, residual, jnp.zeros((2 * rows, 1), F32))
        scale = lax.rsqrt(total / width + EPSILON)

        @pl.when(group == 0)
        def _():
            h1_ref[...] = h1_s[pl.ds(rows, rows)]

        @pl.loop(0, width // tile)
        def _(at):
            cols = tile_of(at)
            n2_all[group, :, cols] = (h1_s[:, cols] * scale * gain_ref[:, cols]).astype(BF)

        normed = n2_all[group]
        dy = dy_all[group]

        @pl.loop(0, hidden // inner)
        def _(at):
            cols = tile_of(at, inner)
            cols_up = pl.ds(pl.multiple_of(hidden + at * inner, inner), inner)
            gate = matmul(normed, gate_w[:, cols])
            up = matmul(normed, up_w[:, cols])
            d_hidden = cols_inner(dy, down_w[cols])
            sig = jax.nn.sigmoid(gate)
            silu = gate * sig
            hid_all[group, :, cols] = (silu * up).astype(BF)
            grad_all[group, :, cols] = (d_hidden * up * sig * (1.0 + gate * (1.0 - sig))).astype(BF)
            grad_all[group, :, cols_up] = (d_hidden * silu).astype(BF)

        hid = hid_all[group]
        d_gate = grad_all[group, :, :hidden]
        d_up = grad_all[group, :, hidden:]
        half = jnp.minimum(group, 1)

        @pl.loop(0, width // tile)
        def _(at):
            cols = tile_of(at)
            part = (cols_inner(d_gate, gate_w[cols]) + cols_inner(d_up, up_w[cols])).astype(BF)
            right_part[half, :, cols] = part[:rows]
            left_part[half, :, cols] = part[rows:]
            mlp_s[slot, :, cols] = matmul(hid, down_w[:, cols]).astype(BF)

        for copy in stores(group, slot):
            copy.start()

        @pl.when(group == 0)
        def _():
            mlp_far[...] = mlp_s[slot, pl.ds(0, rows)]
            for copy in first_copies():
                copy.start()

        @pl.when(group == 1)
        def _():
            mlp_next[0] = mlp_s[slot, pl.ds(0, rows)]
            mlp_next[1] = mlp_s[slot, pl.ds(rows, rows)]
            one, two = first_copies()
            one.wait_recv()
            right_got[0, :, ahead] = add_low(right_part[1, :, ahead], right_got[0, :, ahead])
            right_got[0, :, behind] = right_part[1, :, behind]
            two.wait_recv()
            left_got[0, :, behind] = add_low(left_part[1, :, behind], left_got[0, :, behind])
            left_got[0, :, ahead] = left_part[1, :, ahead]

        @pl.when(group == 2)
        def _():
            ahead_ref[...] = mlp_s[slot, pl.ds(0, rows)]
            behind_ref[...] = mlp_s[slot, pl.ds(rows, rows)]

        @pl.when(group >= 2)
        def _():
            one, two = later_copies(group - 1)
            one.wait_recv()
            right_got[group - 1] = add_low(right_part[1], right_got[group - 1])
            two.wait_recv()
            left_got[group - 1] = add_low(left_part[1], left_got[group - 1])

        @pl.when(group >= 1)
        def _():
            for copy in later_copies(group):
                copy.start()

    far_copies = [
        passing(mlp_far.at[:, ahead], mlp_got.at[0, :, ahead], far_sems, 0, right),
        passing(mlp_far.at[:, behind], mlp_got.at[1, :, behind], far_sems, 1, left),
    ]
    for copy in far_copies:
        copy.start()

    every = steps * 2 * rows

    def dmlp_copy(at, slot):
        return pltpu.make_async_copy(
            dmlp_s.at[slot], dmlp_hbm.at[tile_of(at // 2), tile_of(lax.rem(at, 2), hidden)], grad_sem.at[slot]
        )

    mlp_tiles = 2 * (width // tile)

    @pl.loop(0, mlp_tiles)
    def _(at):
        slot = lax.rem(at, 2)

        @pl.when(at >= 2)
        def _():
            dmlp_copy(at - 2, slot).wait()

        normed = n2_all[:, :, tile_of(at // 2)].reshape(every, tile)
        grads = grad_all[:, :, tile_of(lax.rem(at, 2), hidden)].reshape(every, hidden)
        dmlp_s[slot] = rows_inner(normed, grads).astype(BF)
        dmlp_copy(at, slot).start()

    wide = 512
    across = width // wide

    def ddown_copy(at, slot):
        return pltpu.make_async_copy(
            ddown_s.at[slot],
            ddown_hbm.at[tile_of(at // across, inner), tile_of(lax.rem(at, across), wide)],
            grad_sem.at[2 + slot],
        )

    down_tiles = across * (hidden // inner)

    @pl.loop(0, down_tiles)
    def _(at):
        slot = lax.rem(at, 2)

        @pl.when(at >= 2)
        def _():
            ddown_copy(at - 2, slot).wait()

        hid = hid_all[:, :, tile_of(at // across, inner)].reshape(every, inner)
        dy = dy_all[:, :, tile_of(lax.rem(at, across), wide)].reshape(every, wide)
        ddown_s[slot] = rows_inner(hid, dy).astype(BF)
        ddown_copy(at, slot).start()

    for copy in later_copies(steps - 1):
        copy.wait_recv()
    for flow, have, lack in ((0, ahead, behind), (1, behind, ahead)):
        far_copies[flow].wait_recv()
        mlp_got[flow, :, have] = add_low(mlp_got[flow, :, have], mlp_next[flow, :, have])
        mlp_got[flow, :, lack] = mlp_next[flow, :, lack]
    next_copies = [
        passing(mlp_got.at[0], mlp_got.at[2], far_sems, 2, right),
        passing(mlp_got.at[1], mlp_got.at[3], far_sems, 3, left),
    ]
    for copy in next_copies:
        copy.start()

    def collect(at, state):
        squares, mean = state
        cols = tile_of(at)
        dn2 = (
            left_part[0, :, cols].astype(F32)
            + right_got[steps - 1, :, cols].astype(F32)
            + left_got[steps - 1, :, cols].astype(F32)
        )
        dh1_ref[:, cols] = dn2
        h1 = h1_ref[:, cols]
        squares = squares + jnp.sum(h1 * h1, axis=1, keepdims=True)
        return squares, mean + jnp.sum(gain_ref[:, cols] * dn2 * h1, axis=1, keepdims=True)

    zero = jnp.zeros((rows, 1), F32)
    squares, mean = lax.fori_loop(0, width // tile, collect, (zero, zero))
    scale_own = lax.rsqrt(squares / width + EPSILON)
    pull = scale_own * scale_own * scale_own * (mean / width)

    @pl.loop(0, width // tile)
    def _(at):
        cols = tile_of(at)
        dn2, h1 = dh1_ref[:, cols], h1_ref[:, cols]
        dgain_ref[:, cols] = jnp.sum(dn2 * h1 * scale_own, axis=0, keepdims=True)
        dy = dy_all[0, pl.ds(rows, rows), cols].astype(F32)
        d_resid = dy + scale_own * (gain_ref[:, cols] * dn2) - h1 * pull
        dh1_ref[:, cols] = d_resid
        low_ref[:, cols] = d_resid.astype(BF)

    def da_copy(hop):
        return passing(
            da_part.at[hop], da_ref.at[span(place)], (da_send, da_recv), hop, member(hop)[1]
        )

    low = low_ref[...]

    @pl.loop(1, count)
    def _(hop):
        spot = member(hop)[0]
        da_part[hop] = cols_inner(low, out_w[tile_of(spot, size)]).astype(BF)
        da_copy(hop).start()

    da_ref[span(place)] = cols_inner(low, out_w[tile_of(place, size)]).astype(BF)

    @pl.loop(1, count)
    def _(hop):
        da_copy(hop).wait_recv()
        da_copy(hop).wait_send()

    for flow, held in ((0, ahead_ref), (1, behind_ref)):
        next_copies[flow].wait_recv()
        held[...] = add_low(held[...], mlp_got[2 + flow])
    for copy in (*far_copies, *next_copies, *first_copies()):
        copy.wait_send()
    for step in range(1, steps):
        for copy in later_copies(step):
            copy.wait_send()
    for group in range(steps - 2, steps):
        for copy in stores(group, group % 2):
            copy.wait()
    for at in range(2):
        dmlp_copy(mlp_tiles - 2 + at, (mlp_tiles + at) % 2).wait()
        ddown_copy(down_tiles - 2 + at, (down_tiles + at) % 2).wait()


def mlp_back(tokens, mixed, dy, gain, out_w, gate_w, up_w, down_w, collective_id):
    count = lax.axis_size("head")
    total, width = tokens.shape
    hidden = gate_w.shape[1]
    rows, steps = total // count, count // 2
    size = mixed.shape[1] // count
    inner = 256 if hidden % 256 == 0 else 128
    vmem = pl.BlockSpec(memory_space=pltpu.VMEM)
    hbm = pl.BlockSpec(memory_space=pl.ANY)

    def slots(many, tall, wide, dtype=BF):
        return pltpu.VMEM((many, tall, wide), dtype)

    def shape(*extent, dtype=BF):
        return jax.ShapeDtypeStruct(extent, dtype)

    dma = pltpu.SemaphoreType.DMA
    flops = 2 * total * width * (mixed.shape[1] + 9 * hidden)
    return pl.pallas_call(
        functools.partial(mlp_kernel, count),
        out_shape=[
            shape(total, width), shape(width, 2 * hidden), shape(hidden, width),
            shape(rows, width, dtype=F32), shape(rows, width, dtype=F32), shape(rows, width),
            shape(1, width, dtype=F32), shape(total, size), shape(rows, width), shape(rows, width),
        ],
        in_specs=[hbm] * 3 + [vmem] * 5,
        out_specs=[hbm] * 3 + [vmem] * 7,
        scratch_shapes=[
            slots(2, 2 * rows, width), slots(2, 2 * rows, mixed.shape[1]), slots(2, 2 * rows, width),
            pltpu.VMEM((2 * rows, width), F32),
            slots(steps, 2 * rows, width), slots(steps, 2 * rows, width),
            slots(steps, 2 * rows, hidden), slots(steps, 2 * rows, 2 * hidden),
            slots(2, 256, hidden), slots(2, inner, 512), slots(count, rows, size),
            pltpu.VMEM((rows, width), BF), slots(2, rows, width), slots(4, rows, width),
            slots(2, rows, width), slots(2, rows, width),
            slots(steps, rows, width), slots(steps, rows, width),
            dma((2, 6)), dma((2, 2)), dma((4,)), dma((count,)), dma((count,)),
            dma((count,)), dma((count,)), dma((4,)), dma((4,)),
        ],
        compiler_params=pltpu.CompilerParams(
            collective_id=collective_id, has_side_effects=True, vmem_limit_bytes=VMEM_LIMIT
        ),
        cost_estimate=pl.CostEstimate(flops=flops, bytes_accessed=40 << 20, transcendentals=0),
        name="mlp_back",
    )(tokens, mixed, dy, gain, out_w, gate_w, up_w, down_w)


def entry_kernel(
    count, batches, x_ref, w_ref, out_ref, gain_ref, seg_ref, down_ref,
    n1_ref, q_ref, logit_ref, kv_ref, w_all, out_all, gain_all, seg_all, down_all,
    send_sem, recv_sem, local_sem,
):
    steps = count // 2
    others = batches // 2
    rows, width = x_ref.shape
    depth = w_ref.shape[0]
    size, wide = out_ref.shape
    block = 256
    place, right, left = ring_setup(count)
    head = lax.axis_index("head")
    batch = lax.axis_index("batch")
    across, core, low = batch // 2, lax.rem(batch, 2), lax.rem(head, 2)
    twin = (across * 2 + 1 - core, head)
    mate = (batch, head + 1 - 2 * low)
    spots = [lax.rem(across + hop, others) for hop in range(others)]
    backs = [lax.rem(across + others - hop, others) for hop in range(others)]
    peers = [(spot * 2 + core, head) for spot in spots]
    far_peers = [(spot * 2 + 1 - core, head) for spot in spots]
    greet((twin, mate, right, left, *peers[1:], *far_peers[1:]))
    sems = (send_sem, recv_sem)
    slot = 0
    copies = []

    def go(source, target, device):
        nonlocal slot
        copy = send(source, target, sems, slot, device)
        slot += 1
        copies.append(copy)
        return copy

    def part(at, extent):
        return pl.ds(pl.multiple_of(at * extent, extent), extent)

    def both(view, own):
        out = [go(own, view(batch), peers[hop]) for hop in range(1, others)]
        return out, [go(own, view(batch), twin)]

    def pass_on(view, arrived):
        out = []
        for hop in range(1, others):
            arrived[hop - 1].wait_recv()
            there = view(backs[hop] * 2 + core)
            out.append(go(there, there, twin))
        return out

    local = []

    def stay(source, target):
        copy = pltpu.make_async_copy(source, target, local_sem.at[len(local)])
        copy.start()
        local.append(copy)

    def main_view(at):
        return w_all.at[part(at, depth), pl.ds(0, 3 * size)]

    def mate_view(at):
        return w_all.at[part(at, depth), pl.ds(3 * size, size)]

    def out_view(chunk, at):
        return out_all.at[part(chunk, size), part(at, wide)]

    small = []
    for own, whole in ((gain_ref, gain_all), (seg_ref, seg_all)):
        for device in (twin, *peers[1:], *far_peers[1:]):
            small.append(go(own, whole.at[batch], device))
        stay(own, whole.at[batch])
    from_mate = go(w_ref.at[:, pl.ds(2 * size, size)], mate_view(batch), mate)
    main_out, main_twin = both(main_view, w_ref)
    stay(w_ref, main_view(batch))
    out_peers = [go(out_ref, out_view(place, batch), peers[hop]) for hop in range(1, others)]
    stay(out_ref, out_view(place, batch))
    flows = [[None, None] for _ in range(others)]

    def ring(step):
        for hop in range(others):
            lane = spots[0] if hop == 0 else backs[hop]
            at = lane * 2 + core
            if step == 0 and hop:
                out_peers[hop - 1].wait_recv()
            for flow, chunk, device in ((0, place - step, right), (1, place + step, left)):
                if step:
                    flows[hop][flow].wait_recv()
                target = out_view(lax.rem(chunk + count, count), at)
                source = out_ref if step == 0 and hop == 0 else target
                if step == steps - 1:
                    cut = (pl.ds(flow * (size // 2), size // 2), slice(None))
                    source, target = source.at[cut], target.at[cut]
                flows[hop][flow] = go(source, target, device)

    for copy in small:
        copy.wait_recv()
    for copy in local[:2]:
        copy.wait()

    def normalize(at):
        here = part(at, block)

        def squares(tile, total):
            values = x_ref[here, part(tile, 256)].astype(F32)
            return total + jnp.sum(values * values, axis=1, keepdims=True)

        total = lax.fori_loop(0, width // 256, squares, jnp.zeros((block, 1), F32))
        scale = lax.rsqrt(total / width + EPSILON)

        @pl.loop(0, batches)
        def _(owner):
            for tile in range(depth // 128):
                cols = pl.ds(pl.multiple_of(owner * depth + tile * 128, 128), 128)
                values = x_ref[here, cols].astype(F32) * scale
                n1_ref[here, cols] = (values * gain_all[owner, pl.ds(tile, 1)]).astype(BF)

    blocks = rows // block
    middle = blocks // 2

    @pl.loop(0, middle)
    def _(at):
        normalize(at)

    from_mate.wait_recv()
    mate_out, mate_twin = both(mate_view, mate_view(batch))
    ring(0)

    def down_view(at):
        return down_all.at[:, part(at, down_ref.shape[1])]

    down_out, down_twin = both(down_view, down_ref)
    stay(down_ref, down_view(batch))

    @pl.loop(middle, blocks)
    def _(at):
        normalize(at)

    main_passed = pass_on(main_view, main_out)
    mate_passed = pass_on(mate_view, mate_out)
    for copy in (*main_twin, *mate_twin, *main_passed, *mate_passed):
        copy.wait_recv()
    for copy in local[2:]:
        copy.wait()

    def kv_view(at):
        return kv_ref.at[part(at, rows)]

    @pl.loop(0, blocks)
    def _(at):
        here = part(at, block)
        values = matmul(n1_ref[here], w_all[:, pl.ds(2 * size, 2 * size)])
        one, two = values[:, :size], values[:, size:]
        first = jnp.where(low == 0, one, two).astype(BF)
        second = jnp.where(low == 0, two, one).astype(BF)
        half = size // 2
        there = pl.ds(pl.multiple_of(batch * rows + at * block, block), block)
        kv_ref[there, pl.ds(0, size)] = jnp.concatenate([first[:, :half], second[:, :half]], 1)
        kv_ref[there, pl.ds(size, size)] = jnp.concatenate([first[:, half:], second[:, half:]], 1)

    kv_out, kv_twin = both(kv_view, kv_view(batch))
    ring(1)

    @pl.loop(0, blocks)
    def _(at):
        here = part(at, block)
        values = matmul(n1_ref[here], w_all[:, pl.ds(0, 2 * size)])
        q_ref[here] = values[:, :size].astype(BF)
        logit_ref[here] = values[:, size:]

    for step in range(2, steps):
        ring(step)
    down_passed = pass_on(down_view, down_out)
    kv_passed = pass_on(kv_view, kv_out)
    for pair in flows:
        for copy in pair:
            copy.wait_recv()
    swaps = []
    for hop in range(others):
        there = out_all.at[:, part(spots[hop] * 2 + core, wide)]
        swaps.append(go(there, there, twin))
    for copy in (*kv_twin, *kv_passed, *swaps, *down_twin, *down_passed):
        copy.wait_recv()
    for copy in copies:
        copy.wait_send()


def entry(tokens, w_shard, w_out, gains, segments, w_down, collective_id):
    count = lax.axis_size("head")
    batches = lax.axis_size("batch")
    others = batches // 2
    rows, width = tokens.shape
    size, wide = w_out.shape
    vmem = pl.BlockSpec(memory_space=pltpu.VMEM)
    slots = 6 * batches + others * (count + 3)
    sems = pltpu.SemaphoreType.DMA((slots,))
    return pl.pallas_call(
        functools.partial(entry_kernel, count, batches),
        out_shape=[
            jax.ShapeDtypeStruct((rows, width), BF),
            jax.ShapeDtypeStruct((rows, size), BF),
            jax.ShapeDtypeStruct((rows, size), F32),
            jax.ShapeDtypeStruct((batches * rows, 2 * size), BF),
            jax.ShapeDtypeStruct((width, 4 * size), BF),
            jax.ShapeDtypeStruct((count * size, batches * wide), BF),
            jax.ShapeDtypeStruct((batches, *gains.shape), F32),
            jax.ShapeDtypeStruct((batches, *segments.shape), jnp.int32),
            jax.ShapeDtypeStruct((w_down.shape[0], batches * w_down.shape[1]), BF),
        ],
        in_specs=[vmem] * 6,
        out_specs=[vmem] * 9,
        scratch_shapes=[sems, sems, pltpu.SemaphoreType.DMA((5,))],
        compiler_params=pltpu.CompilerParams(
            collective_id=collective_id, has_side_effects=True, vmem_limit_bytes=VMEM_LIMIT
        ),
        name="entry",
    )(tokens, w_shard, w_out, gains, segments, w_down)


KEY_BLOCK = 512
QUERY_BLOCK = 256


def key_range(start_ref, base, query_block):
    first = query_block * QUERY_BLOCK
    lowest = start_ref[first]
    highest = start_ref[first + QUERY_BLOCK - 1]
    begin = lowest // KEY_BLOCK
    end = (base + first + QUERY_BLOCK - 1) // KEY_BLOCK + 1
    full_begin = jnp.minimum((highest + KEY_BLOCK - 1) // KEY_BLOCK, end)
    full_end = jnp.maximum((base + first + 1) // KEY_BLOCK, full_begin)
    return begin, full_begin, full_end, end


def allowed_pairs(key_block, start_row, base_row):
    shape = (KEY_BLOCK, QUERY_BLOCK)
    key_pos = key_block * KEY_BLOCK + lax.broadcasted_iota(jnp.int32, shape, 0)
    query_pos = base_row + lax.broadcasted_iota(jnp.int32, shape, 1)
    return (key_pos >= start_row) & (key_pos <= query_pos)


def attend_kernel(
    scale, start_sm, base_sm, q_ref, kv_ref, start_ref, logit_ref, o_ref, a_ref, lse_ref
):
    base = base_sm[0]
    size = q_ref.shape[1]
    factor = scale * math.log2(math.e)

    @pl.loop(0, q_ref.shape[0] // QUERY_BLOCK)
    def _(block):
        rows = pl.ds(pl.multiple_of(block * QUERY_BLOCK, QUERY_BLOCK), QUERY_BLOCK)
        queries = q_ref[rows]
        start_row = start_ref[:, rows]
        begin, full_begin, full_end, end = key_range(start_sm, base, block)

        def step(masked, at, state):
            old_max, old_sum, total = state
            keys = pl.ds(pl.multiple_of(at * KEY_BLOCK, KEY_BLOCK), KEY_BLOCK)
            scores = cols_inner(kv_ref[keys, :size], queries)
            if masked:
                allowed = allowed_pairs(at, start_row, base + block * QUERY_BLOCK)
                scores = jnp.where(allowed, scores, MASKED)
            new_max = jnp.maximum(old_max, jnp.max(scores, axis=0, keepdims=True))
            keep = jnp.exp2((old_max - new_max) * factor)
            weights = jnp.exp2(scores * factor - new_max * factor)
            new_sum = old_sum * keep + jnp.sum(weights, axis=0, keepdims=True)
            total = total * keep + rows_inner(kv_ref[keys, size:], weights.astype(BF))
            return new_max, new_sum, total

        state = (
            jnp.full((1, QUERY_BLOCK), MASKED, F32),
            jnp.zeros((1, QUERY_BLOCK), F32),
            jnp.zeros((size, QUERY_BLOCK), F32),
        )
        state = lax.fori_loop(begin, full_begin, functools.partial(step, True), state)
        state = lax.fori_loop(full_begin, full_end, functools.partial(step, False), state)
        state = lax.fori_loop(full_end, end, functools.partial(step, True), state)
        run_max, run_sum, total = state
        lse_ref[:, rows] = run_max * factor + jnp.log2(run_sum)
        attended = (total / run_sum).T
        o_ref[rows] = attended
        a_ref[rows] = (attended * jax.nn.sigmoid(logit_ref[rows])).astype(BF)


def attend_back_kernel(
    scale, start_sm, base_sm, q_ref, kv_ref, start_ref, logit_ref, o_ref, da_ref, lse_ref,
    dq_ref, dg_ref, dkv_ref, dk_acc, dv_acc,
):
    base = base_sm[0]
    size = q_ref.shape[1]
    factor = scale * math.log2(math.e)
    dk_acc[...] = jnp.zeros_like(dk_acc)
    dv_acc[...] = jnp.zeros_like(dv_acc)

    @pl.loop(0, q_ref.shape[0] // QUERY_BLOCK)
    def _(block):
        rows = pl.ds(pl.multiple_of(block * QUERY_BLOCK, QUERY_BLOCK), QUERY_BLOCK)
        queries = q_ref[rows]
        start_row = start_ref[:, rows]
        lse = lse_ref[:, rows]
        gate = jax.nn.sigmoid(logit_ref[rows])
        attended = o_ref[rows]
        d_mixed = da_ref[rows].astype(F32)
        d_attended = (d_mixed * gate).astype(BF)
        dg_ref[rows] = (d_mixed * attended * gate * (1.0 - gate)).astype(BF)
        delta = jnp.sum((d_attended.astype(F32) * attended).T, axis=0, keepdims=True)
        begin, full_begin, full_end, end = key_range(start_sm, base, block)

        def step(masked, at, d_queries):
            keys = pl.ds(pl.multiple_of(at * KEY_BLOCK, KEY_BLOCK), KEY_BLOCK)
            key_block = kv_ref[keys, :size]
            probs = jnp.exp2(cols_inner(key_block, queries) * factor - lse)
            if masked:
                allowed = allowed_pairs(at, start_row, base + block * QUERY_BLOCK)
                probs = jnp.where(allowed, probs, 0.0)
            d_probs = cols_inner(kv_ref[keys, size:], d_attended)
            d_scores = (probs * (d_probs - delta) * scale).astype(BF)
            dv_acc[keys] += matmul(probs.astype(BF), d_attended)
            dk_acc[keys] += matmul(d_scores, queries)
            return d_queries + rows_inner(key_block, d_scores)

        d_queries = jnp.zeros((size, QUERY_BLOCK), F32)
        d_queries = lax.fori_loop(begin, full_begin, functools.partial(step, True), d_queries)
        d_queries = lax.fori_loop(full_begin, full_end, functools.partial(step, False), d_queries)
        d_queries = lax.fori_loop(full_end, end, functools.partial(step, True), d_queries)
        dq_ref[rows] = d_queries.T.astype(BF)

    @pl.loop(0, kv_ref.shape[0] // KEY_BLOCK)
    def _(at):
        keys = pl.ds(pl.multiple_of(at * KEY_BLOCK, KEY_BLOCK), KEY_BLOCK)
        dk, dv = dk_acc[keys].astype(BF), dv_acc[keys].astype(BF)
        half = size // 2
        dkv_ref[keys, :size] = jnp.concatenate([dk[:, :half], dv[:, :half]], axis=1)
        dkv_ref[keys, size:] = jnp.concatenate([dk[:, half:], dv[:, half:]], axis=1)


def fold_kernel(
    batches, part_ref, own_ref, core_got, x_first, x_second, y_first, y_second, held, send_sem, recv_sem
):
    rows, size = own_ref.shape
    half = rows // 2
    others = batches // 2
    head = lax.axis_index("head")
    batch = lax.axis_index("batch")
    across, core, low = batch // 2, lax.rem(batch, 2), lax.rem(head, 2)
    twin = (across * 2 + 1 - core, head)
    mate = (batch, head + 1 - 2 * low)
    spots = [lax.rem(across + hop, others) for hop in range(others)]
    peers = [(spot * 2 + core, head) for spot in spots]
    greet((twin, mate, *peers[1:]))
    sems = (send_sem, recv_sem)
    slot = 0
    copies = []
    mine = pl.ds(pl.multiple_of(low * size, size), size)
    given = pl.ds(pl.multiple_of((1 - low) * size, size), size)
    top, bottom = pl.ds(0, half), pl.ds(half, half)

    def block(at, side):
        return pl.ds(pl.multiple_of((2 * at + side) * rows, rows), rows)

    def go(source, target, device):
        nonlocal slot
        copy = send(source, target, sems, slot, device)
        slot += 1
        copies.append(copy)
        return copy

    order = list(range(1, others)) + [0]
    first = [go(part_ref.at[block(spots[hop], 1 - core)], core_got.at[spots[hop]], twin) for hop in order]
    tops, bottoms = [], []
    for copy, hop in zip(first, order):
        copy.wait_recv()
        spot = spots[hop]
        core_got[spot] = add_low(core_got[spot], part_ref[block(spot, core)])
        bottoms.append(go(core_got.at[spot, bottom, given], y_first.at[spot], mate))
        if hop:
            tops.append(go(core_got.at[spot, top], x_first.at[hop - 1], peers[hop]))
    total = core_got[across, top].astype(F32)
    for hop in range(1, others):
        tops[hop - 1].wait_recv()
        total = total + x_first[hop - 1].astype(F32)
    held[...] = total.astype(BF)
    last = go(held.at[:, given], y_second, mate)
    ends = []
    for copy, hop in zip(bottoms, order):
        copy.wait_recv()
        spot = spots[hop]
        y_first[spot] = add_low(y_first[spot], core_got[spot, bottom, mine])
        if hop:
            ends.append(go(y_first.at[spot], x_second.at[hop - 1], peers[hop]))
    last.wait_recv()
    own_ref[top] = add_low(held[:, mine], y_second[...])
    total = y_first[across].astype(F32)
    for hop in range(1, others):
        ends[hop - 1].wait_recv()
        total = total + x_second[hop - 1].astype(F32)
    own_ref[bottom] = total.astype(BF)
    for copy in copies:
        copy.wait_send()


def fold(part, rows, collective_id):
    batches = lax.axis_size("batch")
    others = batches // 2
    size = part.shape[1] // 2
    half = rows // 2
    vmem = pl.BlockSpec(memory_space=pltpu.VMEM)
    sems = pltpu.SemaphoreType.DMA((4 * others,))
    return pl.pallas_call(
        functools.partial(fold_kernel, batches),
        out_shape=jax.ShapeDtypeStruct((rows, size), BF),
        in_specs=[vmem],
        out_specs=vmem,
        scratch_shapes=[
            pltpu.VMEM((others, rows, 2 * size), BF),
            pltpu.VMEM((others - 1, half, 2 * size), BF),
            pltpu.VMEM((others - 1, half, size), BF),
            pltpu.VMEM((others, half, size), BF),
            pltpu.VMEM((half, size), BF),
            pltpu.VMEM((half, 2 * size), BF),
            sems,
            sems,
        ],
        compiler_params=pltpu.CompilerParams(
            collective_id=collective_id, has_side_effects=True, vmem_limit_bytes=VMEM_LIMIT
        ),
        name="fold",
    )(part)


def tail_kernel(
    count, batches, cat_ref, w_ref, x_ref, gain_ref, dh1_ref, wout_ref, second_ref,
    out_0, out_all, tok_all, gains_ref, wout_own,
    part_ref, tok_ref, got, wout_got, gain_own, gain_got, gain_mid, gain_heads,
    send_sem, recv_sem, local_sem,
):
    steps = count // 2
    rows, width = x_ref.shape
    depth = cat_ref.shape[1]
    tile = 256
    place, right, left = ring_setup(count)
    batch, head = lax.axis_index("batch"), lax.axis_index("head")
    others = [lax.rem(batch + hop, batches) for hop in range(1, batches)]
    members = [(batch, ring_head(lax.rem(place + hop, count), count)) for hop in range(1, count)]
    greet((*members, *[(other, head) for other in others]))
    sems = (send_sem, recv_sem)
    slot = 0
    copies = []

    def go(source, target, device):
        nonlocal slot
        copy = send(source, target, sems, slot, device)
        slot += 1
        copies.append(copy)
        return copy

    def span(owner, extent):
        return pl.ds(pl.multiple_of(lax.rem(owner + count, count) * extent, extent), extent)

    def compute(owner):
        here = span(owner, rows)
        values = cat_ref[here]

        @pl.loop(0, width // tile)
        def _(at):
            cols = pl.ds(pl.multiple_of(at * tile, tile), tile)
            part_ref[here, cols] = cols_inner(values, w_ref[cols, pl.ds(0, depth)]).astype(BF)

    def gather(own, whole, step, last):
        out = []
        for flow, chunk, device in ((0, place - step, right), (1, place + step, left)):
            if last:
                last[flow].wait_recv()
            target = whole.at[lax.rem(chunk + count, count)]
            source = target if step else own
            if step == steps - 1:
                cut = (slice(None), pl.ds(flow * (width // 2), width // 2))
                source, target = source.at[cut], target.at[cut]
            out.append(go(source, target, device))
        return out

    def reduce(parts, held, step, last):
        extent, side = held.shape[2], held.shape[3] // 2
        out = []
        for flow, owner, device in (
            (0, place + steps - step, right),
            (1, place - steps + step, left),
        ):
            have = pl.ds(flow * side, side)
            lack = pl.ds((1 - flow) * side, side)
            mine = parts.at[span(owner, extent)]
            if step == 0:
                out.append(go(mine.at[:, have], held.at[flow, 0, :, have], device))
                continue
            last[flow].wait_recv()
            if step == 1:
                held[flow, 0, :, have] = add_low(held[flow, 0, :, have], mine[:, have])
                held[flow, 0, :, lack] = mine[:, lack]
            else:
                held[flow, step - 1] = add_low(held[flow, step - 1], mine[...])
            out.append(go(held.at[flow, step - 1], held.at[flow, step], device))
        return out

    keep_out = pltpu.make_async_copy(out_0, out_all.at[place], local_sem.at[0])
    keep_out.start()
    compute(place + steps)
    sums = reduce(part_ref, got, 0, None)
    wsums = reduce(wout_ref, wout_got, 0, None)
    outs = gather(out_0, out_all, 0, None)

    @pl.loop(1, count)
    def _(hop):
        compute(place + steps + hop)

    for step in range(1, steps):
        sums = reduce(part_ref, got, step, sums)
        wsums = reduce(wout_ref, wout_got, step, wsums)
        outs = gather(out_0, out_all, step, outs)
    for copy in sums:
        copy.wait_recv()

    def tile_of(at):
        return pl.ds(pl.multiple_of(at * tile, tile), tile)

    def total(cols):
        return (
            part_ref[span(place, rows), cols].astype(F32)
            + got[0, steps - 1, :, cols].astype(F32)
            + got[1, steps - 1, :, cols].astype(F32)
        )

    def collect(at, state):
        squares, mean = state
        cols = tile_of(at)
        x = x_ref[:, cols].astype(F32)
        squares = squares + jnp.sum(x * x, axis=1, keepdims=True)
        return squares, mean + jnp.sum(gain_ref[:, cols] * total(cols) * x, axis=1, keepdims=True)

    zero = jnp.zeros((rows, 1), F32)
    squares, mean = lax.fori_loop(0, width // tile, collect, (zero, zero))
    scale = lax.rsqrt(squares / width + EPSILON)
    pull = scale * scale * scale * (mean / width)

    @pl.loop(0, width // tile)
    def _(at):
        cols = tile_of(at)
        x, dn1 = x_ref[:, cols].astype(F32), total(cols)
        gain_own[pl.ds(0, 1), cols] = jnp.sum(dn1 * x * scale, axis=0, keepdims=True)
        gain_own[pl.ds(1, 1), cols] = second_ref[:, cols]
        tok_ref[:, cols] = (dh1_ref[:, cols] + scale * (gain_ref[:, cols] * dn1) - x * pull).astype(BF)

    keep_tok = pltpu.make_async_copy(tok_ref, tok_all.at[place], local_sem.at[1])
    keep_tok.start()
    toks = gather(tok_ref, tok_all, 0, None)
    wide = width // batches

    def slice_of(at):
        return pl.ds(pl.multiple_of(at * wide, wide), wide)

    gains = [
        go(gain_own.at[:, slice_of(other)], gain_got.at[hop], (other, head))
        for hop, other in enumerate(others)
    ]
    toks = gather(tok_ref, tok_all, 1, toks)
    middle = gain_own[:, slice_of(batch)]
    for hop, copy in enumerate(gains):
        copy.wait_recv()
        middle = middle + gain_got[hop]
    gain_mid[...] = middle
    gain_heads[place] = middle
    gains = [go(gain_mid, gain_heads.at[place], member) for member in members]
    for step in range(2, steps):
        toks = gather(tok_ref, tok_all, step, toks)
    for copy in gains:
        copy.wait_recv()
    middle = gain_heads[0]
    for at in range(1, count):
        middle = middle + gain_heads[at]
    gains_ref[...] = middle
    for copy in (*wsums, *outs):
        copy.wait_recv()
    wout_own[...] = (
        wout_ref[span(place, wout_own.shape[0])].astype(F32)
        + wout_got[0, steps - 1].astype(F32)
        + wout_got[1, steps - 1].astype(F32)
    )
    for copy in toks:
        copy.wait_recv()
    for copy in copies:
        copy.wait_send()
    keep_out.wait()
    keep_tok.wait()


def tail(d_cat, w_in, x_own, gain, d_resid, wout_part, second, pieces, collective_id):
    count = lax.axis_size("head")
    batches = lax.axis_size("batch")
    steps = count // 2
    rows, width = x_own.shape
    size, wide = wout_part.shape[0] // count, wout_part.shape[1]
    vmem = pl.BlockSpec(memory_space=pltpu.VMEM)
    whole = jax.ShapeDtypeStruct((count, rows, width), BF)
    sems = pltpu.SemaphoreType.DMA((5 * count + batches,))
    gains = (2, width // batches)
    return pl.pallas_call(
        functools.partial(tail_kernel, count, batches),
        out_shape=[
            whole,
            whole,
            jax.ShapeDtypeStruct(gains, F32),
            jax.ShapeDtypeStruct((size, wide), F32),
        ],
        in_specs=[vmem] * 8,
        out_specs=[vmem] * 4,
        scratch_shapes=[
            pltpu.VMEM((count * rows, width), BF),
            pltpu.VMEM((rows, width), BF),
            pltpu.VMEM((2, steps, rows, width), BF),
            pltpu.VMEM((2, steps, size, wide), BF),
            pltpu.VMEM((2, width), F32),
            pltpu.VMEM((batches - 1, *gains), F32),
            pltpu.VMEM(gains, F32),
            pltpu.VMEM((count, *gains), F32),
            sems,
            sems,
            pltpu.SemaphoreType.DMA((2,)),
        ],
        compiler_params=pltpu.CompilerParams(
            collective_id=collective_id, has_side_effects=True, vmem_limit_bytes=VMEM_LIMIT
        ),
        cost_estimate=pl.CostEstimate(
            flops=2 * count * rows * width * d_cat.shape[1], bytes_accessed=400 << 20, transcendentals=0
        ),
        name="tail",
    )(d_cat, w_in, x_own, gain, d_resid, wout_part, second, *pieces)


def local_call(kernel, scalars, arrays, outs, scratch, flops, name):
    vmem = pl.BlockSpec(memory_space=pltpu.VMEM)
    smem = pl.BlockSpec(memory_space=pltpu.SMEM)
    return pl.pallas_call(
        kernel,
        out_shape=outs,
        in_specs=[smem] * len(scalars) + [vmem] * len(arrays),
        out_specs=[vmem] * len(outs),
        scratch_shapes=scratch,
        compiler_params=pltpu.CompilerParams(vmem_limit_bytes=VMEM_LIMIT),
        cost_estimate=pl.CostEstimate(flops=flops, bytes_accessed=8 << 20, transcendentals=0),
        name=name,
    )(*scalars, *arrays)


def ring_routes(count):
    spots = [ring_head(at, count) for at in range(count)]
    right = [(spots[at], spots[(at + 1) % count]) for at in range(count)]
    left = [(spots[at], spots[at - 1]) for at in range(count)]
    return right, left


def add_low(one, other):
    return (one.astype(F32) + other.astype(F32)).astype(BF)


def flow_steps(part, going, coming):
    count = lax.axis_size("head")
    place = ring_place(lax.axis_index("head"), count)
    right, left = ring_routes(count)
    rows = part.shape[0] // count
    steps = count // 2

    def mine(owner):
        return lax.dynamic_slice_in_dim(part, lax.rem(owner + count, count) * rows, rows, 0)

    for step in range(2, steps - 1):
        from_left = lax.ppermute(going, "head", right)
        from_right = lax.ppermute(coming, "head", left)
        going = add_low(from_left, mine(place + steps - 1 - step))
        coming = add_low(from_right, mine(place - steps + 1 + step))
        going, coming = yield going, coming
    from_left = lax.ppermute(going, "head", right)
    from_right = lax.ppermute(coming, "head", left)
    yield mine(place).astype(F32) + from_left.astype(F32) + from_right.astype(F32)


def matmul(left, right):
    return jnp.dot(left, right, preferred_element_type=F32)


def rows_inner(left, right):
    return lax.dot_general(left, right, (((0,), (0,)), ((), ())), preferred_element_type=F32)


def cols_inner(left, right):
    return lax.dot_general(left, right, (((1,), (1,)), ((), ())), preferred_element_type=F32)


def rms_scale(values):
    return lax.rsqrt(jnp.mean(values * values, axis=1, keepdims=True) + EPSILON)


def per_device(
    tokens,
    segment_ids,
    norm1_gain,
    w_query,
    w_key,
    w_value,
    w_gate,
    w_out,
    norm2_gain,
    w_mlp_gate,
    w_mlp_up,
    w_down,
    out_grad,
):
    heads = lax.axis_size("head")
    batches = lax.axis_size("batch")
    row_count, width = tokens.shape
    head_size = w_query.shape[1]
    half = w_key.shape[1]
    chunk = row_count // heads
    me = ring_place(lax.axis_index("head"), heads)
    scale_factor = 1.0 / math.sqrt(head_size)

    w_shard = jnp.concatenate([w_query, w_gate, w_key, w_value], axis=1)
    gains = jnp.concatenate([norm1_gain, norm2_gain]).reshape(-1, 128).astype(F32)
    normed_one, queries, gate_logit, kv_all, w_in, out_full, gains, seg_all, down_full = entry(
        tokens, w_shard, w_out, gains, segment_ids.reshape(-1, 128), w_down, 1
    )
    gains, w_mlp_gate, w_mlp_up = lax.optimization_barrier((gains, w_mlp_gate, w_mlp_up))
    seg_all = seg_all.reshape(-1)
    gains = gains.reshape(batches, 2, -1).transpose(1, 0, 2).reshape(2, width)
    gain_one, gain_two = gains[0], gains[1]
    mgate_full = lax.all_gather(w_mlp_gate, "batch", axis=0, tiled=True)
    mup_full = lax.all_gather(w_mlp_up, "batch", axis=0, tiled=True)

    base = lax.axis_index("batch") * row_count
    ids = jnp.arange(DOCUMENTS, dtype=jnp.int32)
    below = jnp.sum((seg_all[None, :] < ids[:, None]).astype(jnp.int32), axis=1)
    starts = jnp.sum(jnp.where(segment_ids[None, :] == ids[:, None], below[:, None], 0), axis=0)
    scalars = (starts, base.reshape(1))
    pair_flops = 4 * row_count * kv_all.shape[0] * head_size
    attended, mixed, lse = local_call(
        functools.partial(attend_kernel, scale_factor),
        scalars,
        (queries, kv_all, starts[None], gate_logit),
        [
            jax.ShapeDtypeStruct((row_count, head_size), F32),
            jax.ShapeDtypeStruct((row_count, head_size), BF),
            jax.ShapeDtypeStruct((1, row_count), F32),
        ],
        [],
        pair_flops,
        "attend",
    )
    (mixed_all,) = spread([mixed], (("head", "cols"),), 2)
    (
        mlp_part, d_mlp, d_down, resid_own, d_resid, d_resid_low, d_gain_two, d_mixed, going, coming,
    ) = mlp_back(
        tokens, mixed_all, out_grad, gain_two[None], out_full, mgate_full, mup_full, down_full, 3
    )
    hold = lax.optimization_barrier
    mixed_own = lax.dynamic_slice_in_dim(mixed_all, me * chunk, chunk, 0)
    flow = flow_steps(mlp_part, going, coming)
    state = next(flow)
    d_out_part = rows_inner(mixed_own, d_resid_low).astype(BF)
    d_out_part = lax.psum_scatter(d_out_part, "batch", scatter_dimension=1, tiled=True)

    d_queries, d_gate_logit, d_kv_all = local_call(
        functools.partial(attend_back_kernel, scale_factor),
        scalars,
        (queries, kv_all, starts[None], gate_logit, attended, d_mixed, lse),
        [
            jax.ShapeDtypeStruct((row_count, head_size), BF),
            jax.ShapeDtypeStruct((row_count, head_size), BF),
            jax.ShapeDtypeStruct(kv_all.shape, BF),
        ],
        [pltpu.VMEM((kv_all.shape[0], head_size), F32)] * 2,
        5 * pair_flops // 2,
        "attend_back",
    )
    d_kv_all, state = hold((d_kv_all, state))
    while isinstance(state, tuple):
        state = flow.send(state)
    d_kv = fold(d_kv_all, row_count, 4)
    d_kv, state, d_out_part, d_down, d_mlp = hold((d_kv, state, d_out_part, d_down, d_mlp))
    out_own = (resid_own + state).astype(BF)
    d_down = lax.psum_scatter(d_down, "batch", scatter_dimension=1, tiled=True)
    d_mlp = lax.psum_scatter(d_mlp, "batch", scatter_dimension=0, tiled=True)
    d_cat = jnp.concatenate([d_queries, d_gate_logit, d_kv], axis=1)
    d_in = rows_inner(normed_one, d_cat).astype(BF)
    d_cat, d_in = hold((d_cat, d_in))
    d_in = lax.psum_scatter(d_in, "batch", scatter_dimension=0, tiled=True)
    inputs_own = lax.dynamic_slice_in_dim(tokens, me * chunk, chunk, 0)
    output, d_tokens, d_gains, d_out = tail(
        d_cat, w_in, inputs_own, gain_one[None], d_resid, d_out_part, d_gain_two, [out_own], 5
    )
    d_tokens, d_in, d_mlp, d_down = hold((d_tokens, d_in, d_mlp, d_down))
    d_in, d_mlp, d_down = d_in.astype(F32), d_mlp.astype(F32), d_down.astype(F32)
    output = output.reshape(row_count, width)
    d_tokens = d_tokens.reshape(row_count, width)
    hidden_own = w_mlp_gate.shape[1]
    return (
        output,
        d_tokens,
        d_gains[0],
        d_in[:, :head_size],
        d_in[:, 2 * head_size : 2 * head_size + half],
        d_in[:, 2 * head_size + half :],
        d_in[:, head_size : 2 * head_size],
        d_out,
        d_gains[1],
        d_mlp[:, :hidden_own],
        d_mlp[:, hidden_own:],
        d_down,
    )


def solution(mesh):
    return jax.shard_map(
        per_device,
        mesh=mesh,
        in_specs=(
            P("batch", None),
            P("batch"),
            P("batch"),
            P("batch", "head"),
            P("batch", "head"),
            P("batch", "head"),
            P("batch", "head"),
            P("head", "batch"),
            P("batch"),
            P("batch", "head"),
            P("batch", "head"),
            P("head", "batch"),
            P("batch", None),
        ),
        out_specs=(
            P("batch", None),
            P("batch", None),
            P("batch"),
            P("batch", "head"),
            P("batch", "head"),
            P("batch", "head"),
            P("batch", "head"),
            P("head", "batch"),
            P("batch"),
            P("batch", "head"),
            P("batch", "head"),
            P("head", "batch"),
        ),
        check_vma=False,
    )
```

```python
import functools
import math

import jax
import jax.numpy as jnp
from jax import lax
from jax.experimental import pallas as pl
from jax.experimental.pallas import tpu as pltpu
from jax.sharding import PartitionSpec as P

EPSILON = 1e-06
MASKED = -1e30
DOCUMENTS = 7
BF = jnp.bfloat16
F32 = jnp.float32


MESH = pl.DeviceIdType.MESH
VMEM_LIMIT = 60 << 20


def ring_place(head, count):
    high, low = head // 2, head % 2
    return (1 - low) * high + low * (count - 1 - high)


def ring_head(place, count):
    low = place // (count // 2)
    high = (1 - low) * place + low * (count - 1 - place)
    return 2 * high + low


def ring_setup(count):
    batch = lax.axis_index("batch")
    place = ring_place(lax.axis_index("head"), count)
    right = (batch, ring_head(lax.rem(place + 1, count), count))
    left = (batch, ring_head(lax.rem(place + count - 1, count), count))
    return place, right, left


def greet(devices):
    barrier = pltpu.get_barrier_semaphore()
    for device in devices:
        pl.semaphore_signal(barrier, inc=1, device_id=device, device_id_type=MESH)
    pl.semaphore_wait(barrier, len(devices))


def send(source, target, sems, slot, device):
    copy = pltpu.make_async_remote_copy(
        src_ref=source,
        dst_ref=target,
        send_sem=sems[0].at[slot],
        recv_sem=sems[1].at[slot],
        device_id=device,
        device_id_type=MESH,
    )
    copy.start()
    return copy


def half_of(extent, flow):
    if extent[1] % 256:
        return (pl.ds(flow * (extent[0] // 2), extent[0] // 2), slice(None))
    return (slice(None), pl.ds(flow * (extent[1] // 2), extent[1] // 2))


def place_of(whole, own, chunk, form):
    rows, wide = own.shape[-2:]
    if form == "lead":
        return whole.at[chunk]
    if form == "rows":
        return whole.at[pl.ds(pl.multiple_of(chunk * rows, rows), rows)]
    return whole.at[:, pl.ds(pl.multiple_of(chunk * wide, wide), wide)]


def spread_kernel(count, batches, plans, *refs):
    steps = count // 2
    arrays = len(plans)
    own_refs, all_refs = refs[:arrays], refs[arrays : 2 * arrays]
    send_sem, recv_sem, local_sem = refs[2 * arrays :]
    place, right, left = ring_setup(count)
    head = lax.axis_index("head")
    batch = lax.axis_index("batch")
    across, core = batch // 2, lax.rem(batch, 2)
    others = batches // 2
    twin = (across * 2 + 1 - core, head)
    peers = [(lax.rem(across + hop, others) * 2 + core, head) for hop in range(1, others)]
    ring = any(axis == "head" for axis, _ in plans)
    grid = any(axis == "batch" for axis, _ in plans)
    greet((right, left) * ring + (twin, *peers) * grid)
    sems = (send_sem, recv_sem)
    slot = 0
    waiting, arriving, local = [], [], []

    def go(source, target, device):
        nonlocal slot
        copy = send(source, target, sems, slot, device)
        slot += 1
        waiting.append(copy)
        return copy

    onward = []
    for index, (axis, form) in enumerate(plans):
        own, whole = own_refs[index], all_refs[index]
        spot = place if axis == "head" else batch
        mine = place_of(whole, own, spot, form)
        copy = pltpu.make_async_copy(own, mine, local_sem.at[index])
        copy.start()
        local.append(copy)
        if axis == "batch":
            for hop, peer in enumerate(peers, 1):
                source = lax.rem(across + others - hop, others) * 2 + core
                onward.append((go(own, mine, peer), place_of(whole, own, source, form)))
            arriving.append(go(own, mine, twin))
    copies = [None] * (2 * arrays)
    for step in range(steps):
        for index, (axis, form) in enumerate(plans):
            if axis != "head":
                continue
            own = own_refs[index]
            for flow, chunk, device in ((0, place - step, right), (1, place + step, left)):
                at = 2 * index + flow
                if step:
                    copies[at].wait_recv()
                chunk = lax.rem(chunk + count, count)
                target = place_of(all_refs[index], own, chunk, form)
                source = target if step else own
                if step == steps - 1:
                    part = half_of(own.shape, flow)
                    source = source.at[part]
                    target = target.at[part]
                copies[at] = go(source, target, device)
        if step == 0 or not ring:
            for copy, block in onward:
                copy.wait_recv()
                arriving.append(go(block, block, twin))
            onward = []
    for copy in copies:
        if copy is not None:
            arriving.append(copy)
    for copy in arriving:
        copy.wait_recv()
    for copy in waiting:
        copy.wait_send()
    for copy in local:
        copy.wait()


def spread(arrays, plans, collective_id):
    count = lax.axis_size("head")
    batches = lax.axis_size("batch")
    shapes = []
    slots = 0
    for array, (axis, form) in zip(arrays, plans):
        many = count if axis == "head" else batches
        slots += count if axis == "head" else batches - 1
        if form == "lead":
            shapes.append((many, *array.shape))
        elif form == "rows":
            shapes.append((many * array.shape[0], array.shape[1]))
        else:
            shapes.append((array.shape[0], many * array.shape[1]))
    hbm = pl.BlockSpec(memory_space=pl.ANY)
    return pl.pallas_call(
        functools.partial(spread_kernel, count, batches, plans),
        out_shape=[jax.ShapeDtypeStruct(shape, a.dtype) for shape, a in zip(shapes, arrays)],
        in_specs=[pl.BlockSpec(memory_space=pltpu.VMEM)] * len(arrays),
        out_specs=[hbm] * len(arrays),
        scratch_shapes=[
            pltpu.SemaphoreType.DMA((slots,)),
            pltpu.SemaphoreType.DMA((slots,)),
            pltpu.SemaphoreType.DMA((len(arrays),)),
        ],
        compiler_params=pltpu.CompilerParams(
            collective_id=collective_id, has_side_effects=True, vmem_limit_bytes=8 << 20
        ),
        name=f"spread_{collective_id}",
    )(*arrays)


def mlp_kernel(
    count, x_hbm, a_hbm, dy_hbm, gain_ref, out_w, gate_w, up_w, down_w,
    mlp_hbm, dmlp_hbm, ddown_hbm, h1_ref, dh1_ref, low_ref, dgain_ref, da_ref, ahead_ref, behind_ref,
    x_s, a_s, mlp_s, h1_s, dy_all, n2_all, hid_all, grad_all, dmlp_s, ddown_s, da_part,
    mlp_far, mlp_next, mlp_got, right_part, left_part, right_got, left_got,
    in_sem, out_sem, grad_sem, send_sem, recv_sem, da_send, da_recv, far_send, far_recv,
):
    steps = count // 2
    rows = x_hbm.shape[0] // count
    width = x_hbm.shape[1]
    hidden = gate_w.shape[1]
    side = width // 2
    tile = 256
    inner = 256 if hidden % 256 == 0 else 128
    size = da_ref.shape[1]
    place, right, left = ring_setup(count)

    def member(hop):
        spot = lax.rem(place + hop, count)
        return spot, (lax.axis_index("batch"), ring_head(spot, count))

    greet([member(hop)[1] for hop in range(1, count)])

    def owners(group):
        first = jnp.where(group == 0, 1, 0)
        one = lax.rem(place + steps - group, count)
        two = lax.rem(place - steps + group + first * steps + count, count)
        return one, two

    def span(owner):
        return pl.ds(pl.multiple_of(owner * rows, rows), rows)

    def tile_of(at, extent=tile):
        return pl.ds(pl.multiple_of(at * extent, extent), extent)

    def loads(group, slot):
        return [
            pltpu.make_async_copy(
                source.at[span(owner)],
                target.at[pl.ds(at * rows, rows)],
                in_sem.at[slot, 2 * index + at],
            )
            for index, (source, target) in enumerate(
                ((x_hbm, x_s.at[slot]), (a_hbm, a_s.at[slot]), (dy_hbm, dy_all.at[group]))
            )
            for at, owner in enumerate(owners(group))
        ]

    def stores(group, slot):
        return [
            pltpu.make_async_copy(
                mlp_s.at[slot, pl.ds(at * rows, rows)], mlp_hbm.at[span(owner)], out_sem.at[slot, at]
            )
            for at, owner in enumerate(owners(group))
        ]

    def passing(source, target, sems, slot, device):
        return pltpu.make_async_remote_copy(
            src_ref=source,
            dst_ref=target,
            send_sem=sems[0].at[slot],
            recv_sem=sems[1].at[slot],
            device_id=device,
            device_id_type=MESH,
        )

    ring_sems, far_sems = (send_sem, recv_sem), (far_send, far_recv)
    ahead, behind = pl.ds(0, side), pl.ds(side, side)

    def first_copies():
        return (
            passing(right_part.at[0, :, ahead], right_got.at[0, :, ahead], ring_sems, 0, right),
            passing(right_part.at[0, :, behind], left_got.at[0, :, behind], ring_sems, steps, left),
        )

    def later_copies(step):
        return (
            passing(right_got.at[step - 1], right_got.at[step], ring_sems, step, right),
            passing(left_got.at[step - 1], left_got.at[step], ring_sems, steps + step, left),
        )

    for copy in loads(0, 0):
        copy.start()

    @pl.loop(0, steps)
    def _(group):
        slot = lax.rem(group, 2)
        for copy in loads(group, slot):
            copy.wait()

        @pl.when(group + 1 < steps)
        def _():
            for copy in loads(group + 1, 1 - slot):
                copy.start()

        @pl.when(group >= 2)
        def _():
            for copy in stores(group - 2, slot):
                copy.wait()

        mixed = a_s[slot]

        def residual(at, total):
            cols = tile_of(at)
            values = x_s[slot, :, cols].astype(F32) + matmul(mixed, out_w[:, cols])
            h1_s[:, cols] = values
            return total + jnp.sum(values * values, axis=1, keepdims=True)

        total = lax.fori_loop(0, width // tile, residual, jnp.zeros((2 * rows, 1), F32))
        scale = lax.rsqrt(total / width + EPSILON)

        @pl.when(group == 0)
        def _():
            h1_ref[...] = h1_s[pl.ds(rows, rows)]

        @pl.loop(0, width // tile)
        def _(at):
            cols = tile_of(at)
            n2_all[group, :, cols] = (h1_s[:, cols] * scale * gain_ref[:, cols]).astype(BF)

        normed = n2_all[group]
        dy = dy_all[group]

        @pl.loop(0, hidden // inner)
        def _(at):
            cols = tile_of(at, inner)
            cols_up = pl.ds(pl.multiple_of(hidden + at * inner, inner), inner)
            gate = matmul(normed, gate_w[:, cols])
            up = matmul(normed, up_w[:, cols])
            d_hidden = cols_inner(dy, down_w[cols])
            sig = jax.nn.sigmoid(gate)
            silu = gate * sig
            hid_all[group, :, cols] = (silu * up).astype(BF)
            grad_all[group, :, cols] = (d_hidden * up * sig * (1.0 + gate * (1.0 - sig))).astype(BF)
            grad_all[group, :, cols_up] = (d_hidden * silu).astype(BF)

        hid = hid_all[group]
        d_gate = grad_all[group, :, :hidden]
        d_up = grad_all[group, :, hidden:]
        half = jnp.minimum(group, 1)

        @pl.loop(0, width // tile)
        def _(at):
            cols = tile_of(at)
            part = (cols_inner(d_gate, gate_w[cols]) + cols_inner(d_up, up_w[cols])).astype(BF)
            right_part[half, :, cols] = part[:rows]
            left_part[half, :, cols] = part[rows:]
            mlp_s[slot, :, cols] = matmul(hid, down_w[:, cols]).astype(BF)

        for copy in stores(group, slot):
            copy.start()

        @pl.when(group == 0)
        def _():
            mlp_far[...] = mlp_s[slot, pl.ds(0, rows)]
            for copy in first_copies():
                copy.start()

        @pl.when(group == 1)
        def _():
            mlp_next[0] = mlp_s[slot, pl.ds(0, rows)]
            mlp_next[1] = mlp_s[slot, pl.ds(rows, rows)]
            one, two = first_copies()
            one.wait_recv()
            right_got[0, :, ahead] = add_low(right_part[1, :, ahead], right_got[0, :, ahead])
            right_got[0, :, behind] = right_part[1, :, behind]
            two.wait_recv()
            left_got[0, :, behind] = add_low(left_part[1, :, behind], left_got[0, :, behind])
            left_got[0, :, ahead] = left_part[1, :, ahead]

        @pl.when(group == 2)
        def _():
            ahead_ref[...] = mlp_s[slot, pl.ds(0, rows)]
            behind_ref[...] = mlp_s[slot, pl.ds(rows, rows)]

        @pl.when(group >= 2)
        def _():
            one, two = later_copies(group - 1)
            one.wait_recv()
            right_got[group - 1] = add_low(right_part[1], right_got[group - 1])
            two.wait_recv()
            left_got[group - 1] = add_low(left_part[1], left_got[group - 1])

        @pl.when(group >= 1)
        def _():
            for copy in later_copies(group):
                copy.start()

    far_copies = [
        passing(mlp_far.at[:, ahead], mlp_got.at[0, :, ahead], far_sems, 0, right),
        passing(mlp_far.at[:, behind], mlp_got.at[1, :, behind], far_sems, 1, left),
    ]
    for copy in far_copies:
        copy.start()

    every = steps * 2 * rows

    def dmlp_copy(at, slot):
        return pltpu.make_async_copy(
            dmlp_s.at[slot], dmlp_hbm.at[tile_of(at // 2), tile_of(lax.rem(at, 2), hidden)], grad_sem.at[slot]
        )

    mlp_tiles = 2 * (width // tile)

    @pl.loop(0, mlp_tiles)
    def _(at):
        slot = lax.rem(at, 2)

        @pl.when(at >= 2)
        def _():
            dmlp_copy(at - 2, slot).wait()

        normed = n2_all[:, :, tile_of(at // 2)].reshape(every, tile)
        grads = grad_all[:, :, tile_of(lax.rem(at, 2), hidden)].reshape(every, hidden)
        dmlp_s[slot] = rows_inner(normed, grads).astype(BF)
        dmlp_copy(at, slot).start()

    wide = 512
    across = width // wide

    def ddown_copy(at, slot):
        return pltpu.make_async_copy(
            ddown_s.at[slot],
            ddown_hbm.at[tile_of(at // across, inner), tile_of(lax.rem(at, across), wide)],
            grad_sem.at[2 + slot],
        )

    down_tiles = across * (hidden // inner)

    @pl.loop(0, down_tiles)
    def _(at):
        slot = lax.rem(at, 2)

        @pl.when(at >= 2)
        def _():
            ddown_copy(at - 2, slot).wait()

        hid = hid_all[:, :, tile_of(at // across, inner)].reshape(every, inner)
        dy = dy_all[:, :, tile_of(lax.rem(at, across), wide)].reshape(every, wide)
        ddown_s[slot] = rows_inner(hid, dy).astype(BF)
        ddown_copy(at, slot).start()

    for copy in later_copies(steps - 1):
        copy.wait_recv()
    for flow, have, lack in ((0, ahead, behind), (1, behind, ahead)):
        far_copies[flow].wait_recv()
        mlp_got[flow, :, have] = add_low(mlp_got[flow, :, have], mlp_next[flow, :, have])
        mlp_got[flow, :, lack] = mlp_next[flow, :, lack]
    next_copies = [
        passing(mlp_got.at[0], mlp_got.at[2], far_sems, 2, right),
        passing(mlp_got.at[1], mlp_got.at[3], far_sems, 3, left),
    ]
    for copy in next_copies:
        copy.start()

    def collect(at, state):
        squares, mean = state
        cols = tile_of(at)
        dn2 = (
            left_part[0, :, cols].astype(F32)
            + right_got[steps - 1, :, cols].astype(F32)
            + left_got[steps - 1, :, cols].astype(F32)
        )
        dh1_ref[:, cols] = dn2
        h1 = h1_ref[:, cols]
        squares = squares + jnp.sum(h1 * h1, axis=1, keepdims=True)
        return squares, mean + jnp.sum(gain_ref[:, cols] * dn2 * h1, axis=1, keepdims=True)

    zero = jnp.zeros((rows, 1), F32)
    squares, mean = lax.fori_loop(0, width // tile, collect, (zero, zero))
    scale_own = lax.rsqrt(squares / width + EPSILON)
    pull = scale_own * scale_own * scale_own * (mean / width)

    @pl.loop(0, width // tile)
    def _(at):
        cols = tile_of(at)
        dn2, h1 = dh1_ref[:, cols], h1_ref[:, cols]
        dgain_ref[:, cols] = jnp.sum(dn2 * h1 * scale_own, axis=0, keepdims=True)
        dy = dy_all[0, pl.ds(rows, rows), cols].astype(F32)
        d_resid = dy + scale_own * (gain_ref[:, cols] * dn2) - h1 * pull
        dh1_ref[:, cols] = d_resid
        low_ref[:, cols] = d_resid.astype(BF)

    def da_copy(hop):
        return passing(
            da_part.at[hop], da_ref.at[span(place)], (da_send, da_recv), hop, member(hop)[1]
        )

    low = low_ref[...]

    @pl.loop(1, count)
    def _(hop):
        spot = member(hop)[0]
        da_part[hop] = cols_inner(low, out_w[tile_of(spot, size)]).astype(BF)
        da_copy(hop).start()

    da_ref[span(place)] = cols_inner(low, out_w[tile_of(place, size)]).astype(BF)

    @pl.loop(1, count)
    def _(hop):
        da_copy(hop).wait_recv()
        da_copy(hop).wait_send()

    for flow, held in ((0, ahead_ref), (1, behind_ref)):
        next_copies[flow].wait_recv()
        held[...] = add_low(held[...], mlp_got[2 + flow])
    for copy in (*far_copies, *next_copies, *first_copies()):
        copy.wait_send()
    for step in range(1, steps):
        for copy in later_copies(step):
            copy.wait_send()
    for group in range(steps - 2, steps):
        for copy in stores(group, group % 2):
            copy.wait()
    for at in range(2):
        dmlp_copy(mlp_tiles - 2 + at, (mlp_tiles + at) % 2).wait()
        ddown_copy(down_tiles - 2 + at, (down_tiles + at) % 2).wait()


def mlp_back(tokens, mixed, dy, gain, out_w, gate_w, up_w, down_w, collective_id):
    count = lax.axis_size("head")
    total, width = tokens.shape
    hidden = gate_w.shape[1]
    rows, steps = total // count, count // 2
    size = mixed.shape[1] // count
    inner = 256 if hidden % 256 == 0 else 128
    vmem = pl.BlockSpec(memory_space=pltpu.VMEM)
    hbm = pl.BlockSpec(memory_space=pl.ANY)

    def slots(many, tall, wide, dtype=BF):
        return pltpu.VMEM((many, tall, wide), dtype)

    def shape(*extent, dtype=BF):
        return jax.ShapeDtypeStruct(extent, dtype)

    dma = pltpu.SemaphoreType.DMA
    flops = 2 * total * width * (mixed.shape[1] + 9 * hidden)
    return pl.pallas_call(
        functools.partial(mlp_kernel, count),
        out_shape=[
            shape(total, width), shape(width, 2 * hidden), shape(hidden, width),
            shape(rows, width, dtype=F32), shape(rows, width, dtype=F32), shape(rows, width),
            shape(1, width, dtype=F32), shape(total, size), shape(rows, width), shape(rows, width),
        ],
        in_specs=[hbm] * 3 + [vmem] * 5,
        out_specs=[hbm] * 3 + [vmem] * 7,
        scratch_shapes=[
            slots(2, 2 * rows, width), slots(2, 2 * rows, mixed.shape[1]), slots(2, 2 * rows, width),
            pltpu.VMEM((2 * rows, width), F32),
            slots(steps, 2 * rows, width), slots(steps, 2 * rows, width),
            slots(steps, 2 * rows, hidden), slots(steps, 2 * rows, 2 * hidden),
            slots(2, 256, hidden), slots(2, inner, 512), slots(count, rows, size),
            pltpu.VMEM((rows, width), BF), slots(2, rows, width), slots(4, rows, width),
            slots(2, rows, width), slots(2, rows, width),
            slots(steps, rows, width), slots(steps, rows, width),
            dma((2, 6)), dma((2, 2)), dma((4,)), dma((count,)), dma((count,)),
            dma((count,)), dma((count,)), dma((4,)), dma((4,)),
        ],
        compiler_params=pltpu.CompilerParams(
            collective_id=collective_id, has_side_effects=True, vmem_limit_bytes=VMEM_LIMIT
        ),
        cost_estimate=pl.CostEstimate(flops=flops, bytes_accessed=40 << 20, transcendentals=0),
        name="mlp_back",
    )(tokens, mixed, dy, gain, out_w, gate_w, up_w, down_w)


def entry_kernel(
    count, batches, x_ref, w_ref, out_ref, gain_ref, seg_ref, down_ref,
    n1_ref, q_ref, logit_ref, kv_ref, w_all, out_all, gain_all, seg_all, down_all,
    send_sem, recv_sem, local_sem,
):
    steps = count // 2
    others = batches // 2
    rows, width = x_ref.shape
    depth = w_ref.shape[0]
    size, wide = out_ref.shape
    block = 256
    place, right, left = ring_setup(count)
    head = lax.axis_index("head")
    batch = lax.axis_index("batch")
    across, core, low = batch // 2, lax.rem(batch, 2), lax.rem(head, 2)
    twin = (across * 2 + 1 - core, head)
    mate = (batch, head + 1 - 2 * low)
    spots = [lax.rem(across + hop, others) for hop in range(others)]
    backs = [lax.rem(across + others - hop, others) for hop in range(others)]
    peers = [(spot * 2 + core, head) for spot in spots]
    far_peers = [(spot * 2 + 1 - core, head) for spot in spots]
    greet((twin, mate, right, left, *peers[1:], *far_peers[1:]))
    sems = (send_sem, recv_sem)
    slot = 0
    copies = []

    def go(source, target, device):
        nonlocal slot
        copy = send(source, target, sems, slot, device)
        slot += 1
        copies.append(copy)
        return copy

    def part(at, extent):
        return pl.ds(pl.multiple_of(at * extent, extent), extent)

    def both(view, own):
        out = [go(own, view(batch), peers[hop]) for hop in range(1, others)]
        return out, [go(own, view(batch), twin)]

    def pass_on(view, arrived):
        out = []
        for hop in range(1, others):
            arrived[hop - 1].wait_recv()
            there = view(backs[hop] * 2 + core)
            out.append(go(there, there, twin))
        return out

    local = []

    def stay(source, target):
        copy = pltpu.make_async_copy(source, target, local_sem.at[len(local)])
        copy.start()
        local.append(copy)

    def main_view(at):
        return w_all.at[part(at, depth), pl.ds(0, 3 * size)]

    def mate_view(at):
        return w_all.at[part(at, depth), pl.ds(3 * size, size)]

    def out_view(chunk, at):
        return out_all.at[part(chunk, size), part(at, wide)]

    small = []
    for own, whole in ((gain_ref, gain_all), (seg_ref, seg_all)):
        for device in (twin, *peers[1:], *far_peers[1:]):
            small.append(go(own, whole.at[batch], device))
        stay(own, whole.at[batch])
    from_mate = go(w_ref.at[:, pl.ds(2 * size, size)], mate_view(batch), mate)
    main_out, main_twin = both(main_view, w_ref)
    stay(w_ref, main_view(batch))
    out_peers = [go(out_ref, out_view(place, batch), peers[hop]) for hop in range(1, others)]
    stay(out_ref, out_view(place, batch))
    flows = [[None, None] for _ in range(others)]

    def ring(step):
        for hop in range(others):
            lane = spots[0] if hop == 0 else backs[hop]
            at = lane * 2 + core
            if step == 0 and hop:
                out_peers[hop - 1].wait_recv()
            for flow, chunk, device in ((0, place - step, right), (1, place + step, left)):
                if step:
                    flows[hop][flow].wait_recv()
                target = out_view(lax.rem(chunk + count, count), at)
                source = out_ref if step == 0 and hop == 0 else target
                if step == steps - 1:
                    cut = (pl.ds(flow * (size // 2), size // 2), slice(None))
                    source, target = source.at[cut], target.at[cut]
                flows[hop][flow] = go(source, target, device)

    for copy in small:
        copy.wait_recv()
    for copy in local[:2]:
        copy.wait()

    def normalize(at):
        here = part(at, block)

        def squares(tile, total):
            values = x_ref[here, part(tile, 256)].astype(F32)
            return total + jnp.sum(values * values, axis=1, keepdims=True)

        total = lax.fori_loop(0, width // 256, squares, jnp.zeros((block, 1), F32))
        scale = lax.rsqrt(total / width + EPSILON)

        @pl.loop(0, batches)
        def _(owner):
            for tile in range(depth // 128):
                cols = pl.ds(pl.multiple_of(owner * depth + tile * 128, 128), 128)
                values = x_ref[here, cols].astype(F32) * scale
                n1_ref[here, cols] = (values * gain_all[owner, pl.ds(tile, 1)]).astype(BF)

    blocks = rows // block
    middle = blocks // 2

    @pl.loop(0, middle)
    def _(at):
        normalize(at)

    from_mate.wait_recv()
    mate_out, mate_twin = both(mate_view, mate_view(batch))
    ring(0)

    def down_view(at):
        return down_all.at[:, part(at, down_ref.shape[1])]

    down_out, down_twin = both(down_view, down_ref)
    stay(down_ref, down_view(batch))

    @pl.loop(middle, blocks)
    def _(at):
        normalize(at)

    main_passed = pass_on(main_view, main_out)
    mate_passed = pass_on(mate_view, mate_out)
    for copy in (*main_twin, *mate_twin, *main_passed, *mate_passed):
        copy.wait_recv()
    for copy in local[2:]:
        copy.wait()

    def kv_view(at):
        return kv_ref.at[part(at, rows)]

    @pl.loop(0, blocks)
    def _(at):
        here = part(at, block)
        values = matmul(n1_ref[here], w_all[:, pl.ds(2 * size, 2 * size)])
        one, two = values[:, :size], values[:, size:]
        first = jnp.where(low == 0, one, two).astype(BF)
        second = jnp.where(low == 0, two, one).astype(BF)
        half = size // 2
        there = pl.ds(pl.multiple_of(batch * rows + at * block, block), block)
        kv_ref[there, pl.ds(0, size)] = jnp.concatenate([first[:, :half], second[:, :half]], 1)
        kv_ref[there, pl.ds(size, size)] = jnp.concatenate([first[:, half:], second[:, half:]], 1)

    kv_out, kv_twin = both(kv_view, kv_view(batch))
    ring(1)

    @pl.loop(0, blocks)
    def _(at):
        here = part(at, block)
        values = matmul(n1_ref[here], w_all[:, pl.ds(0, 2 * size)])
        q_ref[here] = values[:, :size].astype(BF)
        logit_ref[here] = values[:, size:]

    for step in range(2, steps):
        ring(step)
    down_passed = pass_on(down_view, down_out)
    kv_passed = pass_on(kv_view, kv_out)
    for pair in flows:
        for copy in pair:
            copy.wait_recv()
    swaps = []
    for hop in range(others):
        there = out_all.at[:, part(spots[hop] * 2 + core, wide)]
        swaps.append(go(there, there, twin))
    for copy in (*kv_twin, *kv_passed, *swaps, *down_twin, *down_passed):
        copy.wait_recv()
    for copy in copies:
        copy.wait_send()


def entry(tokens, w_shard, w_out, gains, segments, w_down, collective_id):
    count = lax.axis_size("head")
    batches = lax.axis_size("batch")
    others = batches // 2
    rows, width = tokens.shape
    size, wide = w_out.shape
    vmem = pl.BlockSpec(memory_space=pltpu.VMEM)
    slots = 6 * batches + others * (count + 3)
    sems = pltpu.SemaphoreType.DMA((slots,))
    return pl.pallas_call(
        functools.partial(entry_kernel, count, batches),
        out_shape=[
            jax.ShapeDtypeStruct((rows, width), BF),
            jax.ShapeDtypeStruct((rows, size), BF),
            jax.ShapeDtypeStruct((rows, size), F32),
            jax.ShapeDtypeStruct((batches * rows, 2 * size), BF),
            jax.ShapeDtypeStruct((width, 4 * size), BF),
            jax.ShapeDtypeStruct((count * size, batches * wide), BF),
            jax.ShapeDtypeStruct((batches, *gains.shape), F32),
            jax.ShapeDtypeStruct((batches, *segments.shape), jnp.int32),
            jax.ShapeDtypeStruct((w_down.shape[0], batches * w_down.shape[1]), BF),
        ],
        in_specs=[vmem] * 6,
        out_specs=[vmem] * 9,
        scratch_shapes=[sems, sems, pltpu.SemaphoreType.DMA((5,))],
        compiler_params=pltpu.CompilerParams(
            collective_id=collective_id, has_side_effects=True, vmem_limit_bytes=44 << 20
        ),
        name="entry",
    )(tokens, w_shard, w_out, gains, segments, w_down)


KEY_BLOCK = 512
QUERY_BLOCK = 256


def key_range(start_ref, base, query_block):
    first = query_block * QUERY_BLOCK
    lowest = start_ref[first]
    highest = start_ref[first + QUERY_BLOCK - 1]
    begin = lowest // KEY_BLOCK
    end = (base + first + QUERY_BLOCK - 1) // KEY_BLOCK + 1
    full_begin = jnp.minimum((highest + KEY_BLOCK - 1) // KEY_BLOCK, end)
    full_end = jnp.maximum((base + first + 1) // KEY_BLOCK, full_begin)
    return begin, full_begin, full_end, end


def allowed_pairs(key_block, start_row, base_row):
    shape = (KEY_BLOCK, QUERY_BLOCK)
    key_pos = key_block * KEY_BLOCK + lax.broadcasted_iota(jnp.int32, shape, 0)
    query_pos = base_row + lax.broadcasted_iota(jnp.int32, shape, 1)
    return (key_pos >= start_row) & (key_pos <= query_pos)


def attend_kernel(
    scale, start_sm, base_sm, q_ref, kv_ref, start_ref, logit_ref, o_ref, a_ref, lse_ref
):
    base = base_sm[0]
    size = q_ref.shape[1]
    factor = scale * math.log2(math.e)

    @pl.loop(0, q_ref.shape[0] // QUERY_BLOCK)
    def _(block):
        rows = pl.ds(pl.multiple_of(block * QUERY_BLOCK, QUERY_BLOCK), QUERY_BLOCK)
        queries = q_ref[rows]
        start_row = start_ref[:, rows]
        begin, full_begin, full_end, end = key_range(start_sm, base, block)

        def step(masked, at, state):
            old_max, old_sum, total = state
            keys = pl.ds(pl.multiple_of(at * KEY_BLOCK, KEY_BLOCK), KEY_BLOCK)
            scores = cols_inner(kv_ref[keys, :size], queries)
            if masked:
                allowed = allowed_pairs(at, start_row, base + block * QUERY_BLOCK)
                scores = jnp.where(allowed, scores, MASKED)
            new_max = jnp.maximum(old_max, jnp.max(scores, axis=0, keepdims=True))
            keep = jnp.exp2((old_max - new_max) * factor)
            weights = jnp.exp2(scores * factor - new_max * factor)
            new_sum = old_sum * keep + jnp.sum(weights, axis=0, keepdims=True)
            total = total * keep + rows_inner(kv_ref[keys, size:], weights.astype(BF))
            return new_max, new_sum, total

        state = (
            jnp.full((1, QUERY_BLOCK), MASKED, F32),
            jnp.zeros((1, QUERY_BLOCK), F32),
            jnp.zeros((size, QUERY_BLOCK), F32),
        )
        state = lax.fori_loop(begin, full_begin, functools.partial(step, True), state)
        state = lax.fori_loop(full_begin, full_end, functools.partial(step, False), state)
        state = lax.fori_loop(full_end, end, functools.partial(step, True), state)
        run_max, run_sum, total = state
        lse_ref[:, rows] = run_max * factor + jnp.log2(run_sum)
        attended = (total / run_sum).T
        o_ref[rows] = attended
        a_ref[rows] = (attended * jax.nn.sigmoid(logit_ref[rows])).astype(BF)


def attend_back_kernel(
    scale, start_sm, base_sm, q_ref, kv_ref, start_ref, logit_ref, o_ref, da_ref, lse_ref,
    dq_ref, dg_ref, dkv_ref, dk_acc, dv_acc,
):
    base = base_sm[0]
    size = q_ref.shape[1]
    factor = scale * math.log2(math.e)
    dk_acc[...] = jnp.zeros_like(dk_acc)
    dv_acc[...] = jnp.zeros_like(dv_acc)

    @pl.loop(0, q_ref.shape[0] // QUERY_BLOCK)
    def _(block):
        rows = pl.ds(pl.multiple_of(block * QUERY_BLOCK, QUERY_BLOCK), QUERY_BLOCK)
        queries = q_ref[rows]
        start_row = start_ref[:, rows]
        lse = lse_ref[:, rows]
        gate = jax.nn.sigmoid(logit_ref[rows])
        attended = o_ref[rows]
        d_mixed = da_ref[rows].astype(F32)
        d_attended = (d_mixed * gate).astype(BF)
        dg_ref[rows] = (d_mixed * attended * gate * (1.0 - gate)).astype(BF)
        delta = jnp.sum((d_attended.astype(F32) * attended).T, axis=0, keepdims=True)
        begin, full_begin, full_end, end = key_range(start_sm, base, block)

        def step(masked, at, d_queries):
            keys = pl.ds(pl.multiple_of(at * KEY_BLOCK, KEY_BLOCK), KEY_BLOCK)
            key_block = kv_ref[keys, :size]
            probs = jnp.exp2(cols_inner(key_block, queries) * factor - lse)
            if masked:
                allowed = allowed_pairs(at, start_row, base + block * QUERY_BLOCK)
                probs = jnp.where(allowed, probs, 0.0)
            d_probs = cols_inner(kv_ref[keys, size:], d_attended)
            d_scores = (probs * (d_probs - delta) * scale).astype(BF)
            dv_acc[keys] += matmul(probs.astype(BF), d_attended)
            dk_acc[keys] += matmul(d_scores, queries)
            return d_queries + rows_inner(key_block, d_scores)

        d_queries = jnp.zeros((size, QUERY_BLOCK), F32)
        d_queries = lax.fori_loop(begin, full_begin, functools.partial(step, True), d_queries)
        d_queries = lax.fori_loop(full_begin, full_end, functools.partial(step, False), d_queries)
        d_queries = lax.fori_loop(full_end, end, functools.partial(step, True), d_queries)
        dq_ref[rows] = d_queries.T.astype(BF)

    @pl.loop(0, kv_ref.shape[0] // KEY_BLOCK)
    def _(at):
        keys = pl.ds(pl.multiple_of(at * KEY_BLOCK, KEY_BLOCK), KEY_BLOCK)
        dk, dv = dk_acc[keys].astype(BF), dv_acc[keys].astype(BF)
        half = size // 2
        dkv_ref[keys, :size] = jnp.concatenate([dk[:, :half], dv[:, :half]], axis=1)
        dkv_ref[keys, size:] = jnp.concatenate([dk[:, half:], dv[:, half:]], axis=1)


def fold_kernel(
    batches, part_ref, own_ref, core_got, x_first, x_second, y_first, y_second, held, send_sem, recv_sem
):
    rows, size = own_ref.shape
    half = rows // 2
    others = batches // 2
    head = lax.axis_index("head")
    batch = lax.axis_index("batch")
    across, core, low = batch // 2, lax.rem(batch, 2), lax.rem(head, 2)
    twin = (across * 2 + 1 - core, head)
    mate = (batch, head + 1 - 2 * low)
    spots = [lax.rem(across + hop, others) for hop in range(others)]
    peers = [(spot * 2 + core, head) for spot in spots]
    greet((twin, mate, *peers[1:]))
    sems = (send_sem, recv_sem)
    slot = 0
    copies = []
    mine = pl.ds(pl.multiple_of(low * size, size), size)
    given = pl.ds(pl.multiple_of((1 - low) * size, size), size)
    top, bottom = pl.ds(0, half), pl.ds(half, half)

    def block(at, side):
        return pl.ds(pl.multiple_of((2 * at + side) * rows, rows), rows)

    def go(source, target, device):
        nonlocal slot
        copy = send(source, target, sems, slot, device)
        slot += 1
        copies.append(copy)
        return copy

    order = list(range(1, others)) + [0]
    first = [go(part_ref.at[block(spots[hop], 1 - core)], core_got.at[spots[hop]], twin) for hop in order]
    tops, bottoms = [], []
    for copy, hop in zip(first, order):
        copy.wait_recv()
        spot = spots[hop]
        core_got[spot] = add_low(core_got[spot], part_ref[block(spot, core)])
        bottoms.append(go(core_got.at[spot, bottom, given], y_first.at[spot], mate))
        if hop:
            tops.append(go(core_got.at[spot, top], x_first.at[hop - 1], peers[hop]))
    total = core_got[across, top].astype(F32)
    for hop in range(1, others):
        tops[hop - 1].wait_recv()
        total = total + x_first[hop - 1].astype(F32)
    held[...] = total.astype(BF)
    last = go(held.at[:, given], y_second, mate)
    ends = []
    for copy, hop in zip(bottoms, order):
        copy.wait_recv()
        spot = spots[hop]
        y_first[spot] = add_low(y_first[spot], core_got[spot, bottom, mine])
        if hop:
            ends.append(go(y_first.at[spot], x_second.at[hop - 1], peers[hop]))
    last.wait_recv()
    own_ref[top] = add_low(held[:, mine], y_second[...])
    total = y_first[across].astype(F32)
    for hop in range(1, others):
        ends[hop - 1].wait_recv()
        total = total + x_second[hop - 1].astype(F32)
    own_ref[bottom] = total.astype(BF)
    for copy in copies:
        copy.wait_send()


def fold(part, rows, collective_id):
    batches = lax.axis_size("batch")
    others = batches // 2
    size = part.shape[1] // 2
    half = rows // 2
    vmem = pl.BlockSpec(memory_space=pltpu.VMEM)
    sems = pltpu.SemaphoreType.DMA((4 * others,))
    return pl.pallas_call(
        functools.partial(fold_kernel, batches),
        out_shape=jax.ShapeDtypeStruct((rows, size), BF),
        in_specs=[vmem],
        out_specs=vmem,
        scratch_shapes=[
            pltpu.VMEM((others, rows, 2 * size), BF),
            pltpu.VMEM((others - 1, half, 2 * size), BF),
            pltpu.VMEM((others - 1, half, size), BF),
            pltpu.VMEM((others, half, size), BF),
            pltpu.VMEM((half, size), BF),
            pltpu.VMEM((half, 2 * size), BF),
            sems,
            sems,
        ],
        compiler_params=pltpu.CompilerParams(
            collective_id=collective_id, has_side_effects=True, vmem_limit_bytes=20 << 20
        ),
        name="fold",
    )(part)


def tail_kernel(
    count, batches, cat_ref, w_ref, x_ref, gain_ref, dh1_ref, second_ref,
    n1_ref, mixed_ref, low_ref, out_0,
    out_all, tok_all, gains_ref, wout_own, din_ref,
    part_ref, tok_ref, got, wout_got, gain_own, gain_got, gain_mid, gain_heads,
    din_s, din_got, din_x, wout_s, wout_twin, wout_x, wout_part,
    send_sem, recv_sem, local_sem,
):
    steps = count // 2
    rows, width = x_ref.shape
    depth = cat_ref.shape[1]
    tile = 256
    place, right, left = ring_setup(count)
    batch, head = lax.axis_index("batch"), lax.axis_index("head")
    others = [lax.rem(batch + hop, batches) for hop in range(1, batches)]
    members = [(batch, ring_head(lax.rem(place + hop, count), count)) for hop in range(1, count)]
    greet((*members, *[(other, head) for other in others]))
    sems = (send_sem, recv_sem)
    slot = 0
    copies = []

    def go(source, target, device):
        nonlocal slot
        copy = send(source, target, sems, slot, device)
        slot += 1
        copies.append(copy)
        return copy

    across, core = batch // 2, lax.rem(batch, 2)
    spots = [lax.rem(across + hop, batches // 2) for hop in range(batches // 2)]
    order = list(range(1, batches // 2)) + [0]
    twin = (across * 2 + 1 - core, head)

    def scatter_swap(view, held):
        return [go(view(2 * spots[hop] + 1 - core), held.at[spots[hop]], twin) for hop in order]

    def add_tiles(target, one, other):
        @pl.loop(0, target.shape[0] // 128)
        def _(at):
            lines = pl.ds(pl.multiple_of(at * 128, 128), 128)
            total = one[lines].astype(F32) + other[lines].astype(F32)
            target[lines] = total.astype(target.dtype)

    def scatter_cross(view, held, crossed, arriving):
        out = []
        for copy, hop in zip(arriving, order):
            copy.wait_recv()
            spot = spots[hop]
            add_tiles(held.at[spot], held.at[spot], view(2 * spot + core))
            if hop:
                out.append(go(held.at[spot], crossed.at[hop - 1], (spot * 2 + core, head)))
        return out

    def scatter_end(held, crossed, arriving, target):
        for hop, copy in enumerate(arriving):
            copy.wait_recv()
            last = hop == len(arriving) - 1
            add_tiles(target if last else held.at[across], held.at[across], crossed.at[hop])

    def wout_view(at):
        wide = wout_part.shape[1]
        return wout_s.at[:, pl.ds(pl.multiple_of(at * wide, wide), wide)]

    def din_view(at):
        tall = din_ref.shape[0]
        return din_s.at[pl.ds(pl.multiple_of(at * tall, tall), tall)]

    def span(owner, extent):
        return pl.ds(pl.multiple_of(lax.rem(owner + count, count) * extent, extent), extent)

    def compute(owner):
        here = span(owner, rows)
        values = cat_ref[here]

        @pl.loop(0, width // tile)
        def _(at):
            cols = pl.ds(pl.multiple_of(at * tile, tile), tile)
            part_ref[here, cols] = cols_inner(values, w_ref[cols, pl.ds(0, depth)]).astype(BF)

    def gather(own, whole, step, last):
        out = []
        for flow, chunk, device in ((0, place - step, right), (1, place + step, left)):
            if last:
                last[flow].wait_recv()
            target = whole.at[lax.rem(chunk + count, count)]
            source = target if step else own
            if step == steps - 1:
                cut = (slice(None), pl.ds(flow * (width // 2), width // 2))
                source, target = source.at[cut], target.at[cut]
            out.append(go(source, target, device))
        return out

    def reduce(parts, held, step, last):
        extent, side = held.shape[2], held.shape[3] // 2
        out = []
        for flow, owner, device in (
            (0, place + steps - step, right),
            (1, place - steps + step, left),
        ):
            have = pl.ds(flow * side, side)
            lack = pl.ds((1 - flow) * side, side)
            mine = parts.at[span(owner, extent)]
            if step == 0:
                out.append(go(mine.at[:, have], held.at[flow, 0, :, have], device))
                continue
            last[flow].wait_recv()
            if step == 1:
                held[flow, 0, :, have] = add_low(held[flow, 0, :, have], mine[:, have])
                held[flow, 0, :, lack] = mine[:, lack]
            else:
                held[flow, step - 1] = add_low(held[flow, step - 1], mine[...])
            out.append(go(held.at[flow, step - 1], held.at[flow, step], device))
        return out

    keep_out = pltpu.make_async_copy(out_0, out_all.at[place], local_sem.at[0])
    keep_out.start()
    compute(place + steps)
    sums = reduce(part_ref, got, 0, None)
    outs = gather(out_0, out_all, 0, None)

    @pl.loop(1, count)
    def _(hop):
        compute(place + steps + hop)

    @pl.loop(0, width // tile)
    def _(at):
        cols = pl.ds(pl.multiple_of(at * tile, tile), tile)
        wout_s[:, cols] = rows_inner(mixed_ref[...], low_ref[:, cols]).astype(BF)

    wouts = scatter_swap(wout_view, wout_twin)

    @pl.loop(0, width // tile)
    def _(at):
        cols = pl.ds(pl.multiple_of(at * tile, tile), tile)
        din_s[cols] = rows_inner(n1_ref[:, cols], cat_ref[...]).astype(BF)

    dins = scatter_swap(din_view, din_got)
    for step in range(1, steps):
        sums = reduce(part_ref, got, step, sums)
        outs = gather(out_0, out_all, step, outs)
        if step == 1:
            wouts = scatter_cross(wout_view, wout_twin, wout_x, wouts)
            dins = scatter_cross(din_view, din_got, din_x, dins)
    for copy in sums:
        copy.wait_recv()

    def tile_of(at):
        return pl.ds(pl.multiple_of(at * tile, tile), tile)

    def total(cols):
        return (
            part_ref[span(place, rows), cols].astype(F32)
            + got[0, steps - 1, :, cols].astype(F32)
            + got[1, steps - 1, :, cols].astype(F32)
        )

    def collect(at, state):
        squares, mean = state
        cols = tile_of(at)
        x = x_ref[:, cols].astype(F32)
        squares = squares + jnp.sum(x * x, axis=1, keepdims=True)
        return squares, mean + jnp.sum(gain_ref[:, cols] * total(cols) * x, axis=1, keepdims=True)

    zero = jnp.zeros((rows, 1), F32)
    squares, mean = lax.fori_loop(0, width // tile, collect, (zero, zero))
    scale = lax.rsqrt(squares / width + EPSILON)
    pull = scale * scale * scale * (mean / width)

    @pl.loop(0, width // tile)
    def _(at):
        cols = tile_of(at)
        x, dn1 = x_ref[:, cols].astype(F32), total(cols)
        gain_own[pl.ds(0, 1), cols] = jnp.sum(dn1 * x * scale, axis=0, keepdims=True)
        gain_own[pl.ds(1, 1), cols] = second_ref[:, cols]
        tok_ref[:, cols] = (dh1_ref[:, cols] + scale * (gain_ref[:, cols] * dn1) - x * pull).astype(BF)

    keep_tok = pltpu.make_async_copy(tok_ref, tok_all.at[place], local_sem.at[1])
    keep_tok.start()
    toks = gather(tok_ref, tok_all, 0, None)
    scatter_end(wout_twin, wout_x, wouts, wout_part)
    wsums = reduce(wout_part, wout_got, 0, None)
    scatter_end(din_got, din_x, dins, din_ref)
    wide = width // batches

    def slice_of(at):
        return pl.ds(pl.multiple_of(at * wide, wide), wide)

    gains = [
        go(gain_own.at[:, slice_of(other)], gain_got.at[hop], (other, head))
        for hop, other in enumerate(others)
    ]
    toks = gather(tok_ref, tok_all, 1, toks)
    wsums = reduce(wout_part, wout_got, 1, wsums)
    middle = gain_own[:, slice_of(batch)]
    for hop, copy in enumerate(gains):
        copy.wait_recv()
        middle = middle + gain_got[hop]
    gain_mid[...] = middle
    gain_heads[place] = middle
    gains = [go(gain_mid, gain_heads.at[place], member) for member in members]
    for step in range(2, steps):
        toks = gather(tok_ref, tok_all, step, toks)
        wsums = reduce(wout_part, wout_got, step, wsums)
    for copy in gains:
        copy.wait_recv()
    middle = gain_heads[0]
    for at in range(1, count):
        middle = middle + gain_heads[at]
    gains_ref[...] = middle
    for copy in (*wsums, *outs):
        copy.wait_recv()
    wout_own[...] = (
        wout_part[span(place, wout_own.shape[0])].astype(F32)
        + wout_got[0, steps - 1].astype(F32)
        + wout_got[1, steps - 1].astype(F32)
    )
    for copy in toks:
        copy.wait_recv()
    for copy in copies:
        copy.wait_send()
    keep_out.wait()
    keep_tok.wait()


def tail(d_cat, w_in, x_own, gain, d_resid, second, normed, mixed, low, out_own, collective_id):
    count = lax.axis_size("head")
    batches = lax.axis_size("batch")
    steps = count // 2
    rows, width = x_own.shape
    others = batches // 2
    size, wide = mixed.shape[1] // count, width // batches
    depth = d_cat.shape[1]
    vmem = pl.BlockSpec(memory_space=pltpu.VMEM)
    whole = jax.ShapeDtypeStruct((count, rows, width), BF)
    sems = pltpu.SemaphoreType.DMA((5 * count + 3 * batches,))
    gains = (2, width // batches)
    return pl.pallas_call(
        functools.partial(tail_kernel, count, batches),
        out_shape=[
            whole,
            whole,
            jax.ShapeDtypeStruct(gains, F32),
            jax.ShapeDtypeStruct((size, wide), F32),
            jax.ShapeDtypeStruct((wide, depth), F32),
        ],
        in_specs=[vmem] * 10,
        out_specs=[vmem] * 5,
        scratch_shapes=[
            pltpu.VMEM((count * rows, width), BF),
            pltpu.VMEM((rows, width), BF),
            pltpu.VMEM((2, steps, rows, width), BF),
            pltpu.VMEM((2, steps, size, wide), BF),
            pltpu.VMEM((2, width), F32),
            pltpu.VMEM((batches - 1, *gains), F32),
            pltpu.VMEM(gains, F32),
            pltpu.VMEM((count, *gains), F32),
            pltpu.VMEM((width, depth), BF),
            pltpu.VMEM((others, wide, depth), BF),
            pltpu.VMEM((others - 1, wide, depth), BF),
            pltpu.VMEM((count * size, width), BF),
            pltpu.VMEM((others, count * size, wide), BF),
            pltpu.VMEM((others - 1, count * size, wide), BF),
            pltpu.VMEM((count * size, wide), BF),
            sems,
            sems,
            pltpu.SemaphoreType.DMA((2,)),
        ],
        compiler_params=pltpu.CompilerParams(
            collective_id=collective_id, has_side_effects=True, vmem_limit_bytes=52 << 20
        ),
        cost_estimate=pl.CostEstimate(
            flops=2 * count * rows * width * d_cat.shape[1], bytes_accessed=400 << 20, transcendentals=0
        ),
        name="tail",
    )(d_cat, w_in, x_own, gain, d_resid, second, normed, mixed, low, out_own)


def local_call(kernel, scalars, arrays, outs, scratch, flops, name):
    vmem = pl.BlockSpec(memory_space=pltpu.VMEM)
    smem = pl.BlockSpec(memory_space=pltpu.SMEM)
    return pl.pallas_call(
        kernel,
        out_shape=outs,
        in_specs=[smem] * len(scalars) + [vmem] * len(arrays),
        out_specs=[vmem] * len(outs),
        scratch_shapes=scratch,
        compiler_params=pltpu.CompilerParams(vmem_limit_bytes=36 << 20),
        cost_estimate=pl.CostEstimate(flops=flops, bytes_accessed=8 << 20, transcendentals=0),
        name=name,
    )(*scalars, *arrays)


def ring_routes(count):
    spots = [ring_head(at, count) for at in range(count)]
    right = [(spots[at], spots[(at + 1) % count]) for at in range(count)]
    left = [(spots[at], spots[at - 1]) for at in range(count)]
    return right, left


def add_low(one, other):
    return (one.astype(F32) + other.astype(F32)).astype(BF)


def flow_steps(part, going, coming):
    count = lax.axis_size("head")
    place = ring_place(lax.axis_index("head"), count)
    right, left = ring_routes(count)
    rows = part.shape[0] // count
    steps = count // 2

    def mine(owner):
        return lax.dynamic_slice_in_dim(part, lax.rem(owner + count, count) * rows, rows, 0)

    for step in range(2, steps - 1):
        from_left = lax.ppermute(going, "head", right)
        from_right = lax.ppermute(coming, "head", left)
        going = add_low(from_left, mine(place + steps - 1 - step))
        coming = add_low(from_right, mine(place - steps + 1 + step))
        going, coming = yield going, coming
    from_left = lax.ppermute(going, "head", right)
    from_right = lax.ppermute(coming, "head", left)
    yield mine(place).astype(F32) + from_left.astype(F32) + from_right.astype(F32)


def matmul(left, right):
    return jnp.dot(left, right, preferred_element_type=F32)


def rows_inner(left, right):
    return lax.dot_general(left, right, (((0,), (0,)), ((), ())), preferred_element_type=F32)


def cols_inner(left, right):
    return lax.dot_general(left, right, (((1,), (1,)), ((), ())), preferred_element_type=F32)


def rms_scale(values):
    return lax.rsqrt(jnp.mean(values * values, axis=1, keepdims=True) + EPSILON)


def per_device(
    tokens,
    segment_ids,
    norm1_gain,
    w_query,
    w_key,
    w_value,
    w_gate,
    w_out,
    norm2_gain,
    w_mlp_gate,
    w_mlp_up,
    w_down,
    out_grad,
):
    heads = lax.axis_size("head")
    batches = lax.axis_size("batch")
    row_count, width = tokens.shape
    head_size = w_query.shape[1]
    half = w_key.shape[1]
    chunk = row_count // heads
    me = ring_place(lax.axis_index("head"), heads)
    scale_factor = 1.0 / math.sqrt(head_size)

    w_shard = jnp.concatenate([w_query, w_gate, w_key, w_value], axis=1)
    gains = jnp.concatenate([norm1_gain, norm2_gain]).reshape(-1, 128).astype(F32)
    normed_one, queries, gate_logit, kv_all, w_in, out_full, gains, seg_all, down_full = entry(
        tokens, w_shard, w_out, gains, segment_ids.reshape(-1, 128), w_down, 1
    )
    gains, w_mlp_gate, w_mlp_up = lax.optimization_barrier((gains, w_mlp_gate, w_mlp_up))
    seg_all = seg_all.reshape(-1)
    gains = gains.reshape(batches, 2, -1).transpose(1, 0, 2).reshape(2, width)
    gain_one, gain_two = gains[0], gains[1]
    mgate_full = lax.all_gather(w_mlp_gate, "batch", axis=0, tiled=True)
    mup_full = lax.all_gather(w_mlp_up, "batch", axis=0, tiled=True)

    base = lax.axis_index("batch") * row_count
    ids = jnp.arange(DOCUMENTS, dtype=jnp.int32)
    below = jnp.sum((seg_all[None, :] < ids[:, None]).astype(jnp.int32), axis=1)
    starts = jnp.sum(jnp.where(segment_ids[None, :] == ids[:, None], below[:, None], 0), axis=0)
    scalars = (starts, base.reshape(1))
    pair_flops = 4 * row_count * kv_all.shape[0] * head_size
    attended, mixed, lse = local_call(
        functools.partial(attend_kernel, scale_factor),
        scalars,
        (queries, kv_all, starts[None], gate_logit),
        [
            jax.ShapeDtypeStruct((row_count, head_size), F32),
            jax.ShapeDtypeStruct((row_count, head_size), BF),
            jax.ShapeDtypeStruct((1, row_count), F32),
        ],
        [],
        pair_flops,
        "attend",
    )
    (mixed_all,) = spread([mixed], (("head", "cols"),), 2)
    (
        mlp_part, d_mlp, d_down, resid_own, d_resid, d_resid_low, d_gain_two, d_mixed, going, coming,
    ) = mlp_back(
        tokens, mixed_all, out_grad, gain_two[None], out_full, mgate_full, mup_full, down_full, 3
    )
    hold = lax.optimization_barrier
    mixed_own = lax.dynamic_slice_in_dim(mixed_all, me * chunk, chunk, 0)
    flow = flow_steps(mlp_part, going, coming)
    state = next(flow)

    d_queries, d_gate_logit, d_kv_all = local_call(
        functools.partial(attend_back_kernel, scale_factor),
        scalars,
        (queries, kv_all, starts[None], gate_logit, attended, d_mixed, lse),
        [
            jax.ShapeDtypeStruct((row_count, head_size), BF),
            jax.ShapeDtypeStruct((row_count, head_size), BF),
            jax.ShapeDtypeStruct(kv_all.shape, BF),
        ],
        [pltpu.VMEM((kv_all.shape[0], head_size), F32)] * 2,
        5 * pair_flops // 2,
        "attend_back",
    )
    d_kv_all, state = hold((d_kv_all, state))
    while isinstance(state, tuple):
        state = flow.send(state)
    d_kv = fold(d_kv_all, row_count, 4)
    d_kv, state, d_down, d_mlp = hold((d_kv, state, d_down, d_mlp))
    out_own = (resid_own + state).astype(BF)
    d_down = lax.psum_scatter(d_down, "batch", scatter_dimension=1, tiled=True)
    d_mlp = lax.psum_scatter(d_mlp, "batch", scatter_dimension=0, tiled=True)
    d_cat = jnp.concatenate([d_queries, d_gate_logit, d_kv], axis=1)
    inputs_own = lax.dynamic_slice_in_dim(tokens, me * chunk, chunk, 0)
    output, d_tokens, d_gains, d_out, d_in = tail(
        d_cat, w_in, inputs_own, gain_one[None], d_resid, d_gain_two, normed_one, mixed_own,
        d_resid_low, out_own, 5,
    )
    d_tokens, d_mlp, d_down = hold((d_tokens, d_mlp, d_down))
    d_mlp, d_down = d_mlp.astype(F32), d_down.astype(F32)
    output = output.reshape(row_count, width)
    d_tokens = d_tokens.reshape(row_count, width)
    hidden_own = w_mlp_gate.shape[1]
    return (
        output,
        d_tokens,
        d_gains[0],
        d_in[:, :head_size],
        d_in[:, 2 * head_size : 2 * head_size + half],
        d_in[:, 2 * head_size + half :],
        d_in[:, head_size : 2 * head_size],
        d_out,
        d_gains[1],
        d_mlp[:, :hidden_own],
        d_mlp[:, hidden_own:],
        d_down,
    )


def solution(mesh):
    return jax.shard_map(
        per_device,
        mesh=mesh,
        in_specs=(
            P("batch", None),
            P("batch"),
            P("batch"),
            P("batch", "head"),
            P("batch", "head"),
            P("batch", "head"),
            P("batch", "head"),
            P("head", "batch"),
            P("batch"),
            P("batch", "head"),
            P("batch", "head"),
            P("head", "batch"),
            P("batch", None),
        ),
        out_specs=(
            P("batch", None),
            P("batch", None),
            P("batch"),
            P("batch", "head"),
            P("batch", "head"),
            P("batch", "head"),
            P("batch", "head"),
            P("head", "batch"),
            P("batch"),
            P("batch", "head"),
            P("batch", "head"),
            P("head", "batch"),
        ),
        check_vma=False,
    )
```

```python
import functools
import math

import jax
import jax.numpy as jnp
from jax import lax
from jax.experimental import pallas as pl
from jax.experimental.pallas import tpu as pltpu
from jax.sharding import PartitionSpec as P

EPSILON = 1e-06
MASKED = -1e30
DOCUMENTS = 7
BF = jnp.bfloat16
F32 = jnp.float32


MESH = pl.DeviceIdType.MESH
VMEM_LIMIT = 60 << 20


def ring_place(head, count):
    high, low = head // 2, head % 2
    return (1 - low) * high + low * (count - 1 - high)


def ring_head(place, count):
    low = place // (count // 2)
    high = (1 - low) * place + low * (count - 1 - place)
    return 2 * high + low


def ring_setup(count):
    batch = lax.axis_index("batch")
    place = ring_place(lax.axis_index("head"), count)
    right = (batch, ring_head(lax.rem(place + 1, count), count))
    left = (batch, ring_head(lax.rem(place + count - 1, count), count))
    return place, right, left


def greet(devices):
    barrier = pltpu.get_barrier_semaphore()
    for device in devices:
        pl.semaphore_signal(barrier, inc=1, device_id=device, device_id_type=MESH)
    pl.semaphore_wait(barrier, len(devices))


def send(source, target, sems, slot, device):
    copy = pltpu.make_async_remote_copy(
        src_ref=source,
        dst_ref=target,
        send_sem=sems[0].at[slot],
        recv_sem=sems[1].at[slot],
        device_id=device,
        device_id_type=MESH,
    )
    copy.start()
    return copy


def half_of(extent, flow):
    if extent[1] % 256:
        return (pl.ds(flow * (extent[0] // 2), extent[0] // 2), slice(None))
    return (slice(None), pl.ds(flow * (extent[1] // 2), extent[1] // 2))


def place_of(whole, own, chunk, form):
    rows, wide = own.shape[-2:]
    if form == "lead":
        return whole.at[chunk]
    if form == "rows":
        return whole.at[pl.ds(pl.multiple_of(chunk * rows, rows), rows)]
    return whole.at[:, pl.ds(pl.multiple_of(chunk * wide, wide), wide)]


def spread_kernel(count, batches, plans, *refs):
    steps = count // 2
    arrays = len(plans)
    own_refs, all_refs = refs[:arrays], refs[arrays : 2 * arrays]
    send_sem, recv_sem, local_sem = refs[2 * arrays :]
    place, right, left = ring_setup(count)
    head = lax.axis_index("head")
    batch = lax.axis_index("batch")
    across, core = batch // 2, lax.rem(batch, 2)
    others = batches // 2
    twin = (across * 2 + 1 - core, head)
    peers = [(lax.rem(across + hop, others) * 2 + core, head) for hop in range(1, others)]
    ring = any(axis == "head" for axis, _ in plans)
    grid = any(axis == "batch" for axis, _ in plans)
    greet((right, left) * ring + (twin, *peers) * grid)
    sems = (send_sem, recv_sem)
    slot = 0
    waiting, arriving, local = [], [], []

    def go(source, target, device):
        nonlocal slot
        copy = send(source, target, sems, slot, device)
        slot += 1
        waiting.append(copy)
        return copy

    stages = []
    for index, (axis, form) in enumerate(plans):
        own, whole = own_refs[index], all_refs[index]
        spot = place if axis == "head" else batch
        copy = pltpu.make_async_copy(own, place_of(whole, own, spot, form), local_sem.at[index])
        copy.start()
        local.append(copy)
        if axis == "batch":
            stages.append(index)
    onward = []

    def stage():
        for copy, block in onward:
            copy.wait_recv()
            arriving.append(go(block, block, twin))
        onward.clear()
        if stages:
            index = stages.pop(0)
            own, whole, form = own_refs[index], all_refs[index], plans[index][1]
            mine = place_of(whole, own, batch, form)
            for hop, peer in enumerate(peers, 1):
                source = lax.rem(across + others - hop, others) * 2 + core
                onward.append((go(own, mine, peer), place_of(whole, own, source, form)))
            arriving.append(go(own, mine, twin))

    stage()
    copies = [None] * (2 * arrays)
    for step in range(steps):
        for index, (axis, form) in enumerate(plans):
            if axis != "head":
                continue
            own = own_refs[index]
            for flow, chunk, device in ((0, place - step, right), (1, place + step, left)):
                at = 2 * index + flow
                if step:
                    copies[at].wait_recv()
                chunk = lax.rem(chunk + count, count)
                target = place_of(all_refs[index], own, chunk, form)
                source = target if step else own
                if step == steps - 1:
                    part = half_of(own.shape, flow)
                    source = source.at[part]
                    target = target.at[part]
                copies[at] = go(source, target, device)
        if step == steps // 2:
            stage()
    while stages or onward:
        stage()
    for copy in copies:
        if copy is not None:
            arriving.append(copy)
    for copy in arriving:
        copy.wait_recv()
    for copy in waiting:
        copy.wait_send()
    for copy in local:
        copy.wait()


def spread(arrays, plans, collective_id):
    count = lax.axis_size("head")
    batches = lax.axis_size("batch")
    shapes = []
    slots = 0
    for array, (axis, form) in zip(arrays, plans):
        many = count if axis == "head" else batches
        slots += count if axis == "head" else batches - 1
        if form == "lead":
            shapes.append((many, *array.shape))
        elif form == "rows":
            shapes.append((many * array.shape[0], array.shape[1]))
        else:
            shapes.append((array.shape[0], many * array.shape[1]))
    hbm = pl.BlockSpec(memory_space=pl.ANY)
    return pl.pallas_call(
        functools.partial(spread_kernel, count, batches, plans),
        out_shape=[jax.ShapeDtypeStruct(shape, a.dtype) for shape, a in zip(shapes, arrays)],
        in_specs=[pl.BlockSpec(memory_space=pltpu.VMEM)] * len(arrays),
        out_specs=[hbm] * len(arrays),
        scratch_shapes=[
            pltpu.SemaphoreType.DMA((slots,)),
            pltpu.SemaphoreType.DMA((slots,)),
            pltpu.SemaphoreType.DMA((len(arrays),)),
        ],
        compiler_params=pltpu.CompilerParams(
            collective_id=collective_id, has_side_effects=True, vmem_limit_bytes=8 << 20
        ),
        name=f"spread_{collective_id}",
    )(*arrays)


def mlp_kernel(
    count, x_hbm, a_hbm, dy_hbm, gain_ref, out_w, gate_w, up_w, down_w,
    mlp_hbm, dmlp_hbm, ddown_hbm, h1_ref, dh1_ref, low_ref, dgain_ref, da_ref, ahead_ref, behind_ref,
    x_s, a_s, mlp_s, h1_s, dy_all, n2_all, hid_all, grad_all, dmlp_s, ddown_s, da_part,
    mlp_far, mlp_next, mlp_got, right_part, left_part, right_got, left_got,
    in_sem, out_sem, grad_sem, send_sem, recv_sem, da_send, da_recv, far_send, far_recv,
):
    steps = count // 2
    rows = x_hbm.shape[0] // count
    width = x_hbm.shape[1]
    hidden = gate_w.shape[1]
    side = width // 2
    tile = 256
    broad = 1024
    inner = 256 if hidden % 256 == 0 else 128
    size = da_ref.shape[1]
    place, right, left = ring_setup(count)

    def member(hop):
        spot = lax.rem(place + hop, count)
        return spot, (lax.axis_index("batch"), ring_head(spot, count))

    greet([member(hop)[1] for hop in range(1, count)])

    def owners(group):
        first = jnp.where(group == 0, 1, 0)
        one = lax.rem(place + steps - group, count)
        two = lax.rem(place - steps + group + first * steps + count, count)
        return one, two

    def span(owner):
        return pl.ds(pl.multiple_of(owner * rows, rows), rows)

    def tile_of(at, extent=tile):
        return pl.ds(pl.multiple_of(at * extent, extent), extent)

    def loads(group, slot):
        return [
            pltpu.make_async_copy(
                source.at[span(owner)],
                target.at[pl.ds(at * rows, rows)],
                in_sem.at[slot, 2 * index + at],
            )
            for index, (source, target) in enumerate(
                ((x_hbm, x_s.at[slot]), (a_hbm, a_s.at[slot]), (dy_hbm, dy_all.at[group]))
            )
            for at, owner in enumerate(owners(group))
        ]

    def stores(group, slot):
        return [
            pltpu.make_async_copy(
                mlp_s.at[slot, pl.ds(at * rows, rows)], mlp_hbm.at[span(owner)], out_sem.at[slot, at]
            )
            for at, owner in enumerate(owners(group))
        ]

    def passing(source, target, sems, slot, device):
        return pltpu.make_async_remote_copy(
            src_ref=source,
            dst_ref=target,
            send_sem=sems[0].at[slot],
            recv_sem=sems[1].at[slot],
            device_id=device,
            device_id_type=MESH,
        )

    ring_sems, far_sems = (send_sem, recv_sem), (far_send, far_recv)
    ahead, behind = pl.ds(0, side), pl.ds(side, side)

    def first_copies():
        return (
            passing(right_part.at[0, :, ahead], right_got.at[0, :, ahead], ring_sems, 0, right),
            passing(right_part.at[0, :, behind], left_got.at[0, :, behind], ring_sems, steps, left),
        )

    def later_copies(step):
        return (
            passing(right_got.at[step - 1], right_got.at[step], ring_sems, step, right),
            passing(left_got.at[step - 1], left_got.at[step], ring_sems, steps + step, left),
        )

    for copy in loads(0, 0):
        copy.start()

    @pl.loop(0, steps)
    def _(group):
        slot = lax.rem(group, 2)
        for copy in loads(group, slot):
            copy.wait()

        @pl.when(group + 1 < steps)
        def _():
            for copy in loads(group + 1, 1 - slot):
                copy.start()

        @pl.when(group >= 2)
        def _():
            for copy in stores(group - 2, slot):
                copy.wait()

        mixed = a_s[slot]

        def residual(at, total):
            cols = tile_of(at, broad)
            values = x_s[slot, :, cols].astype(F32) + matmul(mixed, out_w[:, cols])
            h1_s[:, cols] = values
            return total + jnp.sum(values * values, axis=1, keepdims=True)

        total = lax.fori_loop(0, width // broad, residual, jnp.zeros((2 * rows, 1), F32))
        scale = lax.rsqrt(total / width + EPSILON)

        @pl.when(group == 0)
        def _():
            h1_ref[...] = h1_s[pl.ds(rows, rows)]

        @pl.loop(0, width // tile)
        def _(at):
            cols = tile_of(at)
            n2_all[group, :, cols] = (h1_s[:, cols] * scale * gain_ref[:, cols]).astype(BF)

        normed = n2_all[group]
        dy = dy_all[group]

        @pl.loop(0, hidden // inner)
        def _(at):
            cols = tile_of(at, inner)
            cols_up = pl.ds(pl.multiple_of(hidden + at * inner, inner), inner)
            gate = matmul(normed, gate_w[:, cols])
            up = matmul(normed, up_w[:, cols])
            d_hidden = cols_inner(dy, down_w[cols])
            sig = jax.nn.sigmoid(gate)
            silu = gate * sig
            hid_all[group, :, cols] = (silu * up).astype(BF)
            grad_all[group, :, cols] = (d_hidden * up * sig * (1.0 + gate * (1.0 - sig))).astype(BF)
            grad_all[group, :, cols_up] = (d_hidden * silu).astype(BF)

        hid = hid_all[group]
        d_gate = grad_all[group, :, :hidden]
        d_up = grad_all[group, :, hidden:]
        half = jnp.minimum(group, 1)

        @pl.loop(0, width // broad)
        def _(at):
            cols = tile_of(at, broad)
            part = (cols_inner(d_gate, gate_w[cols]) + cols_inner(d_up, up_w[cols])).astype(BF)
            right_part[half, :, cols] = part[:rows]
            left_part[half, :, cols] = part[rows:]
            mlp_s[slot, :, cols] = matmul(hid, down_w[:, cols]).astype(BF)

        for copy in stores(group, slot):
            copy.start()

        @pl.when(group == 0)
        def _():
            mlp_far[...] = mlp_s[slot, pl.ds(0, rows)]
            for copy in first_copies():
                copy.start()

        @pl.when(group == 1)
        def _():
            mlp_next[0] = mlp_s[slot, pl.ds(0, rows)]
            mlp_next[1] = mlp_s[slot, pl.ds(rows, rows)]
            one, two = first_copies()
            one.wait_recv()
            right_got[0, :, ahead] = add_low(right_part[1, :, ahead], right_got[0, :, ahead])
            right_got[0, :, behind] = right_part[1, :, behind]
            two.wait_recv()
            left_got[0, :, behind] = add_low(left_part[1, :, behind], left_got[0, :, behind])
            left_got[0, :, ahead] = left_part[1, :, ahead]

        @pl.when(group == 2)
        def _():
            ahead_ref[...] = mlp_s[slot, pl.ds(0, rows)]
            behind_ref[...] = mlp_s[slot, pl.ds(rows, rows)]

        @pl.when(group >= 2)
        def _():
            one, two = later_copies(group - 1)
            one.wait_recv()
            right_got[group - 1] = add_low(right_part[1], right_got[group - 1])
            two.wait_recv()
            left_got[group - 1] = add_low(left_part[1], left_got[group - 1])

        @pl.when(group >= 1)
        def _():
            for copy in later_copies(group):
                copy.start()

    far_copies = [
        passing(mlp_far.at[:, ahead], mlp_got.at[0, :, ahead], far_sems, 0, right),
        passing(mlp_far.at[:, behind], mlp_got.at[1, :, behind], far_sems, 1, left),
    ]
    for copy in far_copies:
        copy.start()

    every = steps * 2 * rows

    def dmlp_copy(at, slot):
        return pltpu.make_async_copy(
            dmlp_s.at[slot], dmlp_hbm.at[tile_of(at // 2), tile_of(lax.rem(at, 2), hidden)], grad_sem.at[slot]
        )

    mlp_tiles = 2 * (width // tile)

    @pl.loop(0, mlp_tiles)
    def _(at):
        slot = lax.rem(at, 2)

        @pl.when(at >= 2)
        def _():
            dmlp_copy(at - 2, slot).wait()

        normed = n2_all[:, :, tile_of(at // 2)].reshape(every, tile)
        grads = grad_all[:, :, tile_of(lax.rem(at, 2), hidden)].reshape(every, hidden)
        dmlp_s[slot] = rows_inner(normed, grads).astype(BF)
        dmlp_copy(at, slot).start()

    wide = 512
    across = width // wide

    def ddown_copy(at, slot):
        return pltpu.make_async_copy(
            ddown_s.at[slot],
            ddown_hbm.at[tile_of(at // across, inner), tile_of(lax.rem(at, across), wide)],
            grad_sem.at[2 + slot],
        )

    down_tiles = across * (hidden // inner)

    @pl.loop(0, down_tiles)
    def _(at):
        slot = lax.rem(at, 2)

        @pl.when(at >= 2)
        def _():
            ddown_copy(at - 2, slot).wait()

        hid = hid_all[:, :, tile_of(at // across, inner)].reshape(every, inner)
        dy = dy_all[:, :, tile_of(lax.rem(at, across), wide)].reshape(every, wide)
        ddown_s[slot] = rows_inner(hid, dy).astype(BF)
        ddown_copy(at, slot).start()

    for copy in later_copies(steps - 1):
        copy.wait_recv()
    for flow, have, lack in ((0, ahead, behind), (1, behind, ahead)):
        far_copies[flow].wait_recv()
        mlp_got[flow, :, have] = add_low(mlp_got[flow, :, have], mlp_next[flow, :, have])
        mlp_got[flow, :, lack] = mlp_next[flow, :, lack]
    next_copies = [
        passing(mlp_got.at[0], mlp_got.at[2], far_sems, 2, right),
        passing(mlp_got.at[1], mlp_got.at[3], far_sems, 3, left),
    ]
    for copy in next_copies:
        copy.start()

    def collect(at, state):
        squares, mean = state
        cols = tile_of(at)
        dn2 = (
            left_part[0, :, cols].astype(F32)
            + right_got[steps - 1, :, cols].astype(F32)
            + left_got[steps - 1, :, cols].astype(F32)
        )
        dh1_ref[:, cols] = dn2
        h1 = h1_ref[:, cols]
        squares = squares + jnp.sum(h1 * h1, axis=1, keepdims=True)
        return squares, mean + jnp.sum(gain_ref[:, cols] * dn2 * h1, axis=1, keepdims=True)

    zero = jnp.zeros((rows, 1), F32)
    squares, mean = lax.fori_loop(0, width // tile, collect, (zero, zero))
    scale_own = lax.rsqrt(squares / width + EPSILON)
    pull = scale_own * scale_own * scale_own * (mean / width)

    @pl.loop(0, width // tile)
    def _(at):
        cols = tile_of(at)
        dn2, h1 = dh1_ref[:, cols], h1_ref[:, cols]
        dgain_ref[:, cols] = jnp.sum(dn2 * h1 * scale_own, axis=0, keepdims=True)
        dy = dy_all[0, pl.ds(rows, rows), cols].astype(F32)
        d_resid = dy + scale_own * (gain_ref[:, cols] * dn2) - h1 * pull
        dh1_ref[:, cols] = d_resid
        low_ref[:, cols] = d_resid.astype(BF)

    def da_copy(hop):
        return passing(
            da_part.at[hop], da_ref.at[span(place)], (da_send, da_recv), hop, member(hop)[1]
        )

    low = low_ref[...]

    @pl.loop(1, count)
    def _(hop):
        spot = member(hop)[0]
        da_part[hop] = cols_inner(low, out_w[tile_of(spot, size)]).astype(BF)
        da_copy(hop).start()

    da_ref[span(place)] = cols_inner(low, out_w[tile_of(place, size)]).astype(BF)

    @pl.loop(1, count)
    def _(hop):
        da_copy(hop).wait_recv()
        da_copy(hop).wait_send()

    for flow, held in ((0, ahead_ref), (1, behind_ref)):
        next_copies[flow].wait_recv()
        held[...] = add_low(held[...], mlp_got[2 + flow])
    for copy in (*far_copies, *next_copies, *first_copies()):
        copy.wait_send()
    for step in range(1, steps):
        for copy in later_copies(step):
            copy.wait_send()
    for group in range(steps - 2, steps):
        for copy in stores(group, group % 2):
            copy.wait()
    for at in range(2):
        dmlp_copy(mlp_tiles - 2 + at, (mlp_tiles + at) % 2).wait()
        ddown_copy(down_tiles - 2 + at, (down_tiles + at) % 2).wait()


def mlp_back(tokens, mixed, dy, gain, out_w, gate_w, up_w, down_w, collective_id):
    count = lax.axis_size("head")
    total, width = tokens.shape
    hidden = gate_w.shape[1]
    rows, steps = total // count, count // 2
    size = mixed.shape[1] // count
    inner = 256 if hidden % 256 == 0 else 128
    vmem = pl.BlockSpec(memory_space=pltpu.VMEM)
    hbm = pl.BlockSpec(memory_space=pl.ANY)

    def slots(many, tall, wide, dtype=BF):
        return pltpu.VMEM((many, tall, wide), dtype)

    def shape(*extent, dtype=BF):
        return jax.ShapeDtypeStruct(extent, dtype)

    dma = pltpu.SemaphoreType.DMA
    flops = 2 * total * width * (mixed.shape[1] + 9 * hidden)
    return pl.pallas_call(
        functools.partial(mlp_kernel, count),
        out_shape=[
            shape(total, width), shape(width, 2 * hidden), shape(hidden, width),
            shape(rows, width, dtype=F32), shape(rows, width, dtype=F32), shape(rows, width),
            shape(1, width, dtype=F32), shape(total, size), shape(rows, width), shape(rows, width),
        ],
        in_specs=[hbm] * 3 + [vmem] * 5,
        out_specs=[hbm] * 3 + [vmem] * 7,
        scratch_shapes=[
            slots(2, 2 * rows, width), slots(2, 2 * rows, mixed.shape[1]), slots(2, 2 * rows, width),
            pltpu.VMEM((2 * rows, width), F32),
            slots(steps, 2 * rows, width), slots(steps, 2 * rows, width),
            slots(steps, 2 * rows, hidden), slots(steps, 2 * rows, 2 * hidden),
            slots(2, 256, hidden), slots(2, inner, 512), slots(count, rows, size),
            pltpu.VMEM((rows, width), BF), slots(2, rows, width), slots(4, rows, width),
            slots(2, rows, width), slots(2, rows, width),
            slots(steps, rows, width), slots(steps, rows, width),
            dma((2, 6)), dma((2, 2)), dma((4,)), dma((count,)), dma((count,)),
            dma((count,)), dma((count,)), dma((4,)), dma((4,)),
        ],
        compiler_params=pltpu.CompilerParams(
            collective_id=collective_id, has_side_effects=True, vmem_limit_bytes=VMEM_LIMIT
        ),
        cost_estimate=pl.CostEstimate(flops=flops, bytes_accessed=40 << 20, transcendentals=0),
        name="mlp_back",
    )(tokens, mixed, dy, gain, out_w, gate_w, up_w, down_w)


def entry_kernel(
    count, batches, x_ref, w_ref, out_ref, gain_ref, seg_ref,
    n1_ref, q_ref, logit_ref, kv_ref, w_all, out_all, gain_all, seg_all,
    send_sem, recv_sem, local_sem,
):
    steps = count // 2
    others = batches // 2
    rows, width = x_ref.shape
    depth = w_ref.shape[0]
    size, wide = out_ref.shape
    block = 256
    place, right, left = ring_setup(count)
    head = lax.axis_index("head")
    batch = lax.axis_index("batch")
    across, core, low = batch // 2, lax.rem(batch, 2), lax.rem(head, 2)
    twin = (across * 2 + 1 - core, head)
    mate = (batch, head + 1 - 2 * low)
    spots = [lax.rem(across + hop, others) for hop in range(others)]
    backs = [lax.rem(across + others - hop, others) for hop in range(others)]
    peers = [(spot * 2 + core, head) for spot in spots]
    far_peers = [(spot * 2 + 1 - core, head) for spot in spots]
    greet((twin, mate, right, left, *peers[1:], *far_peers[1:]))
    sems = (send_sem, recv_sem)
    slot = 0
    copies = []

    def go(source, target, device):
        nonlocal slot
        copy = send(source, target, sems, slot, device)
        slot += 1
        copies.append(copy)
        return copy

    def part(at, extent):
        return pl.ds(pl.multiple_of(at * extent, extent), extent)

    def both(view, own):
        out = [go(own, view(batch), peers[hop]) for hop in range(1, others)]
        return out, [go(own, view(batch), twin)]

    def pass_on(view, arrived):
        out = []
        for hop in range(1, others):
            arrived[hop - 1].wait_recv()
            there = view(backs[hop] * 2 + core)
            out.append(go(there, there, twin))
        return out

    local = []

    def stay(source, target):
        copy = pltpu.make_async_copy(source, target, local_sem.at[len(local)])
        copy.start()
        local.append(copy)

    def main_view(at):
        return w_all.at[part(at, depth), pl.ds(0, 3 * size)]

    def mate_view(at):
        return w_all.at[part(at, depth), pl.ds(3 * size, size)]

    def out_view(chunk, at):
        return out_all.at[part(chunk, size), part(at, wide)]

    small = []
    for own, whole in ((gain_ref, gain_all), (seg_ref, seg_all)):
        for device in (twin, *peers[1:], *far_peers[1:]):
            small.append(go(own, whole.at[batch], device))
        stay(own, whole.at[batch])
    from_mate = go(w_ref.at[:, pl.ds(2 * size, size)], mate_view(batch), mate)
    main_out, main_twin = both(main_view, w_ref)
    stay(w_ref, main_view(batch))
    out_peers = [go(out_ref, out_view(place, batch), peers[hop]) for hop in range(1, others)]
    stay(out_ref, out_view(place, batch))
    flows = [[None, None] for _ in range(others)]

    def ring(step):
        for hop in range(others):
            lane = spots[0] if hop == 0 else backs[hop]
            at = lane * 2 + core
            if step == 0 and hop:
                out_peers[hop - 1].wait_recv()
            for flow, chunk, device in ((0, place - step, right), (1, place + step, left)):
                if step:
                    flows[hop][flow].wait_recv()
                target = out_view(lax.rem(chunk + count, count), at)
                source = out_ref if step == 0 and hop == 0 else target
                if step == steps - 1:
                    cut = (pl.ds(flow * (size // 2), size // 2), slice(None))
                    source, target = source.at[cut], target.at[cut]
                flows[hop][flow] = go(source, target, device)

    for copy in small:
        copy.wait_recv()
    for copy in local[:2]:
        copy.wait()

    def normalize(at):
        here = part(at, block)

        def squares(tile, total):
            values = x_ref[here, part(tile, 256)].astype(F32)
            return total + jnp.sum(values * values, axis=1, keepdims=True)

        total = lax.fori_loop(0, width // 256, squares, jnp.zeros((block, 1), F32))
        scale = lax.rsqrt(total / width + EPSILON)

        @pl.loop(0, batches)
        def _(owner):
            for tile in range(depth // 128):
                cols = pl.ds(pl.multiple_of(owner * depth + tile * 128, 128), 128)
                values = x_ref[here, cols].astype(F32) * scale
                n1_ref[here, cols] = (values * gain_all[owner, pl.ds(tile, 1)]).astype(BF)

    blocks = rows // block
    middle = blocks // 2

    @pl.loop(0, middle)
    def _(at):
        normalize(at)

    from_mate.wait_recv()
    mate_out, mate_twin = both(mate_view, mate_view(batch))
    ring(0)

    @pl.loop(middle, blocks)
    def _(at):
        normalize(at)

    main_passed = pass_on(main_view, main_out)
    mate_passed = pass_on(mate_view, mate_out)
    for copy in (*main_twin, *mate_twin, *main_passed, *mate_passed):
        copy.wait_recv()
    for copy in local[2:]:
        copy.wait()

    def kv_view(at):
        return kv_ref.at[part(at, rows)]

    @pl.loop(0, blocks)
    def _(at):
        here = part(at, block)
        values = matmul(n1_ref[here], w_all[:, pl.ds(2 * size, 2 * size)])
        one, two = values[:, :size], values[:, size:]
        first = jnp.where(low == 0, one, two).astype(BF)
        second = jnp.where(low == 0, two, one).astype(BF)
        half = size // 2
        there = pl.ds(pl.multiple_of(batch * rows + at * block, block), block)
        kv_ref[there, pl.ds(0, size)] = jnp.concatenate([first[:, :half], second[:, :half]], 1)
        kv_ref[there, pl.ds(size, size)] = jnp.concatenate([first[:, half:], second[:, half:]], 1)

    kv_out, kv_twin = both(kv_view, kv_view(batch))
    ring(1)

    @pl.loop(0, blocks)
    def _(at):
        here = part(at, block)
        values = matmul(n1_ref[here], w_all[:, pl.ds(0, 2 * size)])
        q_ref[here] = values[:, :size].astype(BF)
        logit_ref[here] = values[:, size:]

    for step in range(2, steps):
        ring(step)
    kv_passed = pass_on(kv_view, kv_out)
    for pair in flows:
        for copy in pair:
            copy.wait_recv()
    swaps = []
    for hop in range(others):
        there = out_all.at[:, part(spots[hop] * 2 + core, wide)]
        swaps.append(go(there, there, twin))
    for copy in (*kv_twin, *kv_passed, *swaps):
        copy.wait_recv()
    for copy in copies:
        copy.wait_send()


def entry(tokens, w_shard, w_out, gains, segments, collective_id):
    count = lax.axis_size("head")
    batches = lax.axis_size("batch")
    others = batches // 2
    rows, width = tokens.shape
    size, wide = w_out.shape
    vmem = pl.BlockSpec(memory_space=pltpu.VMEM)
    slots = 6 * batches + others * (count + 3)
    sems = pltpu.SemaphoreType.DMA((slots,))
    return pl.pallas_call(
        functools.partial(entry_kernel, count, batches),
        out_shape=[
            jax.ShapeDtypeStruct((rows, width), BF),
            jax.ShapeDtypeStruct((rows, size), BF),
            jax.ShapeDtypeStruct((rows, size), F32),
            jax.ShapeDtypeStruct((batches * rows, 2 * size), BF),
            jax.ShapeDtypeStruct((width, 4 * size), BF),
            jax.ShapeDtypeStruct((count * size, batches * wide), BF),
            jax.ShapeDtypeStruct((batches, *gains.shape), F32),
            jax.ShapeDtypeStruct((batches, *segments.shape), jnp.int32),
        ],
        in_specs=[vmem] * 5,
        out_specs=[vmem] * 8,
        scratch_shapes=[sems, sems, pltpu.SemaphoreType.DMA((5,))],
        compiler_params=pltpu.CompilerParams(
            collective_id=collective_id, has_side_effects=True, vmem_limit_bytes=44 << 20
        ),
        name="entry",
    )(tokens, w_shard, w_out, gains, segments)


KEY_BLOCK = 512
QUERY_BLOCK = 256


def key_range(start_ref, base, query_block):
    first = query_block * QUERY_BLOCK
    lowest = start_ref[first]
    highest = start_ref[first + QUERY_BLOCK - 1]
    begin = lowest // KEY_BLOCK
    end = (base + first + QUERY_BLOCK - 1) // KEY_BLOCK + 1
    full_begin = jnp.minimum((highest + KEY_BLOCK - 1) // KEY_BLOCK, end)
    full_end = jnp.maximum((base + first + 1) // KEY_BLOCK, full_begin)
    return begin, full_begin, full_end, end


def allowed_pairs(key_block, start_row, base_row):
    shape = (KEY_BLOCK, QUERY_BLOCK)
    key_pos = key_block * KEY_BLOCK + lax.broadcasted_iota(jnp.int32, shape, 0)
    query_pos = base_row + lax.broadcasted_iota(jnp.int32, shape, 1)
    return (key_pos >= start_row) & (key_pos <= query_pos)


def attend_kernel(
    scale, start_sm, base_sm, q_ref, kv_ref, start_ref, logit_ref, o_ref, a_ref, lse_ref
):
    base = base_sm[0]
    size = q_ref.shape[1]
    factor = scale * math.log2(math.e)

    @pl.loop(0, q_ref.shape[0] // QUERY_BLOCK)
    def _(block):
        rows = pl.ds(pl.multiple_of(block * QUERY_BLOCK, QUERY_BLOCK), QUERY_BLOCK)
        queries = q_ref[rows]
        start_row = start_ref[:, rows]
        begin, full_begin, full_end, end = key_range(start_sm, base, block)

        def step(masked, at, state):
            old_max, old_sum, total = state
            keys = pl.ds(pl.multiple_of(at * KEY_BLOCK, KEY_BLOCK), KEY_BLOCK)
            scores = cols_inner(kv_ref[keys, :size], queries)
            if masked:
                allowed = allowed_pairs(at, start_row, base + block * QUERY_BLOCK)
                scores = jnp.where(allowed, scores, MASKED)
            new_max = jnp.maximum(old_max, jnp.max(scores, axis=0, keepdims=True))
            keep = jnp.exp2((old_max - new_max) * factor)
            weights = jnp.exp2(scores * factor - new_max * factor)
            new_sum = old_sum * keep + jnp.sum(weights, axis=0, keepdims=True)
            total = total * keep + rows_inner(kv_ref[keys, size:], weights.astype(BF))
            return new_max, new_sum, total

        state = (
            jnp.full((1, QUERY_BLOCK), MASKED, F32),
            jnp.zeros((1, QUERY_BLOCK), F32),
            jnp.zeros((size, QUERY_BLOCK), F32),
        )
        state = lax.fori_loop(begin, full_begin, functools.partial(step, True), state)
        state = lax.fori_loop(full_begin, full_end, functools.partial(step, False), state)
        state = lax.fori_loop(full_end, end, functools.partial(step, True), state)
        run_max, run_sum, total = state
        lse_ref[:, rows] = run_max * factor + jnp.log2(run_sum)
        attended = (total / run_sum).T
        o_ref[rows] = attended
        a_ref[rows] = (attended * jax.nn.sigmoid(logit_ref[rows])).astype(BF)


def attend_back_kernel(
    scale, start_sm, base_sm, q_ref, kv_ref, start_ref, logit_ref, o_ref, da_ref, lse_ref,
    dq_ref, dg_ref, dkv_ref, dk_acc, dv_acc,
):
    base = base_sm[0]
    size = q_ref.shape[1]
    factor = scale * math.log2(math.e)
    dk_acc[...] = jnp.zeros_like(dk_acc)
    dv_acc[...] = jnp.zeros_like(dv_acc)

    @pl.loop(0, q_ref.shape[0] // QUERY_BLOCK)
    def _(block):
        rows = pl.ds(pl.multiple_of(block * QUERY_BLOCK, QUERY_BLOCK), QUERY_BLOCK)
        queries = q_ref[rows]
        start_row = start_ref[:, rows]
        lse = lse_ref[:, rows]
        gate = jax.nn.sigmoid(logit_ref[rows])
        attended = o_ref[rows]
        d_mixed = da_ref[rows].astype(F32)
        d_attended = (d_mixed * gate).astype(BF)
        dg_ref[rows] = (d_mixed * attended * gate * (1.0 - gate)).astype(BF)
        delta = jnp.sum((d_attended.astype(F32) * attended).T, axis=0, keepdims=True)
        begin, full_begin, full_end, end = key_range(start_sm, base, block)

        def step(masked, at, d_queries):
            keys = pl.ds(pl.multiple_of(at * KEY_BLOCK, KEY_BLOCK), KEY_BLOCK)
            key_block = kv_ref[keys, :size]
            probs = jnp.exp2(cols_inner(key_block, queries) * factor - lse)
            if masked:
                allowed = allowed_pairs(at, start_row, base + block * QUERY_BLOCK)
                probs = jnp.where(allowed, probs, 0.0)
            d_probs = cols_inner(kv_ref[keys, size:], d_attended)
            d_scores = (probs * (d_probs - delta) * scale).astype(BF)
            dv_acc[keys] += matmul(probs.astype(BF), d_attended)
            dk_acc[keys] += matmul(d_scores, queries)
            return d_queries + rows_inner(key_block, d_scores)

        d_queries = jnp.zeros((size, QUERY_BLOCK), F32)
        d_queries = lax.fori_loop(begin, full_begin, functools.partial(step, True), d_queries)
        d_queries = lax.fori_loop(full_begin, full_end, functools.partial(step, False), d_queries)
        d_queries = lax.fori_loop(full_end, end, functools.partial(step, True), d_queries)
        dq_ref[rows] = d_queries.T.astype(BF)

    @pl.loop(0, kv_ref.shape[0] // KEY_BLOCK)
    def _(at):
        keys = pl.ds(pl.multiple_of(at * KEY_BLOCK, KEY_BLOCK), KEY_BLOCK)
        dk, dv = dk_acc[keys].astype(BF), dv_acc[keys].astype(BF)
        half = size // 2
        dkv_ref[keys, :size] = jnp.concatenate([dk[:, :half], dv[:, :half]], axis=1)
        dkv_ref[keys, size:] = jnp.concatenate([dk[:, half:], dv[:, half:]], axis=1)


def fold_kernel(
    batches, part_ref, own_ref, core_got, x_first, x_second, y_first, y_second, held, send_sem, recv_sem
):
    rows, size = own_ref.shape
    half = rows // 2
    others = batches // 2
    head = lax.axis_index("head")
    batch = lax.axis_index("batch")
    across, core, low = batch // 2, lax.rem(batch, 2), lax.rem(head, 2)
    twin = (across * 2 + 1 - core, head)
    mate = (batch, head + 1 - 2 * low)
    spots = [lax.rem(across + hop, others) for hop in range(others)]
    peers = [(spot * 2 + core, head) for spot in spots]
    greet((twin, mate, *peers[1:]))
    sems = (send_sem, recv_sem)
    slot = 0
    copies = []
    mine = pl.ds(pl.multiple_of(low * size, size), size)
    given = pl.ds(pl.multiple_of((1 - low) * size, size), size)
    top, bottom = pl.ds(0, half), pl.ds(half, half)

    def block(at, side):
        return pl.ds(pl.multiple_of((2 * at + side) * rows, rows), rows)

    def go(source, target, device):
        nonlocal slot
        copy = send(source, target, sems, slot, device)
        slot += 1
        copies.append(copy)
        return copy

    order = list(range(1, others)) + [0]
    first = [go(part_ref.at[block(spots[hop], 1 - core)], core_got.at[spots[hop]], twin) for hop in order]
    tops, bottoms = [], []
    for copy, hop in zip(first, order):
        copy.wait_recv()
        spot = spots[hop]
        core_got[spot] = add_low(core_got[spot], part_ref[block(spot, core)])
        bottoms.append(go(core_got.at[spot, bottom, given], y_first.at[spot], mate))
        if hop:
            tops.append(go(core_got.at[spot, top], x_first.at[hop - 1], peers[hop]))
    total = core_got[across, top].astype(F32)
    for hop in range(1, others):
        tops[hop - 1].wait_recv()
        total = total + x_first[hop - 1].astype(F32)
    held[...] = total.astype(BF)
    last = go(held.at[:, given], y_second, mate)
    ends = []
    for copy, hop in zip(bottoms, order):
        copy.wait_recv()
        spot = spots[hop]
        y_first[spot] = add_low(y_first[spot], core_got[spot, bottom, mine])
        if hop:
            ends.append(go(y_first.at[spot], x_second.at[hop - 1], peers[hop]))
    last.wait_recv()
    own_ref[top] = add_low(held[:, mine], y_second[...])
    total = y_first[across].astype(F32)
    for hop in range(1, others):
        ends[hop - 1].wait_recv()
        total = total + x_second[hop - 1].astype(F32)
    own_ref[bottom] = total.astype(BF)
    for copy in copies:
        copy.wait_send()


def fold(part, rows, collective_id):
    batches = lax.axis_size("batch")
    others = batches // 2
    size = part.shape[1] // 2
    half = rows // 2
    vmem = pl.BlockSpec(memory_space=pltpu.VMEM)
    sems = pltpu.SemaphoreType.DMA((4 * others,))
    return pl.pallas_call(
        functools.partial(fold_kernel, batches),
        out_shape=jax.ShapeDtypeStruct((rows, size), BF),
        in_specs=[vmem],
        out_specs=vmem,
        scratch_shapes=[
            pltpu.VMEM((others, rows, 2 * size), BF),
            pltpu.VMEM((others - 1, half, 2 * size), BF),
            pltpu.VMEM((others - 1, half, size), BF),
            pltpu.VMEM((others, half, size), BF),
            pltpu.VMEM((half, size), BF),
            pltpu.VMEM((half, 2 * size), BF),
            sems,
            sems,
        ],
        compiler_params=pltpu.CompilerParams(
            collective_id=collective_id, has_side_effects=True, vmem_limit_bytes=20 << 20
        ),
        name="fold",
    )(part)


def tail_kernel(
    count, batches, cat_ref, w_ref, x_ref, gain_ref, dh1_ref, second_ref,
    n1_ref, mixed_ref, low_ref, out_0,
    out_all, tok_all, gains_ref, wout_own, din_ref,
    part_ref, tok_ref, got, wout_got, gain_own, gain_got, gain_mid, gain_heads,
    din_s, din_got, din_x, wout_s, wout_twin, wout_x, wout_part,
    send_sem, recv_sem, local_sem,
):
    steps = count // 2
    rows, width = x_ref.shape
    depth = cat_ref.shape[1]
    tile = 256
    place, right, left = ring_setup(count)
    batch, head = lax.axis_index("batch"), lax.axis_index("head")
    others = [lax.rem(batch + hop, batches) for hop in range(1, batches)]
    members = [(batch, ring_head(lax.rem(place + hop, count), count)) for hop in range(1, count)]
    greet((*members, *[(other, head) for other in others]))
    sems = (send_sem, recv_sem)
    slot = 0
    copies = []

    def go(source, target, device):
        nonlocal slot
        copy = send(source, target, sems, slot, device)
        slot += 1
        copies.append(copy)
        return copy

    across, core = batch // 2, lax.rem(batch, 2)
    spots = [lax.rem(across + hop, batches // 2) for hop in range(batches // 2)]
    order = list(range(1, batches // 2)) + [0]
    twin = (across * 2 + 1 - core, head)

    def scatter_swap(view, held):
        return [go(view(2 * spots[hop] + 1 - core), held.at[spots[hop]], twin) for hop in order]

    def add_tiles(target, one, other):
        @pl.loop(0, target.shape[0] // 128)
        def _(at):
            lines = pl.ds(pl.multiple_of(at * 128, 128), 128)
            total = one[lines].astype(F32) + other[lines].astype(F32)
            target[lines] = total.astype(target.dtype)

    def scatter_cross(view, held, crossed, arriving):
        out = []
        for copy, hop in zip(arriving, order):
            copy.wait_recv()
            spot = spots[hop]
            add_tiles(held.at[spot], held.at[spot], view(2 * spot + core))
            if hop:
                out.append(go(held.at[spot], crossed.at[hop - 1], (spot * 2 + core, head)))
        return out

    def scatter_end(held, crossed, arriving, target):
        for hop, copy in enumerate(arriving):
            copy.wait_recv()
            last = hop == len(arriving) - 1
            add_tiles(target if last else held.at[across], held.at[across], crossed.at[hop])

    def wout_view(at):
        wide = wout_part.shape[1]
        return wout_s.at[:, pl.ds(pl.multiple_of(at * wide, wide), wide)]

    def din_view(at):
        tall = din_ref.shape[0]
        return din_s.at[pl.ds(pl.multiple_of(at * tall, tall), tall)]

    def span(owner, extent):
        return pl.ds(pl.multiple_of(lax.rem(owner + count, count) * extent, extent), extent)

    def compute(owner):
        here = span(owner, rows)
        values = cat_ref[here]

        @pl.loop(0, width // tile)
        def _(at):
            cols = pl.ds(pl.multiple_of(at * tile, tile), tile)
            part_ref[here, cols] = cols_inner(values, w_ref[cols, pl.ds(0, depth)]).astype(BF)

    def gather(own, whole, step, last):
        out = []
        for flow, chunk, device in ((0, place - step, right), (1, place + step, left)):
            if last:
                last[flow].wait_recv()
            target = whole.at[lax.rem(chunk + count, count)]
            source = target if step else own
            if step == steps - 1:
                cut = (slice(None), pl.ds(flow * (width // 2), width // 2))
                source, target = source.at[cut], target.at[cut]
            out.append(go(source, target, device))
        return out

    def reduce(parts, held, step, last):
        extent, side = held.shape[2], held.shape[3] // 2
        out = []
        for flow, owner, device in (
            (0, place + steps - step, right),
            (1, place - steps + step, left),
        ):
            have = pl.ds(flow * side, side)
            lack = pl.ds((1 - flow) * side, side)
            mine = parts.at[span(owner, extent)]
            if step == 0:
                out.append(go(mine.at[:, have], held.at[flow, 0, :, have], device))
                continue
            last[flow].wait_recv()
            if step == 1:
                held[flow, 0, :, have] = add_low(held[flow, 0, :, have], mine[:, have])
                held[flow, 0, :, lack] = mine[:, lack]
            else:
                held[flow, step - 1] = add_low(held[flow, step - 1], mine[...])
            out.append(go(held.at[flow, step - 1], held.at[flow, step], device))
        return out

    keep_out = pltpu.make_async_copy(out_0, out_all.at[place], local_sem.at[0])
    keep_out.start()
    compute(place + steps)
    sums = reduce(part_ref, got, 0, None)
    outs = gather(out_0, out_all, 0, None)

    @pl.loop(1, count)
    def _(hop):
        compute(place + steps + hop)

    @pl.loop(0, width // tile)
    def _(at):
        cols = pl.ds(pl.multiple_of(at * tile, tile), tile)
        wout_s[:, cols] = rows_inner(mixed_ref[...], low_ref[:, cols]).astype(BF)

    wouts = scatter_swap(wout_view, wout_twin)

    @pl.loop(0, width // tile)
    def _(at):
        cols = pl.ds(pl.multiple_of(at * tile, tile), tile)
        din_s[cols] = rows_inner(n1_ref[:, cols], cat_ref[...]).astype(BF)

    dins = scatter_swap(din_view, din_got)
    for step in range(1, steps):
        sums = reduce(part_ref, got, step, sums)
        outs = gather(out_0, out_all, step, outs)
        if step == 1:
            wouts = scatter_cross(wout_view, wout_twin, wout_x, wouts)
            dins = scatter_cross(din_view, din_got, din_x, dins)
    for copy in sums:
        copy.wait_recv()

    def tile_of(at):
        return pl.ds(pl.multiple_of(at * tile, tile), tile)

    def total(cols):
        return (
            part_ref[span(place, rows), cols].astype(F32)
            + got[0, steps - 1, :, cols].astype(F32)
            + got[1, steps - 1, :, cols].astype(F32)
        )

    def collect(at, state):
        squares, mean = state
        cols = tile_of(at)
        x = x_ref[:, cols].astype(F32)
        squares = squares + jnp.sum(x * x, axis=1, keepdims=True)
        return squares, mean + jnp.sum(gain_ref[:, cols] * total(cols) * x, axis=1, keepdims=True)

    zero = jnp.zeros((rows, 1), F32)
    squares, mean = lax.fori_loop(0, width // tile, collect, (zero, zero))
    scale = lax.rsqrt(squares / width + EPSILON)
    pull = scale * scale * scale * (mean / width)

    @pl.loop(0, width // tile)
    def _(at):
        cols = tile_of(at)
        x, dn1 = x_ref[:, cols].astype(F32), total(cols)
        gain_own[pl.ds(0, 1), cols] = jnp.sum(dn1 * x * scale, axis=0, keepdims=True)
        gain_own[pl.ds(1, 1), cols] = second_ref[:, cols]
        tok_ref[:, cols] = (dh1_ref[:, cols] + scale * (gain_ref[:, cols] * dn1) - x * pull).astype(BF)

    keep_tok = pltpu.make_async_copy(tok_ref, tok_all.at[place], local_sem.at[1])
    keep_tok.start()
    toks = gather(tok_ref, tok_all, 0, None)
    scatter_end(wout_twin, wout_x, wouts, wout_part)
    wsums = reduce(wout_part, wout_got, 0, None)
    scatter_end(din_got, din_x, dins, din_ref)
    wide = width // batches

    def slice_of(at):
        return pl.ds(pl.multiple_of(at * wide, wide), wide)

    gains = [
        go(gain_own.at[:, slice_of(other)], gain_got.at[hop], (other, head))
        for hop, other in enumerate(others)
    ]
    toks = gather(tok_ref, tok_all, 1, toks)
    wsums = reduce(wout_part, wout_got, 1, wsums)
    middle = gain_own[:, slice_of(batch)]
    for hop, copy in enumerate(gains):
        copy.wait_recv()
        middle = middle + gain_got[hop]
    gain_mid[...] = middle
    gain_heads[place] = middle
    gains = [go(gain_mid, gain_heads.at[place], member) for member in members]
    for step in range(2, steps):
        toks = gather(tok_ref, tok_all, step, toks)
        wsums = reduce(wout_part, wout_got, step, wsums)
    for copy in gains:
        copy.wait_recv()
    middle = gain_heads[0]
    for at in range(1, count):
        middle = middle + gain_heads[at]
    gains_ref[...] = middle
    for copy in (*wsums, *outs):
        copy.wait_recv()
    wout_own[...] = (
        wout_part[span(place, wout_own.shape[0])].astype(F32)
        + wout_got[0, steps - 1].astype(F32)
        + wout_got[1, steps - 1].astype(F32)
    )
    for copy in toks:
        copy.wait_recv()
    for copy in copies:
        copy.wait_send()
    keep_out.wait()
    keep_tok.wait()


def tail(d_cat, w_in, x_own, gain, d_resid, second, normed, mixed, low, out_own, collective_id):
    count = lax.axis_size("head")
    batches = lax.axis_size("batch")
    steps = count // 2
    rows, width = x_own.shape
    others = batches // 2
    size, wide = mixed.shape[1] // count, width // batches
    depth = d_cat.shape[1]
    vmem = pl.BlockSpec(memory_space=pltpu.VMEM)
    whole = (count, rows, width)
    sems = pltpu.SemaphoreType.DMA((5 * count + 3 * batches,))
    gains = (2, width // batches)
    return pl.pallas_call(
        functools.partial(tail_kernel, count, batches),
        out_shape=[
            jax.ShapeDtypeStruct(whole, BF),
            jax.ShapeDtypeStruct(whole, BF),
            jax.ShapeDtypeStruct(gains, F32),
            jax.ShapeDtypeStruct((size, wide), F32),
            jax.ShapeDtypeStruct((wide, depth), F32),
        ],
        in_specs=[vmem] * 10,
        out_specs=[vmem] * 5,
        scratch_shapes=[
            pltpu.VMEM((count * rows, width), BF),
            pltpu.VMEM((rows, width), BF),
            pltpu.VMEM((2, steps, rows, width), BF),
            pltpu.VMEM((2, steps, size, wide), BF),
            pltpu.VMEM((2, width), F32),
            pltpu.VMEM((batches - 1, *gains), F32),
            pltpu.VMEM(gains, F32),
            pltpu.VMEM((count, *gains), F32),
            pltpu.VMEM((width, depth), BF),
            pltpu.VMEM((others, wide, depth), BF),
            pltpu.VMEM((others - 1, wide, depth), BF),
            pltpu.VMEM((count * size, width), BF),
            pltpu.VMEM((others, count * size, wide), BF),
            pltpu.VMEM((others - 1, count * size, wide), BF),
            pltpu.VMEM((count * size, wide), BF),
            sems,
            sems,
            pltpu.SemaphoreType.DMA((2,)),
        ],
        compiler_params=pltpu.CompilerParams(
            collective_id=collective_id, has_side_effects=True, vmem_limit_bytes=(32 << 20) + 4 * count * size * width
        ),
        cost_estimate=pl.CostEstimate(
            flops=2 * count * rows * width * d_cat.shape[1], bytes_accessed=400 << 20, transcendentals=0
        ),
        name="tail",
    )(d_cat, w_in, x_own, gain, d_resid, second, normed, mixed, low, out_own)


def local_call(kernel, scalars, arrays, outs, scratch, flops, name):
    vmem = pl.BlockSpec(memory_space=pltpu.VMEM)
    smem = pl.BlockSpec(memory_space=pltpu.SMEM)
    return pl.pallas_call(
        kernel,
        out_shape=outs,
        in_specs=[smem] * len(scalars) + [vmem] * len(arrays),
        out_specs=[vmem] * len(outs),
        scratch_shapes=scratch,
        compiler_params=pltpu.CompilerParams(vmem_limit_bytes=36 << 20),
        cost_estimate=pl.CostEstimate(flops=flops, bytes_accessed=8 << 20, transcendentals=0),
        name=name,
    )(*scalars, *arrays)


def ring_routes(count):
    spots = [ring_head(at, count) for at in range(count)]
    right = [(spots[at], spots[(at + 1) % count]) for at in range(count)]
    left = [(spots[at], spots[at - 1]) for at in range(count)]
    return right, left


def add_low(one, other):
    return (one.astype(F32) + other.astype(F32)).astype(BF)


def flow_steps(part, going, coming):
    count = lax.axis_size("head")
    place = ring_place(lax.axis_index("head"), count)
    right, left = ring_routes(count)
    rows = part.shape[0] // count
    steps = count // 2

    def mine(owner):
        return lax.dynamic_slice_in_dim(part, lax.rem(owner + count, count) * rows, rows, 0)

    for step in range(2, steps - 1):
        from_left = lax.ppermute(going, "head", right)
        from_right = lax.ppermute(coming, "head", left)
        going = add_low(from_left, mine(place + steps - 1 - step))
        coming = add_low(from_right, mine(place - steps + 1 + step))
        going, coming = yield going, coming
    from_left = lax.ppermute(going, "head", right)
    from_right = lax.ppermute(coming, "head", left)
    yield mine(place).astype(F32) + from_left.astype(F32) + from_right.astype(F32)


def matmul(left, right):
    return jnp.dot(left, right, preferred_element_type=F32)


def rows_inner(left, right):
    return lax.dot_general(left, right, (((0,), (0,)), ((), ())), preferred_element_type=F32)


def cols_inner(left, right):
    return lax.dot_general(left, right, (((1,), (1,)), ((), ())), preferred_element_type=F32)


def rms_scale(values):
    return lax.rsqrt(jnp.mean(values * values, axis=1, keepdims=True) + EPSILON)


def per_device(
    tokens,
    segment_ids,
    norm1_gain,
    w_query,
    w_key,
    w_value,
    w_gate,
    w_out,
    norm2_gain,
    w_mlp_gate,
    w_mlp_up,
    w_down,
    out_grad,
):
    heads = lax.axis_size("head")
    batches = lax.axis_size("batch")
    row_count, width = tokens.shape
    head_size = w_query.shape[1]
    half = w_key.shape[1]
    chunk = row_count // heads
    me = ring_place(lax.axis_index("head"), heads)
    scale_factor = 1.0 / math.sqrt(head_size)

    w_shard = jnp.concatenate([w_query, w_gate, w_key, w_value], axis=1)
    gains = jnp.concatenate([norm1_gain, norm2_gain]).reshape(-1, 128).astype(F32)
    normed_one, queries, gate_logit, kv_all, w_in, out_full, gains, seg_all = entry(
        tokens, w_shard, w_out, gains, segment_ids.reshape(-1, 128), 1
    )
    gains, w_mlp_gate = lax.optimization_barrier((gains, w_mlp_gate))
    seg_all = seg_all.reshape(-1)
    gains = gains.reshape(batches, 2, -1).transpose(1, 0, 2).reshape(2, width)
    gain_one, gain_two = gains[0], gains[1]
    mgate_full = lax.all_gather(w_mlp_gate, "batch", axis=0, tiled=True)

    base = lax.axis_index("batch") * row_count
    ids = jnp.arange(DOCUMENTS, dtype=jnp.int32)
    below = jnp.sum((seg_all[None, :] < ids[:, None]).astype(jnp.int32), axis=1)
    starts = jnp.sum(jnp.where(segment_ids[None, :] == ids[:, None], below[:, None], 0), axis=0)
    scalars = (starts, base.reshape(1))
    pair_flops = 4 * row_count * kv_all.shape[0] * head_size
    attended, mixed, lse = local_call(
        functools.partial(attend_kernel, scale_factor),
        scalars,
        (queries, kv_all, starts[None], gate_logit),
        [
            jax.ShapeDtypeStruct((row_count, head_size), F32),
            jax.ShapeDtypeStruct((row_count, head_size), BF),
            jax.ShapeDtypeStruct((1, row_count), F32),
        ],
        [],
        pair_flops,
        "attend",
    )
    mixed_all, down_full, mup_full = spread(
        [mixed, w_down, w_mlp_up], (("head", "cols"), ("batch", "cols"), ("batch", "rows")), 2
    )
    (
        mlp_part, d_mlp, d_down, resid_own, d_resid, d_resid_low, d_gain_two, d_mixed, going, coming,
    ) = mlp_back(
        tokens, mixed_all, out_grad, gain_two[None], out_full, mgate_full, mup_full, down_full, 3
    )
    hold = lax.optimization_barrier
    mixed_own = lax.dynamic_slice_in_dim(mixed_all, me * chunk, chunk, 0)
    flow = flow_steps(mlp_part, going, coming)
    state = next(flow)

    d_queries, d_gate_logit, d_kv_all = local_call(
        functools.partial(attend_back_kernel, scale_factor),
        scalars,
        (queries, kv_all, starts[None], gate_logit, attended, d_mixed, lse),
        [
            jax.ShapeDtypeStruct((row_count, head_size), BF),
            jax.ShapeDtypeStruct((row_count, head_size), BF),
            jax.ShapeDtypeStruct(kv_all.shape, BF),
        ],
        [pltpu.VMEM((kv_all.shape[0], head_size), F32)] * 2,
        5 * pair_flops // 2,
        "attend_back",
    )
    d_kv_all, state = hold((d_kv_all, state))
    while isinstance(state, tuple):
        state = flow.send(state)
    d_kv = fold(d_kv_all, row_count, 4)
    d_kv, state, d_down, d_mlp = hold((d_kv, state, d_down, d_mlp))
    out_own = (resid_own + state).astype(BF)
    d_down = lax.psum_scatter(d_down, "batch", scatter_dimension=1, tiled=True)
    d_mlp = lax.psum_scatter(d_mlp, "batch", scatter_dimension=0, tiled=True)
    d_cat = jnp.concatenate([d_queries, d_gate_logit, d_kv], axis=1)
    inputs_own = lax.dynamic_slice_in_dim(tokens, me * chunk, chunk, 0)
    output, d_tokens, d_gains, d_out, d_in = tail(
        d_cat, w_in, inputs_own, gain_one[None], d_resid, d_gain_two, normed_one, mixed_own,
        d_resid_low, out_own, 5,
    )
    d_tokens, d_mlp, d_down = hold((d_tokens, d_mlp, d_down))
    d_mlp, d_down = d_mlp.astype(F32), d_down.astype(F32)
    output = output.reshape(row_count, width)
    d_tokens = d_tokens.reshape(row_count, width)
    hidden_own = w_mlp_gate.shape[1]
    return (
        output,
        d_tokens,
        d_gains[0],
        d_in[:, :head_size],
        d_in[:, 2 * head_size : 2 * head_size + half],
        d_in[:, 2 * head_size + half :],
        d_in[:, head_size : 2 * head_size],
        d_out,
        d_gains[1],
        d_mlp[:, :hidden_own],
        d_mlp[:, hidden_own:],
        d_down,
    )


def solution(mesh):
    return jax.shard_map(
        per_device,
        mesh=mesh,
        in_specs=(
            P("batch", None),
            P("batch"),
            P("batch"),
            P("batch", "head"),
            P("batch", "head"),
            P("batch", "head"),
            P("batch", "head"),
            P("head", "batch"),
            P("batch"),
            P("batch", "head"),
            P("batch", "head"),
            P("head", "batch"),
            P("batch", None),
        ),
        out_specs=(
            P("batch", None),
            P("batch", None),
            P("batch"),
            P("batch", "head"),
            P("batch", "head"),
            P("batch", "head"),
            P("batch", "head"),
            P("head", "batch"),
            P("batch"),
            P("batch", "head"),
            P("batch", "head"),
            P("head", "batch"),
        ),
        check_vma=False,
    )
```

```python
import functools
import math

import jax
import jax.numpy as jnp
from jax import lax
from jax.experimental import pallas as pl
from jax.experimental.pallas import tpu as pltpu
from jax.sharding import PartitionSpec as P

EPSILON = 1e-06
MASKED = -1e30
DOCUMENTS = 7
BF = jnp.bfloat16
F32 = jnp.float32


MESH = pl.DeviceIdType.MESH
VMEM_LIMIT = 60 << 20


def ring_place(head, count):
    high, low = head // 2, head % 2
    return (1 - low) * high + low * (count - 1 - high)


def ring_head(place, count):
    low = place // (count // 2)
    high = (1 - low) * place + low * (count - 1 - place)
    return 2 * high + low


def ring_setup(count):
    batch = lax.axis_index("batch")
    place = ring_place(lax.axis_index("head"), count)
    right = (batch, ring_head(lax.rem(place + 1, count), count))
    left = (batch, ring_head(lax.rem(place + count - 1, count), count))
    return place, right, left


def greet(devices):
    barrier = pltpu.get_barrier_semaphore()
    for device in devices:
        pl.semaphore_signal(barrier, inc=1, device_id=device, device_id_type=MESH)
    pl.semaphore_wait(barrier, len(devices))


def send(source, target, sems, slot, device):
    copy = pltpu.make_async_remote_copy(
        src_ref=source,
        dst_ref=target,
        send_sem=sems[0].at[slot],
        recv_sem=sems[1].at[slot],
        device_id=device,
        device_id_type=MESH,
    )
    copy.start()
    return copy


def half_of(extent, flow):
    if extent[1] % 256:
        return (pl.ds(flow * (extent[0] // 2), extent[0] // 2), slice(None))
    return (slice(None), pl.ds(flow * (extent[1] // 2), extent[1] // 2))


def place_of(whole, own, chunk, form):
    rows, wide = own.shape[-2:]
    if form == "lead":
        return whole.at[chunk]
    if form == "rows":
        return whole.at[pl.ds(pl.multiple_of(chunk * rows, rows), rows)]
    return whole.at[:, pl.ds(pl.multiple_of(chunk * wide, wide), wide)]


def spread_kernel(count, batches, plans, *refs):
    steps = count // 2
    arrays = len(plans)
    own_refs, all_refs = refs[:arrays], refs[arrays : 2 * arrays]
    send_sem, recv_sem, local_sem = refs[2 * arrays :]
    place, right, left = ring_setup(count)
    head = lax.axis_index("head")
    batch = lax.axis_index("batch")
    across, core = batch // 2, lax.rem(batch, 2)
    others = batches // 2
    twin = (across * 2 + 1 - core, head)
    peers = [(lax.rem(across + hop, others) * 2 + core, head) for hop in range(1, others)]
    ring = any(axis == "head" for axis, _ in plans)
    grid = any(axis == "batch" for axis, _ in plans)
    greet((right, left) * ring + (twin, *peers) * grid)
    sems = (send_sem, recv_sem)
    slot = 0
    waiting, arriving, local = [], [], []

    def go(source, target, device):
        nonlocal slot
        copy = send(source, target, sems, slot, device)
        slot += 1
        waiting.append(copy)
        return copy

    stages = []
    for index, (axis, form) in enumerate(plans):
        own, whole = own_refs[index], all_refs[index]
        spot = place if axis == "head" else batch
        copy = pltpu.make_async_copy(own, place_of(whole, own, spot, form), local_sem.at[index])
        copy.start()
        local.append(copy)
        if axis == "batch":
            stages.append(index)
    onward = []

    def stage():
        for copy, block in onward:
            copy.wait_recv()
            arriving.append(go(block, block, twin))
        onward.clear()
        if stages:
            index = stages.pop(0)
            own, whole, form = own_refs[index], all_refs[index], plans[index][1]
            mine = place_of(whole, own, batch, form)
            for hop, peer in enumerate(peers, 1):
                source = lax.rem(across + others - hop, others) * 2 + core
                onward.append((go(own, mine, peer), place_of(whole, own, source, form)))
            arriving.append(go(own, mine, twin))

    stage()
    copies = [None] * (2 * arrays)
    for step in range(steps):
        for index, (axis, form) in enumerate(plans):
            if axis != "head":
                continue
            own = own_refs[index]
            for flow, chunk, device in ((0, place - step, right), (1, place + step, left)):
                at = 2 * index + flow
                if step:
                    copies[at].wait_recv()
                chunk = lax.rem(chunk + count, count)
                target = place_of(all_refs[index], own, chunk, form)
                source = target if step else own
                if step == steps - 1:
                    part = half_of(own.shape, flow)
                    source = source.at[part]
                    target = target.at[part]
                copies[at] = go(source, target, device)
        if step == steps // 2:
            stage()
    while stages or onward:
        stage()
    for copy in copies:
        if copy is not None:
            arriving.append(copy)
    for copy in arriving:
        copy.wait_recv()
    for copy in waiting:
        copy.wait_send()
    for copy in local:
        copy.wait()


def spread(arrays, plans, collective_id):
    count = lax.axis_size("head")
    batches = lax.axis_size("batch")
    shapes = []
    slots = 0
    for array, (axis, form) in zip(arrays, plans):
        many = count if axis == "head" else batches
        slots += count if axis == "head" else batches - 1
        if form == "lead":
            shapes.append((many, *array.shape))
        elif form == "rows":
            shapes.append((many * array.shape[0], array.shape[1]))
        else:
            shapes.append((array.shape[0], many * array.shape[1]))
    hbm = pl.BlockSpec(memory_space=pl.ANY)
    return pl.pallas_call(
        functools.partial(spread_kernel, count, batches, plans),
        out_shape=[jax.ShapeDtypeStruct(shape, a.dtype) for shape, a in zip(shapes, arrays)],
        in_specs=[pl.BlockSpec(memory_space=pltpu.VMEM)] * len(arrays),
        out_specs=[hbm] * len(arrays),
        scratch_shapes=[
            pltpu.SemaphoreType.DMA((slots,)),
            pltpu.SemaphoreType.DMA((slots,)),
            pltpu.SemaphoreType.DMA((len(arrays),)),
        ],
        compiler_params=pltpu.CompilerParams(
            collective_id=collective_id, has_side_effects=True, vmem_limit_bytes=VMEM_LIMIT
        ),
        name=f"spread_{collective_id}",
    )(*arrays)


def mlp_kernel(
    count, x_hbm, a_hbm, dy_hbm, gain_ref, out_hbm, gate_hbm, up_hbm, down_hbm,
    mlp_hbm, dmlp_hbm, ddown_hbm, h1_ref, dh1_ref, low_ref, dgain_ref, da_ref, ahead_ref, behind_ref,
    x_s, a_s, mlp_s, h1_s, dy_all, n2_all, hid_all, grad_all, dmlp_s, ddown_s, da_part,
    mlp_far, mlp_next, mlp_got, right_part, left_part, right_got, left_got,
    out_w, gate_w, up_w, down_w, in_sem, out_sem, grad_sem, weight_sem,
    send_sem, recv_sem, da_send, da_recv, far_send, far_recv,
):
    steps = count // 2
    rows = x_hbm.shape[0] // count
    width = x_hbm.shape[1]
    hidden = gate_w.shape[1]
    weights = [
        pltpu.make_async_copy(source, target, weight_sem.at[index])
        for index, (source, target) in enumerate(
            ((out_hbm, out_w), (gate_hbm, gate_w), (up_hbm, up_w), (down_hbm, down_w))
        )
    ]
    side = width // 2
    tile = 256
    broad = 1024
    inner = 256 if hidden % 256 == 0 else 128
    size = da_ref.shape[1]
    place, right, left = ring_setup(count)

    def member(hop):
        spot = lax.rem(place + hop, count)
        return spot, (lax.axis_index("batch"), ring_head(spot, count))

    def owners(group):
        first = jnp.where(group == 0, 1, 0)
        one = lax.rem(place + steps - group, count)
        two = lax.rem(place - steps + group + first * steps + count, count)
        return one, two

    def span(owner):
        return pl.ds(pl.multiple_of(owner * rows, rows), rows)

    def tile_of(at, extent=tile):
        return pl.ds(pl.multiple_of(at * extent, extent), extent)

    def loads(group, slot):
        return [
            pltpu.make_async_copy(
                source.at[span(owner)],
                target.at[pl.ds(at * rows, rows)],
                in_sem.at[slot, 2 * index + at],
            )
            for index, (source, target) in enumerate(
                ((x_hbm, x_s.at[slot]), (a_hbm, a_s.at[slot]), (dy_hbm, dy_all.at[group]))
            )
            for at, owner in enumerate(owners(group))
        ]

    def stores(group, slot):
        return [
            pltpu.make_async_copy(
                mlp_s.at[slot, pl.ds(at * rows, rows)], mlp_hbm.at[span(owner)], out_sem.at[slot, at]
            )
            for at, owner in enumerate(owners(group))
        ]

    def passing(source, target, sems, slot, device):
        return pltpu.make_async_remote_copy(
            src_ref=source,
            dst_ref=target,
            send_sem=sems[0].at[slot],
            recv_sem=sems[1].at[slot],
            device_id=device,
            device_id_type=MESH,
        )

    ring_sems, far_sems = (send_sem, recv_sem), (far_send, far_recv)
    ahead, behind = pl.ds(0, side), pl.ds(side, side)

    def first_copies():
        return (
            passing(right_part.at[0, :, ahead], right_got.at[0, :, ahead], ring_sems, 0, right),
            passing(right_part.at[0, :, behind], left_got.at[0, :, behind], ring_sems, steps, left),
        )

    def later_copies(step):
        return (
            passing(right_got.at[step - 1], right_got.at[step], ring_sems, step, right),
            passing(left_got.at[step - 1], left_got.at[step], ring_sems, steps + step, left),
        )

    for copy in (*loads(0, 0), *weights):
        copy.start()
    greet([member(hop)[1] for hop in range(1, count)])
    weights[0].wait()

    @pl.loop(0, steps)
    def _(group):
        slot = lax.rem(group, 2)
        for copy in loads(group, slot):
            copy.wait()

        @pl.when(group + 1 < steps)
        def _():
            for copy in loads(group + 1, 1 - slot):
                copy.start()

        @pl.when(group >= 2)
        def _():
            for copy in stores(group - 2, slot):
                copy.wait()

        mixed = a_s[slot]

        def residual(at, total):
            cols = tile_of(at, broad)
            values = x_s[slot, :, cols].astype(F32) + matmul(mixed, out_w[:, cols])
            h1_s[:, cols] = values
            return total + jnp.sum(values * values, axis=1, keepdims=True)

        total = lax.fori_loop(0, width // broad, residual, jnp.zeros((2 * rows, 1), F32))
        scale = lax.rsqrt(total / width + EPSILON)

        @pl.when(group == 0)
        def _():
            h1_ref[...] = h1_s[pl.ds(rows, rows)]
            for copy in weights[1:]:
                copy.wait()

        @pl.loop(0, width // tile)
        def _(at):
            cols = tile_of(at)
            n2_all[group, :, cols] = (h1_s[:, cols] * scale * gain_ref[:, cols]).astype(BF)

        normed = n2_all[group]
        dy = dy_all[group]

        @pl.loop(0, hidden // inner)
        def _(at):
            cols = tile_of(at, inner)
            cols_up = pl.ds(pl.multiple_of(hidden + at * inner, inner), inner)
            gate = matmul(normed, gate_w[:, cols])
            up = matmul(normed, up_w[:, cols])
            d_hidden = cols_inner(dy, down_w[cols])
            sig = jax.nn.sigmoid(gate)
            silu = gate * sig
            hid_all[group, :, cols] = (silu * up).astype(BF)
            grad_all[group, :, cols] = (d_hidden * up * sig * (1.0 + gate * (1.0 - sig))).astype(BF)
            grad_all[group, :, cols_up] = (d_hidden * silu).astype(BF)

        hid = hid_all[group]
        d_gate = grad_all[group, :, :hidden]
        d_up = grad_all[group, :, hidden:]
        half = jnp.minimum(group, 1)

        @pl.loop(0, width // broad)
        def _(at):
            cols = tile_of(at, broad)
            part = (cols_inner(d_gate, gate_w[cols]) + cols_inner(d_up, up_w[cols])).astype(BF)
            right_part[half, :, cols] = part[:rows]
            left_part[half, :, cols] = part[rows:]
            mlp_s[slot, :, cols] = matmul(hid, down_w[:, cols]).astype(BF)

        for copy in stores(group, slot):
            copy.start()

        @pl.when(group == 0)
        def _():
            mlp_far[...] = mlp_s[slot, pl.ds(0, rows)]
            for copy in first_copies():
                copy.start()

        @pl.when(group == 1)
        def _():
            mlp_next[0] = mlp_s[slot, pl.ds(0, rows)]
            mlp_next[1] = mlp_s[slot, pl.ds(rows, rows)]
            one, two = first_copies()
            one.wait_recv()
            right_got[0, :, ahead] = add_low(right_part[1, :, ahead], right_got[0, :, ahead])
            right_got[0, :, behind] = right_part[1, :, behind]
            two.wait_recv()
            left_got[0, :, behind] = add_low(left_part[1, :, behind], left_got[0, :, behind])
            left_got[0, :, ahead] = left_part[1, :, ahead]

        @pl.when(group == 2)
        def _():
            ahead_ref[...] = mlp_s[slot, pl.ds(0, rows)]
            behind_ref[...] = mlp_s[slot, pl.ds(rows, rows)]

        @pl.when(group >= 2)
        def _():
            one, two = later_copies(group - 1)
            one.wait_recv()
            right_got[group - 1] = add_low(right_part[1], right_got[group - 1])
            two.wait_recv()
            left_got[group - 1] = add_low(left_part[1], left_got[group - 1])

        @pl.when(group >= 1)
        def _():
            for copy in later_copies(group):
                copy.start()

    far_copies = [
        passing(mlp_far.at[:, ahead], mlp_got.at[0, :, ahead], far_sems, 0, right),
        passing(mlp_far.at[:, behind], mlp_got.at[1, :, behind], far_sems, 1, left),
    ]
    for copy in far_copies:
        copy.start()

    every = steps * 2 * rows

    def dmlp_copy(at, slot):
        return pltpu.make_async_copy(
            dmlp_s.at[slot], dmlp_hbm.at[tile_of(at // 2), tile_of(lax.rem(at, 2), hidden)], grad_sem.at[slot]
        )

    mlp_tiles = 2 * (width // tile)

    @pl.loop(0, mlp_tiles)
    def _(at):
        slot = lax.rem(at, 2)

        @pl.when(at >= 2)
        def _():
            dmlp_copy(at - 2, slot).wait()

        normed = n2_all[:, :, tile_of(at // 2)].reshape(every, tile)
        grads = grad_all[:, :, tile_of(lax.rem(at, 2), hidden)].reshape(every, hidden)
        dmlp_s[slot] = rows_inner(normed, grads).astype(BF)
        dmlp_copy(at, slot).start()

    wide = 512
    across = width // wide

    def ddown_copy(at, slot):
        return pltpu.make_async_copy(
            ddown_s.at[slot],
            ddown_hbm.at[tile_of(at // across, inner), tile_of(lax.rem(at, across), wide)],
            grad_sem.at[2 + slot],
        )

    down_tiles = across * (hidden // inner)

    @pl.loop(0, down_tiles)
    def _(at):
        slot = lax.rem(at, 2)

        @pl.when(at >= 2)
        def _():
            ddown_copy(at - 2, slot).wait()

        hid = hid_all[:, :, tile_of(at // across, inner)].reshape(every, inner)
        dy = dy_all[:, :, tile_of(lax.rem(at, across), wide)].reshape(every, wide)
        ddown_s[slot] = rows_inner(hid, dy).astype(BF)
        ddown_copy(at, slot).start()

    for copy in later_copies(steps - 1):
        copy.wait_recv()
    for flow, have, lack in ((0, ahead, behind), (1, behind, ahead)):
        far_copies[flow].wait_recv()
        mlp_got[flow, :, have] = add_low(mlp_got[flow, :, have], mlp_next[flow, :, have])
        mlp_got[flow, :, lack] = mlp_next[flow, :, lack]
    next_copies = [
        passing(mlp_got.at[0], mlp_got.at[2], far_sems, 2, right),
        passing(mlp_got.at[1], mlp_got.at[3], far_sems, 3, left),
    ]
    for copy in next_copies:
        copy.start()

    def collect(at, state):
        squares, mean = state
        cols = tile_of(at)
        dn2 = (
            left_part[0, :, cols].astype(F32)
            + right_got[steps - 1, :, cols].astype(F32)
            + left_got[steps - 1, :, cols].astype(F32)
        )
        dh1_ref[:, cols] = dn2
        h1 = h1_ref[:, cols]
        squares = squares + jnp.sum(h1 * h1, axis=1, keepdims=True)
        return squares, mean + jnp.sum(gain_ref[:, cols] * dn2 * h1, axis=1, keepdims=True)

    zero = jnp.zeros((rows, 1), F32)
    squares, mean = lax.fori_loop(0, width // tile, collect, (zero, zero))
    scale_own = lax.rsqrt(squares / width + EPSILON)
    pull = scale_own * scale_own * scale_own * (mean / width)

    @pl.loop(0, width // tile)
    def _(at):
        cols = tile_of(at)
        dn2, h1 = dh1_ref[:, cols], h1_ref[:, cols]
        dgain_ref[:, cols] = jnp.sum(dn2 * h1 * scale_own, axis=0, keepdims=True)
        dy = dy_all[0, pl.ds(rows, rows), cols].astype(F32)
        d_resid = dy + scale_own * (gain_ref[:, cols] * dn2) - h1 * pull
        dh1_ref[:, cols] = d_resid
        low_ref[:, cols] = d_resid.astype(BF)

    def da_copy(hop):
        return passing(
            da_part.at[hop], da_ref.at[span(place)], (da_send, da_recv), hop, member(hop)[1]
        )

    low = low_ref[...]

    @pl.loop(1, count)
    def _(hop):
        spot = member(hop)[0]
        da_part[hop] = cols_inner(low, out_w[tile_of(spot, size)]).astype(BF)
        da_copy(hop).start()

    da_ref[span(place)] = cols_inner(low, out_w[tile_of(place, size)]).astype(BF)

    @pl.loop(1, count)
    def _(hop):
        da_copy(hop).wait_recv()
        da_copy(hop).wait_send()

    for flow, held in ((0, ahead_ref), (1, behind_ref)):
        next_copies[flow].wait_recv()
        held[...] = add_low(held[...], mlp_got[2 + flow])
    for copy in (*far_copies, *next_copies, *first_copies()):
        copy.wait_send()
    for step in range(1, steps):
        for copy in later_copies(step):
            copy.wait_send()
    for group in range(steps - 2, steps):
        for copy in stores(group, group % 2):
            copy.wait()
    for at in range(2):
        dmlp_copy(mlp_tiles - 2 + at, (mlp_tiles + at) % 2).wait()
        ddown_copy(down_tiles - 2 + at, (down_tiles + at) % 2).wait()


def mlp_back(tokens, mixed, dy, gain, out_w, gate_w, up_w, down_w, collective_id):
    count = lax.axis_size("head")
    total, width = tokens.shape
    hidden = gate_w.shape[1]
    rows, steps = total // count, count // 2
    size = mixed.shape[1] // count
    inner = 256 if hidden % 256 == 0 else 128
    vmem = pl.BlockSpec(memory_space=pltpu.VMEM)
    hbm = pl.BlockSpec(memory_space=pl.ANY)

    def slots(many, tall, wide, dtype=BF):
        return pltpu.VMEM((many, tall, wide), dtype)

    def shape(*extent, dtype=BF):
        return jax.ShapeDtypeStruct(extent, dtype)

    dma = pltpu.SemaphoreType.DMA
    flops = 2 * total * width * (mixed.shape[1] + 9 * hidden)
    return pl.pallas_call(
        functools.partial(mlp_kernel, count),
        out_shape=[
            shape(total, width), shape(width, 2 * hidden), shape(hidden, width),
            shape(rows, width, dtype=F32), shape(rows, width, dtype=F32), shape(rows, width),
            shape(1, width, dtype=F32), shape(total, size), shape(rows, width), shape(rows, width),
        ],
        in_specs=[hbm] * 3 + [vmem] + [hbm] * 4,
        out_specs=[hbm] * 3 + [vmem] * 7,
        scratch_shapes=[
            slots(2, 2 * rows, width), slots(2, 2 * rows, mixed.shape[1]), slots(2, 2 * rows, width),
            pltpu.VMEM((2 * rows, width), F32),
            slots(steps, 2 * rows, width), slots(steps, 2 * rows, width),
            slots(steps, 2 * rows, hidden), slots(steps, 2 * rows, 2 * hidden),
            slots(2, 256, hidden), slots(2, inner, 512), slots(count, rows, size),
            pltpu.VMEM((rows, width), BF), slots(2, rows, width), slots(4, rows, width),
            slots(2, rows, width), slots(2, rows, width),
            slots(steps, rows, width), slots(steps, rows, width),
            *[pltpu.VMEM(weight.shape, BF) for weight in (out_w, gate_w, up_w, down_w)],
            dma((2, 6)), dma((2, 2)), dma((4,)), dma((4,)), dma((count,)), dma((count,)),
            dma((count,)), dma((count,)), dma((4,)), dma((4,)),
        ],
        compiler_params=pltpu.CompilerParams(
            collective_id=collective_id, has_side_effects=True, vmem_limit_bytes=VMEM_LIMIT
        ),
        cost_estimate=pl.CostEstimate(flops=flops, bytes_accessed=40 << 20, transcendentals=0),
        name="mlp_back",
    )(tokens, mixed, dy, gain, out_w, gate_w, up_w, down_w)


def entry_kernel(
    count, batches, x_ref, w_ref, out_ref, gain_ref, seg_ref,
    n1_ref, q_ref, logit_ref, kv_ref, w_all, out_all, gain_all, seg_all,
    send_sem, recv_sem, local_sem,
):
    steps = count // 2
    others = batches // 2
    rows, width = x_ref.shape
    depth = w_ref.shape[0]
    size, wide = out_ref.shape
    block = 256
    place, right, left = ring_setup(count)
    head = lax.axis_index("head")
    batch = lax.axis_index("batch")
    across, core, low = batch // 2, lax.rem(batch, 2), lax.rem(head, 2)
    twin = (across * 2 + 1 - core, head)
    mate = (batch, head + 1 - 2 * low)
    spots = [lax.rem(across + hop, others) for hop in range(others)]
    backs = [lax.rem(across + others - hop, others) for hop in range(others)]
    peers = [(spot * 2 + core, head) for spot in spots]
    far_peers = [(spot * 2 + 1 - core, head) for spot in spots]
    greet((twin, mate, right, left, *peers[1:], *far_peers[1:]))
    sems = (send_sem, recv_sem)
    slot = 0
    copies = []

    def go(source, target, device):
        nonlocal slot
        copy = send(source, target, sems, slot, device)
        slot += 1
        copies.append(copy)
        return copy

    def part(at, extent):
        return pl.ds(pl.multiple_of(at * extent, extent), extent)

    def both(view, own):
        out = [go(own, view(batch), peers[hop]) for hop in range(1, others)]
        return out, [go(own, view(batch), twin)]

    def pass_on(view, arrived):
        out = []
        for hop in range(1, others):
            arrived[hop - 1].wait_recv()
            there = view(backs[hop] * 2 + core)
            out.append(go(there, there, twin))
        return out

    local = []

    def stay(source, target):
        copy = pltpu.make_async_copy(source, target, local_sem.at[len(local)])
        copy.start()
        local.append(copy)

    def main_view(at):
        return w_all.at[part(at, depth), pl.ds(0, 3 * size)]

    def mate_view(at):
        return w_all.at[part(at, depth), pl.ds(3 * size, size)]

    def out_view(chunk, at):
        return out_all.at[part(chunk, size), part(at, wide)]

    small = []
    for own, whole in ((gain_ref, gain_all), (seg_ref, seg_all)):
        for device in (twin, *peers[1:], *far_peers[1:]):
            small.append(go(own, whole.at[batch], device))
        stay(own, whole.at[batch])
    from_mate = go(w_ref.at[:, pl.ds(2 * size, size)], mate_view(batch), mate)
    main_out, main_twin = both(main_view, w_ref)
    stay(w_ref, main_view(batch))
    out_peers = [go(out_ref, out_view(place, batch), peers[hop]) for hop in range(1, others)]
    stay(out_ref, out_view(place, batch))
    flows = [[None, None] for _ in range(others)]

    def ring(step):
        for hop in range(others):
            lane = spots[0] if hop == 0 else backs[hop]
            at = lane * 2 + core
            if step == 0 and hop:
                out_peers[hop - 1].wait_recv()
            for flow, chunk, device in ((0, place - step, right), (1, place + step, left)):
                if step:
                    flows[hop][flow].wait_recv()
                target = out_view(lax.rem(chunk + count, count), at)
                source = out_ref if step == 0 and hop == 0 else target
                if step == steps - 1:
                    cut = (pl.ds(flow * (size // 2), size // 2), slice(None))
                    source, target = source.at[cut], target.at[cut]
                flows[hop][flow] = go(source, target, device)

    for copy in small:
        copy.wait_recv()
    for copy in local[:2]:
        copy.wait()

    def normalize(at):
        here = part(at, block)

        def squares(tile, total):
            values = x_ref[here, part(tile, 256)].astype(F32)
            return total + jnp.sum(values * values, axis=1, keepdims=True)

        total = lax.fori_loop(0, width // 256, squares, jnp.zeros((block, 1), F32))
        scale = lax.rsqrt(total / width + EPSILON)

        @pl.loop(0, batches)
        def _(owner):
            for tile in range(depth // 128):
                cols = pl.ds(pl.multiple_of(owner * depth + tile * 128, 128), 128)
                values = x_ref[here, cols].astype(F32) * scale
                n1_ref[here, cols] = (values * gain_all[owner, pl.ds(tile, 1)]).astype(BF)

    blocks = rows // block
    middle = blocks // 2

    @pl.loop(0, middle)
    def _(at):
        normalize(at)

    from_mate.wait_recv()
    mate_out, mate_twin = both(mate_view, mate_view(batch))
    ring(0)

    @pl.loop(middle, blocks)
    def _(at):
        normalize(at)

    main_passed = pass_on(main_view, main_out)
    mate_passed = pass_on(mate_view, mate_out)
    for copy in (*main_twin, *mate_twin, *main_passed, *mate_passed):
        copy.wait_recv()
    for copy in local[2:]:
        copy.wait()

    def kv_view(at):
        return kv_ref.at[part(at, rows)]

    @pl.loop(0, blocks)
    def _(at):
        here = part(at, block)
        values = matmul(n1_ref[here], w_all[:, pl.ds(2 * size, 2 * size)])
        one, two = values[:, :size], values[:, size:]
        first = jnp.where(low == 0, one, two).astype(BF)
        second = jnp.where(low == 0, two, one).astype(BF)
        half = size // 2
        there = pl.ds(pl.multiple_of(batch * rows + at * block, block), block)
        kv_ref[there, pl.ds(0, size)] = jnp.concatenate([first[:, :half], second[:, :half]], 1)
        kv_ref[there, pl.ds(size, size)] = jnp.concatenate([first[:, half:], second[:, half:]], 1)

    kv_out, kv_twin = both(kv_view, kv_view(batch))
    ring(1)

    @pl.loop(0, blocks)
    def _(at):
        here = part(at, block)
        values = matmul(n1_ref[here], w_all[:, pl.ds(0, 2 * size)])
        q_ref[here] = values[:, :size].astype(BF)
        logit_ref[here] = values[:, size:]

    for step in range(2, steps):
        ring(step)
    kv_passed = pass_on(kv_view, kv_out)
    for pair in flows:
        for copy in pair:
            copy.wait_recv()
    swaps = []
    for hop in range(others):
        there = out_all.at[:, part(spots[hop] * 2 + core, wide)]
        swaps.append(go(there, there, twin))
    for copy in (*kv_twin, *kv_passed, *swaps):
        copy.wait_recv()
    for copy in copies:
        copy.wait_send()


def entry(tokens, w_shard, w_out, gains, segments, collective_id):
    count = lax.axis_size("head")
    batches = lax.axis_size("batch")
    others = batches // 2
    rows, width = tokens.shape
    size, wide = w_out.shape
    vmem = pl.BlockSpec(memory_space=pltpu.VMEM)
    slots = 6 * batches + others * (count + 3)
    sems = pltpu.SemaphoreType.DMA((slots,))
    return pl.pallas_call(
        functools.partial(entry_kernel, count, batches),
        out_shape=[
            jax.ShapeDtypeStruct((rows, width), BF),
            jax.ShapeDtypeStruct((rows, size), BF),
            jax.ShapeDtypeStruct((rows, size), F32),
            jax.ShapeDtypeStruct((batches * rows, 2 * size), BF),
            jax.ShapeDtypeStruct((width, 4 * size), BF),
            jax.ShapeDtypeStruct((count * size, batches * wide), BF),
            jax.ShapeDtypeStruct((batches, *gains.shape), F32),
            jax.ShapeDtypeStruct((batches, *segments.shape), jnp.int32),
        ],
        in_specs=[vmem] * 5,
        out_specs=[vmem] * 8,
        scratch_shapes=[sems, sems, pltpu.SemaphoreType.DMA((5,))],
        compiler_params=pltpu.CompilerParams(
            collective_id=collective_id, has_side_effects=True, vmem_limit_bytes=VMEM_LIMIT
        ),
        name="entry",
    )(tokens, w_shard, w_out, gains, segments)


KEY_BLOCK = 512
QUERY_BLOCK = 256


def key_range(start_ref, base, query_block):
    first = query_block * QUERY_BLOCK
    lowest = start_ref[first]
    highest = start_ref[first + QUERY_BLOCK - 1]
    begin = lowest // KEY_BLOCK
    end = (base + first + QUERY_BLOCK - 1) // KEY_BLOCK + 1
    full_begin = jnp.minimum((highest + KEY_BLOCK - 1) // KEY_BLOCK, end)
    full_end = jnp.maximum((base + first + 1) // KEY_BLOCK, full_begin)
    return begin, full_begin, full_end, end


def allowed_pairs(key_block, start_row, base_row):
    shape = (KEY_BLOCK, QUERY_BLOCK)
    key_pos = key_block * KEY_BLOCK + lax.broadcasted_iota(jnp.int32, shape, 0)
    query_pos = base_row + lax.broadcasted_iota(jnp.int32, shape, 1)
    return (key_pos >= start_row) & (key_pos <= query_pos)


def attend_kernel(
    scale, start_sm, base_sm, q_ref, kv_ref, start_ref, logit_ref, o_ref, a_ref, lse_ref
):
    base = base_sm[0]
    size = q_ref.shape[1]
    factor = scale * math.log2(math.e)

    @pl.loop(0, q_ref.shape[0] // QUERY_BLOCK)
    def _(block):
        rows = pl.ds(pl.multiple_of(block * QUERY_BLOCK, QUERY_BLOCK), QUERY_BLOCK)
        queries = q_ref[rows]
        start_row = start_ref[:, rows]
        begin, full_begin, full_end, end = key_range(start_sm, base, block)

        def step(masked, at, state):
            old_max, old_sum, total = state
            keys = pl.ds(pl.multiple_of(at * KEY_BLOCK, KEY_BLOCK), KEY_BLOCK)
            scores = cols_inner(kv_ref[keys, :size], queries)
            if masked:
                allowed = allowed_pairs(at, start_row, base + block * QUERY_BLOCK)
                scores = jnp.where(allowed, scores, MASKED)
            new_max = jnp.maximum(old_max, jnp.max(scores, axis=0, keepdims=True))
            keep = jnp.exp2((old_max - new_max) * factor)
            weights = jnp.exp2(scores * factor - new_max * factor)
            new_sum = old_sum * keep + jnp.sum(weights, axis=0, keepdims=True)
            total = total * keep + rows_inner(kv_ref[keys, size:], weights.astype(BF))
            return new_max, new_sum, total

        state = (
            jnp.full((1, QUERY_BLOCK), MASKED, F32),
            jnp.zeros((1, QUERY_BLOCK), F32),
            jnp.zeros((size, QUERY_BLOCK), F32),
        )
        state = lax.fori_loop(begin, full_begin, functools.partial(step, True), state)
        state = lax.fori_loop(full_begin, full_end, functools.partial(step, False), state)
        state = lax.fori_loop(full_end, end, functools.partial(step, True), state)
        run_max, run_sum, total = state
        lse_ref[:, rows] = run_max * factor + jnp.log2(run_sum)
        attended = (total / run_sum).T
        o_ref[rows] = attended
        a_ref[rows] = (attended * jax.nn.sigmoid(logit_ref[rows])).astype(BF)


def attend_back_kernel(
    scale, start_sm, base_sm, q_ref, kv_ref, start_ref, logit_ref, o_ref, da_ref, lse_ref,
    dq_ref, dg_ref, dkv_ref, dk_acc, dv_acc,
):
    base = base_sm[0]
    size = q_ref.shape[1]
    factor = scale * math.log2(math.e)
    dk_acc[...] = jnp.zeros_like(dk_acc)
    dv_acc[...] = jnp.zeros_like(dv_acc)

    @pl.loop(0, q_ref.shape[0] // QUERY_BLOCK)
    def _(block):
        rows = pl.ds(pl.multiple_of(block * QUERY_BLOCK, QUERY_BLOCK), QUERY_BLOCK)
        queries = q_ref[rows]
        start_row = start_ref[:, rows]
        lse = lse_ref[:, rows]
        gate = jax.nn.sigmoid(logit_ref[rows])
        attended = o_ref[rows]
        d_mixed = da_ref[rows].astype(F32)
        d_attended = (d_mixed * gate).astype(BF)
        dg_ref[rows] = (d_mixed * attended * gate * (1.0 - gate)).astype(BF)
        delta = jnp.sum((d_attended.astype(F32) * attended).T, axis=0, keepdims=True)
        begin, full_begin, full_end, end = key_range(start_sm, base, block)

        def step(masked, at, d_queries):
            keys = pl.ds(pl.multiple_of(at * KEY_BLOCK, KEY_BLOCK), KEY_BLOCK)
            key_block = kv_ref[keys, :size]
            probs = jnp.exp2(cols_inner(key_block, queries) * factor - lse)
            if masked:
                allowed = allowed_pairs(at, start_row, base + block * QUERY_BLOCK)
                probs = jnp.where(allowed, probs, 0.0)
            d_probs = cols_inner(kv_ref[keys, size:], d_attended)
            d_scores = (probs * (d_probs - delta) * scale).astype(BF)
            dv_acc[keys] += matmul(probs.astype(BF), d_attended)
            dk_acc[keys] += matmul(d_scores, queries)
            return d_queries + rows_inner(key_block, d_scores)

        d_queries = jnp.zeros((size, QUERY_BLOCK), F32)
        d_queries = lax.fori_loop(begin, full_begin, functools.partial(step, True), d_queries)
        d_queries = lax.fori_loop(full_begin, full_end, functools.partial(step, False), d_queries)
        d_queries = lax.fori_loop(full_end, end, functools.partial(step, True), d_queries)
        dq_ref[rows] = d_queries.T.astype(BF)

    @pl.loop(0, kv_ref.shape[0] // KEY_BLOCK)
    def _(at):
        keys = pl.ds(pl.multiple_of(at * KEY_BLOCK, KEY_BLOCK), KEY_BLOCK)
        dk, dv = dk_acc[keys].astype(BF), dv_acc[keys].astype(BF)
        half = size // 2
        dkv_ref[keys, :size] = jnp.concatenate([dk[:, :half], dv[:, :half]], axis=1)
        dkv_ref[keys, size:] = jnp.concatenate([dk[:, half:], dv[:, half:]], axis=1)


def fold_kernel(
    batches, part_ref, own_ref, core_got, x_first, x_second, y_first, y_second, held, send_sem, recv_sem
):
    rows, size = own_ref.shape
    half = rows // 2
    others = batches // 2
    head = lax.axis_index("head")
    batch = lax.axis_index("batch")
    across, core, low = batch // 2, lax.rem(batch, 2), lax.rem(head, 2)
    twin = (across * 2 + 1 - core, head)
    mate = (batch, head + 1 - 2 * low)
    spots = [lax.rem(across + hop, others) for hop in range(others)]
    peers = [(spot * 2 + core, head) for spot in spots]
    greet((twin, mate, *peers[1:]))
    sems = (send_sem, recv_sem)
    slot = 0
    copies = []
    mine = pl.ds(pl.multiple_of(low * size, size), size)
    given = pl.ds(pl.multiple_of((1 - low) * size, size), size)
    top, bottom = pl.ds(0, half), pl.ds(half, half)

    def block(at, side):
        return pl.ds(pl.multiple_of((2 * at + side) * rows, rows), rows)

    def go(source, target, device):
        nonlocal slot
        copy = send(source, target, sems, slot, device)
        slot += 1
        copies.append(copy)
        return copy

    order = list(range(1, others)) + [0]
    first = [go(part_ref.at[block(spots[hop], 1 - core)], core_got.at[spots[hop]], twin) for hop in order]
    tops, bottoms = [], []
    for copy, hop in zip(first, order):
        copy.wait_recv()
        spot = spots[hop]
        core_got[spot] = add_low(core_got[spot], part_ref[block(spot, core)])
        bottoms.append(go(core_got.at[spot, bottom, given], y_first.at[spot], mate))
        if hop:
            tops.append(go(core_got.at[spot, top], x_first.at[hop - 1], peers[hop]))
    total = core_got[across, top].astype(F32)
    for hop in range(1, others):
        tops[hop - 1].wait_recv()
        total = total + x_first[hop - 1].astype(F32)
    held[...] = total.astype(BF)
    last = go(held.at[:, given], y_second, mate)
    ends = []
    for copy, hop in zip(bottoms, order):
        copy.wait_recv()
        spot = spots[hop]
        y_first[spot] = add_low(y_first[spot], core_got[spot, bottom, mine])
        if hop:
            ends.append(go(y_first.at[spot], x_second.at[hop - 1], peers[hop]))
    last.wait_recv()
    own_ref[top] = add_low(held[:, mine], y_second[...])
    total = y_first[across].astype(F32)
    for hop in range(1, others):
        ends[hop - 1].wait_recv()
        total = total + x_second[hop - 1].astype(F32)
    own_ref[bottom] = total.astype(BF)
    for copy in copies:
        copy.wait_send()


def fold(part, rows, collective_id):
    batches = lax.axis_size("batch")
    others = batches // 2
    size = part.shape[1] // 2
    half = rows // 2
    vmem = pl.BlockSpec(memory_space=pltpu.VMEM)
    sems = pltpu.SemaphoreType.DMA((4 * others,))
    return pl.pallas_call(
        functools.partial(fold_kernel, batches),
        out_shape=jax.ShapeDtypeStruct((rows, size), BF),
        in_specs=[vmem],
        out_specs=vmem,
        scratch_shapes=[
            pltpu.VMEM((others, rows, 2 * size), BF),
            pltpu.VMEM((others - 1, half, 2 * size), BF),
            pltpu.VMEM((others - 1, half, size), BF),
            pltpu.VMEM((others, half, size), BF),
            pltpu.VMEM((half, size), BF),
            pltpu.VMEM((half, 2 * size), BF),
            sems,
            sems,
        ],
        compiler_params=pltpu.CompilerParams(
            collective_id=collective_id, has_side_effects=True, vmem_limit_bytes=VMEM_LIMIT
        ),
        name="fold",
    )(part)


def tail_kernel(
    count, batches, cat_ref, w_ref, x_ref, gain_ref, dh1_ref, second_ref,
    n1_ref, mixed_ref, low_ref, out_0,
    out_all, tok_all, gains_ref, wout_own, din_ref,
    part_ref, tok_ref, got, wout_got, gain_own, gain_got, gain_mid, gain_heads,
    din_s, din_got, din_x, wout_s, wout_twin, wout_x, wout_part,
    send_sem, recv_sem, local_sem,
):
    steps = count // 2
    rows, width = x_ref.shape
    depth = cat_ref.shape[1]
    tile = 256
    place, right, left = ring_setup(count)
    batch, head = lax.axis_index("batch"), lax.axis_index("head")
    others = [lax.rem(batch + hop, batches) for hop in range(1, batches)]
    members = [(batch, ring_head(lax.rem(place + hop, count), count)) for hop in range(1, count)]
    greet((*members, *[(other, head) for other in others]))
    sems = (send_sem, recv_sem)
    slot = 0
    copies = []

    def go(source, target, device):
        nonlocal slot
        copy = send(source, target, sems, slot, device)
        slot += 1
        copies.append(copy)
        return copy

    across, core = batch // 2, lax.rem(batch, 2)
    spots = [lax.rem(across + hop, batches // 2) for hop in range(batches // 2)]
    order = list(range(1, batches // 2)) + [0]
    twin = (across * 2 + 1 - core, head)

    def scatter_swap(view, held):
        return [go(view(2 * spots[hop] + 1 - core), held.at[spots[hop]], twin) for hop in order]

    def add_tiles(target, one, other):
        @pl.loop(0, target.shape[0] // 128)
        def _(at):
            lines = pl.ds(pl.multiple_of(at * 128, 128), 128)
            total = one[lines].astype(F32) + other[lines].astype(F32)
            target[lines] = total.astype(target.dtype)

    def scatter_cross(view, held, crossed, arriving):
        out = []
        for copy, hop in zip(arriving, order):
            copy.wait_recv()
            spot = spots[hop]
            add_tiles(held.at[spot], held.at[spot], view(2 * spot + core))
            if hop:
                out.append(go(held.at[spot], crossed.at[hop - 1], (spot * 2 + core, head)))
        return out

    def scatter_end(held, crossed, arriving, target):
        for hop, copy in enumerate(arriving):
            copy.wait_recv()
            last = hop == len(arriving) - 1
            add_tiles(target if last else held.at[across], held.at[across], crossed.at[hop])

    def wout_view(at):
        wide = wout_part.shape[1]
        return wout_s.at[:, pl.ds(pl.multiple_of(at * wide, wide), wide)]

    def din_view(at):
        tall = din_ref.shape[0]
        return din_s.at[pl.ds(pl.multiple_of(at * tall, tall), tall)]

    def span(owner, extent):
        return pl.ds(pl.multiple_of(lax.rem(owner + count, count) * extent, extent), extent)

    def compute(owner):
        here = span(owner, rows)
        values = cat_ref[here]

        @pl.loop(0, width // tile)
        def _(at):
            cols = pl.ds(pl.multiple_of(at * tile, tile), tile)
            part_ref[here, cols] = cols_inner(values, w_ref[cols, pl.ds(0, depth)]).astype(BF)

    def gather(own, whole, step, last):
        out = []
        for flow, chunk, device in ((0, place - step, right), (1, place + step, left)):
            if last:
                last[flow].wait_recv()
            target = whole.at[lax.rem(chunk + count, count)]
            source = target if step else own
            if step == steps - 1:
                cut = (slice(None), pl.ds(flow * (width // 2), width // 2))
                source, target = source.at[cut], target.at[cut]
            out.append(go(source, target, device))
        return out

    def reduce(parts, held, step, last):
        extent, side = held.shape[2], held.shape[3] // 2
        out = []
        for flow, owner, device in (
            (0, place + steps - step, right),
            (1, place - steps + step, left),
        ):
            have = pl.ds(flow * side, side)
            lack = pl.ds((1 - flow) * side, side)
            mine = parts.at[span(owner, extent)]
            if step == 0:
                out.append(go(mine.at[:, have], held.at[flow, 0, :, have], device))
                continue
            last[flow].wait_recv()
            if step == 1:
                held[flow, 0, :, have] = add_low(held[flow, 0, :, have], mine[:, have])
                held[flow, 0, :, lack] = mine[:, lack]
            else:
                held[flow, step - 1] = add_low(held[flow, step - 1], mine[...])
            out.append(go(held.at[flow, step - 1], held.at[flow, step], device))
        return out

    keep_out = pltpu.make_async_copy(out_0, out_all.at[place], local_sem.at[0])
    keep_out.start()
    compute(place + steps)
    sums = reduce(part_ref, got, 0, None)
    outs = gather(out_0, out_all, 0, None)

    @pl.loop(1, count)
    def _(hop):
        compute(place + steps + hop)

    @pl.loop(0, width // tile)
    def _(at):
        cols = pl.ds(pl.multiple_of(at * tile, tile), tile)
        wout_s[:, cols] = rows_inner(mixed_ref[...], low_ref[:, cols]).astype(BF)

    wouts = scatter_swap(wout_view, wout_twin)

    @pl.loop(0, width // tile)
    def _(at):
        cols = pl.ds(pl.multiple_of(at * tile, tile), tile)
        din_s[cols] = rows_inner(n1_ref[:, cols], cat_ref[...]).astype(BF)

    dins = scatter_swap(din_view, din_got)
    for step in range(1, steps):
        sums = reduce(part_ref, got, step, sums)
        outs = gather(out_0, out_all, step, outs)
        if step == 1:
            wouts = scatter_cross(wout_view, wout_twin, wout_x, wouts)
            dins = scatter_cross(din_view, din_got, din_x, dins)
    for copy in sums:
        copy.wait_recv()

    def tile_of(at):
        return pl.ds(pl.multiple_of(at * tile, tile), tile)

    def total(cols):
        return (
            part_ref[span(place, rows), cols].astype(F32)
            + got[0, steps - 1, :, cols].astype(F32)
            + got[1, steps - 1, :, cols].astype(F32)
        )

    def collect(at, state):
        squares, mean = state
        cols = tile_of(at)
        x = x_ref[:, cols].astype(F32)
        squares = squares + jnp.sum(x * x, axis=1, keepdims=True)
        return squares, mean + jnp.sum(gain_ref[:, cols] * total(cols) * x, axis=1, keepdims=True)

    zero = jnp.zeros((rows, 1), F32)
    squares, mean = lax.fori_loop(0, width // tile, collect, (zero, zero))
    scale = lax.rsqrt(squares / width + EPSILON)
    pull = scale * scale * scale * (mean / width)

    @pl.loop(0, width // tile)
    def _(at):
        cols = tile_of(at)
        x, dn1 = x_ref[:, cols].astype(F32), total(cols)
        gain_own[pl.ds(0, 1), cols] = jnp.sum(dn1 * x * scale, axis=0, keepdims=True)
        gain_own[pl.ds(1, 1), cols] = second_ref[:, cols]
        tok_ref[:, cols] = (dh1_ref[:, cols] + scale * (gain_ref[:, cols] * dn1) - x * pull).astype(BF)

    keep_tok = pltpu.make_async_copy(tok_ref, tok_all.at[place], local_sem.at[1])
    keep_tok.start()
    toks = gather(tok_ref, tok_all, 0, None)
    scatter_end(wout_twin, wout_x, wouts, wout_part)
    wsums = reduce(wout_part, wout_got, 0, None)
    scatter_end(din_got, din_x, dins, din_ref)
    wide = width // batches

    def slice_of(at):
        return pl.ds(pl.multiple_of(at * wide, wide), wide)

    gains = [
        go(gain_own.at[:, slice_of(other)], gain_got.at[hop], (other, head))
        for hop, other in enumerate(others)
    ]
    toks = gather(tok_ref, tok_all, 1, toks)
    wsums = reduce(wout_part, wout_got, 1, wsums)
    middle = gain_own[:, slice_of(batch)]
    for hop, copy in enumerate(gains):
        copy.wait_recv()
        middle = middle + gain_got[hop]
    gain_mid[...] = middle
    gain_heads[place] = middle
    gains = [go(gain_mid, gain_heads.at[place], member) for member in members]
    for step in range(2, steps):
        toks = gather(tok_ref, tok_all, step, toks)
        wsums = reduce(wout_part, wout_got, step, wsums)
    for copy in gains:
        copy.wait_recv()
    middle = gain_heads[0]
    for at in range(1, count):
        middle = middle + gain_heads[at]
    gains_ref[...] = middle
    for copy in (*wsums, *outs):
        copy.wait_recv()
    wout_own[...] = (
        wout_part[span(place, wout_own.shape[0])].astype(F32)
        + wout_got[0, steps - 1].astype(F32)
        + wout_got[1, steps - 1].astype(F32)
    )
    for copy in toks:
        copy.wait_recv()
    for copy in copies:
        copy.wait_send()
    keep_out.wait()
    keep_tok.wait()


def tail(d_cat, w_in, x_own, gain, d_resid, second, normed, mixed, low, out_own, collective_id):
    count = lax.axis_size("head")
    batches = lax.axis_size("batch")
    steps = count // 2
    rows, width = x_own.shape
    others = batches // 2
    size, wide = mixed.shape[1] // count, width // batches
    depth = d_cat.shape[1]
    vmem = pl.BlockSpec(memory_space=pltpu.VMEM)
    whole = (count, rows, width)
    sems = pltpu.SemaphoreType.DMA((5 * count + 3 * batches,))
    gains = (2, width // batches)
    return pl.pallas_call(
        functools.partial(tail_kernel, count, batches),
        out_shape=[
            jax.ShapeDtypeStruct(whole, BF),
            jax.ShapeDtypeStruct(whole, BF),
            jax.ShapeDtypeStruct(gains, F32),
            jax.ShapeDtypeStruct((size, wide), F32),
            jax.ShapeDtypeStruct((wide, depth), F32),
        ],
        in_specs=[vmem] * 10,
        out_specs=[vmem] * 5,
        scratch_shapes=[
            pltpu.VMEM((count * rows, width), BF),
            pltpu.VMEM((rows, width), BF),
            pltpu.VMEM((2, steps, rows, width), BF),
            pltpu.VMEM((2, steps, size, wide), BF),
            pltpu.VMEM((2, width), F32),
            pltpu.VMEM((batches - 1, *gains), F32),
            pltpu.VMEM(gains, F32),
            pltpu.VMEM((count, *gains), F32),
            pltpu.VMEM((width, depth), BF),
            pltpu.VMEM((others, wide, depth), BF),
            pltpu.VMEM((others - 1, wide, depth), BF),
            pltpu.VMEM((count * size, width), BF),
            pltpu.VMEM((others, count * size, wide), BF),
            pltpu.VMEM((others - 1, count * size, wide), BF),
            pltpu.VMEM((count * size, wide), BF),
            sems,
            sems,
            pltpu.SemaphoreType.DMA((2,)),
        ],
        compiler_params=pltpu.CompilerParams(
            collective_id=collective_id, has_side_effects=True, vmem_limit_bytes=(32 << 20) + 4 * count * size * width
        ),
        cost_estimate=pl.CostEstimate(
            flops=2 * count * rows * width * d_cat.shape[1], bytes_accessed=400 << 20, transcendentals=0
        ),
        name="tail",
    )(d_cat, w_in, x_own, gain, d_resid, second, normed, mixed, low, out_own)


def local_call(kernel, scalars, arrays, outs, scratch, flops, name):
    vmem = pl.BlockSpec(memory_space=pltpu.VMEM)
    smem = pl.BlockSpec(memory_space=pltpu.SMEM)
    return pl.pallas_call(
        kernel,
        out_shape=outs,
        in_specs=[smem] * len(scalars) + [vmem] * len(arrays),
        out_specs=[vmem] * len(outs),
        scratch_shapes=scratch,
        compiler_params=pltpu.CompilerParams(vmem_limit_bytes=VMEM_LIMIT),
        cost_estimate=pl.CostEstimate(flops=flops, bytes_accessed=8 << 20, transcendentals=0),
        name=name,
    )(*scalars, *arrays)


def ring_routes(count):
    spots = [ring_head(at, count) for at in range(count)]
    right = [(spots[at], spots[(at + 1) % count]) for at in range(count)]
    left = [(spots[at], spots[at - 1]) for at in range(count)]
    return right, left


def add_low(one, other):
    return (one.astype(F32) + other.astype(F32)).astype(BF)


def flow_steps(part, going, coming):
    count = lax.axis_size("head")
    place = ring_place(lax.axis_index("head"), count)
    right, left = ring_routes(count)
    rows = part.shape[0] // count
    steps = count // 2

    def mine(owner):
        return lax.dynamic_slice_in_dim(part, lax.rem(owner + count, count) * rows, rows, 0)

    for step in range(2, steps - 1):
        from_left = lax.ppermute(going, "head", right)
        from_right = lax.ppermute(coming, "head", left)
        going = add_low(from_left, mine(place + steps - 1 - step))
        coming = add_low(from_right, mine(place - steps + 1 + step))
        going, coming = yield going, coming
    from_left = lax.ppermute(going, "head", right)
    from_right = lax.ppermute(coming, "head", left)
    yield mine(place).astype(F32) + from_left.astype(F32) + from_right.astype(F32)


def matmul(left, right):
    return jnp.dot(left, right, preferred_element_type=F32)


def rows_inner(left, right):
    return lax.dot_general(left, right, (((0,), (0,)), ((), ())), preferred_element_type=F32)


def cols_inner(left, right):
    return lax.dot_general(left, right, (((1,), (1,)), ((), ())), preferred_element_type=F32)


def rms_scale(values):
    return lax.rsqrt(jnp.mean(values * values, axis=1, keepdims=True) + EPSILON)


def per_device(
    tokens,
    segment_ids,
    norm1_gain,
    w_query,
    w_key,
    w_value,
    w_gate,
    w_out,
    norm2_gain,
    w_mlp_gate,
    w_mlp_up,
    w_down,
    out_grad,
):
    heads = lax.axis_size("head")
    batches = lax.axis_size("batch")
    row_count, width = tokens.shape
    head_size = w_query.shape[1]
    half = w_key.shape[1]
    chunk = row_count // heads
    me = ring_place(lax.axis_index("head"), heads)
    scale_factor = 1.0 / math.sqrt(head_size)

    w_shard = jnp.concatenate([w_query, w_gate, w_key, w_value], axis=1)
    gains = jnp.concatenate([norm1_gain, norm2_gain]).reshape(-1, 128).astype(F32)
    normed_one, queries, gate_logit, kv_all, w_in, out_full, gains, seg_all = entry(
        tokens, w_shard, w_out, gains, segment_ids.reshape(-1, 128), 1
    )
    gains, w_mlp_gate = lax.optimization_barrier((gains, w_mlp_gate))
    seg_all = seg_all.reshape(-1)
    gains = gains.reshape(batches, 2, -1).transpose(1, 0, 2).reshape(2, width)
    gain_one, gain_two = gains[0], gains[1]
    mgate_full = lax.all_gather(w_mlp_gate, "batch", axis=0, tiled=True)

    base = lax.axis_index("batch") * row_count
    ids = jnp.arange(DOCUMENTS, dtype=jnp.int32)
    below = jnp.sum((seg_all[None, :] < ids[:, None]).astype(jnp.int32), axis=1)
    starts = jnp.sum(jnp.where(segment_ids[None, :] == ids[:, None], below[:, None], 0), axis=0)
    scalars = (starts, base.reshape(1))
    pair_flops = 4 * row_count * kv_all.shape[0] * head_size
    attended, mixed, lse = local_call(
        functools.partial(attend_kernel, scale_factor),
        scalars,
        (queries, kv_all, starts[None], gate_logit),
        [
            jax.ShapeDtypeStruct((row_count, head_size), F32),
            jax.ShapeDtypeStruct((row_count, head_size), BF),
            jax.ShapeDtypeStruct((1, row_count), F32),
        ],
        [],
        pair_flops,
        "attend",
    )
    mixed_all, down_full, mup_full = spread(
        [mixed, w_down, w_mlp_up], (("head", "cols"), ("batch", "cols"), ("batch", "rows")), 2
    )
    (
        mlp_part, d_mlp, d_down, resid_own, d_resid, d_resid_low, d_gain_two, d_mixed, going, coming,
    ) = mlp_back(
        tokens, mixed_all, out_grad, gain_two[None], out_full, mgate_full, mup_full, down_full, 3
    )
    hold = lax.optimization_barrier
    mixed_own = lax.dynamic_slice_in_dim(mixed_all, me * chunk, chunk, 0)
    flow = flow_steps(mlp_part, going, coming)
    state = next(flow)

    d_queries, d_gate_logit, d_kv_all = local_call(
        functools.partial(attend_back_kernel, scale_factor),
        scalars,
        (queries, kv_all, starts[None], gate_logit, attended, d_mixed, lse),
        [
            jax.ShapeDtypeStruct((row_count, head_size), BF),
            jax.ShapeDtypeStruct((row_count, head_size), BF),
            jax.ShapeDtypeStruct(kv_all.shape, BF),
        ],
        [pltpu.VMEM((kv_all.shape[0], head_size), F32)] * 2,
        5 * pair_flops // 2,
        "attend_back",
    )
    d_kv_all, state = hold((d_kv_all, state))
    while isinstance(state, tuple):
        state = flow.send(state)
    d_kv = fold(d_kv_all, row_count, 4)
    d_kv, state, d_down, d_mlp = hold((d_kv, state, d_down, d_mlp))
    out_own = (resid_own + state).astype(BF)
    d_down = lax.psum_scatter(d_down, "batch", scatter_dimension=1, tiled=True)
    d_mlp = lax.psum_scatter(d_mlp, "batch", scatter_dimension=0, tiled=True)
    d_cat = jnp.concatenate([d_queries, d_gate_logit, d_kv], axis=1)
    inputs_own = lax.dynamic_slice_in_dim(tokens, me * chunk, chunk, 0)
    output, d_tokens, d_gains, d_out, d_in = tail(
        d_cat, w_in, inputs_own, gain_one[None], d_resid, d_gain_two, normed_one, mixed_own,
        d_resid_low, out_own, 5,
    )
    d_tokens, d_mlp, d_down = hold((d_tokens, d_mlp, d_down))
    d_mlp, d_down = d_mlp.astype(F32), d_down.astype(F32)
    output = output.reshape(row_count, width)
    d_tokens = d_tokens.reshape(row_count, width)
    hidden_own = w_mlp_gate.shape[1]
    return (
        output,
        d_tokens,
        d_gains[0],
        d_in[:, :head_size],
        d_in[:, 2 * head_size : 2 * head_size + half],
        d_in[:, 2 * head_size + half :],
        d_in[:, head_size : 2 * head_size],
        d_out,
        d_gains[1],
        d_mlp[:, :hidden_own],
        d_mlp[:, hidden_own:],
        d_down,
    )


def solution(mesh):
    return jax.shard_map(
        per_device,
        mesh=mesh,
        in_specs=(
            P("batch", None),
            P("batch"),
            P("batch"),
            P("batch", "head"),
            P("batch", "head"),
            P("batch", "head"),
            P("batch", "head"),
            P("head", "batch"),
            P("batch"),
            P("batch", "head"),
            P("batch", "head"),
            P("head", "batch"),
            P("batch", None),
        ),
        out_specs=(
            P("batch", None),
            P("batch", None),
            P("batch"),
            P("batch", "head"),
            P("batch", "head"),
            P("batch", "head"),
            P("batch", "head"),
            P("head", "batch"),
            P("batch"),
            P("batch", "head"),
            P("batch", "head"),
            P("head", "batch"),
        ),
        check_vma=False,
    )
```

```python
import functools
import math

import jax
import jax.numpy as jnp
from jax import lax
from jax.experimental import pallas as pl
from jax.experimental.pallas import tpu as pltpu
from jax.sharding import PartitionSpec as P

EPSILON = 1e-06
MASKED = -1e30
DOCUMENTS = 7
BF = jnp.bfloat16
F32 = jnp.float32


MESH = pl.DeviceIdType.MESH
VMEM_LIMIT = 60 << 20


def ring_place(head, count):
    high, low = head // 2, head % 2
    return (1 - low) * high + low * (count - 1 - high)


def ring_head(place, count):
    low = place // (count // 2)
    high = (1 - low) * place + low * (count - 1 - place)
    return 2 * high + low


def ring_setup(count):
    batch = lax.axis_index("batch")
    place = ring_place(lax.axis_index("head"), count)
    right = (batch, ring_head(lax.rem(place + 1, count), count))
    left = (batch, ring_head(lax.rem(place + count - 1, count), count))
    return place, right, left


def greet(devices):
    barrier = pltpu.get_barrier_semaphore()
    for device in devices:
        pl.semaphore_signal(barrier, inc=1, device_id=device, device_id_type=MESH)
    pl.semaphore_wait(barrier, len(devices))


def send(source, target, sems, slot, device):
    copy = pltpu.make_async_remote_copy(
        src_ref=source,
        dst_ref=target,
        send_sem=sems[0].at[slot],
        recv_sem=sems[1].at[slot],
        device_id=device,
        device_id_type=MESH,
    )
    copy.start()
    return copy


def half_of(extent, flow):
    if extent[1] % 256:
        return (pl.ds(flow * (extent[0] // 2), extent[0] // 2), slice(None))
    return (slice(None), pl.ds(flow * (extent[1] // 2), extent[1] // 2))


def place_of(whole, own, chunk, form):
    rows, wide = own.shape[-2:]
    if form == "lead":
        return whole.at[chunk]
    if form == "rows":
        return whole.at[pl.ds(pl.multiple_of(chunk * rows, rows), rows)]
    return whole.at[:, pl.ds(pl.multiple_of(chunk * wide, wide), wide)]


def spread_kernel(count, batches, plans, *refs):
    steps = count // 2
    arrays = len(plans)
    own_refs, all_refs = refs[:arrays], refs[arrays : 2 * arrays]
    send_sem, recv_sem, local_sem = refs[2 * arrays :]
    place, right, left = ring_setup(count)
    head = lax.axis_index("head")
    batch = lax.axis_index("batch")
    across, core = batch // 2, lax.rem(batch, 2)
    others = batches // 2
    twin = (across * 2 + 1 - core, head)
    peers = [(lax.rem(across + hop, others) * 2 + core, head) for hop in range(1, others)]
    ring = any(axis == "head" for axis, _ in plans)
    grid = any(axis == "batch" for axis, _ in plans)
    greet((right, left) * ring + (twin, *peers) * grid)
    sems = (send_sem, recv_sem)
    slot = 0
    waiting, arriving, local = [], [], []

    def go(source, target, device):
        nonlocal slot
        copy = send(source, target, sems, slot, device)
        slot += 1
        waiting.append(copy)
        return copy

    stages = []
    for index, (axis, form) in enumerate(plans):
        own, whole = own_refs[index], all_refs[index]
        spot = place if axis == "head" else batch
        copy = pltpu.make_async_copy(own, place_of(whole, own, spot, form), local_sem.at[index])
        copy.start()
        local.append(copy)
        if axis == "batch":
            stages.append(index)
    onward = []

    def stage():
        for copy, block in onward:
            copy.wait_recv()
            arriving.append(go(block, block, twin))
        onward.clear()
        if stages:
            index = stages.pop(0)
            own, whole, form = own_refs[index], all_refs[index], plans[index][1]
            mine = place_of(whole, own, batch, form)
            for hop, peer in enumerate(peers, 1):
                source = lax.rem(across + others - hop, others) * 2 + core
                onward.append((go(own, mine, peer), place_of(whole, own, source, form)))
            arriving.append(go(own, mine, twin))

    stage()
    copies = [None] * (2 * arrays)
    for step in range(steps):
        for index, (axis, form) in enumerate(plans):
            if axis != "head":
                continue
            own = own_refs[index]
            for flow, chunk, device in ((0, place - step, right), (1, place + step, left)):
                at = 2 * index + flow
                if step:
                    copies[at].wait_recv()
                chunk = lax.rem(chunk + count, count)
                target = place_of(all_refs[index], own, chunk, form)
                source = target if step else own
                if step == steps - 1:
                    part = half_of(own.shape, flow)
                    source = source.at[part]
                    target = target.at[part]
                copies[at] = go(source, target, device)
        if step == steps // 2:
            stage()
    while stages or onward:
        stage()
    for copy in copies:
        if copy is not None:
            arriving.append(copy)
    for copy in arriving:
        copy.wait_recv()
    for copy in waiting:
        copy.wait_send()
    for copy in local:
        copy.wait()


def spread(arrays, plans, collective_id):
    count = lax.axis_size("head")
    batches = lax.axis_size("batch")
    shapes = []
    slots = 0
    for array, (axis, form) in zip(arrays, plans):
        many = count if axis == "head" else batches
        slots += count if axis == "head" else batches - 1
        if form == "lead":
            shapes.append((many, *array.shape))
        elif form == "rows":
            shapes.append((many * array.shape[0], array.shape[1]))
        else:
            shapes.append((array.shape[0], many * array.shape[1]))
    hbm = pl.BlockSpec(memory_space=pl.ANY)
    return pl.pallas_call(
        functools.partial(spread_kernel, count, batches, plans),
        out_shape=[jax.ShapeDtypeStruct(shape, a.dtype) for shape, a in zip(shapes, arrays)],
        in_specs=[pl.BlockSpec(memory_space=pltpu.VMEM)] * len(arrays),
        out_specs=[hbm] * len(arrays),
        scratch_shapes=[
            pltpu.SemaphoreType.DMA((slots,)),
            pltpu.SemaphoreType.DMA((slots,)),
            pltpu.SemaphoreType.DMA((len(arrays),)),
        ],
        compiler_params=pltpu.CompilerParams(
            collective_id=collective_id, has_side_effects=True, vmem_limit_bytes=VMEM_LIMIT
        ),
        name=f"spread_{collective_id}",
    )(*arrays)


def mlp_kernel(
    count, x_hbm, a_hbm, dy_hbm, gain_ref, out_hbm, gate_hbm, up_hbm, down_hbm,
    mlp_hbm, dmlp_hbm, ddown_hbm, h1_ref, dh1_ref, low_ref, dgain_ref, da_ref, ahead_ref, behind_ref,
    x_s, a_s, mlp_s, h1_s, dy_all, n2_all, hid_all, grad_all, dmlp_s, ddown_s, da_part,
    mlp_far, mlp_next, mlp_got, right_part, left_part, right_got, left_got,
    out_w, gate_w, up_w, down_w, in_sem, out_sem, grad_sem, weight_sem,
    send_sem, recv_sem, da_send, da_recv, far_send, far_recv,
):
    steps = count // 2
    rows = x_hbm.shape[0] // count
    width = x_hbm.shape[1]
    hidden = gate_w.shape[1]
    weights = [
        pltpu.make_async_copy(source, target, weight_sem.at[index])
        for index, (source, target) in enumerate(
            ((out_hbm, out_w), (gate_hbm, gate_w), (up_hbm, up_w), (down_hbm, down_w))
        )
    ]
    side = width // 2
    tile = 256
    broad = 1024
    inner = 256 if hidden % 256 == 0 else 128
    size = da_ref.shape[1]
    place, right, left = ring_setup(count)

    def member(hop):
        spot = lax.rem(place + hop, count)
        return spot, (lax.axis_index("batch"), ring_head(spot, count))

    def owners(group):
        first = jnp.where(group == 0, 1, 0)
        one = lax.rem(place + steps - group, count)
        two = lax.rem(place - steps + group + first * steps + count, count)
        return one, two

    def span(owner):
        return pl.ds(pl.multiple_of(owner * rows, rows), rows)

    def tile_of(at, extent=tile):
        return pl.ds(pl.multiple_of(at * extent, extent), extent)

    def loads(group, slot):
        return [
            pltpu.make_async_copy(
                source.at[span(owner)],
                target.at[pl.ds(at * rows, rows)],
                in_sem.at[slot, 2 * index + at],
            )
            for index, (source, target) in enumerate(
                ((x_hbm, x_s.at[slot]), (a_hbm, a_s.at[slot]), (dy_hbm, dy_all.at[group]))
            )
            for at, owner in enumerate(owners(group))
        ]

    def stores(group, slot):
        return [
            pltpu.make_async_copy(
                mlp_s.at[slot, pl.ds(at * rows, rows)], mlp_hbm.at[span(owner)], out_sem.at[slot, at]
            )
            for at, owner in enumerate(owners(group))
        ]

    def passing(source, target, sems, slot, device):
        return pltpu.make_async_remote_copy(
            src_ref=source,
            dst_ref=target,
            send_sem=sems[0].at[slot],
            recv_sem=sems[1].at[slot],
            device_id=device,
            device_id_type=MESH,
        )

    ring_sems, far_sems = (send_sem, recv_sem), (far_send, far_recv)
    ahead, behind = pl.ds(0, side), pl.ds(side, side)

    def first_copies():
        return (
            passing(right_part.at[0, :, ahead], right_got.at[0, :, ahead], ring_sems, 0, right),
            passing(right_part.at[0, :, behind], left_got.at[0, :, behind], ring_sems, steps, left),
        )

    def later_copies(step):
        return (
            passing(right_got.at[step - 1], right_got.at[step], ring_sems, step, right),
            passing(left_got.at[step - 1], left_got.at[step], ring_sems, steps + step, left),
        )

    for copy in (*loads(0, 0), *weights):
        copy.start()
    greet([member(hop)[1] for hop in range(1, count)])
    weights[0].wait()

    @pl.loop(0, steps)
    def _(group):
        slot = lax.rem(group, 2)
        for copy in loads(group, slot):
            copy.wait()

        @pl.when(group + 1 < steps)
        def _():
            for copy in loads(group + 1, 1 - slot):
                copy.start()

        @pl.when(group >= 2)
        def _():
            for copy in stores(group - 2, slot):
                copy.wait()

        mixed = a_s[slot]

        def residual(at, total):
            cols = tile_of(at, broad)
            values = x_s[slot, :, cols].astype(F32) + matmul(mixed, out_w[:, cols])
            h1_s[:, cols] = values
            return total + jnp.sum(values * values, axis=1, keepdims=True)

        total = lax.fori_loop(0, width // broad, residual, jnp.zeros((2 * rows, 1), F32))
        scale = lax.rsqrt(total / width + EPSILON)

        @pl.when(group == 0)
        def _():
            h1_ref[...] = h1_s[pl.ds(rows, rows)]
            for copy in weights[1:]:
                copy.wait()

        @pl.loop(0, width // tile)
        def _(at):
            cols = tile_of(at)
            n2_all[group, :, cols] = (h1_s[:, cols] * scale * gain_ref[:, cols]).astype(BF)

        normed = n2_all[group]
        dy = dy_all[group]

        @pl.loop(0, hidden // inner)
        def _(at):
            cols = tile_of(at, inner)
            cols_up = pl.ds(pl.multiple_of(hidden + at * inner, inner), inner)
            gate = matmul(normed, gate_w[:, cols])
            up = matmul(normed, up_w[:, cols])
            d_hidden = cols_inner(dy, down_w[cols])
            sig = jax.nn.sigmoid(gate)
            silu = gate * sig
            hid_all[group, :, cols] = (silu * up).astype(BF)
            grad_all[group, :, cols] = (d_hidden * up * sig * (1.0 + gate * (1.0 - sig))).astype(BF)
            grad_all[group, :, cols_up] = (d_hidden * silu).astype(BF)

        hid = hid_all[group]
        d_gate = grad_all[group, :, :hidden]
        d_up = grad_all[group, :, hidden:]
        half = jnp.minimum(group, 1)

        @pl.loop(0, width // broad)
        def _(at):
            cols = tile_of(at, broad)
            part = (cols_inner(d_gate, gate_w[cols]) + cols_inner(d_up, up_w[cols])).astype(BF)
            right_part[half, :, cols] = part[:rows]
            left_part[half, :, cols] = part[rows:]
            mlp_s[slot, :, cols] = matmul(hid, down_w[:, cols]).astype(BF)

        for copy in stores(group, slot):
            copy.start()

        @pl.when(group == 0)
        def _():
            mlp_far[...] = mlp_s[slot, pl.ds(0, rows)]
            for copy in first_copies():
                copy.start()

        @pl.when(group == 1)
        def _():
            mlp_next[0] = mlp_s[slot, pl.ds(0, rows)]
            mlp_next[1] = mlp_s[slot, pl.ds(rows, rows)]
            one, two = first_copies()
            one.wait_recv()
            right_got[0, :, ahead] = add_low(right_part[1, :, ahead], right_got[0, :, ahead])
            right_got[0, :, behind] = right_part[1, :, behind]
            two.wait_recv()
            left_got[0, :, behind] = add_low(left_part[1, :, behind], left_got[0, :, behind])
            left_got[0, :, ahead] = left_part[1, :, ahead]

        @pl.when(group == 2)
        def _():
            ahead_ref[...] = mlp_s[slot, pl.ds(0, rows)]
            behind_ref[...] = mlp_s[slot, pl.ds(rows, rows)]

        @pl.when(group >= 2)
        def _():
            one, two = later_copies(group - 1)
            one.wait_recv()
            right_got[group - 1] = add_low(right_part[1], right_got[group - 1])
            two.wait_recv()
            left_got[group - 1] = add_low(left_part[1], left_got[group - 1])

        @pl.when(group >= 1)
        def _():
            for copy in later_copies(group):
                copy.start()

    far_copies = [
        passing(mlp_far.at[:, ahead], mlp_got.at[0, :, ahead], far_sems, 0, right),
        passing(mlp_far.at[:, behind], mlp_got.at[1, :, behind], far_sems, 1, left),
    ]
    for copy in far_copies:
        copy.start()

    every = steps * 2 * rows

    def dmlp_copy(at, slot):
        return pltpu.make_async_copy(
            dmlp_s.at[slot], dmlp_hbm.at[tile_of(at // 2), tile_of(lax.rem(at, 2), hidden)], grad_sem.at[slot]
        )

    mlp_tiles = 2 * (width // tile)

    @pl.loop(0, mlp_tiles)
    def _(at):
        slot = lax.rem(at, 2)

        @pl.when(at >= 2)
        def _():
            dmlp_copy(at - 2, slot).wait()

        normed = n2_all[:, :, tile_of(at // 2)].reshape(every, tile)
        grads = grad_all[:, :, tile_of(lax.rem(at, 2), hidden)].reshape(every, hidden)
        dmlp_s[slot] = rows_inner(normed, grads).astype(BF)
        dmlp_copy(at, slot).start()

    wide = 512
    across = width // wide

    def ddown_copy(at, slot):
        return pltpu.make_async_copy(
            ddown_s.at[slot],
            ddown_hbm.at[tile_of(at // across, inner), tile_of(lax.rem(at, across), wide)],
            grad_sem.at[2 + slot],
        )

    down_tiles = across * (hidden // inner)

    @pl.loop(0, down_tiles)
    def _(at):
        slot = lax.rem(at, 2)

        @pl.when(at >= 2)
        def _():
            ddown_copy(at - 2, slot).wait()

        hid = hid_all[:, :, tile_of(at // across, inner)].reshape(every, inner)
        dy = dy_all[:, :, tile_of(lax.rem(at, across), wide)].reshape(every, wide)
        ddown_s[slot] = rows_inner(hid, dy).astype(BF)
        ddown_copy(at, slot).start()

    for copy in later_copies(steps - 1):
        copy.wait_recv()
    for flow, have, lack in ((0, ahead, behind), (1, behind, ahead)):
        far_copies[flow].wait_recv()
        mlp_got[flow, :, have] = add_low(mlp_got[flow, :, have], mlp_next[flow, :, have])
        mlp_got[flow, :, lack] = mlp_next[flow, :, lack]
    next_copies = [
        passing(mlp_got.at[0], mlp_got.at[2], far_sems, 2, right),
        passing(mlp_got.at[1], mlp_got.at[3], far_sems, 3, left),
    ]
    for copy in next_copies:
        copy.start()

    def collect(at, state):
        squares, mean = state
        cols = tile_of(at)
        dn2 = (
            left_part[0, :, cols].astype(F32)
            + right_got[steps - 1, :, cols].astype(F32)
            + left_got[steps - 1, :, cols].astype(F32)
        )
        dh1_ref[:, cols] = dn2
        h1 = h1_ref[:, cols]
        squares = squares + jnp.sum(h1 * h1, axis=1, keepdims=True)
        return squares, mean + jnp.sum(gain_ref[:, cols] * dn2 * h1, axis=1, keepdims=True)

    zero = jnp.zeros((rows, 1), F32)
    squares, mean = lax.fori_loop(0, width // tile, collect, (zero, zero))
    scale_own = lax.rsqrt(squares / width + EPSILON)
    pull = scale_own * scale_own * scale_own * (mean / width)

    @pl.loop(0, width // tile)
    def _(at):
        cols = tile_of(at)
        dn2, h1 = dh1_ref[:, cols], h1_ref[:, cols]
        dgain_ref[:, cols] = jnp.sum(dn2 * h1 * scale_own, axis=0, keepdims=True)
        dy = dy_all[0, pl.ds(rows, rows), cols].astype(F32)
        d_resid = dy + scale_own * (gain_ref[:, cols] * dn2) - h1 * pull
        dh1_ref[:, cols] = d_resid
        low_ref[:, cols] = d_resid.astype(BF)

    def da_copy(hop):
        return passing(
            da_part.at[hop], da_ref.at[span(place)], (da_send, da_recv), hop, member(hop)[1]
        )

    low = low_ref[...]

    @pl.loop(1, count)
    def _(hop):
        spot = member(hop)[0]
        da_part[hop] = cols_inner(low, out_w[tile_of(spot, size)]).astype(BF)
        da_copy(hop).start()

    da_ref[span(place)] = cols_inner(low, out_w[tile_of(place, size)]).astype(BF)

    @pl.loop(1, count)
    def _(hop):
        da_copy(hop).wait_recv()
        da_copy(hop).wait_send()

    for flow, held in ((0, ahead_ref), (1, behind_ref)):
        next_copies[flow].wait_recv()
        held[...] = add_low(held[...], mlp_got[2 + flow])
    for copy in (*far_copies, *next_copies, *first_copies()):
        copy.wait_send()
    for step in range(1, steps):
        for copy in later_copies(step):
            copy.wait_send()
    for group in range(steps - 2, steps):
        for copy in stores(group, group % 2):
            copy.wait()
    for at in range(2):
        dmlp_copy(mlp_tiles - 2 + at, (mlp_tiles + at) % 2).wait()
        ddown_copy(down_tiles - 2 + at, (down_tiles + at) % 2).wait()


def mlp_back(tokens, mixed, dy, gain, out_w, gate_w, up_w, down_w, collective_id):
    count = lax.axis_size("head")
    total, width = tokens.shape
    hidden = gate_w.shape[1]
    rows, steps = total // count, count // 2
    size = mixed.shape[1] // count
    inner = 256 if hidden % 256 == 0 else 128
    vmem = pl.BlockSpec(memory_space=pltpu.VMEM)
    hbm = pl.BlockSpec(memory_space=pl.ANY)

    def slots(many, tall, wide, dtype=BF):
        return pltpu.VMEM((many, tall, wide), dtype)

    def shape(*extent, dtype=BF):
        return jax.ShapeDtypeStruct(extent, dtype)

    dma = pltpu.SemaphoreType.DMA
    flops = 2 * total * width * (mixed.shape[1] + 9 * hidden)
    return pl.pallas_call(
        functools.partial(mlp_kernel, count),
        out_shape=[
            shape(total, width), shape(width, 2 * hidden), shape(hidden, width),
            shape(rows, width, dtype=F32), shape(rows, width, dtype=F32), shape(rows, width),
            shape(1, width, dtype=F32), shape(total, size), shape(rows, width), shape(rows, width),
        ],
        in_specs=[hbm] * 3 + [vmem] + [hbm] * 4,
        out_specs=[hbm] * 3 + [vmem] * 7,
        scratch_shapes=[
            slots(2, 2 * rows, width), slots(2, 2 * rows, mixed.shape[1]), slots(2, 2 * rows, width),
            pltpu.VMEM((2 * rows, width), F32),
            slots(steps, 2 * rows, width), slots(steps, 2 * rows, width),
            slots(steps, 2 * rows, hidden), slots(steps, 2 * rows, 2 * hidden),
            slots(2, 256, hidden), slots(2, inner, 512), slots(count, rows, size),
            pltpu.VMEM((rows, width), BF), slots(2, rows, width), slots(4, rows, width),
            slots(2, rows, width), slots(2, rows, width),
            slots(steps, rows, width), slots(steps, rows, width),
            *[pltpu.VMEM(weight.shape, BF) for weight in (out_w, gate_w, up_w, down_w)],
            dma((2, 6)), dma((2, 2)), dma((4,)), dma((4,)), dma((count,)), dma((count,)),
            dma((count,)), dma((count,)), dma((4,)), dma((4,)),
        ],
        compiler_params=pltpu.CompilerParams(
            collective_id=collective_id, has_side_effects=True, vmem_limit_bytes=VMEM_LIMIT
        ),
        cost_estimate=pl.CostEstimate(flops=flops, bytes_accessed=40 << 20, transcendentals=0),
        name="mlp_back",
    )(tokens, mixed, dy, gain, out_w, gate_w, up_w, down_w)


def entry_kernel(
    count, batches, x_ref, w_ref, out_ref, gain_ref, seg_ref,
    n1_ref, q_ref, logit_ref, kv_ref, w_all, out_all, gain_all, seg_all,
    send_sem, recv_sem, local_sem,
):
    steps = count // 2
    others = batches // 2
    rows, width = x_ref.shape
    depth = w_ref.shape[0]
    size, wide = out_ref.shape
    block = 256
    place, right, left = ring_setup(count)
    head = lax.axis_index("head")
    batch = lax.axis_index("batch")
    across, core, low = batch // 2, lax.rem(batch, 2), lax.rem(head, 2)
    twin = (across * 2 + 1 - core, head)
    mate = (batch, head + 1 - 2 * low)
    spots = [lax.rem(across + hop, others) for hop in range(others)]
    backs = [lax.rem(across + others - hop, others) for hop in range(others)]
    peers = [(spot * 2 + core, head) for spot in spots]
    far_peers = [(spot * 2 + 1 - core, head) for spot in spots]
    greet((twin, mate, right, left, *peers[1:], *far_peers[1:]))
    sems = (send_sem, recv_sem)
    slot = 0
    copies = []

    def go(source, target, device):
        nonlocal slot
        copy = send(source, target, sems, slot, device)
        slot += 1
        copies.append(copy)
        return copy

    def part(at, extent):
        return pl.ds(pl.multiple_of(at * extent, extent), extent)

    def both(view, own):
        out = [go(own, view(batch), peers[hop]) for hop in range(1, others)]
        return out, [go(own, view(batch), twin)]

    def pass_on(view, arrived):
        out = []
        for hop in range(1, others):
            arrived[hop - 1].wait_recv()
            there = view(backs[hop] * 2 + core)
            out.append(go(there, there, twin))
        return out

    local = []

    def stay(source, target):
        copy = pltpu.make_async_copy(source, target, local_sem.at[len(local)])
        copy.start()
        local.append(copy)

    def main_view(at):
        return w_all.at[part(at, depth), pl.ds(0, 3 * size)]

    def mate_view(at):
        return w_all.at[part(at, depth), pl.ds(3 * size, size)]

    def out_view(chunk, at):
        return out_all.at[part(chunk, size), part(at, wide)]

    small = []
    for own, whole in ((gain_ref, gain_all), (seg_ref, seg_all)):
        for device in (twin, *peers[1:], *far_peers[1:]):
            small.append(go(own, whole.at[batch], device))
        stay(own, whole.at[batch])
    from_mate = go(w_ref.at[:, pl.ds(2 * size, size)], mate_view(batch), mate)
    main_out, main_twin = both(main_view, w_ref)
    stay(w_ref, main_view(batch))
    out_peers = [go(out_ref, out_view(place, batch), peers[hop]) for hop in range(1, others)]
    stay(out_ref, out_view(place, batch))
    flows = [[None, None] for _ in range(others)]

    def ring(step):
        for hop in range(others):
            lane = spots[0] if hop == 0 else backs[hop]
            at = lane * 2 + core
            if step == 0 and hop:
                out_peers[hop - 1].wait_recv()
            for flow, chunk, device in ((0, place - step, right), (1, place + step, left)):
                if step:
                    flows[hop][flow].wait_recv()
                target = out_view(lax.rem(chunk + count, count), at)
                source = out_ref if step == 0 and hop == 0 else target
                if step == steps - 1:
                    cut = (pl.ds(flow * (size // 2), size // 2), slice(None))
                    source, target = source.at[cut], target.at[cut]
                flows[hop][flow] = go(source, target, device)

    for copy in small:
        copy.wait_recv()
    for copy in local[:2]:
        copy.wait()

    def normalize(at):
        here = part(at, block)

        def squares(tile, total):
            values = x_ref[here, part(tile, 256)].astype(F32)
            return total + jnp.sum(values * values, axis=1, keepdims=True)

        total = lax.fori_loop(0, width // 256, squares, jnp.zeros((block, 1), F32))
        scale = lax.rsqrt(total / width + EPSILON)

        @pl.loop(0, batches)
        def _(owner):
            for tile in range(depth // 128):
                cols = pl.ds(pl.multiple_of(owner * depth + tile * 128, 128), 128)
                values = x_ref[here, cols].astype(F32) * scale
                n1_ref[here, cols] = (values * gain_all[owner, pl.ds(tile, 1)]).astype(BF)

    blocks = rows // block
    middle = blocks // 2

    @pl.loop(0, middle)
    def _(at):
        normalize(at)

    from_mate.wait_recv()
    mate_out, mate_twin = both(mate_view, mate_view(batch))
    ring(0)

    @pl.loop(middle, blocks)
    def _(at):
        normalize(at)

    main_passed = pass_on(main_view, main_out)
    mate_passed = pass_on(mate_view, mate_out)
    for copy in (*main_twin, *mate_twin, *main_passed, *mate_passed):
        copy.wait_recv()
    for copy in local[2:]:
        copy.wait()

    def kv_view(at):
        return kv_ref.at[part(at, rows)]

    @pl.loop(0, blocks)
    def _(at):
        here = part(at, block)
        values = matmul(n1_ref[here], w_all[:, pl.ds(2 * size, 2 * size)])
        one, two = values[:, :size], values[:, size:]
        first = jnp.where(low == 0, one, two).astype(BF)
        second = jnp.where(low == 0, two, one).astype(BF)
        half = size // 2
        there = pl.ds(pl.multiple_of(batch * rows + at * block, block), block)
        kv_ref[there, pl.ds(0, size)] = jnp.concatenate([first[:, :half], second[:, :half]], 1)
        kv_ref[there, pl.ds(size, size)] = jnp.concatenate([first[:, half:], second[:, half:]], 1)

    kv_out, kv_twin = both(kv_view, kv_view(batch))
    ring(1)

    @pl.loop(0, blocks)
    def _(at):
        here = part(at, block)
        values = matmul(n1_ref[here], w_all[:, pl.ds(0, 2 * size)])
        q_ref[here] = values[:, :size].astype(BF)
        logit_ref[here] = values[:, size:]

    for step in range(2, steps):
        ring(step)
    kv_passed = pass_on(kv_view, kv_out)
    for pair in flows:
        for copy in pair:
            copy.wait_recv()
    swaps = []
    for hop in range(others):
        there = out_all.at[:, part(spots[hop] * 2 + core, wide)]
        swaps.append(go(there, there, twin))
    for copy in (*kv_twin, *kv_passed, *swaps):
        copy.wait_recv()
    for copy in copies:
        copy.wait_send()


def entry(tokens, w_shard, w_out, gains, segments, collective_id):
    count = lax.axis_size("head")
    batches = lax.axis_size("batch")
    others = batches // 2
    rows, width = tokens.shape
    size, wide = w_out.shape
    vmem = pl.BlockSpec(memory_space=pltpu.VMEM)
    slots = 6 * batches + others * (count + 3)
    sems = pltpu.SemaphoreType.DMA((slots,))
    return pl.pallas_call(
        functools.partial(entry_kernel, count, batches),
        out_shape=[
            jax.ShapeDtypeStruct((rows, width), BF),
            jax.ShapeDtypeStruct((rows, size), BF),
            jax.ShapeDtypeStruct((rows, size), F32),
            jax.ShapeDtypeStruct((batches * rows, 2 * size), BF),
            jax.ShapeDtypeStruct((width, 4 * size), BF),
            jax.ShapeDtypeStruct((count * size, batches * wide), BF),
            jax.ShapeDtypeStruct((batches, *gains.shape), F32),
            jax.ShapeDtypeStruct((batches, *segments.shape), jnp.int32),
        ],
        in_specs=[vmem] * 5,
        out_specs=[vmem] * 8,
        scratch_shapes=[sems, sems, pltpu.SemaphoreType.DMA((5,))],
        compiler_params=pltpu.CompilerParams(
            collective_id=collective_id, has_side_effects=True, vmem_limit_bytes=VMEM_LIMIT
        ),
        name="entry",
    )(tokens, w_shard, w_out, gains, segments)


KEY_BLOCK = 512
QUERY_BLOCK = 256


def key_range(start_ref, base, query_block):
    first = query_block * QUERY_BLOCK
    lowest = start_ref[first]
    highest = start_ref[first + QUERY_BLOCK - 1]
    begin = lowest // KEY_BLOCK
    end = (base + first + QUERY_BLOCK - 1) // KEY_BLOCK + 1
    full_begin = jnp.minimum((highest + KEY_BLOCK - 1) // KEY_BLOCK, end)
    full_end = jnp.maximum((base + first + 1) // KEY_BLOCK, full_begin)
    return begin, full_begin, full_end, end


def allowed_pairs(key_block, start_row, base_row):
    shape = (KEY_BLOCK, QUERY_BLOCK)
    key_pos = key_block * KEY_BLOCK + lax.broadcasted_iota(jnp.int32, shape, 0)
    query_pos = base_row + lax.broadcasted_iota(jnp.int32, shape, 1)
    return (key_pos >= start_row) & (key_pos <= query_pos)


def attend_kernel(
    scale, start_sm, base_sm, q_ref, kv_ref, start_ref, logit_ref, o_ref, a_ref, lse_ref
):
    base = base_sm[0]
    size = q_ref.shape[1]
    factor = scale * math.log2(math.e)

    @pl.loop(0, q_ref.shape[0] // QUERY_BLOCK)
    def _(block):
        rows = pl.ds(pl.multiple_of(block * QUERY_BLOCK, QUERY_BLOCK), QUERY_BLOCK)
        queries = q_ref[rows]
        start_row = start_ref[:, rows]
        begin, full_begin, full_end, end = key_range(start_sm, base, block)

        def step(masked, at, state):
            old_max, old_sum, total = state
            keys = pl.ds(pl.multiple_of(at * KEY_BLOCK, KEY_BLOCK), KEY_BLOCK)
            scores = cols_inner(kv_ref[keys, :size], queries)
            if masked:
                allowed = allowed_pairs(at, start_row, base + block * QUERY_BLOCK)
                scores = jnp.where(allowed, scores, MASKED)
            new_max = jnp.maximum(old_max, jnp.max(scores, axis=0, keepdims=True))
            keep = jnp.exp2((old_max - new_max) * factor)
            weights = jnp.exp2(scores * factor - new_max * factor)
            new_sum = old_sum * keep + jnp.sum(weights, axis=0, keepdims=True)
            total = total * keep + rows_inner(kv_ref[keys, size:], weights.astype(BF))
            return new_max, new_sum, total

        state = (
            jnp.full((1, QUERY_BLOCK), MASKED, F32),
            jnp.zeros((1, QUERY_BLOCK), F32),
            jnp.zeros((size, QUERY_BLOCK), F32),
        )
        state = lax.fori_loop(begin, full_begin, functools.partial(step, True), state)
        state = lax.fori_loop(full_begin, full_end, functools.partial(step, False), state)
        state = lax.fori_loop(full_end, end, functools.partial(step, True), state)
        run_max, run_sum, total = state
        lse_ref[:, rows] = run_max * factor + jnp.log2(run_sum)
        attended = (total / run_sum).T
        o_ref[rows] = attended
        a_ref[rows] = (attended * jax.nn.sigmoid(logit_ref[rows])).astype(BF)


def attend_back_kernel(
    scale, start_sm, base_sm, q_ref, kv_ref, start_ref, logit_ref, o_ref, da_ref, lse_ref,
    dq_ref, dg_ref, dkv_ref, dk_acc, dv_acc,
):
    base = base_sm[0]
    size = q_ref.shape[1]
    factor = scale * math.log2(math.e)
    dk_acc[...] = jnp.zeros_like(dk_acc)
    dv_acc[...] = jnp.zeros_like(dv_acc)

    @pl.loop(0, q_ref.shape[0] // QUERY_BLOCK)
    def _(block):
        rows = pl.ds(pl.multiple_of(block * QUERY_BLOCK, QUERY_BLOCK), QUERY_BLOCK)
        queries = q_ref[rows]
        start_row = start_ref[:, rows]
        lse = lse_ref[:, rows]
        gate = jax.nn.sigmoid(logit_ref[rows])
        attended = o_ref[rows]
        d_mixed = da_ref[rows].astype(F32)
        d_attended = (d_mixed * gate).astype(BF)
        dg_ref[rows] = (d_mixed * attended * gate * (1.0 - gate)).astype(BF)
        delta = jnp.sum((d_attended.astype(F32) * attended).T, axis=0, keepdims=True)
        begin, full_begin, full_end, end = key_range(start_sm, base, block)

        def step(masked, at, d_queries):
            keys = pl.ds(pl.multiple_of(at * KEY_BLOCK, KEY_BLOCK), KEY_BLOCK)
            key_block = kv_ref[keys, :size]
            probs = jnp.exp2(cols_inner(key_block, queries) * factor - lse)
            if masked:
                allowed = allowed_pairs(at, start_row, base + block * QUERY_BLOCK)
                probs = jnp.where(allowed, probs, 0.0)
            d_probs = cols_inner(kv_ref[keys, size:], d_attended)
            d_scores = (probs * (d_probs - delta) * scale).astype(BF)
            dv_acc[keys] += matmul(probs.astype(BF), d_attended)
            dk_acc[keys] += matmul(d_scores, queries)
            return d_queries + rows_inner(key_block, d_scores)

        d_queries = jnp.zeros((size, QUERY_BLOCK), F32)
        d_queries = lax.fori_loop(begin, full_begin, functools.partial(step, True), d_queries)
        d_queries = lax.fori_loop(full_begin, full_end, functools.partial(step, False), d_queries)
        d_queries = lax.fori_loop(full_end, end, functools.partial(step, True), d_queries)
        dq_ref[rows] = d_queries.T.astype(BF)

    @pl.loop(0, kv_ref.shape[0] // KEY_BLOCK)
    def _(at):
        keys = pl.ds(pl.multiple_of(at * KEY_BLOCK, KEY_BLOCK), KEY_BLOCK)
        dk, dv = dk_acc[keys].astype(BF), dv_acc[keys].astype(BF)
        half = size // 2
        dkv_ref[keys, :size] = jnp.concatenate([dk[:, :half], dv[:, :half]], axis=1)
        dkv_ref[keys, size:] = jnp.concatenate([dk[:, half:], dv[:, half:]], axis=1)


def tail_kernel(
    count, batches, dq_ref, dg_ref, dkv_ref, w_ref, x_ref, gain_ref, dh1_ref, second_ref,
    n1_ref, mixed_ref, low_ref, base_ref, ahead_ref, behind_ref,
    out_all, tok_all, gains_ref, wout_own, din_ref,
    part_ref, tok_ref, got, wout_got, gain_own, gain_got, gain_mid, gain_heads,
    din_s, din_got, din_x, wout_s, wout_twin, wout_x,
    cat_ref, out_s, out_got, core_got, x_first, x_second, y_first, y_second, held, n1_s,
    send_sem, recv_sem, local_sem,
):
    steps = count // 2
    rows, width = x_ref.shape
    depth = cat_ref.shape[1]
    tall, size = dq_ref.shape
    tile = 256
    place, right, left = ring_setup(count)
    batch, head = lax.axis_index("batch"), lax.axis_index("head")
    others = [lax.rem(batch + hop, batches) for hop in range(1, batches)]
    members = [(batch, ring_head(lax.rem(place + hop, count), count)) for hop in range(1, count)]
    greet((*members, *[(other, head) for other in others]))
    sems = (send_sem, recv_sem)
    slot = 0
    copies = []

    def go(source, target, device):
        nonlocal slot
        copy = send(source, target, sems, slot, device)
        slot += 1
        copies.append(copy)
        return copy

    across, core = batch // 2, lax.rem(batch, 2)
    spots = [lax.rem(across + hop, batches // 2) for hop in range(batches // 2)]
    order = list(range(1, batches // 2)) + [0]
    twin = (across * 2 + 1 - core, head)

    def scatter_swap(view, held):
        return [go(view(2 * spots[hop] + 1 - core), held.at[spots[hop]], twin) for hop in order]

    def add_tiles(target, one, other):
        @pl.loop(0, target.shape[0] // 128)
        def _(at):
            lines = pl.ds(pl.multiple_of(at * 128, 128), 128)
            total = one[lines].astype(F32) + other[lines].astype(F32)
            target[lines] = total.astype(target.dtype)

    def scatter_cross(view, held, crossed, arriving):
        out = []
        for copy, hop in zip(arriving, order):
            copy.wait_recv()
            spot = spots[hop]
            add_tiles(held.at[spot], held.at[spot], view(2 * spot + core))
            if hop:
                out.append(go(held.at[spot], crossed.at[hop - 1], (spot * 2 + core, head)))
        return out

    def scatter_end(held, crossed, arriving, target):
        for hop, copy in enumerate(arriving):
            copy.wait_recv()
            last = hop == len(arriving) - 1
            add_tiles(target if last else held.at[across], held.at[across], crossed.at[hop])

    def wout_view(at):
        wide = width // batches
        return wout_s.at[:, pl.ds(pl.multiple_of(at * wide, wide), wide)]

    def din_view(at):
        tall = din_ref.shape[0]
        return din_s.at[pl.ds(pl.multiple_of(at * tall, tall), tall)]

    def span(owner, extent):
        return pl.ds(pl.multiple_of(lax.rem(owner + count, count) * extent, extent), extent)

    def compute(owner):
        here = span(owner, rows)
        values = cat_ref[here]

        @pl.loop(0, width // tile)
        def _(at):
            cols = pl.ds(pl.multiple_of(at * tile, tile), tile)
            part_ref[here, cols] = cols_inner(values, w_ref[cols, pl.ds(0, depth)]).astype(BF)

    def gather(own, whole, step, last):
        out = []
        for flow, chunk, device in ((0, place - step, right), (1, place + step, left)):
            if last:
                last[flow].wait_recv()
            target = whole.at[lax.rem(chunk + count, count)]
            source = target if step else own
            if step == steps - 1:
                cut = (slice(None), pl.ds(flow * (width // 2), width // 2))
                source, target = source.at[cut], target.at[cut]
            out.append(go(source, target, device))
        return out

    def reduce(parts, held, step, last):
        extent, side = held.shape[2], held.shape[3] // 2
        out = []
        for flow, owner, device in (
            (0, place + steps - step, right),
            (1, place - steps + step, left),
        ):
            have = pl.ds(flow * side, side)
            lack = pl.ds((1 - flow) * side, side)
            mine = parts.at[span(owner, extent)]
            if step == 0:
                out.append(go(mine.at[:, have], held.at[flow, 0, :, have], device))
                continue
            last[flow].wait_recv()
            if step == 1:
                held[flow, 0, :, have] = add_low(held[flow, 0, :, have], mine[:, have])
                held[flow, 0, :, lack] = mine[:, lack]
            else:
                held[flow, step - 1] = add_low(held[flow, step - 1], mine[...])
            out.append(go(held.at[flow, step - 1], held.at[flow, step], device))
        return out

    low = lax.rem(head, 2)
    mate = (batch, head + 1 - 2 * low)
    peers = [(spot * 2 + core, head) for spot in spots]
    mine = pl.ds(pl.multiple_of(low * size, size), size)
    given = pl.ds(pl.multiple_of((1 - low) * size, size), size)
    top, bottom = pl.ds(0, tall // 2), pl.ds(tall // 2, tall // 2)
    fresh = pl.ds(2 * size, size)

    def keys_of(at):
        return dkv_ref.at[pl.ds(pl.multiple_of(at * tall, tall), tall)]

    def normed_copy(at, slot):
        cols = pl.ds(pl.multiple_of(at * tile, tile), tile)
        return pltpu.make_async_copy(n1_ref.at[:, cols], n1_s.at[slot], local_sem.at[2 + slot])

    for at in range(2):
        normed_copy(at, at).start()
    last_sums = [go(ahead_ref, out_got.at[0], right), go(behind_ref, out_got.at[1], left)]
    swaps = scatter_swap(keys_of, core_got)
    cat_ref[:, pl.ds(0, size)] = dq_ref[...]
    cat_ref[:, pl.ds(size, size)] = dg_ref[...]

    @pl.loop(0, width // tile)
    def _(at):
        cols = pl.ds(pl.multiple_of(at * tile, tile), tile)
        wout_s[:, cols] = rows_inner(mixed_ref[...], low_ref[:, cols]).astype(BF)

    tops, bottoms = [], []
    for copy, hop in zip(swaps, order):
        copy.wait_recv()
        spot = spots[hop]
        add_tiles(core_got.at[spot], core_got.at[spot], keys_of(2 * spot + core))
        bottoms.append(go(core_got.at[spot, bottom, given], y_first.at[spot], mate))
        if hop:
            tops.append(go(core_got.at[spot, top], x_first.at[hop - 1], peers[hop]))
    wouts = scatter_swap(wout_view, wout_twin)
    for copy in last_sums:
        copy.wait_recv()
    out_s[...] = (
        base_ref[...] + out_got[0].astype(F32) + out_got[1].astype(F32)
    ).astype(BF)
    keep_out = pltpu.make_async_copy(out_s, out_all.at[place], local_sem.at[0])
    keep_out.start()
    outs = gather(out_s, out_all, 0, None)
    total = core_got[across, top].astype(F32)
    for hop, copy in enumerate(tops):
        copy.wait_recv()
        total = total + x_first[hop].astype(F32)
    held[...] = total.astype(BF)
    last = go(held.at[:, given], y_second, mate)
    ends = []
    for copy, hop in zip(bottoms, order):
        copy.wait_recv()
        spot = spots[hop]
        y_first[spot] = add_low(y_first[spot], core_got[spot, bottom, mine])
        if hop:
            ends.append(go(y_first.at[spot], x_second.at[hop - 1], peers[hop]))
    last.wait_recv()
    cat_ref[top, fresh] = add_low(held[:, mine], y_second[...])
    total = y_first[across].astype(F32)
    for hop, copy in enumerate(ends):
        copy.wait_recv()
        total = total + x_second[hop].astype(F32)
    cat_ref[bottom, fresh] = total.astype(BF)

    compute(place + steps)
    sums = reduce(part_ref, got, 0, None)
    outs = gather(out_s, out_all, 1, outs)

    @pl.loop(1, count)
    def _(hop):
        compute(place + steps + hop)

    @pl.loop(0, width // tile)
    def _(at):
        slot = lax.rem(at, 2)
        normed_copy(at, slot).wait()
        cols = pl.ds(pl.multiple_of(at * tile, tile), tile)
        din_s[cols] = rows_inner(n1_s[slot], cat_ref[...]).astype(BF)

        @pl.when(at + 2 < width // tile)
        def _():
            normed_copy(at + 2, slot).start()

    dins = scatter_swap(din_view, din_got)
    for step in range(1, steps):
        sums = reduce(part_ref, got, step, sums)
        if step + 1 < steps:
            outs = gather(out_s, out_all, step + 1, outs)
        if step == 1:
            wouts = scatter_cross(wout_view, wout_twin, wout_x, wouts)
            dins = scatter_cross(din_view, din_got, din_x, dins)
    for copy in sums:
        copy.wait_recv()

    def tile_of(at):
        return pl.ds(pl.multiple_of(at * tile, tile), tile)

    def total(cols):
        return (
            part_ref[span(place, rows), cols].astype(F32)
            + got[0, steps - 1, :, cols].astype(F32)
            + got[1, steps - 1, :, cols].astype(F32)
        )

    def collect(at, state):
        squares, mean = state
        cols = tile_of(at)
        x = x_ref[:, cols].astype(F32)
        squares = squares + jnp.sum(x * x, axis=1, keepdims=True)
        return squares, mean + jnp.sum(gain_ref[:, cols] * total(cols) * x, axis=1, keepdims=True)

    zero = jnp.zeros((rows, 1), F32)
    squares, mean = lax.fori_loop(0, width // tile, collect, (zero, zero))
    scale = lax.rsqrt(squares / width + EPSILON)
    pull = scale * scale * scale * (mean / width)

    @pl.loop(0, width // tile)
    def _(at):
        cols = tile_of(at)
        x, dn1 = x_ref[:, cols].astype(F32), total(cols)
        gain_own[pl.ds(0, 1), cols] = jnp.sum(dn1 * x * scale, axis=0, keepdims=True)
        gain_own[pl.ds(1, 1), cols] = second_ref[:, cols]
        tok_ref[:, cols] = (dh1_ref[:, cols] + scale * (gain_ref[:, cols] * dn1) - x * pull).astype(BF)

    keep_tok = pltpu.make_async_copy(tok_ref, tok_all.at[place], local_sem.at[1])
    keep_tok.start()
    toks = gather(tok_ref, tok_all, 0, None)
    wout_part = wout_twin.at[across]
    scatter_end(wout_twin, wout_x, wouts, wout_part)
    wsums = reduce(wout_part, wout_got, 0, None)
    scatter_end(din_got, din_x, dins, din_ref)
    wide = width // batches

    def slice_of(at):
        return pl.ds(pl.multiple_of(at * wide, wide), wide)

    gains = [
        go(gain_own.at[:, slice_of(other)], gain_got.at[hop], (other, head))
        for hop, other in enumerate(others)
    ]
    toks = gather(tok_ref, tok_all, 1, toks)
    wsums = reduce(wout_part, wout_got, 1, wsums)
    middle = gain_own[:, slice_of(batch)]
    for hop, copy in enumerate(gains):
        copy.wait_recv()
        middle = middle + gain_got[hop]
    gain_mid[...] = middle
    gain_heads[place] = middle
    gains = [go(gain_mid, gain_heads.at[place], member) for member in members]
    for step in range(2, steps):
        toks = gather(tok_ref, tok_all, step, toks)
        wsums = reduce(wout_part, wout_got, step, wsums)
    for copy in gains:
        copy.wait_recv()
    middle = gain_heads[0]
    for at in range(1, count):
        middle = middle + gain_heads[at]
    gains_ref[...] = middle
    for copy in (*wsums, *outs):
        copy.wait_recv()
    wout_own[...] = (
        wout_part[span(place, wout_own.shape[0])].astype(F32)
        + wout_got[0, steps - 1].astype(F32)
        + wout_got[1, steps - 1].astype(F32)
    )
    for copy in toks:
        copy.wait_recv()
    for copy in copies:
        copy.wait_send()
    keep_out.wait()
    keep_tok.wait()


def tail(arrays, collective_id):
    d_queries, _, d_keys, _, x_own, *_, mixed, _, _, _, _ = arrays
    count = lax.axis_size("head")
    batches = lax.axis_size("batch")
    steps = count // 2
    rows, width = x_own.shape
    others = batches // 2
    size, wide = mixed.shape[1] // count, width // batches
    tall, head_size = d_queries.shape
    depth = 3 * head_size
    vmem = pl.BlockSpec(memory_space=pltpu.VMEM)
    whole = (count, rows, width)
    sems = pltpu.SemaphoreType.DMA((6 * count + 6 * batches,))
    gains = (2, width // batches)
    return pl.pallas_call(
        functools.partial(tail_kernel, count, batches),
        out_shape=[
            jax.ShapeDtypeStruct(whole, BF),
            jax.ShapeDtypeStruct(whole, BF),
            jax.ShapeDtypeStruct(gains, F32),
            jax.ShapeDtypeStruct((size, wide), F32),
            jax.ShapeDtypeStruct((wide, depth), F32),
        ],
        in_specs=[vmem] * 8 + [pl.BlockSpec(memory_space=pl.ANY)] + [vmem] * 5,
        out_specs=[vmem] * 5,
        scratch_shapes=[
            pltpu.VMEM((count * rows, width), BF),
            pltpu.VMEM((rows, width), BF),
            pltpu.VMEM((2, steps, rows, width), BF),
            pltpu.VMEM((2, steps, size, wide), BF),
            pltpu.VMEM((2, width), F32),
            pltpu.VMEM((batches - 1, *gains), F32),
            pltpu.VMEM(gains, F32),
            pltpu.VMEM((count, *gains), F32),
            pltpu.VMEM((width, depth), BF),
            pltpu.VMEM((others, wide, depth), BF),
            pltpu.VMEM((others - 1, wide, depth), BF),
            pltpu.VMEM((count * size, width), BF),
            pltpu.VMEM((others, count * size, wide), BF),
            pltpu.VMEM((others - 1, count * size, wide), BF),
            pltpu.VMEM((tall, depth), BF),
            pltpu.VMEM((rows, width), BF),
            pltpu.VMEM((2, rows, width), BF),
            pltpu.VMEM((others, tall, 2 * head_size), BF),
            pltpu.VMEM((others - 1, tall // 2, 2 * head_size), BF),
            pltpu.VMEM((others - 1, tall // 2, head_size), BF),
            pltpu.VMEM((others, tall // 2, head_size), BF),
            pltpu.VMEM((tall // 2, head_size), BF),
            pltpu.VMEM((tall // 2, 2 * head_size), BF),
            pltpu.VMEM((2, tall, 256), BF),
            sems,
            sems,
            pltpu.SemaphoreType.DMA((4,)),
        ],
        compiler_params=pltpu.CompilerParams(
            collective_id=collective_id, has_side_effects=True, vmem_limit_bytes=(36 << 20) + 6 * count * size * width
        ),
        cost_estimate=pl.CostEstimate(
            flops=4 * count * rows * width * depth, bytes_accessed=400 << 20, transcendentals=0
        ),
        name="tail",
    )(*arrays)


def local_call(kernel, scalars, arrays, outs, scratch, flops, name):
    vmem = pl.BlockSpec(memory_space=pltpu.VMEM)
    smem = pl.BlockSpec(memory_space=pltpu.SMEM)
    return pl.pallas_call(
        kernel,
        out_shape=outs,
        in_specs=[smem] * len(scalars) + [vmem] * len(arrays),
        out_specs=[vmem] * len(outs),
        scratch_shapes=scratch,
        compiler_params=pltpu.CompilerParams(vmem_limit_bytes=VMEM_LIMIT),
        cost_estimate=pl.CostEstimate(flops=flops, bytes_accessed=8 << 20, transcendentals=0),
        name=name,
    )(*scalars, *arrays)


def ring_routes(count):
    spots = [ring_head(at, count) for at in range(count)]
    right = [(spots[at], spots[(at + 1) % count]) for at in range(count)]
    left = [(spots[at], spots[at - 1]) for at in range(count)]
    return right, left


def add_low(one, other):
    return (one.astype(F32) + other.astype(F32)).astype(BF)


def flow_steps(part, going, coming):
    count = lax.axis_size("head")
    place = ring_place(lax.axis_index("head"), count)
    right, left = ring_routes(count)
    rows = part.shape[0] // count
    steps = count // 2

    def mine(owner):
        return lax.dynamic_slice_in_dim(part, lax.rem(owner + count, count) * rows, rows, 0)

    for step in range(2, steps - 1):
        from_left = lax.ppermute(going, "head", right)
        from_right = lax.ppermute(coming, "head", left)
        going = add_low(from_left, mine(place + steps - 1 - step))
        coming = add_low(from_right, mine(place - steps + 1 + step))
        going, coming = yield going, coming


def matmul(left, right):
    return jnp.dot(left, right, preferred_element_type=F32)


def rows_inner(left, right):
    return lax.dot_general(left, right, (((0,), (0,)), ((), ())), preferred_element_type=F32)


def cols_inner(left, right):
    return lax.dot_general(left, right, (((1,), (1,)), ((), ())), preferred_element_type=F32)


def rms_scale(values):
    return lax.rsqrt(jnp.mean(values * values, axis=1, keepdims=True) + EPSILON)


def per_device(
    tokens,
    segment_ids,
    norm1_gain,
    w_query,
    w_key,
    w_value,
    w_gate,
    w_out,
    norm2_gain,
    w_mlp_gate,
    w_mlp_up,
    w_down,
    out_grad,
):
    heads = lax.axis_size("head")
    batches = lax.axis_size("batch")
    row_count, width = tokens.shape
    head_size = w_query.shape[1]
    half = w_key.shape[1]
    chunk = row_count // heads
    me = ring_place(lax.axis_index("head"), heads)
    scale_factor = 1.0 / math.sqrt(head_size)

    w_shard = jnp.concatenate([w_query, w_gate, w_key, w_value], axis=1)
    gains = jnp.concatenate([norm1_gain, norm2_gain]).reshape(-1, 128).astype(F32)
    normed_one, queries, gate_logit, kv_all, w_in, out_full, gains, seg_all = entry(
        tokens, w_shard, w_out, gains, segment_ids.reshape(-1, 128), 1
    )
    gains, w_mlp_gate = lax.optimization_barrier((gains, w_mlp_gate))
    seg_all = seg_all.reshape(-1)
    gains = gains.reshape(batches, 2, -1).transpose(1, 0, 2).reshape(2, width)
    gain_one, gain_two = gains[0], gains[1]
    mgate_full = lax.all_gather(w_mlp_gate, "batch", axis=0, tiled=True)

    base = lax.axis_index("batch") * row_count
    ids = jnp.arange(DOCUMENTS, dtype=jnp.int32)
    below = jnp.sum((seg_all[None, :] < ids[:, None]).astype(jnp.int32), axis=1)
    starts = jnp.sum(jnp.where(segment_ids[None, :] == ids[:, None], below[:, None], 0), axis=0)
    scalars = (starts, base.reshape(1))
    pair_flops = 4 * row_count * kv_all.shape[0] * head_size
    attended, mixed, lse = local_call(
        functools.partial(attend_kernel, scale_factor),
        scalars,
        (queries, kv_all, starts[None], gate_logit),
        [
            jax.ShapeDtypeStruct((row_count, head_size), F32),
            jax.ShapeDtypeStruct((row_count, head_size), BF),
            jax.ShapeDtypeStruct((1, row_count), F32),
        ],
        [],
        pair_flops,
        "attend",
    )
    mixed_all, down_full, mup_full = spread(
        [mixed, w_down, w_mlp_up], (("head", "cols"), ("batch", "cols"), ("batch", "rows")), 2
    )
    (
        mlp_part, d_mlp, d_down, resid_own, d_resid, d_resid_low, d_gain_two, d_mixed, going, coming,
    ) = mlp_back(
        tokens, mixed_all, out_grad, gain_two[None], out_full, mgate_full, mup_full, down_full, 3
    )
    hold = lax.optimization_barrier
    mixed_own = lax.dynamic_slice_in_dim(mixed_all, me * chunk, chunk, 0)
    flow = flow_steps(mlp_part, going, coming)
    state = next(flow)

    d_queries, d_gate_logit, d_kv_all = local_call(
        functools.partial(attend_back_kernel, scale_factor),
        scalars,
        (queries, kv_all, starts[None], gate_logit, attended, d_mixed, lse),
        [
            jax.ShapeDtypeStruct((row_count, head_size), BF),
            jax.ShapeDtypeStruct((row_count, head_size), BF),
            jax.ShapeDtypeStruct(kv_all.shape, BF),
        ],
        [pltpu.VMEM((kv_all.shape[0], head_size), F32)] * 2,
        5 * pair_flops // 2,
        "attend_back",
    )
    for _ in range(3, heads // 2 - 1):
        state = flow.send(state)
    d_down = lax.psum_scatter(d_down, "batch", scatter_dimension=1, tiled=True)
    d_mlp = lax.psum_scatter(d_mlp, "batch", scatter_dimension=0, tiled=True)
    inputs_own = lax.dynamic_slice_in_dim(tokens, me * chunk, chunk, 0)
    base_own = resid_own + lax.dynamic_slice_in_dim(mlp_part, me * chunk, chunk, 0).astype(F32)
    output, d_tokens, d_gains, d_out, d_in = tail(
        (
            d_queries, d_gate_logit, d_kv_all, w_in, inputs_own, gain_one[None], d_resid, d_gain_two,
            normed_one, mixed_own, d_resid_low, base_own, *state,
        ),
        5,
    )
    d_tokens, d_mlp, d_down = hold((d_tokens, d_mlp, d_down))
    d_mlp, d_down = d_mlp.astype(F32), d_down.astype(F32)
    output = output.reshape(row_count, width)
    d_tokens = d_tokens.reshape(row_count, width)
    hidden_own = w_mlp_gate.shape[1]
    return (
        output,
        d_tokens,
        d_gains[0],
        d_in[:, :head_size],
        d_in[:, 2 * head_size : 2 * head_size + half],
        d_in[:, 2 * head_size + half :],
        d_in[:, head_size : 2 * head_size],
        d_out,
        d_gains[1],
        d_mlp[:, :hidden_own],
        d_mlp[:, hidden_own:],
        d_down,
    )


def solution(mesh):
    return jax.shard_map(
        per_device,
        mesh=mesh,
        in_specs=(
            P("batch", None),
            P("batch"),
            P("batch"),
            P("batch", "head"),
            P("batch", "head"),
            P("batch", "head"),
            P("batch", "head"),
            P("head", "batch"),
            P("batch"),
            P("batch", "head"),
            P("batch", "head"),
            P("head", "batch"),
            P("batch", None),
        ),
        out_specs=(
            P("batch", None),
            P("batch", None),
            P("batch"),
            P("batch", "head"),
            P("batch", "head"),
            P("batch", "head"),
            P("batch", "head"),
            P("head", "batch"),
            P("batch"),
            P("batch", "head"),
            P("batch", "head"),
            P("head", "batch"),
        ),
        check_vma=False,
    )
```

```python
import functools
import math

import jax
import jax.numpy as jnp
from jax import lax
from jax.experimental import pallas as pl
from jax.experimental.pallas import tpu as pltpu
from jax.sharding import PartitionSpec as P

EPSILON = 1e-06
MASKED = -1e30
DOCUMENTS = 7
BF = jnp.bfloat16
F32 = jnp.float32


MESH = pl.DeviceIdType.MESH
VMEM_LIMIT = 60 << 20


def ring_place(head, count):
    high, low = head // 2, head % 2
    return (1 - low) * high + low * (count - 1 - high)


def ring_head(place, count):
    low = place // (count // 2)
    high = (1 - low) * place + low * (count - 1 - place)
    return 2 * high + low


def ring_setup(count):
    batch = lax.axis_index("batch")
    place = ring_place(lax.axis_index("head"), count)
    right = (batch, ring_head(lax.rem(place + 1, count), count))
    left = (batch, ring_head(lax.rem(place + count - 1, count), count))
    return place, right, left


def greet(devices):
    barrier = pltpu.get_barrier_semaphore()
    for device in devices:
        pl.semaphore_signal(barrier, inc=1, device_id=device, device_id_type=MESH)
    pl.semaphore_wait(barrier, len(devices))


def send(source, target, sems, slot, device):
    copy = pltpu.make_async_remote_copy(
        src_ref=source,
        dst_ref=target,
        send_sem=sems[0].at[slot],
        recv_sem=sems[1].at[slot],
        device_id=device,
        device_id_type=MESH,
    )
    copy.start()
    return copy


def half_of(extent, flow):
    if extent[1] % 256:
        return (pl.ds(flow * (extent[0] // 2), extent[0] // 2), slice(None))
    return (slice(None), pl.ds(flow * (extent[1] // 2), extent[1] // 2))


def place_of(whole, own, chunk, form):
    rows, wide = own.shape[-2:]
    if form == "lead":
        return whole.at[chunk]
    if form == "rows":
        return whole.at[pl.ds(pl.multiple_of(chunk * rows, rows), rows)]
    return whole.at[:, pl.ds(pl.multiple_of(chunk * wide, wide), wide)]


def spread_kernel(count, batches, plans, *refs):
    steps = count // 2
    arrays = len(plans)
    own_refs, all_refs = refs[:arrays], refs[arrays : 2 * arrays]
    send_sem, recv_sem, local_sem = refs[2 * arrays :]
    place, right, left = ring_setup(count)
    head = lax.axis_index("head")
    batch = lax.axis_index("batch")
    across, core = batch // 2, lax.rem(batch, 2)
    others = batches // 2
    twin = (across * 2 + 1 - core, head)
    peers = [(lax.rem(across + hop, others) * 2 + core, head) for hop in range(1, others)]
    ring = any(axis == "head" for axis, _ in plans)
    grid = any(axis == "batch" for axis, _ in plans)
    greet((right, left) * ring + (twin, *peers) * grid)
    sems = (send_sem, recv_sem)
    slot = 0
    waiting, arriving, local = [], [], []

    def go(source, target, device):
        nonlocal slot
        copy = send(source, target, sems, slot, device)
        slot += 1
        waiting.append(copy)
        return copy

    stages = []
    for index, (axis, form) in enumerate(plans):
        own, whole = own_refs[index], all_refs[index]
        spot = place if axis == "head" else batch
        copy = pltpu.make_async_copy(own, place_of(whole, own, spot, form), local_sem.at[index])
        copy.start()
        local.append(copy)
        if axis == "batch":
            stages.append(index)
    onward = []

    def stage():
        for copy, block in onward:
            copy.wait_recv()
            arriving.append(go(block, block, twin))
        onward.clear()
        if stages:
            index = stages.pop(0)
            own, whole, form = own_refs[index], all_refs[index], plans[index][1]
            mine = place_of(whole, own, batch, form)
            for hop, peer in enumerate(peers, 1):
                source = lax.rem(across + others - hop, others) * 2 + core
                onward.append((go(own, mine, peer), place_of(whole, own, source, form)))
            arriving.append(go(own, mine, twin))

    stage()
    copies = [None] * (2 * arrays)
    for step in range(steps):
        for index, (axis, form) in enumerate(plans):
            if axis != "head":
                continue
            own = own_refs[index]
            for flow, chunk, device in ((0, place - step, right), (1, place + step, left)):
                at = 2 * index + flow
                if step:
                    copies[at].wait_recv()
                chunk = lax.rem(chunk + count, count)
                target = place_of(all_refs[index], own, chunk, form)
                source = target if step else own
                if step == steps - 1:
                    part = half_of(own.shape, flow)
                    source = source.at[part]
                    target = target.at[part]
                copies[at] = go(source, target, device)
        if step == steps // 2:
            stage()
    while stages or onward:
        stage()
    for copy in copies:
        if copy is not None:
            arriving.append(copy)
    for copy in arriving:
        copy.wait_recv()
    for copy in waiting:
        copy.wait_send()
    for copy in local:
        copy.wait()


def spread(arrays, plans, collective_id):
    count = lax.axis_size("head")
    batches = lax.axis_size("batch")
    shapes = []
    slots = 0
    for array, (axis, form) in zip(arrays, plans):
        many = count if axis == "head" else batches
        slots += count if axis == "head" else batches - 1
        if form == "lead":
            shapes.append((many, *array.shape))
        elif form == "rows":
            shapes.append((many * array.shape[0], array.shape[1]))
        else:
            shapes.append((array.shape[0], many * array.shape[1]))
    hbm = pl.BlockSpec(memory_space=pl.ANY)
    return pl.pallas_call(
        functools.partial(spread_kernel, count, batches, plans),
        out_shape=[jax.ShapeDtypeStruct(shape, a.dtype) for shape, a in zip(shapes, arrays)],
        in_specs=[pl.BlockSpec(memory_space=pltpu.VMEM)] * len(arrays),
        out_specs=[hbm] * len(arrays),
        scratch_shapes=[
            pltpu.SemaphoreType.DMA((slots,)),
            pltpu.SemaphoreType.DMA((slots,)),
            pltpu.SemaphoreType.DMA((len(arrays),)),
        ],
        compiler_params=pltpu.CompilerParams(
            collective_id=collective_id, has_side_effects=True, vmem_limit_bytes=VMEM_LIMIT
        ),
        name=f"spread_{collective_id}",
    )(*arrays)


def mlp_kernel(
    count, x_hbm, a_hbm, dy_hbm, gain_ref, out_hbm, gate_hbm, up_hbm, down_hbm,
    mlp_hbm, dmlp_hbm, ddown_hbm, h1_ref, dh1_ref, low_ref, dgain_ref, da_ref, ahead_ref, behind_ref,
    x_s, a_s, mlp_s, h1_s, dy_all, n2_all, hid_all, grad_all, dmlp_s, ddown_s, da_part,
    mlp_far, mlp_next, mlp_got, right_part, left_part, right_got, left_got,
    out_w, gate_w, up_w, down_w, in_sem, out_sem, grad_sem, weight_sem,
    send_sem, recv_sem, da_send, da_recv, far_send, far_recv,
):
    steps = count // 2
    rows = x_hbm.shape[0] // count
    width = x_hbm.shape[1]
    hidden = gate_w.shape[1]
    weights = [
        pltpu.make_async_copy(source, target, weight_sem.at[index])
        for index, (source, target) in enumerate(
            ((out_hbm, out_w), (gate_hbm, gate_w), (up_hbm, up_w), (down_hbm, down_w))
        )
    ]
    side = width // 2
    tile = 256
    broad = 1024
    inner = 256 if hidden % 256 == 0 else 128
    size = da_ref.shape[1]
    place, right, left = ring_setup(count)

    def member(hop):
        spot = lax.rem(place + hop, count)
        return spot, (lax.axis_index("batch"), ring_head(spot, count))

    def owners(group):
        first = jnp.where(group == 0, 1, 0)
        one = lax.rem(place + steps - group, count)
        two = lax.rem(place - steps + group + first * steps + count, count)
        return one, two

    def span(owner):
        return pl.ds(pl.multiple_of(owner * rows, rows), rows)

    def tile_of(at, extent=tile):
        return pl.ds(pl.multiple_of(at * extent, extent), extent)

    def loads(group, slot):
        return [
            pltpu.make_async_copy(
                source.at[span(owner)],
                target.at[pl.ds(at * rows, rows)],
                in_sem.at[slot, 2 * index + at],
            )
            for index, (source, target) in enumerate(
                ((x_hbm, x_s.at[slot]), (a_hbm, a_s.at[slot]), (dy_hbm, dy_all.at[group]))
            )
            for at, owner in enumerate(owners(group))
        ]

    def stores(group, slot):
        return [
            pltpu.make_async_copy(
                mlp_s.at[slot, pl.ds(at * rows, rows)], mlp_hbm.at[span(owner)], out_sem.at[slot, at]
            )
            for at, owner in enumerate(owners(group))
        ]

    def passing(source, target, sems, slot, device):
        return pltpu.make_async_remote_copy(
            src_ref=source,
            dst_ref=target,
            send_sem=sems[0].at[slot],
            recv_sem=sems[1].at[slot],
            device_id=device,
            device_id_type=MESH,
        )

    ring_sems, far_sems = (send_sem, recv_sem), (far_send, far_recv)
    ahead, behind = pl.ds(0, side), pl.ds(side, side)

    def first_copies():
        return (
            passing(right_part.at[0, :, ahead], right_got.at[0, :, ahead], ring_sems, 0, right),
            passing(right_part.at[0, :, behind], left_got.at[0, :, behind], ring_sems, steps, left),
        )

    def later_copies(step):
        return (
            passing(right_got.at[step - 1], right_got.at[step], ring_sems, step, right),
            passing(left_got.at[step - 1], left_got.at[step], ring_sems, steps + step, left),
        )

    for copy in (*loads(0, 0), *weights):
        copy.start()
    greet([member(hop)[1] for hop in range(1, count)])
    weights[0].wait()

    @pl.loop(0, steps)
    def _(group):
        slot = lax.rem(group, 2)
        for copy in loads(group, slot):
            copy.wait()

        @pl.when(group + 1 < steps)
        def _():
            for copy in loads(group + 1, 1 - slot):
                copy.start()

        @pl.when(group >= 2)
        def _():
            for copy in stores(group - 2, slot):
                copy.wait()

        mixed = a_s[slot]

        def residual(at, total):
            cols = tile_of(at, broad)
            values = x_s[slot, :, cols].astype(F32) + matmul(mixed, out_w[:, cols])
            h1_s[:, cols] = values
            return total + jnp.sum(values * values, axis=1, keepdims=True)

        total = lax.fori_loop(0, width // broad, residual, jnp.zeros((2 * rows, 1), F32))
        scale = lax.rsqrt(total / width + EPSILON)

        @pl.when(group == 0)
        def _():
            h1_ref[...] = h1_s[pl.ds(rows, rows)]
            for copy in weights[1:]:
                copy.wait()

        @pl.loop(0, width // tile)
        def _(at):
            cols = tile_of(at)
            n2_all[group, :, cols] = (h1_s[:, cols] * scale * gain_ref[:, cols]).astype(BF)

        normed = n2_all[group]
        dy = dy_all[group]

        @pl.loop(0, hidden // inner)
        def _(at):
            cols = tile_of(at, inner)
            cols_up = pl.ds(pl.multiple_of(hidden + at * inner, inner), inner)
            gate = matmul(normed, gate_w[:, cols])
            up = matmul(normed, up_w[:, cols])
            d_hidden = cols_inner(dy, down_w[cols])
            sig = jax.nn.sigmoid(gate)
            silu = gate * sig
            hid_all[group, :, cols] = (silu * up).astype(BF)
            grad_all[group, :, cols] = (d_hidden * up * sig * (1.0 + gate * (1.0 - sig))).astype(BF)
            grad_all[group, :, cols_up] = (d_hidden * silu).astype(BF)

        hid = hid_all[group]
        d_gate = grad_all[group, :, :hidden]
        d_up = grad_all[group, :, hidden:]
        half = jnp.minimum(group, 1)

        @pl.loop(0, width // broad)
        def _(at):
            cols = tile_of(at, broad)
            part = (cols_inner(d_gate, gate_w[cols]) + cols_inner(d_up, up_w[cols])).astype(BF)
            right_part[half, :, cols] = part[:rows]
            left_part[half, :, cols] = part[rows:]
            mlp_s[slot, :, cols] = matmul(hid, down_w[:, cols]).astype(BF)

        for copy in stores(group, slot):
            copy.start()

        @pl.when(group == 0)
        def _():
            mlp_far[...] = mlp_s[slot, pl.ds(0, rows)]
            for copy in first_copies():
                copy.start()

        @pl.when(group == 1)
        def _():
            mlp_next[0] = mlp_s[slot, pl.ds(0, rows)]
            mlp_next[1] = mlp_s[slot, pl.ds(rows, rows)]
            one, two = first_copies()
            one.wait_recv()
            right_got[0, :, ahead] = add_low(right_part[1, :, ahead], right_got[0, :, ahead])
            right_got[0, :, behind] = right_part[1, :, behind]
            two.wait_recv()
            left_got[0, :, behind] = add_low(left_part[1, :, behind], left_got[0, :, behind])
            left_got[0, :, ahead] = left_part[1, :, ahead]

        @pl.when(group == 2)
        def _():
            ahead_ref[...] = mlp_s[slot, pl.ds(0, rows)]
            behind_ref[...] = mlp_s[slot, pl.ds(rows, rows)]

        @pl.when(group >= 2)
        def _():
            one, two = later_copies(group - 1)
            one.wait_recv()
            right_got[group - 1] = add_low(right_part[1], right_got[group - 1])
            two.wait_recv()
            left_got[group - 1] = add_low(left_part[1], left_got[group - 1])

        @pl.when(group >= 1)
        def _():
            for copy in later_copies(group):
                copy.start()

    far_copies = [
        passing(mlp_far.at[:, ahead], mlp_got.at[0, :, ahead], far_sems, 0, right),
        passing(mlp_far.at[:, behind], mlp_got.at[1, :, behind], far_sems, 1, left),
    ]
    for copy in far_copies:
        copy.start()

    every = steps * 2 * rows

    def dmlp_copy(at, slot):
        return pltpu.make_async_copy(
            dmlp_s.at[slot], dmlp_hbm.at[tile_of(at // 2), tile_of(lax.rem(at, 2), hidden)], grad_sem.at[slot]
        )

    mlp_tiles = 2 * (width // tile)

    @pl.loop(0, mlp_tiles)
    def _(at):
        slot = lax.rem(at, 2)

        @pl.when(at >= 2)
        def _():
            dmlp_copy(at - 2, slot).wait()

        normed = n2_all[:, :, tile_of(at // 2)].reshape(every, tile)
        grads = grad_all[:, :, tile_of(lax.rem(at, 2), hidden)].reshape(every, hidden)
        dmlp_s[slot] = rows_inner(normed, grads).astype(BF)
        dmlp_copy(at, slot).start()

    wide = 512
    across = width // wide

    def ddown_copy(at, slot):
        return pltpu.make_async_copy(
            ddown_s.at[slot],
            ddown_hbm.at[tile_of(at // across, inner), tile_of(lax.rem(at, across), wide)],
            grad_sem.at[2 + slot],
        )

    down_tiles = across * (hidden // inner)

    @pl.loop(0, down_tiles)
    def _(at):
        slot = lax.rem(at, 2)

        @pl.when(at >= 2)
        def _():
            ddown_copy(at - 2, slot).wait()

        hid = hid_all[:, :, tile_of(at // across, inner)].reshape(every, inner)
        dy = dy_all[:, :, tile_of(lax.rem(at, across), wide)].reshape(every, wide)
        ddown_s[slot] = rows_inner(hid, dy).astype(BF)
        ddown_copy(at, slot).start()

    for copy in later_copies(steps - 1):
        copy.wait_recv()
    for flow, have, lack in ((0, ahead, behind), (1, behind, ahead)):
        far_copies[flow].wait_recv()
        mlp_got[flow, :, have] = add_low(mlp_got[flow, :, have], mlp_next[flow, :, have])
        mlp_got[flow, :, lack] = mlp_next[flow, :, lack]
    next_copies = [
        passing(mlp_got.at[0], mlp_got.at[2], far_sems, 2, right),
        passing(mlp_got.at[1], mlp_got.at[3], far_sems, 3, left),
    ]
    for copy in next_copies:
        copy.start()

    def collect(at, state):
        squares, mean = state
        cols = tile_of(at)
        dn2 = (
            left_part[0, :, cols].astype(F32)
            + right_got[steps - 1, :, cols].astype(F32)
            + left_got[steps - 1, :, cols].astype(F32)
        )
        dh1_ref[:, cols] = dn2
        h1 = h1_ref[:, cols]
        squares = squares + jnp.sum(h1 * h1, axis=1, keepdims=True)
        return squares, mean + jnp.sum(gain_ref[:, cols] * dn2 * h1, axis=1, keepdims=True)

    zero = jnp.zeros((rows, 1), F32)
    squares, mean = lax.fori_loop(0, width // tile, collect, (zero, zero))
    scale_own = lax.rsqrt(squares / width + EPSILON)
    pull = scale_own * scale_own * scale_own * (mean / width)

    @pl.loop(0, width // tile)
    def _(at):
        cols = tile_of(at)
        dn2, h1 = dh1_ref[:, cols], h1_ref[:, cols]
        dgain_ref[:, cols] = jnp.sum(dn2 * h1 * scale_own, axis=0, keepdims=True)
        dy = dy_all[0, pl.ds(rows, rows), cols].astype(F32)
        d_resid = dy + scale_own * (gain_ref[:, cols] * dn2) - h1 * pull
        dh1_ref[:, cols] = d_resid
        low_ref[:, cols] = d_resid.astype(BF)

    def da_copy(hop):
        return passing(
            da_part.at[hop], da_ref.at[span(place)], (da_send, da_recv), hop, member(hop)[1]
        )

    low = low_ref[...]

    @pl.loop(1, count)
    def _(hop):
        spot = member(hop)[0]
        da_part[hop] = cols_inner(low, out_w[tile_of(spot, size)]).astype(BF)
        da_copy(hop).start()

    da_ref[span(place)] = cols_inner(low, out_w[tile_of(place, size)]).astype(BF)

    @pl.loop(1, count)
    def _(hop):
        da_copy(hop).wait_recv()
        da_copy(hop).wait_send()

    for flow, held in ((0, ahead_ref), (1, behind_ref)):
        next_copies[flow].wait_recv()
        held[...] = add_low(held[...], mlp_got[2 + flow])
    for copy in (*far_copies, *next_copies, *first_copies()):
        copy.wait_send()
    for step in range(1, steps):
        for copy in later_copies(step):
            copy.wait_send()
    for group in range(steps - 2, steps):
        for copy in stores(group, group % 2):
            copy.wait()
    for at in range(2):
        dmlp_copy(mlp_tiles - 2 + at, (mlp_tiles + at) % 2).wait()
        ddown_copy(down_tiles - 2 + at, (down_tiles + at) % 2).wait()


def mlp_back(tokens, mixed, dy, gain, out_w, gate_w, up_w, down_w, collective_id):
    count = lax.axis_size("head")
    total, width = tokens.shape
    hidden = gate_w.shape[1]
    rows, steps = total // count, count // 2
    size = mixed.shape[1] // count
    inner = 256 if hidden % 256 == 0 else 128
    vmem = pl.BlockSpec(memory_space=pltpu.VMEM)
    hbm = pl.BlockSpec(memory_space=pl.ANY)

    def slots(many, tall, wide, dtype=BF):
        return pltpu.VMEM((many, tall, wide), dtype)

    def shape(*extent, dtype=BF):
        return jax.ShapeDtypeStruct(extent, dtype)

    dma = pltpu.SemaphoreType.DMA
    flops = 2 * total * width * (mixed.shape[1] + 9 * hidden)
    return pl.pallas_call(
        functools.partial(mlp_kernel, count),
        out_shape=[
            shape(total, width), shape(width, 2 * hidden), shape(hidden, width),
            shape(rows, width, dtype=F32), shape(rows, width, dtype=F32), shape(rows, width),
            shape(1, width, dtype=F32), shape(total, size), shape(rows, width), shape(rows, width),
        ],
        in_specs=[hbm] * 3 + [vmem] + [hbm] * 4,
        out_specs=[hbm] * 3 + [vmem] * 7,
        scratch_shapes=[
            slots(2, 2 * rows, width), slots(2, 2 * rows, mixed.shape[1]), slots(2, 2 * rows, width),
            pltpu.VMEM((2 * rows, width), F32),
            slots(steps, 2 * rows, width), slots(steps, 2 * rows, width),
            slots(steps, 2 * rows, hidden), slots(steps, 2 * rows, 2 * hidden),
            slots(2, 256, hidden), slots(2, inner, 512), slots(count, rows, size),
            pltpu.VMEM((rows, width), BF), slots(2, rows, width), slots(4, rows, width),
            slots(2, rows, width), slots(2, rows, width),
            slots(steps, rows, width), slots(steps, rows, width),
            *[pltpu.VMEM(weight.shape, BF) for weight in (out_w, gate_w, up_w, down_w)],
            dma((2, 6)), dma((2, 2)), dma((4,)), dma((4,)), dma((count,)), dma((count,)),
            dma((count,)), dma((count,)), dma((4,)), dma((4,)),
        ],
        compiler_params=pltpu.CompilerParams(
            collective_id=collective_id, has_side_effects=True, vmem_limit_bytes=VMEM_LIMIT
        ),
        cost_estimate=pl.CostEstimate(flops=flops, bytes_accessed=40 << 20, transcendentals=0),
        name="mlp_back",
    )(tokens, mixed, dy, gain, out_w, gate_w, up_w, down_w)


def entry_kernel(
    count, batches, x_ref, w_ref, out_ref, gain_ref, seg_ref,
    n1_ref, q_ref, logit_ref, kv_ref, w_all, out_all, gain_all, seg_all,
    send_sem, recv_sem, local_sem,
):
    steps = count // 2
    others = batches // 2
    rows, width = x_ref.shape
    depth = w_ref.shape[0]
    size, wide = out_ref.shape
    block = 256
    place, right, left = ring_setup(count)
    head = lax.axis_index("head")
    batch = lax.axis_index("batch")
    across, core, low = batch // 2, lax.rem(batch, 2), lax.rem(head, 2)
    twin = (across * 2 + 1 - core, head)
    mate = (batch, head + 1 - 2 * low)
    spots = [lax.rem(across + hop, others) for hop in range(others)]
    backs = [lax.rem(across + others - hop, others) for hop in range(others)]
    peers = [(spot * 2 + core, head) for spot in spots]
    far_peers = [(spot * 2 + 1 - core, head) for spot in spots]
    greet((twin, mate, right, left, *peers[1:], *far_peers[1:]))
    sems = (send_sem, recv_sem)
    slot = 0
    copies = []

    def go(source, target, device):
        nonlocal slot
        copy = send(source, target, sems, slot, device)
        slot += 1
        copies.append(copy)
        return copy

    def part(at, extent):
        return pl.ds(pl.multiple_of(at * extent, extent), extent)

    def both(view, own):
        out = [go(own, view(batch), peers[hop]) for hop in range(1, others)]
        return out, [go(own, view(batch), twin)]

    def pass_on(view, arrived):
        out = []
        for hop in range(1, others):
            arrived[hop - 1].wait_recv()
            there = view(backs[hop] * 2 + core)
            out.append(go(there, there, twin))
        return out

    local = []

    def stay(source, target):
        copy = pltpu.make_async_copy(source, target, local_sem.at[len(local)])
        copy.start()
        local.append(copy)

    def main_view(at):
        return w_all.at[part(at, depth), pl.ds(0, 3 * size)]

    def mate_view(at):
        return w_all.at[part(at, depth), pl.ds(3 * size, size)]

    def out_view(chunk, at):
        return out_all.at[part(chunk, size), part(at, wide)]

    small = []
    for own, whole in ((gain_ref, gain_all), (seg_ref, seg_all)):
        for device in (twin, *peers[1:], *far_peers[1:]):
            small.append(go(own, whole.at[batch], device))
        stay(own, whole.at[batch])
    from_mate = go(w_ref.at[:, pl.ds(2 * size, size)], mate_view(batch), mate)
    main_out, main_twin = both(main_view, w_ref)
    stay(w_ref, main_view(batch))
    out_peers = [go(out_ref, out_view(place, batch), peers[hop]) for hop in range(1, others)]
    stay(out_ref, out_view(place, batch))
    flows = [[None, None] for _ in range(others)]

    def ring(step):
        for hop in range(others):
            lane = spots[0] if hop == 0 else backs[hop]
            at = lane * 2 + core
            if step == 0 and hop:
                out_peers[hop - 1].wait_recv()
            for flow, chunk, device in ((0, place - step, right), (1, place + step, left)):
                if step:
                    flows[hop][flow].wait_recv()
                target = out_view(lax.rem(chunk + count, count), at)
                source = out_ref if step == 0 and hop == 0 else target
                if step == steps - 1:
                    cut = (pl.ds(flow * (size // 2), size // 2), slice(None))
                    source, target = source.at[cut], target.at[cut]
                flows[hop][flow] = go(source, target, device)

    for copy in small:
        copy.wait_recv()
    for copy in local[:2]:
        copy.wait()

    def normalize(at):
        here = part(at, block)

        def squares(tile, total):
            values = x_ref[here, part(tile, 256)].astype(F32)
            return total + jnp.sum(values * values, axis=1, keepdims=True)

        total = lax.fori_loop(0, width // 256, squares, jnp.zeros((block, 1), F32))
        scale = lax.rsqrt(total / width + EPSILON)

        @pl.loop(0, batches)
        def _(owner):
            for tile in range(depth // 128):
                cols = pl.ds(pl.multiple_of(owner * depth + tile * 128, 128), 128)
                values = x_ref[here, cols].astype(F32) * scale
                n1_ref[here, cols] = (values * gain_all[owner, pl.ds(tile, 1)]).astype(BF)

    blocks = rows // block
    middle = blocks // 2

    @pl.loop(0, middle)
    def _(at):
        normalize(at)

    from_mate.wait_recv()
    mate_out, mate_twin = both(mate_view, mate_view(batch))
    ring(0)

    @pl.loop(middle, blocks)
    def _(at):
        normalize(at)

    main_passed = pass_on(main_view, main_out)
    mate_passed = pass_on(mate_view, mate_out)
    for copy in (*main_twin, *mate_twin, *main_passed, *mate_passed):
        copy.wait_recv()
    for copy in local[2:]:
        copy.wait()

    def kv_view(at):
        return kv_ref.at[part(at, rows)]

    @pl.loop(0, blocks)
    def _(at):
        here = part(at, block)
        values = matmul(n1_ref[here], w_all[:, pl.ds(2 * size, 2 * size)])
        one, two = values[:, :size], values[:, size:]
        first = jnp.where(low == 0, one, two).astype(BF)
        second = jnp.where(low == 0, two, one).astype(BF)
        half = size // 2
        there = pl.ds(pl.multiple_of(batch * rows + at * block, block), block)
        kv_ref[there, pl.ds(0, size)] = jnp.concatenate([first[:, :half], second[:, :half]], 1)
        kv_ref[there, pl.ds(size, size)] = jnp.concatenate([first[:, half:], second[:, half:]], 1)

    kv_out, kv_twin = both(kv_view, kv_view(batch))
    ring(1)

    @pl.loop(0, blocks)
    def _(at):
        here = part(at, block)
        values = matmul(n1_ref[here], w_all[:, pl.ds(0, 2 * size)])
        q_ref[here] = values[:, :size].astype(BF)
        logit_ref[here] = values[:, size:]

    for step in range(2, steps):
        ring(step)
    kv_passed = pass_on(kv_view, kv_out)
    for pair in flows:
        for copy in pair:
            copy.wait_recv()
    swaps = []
    for hop in range(others):
        there = out_all.at[:, part(spots[hop] * 2 + core, wide)]
        swaps.append(go(there, there, twin))
    for copy in (*kv_twin, *kv_passed, *swaps):
        copy.wait_recv()
    for copy in copies:
        copy.wait_send()


def entry(tokens, w_shard, w_out, gains, segments, collective_id):
    count = lax.axis_size("head")
    batches = lax.axis_size("batch")
    others = batches // 2
    rows, width = tokens.shape
    size, wide = w_out.shape
    vmem = pl.BlockSpec(memory_space=pltpu.VMEM)
    slots = 6 * batches + others * (count + 3)
    sems = pltpu.SemaphoreType.DMA((slots,))
    return pl.pallas_call(
        functools.partial(entry_kernel, count, batches),
        out_shape=[
            jax.ShapeDtypeStruct((rows, width), BF),
            jax.ShapeDtypeStruct((rows, size), BF),
            jax.ShapeDtypeStruct((rows, size), F32),
            jax.ShapeDtypeStruct((batches * rows, 2 * size), BF),
            jax.ShapeDtypeStruct((width, 4 * size), BF),
            jax.ShapeDtypeStruct((count * size, batches * wide), BF),
            jax.ShapeDtypeStruct((batches, *gains.shape), F32),
            jax.ShapeDtypeStruct((batches, *segments.shape), jnp.int32),
        ],
        in_specs=[vmem] * 5,
        out_specs=[vmem] * 8,
        scratch_shapes=[sems, sems, pltpu.SemaphoreType.DMA((5,))],
        compiler_params=pltpu.CompilerParams(
            collective_id=collective_id, has_side_effects=True, vmem_limit_bytes=VMEM_LIMIT
        ),
        name="entry",
    )(tokens, w_shard, w_out, gains, segments)


KEY_BLOCK = 512
QUERY_BLOCK = 256


def key_range(start_ref, base, query_block):
    first = query_block * QUERY_BLOCK
    lowest = start_ref[first]
    highest = start_ref[first + QUERY_BLOCK - 1]
    begin = lowest // KEY_BLOCK
    end = (base + first + QUERY_BLOCK - 1) // KEY_BLOCK + 1
    full_begin = jnp.minimum((highest + KEY_BLOCK - 1) // KEY_BLOCK, end)
    full_end = jnp.maximum((base + first + 1) // KEY_BLOCK, full_begin)
    return begin, full_begin, full_end, end


def allowed_pairs(key_block, start_row, base_row):
    shape = (KEY_BLOCK, QUERY_BLOCK)
    key_pos = key_block * KEY_BLOCK + lax.broadcasted_iota(jnp.int32, shape, 0)
    query_pos = base_row + lax.broadcasted_iota(jnp.int32, shape, 1)
    return (key_pos >= start_row) & (key_pos <= query_pos)


def attend_kernel(
    scale, start_sm, base_sm, q_ref, kv_ref, start_ref, logit_ref, o_ref, a_ref, lse_ref
):
    base = base_sm[0]
    size = q_ref.shape[1]
    factor = scale * math.log2(math.e)

    @pl.loop(0, q_ref.shape[0] // QUERY_BLOCK)
    def _(block):
        rows = pl.ds(pl.multiple_of(block * QUERY_BLOCK, QUERY_BLOCK), QUERY_BLOCK)
        queries = q_ref[rows]
        start_row = start_ref[:, rows]
        begin, full_begin, full_end, end = key_range(start_sm, base, block)

        def step(masked, at, state):
            old_max, old_sum, total = state
            keys = pl.ds(pl.multiple_of(at * KEY_BLOCK, KEY_BLOCK), KEY_BLOCK)
            scores = cols_inner(kv_ref[keys, :size], queries)
            if masked:
                allowed = allowed_pairs(at, start_row, base + block * QUERY_BLOCK)
                scores = jnp.where(allowed, scores, MASKED)
            new_max = jnp.maximum(old_max, jnp.max(scores, axis=0, keepdims=True))
            keep = jnp.exp2((old_max - new_max) * factor)
            weights = jnp.exp2(scores * factor - new_max * factor)
            new_sum = old_sum * keep + jnp.sum(weights, axis=0, keepdims=True)
            total = total * keep + rows_inner(kv_ref[keys, size:], weights.astype(BF))
            return new_max, new_sum, total

        state = (
            jnp.full((1, QUERY_BLOCK), MASKED, F32),
            jnp.zeros((1, QUERY_BLOCK), F32),
            jnp.zeros((size, QUERY_BLOCK), F32),
        )
        state = lax.fori_loop(begin, full_begin, functools.partial(step, True), state)
        state = lax.fori_loop(full_begin, full_end, functools.partial(step, False), state)
        state = lax.fori_loop(full_end, end, functools.partial(step, True), state)
        run_max, run_sum, total = state
        lse_ref[:, rows] = run_max * factor + jnp.log2(run_sum)
        attended = (total / run_sum).T
        o_ref[rows] = attended
        a_ref[rows] = (attended * jax.nn.sigmoid(logit_ref[rows])).astype(BF)


def attend_back_kernel(
    scale, start_sm, base_sm, q_ref, kv_ref, start_ref, logit_ref, o_ref, da_ref, lse_ref,
    dq_ref, dg_ref, dkv_ref, dk_acc, dv_acc,
):
    base = base_sm[0]
    size = q_ref.shape[1]
    factor = scale * math.log2(math.e)
    dk_acc[...] = jnp.zeros_like(dk_acc)
    dv_acc[...] = jnp.zeros_like(dv_acc)

    @pl.loop(0, q_ref.shape[0] // QUERY_BLOCK)
    def _(block):
        rows = pl.ds(pl.multiple_of(block * QUERY_BLOCK, QUERY_BLOCK), QUERY_BLOCK)
        queries = q_ref[rows]
        start_row = start_ref[:, rows]
        lse = lse_ref[:, rows]
        gate = jax.nn.sigmoid(logit_ref[rows])
        attended = o_ref[rows]
        d_mixed = da_ref[rows].astype(F32)
        d_attended = (d_mixed * gate).astype(BF)
        dg_ref[rows] = (d_mixed * attended * gate * (1.0 - gate)).astype(BF)
        delta = jnp.sum((d_attended.astype(F32) * attended).T, axis=0, keepdims=True)
        begin, full_begin, full_end, end = key_range(start_sm, base, block)

        def step(masked, at, d_queries):
            keys = pl.ds(pl.multiple_of(at * KEY_BLOCK, KEY_BLOCK), KEY_BLOCK)
            key_block = kv_ref[keys, :size]
            probs = jnp.exp2(cols_inner(key_block, queries) * factor - lse)
            if masked:
                allowed = allowed_pairs(at, start_row, base + block * QUERY_BLOCK)
                probs = jnp.where(allowed, probs, 0.0)
            d_probs = cols_inner(kv_ref[keys, size:], d_attended)
            d_scores = (probs * (d_probs - delta) * scale).astype(BF)
            dv_acc[keys] += matmul(probs.astype(BF), d_attended)
            dk_acc[keys] += matmul(d_scores, queries)
            return d_queries + rows_inner(key_block, d_scores)

        d_queries = jnp.zeros((size, QUERY_BLOCK), F32)
        d_queries = lax.fori_loop(begin, full_begin, functools.partial(step, True), d_queries)
        d_queries = lax.fori_loop(full_begin, full_end, functools.partial(step, False), d_queries)
        d_queries = lax.fori_loop(full_end, end, functools.partial(step, True), d_queries)
        dq_ref[rows] = d_queries.T.astype(BF)

    @pl.loop(0, kv_ref.shape[0] // KEY_BLOCK)
    def _(at):
        keys = pl.ds(pl.multiple_of(at * KEY_BLOCK, KEY_BLOCK), KEY_BLOCK)
        dk, dv = dk_acc[keys].astype(BF), dv_acc[keys].astype(BF)
        half = size // 2
        dkv_ref[keys, :size] = jnp.concatenate([dk[:, :half], dv[:, :half]], axis=1)
        dkv_ref[keys, size:] = jnp.concatenate([dk[:, half:], dv[:, half:]], axis=1)


def tail_kernel(
    count, batches, dq_ref, dg_ref, dkv_ref, w_ref, gain_ref, dh1_ref, second_ref,
    low_ref, h1_ref, ahead_ref, behind_ref, n1_ref, x_hbm, mixed_hbm, mlp_hbm,
    out_all, tok_all, gains_ref, wout_own, din_ref,
    part_ref, tok_ref, got, wout_got, gain_own, gain_got, gain_mid, gain_heads,
    din_s, din_got, din_x, wout_s, wout_twin, wout_x,
    cat_ref, out_s, out_got, core_got, x_first, x_second, y_first, y_second, held, n1_s,
    x_ref, mixed_ref, mlp_ref, send_sem, recv_sem, local_sem,
):
    steps = count // 2
    rows, width = x_ref.shape
    depth = cat_ref.shape[1]
    tall, size = dq_ref.shape
    tile = 256
    place, right, left = ring_setup(count)
    batch, head = lax.axis_index("batch"), lax.axis_index("head")
    others = [lax.rem(batch + hop, batches) for hop in range(1, batches)]
    members = [(batch, ring_head(lax.rem(place + hop, count), count)) for hop in range(1, count)]
    greet((*members, *[(other, head) for other in others]))
    sems = (send_sem, recv_sem)
    slot = 0
    copies = []

    def go(source, target, device):
        nonlocal slot
        copy = send(source, target, sems, slot, device)
        slot += 1
        copies.append(copy)
        return copy

    across, core = batch // 2, lax.rem(batch, 2)
    spots = [lax.rem(across + hop, batches // 2) for hop in range(batches // 2)]
    order = list(range(1, batches // 2)) + [0]
    twin = (across * 2 + 1 - core, head)

    def scatter_swap(view, held):
        return [go(view(2 * spots[hop] + 1 - core), held.at[spots[hop]], twin) for hop in order]

    def add_tiles(target, one, other):
        @pl.loop(0, target.shape[0] // 128)
        def _(at):
            lines = pl.ds(pl.multiple_of(at * 128, 128), 128)
            total = one[lines].astype(F32) + other[lines].astype(F32)
            target[lines] = total.astype(target.dtype)

    def scatter_cross(view, held, crossed, arriving):
        out = []
        for copy, hop in zip(arriving, order):
            copy.wait_recv()
            spot = spots[hop]
            add_tiles(held.at[spot], held.at[spot], view(2 * spot + core))
            if hop:
                out.append(go(held.at[spot], crossed.at[hop - 1], (spot * 2 + core, head)))
        return out

    def scatter_end(held, crossed, arriving, target):
        for hop, copy in enumerate(arriving):
            copy.wait_recv()
            last = hop == len(arriving) - 1
            add_tiles(target if last else held.at[across], held.at[across], crossed.at[hop])

    def wout_view(at):
        wide = width // batches
        return wout_s.at[:, pl.ds(pl.multiple_of(at * wide, wide), wide)]

    def din_view(at):
        tall = din_ref.shape[0]
        return din_s.at[pl.ds(pl.multiple_of(at * tall, tall), tall)]

    def span(owner, extent):
        return pl.ds(pl.multiple_of(lax.rem(owner + count, count) * extent, extent), extent)

    def compute(owner):
        here = span(owner, rows)
        values = cat_ref[here]

        @pl.loop(0, width // tile)
        def _(at):
            cols = pl.ds(pl.multiple_of(at * tile, tile), tile)
            part_ref[here, cols] = cols_inner(values, w_ref[cols, pl.ds(0, depth)]).astype(BF)

    def gather(own, whole, step, last):
        out = []
        for flow, chunk, device in ((0, place - step, right), (1, place + step, left)):
            if last:
                last[flow].wait_recv()
            target = whole.at[lax.rem(chunk + count, count)]
            source = target if step else own
            if step == steps - 1:
                cut = (slice(None), pl.ds(flow * (width // 2), width // 2))
                source, target = source.at[cut], target.at[cut]
            out.append(go(source, target, device))
        return out

    def reduce(parts, held, step, last):
        extent, side = held.shape[2], held.shape[3] // 2
        out = []
        for flow, owner, device in (
            (0, place + steps - step, right),
            (1, place - steps + step, left),
        ):
            have = pl.ds(flow * side, side)
            lack = pl.ds((1 - flow) * side, side)
            mine = parts.at[span(owner, extent)]
            if step == 0:
                out.append(go(mine.at[:, have], held.at[flow, 0, :, have], device))
                continue
            last[flow].wait_recv()
            if step == 1:
                held[flow, 0, :, have] = add_low(held[flow, 0, :, have], mine[:, have])
                held[flow, 0, :, lack] = mine[:, lack]
            else:
                held[flow, step - 1] = add_low(held[flow, step - 1], mine[...])
            out.append(go(held.at[flow, step - 1], held.at[flow, step], device))
        return out

    low = lax.rem(head, 2)
    mate = (batch, head + 1 - 2 * low)
    peers = [(spot * 2 + core, head) for spot in spots]
    mine = pl.ds(pl.multiple_of(low * size, size), size)
    given = pl.ds(pl.multiple_of((1 - low) * size, size), size)
    top, bottom = pl.ds(0, tall // 2), pl.ds(tall // 2, tall // 2)
    fresh = pl.ds(2 * size, size)

    def keys_of(at):
        return dkv_ref.at[pl.ds(pl.multiple_of(at * tall, tall), tall)]

    def normed_copy(at, slot):
        cols = pl.ds(pl.multiple_of(at * tile, tile), tile)
        return pltpu.make_async_copy(n1_ref.at[:, cols], n1_s.at[slot], local_sem.at[2 + slot])

    own_rows = pl.ds(pl.multiple_of(place * rows, rows), rows)
    fetches = [
        pltpu.make_async_copy(source.at[own_rows], target, local_sem.at[4 + index])
        for index, (source, target) in enumerate(
            ((mixed_hbm, mixed_ref), (mlp_hbm, mlp_ref), (x_hbm, x_ref))
        )
    ]
    for copy in fetches:
        copy.start()
    for at in range(2):
        normed_copy(at, at).start()
    last_sums = [go(ahead_ref, out_got.at[0], right), go(behind_ref, out_got.at[1], left)]
    swaps = scatter_swap(keys_of, core_got)
    cat_ref[:, pl.ds(0, size)] = dq_ref[...]
    cat_ref[:, pl.ds(size, size)] = dg_ref[...]
    for copy in fetches:
        copy.wait()

    @pl.loop(0, width // tile)
    def _(at):
        cols = pl.ds(pl.multiple_of(at * tile, tile), tile)
        wout_s[:, cols] = rows_inner(mixed_ref[...], low_ref[:, cols]).astype(BF)

    tops, bottoms = [], []
    for copy, hop in zip(swaps, order):
        copy.wait_recv()
        spot = spots[hop]
        add_tiles(core_got.at[spot], core_got.at[spot], keys_of(2 * spot + core))
        bottoms.append(go(core_got.at[spot, bottom, given], y_first.at[spot], mate))
        if hop:
            tops.append(go(core_got.at[spot, top], x_first.at[hop - 1], peers[hop]))
    wouts = scatter_swap(wout_view, wout_twin)
    for copy in last_sums:
        copy.wait_recv()
    out_s[...] = (
        h1_ref[...] + mlp_ref[...].astype(F32) + out_got[0].astype(F32) + out_got[1].astype(F32)
    ).astype(BF)
    keep_out = pltpu.make_async_copy(out_s, out_all.at[place], local_sem.at[0])
    keep_out.start()
    outs = gather(out_s, out_all, 0, None)
    total = core_got[across, top].astype(F32)
    for hop, copy in enumerate(tops):
        copy.wait_recv()
        total = total + x_first[hop].astype(F32)
    held[...] = total.astype(BF)
    last = go(held.at[:, given], y_second, mate)
    ends = []
    for copy, hop in zip(bottoms, order):
        copy.wait_recv()
        spot = spots[hop]
        y_first[spot] = add_low(y_first[spot], core_got[spot, bottom, mine])
        if hop:
            ends.append(go(y_first.at[spot], x_second.at[hop - 1], peers[hop]))
    last.wait_recv()
    cat_ref[top, fresh] = add_low(held[:, mine], y_second[...])
    total = y_first[across].astype(F32)
    for hop, copy in enumerate(ends):
        copy.wait_recv()
        total = total + x_second[hop].astype(F32)
    cat_ref[bottom, fresh] = total.astype(BF)

    compute(place + steps)
    sums = reduce(part_ref, got, 0, None)
    outs = gather(out_s, out_all, 1, outs)

    @pl.loop(1, count)
    def _(hop):
        compute(place + steps + hop)

    @pl.loop(0, width // tile)
    def _(at):
        slot = lax.rem(at, 2)
        normed_copy(at, slot).wait()
        cols = pl.ds(pl.multiple_of(at * tile, tile), tile)
        din_s[cols] = rows_inner(n1_s[slot], cat_ref[...]).astype(BF)

        @pl.when(at + 2 < width // tile)
        def _():
            normed_copy(at + 2, slot).start()

    dins = scatter_swap(din_view, din_got)
    for step in range(1, steps):
        sums = reduce(part_ref, got, step, sums)
        if step + 1 < steps:
            outs = gather(out_s, out_all, step + 1, outs)
        if step == 1:
            wouts = scatter_cross(wout_view, wout_twin, wout_x, wouts)
            dins = scatter_cross(din_view, din_got, din_x, dins)
    for copy in sums:
        copy.wait_recv()

    def tile_of(at):
        return pl.ds(pl.multiple_of(at * tile, tile), tile)

    def total(cols):
        return (
            part_ref[span(place, rows), cols].astype(F32)
            + got[0, steps - 1, :, cols].astype(F32)
            + got[1, steps - 1, :, cols].astype(F32)
        )

    def collect(at, state):
        squares, mean = state
        cols = tile_of(at)
        x = x_ref[:, cols].astype(F32)
        squares = squares + jnp.sum(x * x, axis=1, keepdims=True)
        return squares, mean + jnp.sum(gain_ref[:, cols] * total(cols) * x, axis=1, keepdims=True)

    zero = jnp.zeros((rows, 1), F32)
    squares, mean = lax.fori_loop(0, width // tile, collect, (zero, zero))
    scale = lax.rsqrt(squares / width + EPSILON)
    pull = scale * scale * scale * (mean / width)

    @pl.loop(0, width // tile)
    def _(at):
        cols = tile_of(at)
        x, dn1 = x_ref[:, cols].astype(F32), total(cols)
        gain_own[pl.ds(0, 1), cols] = jnp.sum(dn1 * x * scale, axis=0, keepdims=True)
        gain_own[pl.ds(1, 1), cols] = second_ref[:, cols]
        tok_ref[:, cols] = (dh1_ref[:, cols] + scale * (gain_ref[:, cols] * dn1) - x * pull).astype(BF)

    keep_tok = pltpu.make_async_copy(tok_ref, tok_all.at[place], local_sem.at[1])
    keep_tok.start()
    toks = gather(tok_ref, tok_all, 0, None)
    wout_part = wout_twin.at[across]
    scatter_end(wout_twin, wout_x, wouts, wout_part)
    wsums = reduce(wout_part, wout_got, 0, None)
    scatter_end(din_got, din_x, dins, din_ref)
    wide = width // batches

    def slice_of(at):
        return pl.ds(pl.multiple_of(at * wide, wide), wide)

    gains = [
        go(gain_own.at[:, slice_of(other)], gain_got.at[hop], (other, head))
        for hop, other in enumerate(others)
    ]
    toks = gather(tok_ref, tok_all, 1, toks)
    wsums = reduce(wout_part, wout_got, 1, wsums)
    middle = gain_own[:, slice_of(batch)]
    for hop, copy in enumerate(gains):
        copy.wait_recv()
        middle = middle + gain_got[hop]
    gain_mid[...] = middle
    gain_heads[place] = middle
    gains = [go(gain_mid, gain_heads.at[place], member) for member in members]
    for step in range(2, steps):
        toks = gather(tok_ref, tok_all, step, toks)
        wsums = reduce(wout_part, wout_got, step, wsums)
    for copy in gains:
        copy.wait_recv()
    middle = gain_heads[0]
    for at in range(1, count):
        middle = middle + gain_heads[at]
    gains_ref[...] = middle
    for copy in (*wsums, *outs):
        copy.wait_recv()
    wout_own[...] = (
        wout_part[span(place, wout_own.shape[0])].astype(F32)
        + wout_got[0, steps - 1].astype(F32)
        + wout_got[1, steps - 1].astype(F32)
    )
    for copy in toks:
        copy.wait_recv()
    for copy in copies:
        copy.wait_send()
    keep_out.wait()
    keep_tok.wait()


def tail(arrays, collective_id):
    d_queries, tokens, mixed = arrays[0], arrays[-3], arrays[-2]
    count = lax.axis_size("head")
    batches = lax.axis_size("batch")
    steps = count // 2
    rows, width = tokens.shape[0] // count, tokens.shape[1]
    others = batches // 2
    size, wide = mixed.shape[1] // count, width // batches
    tall, head_size = d_queries.shape
    depth = 3 * head_size
    vmem = pl.BlockSpec(memory_space=pltpu.VMEM)
    hbm = pl.BlockSpec(memory_space=pl.ANY)
    whole = (count, rows, width)
    sems = pltpu.SemaphoreType.DMA((6 * count + 6 * batches,))
    gains = (2, width // batches)
    return pl.pallas_call(
        functools.partial(tail_kernel, count, batches),
        out_shape=[
            jax.ShapeDtypeStruct(whole, BF),
            jax.ShapeDtypeStruct(whole, BF),
            jax.ShapeDtypeStruct(gains, F32),
            jax.ShapeDtypeStruct((size, wide), F32),
            jax.ShapeDtypeStruct((wide, depth), F32),
        ],
        in_specs=[vmem] * 11 + [hbm] * 4,
        out_specs=[hbm] * 2 + [vmem] * 3,
        scratch_shapes=[
            pltpu.VMEM((count * rows, width), BF),
            pltpu.VMEM((rows, width), BF),
            pltpu.VMEM((2, steps, rows, width), BF),
            pltpu.VMEM((2, steps, size, wide), BF),
            pltpu.VMEM((2, width), F32),
            pltpu.VMEM((batches - 1, *gains), F32),
            pltpu.VMEM(gains, F32),
            pltpu.VMEM((count, *gains), F32),
            pltpu.VMEM((width, depth), BF),
            pltpu.VMEM((others, wide, depth), BF),
            pltpu.VMEM((others - 1, wide, depth), BF),
            pltpu.VMEM((count * size, width), BF),
            pltpu.VMEM((others, count * size, wide), BF),
            pltpu.VMEM((others - 1, count * size, wide), BF),
            pltpu.VMEM((tall, depth), BF),
            pltpu.VMEM((rows, width), BF),
            pltpu.VMEM((2, rows, width), BF),
            pltpu.VMEM((others, tall, 2 * head_size), BF),
            pltpu.VMEM((others - 1, tall // 2, 2 * head_size), BF),
            pltpu.VMEM((others - 1, tall // 2, head_size), BF),
            pltpu.VMEM((others, tall // 2, head_size), BF),
            pltpu.VMEM((tall // 2, head_size), BF),
            pltpu.VMEM((tall // 2, 2 * head_size), BF),
            pltpu.VMEM((2, tall, 256), BF),
            pltpu.VMEM((rows, width), BF),
            pltpu.VMEM((rows, mixed.shape[1]), BF),
            pltpu.VMEM((rows, width), BF),
            sems,
            sems,
            pltpu.SemaphoreType.DMA((7,)),
        ],
        compiler_params=pltpu.CompilerParams(
            collective_id=collective_id, has_side_effects=True, vmem_limit_bytes=VMEM_LIMIT
        ),
        cost_estimate=pl.CostEstimate(
            flops=4 * count * rows * width * depth, bytes_accessed=400 << 20, transcendentals=0
        ),
        name="tail",
    )(*arrays)


def finish_kernel(out_ref, tok_ref, gate_ref, up_ref, down_ref, *results):
    for source, target in zip((out_ref, tok_ref, gate_ref, up_ref, down_ref), results):
        value = source[...]
        target[...] = value.reshape(target.shape).astype(target.dtype)


def finish(output, d_tokens, d_mlp, d_down):
    count, rows, width = output.shape
    tall, hidden = d_mlp.shape[0], d_mlp.shape[1] // 2
    down_rows, wide = d_down.shape
    whole_in = pl.BlockSpec((1, rows, width), lambda i: (i, 0, 0))
    whole_out = pl.BlockSpec((rows, width), lambda i: (i, 0))
    gate = pl.BlockSpec((tall // count, hidden), lambda i: (i, 0))
    up = pl.BlockSpec((tall // count, hidden), lambda i: (i, 1))
    down = pl.BlockSpec((down_rows // count, wide), lambda i: (i, 0))
    return pl.pallas_call(
        finish_kernel,
        grid=(count,),
        out_shape=[
            jax.ShapeDtypeStruct((count * rows, width), BF),
            jax.ShapeDtypeStruct((count * rows, width), BF),
            jax.ShapeDtypeStruct((tall, hidden), F32),
            jax.ShapeDtypeStruct((tall, hidden), F32),
            jax.ShapeDtypeStruct((down_rows, wide), F32),
        ],
        in_specs=[whole_in, whole_in, gate, up, down],
        out_specs=[whole_out, whole_out, gate, gate, down],
        compiler_params=pltpu.CompilerParams(vmem_limit_bytes=VMEM_LIMIT),
        name="finish",
    )(output, d_tokens, d_mlp, d_mlp, d_down)


def local_call(kernel, scalars, arrays, outs, scratch, flops, name):
    vmem = pl.BlockSpec(memory_space=pltpu.VMEM)
    smem = pl.BlockSpec(memory_space=pltpu.SMEM)
    return pl.pallas_call(
        kernel,
        out_shape=outs,
        in_specs=[smem] * len(scalars) + [vmem] * len(arrays),
        out_specs=[vmem] * len(outs),
        scratch_shapes=scratch,
        compiler_params=pltpu.CompilerParams(vmem_limit_bytes=VMEM_LIMIT),
        cost_estimate=pl.CostEstimate(flops=flops, bytes_accessed=8 << 20, transcendentals=0),
        name=name,
    )(*scalars, *arrays)


def ring_routes(count):
    spots = [ring_head(at, count) for at in range(count)]
    right = [(spots[at], spots[(at + 1) % count]) for at in range(count)]
    left = [(spots[at], spots[at - 1]) for at in range(count)]
    return right, left


def add_low(one, other):
    return (one.astype(F32) + other.astype(F32)).astype(BF)


def flow_steps(part, going, coming):
    count = lax.axis_size("head")
    place = ring_place(lax.axis_index("head"), count)
    right, left = ring_routes(count)
    rows = part.shape[0] // count
    steps = count // 2

    def mine(owner):
        return lax.dynamic_slice_in_dim(part, lax.rem(owner + count, count) * rows, rows, 0)

    for step in range(2, steps - 1):
        from_left = lax.ppermute(going, "head", right)
        from_right = lax.ppermute(coming, "head", left)
        going = add_low(from_left, mine(place + steps - 1 - step))
        coming = add_low(from_right, mine(place - steps + 1 + step))
        going, coming = yield going, coming


def matmul(left, right):
    return jnp.dot(left, right, preferred_element_type=F32)


def rows_inner(left, right):
    return lax.dot_general(left, right, (((0,), (0,)), ((), ())), preferred_element_type=F32)


def cols_inner(left, right):
    return lax.dot_general(left, right, (((1,), (1,)), ((), ())), preferred_element_type=F32)


def rms_scale(values):
    return lax.rsqrt(jnp.mean(values * values, axis=1, keepdims=True) + EPSILON)


def per_device(
    tokens,
    segment_ids,
    norm1_gain,
    w_query,
    w_key,
    w_value,
    w_gate,
    w_out,
    norm2_gain,
    w_mlp_gate,
    w_mlp_up,
    w_down,
    out_grad,
):
    heads = lax.axis_size("head")
    batches = lax.axis_size("batch")
    row_count, width = tokens.shape
    head_size = w_query.shape[1]
    half = w_key.shape[1]
    chunk = row_count // heads
    me = ring_place(lax.axis_index("head"), heads)
    scale_factor = 1.0 / math.sqrt(head_size)

    w_shard = jnp.concatenate([w_query, w_gate, w_key, w_value], axis=1)
    gains = jnp.concatenate([norm1_gain, norm2_gain]).reshape(-1, 128).astype(F32)
    normed_one, queries, gate_logit, kv_all, w_in, out_full, gains, seg_all = entry(
        tokens, w_shard, w_out, gains, segment_ids.reshape(-1, 128), 1
    )
    gains, w_mlp_gate = lax.optimization_barrier((gains, w_mlp_gate))
    seg_all = seg_all.reshape(-1)
    gains = gains.reshape(batches, 2, -1).transpose(1, 0, 2).reshape(2, width)
    gain_one, gain_two = gains[0], gains[1]
    mgate_full = lax.all_gather(w_mlp_gate, "batch", axis=0, tiled=True)

    base = lax.axis_index("batch") * row_count
    ids = jnp.arange(DOCUMENTS, dtype=jnp.int32)
    below = jnp.sum((seg_all[None, :] < ids[:, None]).astype(jnp.int32), axis=1)
    starts = jnp.sum(jnp.where(segment_ids[None, :] == ids[:, None], below[:, None], 0), axis=0)
    scalars = (starts, base.reshape(1))
    pair_flops = 4 * row_count * kv_all.shape[0] * head_size
    attended, mixed, lse = local_call(
        functools.partial(attend_kernel, scale_factor),
        scalars,
        (queries, kv_all, starts[None], gate_logit),
        [
            jax.ShapeDtypeStruct((row_count, head_size), F32),
            jax.ShapeDtypeStruct((row_count, head_size), BF),
            jax.ShapeDtypeStruct((1, row_count), F32),
        ],
        [],
        pair_flops,
        "attend",
    )
    mixed_all, down_full, mup_full = spread(
        [mixed, w_down, w_mlp_up], (("head", "cols"), ("batch", "cols"), ("batch", "rows")), 2
    )
    (
        mlp_part, d_mlp, d_down, resid_own, d_resid, d_resid_low, d_gain_two, d_mixed, going, coming,
    ) = mlp_back(
        tokens, mixed_all, out_grad, gain_two[None], out_full, mgate_full, mup_full, down_full, 3
    )
    hold = lax.optimization_barrier
    flow = flow_steps(mlp_part, going, coming)
    state = next(flow)

    d_queries, d_gate_logit, d_kv_all = local_call(
        functools.partial(attend_back_kernel, scale_factor),
        scalars,
        (queries, kv_all, starts[None], gate_logit, attended, d_mixed, lse),
        [
            jax.ShapeDtypeStruct((row_count, head_size), BF),
            jax.ShapeDtypeStruct((row_count, head_size), BF),
            jax.ShapeDtypeStruct(kv_all.shape, BF),
        ],
        [pltpu.VMEM((kv_all.shape[0], head_size), F32)] * 2,
        5 * pair_flops // 2,
        "attend_back",
    )
    for _ in range(3, heads // 2 - 1):
        state = flow.send(state)
    d_down = lax.psum_scatter(d_down, "batch", scatter_dimension=1, tiled=True)
    d_mlp = lax.psum_scatter(d_mlp, "batch", scatter_dimension=0, tiled=True)
    output, d_tokens, d_gains, d_out, d_in = tail(
        (
            d_queries, d_gate_logit, d_kv_all, w_in, gain_one[None], d_resid, d_gain_two,
            d_resid_low, resid_own, *state, normed_one, tokens, mixed_all, mlp_part,
        ),
        5,
    )
    output, d_tokens, d_mgate, d_mup, d_down = finish(output, d_tokens, d_mlp, d_down)
    return (
        output,
        d_tokens,
        d_gains[0],
        d_in[:, :head_size],
        d_in[:, 2 * head_size : 2 * head_size + half],
        d_in[:, 2 * head_size + half :],
        d_in[:, head_size : 2 * head_size],
        d_out,
        d_gains[1],
        d_mgate,
        d_mup,
        d_down,
    )


def solution(mesh):
    return jax.shard_map(
        per_device,
        mesh=mesh,
        in_specs=(
            P("batch", None),
            P("batch"),
            P("batch"),
            P("batch", "head"),
            P("batch", "head"),
            P("batch", "head"),
            P("batch", "head"),
            P("head", "batch"),
            P("batch"),
            P("batch", "head"),
            P("batch", "head"),
            P("head", "batch"),
            P("batch", None),
        ),
        out_specs=(
            P("batch", None),
            P("batch", None),
            P("batch"),
            P("batch", "head"),
            P("batch", "head"),
            P("batch", "head"),
            P("batch", "head"),
            P("head", "batch"),
            P("batch"),
            P("batch", "head"),
            P("batch", "head"),
            P("head", "batch"),
        ),
        check_vma=False,
    )
```

```python
import functools
import math

import jax
import jax.numpy as jnp
from jax import lax
from jax.experimental import pallas as pl
from jax.experimental.pallas import tpu as pltpu
from jax.sharding import PartitionSpec as P

EPSILON = 1e-06
MASKED = -1e30
DOCUMENTS = 7
BF = jnp.bfloat16
F32 = jnp.float32


MESH = pl.DeviceIdType.MESH
VMEM_LIMIT = 60 << 20


def ring_place(head, count):
    high, low = head // 2, head % 2
    return (1 - low) * high + low * (count - 1 - high)


def ring_head(place, count):
    low = place // (count // 2)
    high = (1 - low) * place + low * (count - 1 - place)
    return 2 * high + low


def ring_setup(count):
    batch = lax.axis_index("batch")
    place = ring_place(lax.axis_index("head"), count)
    right = (batch, ring_head(lax.rem(place + 1, count), count))
    left = (batch, ring_head(lax.rem(place + count - 1, count), count))
    return place, right, left


def greet(devices):
    barrier = pltpu.get_barrier_semaphore()
    for device in devices:
        pl.semaphore_signal(barrier, inc=1, device_id=device, device_id_type=MESH)
    pl.semaphore_wait(barrier, len(devices))


def send(source, target, sems, slot, device):
    copy = pltpu.make_async_remote_copy(
        src_ref=source,
        dst_ref=target,
        send_sem=sems[0].at[slot],
        recv_sem=sems[1].at[slot],
        device_id=device,
        device_id_type=MESH,
    )
    copy.start()
    return copy


def half_of(extent, flow):
    if extent[1] % 256:
        return (pl.ds(flow * (extent[0] // 2), extent[0] // 2), slice(None))
    return (slice(None), pl.ds(flow * (extent[1] // 2), extent[1] // 2))


def place_of(whole, own, chunk, form):
    rows, wide = own.shape[-2:]
    if form == "lead":
        return whole.at[chunk]
    if form == "rows":
        return whole.at[pl.ds(pl.multiple_of(chunk * rows, rows), rows)]
    return whole.at[:, pl.ds(pl.multiple_of(chunk * wide, wide), wide)]


def spread_kernel(count, batches, plans, *refs):
    steps = count // 2
    arrays = len(plans)
    own_refs, all_refs = refs[:arrays], refs[arrays : 2 * arrays]
    send_sem, recv_sem, local_sem = refs[2 * arrays :]
    place, right, left = ring_setup(count)
    head = lax.axis_index("head")
    batch = lax.axis_index("batch")
    across, core = batch // 2, lax.rem(batch, 2)
    others = batches // 2
    twin = (across * 2 + 1 - core, head)
    peers = [(lax.rem(across + hop, others) * 2 + core, head) for hop in range(1, others)]
    ring = any(axis == "head" for axis, _ in plans)
    grid = any(axis == "batch" for axis, _ in plans)
    greet((right, left) * ring + (twin, *peers) * grid)
    sems = (send_sem, recv_sem)
    slot = 0
    waiting, arriving, local = [], [], []

    def go(source, target, device):
        nonlocal slot
        copy = send(source, target, sems, slot, device)
        slot += 1
        waiting.append(copy)
        return copy

    stages = []
    for index, (axis, form) in enumerate(plans):
        own, whole = own_refs[index], all_refs[index]
        spot = place if axis == "head" else batch
        copy = pltpu.make_async_copy(own, place_of(whole, own, spot, form), local_sem.at[index])
        copy.start()
        local.append(copy)
        if axis == "batch":
            stages.append(index)
    onward = []

    def stage():
        for copy, block in onward:
            copy.wait_recv()
            arriving.append(go(block, block, twin))
        onward.clear()
        if stages:
            index = stages.pop(0)
            own, whole, form = own_refs[index], all_refs[index], plans[index][1]
            mine = place_of(whole, own, batch, form)
            for hop, peer in enumerate(peers, 1):
                source = lax.rem(across + others - hop, others) * 2 + core
                onward.append((go(own, mine, peer), place_of(whole, own, source, form)))
            arriving.append(go(own, mine, twin))

    stage()
    copies = [None] * (2 * arrays)
    for step in range(steps):
        for index, (axis, form) in enumerate(plans):
            if axis != "head":
                continue
            own = own_refs[index]
            for flow, chunk, device in ((0, place - step, right), (1, place + step, left)):
                at = 2 * index + flow
                if step:
                    copies[at].wait_recv()
                chunk = lax.rem(chunk + count, count)
                target = place_of(all_refs[index], own, chunk, form)
                source = target if step else own
                if step == steps - 1:
                    part = half_of(own.shape, flow)
                    source = source.at[part]
                    target = target.at[part]
                copies[at] = go(source, target, device)
        if step == steps // 2:
            stage()
    while stages or onward:
        stage()
    for copy in copies:
        if copy is not None:
            arriving.append(copy)
    for copy in arriving:
        copy.wait_recv()
    for copy in waiting:
        copy.wait_send()
    for copy in local:
        copy.wait()


def spread(arrays, plans, collective_id):
    count = lax.axis_size("head")
    batches = lax.axis_size("batch")
    shapes = []
    slots = 0
    for array, (axis, form) in zip(arrays, plans):
        many = count if axis == "head" else batches
        slots += count if axis == "head" else batches - 1
        if form == "lead":
            shapes.append((many, *array.shape))
        elif form == "rows":
            shapes.append((many * array.shape[0], array.shape[1]))
        else:
            shapes.append((array.shape[0], many * array.shape[1]))
    hbm = pl.BlockSpec(memory_space=pl.ANY)
    return pl.pallas_call(
        functools.partial(spread_kernel, count, batches, plans),
        out_shape=[jax.ShapeDtypeStruct(shape, a.dtype) for shape, a in zip(shapes, arrays)],
        in_specs=[pl.BlockSpec(memory_space=pltpu.VMEM)] * len(arrays),
        out_specs=[hbm] * len(arrays),
        scratch_shapes=[
            pltpu.SemaphoreType.DMA((slots,)),
            pltpu.SemaphoreType.DMA((slots,)),
            pltpu.SemaphoreType.DMA((len(arrays),)),
        ],
        compiler_params=pltpu.CompilerParams(
            collective_id=collective_id, has_side_effects=True, vmem_limit_bytes=VMEM_LIMIT
        ),
        name=f"spread_{collective_id}",
    )(*arrays)


def mlp_kernel(
    count, x_hbm, a_hbm, dy_hbm, gain_ref, out_hbm, gate_hbm, up_hbm, down_hbm,
    mlp_hbm, dmlp_hbm, ddown_hbm, h1_ref, dh1_ref, low_ref, dgain_ref, da_ref, ahead_ref, behind_ref,
    x_s, a_s, mlp_s, h1_s, dy_all, n2_all, hid_all, grad_all, dmlp_s, ddown_s, da_part,
    mlp_far, mlp_next, mlp_got, right_part, left_part, right_got, left_got,
    out_w, gate_w, up_w, down_w, in_sem, out_sem, grad_sem, weight_sem,
    send_sem, recv_sem, da_send, da_recv, far_send, far_recv,
):
    steps = count // 2
    rows = x_hbm.shape[0] // count
    width = x_hbm.shape[1]
    hidden = gate_w.shape[1]
    weights = [
        pltpu.make_async_copy(source, target, weight_sem.at[index])
        for index, (source, target) in enumerate(
            ((out_hbm, out_w), (gate_hbm, gate_w), (up_hbm, up_w), (down_hbm, down_w))
        )
    ]
    side = width // 2
    tile = 256
    broad = 1024
    inner = 256 if hidden % 256 == 0 else 128
    size = da_ref.shape[1]
    place, right, left = ring_setup(count)

    def member(hop):
        spot = lax.rem(place + hop, count)
        return spot, (lax.axis_index("batch"), ring_head(spot, count))

    def owners(group):
        first = jnp.where(group == 0, 1, 0)
        one = lax.rem(place + steps - group, count)
        two = lax.rem(place - steps + group + first * steps + count, count)
        return one, two

    def span(owner):
        return pl.ds(pl.multiple_of(owner * rows, rows), rows)

    def tile_of(at, extent=tile):
        return pl.ds(pl.multiple_of(at * extent, extent), extent)

    def loads(group, slot):
        return [
            pltpu.make_async_copy(
                source.at[span(owner)],
                target.at[pl.ds(at * rows, rows)],
                in_sem.at[slot, 2 * index + at],
            )
            for index, (source, target) in enumerate(
                ((x_hbm, x_s.at[slot]), (a_hbm, a_s.at[slot]), (dy_hbm, dy_all.at[group]))
            )
            for at, owner in enumerate(owners(group))
        ]

    def stores(group, slot):
        return [
            pltpu.make_async_copy(
                mlp_s.at[slot, pl.ds(at * rows, rows)], mlp_hbm.at[span(owner)], out_sem.at[slot, at]
            )
            for at, owner in enumerate(owners(group))
        ]

    def passing(source, target, sems, slot, device):
        return pltpu.make_async_remote_copy(
            src_ref=source,
            dst_ref=target,
            send_sem=sems[0].at[slot],
            recv_sem=sems[1].at[slot],
            device_id=device,
            device_id_type=MESH,
        )

    ring_sems, far_sems = (send_sem, recv_sem), (far_send, far_recv)
    ahead, behind = pl.ds(0, side), pl.ds(side, side)

    def first_copies():
        return (
            passing(right_part.at[0, :, ahead], right_got.at[0, :, ahead], ring_sems, 0, right),
            passing(right_part.at[0, :, behind], left_got.at[0, :, behind], ring_sems, steps, left),
        )

    def later_copies(step):
        return (
            passing(right_got.at[step - 1], right_got.at[step], ring_sems, step, right),
            passing(left_got.at[step - 1], left_got.at[step], ring_sems, steps + step, left),
        )

    for copy in (*loads(0, 0), *weights):
        copy.start()
    greet([member(hop)[1] for hop in range(1, count)])
    weights[0].wait()

    @pl.loop(0, steps)
    def _(group):
        slot = lax.rem(group, 2)
        for copy in loads(group, slot):
            copy.wait()

        @pl.when(group + 1 < steps)
        def _():
            for copy in loads(group + 1, 1 - slot):
                copy.start()

        @pl.when(group >= 2)
        def _():
            for copy in stores(group - 2, slot):
                copy.wait()

        mixed = a_s[slot]

        def residual(at, total):
            cols = tile_of(at, broad)
            values = x_s[slot, :, cols].astype(F32) + matmul(mixed, out_w[:, cols])
            h1_s[:, cols] = values
            return total + jnp.sum(values * values, axis=1, keepdims=True)

        total = lax.fori_loop(0, width // broad, residual, jnp.zeros((2 * rows, 1), F32))
        scale = lax.rsqrt(total / width + EPSILON)

        @pl.when(group == 0)
        def _():
            h1_ref[...] = h1_s[pl.ds(rows, rows)]
            for copy in weights[1:]:
                copy.wait()

        @pl.loop(0, width // tile)
        def _(at):
            cols = tile_of(at)
            n2_all[group, :, cols] = (h1_s[:, cols] * scale * gain_ref[:, cols]).astype(BF)

        normed = n2_all[group]
        dy = dy_all[group]

        @pl.loop(0, hidden // inner)
        def _(at):
            cols = tile_of(at, inner)
            cols_up = pl.ds(pl.multiple_of(hidden + at * inner, inner), inner)
            gate = matmul(normed, gate_w[:, cols])
            up = matmul(normed, up_w[:, cols])
            d_hidden = cols_inner(dy, down_w[cols])
            sig = jax.nn.sigmoid(gate)
            silu = gate * sig
            hid_all[group, :, cols] = (silu * up).astype(BF)
            grad_all[group, :, cols] = (d_hidden * up * sig * (1.0 + gate * (1.0 - sig))).astype(BF)
            grad_all[group, :, cols_up] = (d_hidden * silu).astype(BF)

        hid = hid_all[group]
        d_gate = grad_all[group, :, :hidden]
        d_up = grad_all[group, :, hidden:]
        half = jnp.minimum(group, 1)

        @pl.loop(0, width // broad)
        def _(at):
            cols = tile_of(at, broad)
            part = (cols_inner(d_gate, gate_w[cols]) + cols_inner(d_up, up_w[cols])).astype(BF)
            right_part[half, :, cols] = part[:rows]
            left_part[half, :, cols] = part[rows:]

        @pl.when(group == 0)
        def _():
            for copy in first_copies():
                copy.start()

        @pl.when(group == 1)
        def _():
            one, two = first_copies()
            one.wait_recv()
            right_got[0, :, ahead] = add_low(right_part[1, :, ahead], right_got[0, :, ahead])
            right_got[0, :, behind] = right_part[1, :, behind]
            two.wait_recv()
            left_got[0, :, behind] = add_low(left_part[1, :, behind], left_got[0, :, behind])
            left_got[0, :, ahead] = left_part[1, :, ahead]

        @pl.when(group >= 2)
        def _():
            one, two = later_copies(group - 1)
            one.wait_recv()
            right_got[group - 1] = add_low(right_part[1], right_got[group - 1])
            two.wait_recv()
            left_got[group - 1] = add_low(left_part[1], left_got[group - 1])

        @pl.when(group >= 1)
        def _():
            for copy in later_copies(group):
                copy.start()

        @pl.loop(0, width // broad)
        def _(at):
            cols = tile_of(at, broad)
            mlp_s[slot, :, cols] = matmul(hid, down_w[:, cols]).astype(BF)

        for copy in stores(group, slot):
            copy.start()

        @pl.when(group == 0)
        def _():
            mlp_far[...] = mlp_s[slot, pl.ds(0, rows)]

        @pl.when(group == 1)
        def _():
            mlp_next[0] = mlp_s[slot, pl.ds(0, rows)]
            mlp_next[1] = mlp_s[slot, pl.ds(rows, rows)]

        @pl.when(group == 2)
        def _():
            ahead_ref[...] = mlp_s[slot, pl.ds(0, rows)]
            behind_ref[...] = mlp_s[slot, pl.ds(rows, rows)]

    far_copies = [
        passing(mlp_far.at[:, ahead], mlp_got.at[0, :, ahead], far_sems, 0, right),
        passing(mlp_far.at[:, behind], mlp_got.at[1, :, behind], far_sems, 1, left),
    ]
    for copy in far_copies:
        copy.start()

    every = steps * 2 * rows

    def dmlp_copy(at, slot):
        return pltpu.make_async_copy(
            dmlp_s.at[slot], dmlp_hbm.at[tile_of(at // 2), tile_of(lax.rem(at, 2), hidden)], grad_sem.at[slot]
        )

    mlp_tiles = 2 * (width // tile)

    @pl.loop(0, mlp_tiles)
    def _(at):
        slot = lax.rem(at, 2)

        @pl.when(at >= 2)
        def _():
            dmlp_copy(at - 2, slot).wait()

        normed = n2_all[:, :, tile_of(at // 2)].reshape(every, tile)
        grads = grad_all[:, :, tile_of(lax.rem(at, 2), hidden)].reshape(every, hidden)
        dmlp_s[slot] = rows_inner(normed, grads).astype(BF)
        dmlp_copy(at, slot).start()

    wide = 512
    across = width // wide

    def ddown_copy(at, slot):
        return pltpu.make_async_copy(
            ddown_s.at[slot],
            ddown_hbm.at[tile_of(at // across, inner), tile_of(lax.rem(at, across), wide)],
            grad_sem.at[2 + slot],
        )

    down_tiles = across * (hidden // inner)

    @pl.loop(0, down_tiles)
    def _(at):
        slot = lax.rem(at, 2)

        @pl.when(at >= 2)
        def _():
            ddown_copy(at - 2, slot).wait()

        hid = hid_all[:, :, tile_of(at // across, inner)].reshape(every, inner)
        dy = dy_all[:, :, tile_of(lax.rem(at, across), wide)].reshape(every, wide)
        ddown_s[slot] = rows_inner(hid, dy).astype(BF)
        ddown_copy(at, slot).start()

    for copy in later_copies(steps - 1):
        copy.wait_recv()
    for flow, have, lack in ((0, ahead, behind), (1, behind, ahead)):
        far_copies[flow].wait_recv()
        mlp_got[flow, :, have] = add_low(mlp_got[flow, :, have], mlp_next[flow, :, have])
        mlp_got[flow, :, lack] = mlp_next[flow, :, lack]
    next_copies = [
        passing(mlp_got.at[0], mlp_got.at[2], far_sems, 2, right),
        passing(mlp_got.at[1], mlp_got.at[3], far_sems, 3, left),
    ]
    for copy in next_copies:
        copy.start()

    def collect(at, state):
        squares, mean = state
        cols = tile_of(at)
        dn2 = (
            left_part[0, :, cols].astype(F32)
            + right_got[steps - 1, :, cols].astype(F32)
            + left_got[steps - 1, :, cols].astype(F32)
        )
        dh1_ref[:, cols] = dn2
        h1 = h1_ref[:, cols]
        squares = squares + jnp.sum(h1 * h1, axis=1, keepdims=True)
        return squares, mean + jnp.sum(gain_ref[:, cols] * dn2 * h1, axis=1, keepdims=True)

    zero = jnp.zeros((rows, 1), F32)
    squares, mean = lax.fori_loop(0, width // tile, collect, (zero, zero))
    scale_own = lax.rsqrt(squares / width + EPSILON)
    pull = scale_own * scale_own * scale_own * (mean / width)

    @pl.loop(0, width // tile)
    def _(at):
        cols = tile_of(at)
        dn2, h1 = dh1_ref[:, cols], h1_ref[:, cols]
        dgain_ref[:, cols] = jnp.sum(dn2 * h1 * scale_own, axis=0, keepdims=True)
        dy = dy_all[0, pl.ds(rows, rows), cols].astype(F32)
        d_resid = dy + scale_own * (gain_ref[:, cols] * dn2) - h1 * pull
        dh1_ref[:, cols] = d_resid
        low_ref[:, cols] = d_resid.astype(BF)

    def da_copy(hop):
        return passing(
            da_part.at[hop], da_ref.at[span(place)], (da_send, da_recv), hop, member(hop)[1]
        )

    low = low_ref[...]

    @pl.loop(1, count)
    def _(hop):
        spot = member(hop)[0]
        da_part[hop] = cols_inner(low, out_w[tile_of(spot, size)]).astype(BF)
        da_copy(hop).start()

    da_ref[span(place)] = cols_inner(low, out_w[tile_of(place, size)]).astype(BF)

    @pl.loop(1, count)
    def _(hop):
        da_copy(hop).wait_recv()
        da_copy(hop).wait_send()

    for flow, held in ((0, ahead_ref), (1, behind_ref)):
        next_copies[flow].wait_recv()
        held[...] = add_low(held[...], mlp_got[2 + flow])
    for copy in (*far_copies, *next_copies, *first_copies()):
        copy.wait_send()
    for step in range(1, steps):
        for copy in later_copies(step):
            copy.wait_send()
    for group in range(steps - 2, steps):
        for copy in stores(group, group % 2):
            copy.wait()
    for at in range(2):
        dmlp_copy(mlp_tiles - 2 + at, (mlp_tiles + at) % 2).wait()
        ddown_copy(down_tiles - 2 + at, (down_tiles + at) % 2).wait()


def mlp_back(tokens, mixed, dy, gain, out_w, gate_w, up_w, down_w, collective_id):
    count = lax.axis_size("head")
    total, width = tokens.shape
    hidden = gate_w.shape[1]
    rows, steps = total // count, count // 2
    size = mixed.shape[1] // count
    inner = 256 if hidden % 256 == 0 else 128
    vmem = pl.BlockSpec(memory_space=pltpu.VMEM)
    hbm = pl.BlockSpec(memory_space=pl.ANY)

    def slots(many, tall, wide, dtype=BF):
        return pltpu.VMEM((many, tall, wide), dtype)

    def shape(*extent, dtype=BF):
        return jax.ShapeDtypeStruct(extent, dtype)

    dma = pltpu.SemaphoreType.DMA
    flops = 2 * total * width * (mixed.shape[1] + 9 * hidden)
    return pl.pallas_call(
        functools.partial(mlp_kernel, count),
        out_shape=[
            shape(total, width), shape(width, 2 * hidden), shape(hidden, width),
            shape(rows, width, dtype=F32), shape(rows, width, dtype=F32), shape(rows, width),
            shape(1, width, dtype=F32), shape(total, size), shape(rows, width), shape(rows, width),
        ],
        in_specs=[hbm] * 3 + [vmem] + [hbm] * 4,
        out_specs=[hbm] * 3 + [vmem] * 7,
        scratch_shapes=[
            slots(2, 2 * rows, width), slots(2, 2 * rows, mixed.shape[1]), slots(2, 2 * rows, width),
            pltpu.VMEM((2 * rows, width), F32),
            slots(steps, 2 * rows, width), slots(steps, 2 * rows, width),
            slots(steps, 2 * rows, hidden), slots(steps, 2 * rows, 2 * hidden),
            slots(2, 256, hidden), slots(2, inner, 512), slots(count, rows, size),
            pltpu.VMEM((rows, width), BF), slots(2, rows, width), slots(4, rows, width),
            slots(2, rows, width), slots(2, rows, width),
            slots(steps, rows, width), slots(steps, rows, width),
            *[pltpu.VMEM(weight.shape, BF) for weight in (out_w, gate_w, up_w, down_w)],
            dma((2, 6)), dma((2, 2)), dma((4,)), dma((4,)), dma((count,)), dma((count,)),
            dma((count,)), dma((count,)), dma((4,)), dma((4,)),
        ],
        compiler_params=pltpu.CompilerParams(
            collective_id=collective_id, has_side_effects=True, vmem_limit_bytes=VMEM_LIMIT
        ),
        cost_estimate=pl.CostEstimate(flops=flops, bytes_accessed=40 << 20, transcendentals=0),
        name="mlp_back",
    )(tokens, mixed, dy, gain, out_w, gate_w, up_w, down_w)


def entry_kernel(
    count, batches, x_ref, w_ref, out_ref, gain_ref, seg_ref,
    n1_ref, q_ref, logit_ref, kv_ref, w_all, out_all, gain_all, seg_all,
    send_sem, recv_sem, local_sem,
):
    steps = count // 2
    others = batches // 2
    rows, width = x_ref.shape
    depth = w_ref.shape[0]
    size, wide = out_ref.shape
    block = 256
    place, right, left = ring_setup(count)
    head = lax.axis_index("head")
    batch = lax.axis_index("batch")
    across, core, low = batch // 2, lax.rem(batch, 2), lax.rem(head, 2)
    twin = (across * 2 + 1 - core, head)
    mate = (batch, head + 1 - 2 * low)
    spots = [lax.rem(across + hop, others) for hop in range(others)]
    backs = [lax.rem(across + others - hop, others) for hop in range(others)]
    peers = [(spot * 2 + core, head) for spot in spots]
    far_peers = [(spot * 2 + 1 - core, head) for spot in spots]
    greet((twin, mate, right, left, *peers[1:], *far_peers[1:]))
    sems = (send_sem, recv_sem)
    slot = 0
    copies = []

    def go(source, target, device):
        nonlocal slot
        copy = send(source, target, sems, slot, device)
        slot += 1
        copies.append(copy)
        return copy

    def part(at, extent):
        return pl.ds(pl.multiple_of(at * extent, extent), extent)

    def both(view, own):
        out = [go(own, view(batch), peers[hop]) for hop in range(1, others)]
        return out, [go(own, view(batch), twin)]

    def pass_on(view, arrived):
        out = []
        for hop in range(1, others):
            arrived[hop - 1].wait_recv()
            there = view(backs[hop] * 2 + core)
            out.append(go(there, there, twin))
        return out

    local = []

    def stay(source, target):
        copy = pltpu.make_async_copy(source, target, local_sem.at[len(local)])
        copy.start()
        local.append(copy)

    def main_view(at):
        return w_all.at[part(at, depth), pl.ds(0, 3 * size)]

    def mate_view(at):
        return w_all.at[part(at, depth), pl.ds(3 * size, size)]

    def out_view(chunk, at):
        return out_all.at[part(chunk, size), part(at, wide)]

    small = []
    for own, whole in ((gain_ref, gain_all), (seg_ref, seg_all)):
        for device in (twin, *peers[1:], *far_peers[1:]):
            small.append(go(own, whole.at[batch], device))
        stay(own, whole.at[batch])
    from_mate = go(w_ref.at[:, pl.ds(2 * size, size)], mate_view(batch), mate)
    main_out, main_twin = both(main_view, w_ref)
    stay(w_ref, main_view(batch))
    out_peers = [go(out_ref, out_view(place, batch), peers[hop]) for hop in range(1, others)]
    stay(out_ref, out_view(place, batch))
    flows = [[None, None] for _ in range(others)]

    def ring(step):
        for hop in range(others):
            lane = spots[0] if hop == 0 else backs[hop]
            at = lane * 2 + core
            if step == 0 and hop:
                out_peers[hop - 1].wait_recv()
            for flow, chunk, device in ((0, place - step, right), (1, place + step, left)):
                if step:
                    flows[hop][flow].wait_recv()
                target = out_view(lax.rem(chunk + count, count), at)
                source = out_ref if step == 0 and hop == 0 else target
                if step == steps - 1:
                    cut = (pl.ds(flow * (size // 2), size // 2), slice(None))
                    source, target = source.at[cut], target.at[cut]
                flows[hop][flow] = go(source, target, device)

    for copy in small:
        copy.wait_recv()
    for copy in local[:2]:
        copy.wait()

    def normalize(at):
        here = part(at, block)

        def squares(tile, total):
            values = x_ref[here, part(tile, 256)].astype(F32)
            return total + jnp.sum(values * values, axis=1, keepdims=True)

        total = lax.fori_loop(0, width // 256, squares, jnp.zeros((block, 1), F32))
        scale = lax.rsqrt(total / width + EPSILON)

        @pl.loop(0, batches)
        def _(owner):
            for tile in range(depth // 128):
                cols = pl.ds(pl.multiple_of(owner * depth + tile * 128, 128), 128)
                values = x_ref[here, cols].astype(F32) * scale
                n1_ref[here, cols] = (values * gain_all[owner, pl.ds(tile, 1)]).astype(BF)

    blocks = rows // block
    middle = blocks // 2

    @pl.loop(0, middle)
    def _(at):
        normalize(at)

    from_mate.wait_recv()
    mate_out, mate_twin = both(mate_view, mate_view(batch))
    ring(0)

    @pl.loop(middle, blocks)
    def _(at):
        normalize(at)

    main_passed = pass_on(main_view, main_out)
    mate_passed = pass_on(mate_view, mate_out)
    for copy in (*main_twin, *mate_twin, *main_passed, *mate_passed):
        copy.wait_recv()
    for copy in local[2:]:
        copy.wait()

    def kv_view(at):
        return kv_ref.at[part(at, rows)]

    @pl.loop(0, blocks)
    def _(at):
        here = part(at, block)
        values = matmul(n1_ref[here], w_all[:, pl.ds(2 * size, 2 * size)])
        one, two = values[:, :size], values[:, size:]
        first = jnp.where(low == 0, one, two).astype(BF)
        second = jnp.where(low == 0, two, one).astype(BF)
        half = size // 2
        there = pl.ds(pl.multiple_of(batch * rows + at * block, block), block)
        kv_ref[there, pl.ds(0, size)] = jnp.concatenate([first[:, :half], second[:, :half]], 1)
        kv_ref[there, pl.ds(size, size)] = jnp.concatenate([first[:, half:], second[:, half:]], 1)

    kv_out, kv_twin = both(kv_view, kv_view(batch))
    ring(1)

    @pl.loop(0, blocks)
    def _(at):
        here = part(at, block)
        values = matmul(n1_ref[here], w_all[:, pl.ds(0, 2 * size)])
        q_ref[here] = values[:, :size].astype(BF)
        logit_ref[here] = values[:, size:]

    for step in range(2, steps):
        ring(step)
    kv_passed = pass_on(kv_view, kv_out)
    for pair in flows:
        for copy in pair:
            copy.wait_recv()
    swaps = []
    for hop in range(others):
        there = out_all.at[:, part(spots[hop] * 2 + core, wide)]
        swaps.append(go(there, there, twin))
    for copy in (*kv_twin, *kv_passed, *swaps):
        copy.wait_recv()
    for copy in copies:
        copy.wait_send()


def entry(tokens, w_shard, w_out, gains, segments, collective_id):
    count = lax.axis_size("head")
    batches = lax.axis_size("batch")
    others = batches // 2
    rows, width = tokens.shape
    size, wide = w_out.shape
    vmem = pl.BlockSpec(memory_space=pltpu.VMEM)
    slots = 6 * batches + others * (count + 3)
    sems = pltpu.SemaphoreType.DMA((slots,))
    return pl.pallas_call(
        functools.partial(entry_kernel, count, batches),
        out_shape=[
            jax.ShapeDtypeStruct((rows, width), BF),
            jax.ShapeDtypeStruct((rows, size), BF),
            jax.ShapeDtypeStruct((rows, size), F32),
            jax.ShapeDtypeStruct((batches * rows, 2 * size), BF),
            jax.ShapeDtypeStruct((width, 4 * size), BF),
            jax.ShapeDtypeStruct((count * size, batches * wide), BF),
            jax.ShapeDtypeStruct((batches, *gains.shape), F32),
            jax.ShapeDtypeStruct((batches, *segments.shape), jnp.int32),
        ],
        in_specs=[vmem] * 5,
        out_specs=[vmem] * 8,
        scratch_shapes=[sems, sems, pltpu.SemaphoreType.DMA((5,))],
        compiler_params=pltpu.CompilerParams(
            collective_id=collective_id, has_side_effects=True, vmem_limit_bytes=VMEM_LIMIT
        ),
        name="entry",
    )(tokens, w_shard, w_out, gains, segments)


KEY_BLOCK = 512
QUERY_BLOCK = 640


def key_range(start_ref, base, query_block):
    first = query_block * QUERY_BLOCK
    lowest = start_ref[first]
    highest = start_ref[first + QUERY_BLOCK - 1]
    begin = lowest // KEY_BLOCK
    end = (base + first + QUERY_BLOCK - 1) // KEY_BLOCK + 1
    full_begin = jnp.minimum((highest + KEY_BLOCK - 1) // KEY_BLOCK, end)
    full_end = jnp.maximum((base + first + 1) // KEY_BLOCK, full_begin)
    return begin, full_begin, full_end, end


def allowed_pairs(key_block, start_row, base_row):
    shape = (KEY_BLOCK, QUERY_BLOCK)
    key_pos = key_block * KEY_BLOCK + lax.broadcasted_iota(jnp.int32, shape, 0)
    query_pos = base_row + lax.broadcasted_iota(jnp.int32, shape, 1)
    return (key_pos >= start_row) & (key_pos <= query_pos)


def attend_kernel(
    scale, start_sm, base_sm, q_ref, kv_ref, start_ref, logit_ref, o_ref, a_ref, lse_ref
):
    base = base_sm[0]
    size = q_ref.shape[1]
    factor = scale * math.log2(math.e)

    @pl.loop(0, q_ref.shape[0] // QUERY_BLOCK)
    def _(block):
        rows = pl.ds(pl.multiple_of(block * QUERY_BLOCK, QUERY_BLOCK), QUERY_BLOCK)
        queries = q_ref[rows]
        start_row = start_ref[:, rows]
        begin, full_begin, full_end, end = key_range(start_sm, base, block)

        def step(masked, at, state):
            old_max, old_sum, total = state
            keys = pl.ds(pl.multiple_of(at * KEY_BLOCK, KEY_BLOCK), KEY_BLOCK)
            scores = cols_inner(kv_ref[keys, :size], queries)
            if masked:
                allowed = allowed_pairs(at, start_row, base + block * QUERY_BLOCK)
                scores = jnp.where(allowed, scores, MASKED)
            new_max = jnp.maximum(old_max, jnp.max(scores, axis=0, keepdims=True))
            keep = jnp.exp2((old_max - new_max) * factor)
            weights = jnp.exp2(scores * factor - new_max * factor)
            new_sum = old_sum * keep + jnp.sum(weights, axis=0, keepdims=True)
            total = total * keep + rows_inner(kv_ref[keys, size:], weights.astype(BF))
            return new_max, new_sum, total

        state = (
            jnp.full((1, QUERY_BLOCK), MASKED, F32),
            jnp.zeros((1, QUERY_BLOCK), F32),
            jnp.zeros((size, QUERY_BLOCK), F32),
        )
        state = lax.fori_loop(begin, full_begin, functools.partial(step, True), state)
        state = lax.fori_loop(full_begin, full_end, functools.partial(step, False), state)
        state = lax.fori_loop(full_end, end, functools.partial(step, True), state)
        run_max, run_sum, total = state
        lse_ref[:, rows] = run_max * factor + jnp.log2(run_sum)
        attended = (total / run_sum).T
        o_ref[rows] = attended
        a_ref[rows] = (attended * jax.nn.sigmoid(logit_ref[rows])).astype(BF)


def attend_back_kernel(
    scale, start_sm, base_sm, q_ref, kv_ref, start_ref, logit_ref, o_ref, da_ref, lse_ref,
    dq_ref, dg_ref, dkv_ref, dk_acc, dv_acc,
):
    base = base_sm[0]
    size = q_ref.shape[1]
    factor = scale * math.log2(math.e)
    dk_acc[...] = jnp.zeros_like(dk_acc)
    dv_acc[...] = jnp.zeros_like(dv_acc)

    @pl.loop(0, q_ref.shape[0] // QUERY_BLOCK)
    def _(block):
        rows = pl.ds(pl.multiple_of(block * QUERY_BLOCK, QUERY_BLOCK), QUERY_BLOCK)
        queries = q_ref[rows]
        start_row = start_ref[:, rows]
        lse = lse_ref[:, rows]
        gate = jax.nn.sigmoid(logit_ref[rows])
        attended = o_ref[rows]
        d_mixed = da_ref[rows].astype(F32)
        d_attended = (d_mixed * gate).astype(BF)
        dg_ref[rows] = (d_mixed * attended * gate * (1.0 - gate)).astype(BF)
        delta = jnp.sum((d_attended.astype(F32) * attended).T, axis=0, keepdims=True)
        begin, full_begin, full_end, end = key_range(start_sm, base, block)

        def step(masked, at, d_queries):
            keys = pl.ds(pl.multiple_of(at * KEY_BLOCK, KEY_BLOCK), KEY_BLOCK)
            key_block = kv_ref[keys, :size]
            probs = jnp.exp2(cols_inner(key_block, queries) * factor - lse)
            if masked:
                allowed = allowed_pairs(at, start_row, base + block * QUERY_BLOCK)
                probs = jnp.where(allowed, probs, 0.0)
            d_probs = cols_inner(kv_ref[keys, size:], d_attended)
            d_scores = (probs * (d_probs - delta) * scale).astype(BF)
            dv_acc[keys] += matmul(probs.astype(BF), d_attended)
            dk_acc[keys] += matmul(d_scores, queries)
            return d_queries + rows_inner(key_block, d_scores)

        d_queries = jnp.zeros((size, QUERY_BLOCK), F32)
        d_queries = lax.fori_loop(begin, full_begin, functools.partial(step, True), d_queries)
        d_queries = lax.fori_loop(full_begin, full_end, functools.partial(step, False), d_queries)
        d_queries = lax.fori_loop(full_end, end, functools.partial(step, True), d_queries)
        dq_ref[rows] = d_queries.T.astype(BF)

    @pl.loop(0, kv_ref.shape[0] // KEY_BLOCK)
    def _(at):
        keys = pl.ds(pl.multiple_of(at * KEY_BLOCK, KEY_BLOCK), KEY_BLOCK)
        dk, dv = dk_acc[keys].astype(BF), dv_acc[keys].astype(BF)
        half = size // 2
        dkv_ref[keys, :size] = jnp.concatenate([dk[:, :half], dv[:, :half]], axis=1)
        dkv_ref[keys, size:] = jnp.concatenate([dk[:, half:], dv[:, half:]], axis=1)


def tail_kernel(
    count, batches, dq_ref, dg_ref, dkv_ref, w_ref, gain_ref, dh1_ref, second_ref,
    low_ref, h1_ref, ahead_ref, behind_ref, n1_ref, x_hbm, mixed_hbm, mlp_hbm,
    out_all, tok_all, gains_ref, wout_own, din_ref,
    part_ref, tok_ref, got, wout_got, gain_own, gain_got, gain_mid, gain_heads,
    din_s, din_got, din_x, wout_s, wout_twin, wout_x,
    cat_ref, out_s, out_got, core_got, x_first, x_second, y_first, y_second, held, n1_s,
    x_ref, mixed_ref, mlp_ref, send_sem, recv_sem, local_sem,
):
    steps = count // 2
    rows, width = x_ref.shape
    depth = cat_ref.shape[1]
    tall, size = dq_ref.shape
    tile = 256
    place, right, left = ring_setup(count)
    batch, head = lax.axis_index("batch"), lax.axis_index("head")
    others = [lax.rem(batch + hop, batches) for hop in range(1, batches)]
    members = [(batch, ring_head(lax.rem(place + hop, count), count)) for hop in range(1, count)]
    greet((*members, *[(other, head) for other in others]))
    sems = (send_sem, recv_sem)
    slot = 0
    copies = []

    def go(source, target, device):
        nonlocal slot
        copy = send(source, target, sems, slot, device)
        slot += 1
        copies.append(copy)
        return copy

    across, core = batch // 2, lax.rem(batch, 2)
    spots = [lax.rem(across + hop, batches // 2) for hop in range(batches // 2)]
    order = list(range(1, batches // 2)) + [0]
    twin = (across * 2 + 1 - core, head)

    def scatter_swap(view, held):
        return [go(view(2 * spots[hop] + 1 - core), held.at[spots[hop]], twin) for hop in order]

    def add_tiles(target, one, other):
        @pl.loop(0, target.shape[0] // 128)
        def _(at):
            lines = pl.ds(pl.multiple_of(at * 128, 128), 128)
            total = one[lines].astype(F32) + other[lines].astype(F32)
            target[lines] = total.astype(target.dtype)

    def scatter_cross(view, held, crossed, arriving):
        out = []
        for copy, hop in zip(arriving, order):
            copy.wait_recv()
            spot = spots[hop]
            add_tiles(held.at[spot], held.at[spot], view(2 * spot + core))
            if hop:
                out.append(go(held.at[spot], crossed.at[hop - 1], (spot * 2 + core, head)))
        return out

    def scatter_end(held, crossed, arriving, target):
        for hop, copy in enumerate(arriving):
            copy.wait_recv()
            last = hop == len(arriving) - 1
            add_tiles(target if last else held.at[across], held.at[across], crossed.at[hop])

    def wout_view(at):
        wide = width // batches
        return wout_s.at[:, pl.ds(pl.multiple_of(at * wide, wide), wide)]

    def din_view(at):
        tall = din_ref.shape[0]
        return din_s.at[pl.ds(pl.multiple_of(at * tall, tall), tall)]

    def span(owner, extent):
        return pl.ds(pl.multiple_of(lax.rem(owner + count, count) * extent, extent), extent)

    def compute(owner):
        here = span(owner, rows)
        values = cat_ref[here]

        @pl.loop(0, width // tile)
        def _(at):
            cols = pl.ds(pl.multiple_of(at * tile, tile), tile)
            part_ref[here, cols] = cols_inner(values, w_ref[cols, pl.ds(0, depth)]).astype(BF)

    def gather(own, whole, step, last):
        out = []
        for flow, chunk, device in ((0, place - step, right), (1, place + step, left)):
            if last:
                last[flow].wait_recv()
            target = whole.at[lax.rem(chunk + count, count)]
            source = target if step else own
            if step == steps - 1:
                cut = (slice(None), pl.ds(flow * (width // 2), width // 2))
                source, target = source.at[cut], target.at[cut]
            out.append(go(source, target, device))
        return out

    def reduce(parts, held, step, last):
        extent, side = held.shape[2], held.shape[3] // 2
        out = []
        for flow, owner, device in (
            (0, place + steps - step, right),
            (1, place - steps + step, left),
        ):
            have = pl.ds(flow * side, side)
            lack = pl.ds((1 - flow) * side, side)
            mine = parts.at[span(owner, extent)]
            if step == 0:
                out.append(go(mine.at[:, have], held.at[flow, 0, :, have], device))
                continue
            last[flow].wait_recv()
            if step == 1:
                held[flow, 0, :, have] = add_low(held[flow, 0, :, have], mine[:, have])
                held[flow, 0, :, lack] = mine[:, lack]
            else:
                held[flow, step - 1] = add_low(held[flow, step - 1], mine[...])
            out.append(go(held.at[flow, step - 1], held.at[flow, step], device))
        return out

    low = lax.rem(head, 2)
    mate = (batch, head + 1 - 2 * low)
    peers = [(spot * 2 + core, head) for spot in spots]
    mine = pl.ds(pl.multiple_of(low * size, size), size)
    given = pl.ds(pl.multiple_of((1 - low) * size, size), size)
    top, bottom = pl.ds(0, tall // 2), pl.ds(tall // 2, tall // 2)
    fresh = pl.ds(2 * size, size)

    def keys_of(at):
        return dkv_ref.at[pl.ds(pl.multiple_of(at * tall, tall), tall)]

    def normed_copy(at, slot):
        cols = pl.ds(pl.multiple_of(at * tile, tile), tile)
        return pltpu.make_async_copy(n1_ref.at[:, cols], n1_s.at[slot], local_sem.at[2 + slot])

    own_rows = pl.ds(pl.multiple_of(place * rows, rows), rows)
    fetches = [
        pltpu.make_async_copy(source.at[own_rows], target, local_sem.at[4 + index])
        for index, (source, target) in enumerate(
            ((mixed_hbm, mixed_ref), (mlp_hbm, mlp_ref), (x_hbm, x_ref))
        )
    ]
    for copy in fetches:
        copy.start()
    for at in range(2):
        normed_copy(at, at).start()
    last_sums = [go(ahead_ref, out_got.at[0], right), go(behind_ref, out_got.at[1], left)]
    swaps = scatter_swap(keys_of, core_got)
    cat_ref[:, pl.ds(0, size)] = dq_ref[...]
    cat_ref[:, pl.ds(size, size)] = dg_ref[...]
    for copy in fetches:
        copy.wait()

    @pl.loop(0, width // tile)
    def _(at):
        cols = pl.ds(pl.multiple_of(at * tile, tile), tile)
        wout_s[:, cols] = rows_inner(mixed_ref[...], low_ref[:, cols]).astype(BF)

    tops, bottoms = [], []
    for copy, hop in zip(swaps, order):
        copy.wait_recv()
        spot = spots[hop]
        add_tiles(core_got.at[spot], core_got.at[spot], keys_of(2 * spot + core))
        bottoms.append(go(core_got.at[spot, bottom, given], y_first.at[spot], mate))
        if hop:
            tops.append(go(core_got.at[spot, top], x_first.at[hop - 1], peers[hop]))
    wouts = scatter_swap(wout_view, wout_twin)
    for copy in last_sums:
        copy.wait_recv()
    out_s[...] = (
        h1_ref[...] + mlp_ref[...].astype(F32) + out_got[0].astype(F32) + out_got[1].astype(F32)
    ).astype(BF)
    keep_out = pltpu.make_async_copy(out_s, out_all.at[place], local_sem.at[0])
    keep_out.start()
    outs = gather(out_s, out_all, 0, None)
    total = core_got[across, top].astype(F32)
    for hop, copy in enumerate(tops):
        copy.wait_recv()
        total = total + x_first[hop].astype(F32)
    held[...] = total.astype(BF)
    last = go(held.at[:, given], y_second, mate)
    ends = []
    for copy, hop in zip(bottoms, order):
        copy.wait_recv()
        spot = spots[hop]
        y_first[spot] = add_low(y_first[spot], core_got[spot, bottom, mine])
        if hop:
            ends.append(go(y_first.at[spot], x_second.at[hop - 1], peers[hop]))
    last.wait_recv()
    cat_ref[top, fresh] = add_low(held[:, mine], y_second[...])
    total = y_first[across].astype(F32)
    for hop, copy in enumerate(ends):
        copy.wait_recv()
        total = total + x_second[hop].astype(F32)
    cat_ref[bottom, fresh] = total.astype(BF)

    compute(place + steps)
    sums = reduce(part_ref, got, 0, None)
    outs = gather(out_s, out_all, 1, outs)

    @pl.loop(1, count)
    def _(hop):
        compute(place + steps + hop)

    @pl.loop(0, width // tile)
    def _(at):
        slot = lax.rem(at, 2)
        normed_copy(at, slot).wait()
        cols = pl.ds(pl.multiple_of(at * tile, tile), tile)
        din_s[cols] = rows_inner(n1_s[slot], cat_ref[...]).astype(BF)

        @pl.when(at + 2 < width // tile)
        def _():
            normed_copy(at + 2, slot).start()

    dins = scatter_swap(din_view, din_got)
    for step in range(1, steps):
        sums = reduce(part_ref, got, step, sums)
        if 2 <= step < steps - 1:
            outs = gather(out_s, out_all, step, outs)
        if step == 1:
            wouts = scatter_cross(wout_view, wout_twin, wout_x, wouts)
            dins = scatter_cross(din_view, din_got, din_x, dins)
    for copy in sums:
        copy.wait_recv()

    def tile_of(at):
        return pl.ds(pl.multiple_of(at * tile, tile), tile)

    def total(cols):
        return (
            part_ref[span(place, rows), cols].astype(F32)
            + got[0, steps - 1, :, cols].astype(F32)
            + got[1, steps - 1, :, cols].astype(F32)
        )

    def collect(at, state):
        squares, mean = state
        cols = tile_of(at)
        x = x_ref[:, cols].astype(F32)
        squares = squares + jnp.sum(x * x, axis=1, keepdims=True)
        return squares, mean + jnp.sum(gain_ref[:, cols] * total(cols) * x, axis=1, keepdims=True)

    zero = jnp.zeros((rows, 1), F32)
    squares, mean = lax.fori_loop(0, width // tile, collect, (zero, zero))
    scale = lax.rsqrt(squares / width + EPSILON)
    pull = scale * scale * scale * (mean / width)

    @pl.loop(0, width // tile)
    def _(at):
        cols = tile_of(at)
        x, dn1 = x_ref[:, cols].astype(F32), total(cols)
        gain_own[pl.ds(0, 1), cols] = jnp.sum(dn1 * x * scale, axis=0, keepdims=True)
        gain_own[pl.ds(1, 1), cols] = second_ref[:, cols]
        tok_ref[:, cols] = (dh1_ref[:, cols] + scale * (gain_ref[:, cols] * dn1) - x * pull).astype(BF)

    keep_tok = pltpu.make_async_copy(tok_ref, tok_all.at[place], local_sem.at[1])
    keep_tok.start()
    toks = gather(tok_ref, tok_all, 0, None)
    outs = gather(out_s, out_all, steps - 1, outs)
    wout_part = wout_twin.at[across]
    scatter_end(wout_twin, wout_x, wouts, wout_part)
    wsums = reduce(wout_part, wout_got, 0, None)
    scatter_end(din_got, din_x, dins, din_ref)
    wide = width // batches

    def slice_of(at):
        return pl.ds(pl.multiple_of(at * wide, wide), wide)

    gains = [
        go(gain_own.at[:, slice_of(other)], gain_got.at[hop], (other, head))
        for hop, other in enumerate(others)
    ]
    toks = gather(tok_ref, tok_all, 1, toks)
    wsums = reduce(wout_part, wout_got, 1, wsums)
    middle = gain_own[:, slice_of(batch)]
    for hop, copy in enumerate(gains):
        copy.wait_recv()
        middle = middle + gain_got[hop]
    gain_mid[...] = middle
    gain_heads[place] = middle
    gains = [go(gain_mid, gain_heads.at[place], member) for member in members]
    for step in range(2, steps):
        toks = gather(tok_ref, tok_all, step, toks)
        wsums = reduce(wout_part, wout_got, step, wsums)
    for copy in gains:
        copy.wait_recv()
    middle = gain_heads[0]
    for at in range(1, count):
        middle = middle + gain_heads[at]
    gains_ref[...] = middle
    for copy in (*wsums, *outs):
        copy.wait_recv()
    wout_own[...] = (
        wout_part[span(place, wout_own.shape[0])].astype(F32)
        + wout_got[0, steps - 1].astype(F32)
        + wout_got[1, steps - 1].astype(F32)
    )
    for copy in toks:
        copy.wait_recv()
    for copy in copies:
        copy.wait_send()
    keep_out.wait()
    keep_tok.wait()


def tail(arrays, collective_id):
    d_queries, tokens, mixed = arrays[0], arrays[-3], arrays[-2]
    count = lax.axis_size("head")
    batches = lax.axis_size("batch")
    steps = count // 2
    rows, width = tokens.shape[0] // count, tokens.shape[1]
    others = batches // 2
    size, wide = mixed.shape[1] // count, width // batches
    tall, head_size = d_queries.shape
    depth = 3 * head_size
    vmem = pl.BlockSpec(memory_space=pltpu.VMEM)
    hbm = pl.BlockSpec(memory_space=pl.ANY)
    whole = (count, rows, width)
    sems = pltpu.SemaphoreType.DMA((6 * count + 6 * batches,))
    gains = (2, width // batches)
    return pl.pallas_call(
        functools.partial(tail_kernel, count, batches),
        out_shape=[
            jax.ShapeDtypeStruct(whole, BF),
            jax.ShapeDtypeStruct(whole, BF),
            jax.ShapeDtypeStruct(gains, F32),
            jax.ShapeDtypeStruct((size, wide), F32),
            jax.ShapeDtypeStruct((wide, depth), F32),
        ],
        in_specs=[vmem] * 11 + [hbm] * 4,
        out_specs=[hbm] * 2 + [vmem] * 3,
        scratch_shapes=[
            pltpu.VMEM((count * rows, width), BF),
            pltpu.VMEM((rows, width), BF),
            pltpu.VMEM((2, steps, rows, width), BF),
            pltpu.VMEM((2, steps, size, wide), BF),
            pltpu.VMEM((2, width), F32),
            pltpu.VMEM((batches - 1, *gains), F32),
            pltpu.VMEM(gains, F32),
            pltpu.VMEM((count, *gains), F32),
            pltpu.VMEM((width, depth), BF),
            pltpu.VMEM((others, wide, depth), BF),
            pltpu.VMEM((others - 1, wide, depth), BF),
            pltpu.VMEM((count * size, width), BF),
            pltpu.VMEM((others, count * size, wide), BF),
            pltpu.VMEM((others - 1, count * size, wide), BF),
            pltpu.VMEM((tall, depth), BF),
            pltpu.VMEM((rows, width), BF),
            pltpu.VMEM((2, rows, width), BF),
            pltpu.VMEM((others, tall, 2 * head_size), BF),
            pltpu.VMEM((others - 1, tall // 2, 2 * head_size), BF),
            pltpu.VMEM((others - 1, tall // 2, head_size), BF),
            pltpu.VMEM((others, tall // 2, head_size), BF),
            pltpu.VMEM((tall // 2, head_size), BF),
            pltpu.VMEM((tall // 2, 2 * head_size), BF),
            pltpu.VMEM((2, tall, 256), BF),
            pltpu.VMEM((rows, width), BF),
            pltpu.VMEM((rows, mixed.shape[1]), BF),
            pltpu.VMEM((rows, width), BF),
            sems,
            sems,
            pltpu.SemaphoreType.DMA((7,)),
        ],
        compiler_params=pltpu.CompilerParams(
            collective_id=collective_id, has_side_effects=True, vmem_limit_bytes=VMEM_LIMIT
        ),
        cost_estimate=pl.CostEstimate(
            flops=4 * count * rows * width * depth, bytes_accessed=400 << 20, transcendentals=0
        ),
        name="tail",
    )(*arrays)


def finish_kernel(out_ref, tok_ref, mgate_ref, mup_ref, down_ref, in_ref, gains_ref, *results):
    for source, target in zip((out_ref, tok_ref, mgate_ref, mup_ref, down_ref), results):
        target[...] = source[...].reshape(target.shape).astype(target.dtype)
    query, gate, key, value, first, second = results[5:]
    size, half = query.shape[1], key.shape[1]
    query[...] = in_ref[:, :size]
    gate[...] = in_ref[:, size : 2 * size]
    key[...] = in_ref[:, 2 * size : 2 * size + half]
    value[...] = in_ref[:, 2 * size + half :]
    first[...] = gains_ref[pl.ds(0, 1)]
    second[...] = gains_ref[pl.ds(1, 1)]


def finish(output, d_tokens, d_mlp, d_down, d_in, gains):
    count, rows, width = output.shape
    tall, hidden = d_mlp.shape[0], d_mlp.shape[1] // 2
    down_rows, wide = d_down.shape
    depth = d_in.shape[1]
    size = depth // 3

    def strip(high, across, at=0):
        return pl.BlockSpec((high // count, across), lambda i: (i, at))

    def held(*shape):
        return pl.BlockSpec(shape, lambda i: (0, 0))

    def shape(*extent, dtype=F32):
        return jax.ShapeDtypeStruct(extent, dtype)

    whole = pl.BlockSpec((1, rows, width), lambda i: (i, 0, 0))
    return pl.pallas_call(
        finish_kernel,
        grid=(count,),
        out_shape=[
            shape(count * rows, width, dtype=BF), shape(count * rows, width, dtype=BF),
            shape(tall, hidden), shape(tall, hidden), shape(down_rows, wide),
            shape(tall, size), shape(tall, size), shape(tall, size // 2), shape(tall, size // 2),
            shape(1, wide), shape(1, wide),
        ],
        in_specs=[
            whole, whole, strip(tall, hidden), strip(tall, hidden, 1), strip(down_rows, wide),
            strip(tall, depth), held(2, wide),
        ],
        out_specs=[
            strip(count * rows, width), strip(count * rows, width),
            strip(tall, hidden), strip(tall, hidden), strip(down_rows, wide),
            strip(tall, size), strip(tall, size), strip(tall, size // 2), strip(tall, size // 2),
            held(1, wide), held(1, wide),
        ],
        compiler_params=pltpu.CompilerParams(vmem_limit_bytes=VMEM_LIMIT),
        name="finish",
    )(output, d_tokens, d_mlp, d_mlp, d_down, d_in, gains)


def local_call(kernel, scalars, arrays, outs, scratch, flops, name):
    vmem = pl.BlockSpec(memory_space=pltpu.VMEM)
    smem = pl.BlockSpec(memory_space=pltpu.SMEM)
    return pl.pallas_call(
        kernel,
        out_shape=outs,
        in_specs=[smem] * len(scalars) + [vmem] * len(arrays),
        out_specs=[vmem] * len(outs),
        scratch_shapes=scratch,
        compiler_params=pltpu.CompilerParams(vmem_limit_bytes=VMEM_LIMIT),
        cost_estimate=pl.CostEstimate(flops=flops, bytes_accessed=8 << 20, transcendentals=0),
        name=name,
    )(*scalars, *arrays)


def ring_routes(count):
    spots = [ring_head(at, count) for at in range(count)]
    right = [(spots[at], spots[(at + 1) % count]) for at in range(count)]
    left = [(spots[at], spots[at - 1]) for at in range(count)]
    return right, left


def add_low(one, other):
    return (one.astype(F32) + other.astype(F32)).astype(BF)


def flow_steps(part, going, coming):
    count = lax.axis_size("head")
    place = ring_place(lax.axis_index("head"), count)
    right, left = ring_routes(count)
    rows = part.shape[0] // count
    steps = count // 2

    def mine(owner):
        return lax.dynamic_slice_in_dim(part, lax.rem(owner + count, count) * rows, rows, 0)

    for step in range(2, steps - 1):
        from_left = lax.ppermute(going, "head", right)
        from_right = lax.ppermute(coming, "head", left)
        going = add_low(from_left, mine(place + steps - 1 - step))
        coming = add_low(from_right, mine(place - steps + 1 + step))
        going, coming = yield going, coming


def matmul(left, right):
    return jnp.dot(left, right, preferred_element_type=F32)


def rows_inner(left, right):
    return lax.dot_general(left, right, (((0,), (0,)), ((), ())), preferred_element_type=F32)


def cols_inner(left, right):
    return lax.dot_general(left, right, (((1,), (1,)), ((), ())), preferred_element_type=F32)


def rms_scale(values):
    return lax.rsqrt(jnp.mean(values * values, axis=1, keepdims=True) + EPSILON)


def per_device(
    tokens,
    segment_ids,
    norm1_gain,
    w_query,
    w_key,
    w_value,
    w_gate,
    w_out,
    norm2_gain,
    w_mlp_gate,
    w_mlp_up,
    w_down,
    out_grad,
):
    heads = lax.axis_size("head")
    batches = lax.axis_size("batch")
    row_count, width = tokens.shape
    head_size = w_query.shape[1]
    half = w_key.shape[1]
    chunk = row_count // heads
    me = ring_place(lax.axis_index("head"), heads)
    scale_factor = 1.0 / math.sqrt(head_size)

    w_shard = jnp.concatenate([w_query, w_gate, w_key, w_value], axis=1)
    gains = jnp.concatenate([norm1_gain, norm2_gain]).reshape(-1, 128).astype(F32)
    normed_one, queries, gate_logit, kv_all, w_in, out_full, gains, seg_all = entry(
        tokens, w_shard, w_out, gains, segment_ids.reshape(-1, 128), 1
    )
    gains, w_mlp_gate = lax.optimization_barrier((gains, w_mlp_gate))
    seg_all = seg_all.reshape(-1)
    gains = gains.reshape(batches, 2, -1).transpose(1, 0, 2).reshape(2, width)
    gain_one, gain_two = gains[0], gains[1]
    mgate_full = lax.all_gather(w_mlp_gate, "batch", axis=0, tiled=True)

    base = lax.axis_index("batch") * row_count
    ids = jnp.arange(DOCUMENTS, dtype=jnp.int32)
    below = jnp.sum((seg_all[None, :] < ids[:, None]).astype(jnp.int32), axis=1)
    starts = jnp.sum(jnp.where(segment_ids[None, :] == ids[:, None], below[:, None], 0), axis=0)
    scalars = (starts, base.reshape(1))
    pair_flops = 4 * row_count * kv_all.shape[0] * head_size
    attended, mixed, lse = local_call(
        functools.partial(attend_kernel, scale_factor),
        scalars,
        (queries, kv_all, starts[None], gate_logit),
        [
            jax.ShapeDtypeStruct((row_count, head_size), F32),
            jax.ShapeDtypeStruct((row_count, head_size), BF),
            jax.ShapeDtypeStruct((1, row_count), F32),
        ],
        [],
        pair_flops,
        "attend",
    )
    mixed_all, down_full, mup_full = spread(
        [mixed, w_down, w_mlp_up], (("head", "cols"), ("batch", "cols"), ("batch", "rows")), 2
    )
    (
        mlp_part, d_mlp, d_down, resid_own, d_resid, d_resid_low, d_gain_two, d_mixed, going, coming,
    ) = mlp_back(
        tokens, mixed_all, out_grad, gain_two[None], out_full, mgate_full, mup_full, down_full, 3
    )
    hold = lax.optimization_barrier
    flow = flow_steps(mlp_part, going, coming)
    state = next(flow)

    d_queries, d_gate_logit, d_kv_all = local_call(
        functools.partial(attend_back_kernel, scale_factor),
        scalars,
        (queries, kv_all, starts[None], gate_logit, attended, d_mixed, lse),
        [
            jax.ShapeDtypeStruct((row_count, head_size), BF),
            jax.ShapeDtypeStruct((row_count, head_size), BF),
            jax.ShapeDtypeStruct(kv_all.shape, BF),
        ],
        [pltpu.VMEM((kv_all.shape[0], head_size), F32)] * 2,
        5 * pair_flops // 2,
        "attend_back",
    )
    for _ in range(3, heads // 2 - 1):
        state = flow.send(state)
    d_down = lax.psum_scatter(d_down, "batch", scatter_dimension=1, tiled=True)
    d_mlp = lax.psum_scatter(d_mlp, "batch", scatter_dimension=0, tiled=True)
    output, d_tokens, d_gains, d_out, d_in = tail(
        (
            d_queries, d_gate_logit, d_kv_all, w_in, gain_one[None], d_resid, d_gain_two,
            d_resid_low, resid_own, *state, normed_one, tokens, mixed_all, mlp_part,
        ),
        5,
    )
    (
        output, d_tokens, d_mgate, d_mup, d_down, d_query, d_gate, d_key, d_value, d_one, d_two,
    ) = finish(output, d_tokens, d_mlp, d_down, d_in, d_gains)
    return (
        output,
        d_tokens,
        d_one.reshape(-1),
        d_query,
        d_key,
        d_value,
        d_gate,
        d_out,
        d_two.reshape(-1),
        d_mgate,
        d_mup,
        d_down,
    )


def solution(mesh):
    return jax.shard_map(
        per_device,
        mesh=mesh,
        in_specs=(
            P("batch", None),
            P("batch"),
            P("batch"),
            P("batch", "head"),
            P("batch", "head"),
            P("batch", "head"),
            P("batch", "head"),
            P("head", "batch"),
            P("batch"),
            P("batch", "head"),
            P("batch", "head"),
            P("head", "batch"),
            P("batch", None),
        ),
        out_specs=(
            P("batch", None),
            P("batch", None),
            P("batch"),
            P("batch", "head"),
            P("batch", "head"),
            P("batch", "head"),
            P("batch", "head"),
            P("head", "batch"),
            P("batch"),
            P("batch", "head"),
            P("batch", "head"),
            P("head", "batch"),
        ),
        check_vma=False,
    )
```

```python
import functools
import math

import jax
import jax.numpy as jnp
from jax import lax
from jax.experimental import pallas as pl
from jax.experimental.pallas import tpu as pltpu
from jax.sharding import PartitionSpec as P

EPSILON = 1e-06
MASKED = -1e30
DOCUMENTS = 7
BF = jnp.bfloat16
F32 = jnp.float32


MESH = pl.DeviceIdType.MESH
VMEM_LIMIT = 60 << 20


def ring_place(head, count):
    high, low = head // 2, head % 2
    return (1 - low) * high + low * (count - 1 - high)


def ring_head(place, count):
    low = place // (count // 2)
    high = (1 - low) * place + low * (count - 1 - place)
    return 2 * high + low


def ring_setup(count):
    batch = lax.axis_index("batch")
    place = ring_place(lax.axis_index("head"), count)
    right = (batch, ring_head(lax.rem(place + 1, count), count))
    left = (batch, ring_head(lax.rem(place + count - 1, count), count))
    return place, right, left


def greet(devices):
    barrier = pltpu.get_barrier_semaphore()
    for device in devices:
        pl.semaphore_signal(barrier, inc=1, device_id=device, device_id_type=MESH)
    pl.semaphore_wait(barrier, len(devices))


def send(source, target, sems, slot, device):
    copy = pltpu.make_async_remote_copy(
        src_ref=source,
        dst_ref=target,
        send_sem=sems[0].at[slot],
        recv_sem=sems[1].at[slot],
        device_id=device,
        device_id_type=MESH,
    )
    copy.start()
    return copy


def half_of(extent, flow):
    if extent[1] % 256:
        return (pl.ds(flow * (extent[0] // 2), extent[0] // 2), slice(None))
    return (slice(None), pl.ds(flow * (extent[1] // 2), extent[1] // 2))


def place_of(whole, own, chunk, form):
    rows, wide = own.shape[-2:]
    if form == "lead":
        return whole.at[chunk]
    if form == "rows":
        return whole.at[pl.ds(pl.multiple_of(chunk * rows, rows), rows)]
    return whole.at[:, pl.ds(pl.multiple_of(chunk * wide, wide), wide)]


def spread_kernel(count, batches, plans, *refs):
    steps = count // 2
    arrays = len(plans)
    own_refs, all_refs = refs[:arrays], refs[arrays : 2 * arrays]
    send_sem, recv_sem, local_sem = refs[2 * arrays :]
    place, right, left = ring_setup(count)
    head = lax.axis_index("head")
    batch = lax.axis_index("batch")
    across, core = batch // 2, lax.rem(batch, 2)
    others = batches // 2
    twin = (across * 2 + 1 - core, head)
    peers = [(lax.rem(across + hop, others) * 2 + core, head) for hop in range(1, others)]
    ring = any(axis == "head" for axis, _ in plans)
    grid = any(axis == "batch" for axis, _ in plans)
    greet((right, left) * ring + (twin, *peers) * grid)
    sems = (send_sem, recv_sem)
    slot = 0
    waiting, arriving, local = [], [], []

    def go(source, target, device):
        nonlocal slot
        copy = send(source, target, sems, slot, device)
        slot += 1
        waiting.append(copy)
        return copy

    stages = []
    for index, (axis, form) in enumerate(plans):
        own, whole = own_refs[index], all_refs[index]
        spot = place if axis == "head" else batch
        copy = pltpu.make_async_copy(own, place_of(whole, own, spot, form), local_sem.at[index])
        copy.start()
        local.append(copy)
        if axis == "batch":
            stages.append(index)
    onward = []

    def stage():
        for copy, block in onward:
            copy.wait_recv()
            arriving.append(go(block, block, twin))
        onward.clear()
        if stages:
            index = stages.pop(0)
            own, whole, form = own_refs[index], all_refs[index], plans[index][1]
            mine = place_of(whole, own, batch, form)
            for hop, peer in enumerate(peers, 1):
                source = lax.rem(across + others - hop, others) * 2 + core
                onward.append((go(own, mine, peer), place_of(whole, own, source, form)))
            arriving.append(go(own, mine, twin))

    stage()
    copies = [None] * (2 * arrays)
    for step in range(steps):
        for index, (axis, form) in enumerate(plans):
            if axis != "head":
                continue
            own = own_refs[index]
            for flow, chunk, device in ((0, place - step, right), (1, place + step, left)):
                at = 2 * index + flow
                if step:
                    copies[at].wait_recv()
                chunk = lax.rem(chunk + count, count)
                target = place_of(all_refs[index], own, chunk, form)
                source = target if step else own
                if step == steps - 1:
                    part = half_of(own.shape, flow)
                    source = source.at[part]
                    target = target.at[part]
                copies[at] = go(source, target, device)
        if step == steps // 2:
            stage()
    while stages or onward:
        stage()
    for copy in copies:
        if copy is not None:
            arriving.append(copy)
    for copy in arriving:
        copy.wait_recv()
    for copy in waiting:
        copy.wait_send()
    for copy in local:
        copy.wait()


def spread(arrays, plans, collective_id):
    count = lax.axis_size("head")
    batches = lax.axis_size("batch")
    shapes = []
    slots = 0
    for array, (axis, form) in zip(arrays, plans):
        many = count if axis == "head" else batches
        slots += count if axis == "head" else batches - 1
        if form == "lead":
            shapes.append((many, *array.shape))
        elif form == "rows":
            shapes.append((many * array.shape[0], array.shape[1]))
        else:
            shapes.append((array.shape[0], many * array.shape[1]))
    hbm = pl.BlockSpec(memory_space=pl.ANY)
    return pl.pallas_call(
        functools.partial(spread_kernel, count, batches, plans),
        out_shape=[jax.ShapeDtypeStruct(shape, a.dtype) for shape, a in zip(shapes, arrays)],
        in_specs=[pl.BlockSpec(memory_space=pltpu.VMEM)] * len(arrays),
        out_specs=[hbm] * len(arrays),
        scratch_shapes=[
            pltpu.SemaphoreType.DMA((slots,)),
            pltpu.SemaphoreType.DMA((slots,)),
            pltpu.SemaphoreType.DMA((len(arrays),)),
        ],
        compiler_params=pltpu.CompilerParams(
            collective_id=collective_id, has_side_effects=True, vmem_limit_bytes=VMEM_LIMIT
        ),
        name=f"spread_{collective_id}",
    )(*arrays)


def mlp_kernel(
    count, x_hbm, a_hbm, dy_hbm, gain_ref, out_hbm, gate_hbm, up_hbm, top_hbm, low_hbm,
    mlp_hbm, dmlp_hbm, ddown_hbm, h1_ref, dh1_ref, low_ref, dgain_ref, da_ref, ahead_ref, behind_ref,
    x_s, a_s, mlp_s, h1_s, dy_all, n2_all, hid_all, grad_all, dmlp_s, ddown_s, da_part,
    mlp_far, mlp_next, mlp_got, right_part, left_part, right_got, left_got,
    out_w, gate_w, up_w, down_w, in_sem, out_sem, grad_sem, weight_sem,
    send_sem, recv_sem, da_send, da_recv, far_send, far_recv,
):
    steps = count // 2
    rows = x_hbm.shape[0] // count
    width = x_hbm.shape[1]
    hidden = gate_w.shape[1]
    middle = hidden // 2
    weights = [
        pltpu.make_async_copy(source, target, weight_sem.at[index])
        for index, (source, target) in enumerate(
            (
                (out_hbm, out_w), (gate_hbm, gate_w), (up_hbm, up_w),
                (top_hbm, down_w.at[pl.ds(0, middle)]), (low_hbm, down_w.at[pl.ds(middle, middle)]),
            )
        )
    ]
    side = width // 2
    tile = 256
    broad = 1024
    inner = 256 if hidden % 256 == 0 else 128
    size = da_ref.shape[1]
    place, right, left = ring_setup(count)

    def member(hop):
        spot = lax.rem(place + hop, count)
        return spot, (lax.axis_index("batch"), ring_head(spot, count))

    def owners(group):
        first = jnp.where(group == 0, 1, 0)
        one = lax.rem(place + steps - group, count)
        two = lax.rem(place - steps + group + first * steps + count, count)
        return one, two

    def span(owner):
        return pl.ds(pl.multiple_of(owner * rows, rows), rows)

    def tile_of(at, extent=tile):
        return pl.ds(pl.multiple_of(at * extent, extent), extent)

    def loads(group, slot):
        return [
            pltpu.make_async_copy(
                source.at[span(owner)],
                target.at[pl.ds(at * rows, rows)],
                in_sem.at[slot, 2 * index + at],
            )
            for index, (source, target) in enumerate(
                ((x_hbm, x_s.at[slot]), (a_hbm, a_s.at[slot]), (dy_hbm, dy_all.at[group]))
            )
            for at, owner in enumerate(owners(group))
        ]

    def stores(group, slot):
        return [
            pltpu.make_async_copy(
                mlp_s.at[slot, pl.ds(at * rows, rows)], mlp_hbm.at[span(owner)], out_sem.at[slot, at]
            )
            for at, owner in enumerate(owners(group))
        ]

    def passing(source, target, sems, slot, device):
        return pltpu.make_async_remote_copy(
            src_ref=source,
            dst_ref=target,
            send_sem=sems[0].at[slot],
            recv_sem=sems[1].at[slot],
            device_id=device,
            device_id_type=MESH,
        )

    ring_sems, far_sems = (send_sem, recv_sem), (far_send, far_recv)
    ahead, behind = pl.ds(0, side), pl.ds(side, side)

    def first_copies():
        return (
            passing(right_part.at[0, :, ahead], right_got.at[0, :, ahead], ring_sems, 0, right),
            passing(right_part.at[0, :, behind], left_got.at[0, :, behind], ring_sems, steps, left),
        )

    def later_copies(step):
        return (
            passing(right_got.at[step - 1], right_got.at[step], ring_sems, step, right),
            passing(left_got.at[step - 1], left_got.at[step], ring_sems, steps + step, left),
        )

    for copy in (*loads(0, 0), *weights):
        copy.start()
    greet([member(hop)[1] for hop in range(1, count)])
    weights[0].wait()

    @pl.loop(0, steps)
    def _(group):
        slot = lax.rem(group, 2)
        for copy in loads(group, slot):
            copy.wait()

        @pl.when(group + 1 < steps)
        def _():
            for copy in loads(group + 1, 1 - slot):
                copy.start()

        @pl.when(group >= 2)
        def _():
            for copy in stores(group - 2, slot):
                copy.wait()

        mixed = a_s[slot]

        def residual(at, total):
            cols = tile_of(at, broad)
            values = x_s[slot, :, cols].astype(F32) + matmul(mixed, out_w[:, cols])
            h1_s[:, cols] = values
            return total + jnp.sum(values * values, axis=1, keepdims=True)

        total = lax.fori_loop(0, width // broad, residual, jnp.zeros((2 * rows, 1), F32))
        scale = lax.rsqrt(total / width + EPSILON)

        @pl.when(group == 0)
        def _():
            h1_ref[...] = h1_s[pl.ds(rows, rows)]
            for copy in weights[1:]:
                copy.wait()

        @pl.loop(0, width // tile)
        def _(at):
            cols = tile_of(at)
            n2_all[group, :, cols] = (h1_s[:, cols] * scale * gain_ref[:, cols]).astype(BF)

        normed = n2_all[group]
        dy = dy_all[group]

        @pl.loop(0, hidden // inner)
        def _(at):
            cols = tile_of(at, inner)
            cols_up = pl.ds(pl.multiple_of(hidden + at * inner, inner), inner)
            gate = matmul(normed, gate_w[:, cols])
            up = matmul(normed, up_w[:, cols])
            d_hidden = cols_inner(dy, down_w[cols])
            sig = jax.nn.sigmoid(gate)
            silu = gate * sig
            hid_all[group, :, cols] = (silu * up).astype(BF)
            grad_all[group, :, cols] = (d_hidden * up * sig * (1.0 + gate * (1.0 - sig))).astype(BF)
            grad_all[group, :, cols_up] = (d_hidden * silu).astype(BF)

        hid = hid_all[group]
        d_gate = grad_all[group, :, :hidden]
        d_up = grad_all[group, :, hidden:]
        half = jnp.minimum(group, 1)

        @pl.loop(0, width // broad)
        def _(at):
            cols = tile_of(at, broad)
            part = (cols_inner(d_gate, gate_w[cols]) + cols_inner(d_up, up_w[cols])).astype(BF)
            right_part[half, :, cols] = part[:rows]
            left_part[half, :, cols] = part[rows:]

        @pl.when(group == 0)
        def _():
            for copy in first_copies():
                copy.start()

        @pl.when(group == 1)
        def _():
            one, two = first_copies()
            one.wait_recv()
            right_got[0, :, ahead] = add_low(right_part[1, :, ahead], right_got[0, :, ahead])
            right_got[0, :, behind] = right_part[1, :, behind]
            two.wait_recv()
            left_got[0, :, behind] = add_low(left_part[1, :, behind], left_got[0, :, behind])
            left_got[0, :, ahead] = left_part[1, :, ahead]

        @pl.when(group >= 2)
        def _():
            one, two = later_copies(group - 1)
            one.wait_recv()
            right_got[group - 1] = add_low(right_part[1], right_got[group - 1])
            two.wait_recv()
            left_got[group - 1] = add_low(left_part[1], left_got[group - 1])

        @pl.when(group >= 1)
        def _():
            for copy in later_copies(group):
                copy.start()

        @pl.loop(0, width // broad)
        def _(at):
            cols = tile_of(at, broad)
            mlp_s[slot, :, cols] = matmul(hid, down_w[:, cols]).astype(BF)

        for copy in stores(group, slot):
            copy.start()

        @pl.when(group == 0)
        def _():
            mlp_far[...] = mlp_s[slot, pl.ds(0, rows)]

        @pl.when(group == 1)
        def _():
            mlp_next[0] = mlp_s[slot, pl.ds(0, rows)]
            mlp_next[1] = mlp_s[slot, pl.ds(rows, rows)]

        @pl.when(group == 2)
        def _():
            ahead_ref[...] = mlp_s[slot, pl.ds(0, rows)]
            behind_ref[...] = mlp_s[slot, pl.ds(rows, rows)]

    far_copies = [
        passing(mlp_far.at[:, ahead], mlp_got.at[0, :, ahead], far_sems, 0, right),
        passing(mlp_far.at[:, behind], mlp_got.at[1, :, behind], far_sems, 1, left),
    ]
    for copy in far_copies:
        copy.start()

    every = steps * 2 * rows

    def dmlp_copy(at, slot):
        return pltpu.make_async_copy(
            dmlp_s.at[slot], dmlp_hbm.at[tile_of(at // 2), tile_of(lax.rem(at, 2), hidden)], grad_sem.at[slot]
        )

    mlp_tiles = 2 * (width // tile)

    @pl.loop(0, mlp_tiles)
    def _(at):
        slot = lax.rem(at, 2)

        @pl.when(at >= 2)
        def _():
            dmlp_copy(at - 2, slot).wait()

        normed = n2_all[:, :, tile_of(at // 2)].reshape(every, tile)
        grads = grad_all[:, :, tile_of(lax.rem(at, 2), hidden)].reshape(every, hidden)
        dmlp_s[slot] = rows_inner(normed, grads).astype(BF)
        dmlp_copy(at, slot).start()

    wide = 512
    across = width // wide

    def ddown_copy(at, slot):
        return pltpu.make_async_copy(
            ddown_s.at[slot],
            ddown_hbm.at[tile_of(at // across, inner), tile_of(lax.rem(at, across), wide)],
            grad_sem.at[2 + slot],
        )

    down_tiles = across * (hidden // inner)

    @pl.loop(0, down_tiles)
    def _(at):
        slot = lax.rem(at, 2)

        @pl.when(at >= 2)
        def _():
            ddown_copy(at - 2, slot).wait()

        hid = hid_all[:, :, tile_of(at // across, inner)].reshape(every, inner)
        dy = dy_all[:, :, tile_of(lax.rem(at, across), wide)].reshape(every, wide)
        ddown_s[slot] = rows_inner(hid, dy).astype(BF)
        ddown_copy(at, slot).start()

    for copy in later_copies(steps - 1):
        copy.wait_recv()
    for flow, have, lack in ((0, ahead, behind), (1, behind, ahead)):
        far_copies[flow].wait_recv()
        mlp_got[flow, :, have] = add_low(mlp_got[flow, :, have], mlp_next[flow, :, have])
        mlp_got[flow, :, lack] = mlp_next[flow, :, lack]
    next_copies = [
        passing(mlp_got.at[0], mlp_got.at[2], far_sems, 2, right),
        passing(mlp_got.at[1], mlp_got.at[3], far_sems, 3, left),
    ]
    for copy in next_copies:
        copy.start()

    def collect(at, state):
        squares, mean = state
        cols = tile_of(at)
        dn2 = (
            left_part[0, :, cols].astype(F32)
            + right_got[steps - 1, :, cols].astype(F32)
            + left_got[steps - 1, :, cols].astype(F32)
        )
        dh1_ref[:, cols] = dn2
        h1 = h1_ref[:, cols]
        squares = squares + jnp.sum(h1 * h1, axis=1, keepdims=True)
        return squares, mean + jnp.sum(gain_ref[:, cols] * dn2 * h1, axis=1, keepdims=True)

    zero = jnp.zeros((rows, 1), F32)
    squares, mean = lax.fori_loop(0, width // tile, collect, (zero, zero))
    scale_own = lax.rsqrt(squares / width + EPSILON)
    pull = scale_own * scale_own * scale_own * (mean / width)

    @pl.loop(0, width // tile)
    def _(at):
        cols = tile_of(at)
        dn2, h1 = dh1_ref[:, cols], h1_ref[:, cols]
        dgain_ref[:, cols] = jnp.sum(dn2 * h1 * scale_own, axis=0, keepdims=True)
        dy = dy_all[0, pl.ds(rows, rows), cols].astype(F32)
        d_resid = dy + scale_own * (gain_ref[:, cols] * dn2) - h1 * pull
        dh1_ref[:, cols] = d_resid
        low_ref[:, cols] = d_resid.astype(BF)

    def da_copy(hop):
        return passing(
            da_part.at[hop], da_ref.at[span(place)], (da_send, da_recv), hop, member(hop)[1]
        )

    low = low_ref[...]

    @pl.loop(1, count)
    def _(hop):
        spot = member(hop)[0]
        da_part[hop] = cols_inner(low, out_w[tile_of(spot, size)]).astype(BF)
        da_copy(hop).start()

    da_ref[span(place)] = cols_inner(low, out_w[tile_of(place, size)]).astype(BF)

    @pl.loop(1, count)
    def _(hop):
        da_copy(hop).wait_recv()
        da_copy(hop).wait_send()

    for flow, held in ((0, ahead_ref), (1, behind_ref)):
        next_copies[flow].wait_recv()
        held[...] = add_low(held[...], mlp_got[2 + flow])
    for copy in (*far_copies, *next_copies, *first_copies()):
        copy.wait_send()
    for step in range(1, steps):
        for copy in later_copies(step):
            copy.wait_send()
    for group in range(steps - 2, steps):
        for copy in stores(group, group % 2):
            copy.wait()
    for at in range(2):
        dmlp_copy(mlp_tiles - 2 + at, (mlp_tiles + at) % 2).wait()
        ddown_copy(down_tiles - 2 + at, (down_tiles + at) % 2).wait()


def mlp_back(tokens, mixed, dy, gain, out_w, gate_w, up_w, down_top, down_low, collective_id):
    count = lax.axis_size("head")
    total, width = tokens.shape
    hidden = gate_w.shape[1]
    rows, steps = total // count, count // 2
    size = mixed.shape[1] // count
    inner = 256 if hidden % 256 == 0 else 128
    vmem = pl.BlockSpec(memory_space=pltpu.VMEM)
    hbm = pl.BlockSpec(memory_space=pl.ANY)

    def slots(many, tall, wide, dtype=BF):
        return pltpu.VMEM((many, tall, wide), dtype)

    def shape(*extent, dtype=BF):
        return jax.ShapeDtypeStruct(extent, dtype)

    dma = pltpu.SemaphoreType.DMA
    flops = 2 * total * width * (mixed.shape[1] + 9 * hidden)
    return pl.pallas_call(
        functools.partial(mlp_kernel, count),
        out_shape=[
            shape(total, width), shape(width, 2 * hidden), shape(hidden, width),
            shape(rows, width, dtype=F32), shape(rows, width, dtype=F32), shape(rows, width),
            shape(1, width, dtype=F32), shape(total, size), shape(rows, width), shape(rows, width),
        ],
        in_specs=[hbm] * 3 + [vmem] + [hbm] * 5,
        out_specs=[hbm] * 3 + [vmem] * 7,
        scratch_shapes=[
            slots(2, 2 * rows, width), slots(2, 2 * rows, mixed.shape[1]), slots(2, 2 * rows, width),
            pltpu.VMEM((2 * rows, width), F32),
            slots(steps, 2 * rows, width), slots(steps, 2 * rows, width),
            slots(steps, 2 * rows, hidden), slots(steps, 2 * rows, 2 * hidden),
            slots(2, 256, hidden), slots(2, inner, 512), slots(count, rows, size),
            pltpu.VMEM((rows, width), BF), slots(2, rows, width), slots(4, rows, width),
            slots(2, rows, width), slots(2, rows, width),
            slots(steps, rows, width), slots(steps, rows, width),
            *[pltpu.VMEM(weight.shape, BF) for weight in (out_w, gate_w, up_w)],
            pltpu.VMEM((hidden, width), BF),
            dma((2, 6)), dma((2, 2)), dma((4,)), dma((5,)), dma((count,)), dma((count,)),
            dma((count,)), dma((count,)), dma((4,)), dma((4,)),
        ],
        compiler_params=pltpu.CompilerParams(
            collective_id=collective_id, has_side_effects=True, vmem_limit_bytes=VMEM_LIMIT
        ),
        cost_estimate=pl.CostEstimate(flops=flops, bytes_accessed=40 << 20, transcendentals=0),
        name="mlp_back",
    )(tokens, mixed, dy, gain, out_w, gate_w, up_w, down_top, down_low)


def entry_kernel(
    count, batches, x_ref, w_ref, out_ref, gain_ref, seg_ref, down_ref,
    n1_hbm, q_ref, logit_ref, kv_ref, w_all, out_all, gain_all, seg_all, down_all,
    x_s, n1_ref, send_sem, recv_sem, local_sem, x_sem, n1_sem,
):
    steps = count // 2
    others = batches // 2
    rows, width = x_ref.shape
    depth = w_ref.shape[0]
    size, wide = out_ref.shape
    block = 256
    blocks = rows // block

    def x_copy(at):
        here = pl.ds(pl.multiple_of(at * block, block), block)
        return pltpu.make_async_copy(x_ref.at[here], x_s.at[here], x_sem.at[at])

    def n1_copy(at):
        here = pl.ds(pl.multiple_of(at * block, block), block)
        return pltpu.make_async_copy(n1_ref.at[here], n1_hbm.at[here], n1_sem.at[at])

    for at in range(blocks):
        x_copy(at).start()
    place, right, left = ring_setup(count)
    head = lax.axis_index("head")
    batch = lax.axis_index("batch")
    across, core, low = batch // 2, lax.rem(batch, 2), lax.rem(head, 2)
    twin = (across * 2 + 1 - core, head)
    mate = (batch, head + 1 - 2 * low)
    spots = [lax.rem(across + hop, others) for hop in range(others)]
    backs = [lax.rem(across + others - hop, others) for hop in range(others)]
    peers = [(spot * 2 + core, head) for spot in spots]
    far_peers = [(spot * 2 + 1 - core, head) for spot in spots]
    greet((twin, mate, right, left, *peers[1:], *far_peers[1:]))
    sems = (send_sem, recv_sem)
    slot = 0
    copies = []

    def go(source, target, device):
        nonlocal slot
        copy = send(source, target, sems, slot, device)
        slot += 1
        copies.append(copy)
        return copy

    def part(at, extent):
        return pl.ds(pl.multiple_of(at * extent, extent), extent)

    def both(view, own):
        out = [go(own, view(batch), peers[hop]) for hop in range(1, others)]
        return out, [go(own, view(batch), twin)]

    def pass_on(view, arrived):
        out = []
        for hop in range(1, others):
            arrived[hop - 1].wait_recv()
            there = view(backs[hop] * 2 + core)
            out.append(go(there, there, twin))
        return out

    local = []

    def stay(source, target):
        copy = pltpu.make_async_copy(source, target, local_sem.at[len(local)])
        copy.start()
        local.append(copy)

    def main_view(at):
        return w_all.at[part(at, depth), pl.ds(0, 3 * size)]

    def mate_view(at):
        return w_all.at[part(at, depth), pl.ds(3 * size, size)]

    def out_view(chunk, at):
        return out_all.at[part(chunk, size), part(at, wide)]

    small = []
    for own, whole in ((gain_ref, gain_all), (seg_ref, seg_all)):
        for device in (twin, *peers[1:], *far_peers[1:]):
            small.append(go(own, whole.at[batch], device))
        stay(own, whole.at[batch])
    from_mate = go(w_ref.at[:, pl.ds(2 * size, size)], mate_view(batch), mate)
    main_out, main_twin = both(main_view, w_ref)
    stay(w_ref, main_view(batch))
    out_peers = [go(out_ref, out_view(place, batch), peers[hop]) for hop in range(1, others)]
    stay(out_ref, out_view(place, batch))
    flows = [[None, None] for _ in range(others)]

    def ring(step):
        for hop in range(others):
            lane = spots[0] if hop == 0 else backs[hop]
            at = lane * 2 + core
            if step == 0 and hop:
                out_peers[hop - 1].wait_recv()
            for flow, chunk, device in ((0, place - step, right), (1, place + step, left)):
                if step:
                    flows[hop][flow].wait_recv()
                target = out_view(lax.rem(chunk + count, count), at)
                source = out_ref if step == 0 and hop == 0 else target
                if step == steps - 1:
                    cut = (pl.ds(flow * (size // 2), size // 2), slice(None))
                    source, target = source.at[cut], target.at[cut]
                flows[hop][flow] = go(source, target, device)

    for copy in small:
        copy.wait_recv()
    for copy in local[:2]:
        copy.wait()

    def normalize(at):
        here = part(at, block)
        x_copy(at).wait()

        def squares(tile, total):
            values = x_s[here, part(tile, 256)].astype(F32)
            return total + jnp.sum(values * values, axis=1, keepdims=True)

        total = lax.fori_loop(0, width // 256, squares, jnp.zeros((block, 1), F32))
        scale = lax.rsqrt(total / width + EPSILON)

        @pl.loop(0, batches)
        def _(owner):
            for tile in range(depth // 128):
                cols = pl.ds(pl.multiple_of(owner * depth + tile * 128, 128), 128)
                values = x_s[here, cols].astype(F32) * scale
                n1_ref[here, cols] = (values * gain_all[owner, pl.ds(tile, 1)]).astype(BF)

        n1_copy(at).start()

    middle = blocks // 2

    @pl.loop(0, middle)
    def _(at):
        normalize(at)

    from_mate.wait_recv()
    mate_out, mate_twin = both(mate_view, mate_view(batch))
    ring(0)

    def down_view(at):
        return down_all.at[:, part(at, down_ref.shape[1])]

    down_out, down_twin = both(down_view, down_ref)
    stay(down_ref, down_view(batch))

    @pl.loop(middle, blocks)
    def _(at):
        normalize(at)

    main_passed = pass_on(main_view, main_out)
    mate_passed = pass_on(mate_view, mate_out)
    for copy in (*main_twin, *mate_twin, *main_passed, *mate_passed):
        copy.wait_recv()
    for copy in local[2:]:
        copy.wait()

    def kv_view(at):
        return kv_ref.at[part(at, rows)]

    @pl.loop(0, blocks)
    def _(at):
        here = part(at, block)
        values = matmul(n1_ref[here], w_all[:, pl.ds(2 * size, 2 * size)])
        one, two = values[:, :size], values[:, size:]
        first = jnp.where(low == 0, one, two).astype(BF)
        second = jnp.where(low == 0, two, one).astype(BF)
        half = size // 2
        there = pl.ds(pl.multiple_of(batch * rows + at * block, block), block)
        kv_ref[there, pl.ds(0, size)] = jnp.concatenate([first[:, :half], second[:, :half]], 1)
        kv_ref[there, pl.ds(size, size)] = jnp.concatenate([first[:, half:], second[:, half:]], 1)

    kv_out, kv_twin = both(kv_view, kv_view(batch))
    ring(1)

    @pl.loop(0, blocks)
    def _(at):
        here = part(at, block)
        values = matmul(n1_ref[here], w_all[:, pl.ds(0, 2 * size)])
        q_ref[here] = values[:, :size].astype(BF)
        logit_ref[here] = values[:, size:]

    for step in range(2, steps):
        ring(step)
    down_passed = pass_on(down_view, down_out)
    kv_passed = pass_on(kv_view, kv_out)
    for pair in flows:
        for copy in pair:
            copy.wait_recv()
    swaps = []
    for hop in range(others):
        there = out_all.at[:, part(spots[hop] * 2 + core, wide)]
        swaps.append(go(there, there, twin))
    for copy in (*kv_twin, *kv_passed, *swaps, *down_twin, *down_passed):
        copy.wait_recv()
    for copy in copies:
        copy.wait_send()
    for at in range(blocks):
        n1_copy(at).wait()


def entry(tokens, w_shard, w_out, gains, segments, w_down, collective_id):
    count = lax.axis_size("head")
    batches = lax.axis_size("batch")
    others = batches // 2
    rows, width = tokens.shape
    size, wide = w_out.shape
    vmem = pl.BlockSpec(memory_space=pltpu.VMEM)
    hbm = pl.BlockSpec(memory_space=pl.ANY)
    slots = 6 * batches + others * (count + 3)
    sems = pltpu.SemaphoreType.DMA((slots,))
    return pl.pallas_call(
        functools.partial(entry_kernel, count, batches),
        out_shape=[
            jax.ShapeDtypeStruct((rows, width), BF),
            jax.ShapeDtypeStruct((rows, size), BF),
            jax.ShapeDtypeStruct((rows, size), F32),
            jax.ShapeDtypeStruct((batches * rows, 2 * size), BF),
            jax.ShapeDtypeStruct((width, 4 * size), BF),
            jax.ShapeDtypeStruct((count * size, batches * wide), BF),
            jax.ShapeDtypeStruct((batches, *gains.shape), F32),
            jax.ShapeDtypeStruct((batches, *segments.shape), jnp.int32),
            jax.ShapeDtypeStruct((w_down.shape[0], batches * w_down.shape[1]), BF),
        ],
        in_specs=[hbm] + [vmem] * 5,
        out_specs=[hbm] + [vmem] * 4 + [hbm] + [vmem] * 2 + [hbm],
        scratch_shapes=[
            pltpu.VMEM((rows, width), BF), pltpu.VMEM((rows, width), BF),
            sems, sems, pltpu.SemaphoreType.DMA((5,)),
            pltpu.SemaphoreType.DMA((rows // 256,)), pltpu.SemaphoreType.DMA((rows // 256,)),
        ],
        compiler_params=pltpu.CompilerParams(
            collective_id=collective_id, has_side_effects=True, vmem_limit_bytes=VMEM_LIMIT
        ),
        name="entry",
    )(tokens, w_shard, w_out, gains, segments, w_down)


KEY_BLOCK = 512
QUERY_BLOCK = 640


def key_range(start_ref, base, query_block):
    first = query_block * QUERY_BLOCK
    lowest = start_ref[first]
    highest = start_ref[first + QUERY_BLOCK - 1]
    begin = lowest // KEY_BLOCK
    end = (base + first + QUERY_BLOCK - 1) // KEY_BLOCK + 1
    full_begin = jnp.minimum((highest + KEY_BLOCK - 1) // KEY_BLOCK, end)
    full_end = jnp.maximum((base + first + 1) // KEY_BLOCK, full_begin)
    return begin, full_begin, full_end, end


def allowed_pairs(key_block, start_row, base_row):
    shape = (KEY_BLOCK, QUERY_BLOCK)
    key_pos = key_block * KEY_BLOCK + lax.broadcasted_iota(jnp.int32, shape, 0)
    query_pos = base_row + lax.broadcasted_iota(jnp.int32, shape, 1)
    return (key_pos >= start_row) & (key_pos <= query_pos)


def attend_kernel(
    scale, start_sm, base_sm, q_ref, kv_ref, start_ref, logit_ref, o_ref, a_ref, lse_ref
):
    base = base_sm[0]
    size = q_ref.shape[1]
    factor = scale * math.log2(math.e)

    @pl.loop(0, q_ref.shape[0] // QUERY_BLOCK)
    def _(block):
        rows = pl.ds(pl.multiple_of(block * QUERY_BLOCK, QUERY_BLOCK), QUERY_BLOCK)
        queries = q_ref[rows]
        start_row = start_ref[:, rows]
        begin, full_begin, full_end, end = key_range(start_sm, base, block)

        def step(masked, at, state):
            old_max, old_sum, total = state
            keys = pl.ds(pl.multiple_of(at * KEY_BLOCK, KEY_BLOCK), KEY_BLOCK)
            scores = cols_inner(kv_ref[keys, :size], queries)
            if masked:
                allowed = allowed_pairs(at, start_row, base + block * QUERY_BLOCK)
                scores = jnp.where(allowed, scores, MASKED)
            new_max = jnp.maximum(old_max, jnp.max(scores, axis=0, keepdims=True))
            keep = jnp.exp2((old_max - new_max) * factor)
            weights = jnp.exp2(scores * factor - new_max * factor)
            new_sum = old_sum * keep + jnp.sum(weights, axis=0, keepdims=True)
            total = total * keep + rows_inner(kv_ref[keys, size:], weights.astype(BF))
            return new_max, new_sum, total

        state = (
            jnp.full((1, QUERY_BLOCK), MASKED, F32),
            jnp.zeros((1, QUERY_BLOCK), F32),
            jnp.zeros((size, QUERY_BLOCK), F32),
        )
        state = lax.fori_loop(begin, full_begin, functools.partial(step, True), state)
        state = lax.fori_loop(full_begin, full_end, functools.partial(step, False), state)
        state = lax.fori_loop(full_end, end, functools.partial(step, True), state)
        run_max, run_sum, total = state
        lse_ref[:, rows] = run_max * factor + jnp.log2(run_sum)
        attended = (total / run_sum).T
        o_ref[rows] = attended
        a_ref[rows] = (attended * jax.nn.sigmoid(logit_ref[rows])).astype(BF)


def attend_back_kernel(
    scale, start_sm, base_sm, q_ref, kv_ref, start_ref, logit_ref, o_ref, da_ref, lse_ref,
    dq_ref, dg_ref, dkv_ref, dk_acc, dv_acc,
):
    base = base_sm[0]
    size = q_ref.shape[1]
    factor = scale * math.log2(math.e)
    dk_acc[...] = jnp.zeros_like(dk_acc)
    dv_acc[...] = jnp.zeros_like(dv_acc)

    @pl.loop(0, q_ref.shape[0] // QUERY_BLOCK)
    def _(block):
        rows = pl.ds(pl.multiple_of(block * QUERY_BLOCK, QUERY_BLOCK), QUERY_BLOCK)
        queries = q_ref[rows]
        start_row = start_ref[:, rows]
        lse = lse_ref[:, rows]
        gate = jax.nn.sigmoid(logit_ref[rows])
        attended = o_ref[rows]
        d_mixed = da_ref[rows].astype(F32)
        d_attended = (d_mixed * gate).astype(BF)
        dg_ref[rows] = (d_mixed * attended * gate * (1.0 - gate)).astype(BF)
        delta = jnp.sum((d_attended.astype(F32) * attended).T, axis=0, keepdims=True)
        begin, full_begin, full_end, end = key_range(start_sm, base, block)

        def step(masked, at, d_queries):
            keys = pl.ds(pl.multiple_of(at * KEY_BLOCK, KEY_BLOCK), KEY_BLOCK)
            key_block = kv_ref[keys, :size]
            probs = jnp.exp2(cols_inner(key_block, queries) * factor - lse)
            if masked:
                allowed = allowed_pairs(at, start_row, base + block * QUERY_BLOCK)
                probs = jnp.where(allowed, probs, 0.0)
            d_probs = cols_inner(kv_ref[keys, size:], d_attended)
            d_scores = (probs * (d_probs - delta) * scale).astype(BF)
            dv_acc[keys] += matmul(probs.astype(BF), d_attended)
            dk_acc[keys] += matmul(d_scores, queries)
            return d_queries + rows_inner(key_block, d_scores)

        d_queries = jnp.zeros((size, QUERY_BLOCK), F32)
        d_queries = lax.fori_loop(begin, full_begin, functools.partial(step, True), d_queries)
        d_queries = lax.fori_loop(full_begin, full_end, functools.partial(step, False), d_queries)
        d_queries = lax.fori_loop(full_end, end, functools.partial(step, True), d_queries)
        dq_ref[rows] = d_queries.T.astype(BF)

    @pl.loop(0, kv_ref.shape[0] // KEY_BLOCK)
    def _(at):
        keys = pl.ds(pl.multiple_of(at * KEY_BLOCK, KEY_BLOCK), KEY_BLOCK)
        dk, dv = dk_acc[keys].astype(BF), dv_acc[keys].astype(BF)
        half = size // 2
        dkv_ref[keys, :size] = jnp.concatenate([dk[:, :half], dv[:, :half]], axis=1)
        dkv_ref[keys, size:] = jnp.concatenate([dk[:, half:], dv[:, half:]], axis=1)


def tail_kernel(
    count, batches, dq_ref, dg_ref, dkv_ref, w_ref, gain_ref, dh1_ref, second_ref,
    low_ref, h1_ref, ahead_ref, behind_ref, n1_ref, x_hbm, mixed_hbm, mlp_hbm,
    out_all, tok_all, gains_ref, wout_own, din_ref, key_ref, value_ref,
    part_ref, tok_ref, got, wout_got, gain_own, gain_got, gain_mid, gain_heads,
    din_s, din_got, din_x, wout_s, wout_twin, wout_x,
    cat_ref, out_s, out_got, core_got, x_first, x_second, y_first, y_second, held, n1_s,
    x_ref, mixed_ref, mlp_ref, send_sem, recv_sem, local_sem,
):
    steps = count // 2
    rows, width = x_ref.shape
    depth = cat_ref.shape[1]
    tall, size = dq_ref.shape
    tile = 256
    place, right, left = ring_setup(count)
    batch, head = lax.axis_index("batch"), lax.axis_index("head")
    others = [lax.rem(batch + hop, batches) for hop in range(1, batches)]
    members = [(batch, ring_head(lax.rem(place + hop, count), count)) for hop in range(1, count)]
    greet((*members, *[(other, head) for other in others]))
    sems = (send_sem, recv_sem)
    slot = 0
    copies = []

    def go(source, target, device):
        nonlocal slot
        copy = send(source, target, sems, slot, device)
        slot += 1
        copies.append(copy)
        return copy

    across, core = batch // 2, lax.rem(batch, 2)
    spots = [lax.rem(across + hop, batches // 2) for hop in range(batches // 2)]
    order = list(range(1, batches // 2)) + [0]
    twin = (across * 2 + 1 - core, head)

    def scatter_swap(view, held):
        return [go(view(2 * spots[hop] + 1 - core), held.at[spots[hop]], twin) for hop in order]

    def add_tiles(target, one, other):
        @pl.loop(0, target.shape[0] // 128)
        def _(at):
            lines = pl.ds(pl.multiple_of(at * 128, 128), 128)
            total = one[lines].astype(F32) + other[lines].astype(F32)
            target[lines] = total.astype(target.dtype)

    def scatter_cross(view, held, crossed, arriving):
        out = []
        for copy, hop in zip(arriving, order):
            copy.wait_recv()
            spot = spots[hop]
            add_tiles(held.at[spot], held.at[spot], view(2 * spot + core))
            if hop:
                out.append(go(held.at[spot], crossed.at[hop - 1], (spot * 2 + core, head)))
        return out

    def scatter_end(held, crossed, arriving, target):
        for hop, copy in enumerate(arriving):
            copy.wait_recv()
            last = hop == len(arriving) - 1
            add_tiles(target if last else held.at[across], held.at[across], crossed.at[hop])

    def wout_view(at):
        wide = width // batches
        return wout_s.at[:, pl.ds(pl.multiple_of(at * wide, wide), wide)]

    def din_view(at):
        tall = din_ref.shape[0]
        return din_s.at[pl.ds(pl.multiple_of(at * tall, tall), tall)]

    def span(owner, extent):
        return pl.ds(pl.multiple_of(lax.rem(owner + count, count) * extent, extent), extent)

    def compute(owner):
        here = span(owner, rows)
        values = cat_ref[here]

        @pl.loop(0, width // tile)
        def _(at):
            cols = pl.ds(pl.multiple_of(at * tile, tile), tile)
            part_ref[here, cols] = cols_inner(values, w_ref[cols, pl.ds(0, depth)]).astype(BF)

    def gather(own, whole, step, last):
        out = []
        for flow, chunk, device in ((0, place - step, right), (1, place + step, left)):
            if last:
                last[flow].wait_recv()
            target = whole.at[lax.rem(chunk + count, count)]
            source = target if step else own
            if step == steps - 1:
                cut = (slice(None), pl.ds(flow * (width // 2), width // 2))
                source, target = source.at[cut], target.at[cut]
            out.append(go(source, target, device))
        return out

    def reduce(parts, held, step, last):
        extent, side = held.shape[2], held.shape[3] // 2
        out = []
        for flow, owner, device in (
            (0, place + steps - step, right),
            (1, place - steps + step, left),
        ):
            have = pl.ds(flow * side, side)
            lack = pl.ds((1 - flow) * side, side)
            mine = parts.at[span(owner, extent)]
            if step == 0:
                out.append(go(mine.at[:, have], held.at[flow, 0, :, have], device))
                continue
            last[flow].wait_recv()
            if step == 1:
                held[flow, 0, :, have] = add_low(held[flow, 0, :, have], mine[:, have])
                held[flow, 0, :, lack] = mine[:, lack]
            else:
                held[flow, step - 1] = add_low(held[flow, step - 1], mine[...])
            out.append(go(held.at[flow, step - 1], held.at[flow, step], device))
        return out

    low = lax.rem(head, 2)
    mate = (batch, head + 1 - 2 * low)
    peers = [(spot * 2 + core, head) for spot in spots]
    mine = pl.ds(pl.multiple_of(low * size, size), size)
    given = pl.ds(pl.multiple_of((1 - low) * size, size), size)
    top, bottom = pl.ds(0, tall // 2), pl.ds(tall // 2, tall // 2)
    fresh = pl.ds(2 * size, size)

    def keys_of(at):
        return dkv_ref.at[pl.ds(pl.multiple_of(at * tall, tall), tall)]

    def normed_copy(at, slot):
        cols = pl.ds(pl.multiple_of(at * tile, tile), tile)
        return pltpu.make_async_copy(n1_ref.at[:, cols], n1_s.at[slot], local_sem.at[2 + slot])

    own_rows = pl.ds(pl.multiple_of(place * rows, rows), rows)
    fetches = [
        pltpu.make_async_copy(source.at[own_rows], target, local_sem.at[4 + index])
        for index, (source, target) in enumerate(
            ((mixed_hbm, mixed_ref), (mlp_hbm, mlp_ref), (x_hbm, x_ref))
        )
    ]
    for copy in fetches:
        copy.start()
    for at in range(2):
        normed_copy(at, at).start()
    last_sums = [go(ahead_ref, out_got.at[0], right), go(behind_ref, out_got.at[1], left)]
    swaps = scatter_swap(keys_of, core_got)
    cat_ref[:, pl.ds(0, size)] = dq_ref[...]
    cat_ref[:, pl.ds(size, size)] = dg_ref[...]
    for copy in fetches:
        copy.wait()

    @pl.loop(0, width // tile)
    def _(at):
        cols = pl.ds(pl.multiple_of(at * tile, tile), tile)
        wout_s[:, cols] = rows_inner(mixed_ref[...], low_ref[:, cols]).astype(BF)

    tops, bottoms = [], []
    for copy, hop in zip(swaps, order):
        copy.wait_recv()
        spot = spots[hop]
        add_tiles(core_got.at[spot], core_got.at[spot], keys_of(2 * spot + core))
        bottoms.append(go(core_got.at[spot, bottom, given], y_first.at[spot], mate))
        if hop:
            tops.append(go(core_got.at[spot, top], x_first.at[hop - 1], peers[hop]))
    wouts = scatter_swap(wout_view, wout_twin)
    for copy in last_sums:
        copy.wait_recv()
    out_s[...] = (
        h1_ref[...] + mlp_ref[...].astype(F32) + out_got[0].astype(F32) + out_got[1].astype(F32)
    ).astype(BF)
    keep_out = pltpu.make_async_copy(out_s, out_all.at[place], local_sem.at[0])
    keep_out.start()
    outs = gather(out_s, out_all, 0, None)
    total = core_got[across, top].astype(F32)
    for hop, copy in enumerate(tops):
        copy.wait_recv()
        total = total + x_first[hop].astype(F32)
    held[...] = total.astype(BF)
    last = go(held.at[:, given], y_second, mate)
    ends = []
    for copy, hop in zip(bottoms, order):
        copy.wait_recv()
        spot = spots[hop]
        y_first[spot] = add_low(y_first[spot], core_got[spot, bottom, mine])
        if hop:
            ends.append(go(y_first.at[spot], x_second.at[hop - 1], peers[hop]))
    last.wait_recv()
    cat_ref[top, fresh] = add_low(held[:, mine], y_second[...])
    total = y_first[across].astype(F32)
    for hop, copy in enumerate(ends):
        copy.wait_recv()
        total = total + x_second[hop].astype(F32)
    cat_ref[bottom, fresh] = total.astype(BF)

    compute(place + steps)
    sums = reduce(part_ref, got, 0, None)
    outs = gather(out_s, out_all, 1, outs)

    @pl.loop(1, count)
    def _(hop):
        compute(place + steps + hop)

    @pl.loop(0, width // tile)
    def _(at):
        slot = lax.rem(at, 2)
        normed_copy(at, slot).wait()
        cols = pl.ds(pl.multiple_of(at * tile, tile), tile)
        din_s[cols] = rows_inner(n1_s[slot], cat_ref[...]).astype(BF)

        @pl.when(at + 2 < width // tile)
        def _():
            normed_copy(at + 2, slot).start()

    dins = scatter_swap(din_view, din_got)
    for step in range(1, steps):
        sums = reduce(part_ref, got, step, sums)
        if 2 <= step < steps - 1:
            outs = gather(out_s, out_all, step, outs)
        if step == 1:
            wouts = scatter_cross(wout_view, wout_twin, wout_x, wouts)
            dins = scatter_cross(din_view, din_got, din_x, dins)
    for copy in sums:
        copy.wait_recv()

    def tile_of(at):
        return pl.ds(pl.multiple_of(at * tile, tile), tile)

    def total(cols):
        return (
            part_ref[span(place, rows), cols].astype(F32)
            + got[0, steps - 1, :, cols].astype(F32)
            + got[1, steps - 1, :, cols].astype(F32)
        )

    def collect(at, state):
        squares, mean = state
        cols = tile_of(at)
        x = x_ref[:, cols].astype(F32)
        squares = squares + jnp.sum(x * x, axis=1, keepdims=True)
        return squares, mean + jnp.sum(gain_ref[:, cols] * total(cols) * x, axis=1, keepdims=True)

    zero = jnp.zeros((rows, 1), F32)
    squares, mean = lax.fori_loop(0, width // tile, collect, (zero, zero))
    scale = lax.rsqrt(squares / width + EPSILON)
    pull = scale * scale * scale * (mean / width)

    @pl.loop(0, width // tile)
    def _(at):
        cols = tile_of(at)
        x, dn1 = x_ref[:, cols].astype(F32), total(cols)
        gain_own[pl.ds(0, 1), cols] = jnp.sum(dn1 * x * scale, axis=0, keepdims=True)
        gain_own[pl.ds(1, 1), cols] = second_ref[:, cols]
        tok_ref[:, cols] = (dh1_ref[:, cols] + scale * (gain_ref[:, cols] * dn1) - x * pull).astype(BF)

    keep_tok = pltpu.make_async_copy(tok_ref, tok_all.at[place], local_sem.at[1])
    keep_tok.start()
    toks = gather(tok_ref, tok_all, 0, None)
    outs = gather(out_s, out_all, steps - 1, outs)
    wout_part = wout_twin.at[across]
    scatter_end(wout_twin, wout_x, wouts, wout_part)
    wsums = reduce(wout_part, wout_got, 0, None)
    scatter_end(din_got, din_x, dins, din_ref)
    narrow = din_ref[:, pl.ds(2 * size, size)].T
    key_ref[...] = narrow[: size // 2]
    value_ref[...] = narrow[size // 2 :]
    wide = width // batches

    def slice_of(at):
        return pl.ds(pl.multiple_of(at * wide, wide), wide)

    gains = [
        go(gain_own.at[:, slice_of(other)], gain_got.at[hop], (other, head))
        for hop, other in enumerate(others)
    ]
    toks = gather(tok_ref, tok_all, 1, toks)
    wsums = reduce(wout_part, wout_got, 1, wsums)
    middle = gain_own[:, slice_of(batch)]
    for hop, copy in enumerate(gains):
        copy.wait_recv()
        middle = middle + gain_got[hop]
    gain_mid[...] = middle
    gain_heads[place] = middle
    gains = [go(gain_mid, gain_heads.at[place], member) for member in members]
    for step in range(2, steps):
        toks = gather(tok_ref, tok_all, step, toks)
        wsums = reduce(wout_part, wout_got, step, wsums)
    for copy in gains:
        copy.wait_recv()
    middle = gain_heads[0]
    for at in range(1, count):
        middle = middle + gain_heads[at]
    gains_ref[...] = middle
    for copy in (*wsums, *outs):
        copy.wait_recv()
    wout_own[...] = (
        wout_part[span(place, wout_own.shape[0])].astype(F32)
        + wout_got[0, steps - 1].astype(F32)
        + wout_got[1, steps - 1].astype(F32)
    )
    for copy in toks:
        copy.wait_recv()
    for copy in copies:
        copy.wait_send()
    keep_out.wait()
    keep_tok.wait()


def tail(arrays, collective_id):
    d_queries, tokens, mixed = arrays[0], arrays[-3], arrays[-2]
    count = lax.axis_size("head")
    batches = lax.axis_size("batch")
    steps = count // 2
    rows, width = tokens.shape[0] // count, tokens.shape[1]
    others = batches // 2
    size, wide = mixed.shape[1] // count, width // batches
    tall, head_size = d_queries.shape
    depth = 3 * head_size
    vmem = pl.BlockSpec(memory_space=pltpu.VMEM)
    hbm = pl.BlockSpec(memory_space=pl.ANY)
    whole = (count, rows, width)
    sems = pltpu.SemaphoreType.DMA((6 * count + 6 * batches,))
    gains = (2, width // batches)
    return pl.pallas_call(
        functools.partial(tail_kernel, count, batches),
        out_shape=[
            jax.ShapeDtypeStruct(whole, BF),
            jax.ShapeDtypeStruct(whole, BF),
            jax.ShapeDtypeStruct(gains, F32),
            jax.ShapeDtypeStruct((size, wide), F32),
            jax.ShapeDtypeStruct((wide, depth), F32),
            jax.ShapeDtypeStruct((size // 2, wide), F32),
            jax.ShapeDtypeStruct((size // 2, wide), F32),
        ],
        in_specs=[vmem] * 11 + [hbm] * 4,
        out_specs=[hbm] * 2 + [vmem] * 5,
        scratch_shapes=[
            pltpu.VMEM((count * rows, width), BF),
            pltpu.VMEM((rows, width), BF),
            pltpu.VMEM((2, steps, rows, width), BF),
            pltpu.VMEM((2, steps, size, wide), BF),
            pltpu.VMEM((2, width), F32),
            pltpu.VMEM((batches - 1, *gains), F32),
            pltpu.VMEM(gains, F32),
            pltpu.VMEM((count, *gains), F32),
            pltpu.VMEM((width, depth), BF),
            pltpu.VMEM((others, wide, depth), BF),
            pltpu.VMEM((others - 1, wide, depth), BF),
            pltpu.VMEM((count * size, width), BF),
            pltpu.VMEM((others, count * size, wide), BF),
            pltpu.VMEM((others - 1, count * size, wide), BF),
            pltpu.VMEM((tall, depth), BF),
            pltpu.VMEM((rows, width), BF),
            pltpu.VMEM((2, rows, width), BF),
            pltpu.VMEM((others, tall, 2 * head_size), BF),
            pltpu.VMEM((others - 1, tall // 2, 2 * head_size), BF),
            pltpu.VMEM((others - 1, tall // 2, head_size), BF),
            pltpu.VMEM((others, tall // 2, head_size), BF),
            pltpu.VMEM((tall // 2, head_size), BF),
            pltpu.VMEM((tall // 2, 2 * head_size), BF),
            pltpu.VMEM((2, tall, 256), BF),
            pltpu.VMEM((rows, width), BF),
            pltpu.VMEM((rows, mixed.shape[1]), BF),
            pltpu.VMEM((rows, width), BF),
            sems,
            sems,
            pltpu.SemaphoreType.DMA((7,)),
        ],
        compiler_params=pltpu.CompilerParams(
            collective_id=collective_id, has_side_effects=True, vmem_limit_bytes=VMEM_LIMIT
        ),
        cost_estimate=pl.CostEstimate(
            flops=4 * count * rows * width * depth, bytes_accessed=400 << 20, transcendentals=0
        ),
        name="tail",
    )(*arrays)


def finish_kernel(
    out_ref, tok_ref, mgate_ref, mup_ref, down_ref, in_ref, gains_ref, key_ref, value_ref, wout_ref, *results
):
    for source, target in zip((out_ref, tok_ref, mgate_ref, mup_ref, down_ref), results):
        target[...] = source[...].reshape(target.shape).astype(target.dtype)
    query, gate, first, second, key, value, wout = results[5:]
    key[...] = key_ref[...]
    value[...] = value_ref[...]
    wout[...] = wout_ref[...]
    size = query.shape[1]
    query[...] = in_ref[:, :size]
    gate[...] = in_ref[:, size : 2 * size]
    first[...] = gains_ref[pl.ds(0, 1)]
    second[...] = gains_ref[pl.ds(1, 1)]


def finish(output, d_tokens, d_mlp, d_down, d_in, gains, *rest):
    count, rows, width = output.shape
    tall, hidden = d_mlp.shape[0], d_mlp.shape[1] // 2
    down_rows, wide = d_down.shape
    depth = d_in.shape[1]
    size = depth // 3
    parts = max(1, 16 // count)
    grid = count * parts

    def strip(high, across, at=0):
        return pl.BlockSpec((high // grid, across), lambda i: (i, at))

    def held(*shape):
        return pl.BlockSpec(shape, lambda i: (0, 0))

    def shape(*extent, dtype=F32):
        return jax.ShapeDtypeStruct(extent, dtype)

    whole = pl.BlockSpec((1, rows // parts, width), lambda i: (i // parts, i % parts, 0))
    return pl.pallas_call(
        finish_kernel,
        grid=(grid,),
        out_shape=[
            shape(count * rows, width, dtype=BF), shape(count * rows, width, dtype=BF),
            shape(tall, hidden), shape(tall, hidden), shape(down_rows, wide),
            shape(tall, size), shape(tall, size),
            shape(1, wide), shape(1, wide), *[shape(*a.shape) for a in rest],
        ],
        in_specs=[
            whole, whole, strip(tall, hidden), strip(tall, hidden, 1), strip(down_rows, wide),
            strip(tall, depth), held(2, wide), *[held(*a.shape) for a in rest],
        ],
        out_specs=[
            strip(count * rows, width), strip(count * rows, width),
            strip(tall, hidden), strip(tall, hidden), strip(down_rows, wide),
            strip(tall, size), strip(tall, size),
            held(1, wide), held(1, wide), *[held(*a.shape) for a in rest],
        ],
        compiler_params=pltpu.CompilerParams(vmem_limit_bytes=VMEM_LIMIT),
        name="finish",
    )(output, d_tokens, d_mlp, d_mlp, d_down, d_in, gains, *rest)


def local_call(kernel, scalars, arrays, outs, scratch, flops, name):
    vmem = pl.BlockSpec(memory_space=pltpu.VMEM)
    smem = pl.BlockSpec(memory_space=pltpu.SMEM)
    return pl.pallas_call(
        kernel,
        out_shape=outs,
        in_specs=[smem] * len(scalars) + [vmem] * len(arrays),
        out_specs=[vmem] * len(outs),
        scratch_shapes=scratch,
        compiler_params=pltpu.CompilerParams(vmem_limit_bytes=VMEM_LIMIT),
        cost_estimate=pl.CostEstimate(flops=flops, bytes_accessed=8 << 20, transcendentals=0),
        name=name,
    )(*scalars, *arrays)


def ring_routes(count):
    spots = [ring_head(at, count) for at in range(count)]
    right = [(spots[at], spots[(at + 1) % count]) for at in range(count)]
    left = [(spots[at], spots[at - 1]) for at in range(count)]
    return right, left


def add_low(one, other):
    return (one.astype(F32) + other.astype(F32)).astype(BF)


def flow_steps(part, going, coming):
    count = lax.axis_size("head")
    place = ring_place(lax.axis_index("head"), count)
    right, left = ring_routes(count)
    rows = part.shape[0] // count
    steps = count // 2

    def mine(owner):
        return lax.dynamic_slice_in_dim(part, lax.rem(owner + count, count) * rows, rows, 0)

    for step in range(2, steps - 1):
        from_left = lax.ppermute(going, "head", right)
        from_right = lax.ppermute(coming, "head", left)
        going = add_low(from_left, mine(place + steps - 1 - step))
        coming = add_low(from_right, mine(place - steps + 1 + step))
        going, coming = yield going, coming


def matmul(left, right):
    return jnp.dot(left, right, preferred_element_type=F32)


def rows_inner(left, right):
    return lax.dot_general(left, right, (((0,), (0,)), ((), ())), preferred_element_type=F32)


def cols_inner(left, right):
    return lax.dot_general(left, right, (((1,), (1,)), ((), ())), preferred_element_type=F32)


def rms_scale(values):
    return lax.rsqrt(jnp.mean(values * values, axis=1, keepdims=True) + EPSILON)


def per_device(
    tokens,
    segment_ids,
    norm1_gain,
    w_query,
    w_key,
    w_value,
    w_gate,
    w_out,
    norm2_gain,
    w_mlp_gate,
    w_mlp_up,
    w_down,
    out_grad,
):
    heads = lax.axis_size("head")
    batches = lax.axis_size("batch")
    row_count, width = tokens.shape
    head_size = w_query.shape[1]
    half = w_key.shape[1]
    chunk = row_count // heads
    me = ring_place(lax.axis_index("head"), heads)
    scale_factor = 1.0 / math.sqrt(head_size)

    down_parts = jnp.split(w_down, 2, axis=0)
    w_shard = jnp.concatenate([w_query, w_gate, w_key, w_value], axis=1)
    gains = jnp.concatenate([norm1_gain, norm2_gain]).reshape(-1, 128).astype(F32)
    normed_one, queries, gate_logit, kv_all, w_in, out_full, gains, seg_all, down_top = entry(
        tokens, w_shard, w_out, gains, segment_ids.reshape(-1, 128), down_parts[0], 1
    )
    gains, w_mlp_gate = lax.optimization_barrier((gains, w_mlp_gate))
    seg_all = seg_all.reshape(-1)
    gains = gains.reshape(batches, 2, -1).transpose(1, 0, 2).reshape(2, width)
    gain_one, gain_two = gains[0], gains[1]
    mgate_full = lax.all_gather(w_mlp_gate, "batch", axis=0, tiled=True)

    base = lax.axis_index("batch") * row_count
    ids = jnp.arange(DOCUMENTS, dtype=jnp.int32)
    below = jnp.sum((seg_all[None, :] < ids[:, None]).astype(jnp.int32), axis=1)
    starts = jnp.sum(jnp.where(segment_ids[None, :] == ids[:, None], below[:, None], 0), axis=0)
    scalars = (starts, base.reshape(1))
    pair_flops = 4 * row_count * kv_all.shape[0] * head_size
    attended, mixed, lse = local_call(
        functools.partial(attend_kernel, scale_factor),
        scalars,
        (queries, kv_all, starts[None], gate_logit),
        [
            jax.ShapeDtypeStruct((row_count, head_size), F32),
            jax.ShapeDtypeStruct((row_count, head_size), BF),
            jax.ShapeDtypeStruct((1, row_count), F32),
        ],
        [],
        pair_flops,
        "attend",
    )
    mixed_all, down_low, mup_full = spread(
        [mixed, down_parts[1], w_mlp_up], (("head", "cols"), ("batch", "cols"), ("batch", "rows")), 2
    )
    (
        mlp_part, d_mlp, d_down, resid_own, d_resid, d_resid_low, d_gain_two, d_mixed, going, coming,
    ) = mlp_back(
        tokens, mixed_all, out_grad, gain_two[None], out_full, mgate_full, mup_full, down_top, down_low, 3
    )
    hold = lax.optimization_barrier
    flow = flow_steps(mlp_part, going, coming)
    state = next(flow)

    d_queries, d_gate_logit, d_kv_all = local_call(
        functools.partial(attend_back_kernel, scale_factor),
        scalars,
        (queries, kv_all, starts[None], gate_logit, attended, d_mixed, lse),
        [
            jax.ShapeDtypeStruct((row_count, head_size), BF),
            jax.ShapeDtypeStruct((row_count, head_size), BF),
            jax.ShapeDtypeStruct(kv_all.shape, BF),
        ],
        [pltpu.VMEM((kv_all.shape[0], head_size), F32)] * 2,
        5 * pair_flops // 2,
        "attend_back",
    )
    for _ in range(3, heads // 2 - 1):
        state = flow.send(state)
    d_down = lax.psum_scatter(d_down, "batch", scatter_dimension=1, tiled=True)
    d_mlp = lax.psum_scatter(d_mlp, "batch", scatter_dimension=0, tiled=True)
    output, d_tokens, d_gains, d_out, d_in, d_key, d_value = tail(
        (
            d_queries, d_gate_logit, d_kv_all, w_in, gain_one[None], d_resid, d_gain_two,
            d_resid_low, resid_own, *state, normed_one, tokens, mixed_all, mlp_part,
        ),
        5,
    )
    (
        output, d_tokens, d_mgate, d_mup, d_down, d_query, d_gate, d_one, d_two,
        d_key, d_value, d_out,
    ) = finish(output, d_tokens, d_mlp, d_down, d_in, d_gains, d_key, d_value, d_out)
    return (
        output,
        d_tokens,
        d_one.reshape(-1),
        d_query,
        d_key.T,
        d_value.T,
        d_gate,
        d_out,
        d_two.reshape(-1),
        d_mgate,
        d_mup,
        d_down,
    )


def solution(mesh):
    return jax.shard_map(
        per_device,
        mesh=mesh,
        in_specs=(
            P("batch", None),
            P("batch"),
            P("batch"),
            P("batch", "head"),
            P("batch", "head"),
            P("batch", "head"),
            P("batch", "head"),
            P("head", "batch"),
            P("batch"),
            P("batch", "head"),
            P("batch", "head"),
            P("head", "batch"),
            P("batch", None),
        ),
        out_specs=(
            P("batch", None),
            P("batch", None),
            P("batch"),
            P("batch", "head"),
            P("batch", "head"),
            P("batch", "head"),
            P("batch", "head"),
            P("head", "batch"),
            P("batch"),
            P("batch", "head"),
            P("batch", "head"),
            P("head", "batch"),
        ),
        check_vma=False,
    )
```

```python
import functools
import math

import jax
import jax.numpy as jnp
from jax import lax
from jax.experimental import pallas as pl
from jax.experimental.pallas import tpu as pltpu
from jax.sharding import PartitionSpec as P

EPSILON = 1e-06
MASKED = -1e30
DOCUMENTS = 7
BF = jnp.bfloat16
F32 = jnp.float32


MESH = pl.DeviceIdType.MESH
VMEM_LIMIT = 60 << 20


def ring_place(head, count):
    high, low = head // 2, head % 2
    return (1 - low) * high + low * (count - 1 - high)


def ring_head(place, count):
    low = place // (count // 2)
    high = (1 - low) * place + low * (count - 1 - place)
    return 2 * high + low


def ring_setup(count):
    batch = lax.axis_index("batch")
    place = ring_place(lax.axis_index("head"), count)
    right = (batch, ring_head(lax.rem(place + 1, count), count))
    left = (batch, ring_head(lax.rem(place + count - 1, count), count))
    return place, right, left


def greet(devices):
    barrier = pltpu.get_barrier_semaphore()
    for device in devices:
        pl.semaphore_signal(barrier, inc=1, device_id=device, device_id_type=MESH)
    pl.semaphore_wait(barrier, len(devices))


def send(source, target, sems, slot, device):
    copy = pltpu.make_async_remote_copy(
        src_ref=source,
        dst_ref=target,
        send_sem=sems[0].at[slot],
        recv_sem=sems[1].at[slot],
        device_id=device,
        device_id_type=MESH,
    )
    copy.start()
    return copy


def half_of(extent, flow):
    if extent[1] % 256:
        return (pl.ds(flow * (extent[0] // 2), extent[0] // 2), slice(None))
    return (slice(None), pl.ds(flow * (extent[1] // 2), extent[1] // 2))


def place_of(whole, own, chunk, form):
    rows, wide = own.shape[-2:]
    if form == "lead":
        return whole.at[chunk]
    if form == "rows":
        return whole.at[pl.ds(pl.multiple_of(chunk * rows, rows), rows)]
    return whole.at[:, pl.ds(pl.multiple_of(chunk * wide, wide), wide)]


def spread_kernel(count, batches, plans, *refs):
    steps = count // 2
    arrays = len(plans)
    own_refs, all_refs = list(refs[:arrays]), refs[arrays : 2 * arrays]
    for index, (_, form) in enumerate(plans):
        if form == "low":
            half = own_refs[index].shape[0] // 2
            own_refs[index] = own_refs[index].at[pl.ds(half, half)]
    send_sem, recv_sem, local_sem = refs[2 * arrays :]
    place, right, left = ring_setup(count)
    head = lax.axis_index("head")
    batch = lax.axis_index("batch")
    across, core = batch // 2, lax.rem(batch, 2)
    others = batches // 2
    twin = (across * 2 + 1 - core, head)
    peers = [(lax.rem(across + hop, others) * 2 + core, head) for hop in range(1, others)]
    ring = any(axis == "head" for axis, _ in plans)
    grid = any(axis == "batch" for axis, _ in plans)
    greet((right, left) * ring + (twin, *peers) * grid)
    sems = (send_sem, recv_sem)
    slot = 0
    waiting, arriving, local = [], [], []

    def go(source, target, device):
        nonlocal slot
        copy = send(source, target, sems, slot, device)
        slot += 1
        waiting.append(copy)
        return copy

    stages = []
    for index, (axis, form) in enumerate(plans):
        own, whole = own_refs[index], all_refs[index]
        spot = place if axis == "head" else batch
        copy = pltpu.make_async_copy(own, place_of(whole, own, spot, form), local_sem.at[index])
        copy.start()
        local.append(copy)
        if axis == "batch":
            stages.append(index)
    onward = []

    def stage():
        for copy, block in onward:
            copy.wait_recv()
            arriving.append(go(block, block, twin))
        onward.clear()
        if stages:
            index = stages.pop(0)
            own, whole, form = own_refs[index], all_refs[index], plans[index][1]
            mine = place_of(whole, own, batch, form)
            for hop, peer in enumerate(peers, 1):
                source = lax.rem(across + others - hop, others) * 2 + core
                onward.append((go(own, mine, peer), place_of(whole, own, source, form)))
            arriving.append(go(own, mine, twin))

    stage()
    copies = [None] * (2 * arrays)
    for step in range(steps):
        for index, (axis, form) in enumerate(plans):
            if axis != "head":
                continue
            own = own_refs[index]
            for flow, chunk, device in ((0, place - step, right), (1, place + step, left)):
                at = 2 * index + flow
                if step:
                    copies[at].wait_recv()
                chunk = lax.rem(chunk + count, count)
                target = place_of(all_refs[index], own, chunk, form)
                source = target if step else own
                if step == steps - 1:
                    part = half_of(own.shape, flow)
                    source = source.at[part]
                    target = target.at[part]
                copies[at] = go(source, target, device)
        if step == steps // 2:
            stage()
    while stages or onward:
        stage()
    for copy in copies:
        if copy is not None:
            arriving.append(copy)
    for copy in arriving:
        copy.wait_recv()
    for copy in waiting:
        copy.wait_send()
    for copy in local:
        copy.wait()


def spread(arrays, plans, collective_id):
    count = lax.axis_size("head")
    batches = lax.axis_size("batch")
    shapes = []
    slots = 0
    for array, (axis, form) in zip(arrays, plans):
        many = count if axis == "head" else batches
        slots += count if axis == "head" else batches - 1
        if form == "lead":
            shapes.append((many, *array.shape))
        elif form == "rows":
            shapes.append((many * array.shape[0], array.shape[1]))
        else:
            tall = array.shape[0] // (2 if form == "low" else 1)
            shapes.append((tall, many * array.shape[1]))
    hbm = pl.BlockSpec(memory_space=pl.ANY)
    return pl.pallas_call(
        functools.partial(spread_kernel, count, batches, plans),
        out_shape=[jax.ShapeDtypeStruct(shape, a.dtype) for shape, a in zip(shapes, arrays)],
        in_specs=[pl.BlockSpec(memory_space=pltpu.VMEM)] * len(arrays),
        out_specs=[hbm] * len(arrays),
        scratch_shapes=[
            pltpu.SemaphoreType.DMA((slots,)),
            pltpu.SemaphoreType.DMA((slots,)),
            pltpu.SemaphoreType.DMA((len(arrays),)),
        ],
        compiler_params=pltpu.CompilerParams(
            collective_id=collective_id, has_side_effects=True, vmem_limit_bytes=VMEM_LIMIT
        ),
        name=f"spread_{collective_id}",
    )(*arrays)


def mlp_kernel(
    count, x_hbm, a_hbm, dy_hbm, gain_ref, out_hbm, gate_hbm, up_hbm, top_hbm, low_hbm,
    mlp_hbm, dmlp_hbm, ddown_hbm, h1_ref, dh1_ref, low_ref, dgain_ref, da_ref, ahead_ref, behind_ref,
    x_s, a_s, mlp_s, h1_s, dy_all, n2_all, hid_all, grad_all, dmlp_s, ddown_s, da_part,
    mlp_far, mlp_next, mlp_got, right_part, left_part, right_got, left_got,
    out_w, gate_w, up_w, down_w, in_sem, out_sem, grad_sem, weight_sem,
    send_sem, recv_sem, da_send, da_recv, far_send, far_recv,
):
    steps = count // 2
    rows = x_hbm.shape[0] // count
    width = x_hbm.shape[1]
    hidden = gate_w.shape[1]
    middle = hidden // 2
    weights = [
        pltpu.make_async_copy(source, target, weight_sem.at[index])
        for index, (source, target) in enumerate(
            (
                (out_hbm, out_w), (gate_hbm, gate_w), (up_hbm, up_w),
                (top_hbm, down_w.at[pl.ds(0, middle)]), (low_hbm, down_w.at[pl.ds(middle, middle)]),
            )
        )
    ]
    side = width // 2
    tile = 256
    broad = 1024
    inner = 256 if hidden % 256 == 0 else 128
    size = da_ref.shape[1]
    place, right, left = ring_setup(count)

    def member(hop):
        spot = lax.rem(place + hop, count)
        return spot, (lax.axis_index("batch"), ring_head(spot, count))

    def owners(group):
        first = jnp.where(group == 0, 1, 0)
        one = lax.rem(place + steps - group, count)
        two = lax.rem(place - steps + group + first * steps + count, count)
        return one, two

    def span(owner):
        return pl.ds(pl.multiple_of(owner * rows, rows), rows)

    def tile_of(at, extent=tile):
        return pl.ds(pl.multiple_of(at * extent, extent), extent)

    def loads(group, slot):
        return [
            pltpu.make_async_copy(
                source.at[span(owner)],
                target.at[pl.ds(at * rows, rows)],
                in_sem.at[slot, 2 * index + at],
            )
            for index, (source, target) in enumerate(
                ((x_hbm, x_s.at[slot]), (a_hbm, a_s.at[slot]), (dy_hbm, dy_all.at[group]))
            )
            for at, owner in enumerate(owners(group))
        ]

    def stores(group, slot):
        return [
            pltpu.make_async_copy(
                mlp_s.at[slot, pl.ds(at * rows, rows)], mlp_hbm.at[span(owner)], out_sem.at[slot, at]
            )
            for at, owner in enumerate(owners(group))
        ]

    def passing(source, target, sems, slot, device):
        return pltpu.make_async_remote_copy(
            src_ref=source,
            dst_ref=target,
            send_sem=sems[0].at[slot],
            recv_sem=sems[1].at[slot],
            device_id=device,
            device_id_type=MESH,
        )

    ring_sems, far_sems = (send_sem, recv_sem), (far_send, far_recv)
    ahead, behind = pl.ds(0, side), pl.ds(side, side)

    def first_copies():
        return (
            passing(right_part.at[0, :, ahead], right_got.at[0, :, ahead], ring_sems, 0, right),
            passing(right_part.at[0, :, behind], left_got.at[0, :, behind], ring_sems, steps, left),
        )

    def later_copies(step):
        return (
            passing(right_got.at[step - 1], right_got.at[step], ring_sems, step, right),
            passing(left_got.at[step - 1], left_got.at[step], ring_sems, steps + step, left),
        )

    for copy in (*loads(0, 0), *weights):
        copy.start()
    greet([member(hop)[1] for hop in range(1, count)])
    weights[0].wait()

    @pl.loop(0, steps)
    def _(group):
        slot = lax.rem(group, 2)
        for copy in loads(group, slot):
            copy.wait()

        @pl.when(group + 1 < steps)
        def _():
            for copy in loads(group + 1, 1 - slot):
                copy.start()

        @pl.when(group >= 2)
        def _():
            for copy in stores(group - 2, slot):
                copy.wait()

        mixed = a_s[slot]

        def residual(at, total):
            cols = tile_of(at, broad)
            values = x_s[slot, :, cols].astype(F32) + matmul(mixed, out_w[:, cols])
            h1_s[:, cols] = values
            return total + jnp.sum(values * values, axis=1, keepdims=True)

        total = lax.fori_loop(0, width // broad, residual, jnp.zeros((2 * rows, 1), F32))
        scale = lax.rsqrt(total / width + EPSILON)

        @pl.when(group == 0)
        def _():
            h1_ref[...] = h1_s[pl.ds(rows, rows)]
            for copy in weights[1:]:
                copy.wait()

        @pl.loop(0, width // tile)
        def _(at):
            cols = tile_of(at)
            n2_all[group, :, cols] = (h1_s[:, cols] * scale * gain_ref[:, cols]).astype(BF)

        normed = n2_all[group]
        dy = dy_all[group]

        @pl.loop(0, hidden // inner)
        def _(at):
            cols = tile_of(at, inner)
            cols_up = pl.ds(pl.multiple_of(hidden + at * inner, inner), inner)
            gate = matmul(normed, gate_w[:, cols])
            up = matmul(normed, up_w[:, cols])
            d_hidden = cols_inner(dy, down_w[cols])
            sig = jax.nn.sigmoid(gate)
            silu = gate * sig
            hid_all[group, :, cols] = (silu * up).astype(BF)
            grad_all[group, :, cols] = (d_hidden * up * sig * (1.0 + gate * (1.0 - sig))).astype(BF)
            grad_all[group, :, cols_up] = (d_hidden * silu).astype(BF)

        hid = hid_all[group]
        d_gate = grad_all[group, :, :hidden]
        d_up = grad_all[group, :, hidden:]
        half = jnp.minimum(group, 1)

        @pl.loop(0, width // broad)
        def _(at):
            cols = tile_of(at, broad)
            part = (cols_inner(d_gate, gate_w[cols]) + cols_inner(d_up, up_w[cols])).astype(BF)
            right_part[half, :, cols] = part[:rows]
            left_part[half, :, cols] = part[rows:]

        @pl.when(group == 0)
        def _():
            for copy in first_copies():
                copy.start()

        @pl.when(group == 1)
        def _():
            one, two = first_copies()
            one.wait_recv()
            right_got[0, :, ahead] = add_low(right_part[1, :, ahead], right_got[0, :, ahead])
            right_got[0, :, behind] = right_part[1, :, behind]
            two.wait_recv()
            left_got[0, :, behind] = add_low(left_part[1, :, behind], left_got[0, :, behind])
            left_got[0, :, ahead] = left_part[1, :, ahead]

        @pl.when(group >= 2)
        def _():
            one, two = later_copies(group - 1)
            one.wait_recv()
            right_got[group - 1] = add_low(right_part[1], right_got[group - 1])
            two.wait_recv()
            left_got[group - 1] = add_low(left_part[1], left_got[group - 1])

        @pl.when(group >= 1)
        def _():
            for copy in later_copies(group):
                copy.start()

        @pl.loop(0, width // broad)
        def _(at):
            cols = tile_of(at, broad)
            mlp_s[slot, :, cols] = matmul(hid, down_w[:, cols]).astype(BF)

        for copy in stores(group, slot):
            copy.start()

        @pl.when(group == 0)
        def _():
            mlp_far[...] = mlp_s[slot, pl.ds(0, rows)]

        @pl.when(group == 1)
        def _():
            mlp_next[0] = mlp_s[slot, pl.ds(0, rows)]
            mlp_next[1] = mlp_s[slot, pl.ds(rows, rows)]

        @pl.when(group == 2)
        def _():
            ahead_ref[...] = mlp_s[slot, pl.ds(0, rows)]
            behind_ref[...] = mlp_s[slot, pl.ds(rows, rows)]

    far_copies = [
        passing(mlp_far.at[:, ahead], mlp_got.at[0, :, ahead], far_sems, 0, right),
        passing(mlp_far.at[:, behind], mlp_got.at[1, :, behind], far_sems, 1, left),
    ]
    for copy in far_copies:
        copy.start()

    every = steps * 2 * rows

    def dmlp_copy(at, slot):
        return pltpu.make_async_copy(
            dmlp_s.at[slot], dmlp_hbm.at[tile_of(at // 2), tile_of(lax.rem(at, 2), hidden)], grad_sem.at[slot]
        )

    mlp_tiles = 2 * (width // tile)

    @pl.loop(0, mlp_tiles)
    def _(at):
        slot = lax.rem(at, 2)

        @pl.when(at >= 2)
        def _():
            dmlp_copy(at - 2, slot).wait()

        normed = n2_all[:, :, tile_of(at // 2)].reshape(every, tile)
        grads = grad_all[:, :, tile_of(lax.rem(at, 2), hidden)].reshape(every, hidden)
        dmlp_s[slot] = rows_inner(normed, grads).astype(BF)
        dmlp_copy(at, slot).start()

    wide = 512
    across = width // wide

    def ddown_copy(at, slot):
        return pltpu.make_async_copy(
            ddown_s.at[slot],
            ddown_hbm.at[tile_of(at // across, inner), tile_of(lax.rem(at, across), wide)],
            grad_sem.at[2 + slot],
        )

    down_tiles = across * (hidden // inner)

    @pl.loop(0, down_tiles)
    def _(at):
        slot = lax.rem(at, 2)

        @pl.when(at >= 2)
        def _():
            ddown_copy(at - 2, slot).wait()

        hid = hid_all[:, :, tile_of(at // across, inner)].reshape(every, inner)
        dy = dy_all[:, :, tile_of(lax.rem(at, across), wide)].reshape(every, wide)
        ddown_s[slot] = rows_inner(hid, dy).astype(BF)
        ddown_copy(at, slot).start()

    for copy in later_copies(steps - 1):
        copy.wait_recv()
    for flow, have, lack in ((0, ahead, behind), (1, behind, ahead)):
        far_copies[flow].wait_recv()
        mlp_got[flow, :, have] = add_low(mlp_got[flow, :, have], mlp_next[flow, :, have])
        mlp_got[flow, :, lack] = mlp_next[flow, :, lack]
    next_copies = [
        passing(mlp_got.at[0], mlp_got.at[2], far_sems, 2, right),
        passing(mlp_got.at[1], mlp_got.at[3], far_sems, 3, left),
    ]
    for copy in next_copies:
        copy.start()

    def collect(at, state):
        squares, mean = state
        cols = tile_of(at)
        dn2 = (
            left_part[0, :, cols].astype(F32)
            + right_got[steps - 1, :, cols].astype(F32)
            + left_got[steps - 1, :, cols].astype(F32)
        )
        dh1_ref[:, cols] = dn2
        h1 = h1_ref[:, cols]
        squares = squares + jnp.sum(h1 * h1, axis=1, keepdims=True)
        return squares, mean + jnp.sum(gain_ref[:, cols] * dn2 * h1, axis=1, keepdims=True)

    zero = jnp.zeros((rows, 1), F32)
    squares, mean = lax.fori_loop(0, width // tile, collect, (zero, zero))
    scale_own = lax.rsqrt(squares / width + EPSILON)
    pull = scale_own * scale_own * scale_own * (mean / width)

    @pl.loop(0, width // tile)
    def _(at):
        cols = tile_of(at)
        dn2, h1 = dh1_ref[:, cols], h1_ref[:, cols]
        dgain_ref[:, cols] = jnp.sum(dn2 * h1 * scale_own, axis=0, keepdims=True)
        dy = dy_all[0, pl.ds(rows, rows), cols].astype(F32)
        d_resid = dy + scale_own * (gain_ref[:, cols] * dn2) - h1 * pull
        dh1_ref[:, cols] = d_resid
        low_ref[:, cols] = d_resid.astype(BF)

    def da_copy(hop):
        return passing(
            da_part.at[hop], da_ref.at[span(place)], (da_send, da_recv), hop, member(hop)[1]
        )

    low = low_ref[...]

    @pl.loop(1, count)
    def _(hop):
        spot = member(hop)[0]
        da_part[hop] = cols_inner(low, out_w[tile_of(spot, size)]).astype(BF)
        da_copy(hop).start()

    da_ref[span(place)] = cols_inner(low, out_w[tile_of(place, size)]).astype(BF)

    @pl.loop(1, count)
    def _(hop):
        da_copy(hop).wait_recv()
        da_copy(hop).wait_send()

    for flow, held in ((0, ahead_ref), (1, behind_ref)):
        next_copies[flow].wait_recv()
        held[...] = add_low(held[...], mlp_got[2 + flow])
    for copy in (*far_copies, *next_copies, *first_copies()):
        copy.wait_send()
    for step in range(1, steps):
        for copy in later_copies(step):
            copy.wait_send()
    for group in range(steps - 2, steps):
        for copy in stores(group, group % 2):
            copy.wait()
    for at in range(2):
        dmlp_copy(mlp_tiles - 2 + at, (mlp_tiles + at) % 2).wait()
        ddown_copy(down_tiles - 2 + at, (down_tiles + at) % 2).wait()


def mlp_back(tokens, mixed, dy, gain, out_w, gate_w, up_w, down_top, down_low, collective_id):
    count = lax.axis_size("head")
    total, width = tokens.shape
    hidden = gate_w.shape[1]
    rows, steps = total // count, count // 2
    size = mixed.shape[1] // count
    inner = 256 if hidden % 256 == 0 else 128
    vmem = pl.BlockSpec(memory_space=pltpu.VMEM)
    hbm = pl.BlockSpec(memory_space=pl.ANY)

    def slots(many, tall, wide, dtype=BF):
        return pltpu.VMEM((many, tall, wide), dtype)

    def shape(*extent, dtype=BF):
        return jax.ShapeDtypeStruct(extent, dtype)

    dma = pltpu.SemaphoreType.DMA
    flops = 2 * total * width * (mixed.shape[1] + 9 * hidden)
    return pl.pallas_call(
        functools.partial(mlp_kernel, count),
        out_shape=[
            shape(total, width), shape(width, 2 * hidden), shape(hidden, width),
            shape(rows, width, dtype=F32), shape(rows, width, dtype=F32), shape(rows, width),
            shape(1, width, dtype=F32), shape(total, size), shape(rows, width), shape(rows, width),
        ],
        in_specs=[hbm] * 3 + [vmem] + [hbm] * 5,
        out_specs=[hbm] * 3 + [vmem] * 7,
        scratch_shapes=[
            slots(2, 2 * rows, width), slots(2, 2 * rows, mixed.shape[1]), slots(2, 2 * rows, width),
            pltpu.VMEM((2 * rows, width), F32),
            slots(steps, 2 * rows, width), slots(steps, 2 * rows, width),
            slots(steps, 2 * rows, hidden), slots(steps, 2 * rows, 2 * hidden),
            slots(2, 256, hidden), slots(2, inner, 512), slots(count, rows, size),
            pltpu.VMEM((rows, width), BF), slots(2, rows, width), slots(4, rows, width),
            slots(2, rows, width), slots(2, rows, width),
            slots(steps, rows, width), slots(steps, rows, width),
            *[pltpu.VMEM(weight.shape, BF) for weight in (out_w, gate_w, up_w)],
            pltpu.VMEM((hidden, width), BF),
            dma((2, 6)), dma((2, 2)), dma((4,)), dma((5,)), dma((count,)), dma((count,)),
            dma((count,)), dma((count,)), dma((4,)), dma((4,)),
        ],
        compiler_params=pltpu.CompilerParams(
            collective_id=collective_id, has_side_effects=True, vmem_limit_bytes=VMEM_LIMIT
        ),
        cost_estimate=pl.CostEstimate(flops=flops, bytes_accessed=40 << 20, transcendentals=0),
        name="mlp_back",
    )(tokens, mixed, dy, gain, out_w, gate_w, up_w, down_top, down_low)


def entry_kernel(
    count, batches, x_ref, w_ref, out_ref, gain_ref, seg_ref, down_ref,
    n1_hbm, q_ref, logit_ref, kv_ref, w_all, out_all, gain_all, seg_all, down_all,
    x_s, n1_ref, send_sem, recv_sem, local_sem, x_sem, n1_sem,
):
    steps = count // 2
    others = batches // 2
    rows, width = x_ref.shape
    depth = w_ref.shape[0]
    size, wide = out_ref.shape
    block = 256
    blocks = rows // block

    def x_copy(at):
        here = pl.ds(pl.multiple_of(at * block, block), block)
        return pltpu.make_async_copy(x_ref.at[here], x_s.at[here], x_sem.at[at])

    def n1_copy(at):
        here = pl.ds(pl.multiple_of(at * block, block), block)
        return pltpu.make_async_copy(n1_ref.at[here], n1_hbm.at[here], n1_sem.at[at])

    for at in range(blocks):
        x_copy(at).start()
    place, right, left = ring_setup(count)
    head = lax.axis_index("head")
    batch = lax.axis_index("batch")
    across, core, low = batch // 2, lax.rem(batch, 2), lax.rem(head, 2)
    twin = (across * 2 + 1 - core, head)
    mate = (batch, head + 1 - 2 * low)
    spots = [lax.rem(across + hop, others) for hop in range(others)]
    backs = [lax.rem(across + others - hop, others) for hop in range(others)]
    peers = [(spot * 2 + core, head) for spot in spots]
    far_peers = [(spot * 2 + 1 - core, head) for spot in spots]
    greet((twin, mate, right, left, *peers[1:], *far_peers[1:]))
    sems = (send_sem, recv_sem)
    slot = 0
    copies = []

    def go(source, target, device):
        nonlocal slot
        copy = send(source, target, sems, slot, device)
        slot += 1
        copies.append(copy)
        return copy

    def part(at, extent):
        return pl.ds(pl.multiple_of(at * extent, extent), extent)

    def both(view, own):
        out = [go(own, view(batch), peers[hop]) for hop in range(1, others)]
        return out, [go(own, view(batch), twin)]

    def pass_on(view, arrived):
        out = []
        for hop in range(1, others):
            arrived[hop - 1].wait_recv()
            there = view(backs[hop] * 2 + core)
            out.append(go(there, there, twin))
        return out

    local = []

    def stay(source, target):
        copy = pltpu.make_async_copy(source, target, local_sem.at[len(local)])
        copy.start()
        local.append(copy)

    def main_view(at):
        return w_all.at[part(at, depth), pl.ds(0, 3 * size)]

    def mate_view(at):
        return w_all.at[part(at, depth), pl.ds(3 * size, size)]

    def out_view(chunk, at):
        return out_all.at[part(chunk, size), part(at, wide)]

    small = []
    for own, whole in ((gain_ref, gain_all), (seg_ref, seg_all)):
        for device in (twin, *peers[1:], *far_peers[1:]):
            small.append(go(own, whole.at[batch], device))
        stay(own, whole.at[batch])
    from_mate = go(w_ref.at[:, pl.ds(2 * size, size)], mate_view(batch), mate)
    main_out, main_twin = both(main_view, w_ref)
    stay(w_ref, main_view(batch))
    out_peers = [go(out_ref, out_view(place, batch), peers[hop]) for hop in range(1, others)]
    stay(out_ref, out_view(place, batch))
    flows = [[None, None] for _ in range(others)]

    def ring(step):
        for hop in range(others):
            lane = spots[0] if hop == 0 else backs[hop]
            at = lane * 2 + core
            if step == 0 and hop:
                out_peers[hop - 1].wait_recv()
            for flow, chunk, device in ((0, place - step, right), (1, place + step, left)):
                if step:
                    flows[hop][flow].wait_recv()
                target = out_view(lax.rem(chunk + count, count), at)
                source = out_ref if step == 0 and hop == 0 else target
                if step == steps - 1:
                    cut = (pl.ds(flow * (size // 2), size // 2), slice(None))
                    source, target = source.at[cut], target.at[cut]
                flows[hop][flow] = go(source, target, device)

    for copy in small:
        copy.wait_recv()
    for copy in local[:2]:
        copy.wait()

    def normalize(at):
        here = part(at, block)
        x_copy(at).wait()

        def squares(tile, total):
            values = x_s[here, part(tile, 256)].astype(F32)
            return total + jnp.sum(values * values, axis=1, keepdims=True)

        total = lax.fori_loop(0, width // 256, squares, jnp.zeros((block, 1), F32))
        scale = lax.rsqrt(total / width + EPSILON)

        @pl.loop(0, batches)
        def _(owner):
            for tile in range(depth // 128):
                cols = pl.ds(pl.multiple_of(owner * depth + tile * 128, 128), 128)
                values = x_s[here, cols].astype(F32) * scale
                n1_ref[here, cols] = (values * gain_all[owner, pl.ds(tile, 1)]).astype(BF)

        n1_copy(at).start()

    middle = blocks // 2

    @pl.loop(0, middle)
    def _(at):
        normalize(at)

    from_mate.wait_recv()
    mate_out, mate_twin = both(mate_view, mate_view(batch))
    ring(0)

    def down_view(at):
        return down_all.at[:, part(at, down_ref.shape[1])]

    down_own = down_ref.at[pl.ds(0, down_ref.shape[0] // 2)]
    down_out, down_twin = both(down_view, down_own)
    stay(down_own, down_view(batch))

    @pl.loop(middle, blocks)
    def _(at):
        normalize(at)

    main_passed = pass_on(main_view, main_out)
    mate_passed = pass_on(mate_view, mate_out)
    for copy in (*main_twin, *mate_twin, *main_passed, *mate_passed):
        copy.wait_recv()
    for copy in local[2:]:
        copy.wait()

    def kv_view(at):
        return kv_ref.at[part(at, rows)]

    @pl.loop(0, blocks)
    def _(at):
        here = part(at, block)
        values = matmul(n1_ref[here], w_all[:, pl.ds(2 * size, 2 * size)])
        one, two = values[:, :size], values[:, size:]
        first = jnp.where(low == 0, one, two).astype(BF)
        second = jnp.where(low == 0, two, one).astype(BF)
        half = size // 2
        there = pl.ds(pl.multiple_of(batch * rows + at * block, block), block)
        kv_ref[there, pl.ds(0, size)] = jnp.concatenate([first[:, :half], second[:, :half]], 1)
        kv_ref[there, pl.ds(size, size)] = jnp.concatenate([first[:, half:], second[:, half:]], 1)

    kv_out, kv_twin = both(kv_view, kv_view(batch))
    ring(1)

    @pl.loop(0, blocks)
    def _(at):
        here = part(at, block)
        values = matmul(n1_ref[here], w_all[:, pl.ds(0, 2 * size)])
        q_ref[here] = values[:, :size].astype(BF)
        logit_ref[here] = values[:, size:]

    for step in range(2, steps):
        ring(step)
    down_passed = pass_on(down_view, down_out)
    kv_passed = pass_on(kv_view, kv_out)
    for pair in flows:
        for copy in pair:
            copy.wait_recv()
    swaps = []
    for hop in range(others):
        there = out_all.at[:, part(spots[hop] * 2 + core, wide)]
        swaps.append(go(there, there, twin))
    for copy in (*kv_twin, *kv_passed, *swaps, *down_twin, *down_passed):
        copy.wait_recv()
    for copy in copies:
        copy.wait_send()
    for at in range(blocks):
        n1_copy(at).wait()


def entry(tokens, w_shard, w_out, gains, segments, w_down, collective_id):
    count = lax.axis_size("head")
    batches = lax.axis_size("batch")
    others = batches // 2
    rows, width = tokens.shape
    size, wide = w_out.shape
    vmem = pl.BlockSpec(memory_space=pltpu.VMEM)
    hbm = pl.BlockSpec(memory_space=pl.ANY)
    slots = 6 * batches + others * (count + 3)
    sems = pltpu.SemaphoreType.DMA((slots,))
    return pl.pallas_call(
        functools.partial(entry_kernel, count, batches),
        out_shape=[
            jax.ShapeDtypeStruct((rows, width), BF),
            jax.ShapeDtypeStruct((rows, size), BF),
            jax.ShapeDtypeStruct((rows, size), F32),
            jax.ShapeDtypeStruct((batches * rows, 2 * size), BF),
            jax.ShapeDtypeStruct((width, 4 * size), BF),
            jax.ShapeDtypeStruct((count * size, batches * wide), BF),
            jax.ShapeDtypeStruct((batches, *gains.shape), F32),
            jax.ShapeDtypeStruct((batches, *segments.shape), jnp.int32),
            jax.ShapeDtypeStruct((w_down.shape[0] // 2, batches * w_down.shape[1]), BF),
        ],
        in_specs=[hbm] + [vmem] * 5,
        out_specs=[hbm] + [vmem] * 4 + [hbm] + [vmem] * 2 + [hbm],
        scratch_shapes=[
            pltpu.VMEM((rows, width), BF), pltpu.VMEM((rows, width), BF),
            sems, sems, pltpu.SemaphoreType.DMA((5,)),
            pltpu.SemaphoreType.DMA((rows // 256,)), pltpu.SemaphoreType.DMA((rows // 256,)),
        ],
        compiler_params=pltpu.CompilerParams(
            collective_id=collective_id, has_side_effects=True, vmem_limit_bytes=VMEM_LIMIT
        ),
        name="entry",
    )(tokens, w_shard, w_out, gains, segments, w_down)


KEY_BLOCK = 512
QUERY_BLOCK = 640


def key_range(start_ref, base, query_block):
    first = query_block * QUERY_BLOCK
    lowest = start_ref[first]
    highest = start_ref[first + QUERY_BLOCK - 1]
    begin = lowest // KEY_BLOCK
    end = (base + first + QUERY_BLOCK - 1) // KEY_BLOCK + 1
    full_begin = jnp.minimum((highest + KEY_BLOCK - 1) // KEY_BLOCK, end)
    full_end = jnp.maximum((base + first + 1) // KEY_BLOCK, full_begin)
    return begin, full_begin, full_end, end


def allowed_pairs(key_block, start_row, base_row):
    shape = (KEY_BLOCK, QUERY_BLOCK)
    key_pos = key_block * KEY_BLOCK + lax.broadcasted_iota(jnp.int32, shape, 0)
    query_pos = base_row + lax.broadcasted_iota(jnp.int32, shape, 1)
    return (key_pos >= start_row) & (key_pos <= query_pos)


def attend_kernel(
    scale, start_sm, base_sm, q_ref, kv_ref, start_ref, logit_ref, o_ref, a_ref, lse_ref
):
    base = base_sm[0]
    size = q_ref.shape[1]
    factor = scale * math.log2(math.e)

    @pl.loop(0, q_ref.shape[0] // QUERY_BLOCK)
    def _(block):
        rows = pl.ds(pl.multiple_of(block * QUERY_BLOCK, QUERY_BLOCK), QUERY_BLOCK)
        queries = q_ref[rows]
        start_row = start_ref[:, rows]
        begin, full_begin, full_end, end = key_range(start_sm, base, block)

        def step(masked, at, state):
            old_max, old_sum, total = state
            keys = pl.ds(pl.multiple_of(at * KEY_BLOCK, KEY_BLOCK), KEY_BLOCK)
            scores = cols_inner(kv_ref[keys, :size], queries)
            if masked:
                allowed = allowed_pairs(at, start_row, base + block * QUERY_BLOCK)
                scores = jnp.where(allowed, scores, MASKED)
            new_max = jnp.maximum(old_max, jnp.max(scores, axis=0, keepdims=True))
            keep = jnp.exp2((old_max - new_max) * factor)
            weights = jnp.exp2(scores * factor - new_max * factor)
            new_sum = old_sum * keep + jnp.sum(weights, axis=0, keepdims=True)
            total = total * keep + rows_inner(kv_ref[keys, size:], weights.astype(BF))
            return new_max, new_sum, total

        state = (
            jnp.full((1, QUERY_BLOCK), MASKED, F32),
            jnp.zeros((1, QUERY_BLOCK), F32),
            jnp.zeros((size, QUERY_BLOCK), F32),
        )
        state = lax.fori_loop(begin, full_begin, functools.partial(step, True), state)
        state = lax.fori_loop(full_begin, full_end, functools.partial(step, False), state)
        state = lax.fori_loop(full_end, end, functools.partial(step, True), state)
        run_max, run_sum, total = state
        lse_ref[:, rows] = run_max * factor + jnp.log2(run_sum)
        attended = (total / run_sum).T
        o_ref[rows] = attended
        a_ref[rows] = (attended * jax.nn.sigmoid(logit_ref[rows])).astype(BF)


def attend_back_kernel(
    scale, start_sm, base_sm, q_ref, kv_ref, start_ref, logit_ref, o_ref, da_ref, lse_ref,
    dq_ref, dg_ref, dkv_ref, dk_acc, dv_acc,
):
    base = base_sm[0]
    size = q_ref.shape[1]
    factor = scale * math.log2(math.e)
    dk_acc[...] = jnp.zeros_like(dk_acc)
    dv_acc[...] = jnp.zeros_like(dv_acc)

    @pl.loop(0, q_ref.shape[0] // QUERY_BLOCK)
    def _(block):
        rows = pl.ds(pl.multiple_of(block * QUERY_BLOCK, QUERY_BLOCK), QUERY_BLOCK)
        queries = q_ref[rows]
        start_row = start_ref[:, rows]
        lse = lse_ref[:, rows]
        gate = jax.nn.sigmoid(logit_ref[rows])
        attended = o_ref[rows]
        d_mixed = da_ref[rows].astype(F32)
        d_attended = (d_mixed * gate).astype(BF)
        dg_ref[rows] = (d_mixed * attended * gate * (1.0 - gate)).astype(BF)
        delta = jnp.sum((d_attended.astype(F32) * attended).T, axis=0, keepdims=True)
        begin, full_begin, full_end, end = key_range(start_sm, base, block)

        def step(masked, at, d_queries):
            keys = pl.ds(pl.multiple_of(at * KEY_BLOCK, KEY_BLOCK), KEY_BLOCK)
            key_block = kv_ref[keys, :size]
            probs = jnp.exp2(cols_inner(key_block, queries) * factor - lse)
            if masked:
                allowed = allowed_pairs(at, start_row, base + block * QUERY_BLOCK)
                probs = jnp.where(allowed, probs, 0.0)
            d_probs = cols_inner(kv_ref[keys, size:], d_attended)
            d_scores = (probs * (d_probs - delta) * scale).astype(BF)
            dv_acc[keys] += matmul(probs.astype(BF), d_attended)
            dk_acc[keys] += matmul(d_scores, queries)
            return d_queries + rows_inner(key_block, d_scores)

        d_queries = jnp.zeros((size, QUERY_BLOCK), F32)
        d_queries = lax.fori_loop(begin, full_begin, functools.partial(step, True), d_queries)
        d_queries = lax.fori_loop(full_begin, full_end, functools.partial(step, False), d_queries)
        d_queries = lax.fori_loop(full_end, end, functools.partial(step, True), d_queries)
        dq_ref[rows] = d_queries.T.astype(BF)

    @pl.loop(0, kv_ref.shape[0] // KEY_BLOCK)
    def _(at):
        keys = pl.ds(pl.multiple_of(at * KEY_BLOCK, KEY_BLOCK), KEY_BLOCK)
        dk, dv = dk_acc[keys].astype(BF), dv_acc[keys].astype(BF)
        half = size // 2
        dkv_ref[keys, :size] = jnp.concatenate([dk[:, :half], dv[:, :half]], axis=1)
        dkv_ref[keys, size:] = jnp.concatenate([dk[:, half:], dv[:, half:]], axis=1)


def tail_kernel(
    count, batches, dq_ref, dg_ref, dkv_ref, w_ref, gain_ref, dh1_ref, second_ref,
    low_ref, h1_ref, ahead_ref, behind_ref, n1_ref, x_hbm, mixed_hbm, mlp_hbm,
    out_all, tok_all, gains_ref, wout_own, din_ref, key_ref, value_ref,
    part_ref, tok_ref, got, wout_got, gain_own, gain_got, gain_mid, gain_heads,
    din_s, din_got, din_x, wout_s, wout_twin, wout_x,
    cat_ref, out_s, out_got, core_got, x_first, x_second, y_first, y_second, held, n1_s,
    x_ref, mixed_ref, mlp_ref, mlp_next, send_sem, recv_sem, local_sem,
):
    steps = count // 2
    rows, width = x_ref.shape
    depth = cat_ref.shape[1]
    tall, size = dq_ref.shape
    tile = 256
    place, right, left = ring_setup(count)
    batch, head = lax.axis_index("batch"), lax.axis_index("head")
    others = [lax.rem(batch + hop, batches) for hop in range(1, batches)]
    members = [(batch, ring_head(lax.rem(place + hop, count), count)) for hop in range(1, count)]
    greet((*members, *[(other, head) for other in others]))
    sems = (send_sem, recv_sem)
    slot = 0
    copies = []

    def go(source, target, device):
        nonlocal slot
        copy = send(source, target, sems, slot, device)
        slot += 1
        copies.append(copy)
        return copy

    across, core = batch // 2, lax.rem(batch, 2)
    spots = [lax.rem(across + hop, batches // 2) for hop in range(batches // 2)]
    order = list(range(1, batches // 2)) + [0]
    twin = (across * 2 + 1 - core, head)

    def scatter_swap(view, held):
        return [go(view(2 * spots[hop] + 1 - core), held.at[spots[hop]], twin) for hop in order]

    def add_tiles(target, one, other):
        @pl.loop(0, target.shape[0] // 128)
        def _(at):
            lines = pl.ds(pl.multiple_of(at * 128, 128), 128)
            total = one[lines].astype(F32) + other[lines].astype(F32)
            target[lines] = total.astype(target.dtype)

    def scatter_cross(view, held, crossed, arriving):
        out = []
        for copy, hop in zip(arriving, order):
            copy.wait_recv()
            spot = spots[hop]
            add_tiles(held.at[spot], held.at[spot], view(2 * spot + core))
            if hop:
                out.append(go(held.at[spot], crossed.at[hop - 1], (spot * 2 + core, head)))
        return out

    def scatter_end(held, crossed, arriving, target):
        for hop, copy in enumerate(arriving):
            copy.wait_recv()
            last = hop == len(arriving) - 1
            add_tiles(target if last else held.at[across], held.at[across], crossed.at[hop])

    def wout_view(at):
        wide = width // batches
        return wout_s.at[:, pl.ds(pl.multiple_of(at * wide, wide), wide)]

    def din_view(at):
        tall = din_ref.shape[0]
        return din_s.at[pl.ds(pl.multiple_of(at * tall, tall), tall)]

    def span(owner, extent):
        return pl.ds(pl.multiple_of(lax.rem(owner + count, count) * extent, extent), extent)

    def compute(owner):
        here = span(owner, rows)
        values = cat_ref[here]

        @pl.loop(0, width // tile)
        def _(at):
            cols = pl.ds(pl.multiple_of(at * tile, tile), tile)
            part_ref[here, cols] = cols_inner(values, w_ref[cols, pl.ds(0, depth)]).astype(BF)

    def gather(own, whole, step, last):
        out = []
        for flow, chunk, device in ((0, place - step, right), (1, place + step, left)):
            if last:
                last[flow].wait_recv()
            target = whole.at[lax.rem(chunk + count, count)]
            source = target if step else own
            if step == steps - 1:
                cut = (slice(None), pl.ds(flow * (width // 2), width // 2))
                source, target = source.at[cut], target.at[cut]
            out.append(go(source, target, device))
        return out

    def reduce(parts, held, step, last):
        extent, side = held.shape[2], held.shape[3] // 2
        out = []
        for flow, owner, device in (
            (0, place + steps - step, right),
            (1, place - steps + step, left),
        ):
            have = pl.ds(flow * side, side)
            lack = pl.ds((1 - flow) * side, side)
            mine = parts.at[span(owner, extent)]
            if step == 0:
                out.append(go(mine.at[:, have], held.at[flow, 0, :, have], device))
                continue
            last[flow].wait_recv()
            if step == 1:
                held[flow, 0, :, have] = add_low(held[flow, 0, :, have], mine[:, have])
                held[flow, 0, :, lack] = mine[:, lack]
            else:
                held[flow, step - 1] = add_low(held[flow, step - 1], mine[...])
            out.append(go(held.at[flow, step - 1], held.at[flow, step], device))
        return out

    low = lax.rem(head, 2)
    mate = (batch, head + 1 - 2 * low)
    peers = [(spot * 2 + core, head) for spot in spots]
    mine = pl.ds(pl.multiple_of(low * size, size), size)
    given = pl.ds(pl.multiple_of((1 - low) * size, size), size)
    top, bottom = pl.ds(0, tall // 2), pl.ds(tall // 2, tall // 2)
    fresh = pl.ds(2 * size, size)

    def keys_of(at):
        return dkv_ref.at[pl.ds(pl.multiple_of(at * tall, tall), tall)]

    def normed_copy(at, slot):
        cols = pl.ds(pl.multiple_of(at * tile, tile), tile)
        return pltpu.make_async_copy(n1_ref.at[:, cols], n1_s.at[slot], local_sem.at[2 + slot])

    own_rows = pl.ds(pl.multiple_of(place * rows, rows), rows)
    fetches = [
        pltpu.make_async_copy(source.at[own_rows], target, local_sem.at[4 + index])
        for index, (source, target) in enumerate(
            ((mixed_hbm, mixed_ref), (mlp_hbm, mlp_ref), (x_hbm, x_ref))
        )
    ]
    nexts = [
        pltpu.make_async_copy(mlp_hbm.at[span(place + shift, rows)], mlp_next.at[at], local_sem.at[7 + at])
        for at, shift in enumerate((1, -1))
    ]
    for copy in (*nexts, *fetches):
        copy.start()
    for at in range(2):
        normed_copy(at, at).start()
    swaps = scatter_swap(keys_of, core_got)
    last_sums = []
    for at, (held_part, device) in enumerate(((ahead_ref, right), (behind_ref, left))):
        nexts[at].wait()
        mlp_next[at] = add_low(mlp_next[at], held_part[...])
        last_sums.append(go(mlp_next.at[at], out_got.at[at], device))
    cat_ref[:, pl.ds(0, size)] = dq_ref[...]
    cat_ref[:, pl.ds(size, size)] = dg_ref[...]
    for copy in fetches:
        copy.wait()

    @pl.loop(0, width // tile)
    def _(at):
        cols = pl.ds(pl.multiple_of(at * tile, tile), tile)
        wout_s[:, cols] = rows_inner(mixed_ref[...], low_ref[:, cols]).astype(BF)

    tops, bottoms = [], []
    for copy, hop in zip(swaps, order):
        copy.wait_recv()
        spot = spots[hop]
        add_tiles(core_got.at[spot], core_got.at[spot], keys_of(2 * spot + core))
        bottoms.append(go(core_got.at[spot, bottom, given], y_first.at[spot], mate))
        if hop:
            tops.append(go(core_got.at[spot, top], x_first.at[hop - 1], peers[hop]))
    wouts = scatter_swap(wout_view, wout_twin)
    for copy in last_sums:
        copy.wait_recv()
    out_s[...] = (
        h1_ref[...] + mlp_ref[...].astype(F32) + out_got[0].astype(F32) + out_got[1].astype(F32)
    ).astype(BF)
    keep_out = pltpu.make_async_copy(out_s, out_all.at[place], local_sem.at[0])
    keep_out.start()
    outs = gather(out_s, out_all, 0, None)
    total = core_got[across, top].astype(F32)
    for hop, copy in enumerate(tops):
        copy.wait_recv()
        total = total + x_first[hop].astype(F32)
    held[...] = total.astype(BF)
    last = go(held.at[:, given], y_second, mate)
    ends = []
    for copy, hop in zip(bottoms, order):
        copy.wait_recv()
        spot = spots[hop]
        y_first[spot] = add_low(y_first[spot], core_got[spot, bottom, mine])
        if hop:
            ends.append(go(y_first.at[spot], x_second.at[hop - 1], peers[hop]))
    last.wait_recv()
    cat_ref[top, fresh] = add_low(held[:, mine], y_second[...])
    total = y_first[across].astype(F32)
    for hop, copy in enumerate(ends):
        copy.wait_recv()
        total = total + x_second[hop].astype(F32)
    cat_ref[bottom, fresh] = total.astype(BF)

    compute(place + steps)
    sums = reduce(part_ref, got, 0, None)
    outs = gather(out_s, out_all, 1, outs)

    @pl.loop(1, count)
    def _(hop):
        compute(place + steps + hop)

    @pl.loop(0, width // tile)
    def _(at):
        slot = lax.rem(at, 2)
        normed_copy(at, slot).wait()
        cols = pl.ds(pl.multiple_of(at * tile, tile), tile)
        din_s[cols] = rows_inner(n1_s[slot], cat_ref[...]).astype(BF)

        @pl.when(at + 2 < width // tile)
        def _():
            normed_copy(at + 2, slot).start()

    dins = scatter_swap(din_view, din_got)
    for step in range(1, steps):
        sums = reduce(part_ref, got, step, sums)
        if 2 <= step < steps - 1:
            outs = gather(out_s, out_all, step, outs)
        if step == 1:
            wouts = scatter_cross(wout_view, wout_twin, wout_x, wouts)
            dins = scatter_cross(din_view, din_got, din_x, dins)
    for copy in sums:
        copy.wait_recv()

    def tile_of(at):
        return pl.ds(pl.multiple_of(at * tile, tile), tile)

    def total(cols):
        return (
            part_ref[span(place, rows), cols].astype(F32)
            + got[0, steps - 1, :, cols].astype(F32)
            + got[1, steps - 1, :, cols].astype(F32)
        )

    def collect(at, state):
        squares, mean = state
        cols = tile_of(at)
        x = x_ref[:, cols].astype(F32)
        squares = squares + jnp.sum(x * x, axis=1, keepdims=True)
        return squares, mean + jnp.sum(gain_ref[:, cols] * total(cols) * x, axis=1, keepdims=True)

    zero = jnp.zeros((rows, 1), F32)
    squares, mean = lax.fori_loop(0, width // tile, collect, (zero, zero))
    scale = lax.rsqrt(squares / width + EPSILON)
    pull = scale * scale * scale * (mean / width)

    @pl.loop(0, width // tile)
    def _(at):
        cols = tile_of(at)
        x, dn1 = x_ref[:, cols].astype(F32), total(cols)
        gain_own[pl.ds(0, 1), cols] = jnp.sum(dn1 * x * scale, axis=0, keepdims=True)
        gain_own[pl.ds(1, 1), cols] = second_ref[:, cols]
        tok_ref[:, cols] = (dh1_ref[:, cols] + scale * (gain_ref[:, cols] * dn1) - x * pull).astype(BF)

    keep_tok = pltpu.make_async_copy(tok_ref, tok_all.at[place], local_sem.at[1])
    keep_tok.start()
    toks = gather(tok_ref, tok_all, 0, None)
    outs = gather(out_s, out_all, steps - 1, outs)
    wout_part = wout_twin.at[across]
    scatter_end(wout_twin, wout_x, wouts, wout_part)
    wsums = reduce(wout_part, wout_got, 0, None)
    scatter_end(din_got, din_x, dins, din_ref)
    narrow = din_ref[:, pl.ds(2 * size, size)].T
    key_ref[...] = narrow[: size // 2]
    value_ref[...] = narrow[size // 2 :]
    wide = width // batches

    def slice_of(at):
        return pl.ds(pl.multiple_of(at * wide, wide), wide)

    gains = [
        go(gain_own.at[:, slice_of(other)], gain_got.at[hop], (other, head))
        for hop, other in enumerate(others)
    ]
    toks = gather(tok_ref, tok_all, 1, toks)
    wsums = reduce(wout_part, wout_got, 1, wsums)
    middle = gain_own[:, slice_of(batch)]
    for hop, copy in enumerate(gains):
        copy.wait_recv()
        middle = middle + gain_got[hop]
    gain_mid[...] = middle
    gain_heads[place] = middle
    gains = [go(gain_mid, gain_heads.at[place], member) for member in members]
    for step in range(2, steps):
        toks = gather(tok_ref, tok_all, step, toks)
        wsums = reduce(wout_part, wout_got, step, wsums)
    for copy in gains:
        copy.wait_recv()
    middle = gain_heads[0]
    for at in range(1, count):
        middle = middle + gain_heads[at]
    gains_ref[...] = middle
    for copy in (*wsums, *outs):
        copy.wait_recv()
    wout_own[...] = (
        wout_part[span(place, wout_own.shape[0])].astype(F32)
        + wout_got[0, steps - 1].astype(F32)
        + wout_got[1, steps - 1].astype(F32)
    )
    for copy in toks:
        copy.wait_recv()
    for copy in copies:
        copy.wait_send()
    keep_out.wait()
    keep_tok.wait()


def tail(arrays, collective_id):
    d_queries, tokens, mixed = arrays[0], arrays[-3], arrays[-2]
    count = lax.axis_size("head")
    batches = lax.axis_size("batch")
    steps = count // 2
    rows, width = tokens.shape[0] // count, tokens.shape[1]
    others = batches // 2
    size, wide = mixed.shape[1] // count, width // batches
    tall, head_size = d_queries.shape
    depth = 3 * head_size
    vmem = pl.BlockSpec(memory_space=pltpu.VMEM)
    hbm = pl.BlockSpec(memory_space=pl.ANY)
    whole = (count, rows, width)
    sems = pltpu.SemaphoreType.DMA((6 * count + 6 * batches,))
    gains = (2, width // batches)
    return pl.pallas_call(
        functools.partial(tail_kernel, count, batches),
        out_shape=[
            jax.ShapeDtypeStruct(whole, BF),
            jax.ShapeDtypeStruct(whole, BF),
            jax.ShapeDtypeStruct(gains, F32),
            jax.ShapeDtypeStruct((size, wide), F32),
            jax.ShapeDtypeStruct((wide, depth), F32),
            jax.ShapeDtypeStruct((size // 2, wide), F32),
            jax.ShapeDtypeStruct((size // 2, wide), F32),
        ],
        in_specs=[vmem] * 11 + [hbm] * 4,
        out_specs=[hbm] * 2 + [vmem] * 5,
        scratch_shapes=[
            pltpu.VMEM((count * rows, width), BF),
            pltpu.VMEM((rows, width), BF),
            pltpu.VMEM((2, steps, rows, width), BF),
            pltpu.VMEM((2, steps, size, wide), BF),
            pltpu.VMEM((2, width), F32),
            pltpu.VMEM((batches - 1, *gains), F32),
            pltpu.VMEM(gains, F32),
            pltpu.VMEM((count, *gains), F32),
            pltpu.VMEM((width, depth), BF),
            pltpu.VMEM((others, wide, depth), BF),
            pltpu.VMEM((others - 1, wide, depth), BF),
            pltpu.VMEM((count * size, width), BF),
            pltpu.VMEM((others, count * size, wide), BF),
            pltpu.VMEM((others - 1, count * size, wide), BF),
            pltpu.VMEM((tall, depth), BF),
            pltpu.VMEM((rows, width), BF),
            pltpu.VMEM((2, rows, width), BF),
            pltpu.VMEM((others, tall, 2 * head_size), BF),
            pltpu.VMEM((others - 1, tall // 2, 2 * head_size), BF),
            pltpu.VMEM((others - 1, tall // 2, head_size), BF),
            pltpu.VMEM((others, tall // 2, head_size), BF),
            pltpu.VMEM((tall // 2, head_size), BF),
            pltpu.VMEM((tall // 2, 2 * head_size), BF),
            pltpu.VMEM((2, tall, 256), BF),
            pltpu.VMEM((rows, width), BF),
            pltpu.VMEM((rows, mixed.shape[1]), BF),
            pltpu.VMEM((rows, width), BF),
            pltpu.VMEM((2, rows, width), BF),
            sems,
            sems,
            pltpu.SemaphoreType.DMA((9,)),
        ],
        compiler_params=pltpu.CompilerParams(
            collective_id=collective_id, has_side_effects=True, vmem_limit_bytes=VMEM_LIMIT
        ),
        cost_estimate=pl.CostEstimate(
            flops=4 * count * rows * width * depth, bytes_accessed=400 << 20, transcendentals=0
        ),
        name="tail",
    )(*arrays)


def finish_kernel(
    out_hbm, tok_hbm, mlp_ref, down_ref, in_ref, gains_ref, key_ref, value_ref, wout_ref,
    output, d_tokens, mgate, mup, down, query, gate, first, second, key, value, wout, sem,
):
    count, rows = out_hbm.shape[:2]
    moves = [
        pltpu.make_async_copy(source.at[at], target.at[pl.ds(at * rows, rows)], sem.at[index * count + at])
        for index, (source, target) in enumerate(((out_hbm, output), (tok_hbm, d_tokens)))
        for at in range(count)
    ]
    for copy in moves:
        copy.start()
    hidden = mgate.shape[1]
    size = query.shape[1]

    def convert(target, source, start):
        tall = 32

        @pl.loop(0, target.shape[0] // tall)
        def _(at):
            lines = pl.ds(pl.multiple_of(at * tall, tall), tall)
            target[lines] = source[lines, pl.ds(start, target.shape[1])].astype(target.dtype)

    convert(mgate, mlp_ref, 0)
    convert(mup, mlp_ref, hidden)
    convert(down, down_ref, 0)
    convert(query, in_ref, 0)
    convert(gate, in_ref, size)
    key[...] = key_ref[...]
    value[...] = value_ref[...]
    wout[...] = wout_ref[...]
    first[...] = gains_ref[pl.ds(0, 1)]
    second[...] = gains_ref[pl.ds(1, 1)]
    for copy in moves:
        copy.wait()


def finish(output, d_tokens, d_mlp, d_down, d_in, gains, *rest):
    count, rows, width = output.shape
    tall, hidden = d_mlp.shape[0], d_mlp.shape[1] // 2
    down_rows, wide = d_down.shape
    size = d_in.shape[1] // 3
    vmem = pl.BlockSpec(memory_space=pltpu.VMEM)
    hbm = pl.BlockSpec(memory_space=pl.ANY)

    def shape(*extent, dtype=F32):
        return jax.ShapeDtypeStruct(extent, dtype)

    return pl.pallas_call(
        finish_kernel,
        out_shape=[
            shape(count * rows, width, dtype=BF), shape(count * rows, width, dtype=BF),
            shape(tall, hidden), shape(tall, hidden), shape(down_rows, wide),
            shape(tall, size), shape(tall, size),
            shape(1, wide), shape(1, wide), *[shape(*a.shape) for a in rest],
        ],
        in_specs=[hbm] * 2 + [vmem] * 7,
        out_specs=[hbm] * 2 + [vmem] * 10,
        scratch_shapes=[pltpu.SemaphoreType.DMA((2 * count,))],
        compiler_params=pltpu.CompilerParams(vmem_limit_bytes=VMEM_LIMIT),
        name="finish",
    )(output, d_tokens, d_mlp, d_down, d_in, gains, *rest)


def local_call(kernel, scalars, arrays, outs, scratch, flops, name):
    vmem = pl.BlockSpec(memory_space=pltpu.VMEM)
    smem = pl.BlockSpec(memory_space=pltpu.SMEM)
    return pl.pallas_call(
        kernel,
        out_shape=outs,
        in_specs=[smem] * len(scalars) + [vmem] * len(arrays),
        out_specs=[vmem] * len(outs),
        scratch_shapes=scratch,
        compiler_params=pltpu.CompilerParams(vmem_limit_bytes=VMEM_LIMIT),
        cost_estimate=pl.CostEstimate(flops=flops, bytes_accessed=8 << 20, transcendentals=0),
        name=name,
    )(*scalars, *arrays)


def ring_routes(count):
    spots = [ring_head(at, count) for at in range(count)]
    right = [(spots[at], spots[(at + 1) % count]) for at in range(count)]
    left = [(spots[at], spots[at - 1]) for at in range(count)]
    return right, left


def add_low(one, other):
    return (one.astype(F32) + other.astype(F32)).astype(BF)


def flow_steps(part, going, coming):
    count = lax.axis_size("head")
    place = ring_place(lax.axis_index("head"), count)
    right, left = ring_routes(count)
    rows = part.shape[0] // count
    steps = count // 2

    def mine(owner):
        return lax.dynamic_slice_in_dim(part, lax.rem(owner + count, count) * rows, rows, 0)

    for step in range(2, steps - 1):
        going = lax.ppermute(going, "head", right)
        coming = lax.ppermute(coming, "head", left)
        if step < steps - 2:
            going = add_low(going, mine(place + steps - 1 - step))
            coming = add_low(coming, mine(place - steps + 1 + step))
    return going, coming


def matmul(left, right):
    return jnp.dot(left, right, preferred_element_type=F32)


def rows_inner(left, right):
    return lax.dot_general(left, right, (((0,), (0,)), ((), ())), preferred_element_type=F32)


def cols_inner(left, right):
    return lax.dot_general(left, right, (((1,), (1,)), ((), ())), preferred_element_type=F32)


def rms_scale(values):
    return lax.rsqrt(jnp.mean(values * values, axis=1, keepdims=True) + EPSILON)


def per_device(
    tokens,
    segment_ids,
    norm1_gain,
    w_query,
    w_key,
    w_value,
    w_gate,
    w_out,
    norm2_gain,
    w_mlp_gate,
    w_mlp_up,
    w_down,
    out_grad,
):
    heads = lax.axis_size("head")
    batches = lax.axis_size("batch")
    row_count, width = tokens.shape
    head_size = w_query.shape[1]
    half = w_key.shape[1]
    chunk = row_count // heads
    me = ring_place(lax.axis_index("head"), heads)
    scale_factor = 1.0 / math.sqrt(head_size)

    w_shard = jnp.concatenate([w_query, w_gate, w_key, w_value], axis=1)
    gains = jnp.concatenate([norm1_gain, norm2_gain]).reshape(-1, 128).astype(F32)
    normed_one, queries, gate_logit, kv_all, w_in, out_full, gains, seg_all, down_top = entry(
        tokens, w_shard, w_out, gains, segment_ids.reshape(-1, 128), w_down, 1
    )
    gains, w_mlp_gate = lax.optimization_barrier((gains, w_mlp_gate))
    seg_all = seg_all.reshape(-1)
    gains = gains.reshape(batches, 2, -1).transpose(1, 0, 2).reshape(2, width)
    gain_one, gain_two = gains[0], gains[1]
    mgate_full = lax.all_gather(w_mlp_gate, "batch", axis=0, tiled=True)

    base = lax.axis_index("batch") * row_count
    ids = jnp.arange(DOCUMENTS, dtype=jnp.int32)
    below = jnp.sum((seg_all[None, :] < ids[:, None]).astype(jnp.int32), axis=1)
    starts = jnp.sum(jnp.where(segment_ids[None, :] == ids[:, None], below[:, None], 0), axis=0)
    scalars = (starts, base.reshape(1))
    pair_flops = 4 * row_count * kv_all.shape[0] * head_size
    attended, mixed, lse = local_call(
        functools.partial(attend_kernel, scale_factor),
        scalars,
        (queries, kv_all, starts[None], gate_logit),
        [
            jax.ShapeDtypeStruct((row_count, head_size), F32),
            jax.ShapeDtypeStruct((row_count, head_size), BF),
            jax.ShapeDtypeStruct((1, row_count), F32),
        ],
        [],
        pair_flops,
        "attend",
    )
    mixed_all, down_low, mup_full = spread(
        [mixed, w_down, w_mlp_up], (("head", "cols"), ("batch", "low"), ("batch", "rows")), 2
    )
    (
        mlp_part, d_mlp, d_down, resid_own, d_resid, d_resid_low, d_gain_two, d_mixed, going, coming,
    ) = mlp_back(
        tokens, mixed_all, out_grad, gain_two[None], out_full, mgate_full, mup_full, down_top, down_low, 3
    )
    hold = lax.optimization_barrier
    state = flow_steps(mlp_part, going, coming)

    d_queries, d_gate_logit, d_kv_all = local_call(
        functools.partial(attend_back_kernel, scale_factor),
        scalars,
        (queries, kv_all, starts[None], gate_logit, attended, d_mixed, lse),
        [
            jax.ShapeDtypeStruct((row_count, head_size), BF),
            jax.ShapeDtypeStruct((row_count, head_size), BF),
            jax.ShapeDtypeStruct(kv_all.shape, BF),
        ],
        [pltpu.VMEM((kv_all.shape[0], head_size), F32)] * 2,
        5 * pair_flops // 2,
        "attend_back",
    )
    d_down = lax.psum_scatter(d_down, "batch", scatter_dimension=1, tiled=True)
    d_mlp = lax.psum_scatter(d_mlp, "batch", scatter_dimension=0, tiled=True)
    output, d_tokens, d_gains, d_out, d_in, d_key, d_value = tail(
        (
            d_queries, d_gate_logit, d_kv_all, w_in, gain_one[None], d_resid, d_gain_two,
            d_resid_low, resid_own, *state, normed_one, tokens, mixed_all, mlp_part,
        ),
        5,
    )
    (
        output, d_tokens, d_mgate, d_mup, d_down, d_query, d_gate, d_one, d_two,
        d_key, d_value, d_out,
    ) = finish(output, d_tokens, d_mlp, d_down, d_in, d_gains, d_key, d_value, d_out)
    return (
        output,
        d_tokens,
        d_one.reshape(-1),
        d_query,
        d_key.T,
        d_value.T,
        d_gate,
        d_out,
        d_two.reshape(-1),
        d_mgate,
        d_mup,
        d_down,
    )


def solution(mesh):
    return jax.shard_map(
        per_device,
        mesh=mesh,
        in_specs=(
            P("batch", None),
            P("batch"),
            P("batch"),
            P("batch", "head"),
            P("batch", "head"),
            P("batch", "head"),
            P("batch", "head"),
            P("head", "batch"),
            P("batch"),
            P("batch", "head"),
            P("batch", "head"),
            P("head", "batch"),
            P("batch", None),
        ),
        out_specs=(
            P("batch", None),
            P("batch", None),
            P("batch"),
            P("batch", "head"),
            P("batch", "head"),
            P("batch", "head"),
            P("batch", "head"),
            P("head", "batch"),
            P("batch"),
            P("batch", "head"),
            P("batch", "head"),
            P("head", "batch"),
        ),
        check_vma=False,
    )
```

```python
import functools
import math

import jax
import jax.numpy as jnp
from jax import lax
from jax.experimental import pallas as pl
from jax.experimental.pallas import tpu as pltpu
from jax.sharding import PartitionSpec as P

EPSILON = 1e-06
MASKED = -1e30
DOCUMENTS = 7
BF = jnp.bfloat16
F32 = jnp.float32


MESH = pl.DeviceIdType.MESH
VMEM_LIMIT = 60 << 20


def ring_place(head, count):
    high, low = head // 2, head % 2
    return (1 - low) * high + low * (count - 1 - high)


def ring_head(place, count):
    low = place // (count // 2)
    high = (1 - low) * place + low * (count - 1 - place)
    return 2 * high + low


def ring_setup(count):
    batch = lax.axis_index("batch")
    place = ring_place(lax.axis_index("head"), count)
    right = (batch, ring_head(lax.rem(place + 1, count), count))
    left = (batch, ring_head(lax.rem(place + count - 1, count), count))
    return place, right, left


def greet(devices):
    barrier = pltpu.get_barrier_semaphore()
    for device in devices:
        pl.semaphore_signal(barrier, inc=1, device_id=device, device_id_type=MESH)
    pl.semaphore_wait(barrier, len(devices))


def send(source, target, sems, slot, device):
    copy = pltpu.make_async_remote_copy(
        src_ref=source,
        dst_ref=target,
        send_sem=sems[0].at[slot],
        recv_sem=sems[1].at[slot],
        device_id=device,
        device_id_type=MESH,
    )
    copy.start()
    return copy


def half_of(extent, flow):
    if extent[1] % 256:
        return (pl.ds(flow * (extent[0] // 2), extent[0] // 2), slice(None))
    return (slice(None), pl.ds(flow * (extent[1] // 2), extent[1] // 2))


def place_of(whole, own, chunk, form):
    rows, wide = own.shape[-2:]
    if form == "lead":
        return whole.at[chunk]
    if form == "rows":
        return whole.at[pl.ds(pl.multiple_of(chunk * rows, rows), rows)]
    return whole.at[:, pl.ds(pl.multiple_of(chunk * wide, wide), wide)]


def spread_kernel(count, batches, plans, *refs):
    steps = count // 2
    arrays = len(plans)
    own_refs, all_refs = list(refs[:arrays]), refs[arrays : 2 * arrays]
    for index, (_, form) in enumerate(plans):
        if form == "low":
            half = own_refs[index].shape[0] // 2
            own_refs[index] = own_refs[index].at[pl.ds(half, half)]
    send_sem, recv_sem, local_sem = refs[2 * arrays :]
    place, right, left = ring_setup(count)
    head = lax.axis_index("head")
    batch = lax.axis_index("batch")
    across, core = batch // 2, lax.rem(batch, 2)
    others = batches // 2
    twin = (across * 2 + 1 - core, head)
    peers = [(lax.rem(across + hop, others) * 2 + core, head) for hop in range(1, others)]
    ring = any(axis == "head" for axis, _ in plans)
    grid = any(axis == "batch" for axis, _ in plans)
    greet((right, left) * ring + (twin, *peers) * grid)
    sems = (send_sem, recv_sem)
    slot = 0
    waiting, arriving, local = [], [], []

    def go(source, target, device):
        nonlocal slot
        copy = send(source, target, sems, slot, device)
        slot += 1
        waiting.append(copy)
        return copy

    stages = []
    for index, (axis, form) in enumerate(plans):
        own, whole = own_refs[index], all_refs[index]
        spot = place if axis == "head" else batch
        copy = pltpu.make_async_copy(own, place_of(whole, own, spot, form), local_sem.at[index])
        copy.start()
        local.append(copy)
        if axis == "batch":
            stages.append(index)
    onward = []

    def stage():
        for copy, block in onward:
            copy.wait_recv()
            arriving.append(go(block, block, twin))
        onward.clear()
        if stages:
            index = stages.pop(0)
            own, whole, form = own_refs[index], all_refs[index], plans[index][1]
            mine = place_of(whole, own, batch, form)
            for hop, peer in enumerate(peers, 1):
                source = lax.rem(across + others - hop, others) * 2 + core
                onward.append((go(own, mine, peer), place_of(whole, own, source, form)))
            arriving.append(go(own, mine, twin))

    stage()
    copies = [None] * (2 * arrays)
    for step in range(steps):
        for index, (axis, form) in enumerate(plans):
            if axis != "head":
                continue
            own = own_refs[index]
            for flow, chunk, device in ((0, place - step, right), (1, place + step, left)):
                at = 2 * index + flow
                if step:
                    copies[at].wait_recv()
                chunk = lax.rem(chunk + count, count)
                target = place_of(all_refs[index], own, chunk, form)
                source = target if step else own
                if step == steps - 1:
                    part = half_of(own.shape, flow)
                    source = source.at[part]
                    target = target.at[part]
                copies[at] = go(source, target, device)
        if step == steps // 2:
            stage()
    while stages or onward:
        stage()
    for copy in copies:
        if copy is not None:
            arriving.append(copy)
    for copy in arriving:
        copy.wait_recv()
    for copy in waiting:
        copy.wait_send()
    for copy in local:
        copy.wait()


def spread(arrays, plans, collective_id):
    count = lax.axis_size("head")
    batches = lax.axis_size("batch")
    shapes = []
    slots = 0
    for array, (axis, form) in zip(arrays, plans):
        many = count if axis == "head" else batches
        slots += count if axis == "head" else batches - 1
        if form == "lead":
            shapes.append((many, *array.shape))
        elif form == "rows":
            shapes.append((many * array.shape[0], array.shape[1]))
        else:
            tall = array.shape[0] // (2 if form == "low" else 1)
            shapes.append((tall, many * array.shape[1]))
    hbm = pl.BlockSpec(memory_space=pl.ANY)
    return pl.pallas_call(
        functools.partial(spread_kernel, count, batches, plans),
        out_shape=[jax.ShapeDtypeStruct(shape, a.dtype) for shape, a in zip(shapes, arrays)],
        in_specs=[pl.BlockSpec(memory_space=pltpu.VMEM)] * len(arrays),
        out_specs=[hbm] * len(arrays),
        scratch_shapes=[
            pltpu.SemaphoreType.DMA((slots,)),
            pltpu.SemaphoreType.DMA((slots,)),
            pltpu.SemaphoreType.DMA((len(arrays),)),
        ],
        compiler_params=pltpu.CompilerParams(
            collective_id=collective_id, has_side_effects=True, vmem_limit_bytes=VMEM_LIMIT
        ),
        name=f"spread_{collective_id}",
    )(*arrays)


def mlp_kernel(
    count, x_hbm, a_hbm, dy_hbm, gain_ref, out_hbm, gate_hbm, up_hbm, top_hbm, low_hbm,
    mlp_hbm, dmlp_hbm, ddown_hbm, h1_ref, dh1_ref, low_ref, dgain_ref, da_ref, ahead_ref, behind_ref,
    x_s, a_s, mlp_s, h1_s, dy_all, n2_all, hid_all, grad_all, dmlp_s, ddown_s, da_part,
    mlp_far, mlp_next, mlp_got, right_part, left_part, right_got, left_got,
    out_w, gate_w, up_w, down_w, in_sem, out_sem, grad_sem, weight_sem,
    send_sem, recv_sem, da_send, da_recv, far_send, far_recv,
):
    steps = count // 2
    rows = x_hbm.shape[0] // count
    width = x_hbm.shape[1]
    hidden = gate_w.shape[1]
    middle = hidden // 2
    weights = [
        pltpu.make_async_copy(source, target, weight_sem.at[index])
        for index, (source, target) in enumerate(
            (
                (out_hbm, out_w), (gate_hbm, gate_w), (up_hbm, up_w),
                (top_hbm, down_w.at[pl.ds(0, middle)]), (low_hbm, down_w.at[pl.ds(middle, middle)]),
            )
        )
    ]
    side = width // 2
    tile = 256
    broad = 1024
    inner = 256 if hidden % 256 == 0 else 128
    size = da_ref.shape[1]
    place, right, left = ring_setup(count)

    def member(hop):
        spot = lax.rem(place + hop, count)
        return spot, (lax.axis_index("batch"), ring_head(spot, count))

    def owners(group):
        first = jnp.where(group == 0, 1, 0)
        one = lax.rem(place + steps - group, count)
        two = lax.rem(place - steps + group + first * steps + count, count)
        return one, two

    def span(owner):
        return pl.ds(pl.multiple_of(owner * rows, rows), rows)

    def tile_of(at, extent=tile):
        return pl.ds(pl.multiple_of(at * extent, extent), extent)

    def loads(group, slot):
        return [
            pltpu.make_async_copy(
                source.at[span(owner)],
                target.at[pl.ds(at * rows, rows)],
                in_sem.at[slot, 2 * index + at],
            )
            for index, (source, target) in enumerate(
                ((x_hbm, x_s.at[slot]), (a_hbm, a_s.at[slot]), (dy_hbm, dy_all.at[group]))
            )
            for at, owner in enumerate(owners(group))
        ]

    def stores(group, slot):
        return [
            pltpu.make_async_copy(
                mlp_s.at[slot, pl.ds(at * rows, rows)], mlp_hbm.at[span(owner)], out_sem.at[slot, at]
            )
            for at, owner in enumerate(owners(group))
        ]

    def passing(source, target, sems, slot, device):
        return pltpu.make_async_remote_copy(
            src_ref=source,
            dst_ref=target,
            send_sem=sems[0].at[slot],
            recv_sem=sems[1].at[slot],
            device_id=device,
            device_id_type=MESH,
        )

    ring_sems, far_sems = (send_sem, recv_sem), (far_send, far_recv)
    ahead, behind = pl.ds(0, side), pl.ds(side, side)

    def first_copies():
        return (
            passing(right_part.at[0, :, ahead], right_got.at[0, :, ahead], ring_sems, 0, right),
            passing(right_part.at[0, :, behind], left_got.at[0, :, behind], ring_sems, steps, left),
        )

    def later_copies(step):
        return (
            passing(right_got.at[step - 1], right_got.at[step], ring_sems, step, right),
            passing(left_got.at[step - 1], left_got.at[step], ring_sems, steps + step, left),
        )

    for copy in (*loads(0, 0), *weights):
        copy.start()
    greet([member(hop)[1] for hop in range(1, count)])
    weights[0].wait()

    @pl.loop(0, steps)
    def _(group):
        slot = lax.rem(group, 2)
        for copy in loads(group, slot):
            copy.wait()

        @pl.when(group + 1 < steps)
        def _():
            for copy in loads(group + 1, 1 - slot):
                copy.start()

        @pl.when(group >= 2)
        def _():
            for copy in stores(group - 2, slot):
                copy.wait()

        mixed = a_s[slot]

        def residual(at, total):
            cols = tile_of(at, broad)
            values = x_s[slot, :, cols].astype(F32) + matmul(mixed, out_w[:, cols])
            h1_s[:, cols] = values
            return total + jnp.sum(values * values, axis=1, keepdims=True)

        total = lax.fori_loop(0, width // broad, residual, jnp.zeros((2 * rows, 1), F32))
        scale = lax.rsqrt(total / width + EPSILON)

        @pl.when(group == 0)
        def _():
            h1_ref[...] = h1_s[pl.ds(rows, rows)]
            for copy in weights[1:]:
                copy.wait()

        @pl.loop(0, width // tile)
        def _(at):
            cols = tile_of(at)
            n2_all[group, :, cols] = (h1_s[:, cols] * scale * gain_ref[:, cols]).astype(BF)

        normed = n2_all[group]
        dy = dy_all[group]

        @pl.loop(0, hidden // inner)
        def _(at):
            cols = tile_of(at, inner)
            cols_up = pl.ds(pl.multiple_of(hidden + at * inner, inner), inner)
            gate = matmul(normed, gate_w[:, cols])
            up = matmul(normed, up_w[:, cols])
            d_hidden = cols_inner(dy, down_w[cols])
            sig = jax.nn.sigmoid(gate)
            silu = gate * sig
            hid_all[group, :, cols] = (silu * up).astype(BF)
            grad_all[group, :, cols] = (d_hidden * up * sig * (1.0 + gate * (1.0 - sig))).astype(BF)
            grad_all[group, :, cols_up] = (d_hidden * silu).astype(BF)

        hid = hid_all[group]
        d_gate = grad_all[group, :, :hidden]
        d_up = grad_all[group, :, hidden:]
        half = jnp.minimum(group, 1)

        @pl.loop(0, width // broad)
        def _(at):
            cols = tile_of(at, broad)
            part = (cols_inner(d_gate, gate_w[cols]) + cols_inner(d_up, up_w[cols])).astype(BF)
            right_part[half, :, cols] = part[:rows]
            left_part[half, :, cols] = part[rows:]

        @pl.when(group == 0)
        def _():
            for copy in first_copies():
                copy.start()

        @pl.when(group == 1)
        def _():
            one, two = first_copies()
            one.wait_recv()
            right_got[0, :, ahead] = add_low(right_part[1, :, ahead], right_got[0, :, ahead])
            right_got[0, :, behind] = right_part[1, :, behind]
            two.wait_recv()
            left_got[0, :, behind] = add_low(left_part[1, :, behind], left_got[0, :, behind])
            left_got[0, :, ahead] = left_part[1, :, ahead]

        @pl.when(group >= 2)
        def _():
            one, two = later_copies(group - 1)
            one.wait_recv()
            right_got[group - 1] = add_low(right_part[1], right_got[group - 1])
            two.wait_recv()
            left_got[group - 1] = add_low(left_part[1], left_got[group - 1])

        @pl.when(group >= 1)
        def _():
            for copy in later_copies(group):
                copy.start()

        @pl.loop(0, width // broad)
        def _(at):
            cols = tile_of(at, broad)
            mlp_s[slot, :, cols] = matmul(hid, down_w[:, cols]).astype(BF)

        for copy in stores(group, slot):
            copy.start()

        @pl.when(group == 0)
        def _():
            mlp_far[...] = mlp_s[slot, pl.ds(0, rows)]

        @pl.when(group == 1)
        def _():
            mlp_next[0] = mlp_s[slot, pl.ds(0, rows)]
            mlp_next[1] = mlp_s[slot, pl.ds(rows, rows)]

        @pl.when(group == 2)
        def _():
            ahead_ref[...] = mlp_s[slot, pl.ds(0, rows)]
            behind_ref[...] = mlp_s[slot, pl.ds(rows, rows)]

    far_copies = [
        passing(mlp_far.at[:, ahead], mlp_got.at[0, :, ahead], far_sems, 0, right),
        passing(mlp_far.at[:, behind], mlp_got.at[1, :, behind], far_sems, 1, left),
    ]
    for copy in far_copies:
        copy.start()

    every = steps * 2 * rows

    def dmlp_copy(at, slot):
        return pltpu.make_async_copy(
            dmlp_s.at[slot], dmlp_hbm.at[tile_of(at // 2), tile_of(lax.rem(at, 2), hidden)], grad_sem.at[slot]
        )

    mlp_tiles = 2 * (width // tile)

    @pl.loop(0, mlp_tiles)
    def _(at):
        slot = lax.rem(at, 2)

        @pl.when(at >= 2)
        def _():
            dmlp_copy(at - 2, slot).wait()

        normed = n2_all[:, :, tile_of(at // 2)].reshape(every, tile)
        grads = grad_all[:, :, tile_of(lax.rem(at, 2), hidden)].reshape(every, hidden)
        dmlp_s[slot] = rows_inner(normed, grads).astype(BF)
        dmlp_copy(at, slot).start()

    wide = 512
    across = width // wide

    def ddown_copy(at, slot):
        return pltpu.make_async_copy(
            ddown_s.at[slot],
            ddown_hbm.at[tile_of(at // across, inner), tile_of(lax.rem(at, across), wide)],
            grad_sem.at[2 + slot],
        )

    down_tiles = across * (hidden // inner)

    @pl.loop(0, down_tiles)
    def _(at):
        slot = lax.rem(at, 2)

        @pl.when(at >= 2)
        def _():
            ddown_copy(at - 2, slot).wait()

        hid = hid_all[:, :, tile_of(at // across, inner)].reshape(every, inner)
        dy = dy_all[:, :, tile_of(lax.rem(at, across), wide)].reshape(every, wide)
        ddown_s[slot] = rows_inner(hid, dy).astype(BF)
        ddown_copy(at, slot).start()

    for copy in later_copies(steps - 1):
        copy.wait_recv()
    for flow, have, lack in ((0, ahead, behind), (1, behind, ahead)):
        far_copies[flow].wait_recv()
        mlp_got[flow, :, have] = add_low(mlp_got[flow, :, have], mlp_next[flow, :, have])
        mlp_got[flow, :, lack] = mlp_next[flow, :, lack]
    next_copies = [
        passing(mlp_got.at[0], mlp_got.at[2], far_sems, 2, right),
        passing(mlp_got.at[1], mlp_got.at[3], far_sems, 3, left),
    ]
    for copy in next_copies:
        copy.start()

    def collect(at, state):
        squares, mean = state
        cols = tile_of(at)
        dn2 = (
            left_part[0, :, cols].astype(F32)
            + right_got[steps - 1, :, cols].astype(F32)
            + left_got[steps - 1, :, cols].astype(F32)
        )
        dh1_ref[:, cols] = dn2
        h1 = h1_ref[:, cols]
        squares = squares + jnp.sum(h1 * h1, axis=1, keepdims=True)
        return squares, mean + jnp.sum(gain_ref[:, cols] * dn2 * h1, axis=1, keepdims=True)

    zero = jnp.zeros((rows, 1), F32)
    squares, mean = lax.fori_loop(0, width // tile, collect, (zero, zero))
    scale_own = lax.rsqrt(squares / width + EPSILON)
    pull = scale_own * scale_own * scale_own * (mean / width)

    @pl.loop(0, width // tile)
    def _(at):
        cols = tile_of(at)
        dn2, h1 = dh1_ref[:, cols], h1_ref[:, cols]
        dgain_ref[:, cols] = jnp.sum(dn2 * h1 * scale_own, axis=0, keepdims=True)
        dy = dy_all[0, pl.ds(rows, rows), cols].astype(F32)
        d_resid = dy + scale_own * (gain_ref[:, cols] * dn2) - h1 * pull
        dh1_ref[:, cols] = d_resid
        low_ref[:, cols] = d_resid.astype(BF)

    def da_copy(hop):
        return passing(
            da_part.at[hop], da_ref.at[span(place)], (da_send, da_recv), hop, member(hop)[1]
        )

    low = low_ref[...]

    @pl.loop(1, count)
    def _(hop):
        spot = member(hop)[0]
        da_part[hop] = cols_inner(low, out_w[tile_of(spot, size)]).astype(BF)
        da_copy(hop).start()

    da_ref[span(place)] = cols_inner(low, out_w[tile_of(place, size)]).astype(BF)

    @pl.loop(1, count)
    def _(hop):
        da_copy(hop).wait_recv()
        da_copy(hop).wait_send()

    for flow, held in ((0, ahead_ref), (1, behind_ref)):
        next_copies[flow].wait_recv()
        held[...] = add_low(held[...], mlp_got[2 + flow])
    for copy in (*far_copies, *next_copies, *first_copies()):
        copy.wait_send()
    for step in range(1, steps):
        for copy in later_copies(step):
            copy.wait_send()
    for group in range(steps - 2, steps):
        for copy in stores(group, group % 2):
            copy.wait()
    for at in range(2):
        dmlp_copy(mlp_tiles - 2 + at, (mlp_tiles + at) % 2).wait()
        ddown_copy(down_tiles - 2 + at, (down_tiles + at) % 2).wait()


def mlp_back(tokens, mixed, dy, gain, out_w, gate_w, up_w, down_top, down_low, collective_id):
    count = lax.axis_size("head")
    total, width = tokens.shape
    hidden = gate_w.shape[1]
    rows, steps = total // count, count // 2
    size = mixed.shape[1] // count
    inner = 256 if hidden % 256 == 0 else 128
    vmem = pl.BlockSpec(memory_space=pltpu.VMEM)
    hbm = pl.BlockSpec(memory_space=pl.ANY)

    def slots(many, tall, wide, dtype=BF):
        return pltpu.VMEM((many, tall, wide), dtype)

    def shape(*extent, dtype=BF):
        return jax.ShapeDtypeStruct(extent, dtype)

    dma = pltpu.SemaphoreType.DMA
    flops = 2 * total * width * (mixed.shape[1] + 9 * hidden)
    return pl.pallas_call(
        functools.partial(mlp_kernel, count),
        out_shape=[
            shape(total, width), shape(width, 2 * hidden), shape(hidden, width),
            shape(rows, width, dtype=F32), shape(rows, width, dtype=F32), shape(rows, width),
            shape(1, width, dtype=F32), shape(total, size), shape(rows, width), shape(rows, width),
        ],
        in_specs=[hbm] * 3 + [vmem] + [hbm] * 5,
        out_specs=[hbm] * 3 + [vmem] * 7,
        scratch_shapes=[
            slots(2, 2 * rows, width), slots(2, 2 * rows, mixed.shape[1]), slots(2, 2 * rows, width),
            pltpu.VMEM((2 * rows, width), F32),
            slots(steps, 2 * rows, width), slots(steps, 2 * rows, width),
            slots(steps, 2 * rows, hidden), slots(steps, 2 * rows, 2 * hidden),
            slots(2, 256, hidden), slots(2, inner, 512), slots(count, rows, size),
            pltpu.VMEM((rows, width), BF), slots(2, rows, width), slots(4, rows, width),
            slots(2, rows, width), slots(2, rows, width),
            slots(steps, rows, width), slots(steps, rows, width),
            *[pltpu.VMEM(weight.shape, BF) for weight in (out_w, gate_w, up_w)],
            pltpu.VMEM((hidden, width), BF),
            dma((2, 6)), dma((2, 2)), dma((4,)), dma((5,)), dma((count,)), dma((count,)),
            dma((count,)), dma((count,)), dma((4,)), dma((4,)),
        ],
        compiler_params=pltpu.CompilerParams(
            collective_id=collective_id, has_side_effects=True, vmem_limit_bytes=VMEM_LIMIT
        ),
        cost_estimate=pl.CostEstimate(flops=flops, bytes_accessed=40 << 20, transcendentals=0),
        name="mlp_back",
    )(tokens, mixed, dy, gain, out_w, gate_w, up_w, down_top, down_low)


def entry_kernel(
    count, batches, x_ref, w_ref, out_ref, gain_ref, seg_ref, down_ref,
    n1_hbm, q_ref, logit_ref, kv_ref, w_all, out_all, gain_all, seg_all, down_all,
    x_s, n1_ref, send_sem, recv_sem, local_sem, x_sem, n1_sem,
):
    steps = count // 2
    others = batches // 2
    rows, width = x_ref.shape
    depth = w_ref.shape[0]
    size, wide = out_ref.shape
    block = 256
    blocks = rows // block

    def x_copy(at):
        here = pl.ds(pl.multiple_of(at * block, block), block)
        return pltpu.make_async_copy(x_ref.at[here], x_s.at[here], x_sem.at[at])

    def n1_copy(at):
        here = pl.ds(pl.multiple_of(at * block, block), block)
        return pltpu.make_async_copy(n1_ref.at[here], n1_hbm.at[here], n1_sem.at[at])

    for at in range(blocks):
        x_copy(at).start()
    place, right, left = ring_setup(count)
    head = lax.axis_index("head")
    batch = lax.axis_index("batch")
    across, core, low = batch // 2, lax.rem(batch, 2), lax.rem(head, 2)
    twin = (across * 2 + 1 - core, head)
    mate = (batch, head + 1 - 2 * low)
    spots = [lax.rem(across + hop, others) for hop in range(others)]
    backs = [lax.rem(across + others - hop, others) for hop in range(others)]
    peers = [(spot * 2 + core, head) for spot in spots]
    far_peers = [(spot * 2 + 1 - core, head) for spot in spots]
    greet((twin, mate, right, left, *peers[1:], *far_peers[1:]))
    sems = (send_sem, recv_sem)
    slot = 0
    copies = []

    def go(source, target, device):
        nonlocal slot
        copy = send(source, target, sems, slot, device)
        slot += 1
        copies.append(copy)
        return copy

    def part(at, extent):
        return pl.ds(pl.multiple_of(at * extent, extent), extent)

    def both(view, own):
        out = [go(own, view(batch), peers[hop]) for hop in range(1, others)]
        return out, [go(own, view(batch), twin)]

    def pass_on(view, arrived):
        out = []
        for hop in range(1, others):
            arrived[hop - 1].wait_recv()
            there = view(backs[hop] * 2 + core)
            out.append(go(there, there, twin))
        return out

    local = []

    def stay(source, target):
        copy = pltpu.make_async_copy(source, target, local_sem.at[len(local)])
        copy.start()
        local.append(copy)

    def main_view(at):
        return w_all.at[part(at, depth), pl.ds(0, 3 * size)]

    def mate_view(at):
        return w_all.at[part(at, depth), pl.ds(3 * size, size)]

    def out_view(chunk, at):
        return out_all.at[part(chunk, size), part(at, wide)]

    small = []
    for own, whole in ((gain_ref, gain_all), (seg_ref, seg_all)):
        for device in (twin, *peers[1:], *far_peers[1:]):
            small.append(go(own, whole.at[batch], device))
        stay(own, whole.at[batch])
    from_mate = go(w_ref.at[:, pl.ds(2 * size, size)], mate_view(batch), mate)
    main_out, main_twin = both(main_view, w_ref)
    stay(w_ref, main_view(batch))
    out_peers = [go(out_ref, out_view(place, batch), peers[hop]) for hop in range(1, others)]
    stay(out_ref, out_view(place, batch))
    flows = [[None, None] for _ in range(others)]

    def ring(step):
        for hop in range(others):
            lane = spots[0] if hop == 0 else backs[hop]
            at = lane * 2 + core
            if step == 0 and hop:
                out_peers[hop - 1].wait_recv()
            for flow, chunk, device in ((0, place - step, right), (1, place + step, left)):
                if step:
                    flows[hop][flow].wait_recv()
                target = out_view(lax.rem(chunk + count, count), at)
                source = out_ref if step == 0 and hop == 0 else target
                if step == steps - 1:
                    cut = (pl.ds(flow * (size // 2), size // 2), slice(None))
                    source, target = source.at[cut], target.at[cut]
                flows[hop][flow] = go(source, target, device)

    for copy in small:
        copy.wait_recv()
    for copy in local[:2]:
        copy.wait()

    def normalize(at):
        here = part(at, block)
        x_copy(at).wait()

        def squares(tile, total):
            values = x_s[here, part(tile, 256)].astype(F32)
            return total + jnp.sum(values * values, axis=1, keepdims=True)

        total = lax.fori_loop(0, width // 256, squares, jnp.zeros((block, 1), F32))
        scale = lax.rsqrt(total / width + EPSILON)

        @pl.loop(0, batches)
        def _(owner):
            for tile in range(depth // 128):
                cols = pl.ds(pl.multiple_of(owner * depth + tile * 128, 128), 128)
                values = x_s[here, cols].astype(F32) * scale
                n1_ref[here, cols] = (values * gain_all[owner, pl.ds(tile, 1)]).astype(BF)

        n1_copy(at).start()

    middle = blocks // 2

    @pl.loop(0, middle)
    def _(at):
        normalize(at)

    from_mate.wait_recv()
    mate_out, mate_twin = both(mate_view, mate_view(batch))
    ring(0)

    def down_view(at):
        return down_all.at[:, part(at, down_ref.shape[1])]

    down_own = down_ref.at[pl.ds(0, down_ref.shape[0] // 2)]
    down_out, down_twin = both(down_view, down_own)
    stay(down_own, down_view(batch))

    @pl.loop(middle, blocks)
    def _(at):
        normalize(at)

    main_passed = pass_on(main_view, main_out)
    mate_passed = pass_on(mate_view, mate_out)
    for copy in (*main_twin, *mate_twin, *main_passed, *mate_passed):
        copy.wait_recv()
    for copy in local[2:]:
        copy.wait()

    def kv_view(at):
        return kv_ref.at[part(at, rows)]

    @pl.loop(0, blocks)
    def _(at):
        here = part(at, block)
        values = matmul(n1_ref[here], w_all[:, pl.ds(2 * size, 2 * size)])
        one, two = values[:, :size], values[:, size:]
        first = jnp.where(low == 0, one, two).astype(BF)
        second = jnp.where(low == 0, two, one).astype(BF)
        half = size // 2
        there = pl.ds(pl.multiple_of(batch * rows + at * block, block), block)
        kv_ref[there, pl.ds(0, size)] = jnp.concatenate([first[:, :half], second[:, :half]], 1)
        kv_ref[there, pl.ds(size, size)] = jnp.concatenate([first[:, half:], second[:, half:]], 1)

    kv_out, kv_twin = both(kv_view, kv_view(batch))
    ring(1)

    @pl.loop(0, blocks)
    def _(at):
        here = part(at, block)
        values = matmul(n1_ref[here], w_all[:, pl.ds(0, 2 * size)])
        q_ref[here] = values[:, :size].astype(BF)
        logit_ref[here] = values[:, size:]

    for step in range(2, steps):
        ring(step)
    down_passed = pass_on(down_view, down_out)
    kv_passed = pass_on(kv_view, kv_out)
    for pair in flows:
        for copy in pair:
            copy.wait_recv()
    swaps = []
    for hop in range(others):
        there = out_all.at[:, part(spots[hop] * 2 + core, wide)]
        swaps.append(go(there, there, twin))
    for copy in (*kv_twin, *kv_passed, *swaps, *down_twin, *down_passed):
        copy.wait_recv()
    for copy in copies:
        copy.wait_send()
    for at in range(blocks):
        n1_copy(at).wait()


def entry(tokens, w_shard, w_out, gains, segments, w_down, collective_id):
    count = lax.axis_size("head")
    batches = lax.axis_size("batch")
    others = batches // 2
    rows, width = tokens.shape
    size, wide = w_out.shape
    vmem = pl.BlockSpec(memory_space=pltpu.VMEM)
    hbm = pl.BlockSpec(memory_space=pl.ANY)
    slots = 6 * batches + others * (count + 3)
    sems = pltpu.SemaphoreType.DMA((slots,))
    return pl.pallas_call(
        functools.partial(entry_kernel, count, batches),
        out_shape=[
            jax.ShapeDtypeStruct((rows, width), BF),
            jax.ShapeDtypeStruct((rows, size), BF),
            jax.ShapeDtypeStruct((rows, size), F32),
            jax.ShapeDtypeStruct((batches * rows, 2 * size), BF),
            jax.ShapeDtypeStruct((width, 4 * size), BF),
            jax.ShapeDtypeStruct((count * size, batches * wide), BF),
            jax.ShapeDtypeStruct((batches, *gains.shape), F32),
            jax.ShapeDtypeStruct((batches, *segments.shape), jnp.int32),
            jax.ShapeDtypeStruct((w_down.shape[0] // 2, batches * w_down.shape[1]), BF),
        ],
        in_specs=[hbm] + [vmem] * 5,
        out_specs=[hbm] + [vmem] * 4 + [hbm] + [vmem] * 2 + [hbm],
        scratch_shapes=[
            pltpu.VMEM((rows, width), BF), pltpu.VMEM((rows, width), BF),
            sems, sems, pltpu.SemaphoreType.DMA((5,)),
            pltpu.SemaphoreType.DMA((rows // 256,)), pltpu.SemaphoreType.DMA((rows // 256,)),
        ],
        compiler_params=pltpu.CompilerParams(
            collective_id=collective_id, has_side_effects=True, vmem_limit_bytes=VMEM_LIMIT
        ),
        name="entry",
    )(tokens, w_shard, w_out, gains, segments, w_down)


KEY_BLOCK = 512
QUERY_BLOCK = 640


def key_range(start_ref, base, query_block):
    first = query_block * QUERY_BLOCK
    lowest = start_ref[first]
    highest = start_ref[first + QUERY_BLOCK - 1]
    begin = lowest // KEY_BLOCK
    end = (base + first + QUERY_BLOCK - 1) // KEY_BLOCK + 1
    full_begin = jnp.minimum((highest + KEY_BLOCK - 1) // KEY_BLOCK, end)
    full_end = jnp.maximum((base + first + 1) // KEY_BLOCK, full_begin)
    return begin, full_begin, full_end, end


def allowed_pairs(key_block, start_row, base_row):
    shape = (KEY_BLOCK, QUERY_BLOCK)
    key_pos = key_block * KEY_BLOCK + lax.broadcasted_iota(jnp.int32, shape, 0)
    query_pos = base_row + lax.broadcasted_iota(jnp.int32, shape, 1)
    return (key_pos >= start_row) & (key_pos <= query_pos)


def attend_kernel(
    scale, start_sm, base_sm, q_ref, kv_ref, start_ref, logit_ref, o_ref, a_ref, lse_ref
):
    base = base_sm[0]
    size = q_ref.shape[1]
    factor = scale * math.log2(math.e)

    @pl.loop(0, q_ref.shape[0] // QUERY_BLOCK)
    def _(block):
        rows = pl.ds(pl.multiple_of(block * QUERY_BLOCK, QUERY_BLOCK), QUERY_BLOCK)
        queries = q_ref[rows]
        start_row = start_ref[:, rows]
        begin, full_begin, full_end, end = key_range(start_sm, base, block)

        def step(masked, at, state):
            old_max, old_sum, total = state
            keys = pl.ds(pl.multiple_of(at * KEY_BLOCK, KEY_BLOCK), KEY_BLOCK)
            scores = cols_inner(kv_ref[keys, :size], queries)
            if masked:
                allowed = allowed_pairs(at, start_row, base + block * QUERY_BLOCK)
                scores = jnp.where(allowed, scores, MASKED)
            new_max = jnp.maximum(old_max, jnp.max(scores, axis=0, keepdims=True))
            keep = jnp.exp2((old_max - new_max) * factor)
            weights = jnp.exp2(scores * factor - new_max * factor)
            new_sum = old_sum * keep + jnp.sum(weights, axis=0, keepdims=True)
            total = total * keep + rows_inner(kv_ref[keys, size:], weights.astype(BF))
            return new_max, new_sum, total

        state = (
            jnp.full((1, QUERY_BLOCK), MASKED, F32),
            jnp.zeros((1, QUERY_BLOCK), F32),
            jnp.zeros((size, QUERY_BLOCK), F32),
        )
        state = lax.fori_loop(begin, full_begin, functools.partial(step, True), state)
        state = lax.fori_loop(full_begin, full_end, functools.partial(step, False), state)
        state = lax.fori_loop(full_end, end, functools.partial(step, True), state)
        run_max, run_sum, total = state
        lse_ref[:, rows] = run_max * factor + jnp.log2(run_sum)
        attended = (total / run_sum).T
        o_ref[rows] = attended
        a_ref[rows] = (attended * jax.nn.sigmoid(logit_ref[rows])).astype(BF)


def attend_back_kernel(
    scale, start_sm, base_sm, q_ref, kv_ref, start_ref, logit_ref, o_ref, da_ref, lse_ref,
    dq_ref, dg_ref, dkv_ref, dk_acc, dv_acc,
):
    base = base_sm[0]
    size = q_ref.shape[1]
    factor = scale * math.log2(math.e)
    dk_acc[...] = jnp.zeros_like(dk_acc)
    dv_acc[...] = jnp.zeros_like(dv_acc)

    @pl.loop(0, q_ref.shape[0] // QUERY_BLOCK)
    def _(block):
        rows = pl.ds(pl.multiple_of(block * QUERY_BLOCK, QUERY_BLOCK), QUERY_BLOCK)
        queries = q_ref[rows]
        start_row = start_ref[:, rows]
        lse = lse_ref[:, rows]
        gate = jax.nn.sigmoid(logit_ref[rows])
        attended = o_ref[rows]
        d_mixed = da_ref[rows].astype(F32)
        d_attended = (d_mixed * gate).astype(BF)
        dg_ref[rows] = (d_mixed * attended * gate * (1.0 - gate)).astype(BF)
        delta = jnp.sum((d_attended.astype(F32) * attended).T, axis=0, keepdims=True)
        begin, full_begin, full_end, end = key_range(start_sm, base, block)

        def step(masked, at, d_queries):
            keys = pl.ds(pl.multiple_of(at * KEY_BLOCK, KEY_BLOCK), KEY_BLOCK)
            key_block = kv_ref[keys, :size]
            probs = jnp.exp2(cols_inner(key_block, queries) * factor - lse)
            if masked:
                allowed = allowed_pairs(at, start_row, base + block * QUERY_BLOCK)
                probs = jnp.where(allowed, probs, 0.0)
            d_probs = cols_inner(kv_ref[keys, size:], d_attended)
            d_scores = (probs * (d_probs - delta) * scale).astype(BF)
            dv_acc[keys] += matmul(probs.astype(BF), d_attended)
            dk_acc[keys] += matmul(d_scores, queries)
            return d_queries + rows_inner(key_block, d_scores)

        d_queries = jnp.zeros((size, QUERY_BLOCK), F32)
        d_queries = lax.fori_loop(begin, full_begin, functools.partial(step, True), d_queries)
        d_queries = lax.fori_loop(full_begin, full_end, functools.partial(step, False), d_queries)
        d_queries = lax.fori_loop(full_end, end, functools.partial(step, True), d_queries)
        dq_ref[rows] = d_queries.T.astype(BF)

    @pl.loop(0, kv_ref.shape[0] // KEY_BLOCK)
    def _(at):
        keys = pl.ds(pl.multiple_of(at * KEY_BLOCK, KEY_BLOCK), KEY_BLOCK)
        dk, dv = dk_acc[keys].astype(BF), dv_acc[keys].astype(BF)
        half = size // 2
        dkv_ref[keys, :size] = jnp.concatenate([dk[:, :half], dv[:, :half]], axis=1)
        dkv_ref[keys, size:] = jnp.concatenate([dk[:, half:], dv[:, half:]], axis=1)


def tail_kernel(
    count, batches, dq_ref, dg_ref, dkv_ref, w_ref, gain_ref, dh1_ref, second_ref,
    low_ref, h1_ref, ahead_ref, behind_ref, n1_ref, x_hbm, mixed_hbm, mlp_hbm,
    out_all, tok_all, gains_ref, wout_own, din_ref, key_ref, value_ref,
    part_ref, tok_ref, got, wout_got, gain_own, gain_got, gain_mid, gain_heads,
    din_s, din_got, din_x, wout_s, wout_twin, wout_x,
    cat_ref, out_s, out_got, core_got, x_first, x_second, y_first, y_second, held, n1_s,
    x_ref, mixed_ref, mlp_ref, mlp_next, send_sem, recv_sem, local_sem,
):
    steps = count // 2
    rows, width = x_ref.shape
    depth = cat_ref.shape[1]
    tall, size = dq_ref.shape
    tile = 256
    place, right, left = ring_setup(count)
    batch, head = lax.axis_index("batch"), lax.axis_index("head")
    others = [lax.rem(batch + hop, batches) for hop in range(1, batches)]
    members = [(batch, ring_head(lax.rem(place + hop, count), count)) for hop in range(1, count)]
    greet((*members, *[(other, head) for other in others]))
    sems = (send_sem, recv_sem)
    slot = 0
    copies = []

    def go(source, target, device):
        nonlocal slot
        copy = send(source, target, sems, slot, device)
        slot += 1
        copies.append(copy)
        return copy

    across, core = batch // 2, lax.rem(batch, 2)
    spots = [lax.rem(across + hop, batches // 2) for hop in range(batches // 2)]
    order = list(range(1, batches // 2)) + [0]
    twin = (across * 2 + 1 - core, head)

    def scatter_swap(view, held):
        return [go(view(2 * spots[hop] + 1 - core), held.at[spots[hop]], twin) for hop in order]

    def add_tiles(target, one, other):
        @pl.loop(0, target.shape[0] // 128)
        def _(at):
            lines = pl.ds(pl.multiple_of(at * 128, 128), 128)
            total = one[lines].astype(F32) + other[lines].astype(F32)
            target[lines] = total.astype(target.dtype)

    def scatter_cross(view, held, crossed, arriving):
        out = []
        for copy, hop in zip(arriving, order):
            copy.wait_recv()
            spot = spots[hop]
            add_tiles(held.at[spot], held.at[spot], view(2 * spot + core))
            if hop:
                out.append(go(held.at[spot], crossed.at[hop - 1], (spot * 2 + core, head)))
        return out

    def scatter_end(held, crossed, arriving, target):
        for hop, copy in enumerate(arriving):
            copy.wait_recv()
            last = hop == len(arriving) - 1
            add_tiles(target if last else held.at[across], held.at[across], crossed.at[hop])

    def wout_view(at):
        wide = width // batches
        return wout_s.at[:, pl.ds(pl.multiple_of(at * wide, wide), wide)]

    def din_view(at):
        tall = din_ref.shape[0]
        return din_s.at[pl.ds(pl.multiple_of(at * tall, tall), tall)]

    def span(owner, extent):
        return pl.ds(pl.multiple_of(lax.rem(owner + count, count) * extent, extent), extent)

    def compute(owner):
        here = span(owner, rows)
        values = cat_ref[here]

        @pl.loop(0, width // tile)
        def _(at):
            cols = pl.ds(pl.multiple_of(at * tile, tile), tile)
            part_ref[here, cols] = cols_inner(values, w_ref[cols, pl.ds(0, depth)]).astype(BF)

    def gather(own, whole, step, last):
        out = []
        for flow, chunk, device in ((0, place - step, right), (1, place + step, left)):
            if last:
                last[flow].wait_recv()
            target = whole.at[lax.rem(chunk + count, count)]
            source = target if step else own
            if step == steps - 1:
                cut = (slice(None), pl.ds(flow * (width // 2), width // 2))
                source, target = source.at[cut], target.at[cut]
            out.append(go(source, target, device))
        return out

    def reduce(parts, held, step, last):
        extent, side = held.shape[2], held.shape[3] // 2
        out = []
        for flow, owner, device in (
            (0, place + steps - step, right),
            (1, place - steps + step, left),
        ):
            have = pl.ds(flow * side, side)
            lack = pl.ds((1 - flow) * side, side)
            mine = parts.at[span(owner, extent)]
            if step == 0:
                out.append(go(mine.at[:, have], held.at[flow, 0, :, have], device))
                continue
            last[flow].wait_recv()
            if step == 1:
                held[flow, 0, :, have] = add_low(held[flow, 0, :, have], mine[:, have])
                held[flow, 0, :, lack] = mine[:, lack]
            else:
                held[flow, step - 1] = add_low(held[flow, step - 1], mine[...])
            out.append(go(held.at[flow, step - 1], held.at[flow, step], device))
        return out

    low = lax.rem(head, 2)
    mate = (batch, head + 1 - 2 * low)
    peers = [(spot * 2 + core, head) for spot in spots]
    mine = pl.ds(pl.multiple_of(low * size, size), size)
    given = pl.ds(pl.multiple_of((1 - low) * size, size), size)
    top, bottom = pl.ds(0, tall // 2), pl.ds(tall // 2, tall // 2)
    fresh = pl.ds(2 * size, size)

    def keys_of(at):
        return dkv_ref.at[pl.ds(pl.multiple_of(at * tall, tall), tall)]

    def normed_copy(at, slot):
        cols = pl.ds(pl.multiple_of(at * tile, tile), tile)
        return pltpu.make_async_copy(n1_ref.at[:, cols], n1_s.at[slot], local_sem.at[2 + slot])

    own_rows = pl.ds(pl.multiple_of(place * rows, rows), rows)
    fetches = [
        pltpu.make_async_copy(source.at[own_rows], target, local_sem.at[4 + index])
        for index, (source, target) in enumerate(
            ((mixed_hbm, mixed_ref), (mlp_hbm, mlp_ref), (x_hbm, x_ref))
        )
    ]
    nexts = [
        pltpu.make_async_copy(mlp_hbm.at[span(place + shift, rows)], mlp_next.at[at], local_sem.at[7 + at])
        for at, shift in enumerate((1, -1))
    ]
    for copy in (*nexts, *fetches):
        copy.start()
    for at in range(2):
        normed_copy(at, at).start()
    swaps = scatter_swap(keys_of, core_got)
    last_sums = []
    for at, (held_part, device) in enumerate(((ahead_ref, right), (behind_ref, left))):
        nexts[at].wait()
        mlp_next[at] = add_low(mlp_next[at], held_part[...])
        last_sums.append(go(mlp_next.at[at], out_got.at[at], device))
    cat_ref[:, pl.ds(0, size)] = dq_ref[...]
    cat_ref[:, pl.ds(size, size)] = dg_ref[...]
    for copy in fetches:
        copy.wait()

    @pl.loop(0, width // tile)
    def _(at):
        cols = pl.ds(pl.multiple_of(at * tile, tile), tile)
        wout_s[:, cols] = rows_inner(mixed_ref[...], low_ref[:, cols]).astype(BF)

    tops, bottoms = [], []
    for copy, hop in zip(swaps, order):
        copy.wait_recv()
        spot = spots[hop]
        add_tiles(core_got.at[spot], core_got.at[spot], keys_of(2 * spot + core))
        bottoms.append(go(core_got.at[spot, bottom, given], y_first.at[spot], mate))
        if hop:
            tops.append(go(core_got.at[spot, top], x_first.at[hop - 1], peers[hop]))
    wouts = scatter_swap(wout_view, wout_twin)
    for copy in last_sums:
        copy.wait_recv()
    out_s[...] = (
        h1_ref[...] + mlp_ref[...].astype(F32) + out_got[0].astype(F32) + out_got[1].astype(F32)
    ).astype(BF)
    keep_out = pltpu.make_async_copy(out_s, out_all.at[place], local_sem.at[0])
    keep_out.start()
    outs = gather(out_s, out_all, 0, None)
    total = core_got[across, top].astype(F32)
    for hop, copy in enumerate(tops):
        copy.wait_recv()
        total = total + x_first[hop].astype(F32)
    held[...] = total.astype(BF)
    last = go(held.at[:, given], y_second, mate)
    ends = []
    for copy, hop in zip(bottoms, order):
        copy.wait_recv()
        spot = spots[hop]
        y_first[spot] = add_low(y_first[spot], core_got[spot, bottom, mine])
        if hop:
            ends.append(go(y_first.at[spot], x_second.at[hop - 1], peers[hop]))
    last.wait_recv()
    cat_ref[top, fresh] = add_low(held[:, mine], y_second[...])
    total = y_first[across].astype(F32)
    for hop, copy in enumerate(ends):
        copy.wait_recv()
        total = total + x_second[hop].astype(F32)
    cat_ref[bottom, fresh] = total.astype(BF)

    compute(place + steps)
    sums = reduce(part_ref, got, 0, None)
    outs = gather(out_s, out_all, 1, outs)

    @pl.loop(1, count)
    def _(hop):
        compute(place + steps + hop)

    @pl.loop(0, width // tile)
    def _(at):
        slot = lax.rem(at, 2)
        normed_copy(at, slot).wait()
        cols = pl.ds(pl.multiple_of(at * tile, tile), tile)
        din_s[cols] = rows_inner(n1_s[slot], cat_ref[...]).astype(BF)

        @pl.when(at + 2 < width // tile)
        def _():
            normed_copy(at + 2, slot).start()

    dins = scatter_swap(din_view, din_got)
    for step in range(1, steps):
        sums = reduce(part_ref, got, step, sums)
        if 2 <= step < steps - 1:
            outs = gather(out_s, out_all, step, outs)
        if step == 1:
            wouts = scatter_cross(wout_view, wout_twin, wout_x, wouts)
            dins = scatter_cross(din_view, din_got, din_x, dins)
    for copy in sums:
        copy.wait_recv()

    def tile_of(at):
        return pl.ds(pl.multiple_of(at * tile, tile), tile)

    def total(cols):
        return (
            part_ref[span(place, rows), cols].astype(F32)
            + got[0, steps - 1, :, cols].astype(F32)
            + got[1, steps - 1, :, cols].astype(F32)
        )

    def collect(at, state):
        squares, mean = state
        cols = tile_of(at)
        x = x_ref[:, cols].astype(F32)
        squares = squares + jnp.sum(x * x, axis=1, keepdims=True)
        return squares, mean + jnp.sum(gain_ref[:, cols] * total(cols) * x, axis=1, keepdims=True)

    zero = jnp.zeros((rows, 1), F32)
    squares, mean = lax.fori_loop(0, width // tile, collect, (zero, zero))
    scale = lax.rsqrt(squares / width + EPSILON)
    pull = scale * scale * scale * (mean / width)

    @pl.loop(0, width // tile)
    def _(at):
        cols = tile_of(at)
        x, dn1 = x_ref[:, cols].astype(F32), total(cols)
        gain_own[pl.ds(0, 1), cols] = jnp.sum(dn1 * x * scale, axis=0, keepdims=True)
        gain_own[pl.ds(1, 1), cols] = second_ref[:, cols]
        tok_ref[:, cols] = (dh1_ref[:, cols] + scale * (gain_ref[:, cols] * dn1) - x * pull).astype(BF)

    keep_tok = pltpu.make_async_copy(tok_ref, tok_all.at[place], local_sem.at[1])
    keep_tok.start()
    toks = gather(tok_ref, tok_all, 0, None)
    outs = gather(out_s, out_all, steps - 1, outs)
    wout_part = wout_twin.at[across]
    scatter_end(wout_twin, wout_x, wouts, wout_part)
    wsums = reduce(wout_part, wout_got, 0, None)
    scatter_end(din_got, din_x, dins, din_ref)
    narrow = din_ref[:, pl.ds(2 * size, size)].T
    key_ref[...] = narrow[: size // 2]
    value_ref[...] = narrow[size // 2 :]
    wide = width // batches

    def slice_of(at):
        return pl.ds(pl.multiple_of(at * wide, wide), wide)

    gains = [
        go(gain_own.at[:, slice_of(other)], gain_got.at[hop], (other, head))
        for hop, other in enumerate(others)
    ]
    toks = gather(tok_ref, tok_all, 1, toks)
    wsums = reduce(wout_part, wout_got, 1, wsums)
    middle = gain_own[:, slice_of(batch)]
    for hop, copy in enumerate(gains):
        copy.wait_recv()
        middle = middle + gain_got[hop]
    gain_mid[...] = middle
    gain_heads[place] = middle
    gains = [go(gain_mid, gain_heads.at[place], member) for member in members]
    for step in range(2, steps):
        toks = gather(tok_ref, tok_all, step, toks)
        wsums = reduce(wout_part, wout_got, step, wsums)
    for copy in gains:
        copy.wait_recv()
    middle = gain_heads[0]
    for at in range(1, count):
        middle = middle + gain_heads[at]
    gains_ref[...] = middle
    for copy in (*wsums, *outs):
        copy.wait_recv()
    wout_own[...] = (
        wout_part[span(place, wout_own.shape[0])].astype(F32)
        + wout_got[0, steps - 1].astype(F32)
        + wout_got[1, steps - 1].astype(F32)
    )
    for copy in toks:
        copy.wait_recv()
    for copy in copies:
        copy.wait_send()
    keep_out.wait()
    keep_tok.wait()


def tail(arrays, collective_id):
    d_queries, tokens, mixed = arrays[0], arrays[-3], arrays[-2]
    count = lax.axis_size("head")
    batches = lax.axis_size("batch")
    steps = count // 2
    rows, width = tokens.shape[0] // count, tokens.shape[1]
    others = batches // 2
    size, wide = mixed.shape[1] // count, width // batches
    tall, head_size = d_queries.shape
    depth = 3 * head_size
    vmem = pl.BlockSpec(memory_space=pltpu.VMEM)
    hbm = pl.BlockSpec(memory_space=pl.ANY)
    whole = (count, rows, width)
    sems = pltpu.SemaphoreType.DMA((6 * count + 6 * batches,))
    gains = (2, width // batches)
    return pl.pallas_call(
        functools.partial(tail_kernel, count, batches),
        out_shape=[
            jax.ShapeDtypeStruct(whole, BF),
            jax.ShapeDtypeStruct(whole, BF),
            jax.ShapeDtypeStruct(gains, F32),
            jax.ShapeDtypeStruct((size, wide), F32),
            jax.ShapeDtypeStruct((wide, depth), F32),
            jax.ShapeDtypeStruct((size // 2, wide), F32),
            jax.ShapeDtypeStruct((size // 2, wide), F32),
        ],
        in_specs=[vmem] * 11 + [hbm] * 4,
        out_specs=[hbm] * 2 + [vmem] * 5,
        scratch_shapes=[
            pltpu.VMEM((count * rows, width), BF),
            pltpu.VMEM((rows, width), BF),
            pltpu.VMEM((2, steps, rows, width), BF),
            pltpu.VMEM((2, steps, size, wide), BF),
            pltpu.VMEM((2, width), F32),
            pltpu.VMEM((batches - 1, *gains), F32),
            pltpu.VMEM(gains, F32),
            pltpu.VMEM((count, *gains), F32),
            pltpu.VMEM((width, depth), BF),
            pltpu.VMEM((others, wide, depth), BF),
            pltpu.VMEM((others - 1, wide, depth), BF),
            pltpu.VMEM((count * size, width), BF),
            pltpu.VMEM((others, count * size, wide), BF),
            pltpu.VMEM((others - 1, count * size, wide), BF),
            pltpu.VMEM((tall, depth), BF),
            pltpu.VMEM((rows, width), BF),
            pltpu.VMEM((2, rows, width), BF),
            pltpu.VMEM((others, tall, 2 * head_size), BF),
            pltpu.VMEM((others - 1, tall // 2, 2 * head_size), BF),
            pltpu.VMEM((others - 1, tall // 2, head_size), BF),
            pltpu.VMEM((others, tall // 2, head_size), BF),
            pltpu.VMEM((tall // 2, head_size), BF),
            pltpu.VMEM((tall // 2, 2 * head_size), BF),
            pltpu.VMEM((2, tall, 256), BF),
            pltpu.VMEM((rows, width), BF),
            pltpu.VMEM((rows, mixed.shape[1]), BF),
            pltpu.VMEM((rows, width), BF),
            pltpu.VMEM((2, rows, width), BF),
            sems,
            sems,
            pltpu.SemaphoreType.DMA((9,)),
        ],
        compiler_params=pltpu.CompilerParams(
            collective_id=collective_id, has_side_effects=True, vmem_limit_bytes=VMEM_LIMIT
        ),
        cost_estimate=pl.CostEstimate(
            flops=4 * count * rows * width * depth, bytes_accessed=400 << 20, transcendentals=0
        ),
        name="tail",
    )(*arrays)


def finish_kernel(
    out_hbm, tok_hbm, mlp_ref, down_ref, in_ref, gains_ref, key_ref, value_ref, wout_ref,
    output, d_tokens, mgate, mup, down, query, gate, first, second, key, value, wout,
    held, load_sem, store_sem,
):
    count, rows = out_hbm.shape[:2]
    loads, stores = [], []
    for index, (source, target) in enumerate(((out_hbm, output), (tok_hbm, d_tokens))):
        for at in range(count):
            slot = index * count + at
            loads.append(pltpu.make_async_copy(source.at[at], held.at[slot], load_sem.at[slot]))
            stores.append(
                pltpu.make_async_copy(
                    held.at[slot], target.at[pl.ds(at * rows, rows)], store_sem.at[slot]
                )
            )
    for copy in loads:
        copy.start()
    hidden = mgate.shape[1]
    size = query.shape[1]

    def convert(target, source, start):
        tall = 32

        @pl.loop(0, target.shape[0] // tall)
        def _(at):
            lines = pl.ds(pl.multiple_of(at * tall, tall), tall)
            target[lines] = source[lines, pl.ds(start, target.shape[1])].astype(target.dtype)

    for load, store in zip(loads, stores):
        load.wait()
        store.start()
    convert(mgate, mlp_ref, 0)
    convert(mup, mlp_ref, hidden)
    convert(down, down_ref, 0)
    convert(query, in_ref, 0)
    convert(gate, in_ref, size)
    key[...] = key_ref[...]
    value[...] = value_ref[...]
    wout[...] = wout_ref[...]
    first[...] = gains_ref[pl.ds(0, 1)]
    second[...] = gains_ref[pl.ds(1, 1)]
    for copy in stores:
        copy.wait()


def finish(output, d_tokens, d_mlp, d_down, d_in, gains, *rest):
    count, rows, width = output.shape
    tall, hidden = d_mlp.shape[0], d_mlp.shape[1] // 2
    down_rows, wide = d_down.shape
    size = d_in.shape[1] // 3
    vmem = pl.BlockSpec(memory_space=pltpu.VMEM)
    hbm = pl.BlockSpec(memory_space=pl.ANY)

    def shape(*extent, dtype=F32):
        return jax.ShapeDtypeStruct(extent, dtype)

    return pl.pallas_call(
        finish_kernel,
        out_shape=[
            shape(count * rows, width, dtype=BF), shape(count * rows, width, dtype=BF),
            shape(tall, hidden), shape(tall, hidden), shape(down_rows, wide),
            shape(tall, size), shape(tall, size),
            shape(1, wide), shape(1, wide), *[shape(*a.shape) for a in rest],
        ],
        in_specs=[hbm] * 2 + [vmem] * 7,
        out_specs=[hbm] * 2 + [vmem] * 10,
        scratch_shapes=[
            pltpu.VMEM((2 * count, rows, width), BF),
            pltpu.SemaphoreType.DMA((2 * count,)),
            pltpu.SemaphoreType.DMA((2 * count,)),
        ],
        compiler_params=pltpu.CompilerParams(vmem_limit_bytes=VMEM_LIMIT),
        name="finish",
    )(output, d_tokens, d_mlp, d_down, d_in, gains, *rest)


def local_call(kernel, scalars, arrays, outs, scratch, flops, name):
    vmem = pl.BlockSpec(memory_space=pltpu.VMEM)
    smem = pl.BlockSpec(memory_space=pltpu.SMEM)
    return pl.pallas_call(
        kernel,
        out_shape=outs,
        in_specs=[smem] * len(scalars) + [vmem] * len(arrays),
        out_specs=[vmem] * len(outs),
        scratch_shapes=scratch,
        compiler_params=pltpu.CompilerParams(vmem_limit_bytes=VMEM_LIMIT),
        cost_estimate=pl.CostEstimate(flops=flops, bytes_accessed=8 << 20, transcendentals=0),
        name=name,
    )(*scalars, *arrays)


def ring_routes(count):
    spots = [ring_head(at, count) for at in range(count)]
    right = [(spots[at], spots[(at + 1) % count]) for at in range(count)]
    left = [(spots[at], spots[at - 1]) for at in range(count)]
    return right, left


def add_low(one, other):
    return (one.astype(F32) + other.astype(F32)).astype(BF)


def flow_steps(part, going, coming):
    count = lax.axis_size("head")
    place = ring_place(lax.axis_index("head"), count)
    right, left = ring_routes(count)
    rows = part.shape[0] // count
    steps = count // 2

    def mine(owner):
        return lax.dynamic_slice_in_dim(part, lax.rem(owner + count, count) * rows, rows, 0)

    for step in range(2, steps - 1):
        going = lax.ppermute(going, "head", right)
        coming = lax.ppermute(coming, "head", left)
        if step < steps - 2:
            going = add_low(going, mine(place + steps - 1 - step))
            coming = add_low(coming, mine(place - steps + 1 + step))
    return going, coming


def matmul(left, right):
    return jnp.dot(left, right, preferred_element_type=F32)


def rows_inner(left, right):
    return lax.dot_general(left, right, (((0,), (0,)), ((), ())), preferred_element_type=F32)


def cols_inner(left, right):
    return lax.dot_general(left, right, (((1,), (1,)), ((), ())), preferred_element_type=F32)


def rms_scale(values):
    return lax.rsqrt(jnp.mean(values * values, axis=1, keepdims=True) + EPSILON)


def per_device(
    tokens,
    segment_ids,
    norm1_gain,
    w_query,
    w_key,
    w_value,
    w_gate,
    w_out,
    norm2_gain,
    w_mlp_gate,
    w_mlp_up,
    w_down,
    out_grad,
):
    heads = lax.axis_size("head")
    batches = lax.axis_size("batch")
    row_count, width = tokens.shape
    head_size = w_query.shape[1]
    half = w_key.shape[1]
    chunk = row_count // heads
    me = ring_place(lax.axis_index("head"), heads)
    scale_factor = 1.0 / math.sqrt(head_size)

    w_shard = jnp.concatenate([w_query, w_gate, w_key, w_value], axis=1)
    gains = jnp.concatenate([norm1_gain, norm2_gain]).reshape(-1, 128).astype(F32)
    normed_one, queries, gate_logit, kv_all, w_in, out_full, gains, seg_all, down_top = entry(
        tokens, w_shard, w_out, gains, segment_ids.reshape(-1, 128), w_down, 1
    )
    gains, w_mlp_gate = lax.optimization_barrier((gains, w_mlp_gate))
    seg_all = seg_all.reshape(-1)
    gains = gains.reshape(batches, 2, -1).transpose(1, 0, 2).reshape(2, width)
    gain_one, gain_two = gains[0], gains[1]
    mgate_full = lax.all_gather(w_mlp_gate, "batch", axis=0, tiled=True)

    base = lax.axis_index("batch") * row_count
    ids = jnp.arange(DOCUMENTS, dtype=jnp.int32)
    below = jnp.sum((seg_all[None, :] < ids[:, None]).astype(jnp.int32), axis=1)
    starts = jnp.sum(jnp.where(segment_ids[None, :] == ids[:, None], below[:, None], 0), axis=0)
    scalars = (starts, base.reshape(1))
    pair_flops = 4 * row_count * kv_all.shape[0] * head_size
    attended, mixed, lse = local_call(
        functools.partial(attend_kernel, scale_factor),
        scalars,
        (queries, kv_all, starts[None], gate_logit),
        [
            jax.ShapeDtypeStruct((row_count, head_size), F32),
            jax.ShapeDtypeStruct((row_count, head_size), BF),
            jax.ShapeDtypeStruct((1, row_count), F32),
        ],
        [],
        pair_flops,
        "attend",
    )
    mixed_all, down_low, mup_full = spread(
        [mixed, w_down, w_mlp_up], (("head", "cols"), ("batch", "low"), ("batch", "rows")), 2
    )
    (
        mlp_part, d_mlp, d_down, resid_own, d_resid, d_resid_low, d_gain_two, d_mixed, going, coming,
    ) = mlp_back(
        tokens, mixed_all, out_grad, gain_two[None], out_full, mgate_full, mup_full, down_top, down_low, 3
    )
    hold = lax.optimization_barrier
    state = flow_steps(mlp_part, going, coming)

    d_queries, d_gate_logit, d_kv_all = local_call(
        functools.partial(attend_back_kernel, scale_factor),
        scalars,
        (queries, kv_all, starts[None], gate_logit, attended, d_mixed, lse),
        [
            jax.ShapeDtypeStruct((row_count, head_size), BF),
            jax.ShapeDtypeStruct((row_count, head_size), BF),
            jax.ShapeDtypeStruct(kv_all.shape, BF),
        ],
        [pltpu.VMEM((kv_all.shape[0], head_size), F32)] * 2,
        5 * pair_flops // 2,
        "attend_back",
    )
    d_down = lax.psum_scatter(d_down, "batch", scatter_dimension=1, tiled=True)
    d_mlp = lax.psum_scatter(d_mlp, "batch", scatter_dimension=0, tiled=True)
    output, d_tokens, d_gains, d_out, d_in, d_key, d_value = tail(
        (
            d_queries, d_gate_logit, d_kv_all, w_in, gain_one[None], d_resid, d_gain_two,
            d_resid_low, resid_own, *state, normed_one, tokens, mixed_all, mlp_part,
        ),
        5,
    )
    (
        output, d_tokens, d_mgate, d_mup, d_down, d_query, d_gate, d_one, d_two,
        d_key, d_value, d_out,
    ) = finish(output, d_tokens, d_mlp, d_down, d_in, d_gains, d_key, d_value, d_out)
    return (
        output,
        d_tokens,
        d_one.reshape(-1),
        d_query,
        d_key.T,
        d_value.T,
        d_gate,
        d_out,
        d_two.reshape(-1),
        d_mgate,
        d_mup,
        d_down,
    )


def solution(mesh):
    return jax.shard_map(
        per_device,
        mesh=mesh,
        in_specs=(
            P("batch", None),
            P("batch"),
            P("batch"),
            P("batch", "head"),
            P("batch", "head"),
            P("batch", "head"),
            P("batch", "head"),
            P("head", "batch"),
            P("batch"),
            P("batch", "head"),
            P("batch", "head"),
            P("head", "batch"),
            P("batch", None),
        ),
        out_specs=(
            P("batch", None),
            P("batch", None),
            P("batch"),
            P("batch", "head"),
            P("batch", "head"),
            P("batch", "head"),
            P("batch", "head"),
            P("head", "batch"),
            P("batch"),
            P("batch", "head"),
            P("batch", "head"),
            P("head", "batch"),
        ),
        check_vma=False,
    )
```

```python
import functools
import math

import jax
import jax.numpy as jnp
from jax import lax
from jax.experimental import pallas as pl
from jax.experimental.pallas import tpu as pltpu
from jax.sharding import PartitionSpec as P

EPSILON = 1e-06
MASKED = -1e30
DOCUMENTS = 7
BF = jnp.bfloat16
F32 = jnp.float32


MESH = pl.DeviceIdType.MESH
VMEM_LIMIT = 60 << 20


def ring_place(head, count):
    high, low = head // 2, head % 2
    return (1 - low) * high + low * (count - 1 - high)


def ring_head(place, count):
    low = place // (count // 2)
    high = (1 - low) * place + low * (count - 1 - place)
    return 2 * high + low


def ring_setup(count):
    batch = lax.axis_index("batch")
    place = ring_place(lax.axis_index("head"), count)
    right = (batch, ring_head(lax.rem(place + 1, count), count))
    left = (batch, ring_head(lax.rem(place + count - 1, count), count))
    return place, right, left


def greet(devices):
    barrier = pltpu.get_barrier_semaphore()
    for device in devices:
        pl.semaphore_signal(barrier, inc=1, device_id=device, device_id_type=MESH)
    pl.semaphore_wait(barrier, len(devices))


def send(source, target, sems, slot, device):
    copy = pltpu.make_async_remote_copy(
        src_ref=source,
        dst_ref=target,
        send_sem=sems[0].at[slot],
        recv_sem=sems[1].at[slot],
        device_id=device,
        device_id_type=MESH,
    )
    copy.start()
    return copy


def half_of(extent, flow):
    if extent[1] % 256:
        return (pl.ds(flow * (extent[0] // 2), extent[0] // 2), slice(None))
    return (slice(None), pl.ds(flow * (extent[1] // 2), extent[1] // 2))


def place_of(whole, own, chunk, form):
    rows, wide = own.shape[-2:]
    if form == "lead":
        return whole.at[chunk]
    if form == "rows":
        return whole.at[pl.ds(pl.multiple_of(chunk * rows, rows), rows)]
    return whole.at[:, pl.ds(pl.multiple_of(chunk * wide, wide), wide)]


def spread_kernel(count, batches, plans, *refs):
    steps = count // 2
    arrays = len(plans)
    own_refs, all_refs = list(refs[:arrays]), refs[arrays : 2 * arrays]
    for index, (_, form) in enumerate(plans):
        if form == "low":
            half = own_refs[index].shape[0] // 2
            own_refs[index] = own_refs[index].at[pl.ds(half, half)]
    send_sem, recv_sem, local_sem = refs[2 * arrays :]
    place, right, left = ring_setup(count)
    head = lax.axis_index("head")
    batch = lax.axis_index("batch")
    across, core = batch // 2, lax.rem(batch, 2)
    others = batches // 2
    twin = (across * 2 + 1 - core, head)
    peers = [(lax.rem(across + hop, others) * 2 + core, head) for hop in range(1, others)]
    ring = any(axis == "head" for axis, _ in plans)
    grid = any(axis == "batch" for axis, _ in plans)
    greet((right, left) * ring + (twin, *peers) * grid)
    sems = (send_sem, recv_sem)
    slot = 0
    waiting, arriving, local = [], [], []

    def go(source, target, device):
        nonlocal slot
        copy = send(source, target, sems, slot, device)
        slot += 1
        waiting.append(copy)
        return copy

    stages = []
    for index, (axis, form) in enumerate(plans):
        own, whole = own_refs[index], all_refs[index]
        spot = place if axis == "head" else batch
        copy = pltpu.make_async_copy(own, place_of(whole, own, spot, form), local_sem.at[index])
        copy.start()
        local.append(copy)
        if axis == "batch":
            stages.append(index)
    onward = []

    def stage():
        for copy, block in onward:
            copy.wait_recv()
            arriving.append(go(block, block, twin))
        onward.clear()
        if stages:
            index = stages.pop(0)
            own, whole, form = own_refs[index], all_refs[index], plans[index][1]
            mine = place_of(whole, own, batch, form)
            for hop, peer in enumerate(peers, 1):
                source = lax.rem(across + others - hop, others) * 2 + core
                onward.append((go(own, mine, peer), place_of(whole, own, source, form)))
            arriving.append(go(own, mine, twin))

    stage()
    copies = [None] * (2 * arrays)
    for step in range(steps):
        for index, (axis, form) in enumerate(plans):
            if axis != "head":
                continue
            own = own_refs[index]
            for flow, chunk, device in ((0, place - step, right), (1, place + step, left)):
                at = 2 * index + flow
                if step:
                    copies[at].wait_recv()
                chunk = lax.rem(chunk + count, count)
                target = place_of(all_refs[index], own, chunk, form)
                source = target if step else own
                if step == steps - 1:
                    part = half_of(own.shape, flow)
                    source = source.at[part]
                    target = target.at[part]
                copies[at] = go(source, target, device)
        if step == steps // 2:
            stage()
    while stages or onward:
        stage()
    for copy in copies:
        if copy is not None:
            arriving.append(copy)
    for copy in arriving:
        copy.wait_recv()
    for copy in waiting:
        copy.wait_send()
    for copy in local:
        copy.wait()


def spread(arrays, plans, collective_id):
    count = lax.axis_size("head")
    batches = lax.axis_size("batch")
    shapes = []
    slots = 0
    for array, (axis, form) in zip(arrays, plans):
        many = count if axis == "head" else batches
        slots += count if axis == "head" else batches - 1
        if form == "lead":
            shapes.append((many, *array.shape))
        elif form == "rows":
            shapes.append((many * array.shape[0], array.shape[1]))
        else:
            tall = array.shape[0] // (2 if form == "low" else 1)
            shapes.append((tall, many * array.shape[1]))
    hbm = pl.BlockSpec(memory_space=pl.ANY)
    return pl.pallas_call(
        functools.partial(spread_kernel, count, batches, plans),
        out_shape=[jax.ShapeDtypeStruct(shape, a.dtype) for shape, a in zip(shapes, arrays)],
        in_specs=[pl.BlockSpec(memory_space=pltpu.VMEM)] * len(arrays),
        out_specs=[hbm] * len(arrays),
        scratch_shapes=[
            pltpu.SemaphoreType.DMA((slots,)),
            pltpu.SemaphoreType.DMA((slots,)),
            pltpu.SemaphoreType.DMA((len(arrays),)),
        ],
        compiler_params=pltpu.CompilerParams(
            collective_id=collective_id, has_side_effects=True, vmem_limit_bytes=VMEM_LIMIT
        ),
        name=f"spread_{collective_id}",
    )(*arrays)


def mlp_kernel(
    count, x_hbm, a_hbm, dy_hbm, gain_ref, out_hbm, gate_hbm, up_hbm, top_hbm, low_hbm,
    mlp_hbm, dmlp_hbm, ddown_hbm, h1_ref, dh1_ref, low_ref, dgain_ref, da_ref, ahead_ref, behind_ref,
    x_s, a_s, mlp_s, h1_s, dy_all, n2_all, hid_all, grad_all, dmlp_s, ddown_s, da_part,
    mlp_far, mlp_next, mlp_got, right_part, left_part, right_got, left_got,
    out_w, gate_w, up_w, down_w, in_sem, out_sem, grad_sem, weight_sem,
    send_sem, recv_sem, da_send, da_recv, far_send, far_recv,
):
    steps = count // 2
    rows = x_hbm.shape[0] // count
    width = x_hbm.shape[1]
    hidden = gate_w.shape[1]
    middle = hidden // 2
    weights = [
        pltpu.make_async_copy(source, target, weight_sem.at[index])
        for index, (source, target) in enumerate(
            (
                (out_hbm, out_w), (gate_hbm, gate_w), (up_hbm, up_w),
                (top_hbm, down_w.at[pl.ds(0, middle)]), (low_hbm, down_w.at[pl.ds(middle, middle)]),
            )
        )
    ]
    side = width // 2
    tile = 256
    broad = 1024
    inner = 256 if hidden % 256 == 0 else 128
    size = da_ref.shape[1]
    place, right, left = ring_setup(count)

    def member(hop):
        spot = lax.rem(place + hop, count)
        return spot, (lax.axis_index("batch"), ring_head(spot, count))

    def owners(group):
        first = jnp.where(group == 0, 1, 0)
        one = lax.rem(place + steps - group, count)
        two = lax.rem(place - steps + group + first * steps + count, count)
        return one, two

    def span(owner):
        return pl.ds(pl.multiple_of(owner * rows, rows), rows)

    def tile_of(at, extent=tile):
        return pl.ds(pl.multiple_of(at * extent, extent), extent)

    def loads(group, slot):
        return [
            pltpu.make_async_copy(
                source.at[span(owner)],
                target.at[pl.ds(at * rows, rows)],
                in_sem.at[slot, 2 * index + at],
            )
            for index, (source, target) in enumerate(
                ((x_hbm, x_s.at[slot]), (a_hbm, a_s.at[slot]), (dy_hbm, dy_all.at[group]))
            )
            for at, owner in enumerate(owners(group))
        ]

    def stores(group, slot):
        return [
            pltpu.make_async_copy(
                mlp_s.at[slot, pl.ds(at * rows, rows)], mlp_hbm.at[span(owner)], out_sem.at[slot, at]
            )
            for at, owner in enumerate(owners(group))
        ]

    def passing(source, target, sems, slot, device):
        return pltpu.make_async_remote_copy(
            src_ref=source,
            dst_ref=target,
            send_sem=sems[0].at[slot],
            recv_sem=sems[1].at[slot],
            device_id=device,
            device_id_type=MESH,
        )

    ring_sems, far_sems = (send_sem, recv_sem), (far_send, far_recv)
    ahead, behind = pl.ds(0, side), pl.ds(side, side)

    def first_copies():
        return (
            passing(right_part.at[0, :, ahead], right_got.at[0, :, ahead], ring_sems, 0, right),
            passing(right_part.at[0, :, behind], left_got.at[0, :, behind], ring_sems, steps, left),
        )

    def later_copies(step):
        return (
            passing(right_got.at[step - 1], right_got.at[step], ring_sems, step, right),
            passing(left_got.at[step - 1], left_got.at[step], ring_sems, steps + step, left),
        )

    for copy in (*loads(0, 0), *weights):
        copy.start()
    greet([member(hop)[1] for hop in range(1, count)])
    weights[0].wait()

    @pl.loop(0, steps)
    def _(group):
        slot = lax.rem(group, 2)
        for copy in loads(group, slot):
            copy.wait()

        @pl.when(group + 1 < steps)
        def _():
            for copy in loads(group + 1, 1 - slot):
                copy.start()

        @pl.when(group >= 2)
        def _():
            for copy in stores(group - 2, slot):
                copy.wait()

        mixed = a_s[slot]

        def residual(at, total):
            cols = tile_of(at, broad)
            values = x_s[slot, :, cols].astype(F32) + matmul(mixed, out_w[:, cols])
            h1_s[:, cols] = values
            return total + jnp.sum(values * values, axis=1, keepdims=True)

        total = lax.fori_loop(0, width // broad, residual, jnp.zeros((2 * rows, 1), F32))
        scale = lax.rsqrt(total / width + EPSILON)

        @pl.when(group == 0)
        def _():
            h1_ref[...] = h1_s[pl.ds(rows, rows)]
            for copy in weights[1:]:
                copy.wait()

        @pl.loop(0, width // tile)
        def _(at):
            cols = tile_of(at)
            n2_all[group, :, cols] = (h1_s[:, cols] * scale * gain_ref[:, cols]).astype(BF)

        normed = n2_all[group]
        dy = dy_all[group]

        @pl.loop(0, hidden // inner)
        def _(at):
            cols = tile_of(at, inner)
            cols_up = pl.ds(pl.multiple_of(hidden + at * inner, inner), inner)
            gate = matmul(normed, gate_w[:, cols])
            up = matmul(normed, up_w[:, cols])
            d_hidden = cols_inner(dy, down_w[cols])
            sig = jax.nn.sigmoid(gate)
            silu = gate * sig
            hid_all[group, :, cols] = (silu * up).astype(BF)
            grad_all[group, :, cols] = (d_hidden * up * sig * (1.0 + gate * (1.0 - sig))).astype(BF)
            grad_all[group, :, cols_up] = (d_hidden * silu).astype(BF)

        hid = hid_all[group]
        d_gate = grad_all[group, :, :hidden]
        d_up = grad_all[group, :, hidden:]
        half = jnp.minimum(group, 1)

        @pl.loop(0, width // broad)
        def _(at):
            cols = tile_of(at, broad)
            part = (cols_inner(d_gate, gate_w[cols]) + cols_inner(d_up, up_w[cols])).astype(BF)
            right_part[half, :, cols] = part[:rows]
            left_part[half, :, cols] = part[rows:]

        @pl.when(group == 0)
        def _():
            for copy in first_copies():
                copy.start()

        @pl.when(group == 1)
        def _():
            one, two = first_copies()
            one.wait_recv()
            right_got[0, :, ahead] = add_low(right_part[1, :, ahead], right_got[0, :, ahead])
            right_got[0, :, behind] = right_part[1, :, behind]
            two.wait_recv()
            left_got[0, :, behind] = add_low(left_part[1, :, behind], left_got[0, :, behind])
            left_got[0, :, ahead] = left_part[1, :, ahead]

        @pl.when(group >= 2)
        def _():
            one, two = later_copies(group - 1)
            one.wait_recv()
            right_got[group - 1] = add_low(right_part[1], right_got[group - 1])
            two.wait_recv()
            left_got[group - 1] = add_low(left_part[1], left_got[group - 1])

        @pl.when(group >= 1)
        def _():
            for copy in later_copies(group):
                copy.start()

        @pl.loop(0, width // broad)
        def _(at):
            cols = tile_of(at, broad)
            mlp_s[slot, :, cols] = matmul(hid, down_w[:, cols]).astype(BF)

        for copy in stores(group, slot):
            copy.start()

        @pl.when(group == 0)
        def _():
            mlp_far[...] = mlp_s[slot, pl.ds(0, rows)]

        @pl.when(group == 1)
        def _():
            mlp_next[0] = mlp_s[slot, pl.ds(0, rows)]
            mlp_next[1] = mlp_s[slot, pl.ds(rows, rows)]

        @pl.when(group == 2)
        def _():
            ahead_ref[...] = mlp_s[slot, pl.ds(0, rows)]
            behind_ref[...] = mlp_s[slot, pl.ds(rows, rows)]

    far_copies = [
        passing(mlp_far.at[:, ahead], mlp_got.at[0, :, ahead], far_sems, 0, right),
        passing(mlp_far.at[:, behind], mlp_got.at[1, :, behind], far_sems, 1, left),
    ]
    for copy in far_copies:
        copy.start()

    every = steps * 2 * rows

    def dmlp_copy(at, slot):
        return pltpu.make_async_copy(
            dmlp_s.at[slot], dmlp_hbm.at[tile_of(at // 2), tile_of(lax.rem(at, 2), hidden)], grad_sem.at[slot]
        )

    mlp_tiles = 2 * (width // tile)

    @pl.loop(0, mlp_tiles)
    def _(at):
        slot = lax.rem(at, 2)

        @pl.when(at >= 2)
        def _():
            dmlp_copy(at - 2, slot).wait()

        normed = n2_all[:, :, tile_of(at // 2)].reshape(every, tile)
        grads = grad_all[:, :, tile_of(lax.rem(at, 2), hidden)].reshape(every, hidden)
        dmlp_s[slot] = rows_inner(normed, grads).astype(BF)
        dmlp_copy(at, slot).start()

    wide = 512
    across = width // wide

    def ddown_copy(at, slot):
        return pltpu.make_async_copy(
            ddown_s.at[slot],
            ddown_hbm.at[tile_of(at // across, inner), tile_of(lax.rem(at, across), wide)],
            grad_sem.at[2 + slot],
        )

    down_tiles = across * (hidden // inner)

    @pl.loop(0, down_tiles)
    def _(at):
        slot = lax.rem(at, 2)

        @pl.when(at >= 2)
        def _():
            ddown_copy(at - 2, slot).wait()

        hid = hid_all[:, :, tile_of(at // across, inner)].reshape(every, inner)
        dy = dy_all[:, :, tile_of(lax.rem(at, across), wide)].reshape(every, wide)
        ddown_s[slot] = rows_inner(hid, dy).astype(BF)
        ddown_copy(at, slot).start()

    for copy in later_copies(steps - 1):
        copy.wait_recv()
    for flow, have, lack in ((0, ahead, behind), (1, behind, ahead)):
        far_copies[flow].wait_recv()
        mlp_got[flow, :, have] = add_low(mlp_got[flow, :, have], mlp_next[flow, :, have])
        mlp_got[flow, :, lack] = mlp_next[flow, :, lack]
    next_copies = [
        passing(mlp_got.at[0], mlp_got.at[2], far_sems, 2, right),
        passing(mlp_got.at[1], mlp_got.at[3], far_sems, 3, left),
    ]
    for copy in next_copies:
        copy.start()

    def collect(at, state):
        squares, mean = state
        cols = tile_of(at)
        dn2 = (
            left_part[0, :, cols].astype(F32)
            + right_got[steps - 1, :, cols].astype(F32)
            + left_got[steps - 1, :, cols].astype(F32)
        )
        dh1_ref[:, cols] = dn2
        h1 = h1_ref[:, cols]
        squares = squares + jnp.sum(h1 * h1, axis=1, keepdims=True)
        return squares, mean + jnp.sum(gain_ref[:, cols] * dn2 * h1, axis=1, keepdims=True)

    zero = jnp.zeros((rows, 1), F32)
    squares, mean = lax.fori_loop(0, width // tile, collect, (zero, zero))
    scale_own = lax.rsqrt(squares / width + EPSILON)
    pull = scale_own * scale_own * scale_own * (mean / width)

    @pl.loop(0, width // tile)
    def _(at):
        cols = tile_of(at)
        dn2, h1 = dh1_ref[:, cols], h1_ref[:, cols]
        dgain_ref[:, cols] = jnp.sum(dn2 * h1 * scale_own, axis=0, keepdims=True)
        dy = dy_all[0, pl.ds(rows, rows), cols].astype(F32)
        d_resid = dy + scale_own * (gain_ref[:, cols] * dn2) - h1 * pull
        dh1_ref[:, cols] = d_resid
        low_ref[:, cols] = d_resid.astype(BF)

    def da_copy(hop):
        return passing(
            da_part.at[hop], da_ref.at[span(place)], (da_send, da_recv), hop, member(hop)[1]
        )

    low = low_ref[...]

    @pl.loop(1, count)
    def _(hop):
        spot = member(hop)[0]
        da_part[hop] = cols_inner(low, out_w[tile_of(spot, size)]).astype(BF)
        da_copy(hop).start()

    da_ref[span(place)] = cols_inner(low, out_w[tile_of(place, size)]).astype(BF)

    @pl.loop(1, count)
    def _(hop):
        da_copy(hop).wait_recv()
        da_copy(hop).wait_send()

    for flow, held in ((0, ahead_ref), (1, behind_ref)):
        next_copies[flow].wait_recv()
        held[...] = add_low(held[...], mlp_got[2 + flow])
    for copy in (*far_copies, *next_copies, *first_copies()):
        copy.wait_send()
    for step in range(1, steps):
        for copy in later_copies(step):
            copy.wait_send()
    for group in range(steps - 2, steps):
        for copy in stores(group, group % 2):
            copy.wait()
    for at in range(2):
        dmlp_copy(mlp_tiles - 2 + at, (mlp_tiles + at) % 2).wait()
        ddown_copy(down_tiles - 2 + at, (down_tiles + at) % 2).wait()


def mlp_back(tokens, mixed, dy, gain, out_w, gate_w, up_w, down_top, down_low, collective_id):
    count = lax.axis_size("head")
    total, width = tokens.shape
    hidden = gate_w.shape[1]
    rows, steps = total // count, count // 2
    size = mixed.shape[1] // count
    inner = 256 if hidden % 256 == 0 else 128
    vmem = pl.BlockSpec(memory_space=pltpu.VMEM)
    hbm = pl.BlockSpec(memory_space=pl.ANY)

    def slots(many, tall, wide, dtype=BF):
        return pltpu.VMEM((many, tall, wide), dtype)

    def shape(*extent, dtype=BF):
        return jax.ShapeDtypeStruct(extent, dtype)

    dma = pltpu.SemaphoreType.DMA
    flops = 2 * total * width * (mixed.shape[1] + 9 * hidden)
    return pl.pallas_call(
        functools.partial(mlp_kernel, count),
        out_shape=[
            shape(total, width), shape(width, 2 * hidden), shape(hidden, width),
            shape(rows, width, dtype=F32), shape(rows, width, dtype=F32), shape(rows, width),
            shape(1, width, dtype=F32), shape(total, size), shape(rows, width), shape(rows, width),
        ],
        in_specs=[hbm] * 3 + [vmem] + [hbm] * 5,
        out_specs=[hbm] * 3 + [vmem] * 7,
        scratch_shapes=[
            slots(2, 2 * rows, width), slots(2, 2 * rows, mixed.shape[1]), slots(2, 2 * rows, width),
            pltpu.VMEM((2 * rows, width), F32),
            slots(steps, 2 * rows, width), slots(steps, 2 * rows, width),
            slots(steps, 2 * rows, hidden), slots(steps, 2 * rows, 2 * hidden),
            slots(2, 256, hidden), slots(2, inner, 512), slots(count, rows, size),
            pltpu.VMEM((rows, width), BF), slots(2, rows, width), slots(4, rows, width),
            slots(2, rows, width), slots(2, rows, width),
            slots(steps, rows, width), slots(steps, rows, width),
            *[pltpu.VMEM(weight.shape, BF) for weight in (out_w, gate_w, up_w)],
            pltpu.VMEM((hidden, width), BF),
            dma((2, 6)), dma((2, 2)), dma((4,)), dma((5,)), dma((count,)), dma((count,)),
            dma((count,)), dma((count,)), dma((4,)), dma((4,)),
        ],
        compiler_params=pltpu.CompilerParams(
            collective_id=collective_id, has_side_effects=True, vmem_limit_bytes=VMEM_LIMIT
        ),
        cost_estimate=pl.CostEstimate(flops=flops, bytes_accessed=40 << 20, transcendentals=0),
        name="mlp_back",
    )(tokens, mixed, dy, gain, out_w, gate_w, up_w, down_top, down_low)


def entry_kernel(
    count, batches, x_ref, w_ref, out_ref, gain_ref, seg_ref, down_ref,
    n1_hbm, q_ref, logit_ref, kv_ref, w_all, out_all, gain_all, seg_all, down_all,
    x_s, n1_ref, send_sem, recv_sem, local_sem, x_sem, n1_sem,
):
    steps = count // 2
    others = batches // 2
    rows, width = x_ref.shape
    depth = w_ref.shape[0]
    size, wide = out_ref.shape
    block = 256
    blocks = rows // block

    def x_copy(at):
        here = pl.ds(pl.multiple_of(at * block, block), block)
        return pltpu.make_async_copy(x_ref.at[here], x_s.at[here], x_sem.at[at])

    def n1_copy(at):
        here = pl.ds(pl.multiple_of(at * block, block), block)
        return pltpu.make_async_copy(n1_ref.at[here], n1_hbm.at[here], n1_sem.at[at])

    for at in range(blocks):
        x_copy(at).start()
    place, right, left = ring_setup(count)
    head = lax.axis_index("head")
    batch = lax.axis_index("batch")
    across, core, low = batch // 2, lax.rem(batch, 2), lax.rem(head, 2)
    twin = (across * 2 + 1 - core, head)
    mate = (batch, head + 1 - 2 * low)
    spots = [lax.rem(across + hop, others) for hop in range(others)]
    backs = [lax.rem(across + others - hop, others) for hop in range(others)]
    peers = [(spot * 2 + core, head) for spot in spots]
    far_peers = [(spot * 2 + 1 - core, head) for spot in spots]
    greet((twin, mate, right, left, *peers[1:], *far_peers[1:]))
    sems = (send_sem, recv_sem)
    slot = 0
    copies = []

    def go(source, target, device):
        nonlocal slot
        copy = send(source, target, sems, slot, device)
        slot += 1
        copies.append(copy)
        return copy

    def part(at, extent):
        return pl.ds(pl.multiple_of(at * extent, extent), extent)

    def both(view, own):
        out = [go(own, view(batch), peers[hop]) for hop in range(1, others)]
        return out, [go(own, view(batch), twin)]

    def pass_on(view, arrived):
        out = []
        for hop in range(1, others):
            arrived[hop - 1].wait_recv()
            there = view(backs[hop] * 2 + core)
            out.append(go(there, there, twin))
        return out

    local = []

    def stay(source, target):
        copy = pltpu.make_async_copy(source, target, local_sem.at[len(local)])
        copy.start()
        local.append(copy)

    def main_view(at):
        return w_all.at[part(at, depth), pl.ds(0, 3 * size)]

    def mate_view(at):
        return w_all.at[part(at, depth), pl.ds(3 * size, size)]

    def out_view(chunk, at):
        return out_all.at[part(chunk, size), part(at, wide)]

    small = []
    for own, whole in ((gain_ref, gain_all), (seg_ref, seg_all)):
        for device in (twin, *peers[1:], *far_peers[1:]):
            small.append(go(own, whole.at[batch], device))
        stay(own, whole.at[batch])
    from_mate = go(w_ref.at[:, pl.ds(2 * size, size)], mate_view(batch), mate)
    main_out, main_twin = both(main_view, w_ref)
    stay(w_ref, main_view(batch))
    out_peers = [go(out_ref, out_view(place, batch), peers[hop]) for hop in range(1, others)]
    stay(out_ref, out_view(place, batch))
    flows = [[None, None] for _ in range(others)]

    def ring(step):
        for hop in range(others):
            lane = spots[0] if hop == 0 else backs[hop]
            at = lane * 2 + core
            if step == 0 and hop:
                out_peers[hop - 1].wait_recv()
            for flow, chunk, device in ((0, place - step, right), (1, place + step, left)):
                if step:
                    flows[hop][flow].wait_recv()
                target = out_view(lax.rem(chunk + count, count), at)
                source = out_ref if step == 0 and hop == 0 else target
                if step == steps - 1:
                    cut = (pl.ds(flow * (size // 2), size // 2), slice(None))
                    source, target = source.at[cut], target.at[cut]
                flows[hop][flow] = go(source, target, device)

    for copy in small:
        copy.wait_recv()
    for copy in local[:2]:
        copy.wait()

    def normalize(at):
        here = part(at, block)
        x_copy(at).wait()

        def squares(tile, total):
            values = x_s[here, part(tile, 256)].astype(F32)
            return total + jnp.sum(values * values, axis=1, keepdims=True)

        total = lax.fori_loop(0, width // 256, squares, jnp.zeros((block, 1), F32))
        scale = lax.rsqrt(total / width + EPSILON)

        @pl.loop(0, batches)
        def _(owner):
            for tile in range(depth // 128):
                cols = pl.ds(pl.multiple_of(owner * depth + tile * 128, 128), 128)
                values = x_s[here, cols].astype(F32) * scale
                n1_ref[here, cols] = (values * gain_all[owner, pl.ds(tile, 1)]).astype(BF)

        n1_copy(at).start()

    middle = blocks // 2

    @pl.loop(0, middle)
    def _(at):
        normalize(at)

    from_mate.wait_recv()
    mate_out, mate_twin = both(mate_view, mate_view(batch))
    ring(0)

    def down_view(at):
        return down_all.at[:, part(at, down_ref.shape[1])]

    down_own = down_ref.at[pl.ds(0, down_ref.shape[0] // 2)]
    down_out, down_twin = both(down_view, down_own)
    stay(down_own, down_view(batch))

    @pl.loop(middle, blocks)
    def _(at):
        normalize(at)

    main_passed = pass_on(main_view, main_out)
    mate_passed = pass_on(mate_view, mate_out)
    for copy in (*main_twin, *mate_twin, *main_passed, *mate_passed):
        copy.wait_recv()
    for copy in local[2:]:
        copy.wait()

    def kv_view(at):
        return kv_ref.at[part(at, rows)]

    @pl.loop(0, blocks)
    def _(at):
        here = part(at, block)
        values = matmul(n1_ref[here], w_all[:, pl.ds(2 * size, 2 * size)])
        one, two = values[:, :size], values[:, size:]
        first = jnp.where(low == 0, one, two).astype(BF)
        second = jnp.where(low == 0, two, one).astype(BF)
        half = size // 2
        there = pl.ds(pl.multiple_of(batch * rows + at * block, block), block)
        kv_ref[there, pl.ds(0, size)] = jnp.concatenate([first[:, :half], second[:, :half]], 1)
        kv_ref[there, pl.ds(size, size)] = jnp.concatenate([first[:, half:], second[:, half:]], 1)

    kv_out, kv_twin = both(kv_view, kv_view(batch))
    ring(1)

    @pl.loop(0, blocks)
    def _(at):
        here = part(at, block)
        values = matmul(n1_ref[here], w_all[:, pl.ds(0, 2 * size)])
        q_ref[here] = values[:, :size].astype(BF)
        logit_ref[here] = values[:, size:]

    for step in range(2, steps):
        ring(step)
    down_passed = pass_on(down_view, down_out)
    kv_passed = pass_on(kv_view, kv_out)
    for pair in flows:
        for copy in pair:
            copy.wait_recv()
    swaps = []
    for hop in range(others):
        there = out_all.at[:, part(spots[hop] * 2 + core, wide)]
        swaps.append(go(there, there, twin))
    for copy in (*kv_twin, *kv_passed, *swaps, *down_twin, *down_passed):
        copy.wait_recv()
    for copy in copies:
        copy.wait_send()
    for at in range(blocks):
        n1_copy(at).wait()


def entry(tokens, w_shard, w_out, gains, segments, w_down, collective_id):
    count = lax.axis_size("head")
    batches = lax.axis_size("batch")
    others = batches // 2
    rows, width = tokens.shape
    size, wide = w_out.shape
    vmem = pl.BlockSpec(memory_space=pltpu.VMEM)
    hbm = pl.BlockSpec(memory_space=pl.ANY)
    slots = 6 * batches + others * (count + 3)
    sems = pltpu.SemaphoreType.DMA((slots,))
    return pl.pallas_call(
        functools.partial(entry_kernel, count, batches),
        out_shape=[
            jax.ShapeDtypeStruct((rows, width), BF),
            jax.ShapeDtypeStruct((rows, size), BF),
            jax.ShapeDtypeStruct((rows, size), F32),
            jax.ShapeDtypeStruct((batches * rows, 2 * size), BF),
            jax.ShapeDtypeStruct((width, 4 * size), BF),
            jax.ShapeDtypeStruct((count * size, batches * wide), BF),
            jax.ShapeDtypeStruct((batches, *gains.shape), F32),
            jax.ShapeDtypeStruct((batches, *segments.shape), jnp.int32),
            jax.ShapeDtypeStruct((w_down.shape[0] // 2, batches * w_down.shape[1]), BF),
        ],
        in_specs=[hbm] + [vmem] * 5,
        out_specs=[hbm] + [vmem] * 4 + [hbm] + [vmem] * 2 + [hbm],
        scratch_shapes=[
            pltpu.VMEM((rows, width), BF), pltpu.VMEM((rows, width), BF),
            sems, sems, pltpu.SemaphoreType.DMA((5,)),
            pltpu.SemaphoreType.DMA((rows // 256,)), pltpu.SemaphoreType.DMA((rows // 256,)),
        ],
        compiler_params=pltpu.CompilerParams(
            collective_id=collective_id, has_side_effects=True, vmem_limit_bytes=VMEM_LIMIT
        ),
        name="entry",
    )(tokens, w_shard, w_out, gains, segments, w_down)


KEY_BLOCK = 512
QUERY_BLOCK = 640


def key_range(start_ref, base, query_block):
    first = query_block * QUERY_BLOCK
    lowest = start_ref[first]
    highest = start_ref[first + QUERY_BLOCK - 1]
    begin = lowest // KEY_BLOCK
    end = (base + first + QUERY_BLOCK - 1) // KEY_BLOCK + 1
    full_begin = jnp.minimum((highest + KEY_BLOCK - 1) // KEY_BLOCK, end)
    full_end = jnp.maximum((base + first + 1) // KEY_BLOCK, full_begin)
    return begin, full_begin, full_end, end


def allowed_pairs(key_block, start_row, base_row):
    shape = (KEY_BLOCK, QUERY_BLOCK)
    key_pos = key_block * KEY_BLOCK + lax.broadcasted_iota(jnp.int32, shape, 0)
    query_pos = base_row + lax.broadcasted_iota(jnp.int32, shape, 1)
    return (key_pos >= start_row) & (key_pos <= query_pos)


def attend_kernel(
    scale, start_sm, base_sm, q_ref, kv_ref, start_ref, logit_ref, o_ref, a_ref, lse_ref
):
    base = base_sm[0]
    size = q_ref.shape[1]
    factor = scale * math.log2(math.e)

    @pl.loop(0, q_ref.shape[0] // QUERY_BLOCK)
    def _(block):
        rows = pl.ds(pl.multiple_of(block * QUERY_BLOCK, QUERY_BLOCK), QUERY_BLOCK)
        queries = q_ref[rows]
        start_row = start_ref[:, rows]
        begin, full_begin, full_end, end = key_range(start_sm, base, block)

        def step(masked, at, state):
            old_max, old_sum, total = state
            keys = pl.ds(pl.multiple_of(at * KEY_BLOCK, KEY_BLOCK), KEY_BLOCK)
            scores = cols_inner(kv_ref[keys, :size], queries)
            if masked:
                allowed = allowed_pairs(at, start_row, base + block * QUERY_BLOCK)
                scores = jnp.where(allowed, scores, MASKED)
            new_max = jnp.maximum(old_max, jnp.max(scores, axis=0, keepdims=True))
            keep = jnp.exp2((old_max - new_max) * factor)
            weights = jnp.exp2(scores * factor - new_max * factor)
            new_sum = old_sum * keep + jnp.sum(weights, axis=0, keepdims=True)
            total = total * keep + rows_inner(kv_ref[keys, size:], weights.astype(BF))
            return new_max, new_sum, total

        state = (
            jnp.full((1, QUERY_BLOCK), MASKED, F32),
            jnp.zeros((1, QUERY_BLOCK), F32),
            jnp.zeros((size, QUERY_BLOCK), F32),
        )
        state = lax.fori_loop(begin, full_begin, functools.partial(step, True), state)
        state = lax.fori_loop(full_begin, full_end, functools.partial(step, False), state)
        state = lax.fori_loop(full_end, end, functools.partial(step, True), state)
        run_max, run_sum, total = state
        lse_ref[:, rows] = run_max * factor + jnp.log2(run_sum)
        attended = (total / run_sum).T
        o_ref[rows] = attended
        a_ref[rows] = (attended * jax.nn.sigmoid(logit_ref[rows])).astype(BF)


def attend_back_kernel(
    scale, start_sm, base_sm, q_ref, kv_ref, start_ref, logit_ref, o_ref, da_ref, lse_ref,
    dq_ref, dg_ref, dkv_ref, dk_acc, dv_acc,
):
    base = base_sm[0]
    size = q_ref.shape[1]
    factor = scale * math.log2(math.e)
    dk_acc[...] = jnp.zeros_like(dk_acc)
    dv_acc[...] = jnp.zeros_like(dv_acc)

    @pl.loop(0, q_ref.shape[0] // QUERY_BLOCK)
    def _(block):
        rows = pl.ds(pl.multiple_of(block * QUERY_BLOCK, QUERY_BLOCK), QUERY_BLOCK)
        queries = q_ref[rows]
        start_row = start_ref[:, rows]
        lse = lse_ref[:, rows]
        gate = jax.nn.sigmoid(logit_ref[rows])
        attended = o_ref[rows]
        d_mixed = da_ref[rows].astype(F32)
        d_attended = (d_mixed * gate).astype(BF)
        dg_ref[rows] = (d_mixed * attended * gate * (1.0 - gate)).astype(BF)
        delta = jnp.sum((d_attended.astype(F32) * attended).T, axis=0, keepdims=True)
        begin, full_begin, full_end, end = key_range(start_sm, base, block)

        def step(masked, at, d_queries):
            keys = pl.ds(pl.multiple_of(at * KEY_BLOCK, KEY_BLOCK), KEY_BLOCK)
            key_block = kv_ref[keys, :size]
            probs = jnp.exp2(cols_inner(key_block, queries) * factor - lse)
            if masked:
                allowed = allowed_pairs(at, start_row, base + block * QUERY_BLOCK)
                probs = jnp.where(allowed, probs, 0.0)
            d_probs = cols_inner(kv_ref[keys, size:], d_attended)
            d_scores = (probs * (d_probs - delta) * scale).astype(BF)
            dv_acc[keys] += matmul(probs.astype(BF), d_attended)
            dk_acc[keys] += matmul(d_scores, queries)
            return d_queries + rows_inner(key_block, d_scores)

        d_queries = jnp.zeros((size, QUERY_BLOCK), F32)
        d_queries = lax.fori_loop(begin, full_begin, functools.partial(step, True), d_queries)
        d_queries = lax.fori_loop(full_begin, full_end, functools.partial(step, False), d_queries)
        d_queries = lax.fori_loop(full_end, end, functools.partial(step, True), d_queries)
        dq_ref[rows] = d_queries.T.astype(BF)

    @pl.loop(0, kv_ref.shape[0] // KEY_BLOCK)
    def _(at):
        keys = pl.ds(pl.multiple_of(at * KEY_BLOCK, KEY_BLOCK), KEY_BLOCK)
        dk, dv = dk_acc[keys].astype(BF), dv_acc[keys].astype(BF)
        half = size // 2
        dkv_ref[keys, :size] = jnp.concatenate([dk[:, :half], dv[:, :half]], axis=1)
        dkv_ref[keys, size:] = jnp.concatenate([dk[:, half:], dv[:, half:]], axis=1)


def tail_kernel(
    count, batches, dq_ref, dg_ref, dkv_ref, w_ref, gain_ref, dh1_ref, second_ref,
    low_ref, h1_ref, ahead_ref, behind_ref, n1_ref, x_hbm, mixed_hbm, mlp_hbm,
    out_all, tok_all, gains_ref, wout_own, din_ref, key_ref, value_ref,
    part_ref, tok_ref, got, wout_got, gain_own, gain_got, gain_mid, gain_heads,
    din_s, din_got, din_x, wout_s, wout_twin, wout_x,
    cat_ref, out_s, out_got, core_got, x_first, x_second, y_first, y_second, held, n1_s,
    x_ref, mixed_ref, mlp_ref, mlp_next, send_sem, recv_sem, local_sem,
):
    steps = count // 2
    rows, width = x_ref.shape
    depth = cat_ref.shape[1]
    tall, size = dq_ref.shape
    tile = 256
    place, right, left = ring_setup(count)
    batch, head = lax.axis_index("batch"), lax.axis_index("head")
    others = [lax.rem(batch + hop, batches) for hop in range(1, batches)]
    members = [(batch, ring_head(lax.rem(place + hop, count), count)) for hop in range(1, count)]
    greet((*members, *[(other, head) for other in others]))
    sems = (send_sem, recv_sem)
    slot = 0
    copies = []

    def go(source, target, device):
        nonlocal slot
        copy = send(source, target, sems, slot, device)
        slot += 1
        copies.append(copy)
        return copy

    across, core = batch // 2, lax.rem(batch, 2)
    spots = [lax.rem(across + hop, batches // 2) for hop in range(batches // 2)]
    order = list(range(1, batches // 2)) + [0]
    twin = (across * 2 + 1 - core, head)

    def scatter_swap(view, held):
        return [go(view(2 * spots[hop] + 1 - core), held.at[spots[hop]], twin) for hop in order]

    def add_tiles(target, one, other):
        @pl.loop(0, target.shape[0] // 128)
        def _(at):
            lines = pl.ds(pl.multiple_of(at * 128, 128), 128)
            total = one[lines].astype(F32) + other[lines].astype(F32)
            target[lines] = total.astype(target.dtype)

    def scatter_cross(view, held, crossed, arriving):
        out = []
        for copy, hop in zip(arriving, order):
            copy.wait_recv()
            spot = spots[hop]
            add_tiles(held.at[spot], held.at[spot], view(2 * spot + core))
            if hop:
                out.append(go(held.at[spot], crossed.at[hop - 1], (spot * 2 + core, head)))
        return out

    def scatter_end(held, crossed, arriving, target):
        for hop, copy in enumerate(arriving):
            copy.wait_recv()
            last = hop == len(arriving) - 1
            add_tiles(target if last else held.at[across], held.at[across], crossed.at[hop])

    def wout_view(at):
        wide = width // batches
        return wout_s.at[:, pl.ds(pl.multiple_of(at * wide, wide), wide)]

    def din_view(at):
        tall = din_ref.shape[0]
        return din_s.at[pl.ds(pl.multiple_of(at * tall, tall), tall)]

    def span(owner, extent):
        return pl.ds(pl.multiple_of(lax.rem(owner + count, count) * extent, extent), extent)

    def compute(owner):
        here = span(owner, rows)
        values = cat_ref[here]

        @pl.loop(0, width // tile)
        def _(at):
            cols = pl.ds(pl.multiple_of(at * tile, tile), tile)
            part_ref[here, cols] = cols_inner(values, w_ref[cols, pl.ds(0, depth)]).astype(BF)

    def gather(own, whole, step, last, start=0, many=1):
        out = []
        span_wide = width // many
        for flow, chunk, device in ((0, place - step, right), (1, place + step, left)):
            if last:
                last[flow].wait_recv()
            target = whole.at[lax.rem(chunk + count, count)]
            source = target if step else own
            cut = (slice(None), pl.ds(start, span_wide))
            if step == steps - 1:
                cut = (slice(None), pl.ds(start + flow * (span_wide // 2), span_wide // 2))
            out.append(go(source.at[cut], target.at[cut], device))
        return out

    def gather_halves(own, whole, step, last):
        last = last or (None, None)
        return [gather(own, whole, step, last[at], at * (width // 2), 2) for at in range(2)]

    def reduce(parts, held, step, last):
        extent, side = held.shape[2], held.shape[3] // 2
        out = []
        for flow, owner, device in (
            (0, place + steps - step, right),
            (1, place - steps + step, left),
        ):
            have = pl.ds(flow * side, side)
            lack = pl.ds((1 - flow) * side, side)
            mine = parts.at[span(owner, extent)]
            if step == 0:
                out.append(go(mine.at[:, have], held.at[flow, 0, :, have], device))
                continue
            last[flow].wait_recv()
            if step == 1:
                held[flow, 0, :, have] = add_low(held[flow, 0, :, have], mine[:, have])
                held[flow, 0, :, lack] = mine[:, lack]
            else:
                held[flow, step - 1] = add_low(held[flow, step - 1], mine[...])
            out.append(go(held.at[flow, step - 1], held.at[flow, step], device))
        return out

    low = lax.rem(head, 2)
    mate = (batch, head + 1 - 2 * low)
    peers = [(spot * 2 + core, head) for spot in spots]
    mine = pl.ds(pl.multiple_of(low * size, size), size)
    given = pl.ds(pl.multiple_of((1 - low) * size, size), size)
    top, bottom = pl.ds(0, tall // 2), pl.ds(tall // 2, tall // 2)
    fresh = pl.ds(2 * size, size)

    def keys_of(at):
        return dkv_ref.at[pl.ds(pl.multiple_of(at * tall, tall), tall)]

    def normed_copy(at, slot):
        cols = pl.ds(pl.multiple_of(at * tile, tile), tile)
        return pltpu.make_async_copy(n1_ref.at[:, cols], n1_s.at[slot], local_sem.at[2 + slot])

    own_rows = pl.ds(pl.multiple_of(place * rows, rows), rows)
    fetches = [
        pltpu.make_async_copy(source.at[own_rows], target, local_sem.at[4 + index])
        for index, (source, target) in enumerate(
            ((mixed_hbm, mixed_ref), (mlp_hbm, mlp_ref), (x_hbm, x_ref))
        )
    ]
    nexts = [
        pltpu.make_async_copy(mlp_hbm.at[span(place + shift, rows)], mlp_next.at[at], local_sem.at[7 + at])
        for at, shift in enumerate((1, -1))
    ]
    for copy in (*nexts, *fetches):
        copy.start()
    for at in range(2):
        normed_copy(at, at).start()
    swaps = scatter_swap(keys_of, core_got)
    last_sums = []
    for at, (held_part, device) in enumerate(((ahead_ref, right), (behind_ref, left))):
        nexts[at].wait()
        mlp_next[at] = add_low(mlp_next[at], held_part[...])
        last_sums.append(go(mlp_next.at[at], out_got.at[at], device))
    cat_ref[:, pl.ds(0, size)] = dq_ref[...]
    cat_ref[:, pl.ds(size, size)] = dg_ref[...]
    for copy in fetches:
        copy.wait()

    @pl.loop(0, width // tile)
    def _(at):
        cols = pl.ds(pl.multiple_of(at * tile, tile), tile)
        wout_s[:, cols] = rows_inner(mixed_ref[...], low_ref[:, cols]).astype(BF)

    tops, bottoms = [], []
    for copy, hop in zip(swaps, order):
        copy.wait_recv()
        spot = spots[hop]
        add_tiles(core_got.at[spot], core_got.at[spot], keys_of(2 * spot + core))
        bottoms.append(go(core_got.at[spot, bottom, given], y_first.at[spot], mate))
        if hop:
            tops.append(go(core_got.at[spot, top], x_first.at[hop - 1], peers[hop]))
    wouts = scatter_swap(wout_view, wout_twin)
    for copy in last_sums:
        copy.wait_recv()
    out_s[...] = (
        h1_ref[...] + mlp_ref[...].astype(F32) + out_got[0].astype(F32) + out_got[1].astype(F32)
    ).astype(BF)
    keep_out = pltpu.make_async_copy(out_s, out_all.at[place], local_sem.at[0])
    keep_out.start()
    outs = gather(out_s, out_all, 0, None)
    total = core_got[across, top].astype(F32)
    for hop, copy in enumerate(tops):
        copy.wait_recv()
        total = total + x_first[hop].astype(F32)
    held[...] = total.astype(BF)
    last = go(held.at[:, given], y_second, mate)
    ends = []
    for copy, hop in zip(bottoms, order):
        copy.wait_recv()
        spot = spots[hop]
        y_first[spot] = add_low(y_first[spot], core_got[spot, bottom, mine])
        if hop:
            ends.append(go(y_first.at[spot], x_second.at[hop - 1], peers[hop]))
    last.wait_recv()
    cat_ref[top, fresh] = add_low(held[:, mine], y_second[...])
    total = y_first[across].astype(F32)
    for hop, copy in enumerate(ends):
        copy.wait_recv()
        total = total + x_second[hop].astype(F32)
    cat_ref[bottom, fresh] = total.astype(BF)

    compute(place + steps)
    sums = reduce(part_ref, got, 0, None)
    outs = gather(out_s, out_all, 1, outs)

    @pl.loop(1, count)
    def _(hop):
        compute(place + steps + hop)

    @pl.loop(0, width // tile)
    def _(at):
        slot = lax.rem(at, 2)
        normed_copy(at, slot).wait()
        cols = pl.ds(pl.multiple_of(at * tile, tile), tile)
        din_s[cols] = rows_inner(n1_s[slot], cat_ref[...]).astype(BF)

        @pl.when(at + 2 < width // tile)
        def _():
            normed_copy(at + 2, slot).start()

    dins = scatter_swap(din_view, din_got)
    for step in range(1, steps):
        sums = reduce(part_ref, got, step, sums)
        if 2 <= step < steps - 1:
            outs = gather(out_s, out_all, step, outs)
        if step == 1:
            wouts = scatter_cross(wout_view, wout_twin, wout_x, wouts)
            dins = scatter_cross(din_view, din_got, din_x, dins)
    for copy in sums:
        copy.wait_recv()

    def tile_of(at):
        return pl.ds(pl.multiple_of(at * tile, tile), tile)

    def total(cols):
        return (
            part_ref[span(place, rows), cols].astype(F32)
            + got[0, steps - 1, :, cols].astype(F32)
            + got[1, steps - 1, :, cols].astype(F32)
        )

    def collect(at, state):
        squares, mean = state
        cols = tile_of(at)
        x = x_ref[:, cols].astype(F32)
        squares = squares + jnp.sum(x * x, axis=1, keepdims=True)
        return squares, mean + jnp.sum(gain_ref[:, cols] * total(cols) * x, axis=1, keepdims=True)

    zero = jnp.zeros((rows, 1), F32)
    squares, mean = lax.fori_loop(0, width // tile, collect, (zero, zero))
    scale = lax.rsqrt(squares / width + EPSILON)
    pull = scale * scale * scale * (mean / width)

    @pl.loop(0, width // tile)
    def _(at):
        cols = tile_of(at)
        x, dn1 = x_ref[:, cols].astype(F32), total(cols)
        gain_own[pl.ds(0, 1), cols] = jnp.sum(dn1 * x * scale, axis=0, keepdims=True)
        gain_own[pl.ds(1, 1), cols] = second_ref[:, cols]
        tok_ref[:, cols] = (dh1_ref[:, cols] + scale * (gain_ref[:, cols] * dn1) - x * pull).astype(BF)

    keep_tok = pltpu.make_async_copy(tok_ref, tok_all.at[place], local_sem.at[1])
    keep_tok.start()
    toks = gather_halves(tok_ref, tok_all, 0, None)
    outs = gather(out_s, out_all, steps - 1, outs)
    wout_part = wout_twin.at[across]
    scatter_end(wout_twin, wout_x, wouts, wout_part)
    wsums = reduce(wout_part, wout_got, 0, None)
    scatter_end(din_got, din_x, dins, din_ref)
    narrow = din_ref[:, pl.ds(2 * size, size)].T
    key_ref[...] = narrow[: size // 2]
    value_ref[...] = narrow[size // 2 :]
    wide = width // batches

    def slice_of(at):
        return pl.ds(pl.multiple_of(at * wide, wide), wide)

    gains = [
        go(gain_own.at[:, slice_of(other)], gain_got.at[hop], (other, head))
        for hop, other in enumerate(others)
    ]
    toks = gather_halves(tok_ref, tok_all, 1, toks)
    wsums = reduce(wout_part, wout_got, 1, wsums)
    middle = gain_own[:, slice_of(batch)]
    for hop, copy in enumerate(gains):
        copy.wait_recv()
        middle = middle + gain_got[hop]
    gain_mid[...] = middle
    gain_heads[place] = middle
    gains = [go(gain_mid, gain_heads.at[place], member) for member in members]
    for step in range(2, steps):
        toks = gather_halves(tok_ref, tok_all, step, toks)
        wsums = reduce(wout_part, wout_got, step, wsums)
    for copy in gains:
        copy.wait_recv()
    middle = gain_heads[0]
    for at in range(1, count):
        middle = middle + gain_heads[at]
    gains_ref[...] = middle
    for copy in (*wsums, *outs):
        copy.wait_recv()
    wout_own[...] = (
        wout_part[span(place, wout_own.shape[0])].astype(F32)
        + wout_got[0, steps - 1].astype(F32)
        + wout_got[1, steps - 1].astype(F32)
    )
    for copy in (*toks[0], *toks[1]):
        copy.wait_recv()
    for copy in copies:
        copy.wait_send()
    keep_out.wait()
    keep_tok.wait()


def tail(arrays, collective_id):
    d_queries, tokens, mixed = arrays[0], arrays[-3], arrays[-2]
    count = lax.axis_size("head")
    batches = lax.axis_size("batch")
    steps = count // 2
    rows, width = tokens.shape[0] // count, tokens.shape[1]
    others = batches // 2
    size, wide = mixed.shape[1] // count, width // batches
    tall, head_size = d_queries.shape
    depth = 3 * head_size
    vmem = pl.BlockSpec(memory_space=pltpu.VMEM)
    hbm = pl.BlockSpec(memory_space=pl.ANY)
    whole = (count, rows, width)
    sems = pltpu.SemaphoreType.DMA((6 * count + 6 * batches,))
    gains = (2, width // batches)
    return pl.pallas_call(
        functools.partial(tail_kernel, count, batches),
        out_shape=[
            jax.ShapeDtypeStruct(whole, BF),
            jax.ShapeDtypeStruct(whole, BF),
            jax.ShapeDtypeStruct(gains, F32),
            jax.ShapeDtypeStruct((size, wide), F32),
            jax.ShapeDtypeStruct((wide, depth), F32),
            jax.ShapeDtypeStruct((size // 2, wide), F32),
            jax.ShapeDtypeStruct((size // 2, wide), F32),
        ],
        in_specs=[vmem] * 11 + [hbm] * 4,
        out_specs=[hbm] * 2 + [vmem] * 5,
        scratch_shapes=[
            pltpu.VMEM((count * rows, width), BF),
            pltpu.VMEM((rows, width), BF),
            pltpu.VMEM((2, steps, rows, width), BF),
            pltpu.VMEM((2, steps, size, wide), BF),
            pltpu.VMEM((2, width), F32),
            pltpu.VMEM((batches - 1, *gains), F32),
            pltpu.VMEM(gains, F32),
            pltpu.VMEM((count, *gains), F32),
            pltpu.VMEM((width, depth), BF),
            pltpu.VMEM((others, wide, depth), BF),
            pltpu.VMEM((others - 1, wide, depth), BF),
            pltpu.VMEM((count * size, width), BF),
            pltpu.VMEM((others, count * size, wide), BF),
            pltpu.VMEM((others - 1, count * size, wide), BF),
            pltpu.VMEM((tall, depth), BF),
            pltpu.VMEM((rows, width), BF),
            pltpu.VMEM((2, rows, width), BF),
            pltpu.VMEM((others, tall, 2 * head_size), BF),
            pltpu.VMEM((others - 1, tall // 2, 2 * head_size), BF),
            pltpu.VMEM((others - 1, tall // 2, head_size), BF),
            pltpu.VMEM((others, tall // 2, head_size), BF),
            pltpu.VMEM((tall // 2, head_size), BF),
            pltpu.VMEM((tall // 2, 2 * head_size), BF),
            pltpu.VMEM((2, tall, 256), BF),
            pltpu.VMEM((rows, width), BF),
            pltpu.VMEM((rows, mixed.shape[1]), BF),
            pltpu.VMEM((rows, width), BF),
            pltpu.VMEM((2, rows, width), BF),
            sems,
            sems,
            pltpu.SemaphoreType.DMA((9,)),
        ],
        compiler_params=pltpu.CompilerParams(
            collective_id=collective_id, has_side_effects=True, vmem_limit_bytes=VMEM_LIMIT
        ),
        cost_estimate=pl.CostEstimate(
            flops=4 * count * rows * width * depth, bytes_accessed=400 << 20, transcendentals=0
        ),
        name="tail",
    )(*arrays)


def finish_kernel(
    out_hbm, tok_hbm, mlp_ref, down_ref, in_ref, gains_ref, key_ref, value_ref, wout_ref,
    output, d_tokens, mgate, mup, down, query, gate, first, second, key, value, wout,
    held, load_sem, store_sem,
):
    count, rows = out_hbm.shape[:2]
    loads, stores = [], []
    for index, (source, target) in enumerate(((out_hbm, output), (tok_hbm, d_tokens))):
        for at in range(count):
            slot = index * count + at
            loads.append(pltpu.make_async_copy(source.at[at], held.at[slot], load_sem.at[slot]))
            stores.append(
                pltpu.make_async_copy(
                    held.at[slot], target.at[pl.ds(at * rows, rows)], store_sem.at[slot]
                )
            )
    for copy in loads:
        copy.start()
    hidden = mgate.shape[1]
    size = query.shape[1]

    def convert(target, source, start):
        tall = 32

        @pl.loop(0, target.shape[0] // tall)
        def _(at):
            lines = pl.ds(pl.multiple_of(at * tall, tall), tall)
            target[lines] = source[lines, pl.ds(start, target.shape[1])].astype(target.dtype)

    for load, store in zip(loads, stores):
        load.wait()
        store.start()
    convert(mgate, mlp_ref, 0)
    convert(mup, mlp_ref, hidden)
    convert(down, down_ref, 0)
    convert(query, in_ref, 0)
    convert(gate, in_ref, size)
    key[...] = key_ref[...]
    value[...] = value_ref[...]
    wout[...] = wout_ref[...]
    first[...] = gains_ref[pl.ds(0, 1)]
    second[...] = gains_ref[pl.ds(1, 1)]
    for copy in stores:
        copy.wait()


def finish(output, d_tokens, d_mlp, d_down, d_in, gains, *rest):
    count, rows, width = output.shape
    tall, hidden = d_mlp.shape[0], d_mlp.shape[1] // 2
    down_rows, wide = d_down.shape
    size = d_in.shape[1] // 3
    vmem = pl.BlockSpec(memory_space=pltpu.VMEM)
    hbm = pl.BlockSpec(memory_space=pl.ANY)

    def shape(*extent, dtype=F32):
        return jax.ShapeDtypeStruct(extent, dtype)

    return pl.pallas_call(
        finish_kernel,
        out_shape=[
            shape(count * rows, width, dtype=BF), shape(count * rows, width, dtype=BF),
            shape(tall, hidden), shape(tall, hidden), shape(down_rows, wide),
            shape(tall, size), shape(tall, size),
            shape(1, wide), shape(1, wide), *[shape(*a.shape) for a in rest],
        ],
        in_specs=[hbm] * 2 + [vmem] * 7,
        out_specs=[hbm] * 2 + [vmem] * 10,
        scratch_shapes=[
            pltpu.VMEM((2 * count, rows, width), BF),
            pltpu.SemaphoreType.DMA((2 * count,)),
            pltpu.SemaphoreType.DMA((2 * count,)),
        ],
        compiler_params=pltpu.CompilerParams(vmem_limit_bytes=VMEM_LIMIT),
        name="finish",
    )(output, d_tokens, d_mlp, d_down, d_in, gains, *rest)


def local_call(kernel, scalars, arrays, outs, scratch, flops, name):
    vmem = pl.BlockSpec(memory_space=pltpu.VMEM)
    smem = pl.BlockSpec(memory_space=pltpu.SMEM)
    return pl.pallas_call(
        kernel,
        out_shape=outs,
        in_specs=[smem] * len(scalars) + [vmem] * len(arrays),
        out_specs=[vmem] * len(outs),
        scratch_shapes=scratch,
        compiler_params=pltpu.CompilerParams(vmem_limit_bytes=VMEM_LIMIT),
        cost_estimate=pl.CostEstimate(flops=flops, bytes_accessed=8 << 20, transcendentals=0),
        name=name,
    )(*scalars, *arrays)


def ring_routes(count):
    spots = [ring_head(at, count) for at in range(count)]
    right = [(spots[at], spots[(at + 1) % count]) for at in range(count)]
    left = [(spots[at], spots[at - 1]) for at in range(count)]
    return right, left


def add_low(one, other):
    return (one.astype(F32) + other.astype(F32)).astype(BF)


def flow_steps(part, going, coming):
    count = lax.axis_size("head")
    place = ring_place(lax.axis_index("head"), count)
    right, left = ring_routes(count)
    rows = part.shape[0] // count
    steps = count // 2

    def mine(owner):
        return lax.dynamic_slice_in_dim(part, lax.rem(owner + count, count) * rows, rows, 0)

    for step in range(2, steps - 1):
        going = lax.ppermute(going, "head", right)
        coming = lax.ppermute(coming, "head", left)
        if step < steps - 2:
            going = add_low(going, mine(place + steps - 1 - step))
            coming = add_low(coming, mine(place - steps + 1 + step))
    return going, coming


def matmul(left, right):
    return jnp.dot(left, right, preferred_element_type=F32)


def rows_inner(left, right):
    return lax.dot_general(left, right, (((0,), (0,)), ((), ())), preferred_element_type=F32)


def cols_inner(left, right):
    return lax.dot_general(left, right, (((1,), (1,)), ((), ())), preferred_element_type=F32)


def rms_scale(values):
    return lax.rsqrt(jnp.mean(values * values, axis=1, keepdims=True) + EPSILON)


def per_device(
    tokens,
    segment_ids,
    norm1_gain,
    w_query,
    w_key,
    w_value,
    w_gate,
    w_out,
    norm2_gain,
    w_mlp_gate,
    w_mlp_up,
    w_down,
    out_grad,
):
    heads = lax.axis_size("head")
    batches = lax.axis_size("batch")
    row_count, width = tokens.shape
    head_size = w_query.shape[1]
    half = w_key.shape[1]
    chunk = row_count // heads
    me = ring_place(lax.axis_index("head"), heads)
    scale_factor = 1.0 / math.sqrt(head_size)

    w_shard = jnp.concatenate([w_query, w_gate, w_key, w_value], axis=1)
    gains = jnp.concatenate([norm1_gain, norm2_gain]).reshape(-1, 128).astype(F32)
    normed_one, queries, gate_logit, kv_all, w_in, out_full, gains, seg_all, down_top = entry(
        tokens, w_shard, w_out, gains, segment_ids.reshape(-1, 128), w_down, 1
    )
    gains, w_mlp_gate = lax.optimization_barrier((gains, w_mlp_gate))
    seg_all = seg_all.reshape(-1)
    gains = gains.reshape(batches, 2, -1).transpose(1, 0, 2).reshape(2, width)
    gain_one, gain_two = gains[0], gains[1]
    mgate_full = lax.all_gather(w_mlp_gate, "batch", axis=0, tiled=True)

    base = lax.axis_index("batch") * row_count
    ids = jnp.arange(DOCUMENTS, dtype=jnp.int32)
    below = jnp.sum((seg_all[None, :] < ids[:, None]).astype(jnp.int32), axis=1)
    starts = jnp.sum(jnp.where(segment_ids[None, :] == ids[:, None], below[:, None], 0), axis=0)
    scalars = (starts, base.reshape(1))
    pair_flops = 4 * row_count * kv_all.shape[0] * head_size
    attended, mixed, lse = local_call(
        functools.partial(attend_kernel, scale_factor),
        scalars,
        (queries, kv_all, starts[None], gate_logit),
        [
            jax.ShapeDtypeStruct((row_count, head_size), F32),
            jax.ShapeDtypeStruct((row_count, head_size), BF),
            jax.ShapeDtypeStruct((1, row_count), F32),
        ],
        [],
        pair_flops,
        "attend",
    )
    mixed_all, down_low, mup_full = spread(
        [mixed, w_down, w_mlp_up], (("head", "cols"), ("batch", "low"), ("batch", "rows")), 2
    )
    (
        mlp_part, d_mlp, d_down, resid_own, d_resid, d_resid_low, d_gain_two, d_mixed, going, coming,
    ) = mlp_back(
        tokens, mixed_all, out_grad, gain_two[None], out_full, mgate_full, mup_full, down_top, down_low, 3
    )
    hold = lax.optimization_barrier
    state = flow_steps(mlp_part, going, coming)

    d_queries, d_gate_logit, d_kv_all = local_call(
        functools.partial(attend_back_kernel, scale_factor),
        scalars,
        (queries, kv_all, starts[None], gate_logit, attended, d_mixed, lse),
        [
            jax.ShapeDtypeStruct((row_count, head_size), BF),
            jax.ShapeDtypeStruct((row_count, head_size), BF),
            jax.ShapeDtypeStruct(kv_all.shape, BF),
        ],
        [pltpu.VMEM((kv_all.shape[0], head_size), F32)] * 2,
        5 * pair_flops // 2,
        "attend_back",
    )
    d_down = lax.psum_scatter(d_down, "batch", scatter_dimension=1, tiled=True)
    d_mlp = lax.psum_scatter(d_mlp, "batch", scatter_dimension=0, tiled=True)
    output, d_tokens, d_gains, d_out, d_in, d_key, d_value = tail(
        (
            d_queries, d_gate_logit, d_kv_all, w_in, gain_one[None], d_resid, d_gain_two,
            d_resid_low, resid_own, *state, normed_one, tokens, mixed_all, mlp_part,
        ),
        5,
    )
    (
        output, d_tokens, d_mgate, d_mup, d_down, d_query, d_gate, d_one, d_two,
        d_key, d_value, d_out,
    ) = finish(output, d_tokens, d_mlp, d_down, d_in, d_gains, d_key, d_value, d_out)
    return (
        output,
        d_tokens,
        d_one.reshape(-1),
        d_query,
        d_key.T,
        d_value.T,
        d_gate,
        d_out,
        d_two.reshape(-1),
        d_mgate,
        d_mup,
        d_down,
    )


def solution(mesh):
    return jax.shard_map(
        per_device,
        mesh=mesh,
        in_specs=(
            P("batch", None),
            P("batch"),
            P("batch"),
            P("batch", "head"),
            P("batch", "head"),
            P("batch", "head"),
            P("batch", "head"),
            P("head", "batch"),
            P("batch"),
            P("batch", "head"),
            P("batch", "head"),
            P("head", "batch"),
            P("batch", None),
        ),
        out_specs=(
            P("batch", None),
            P("batch", None),
            P("batch"),
            P("batch", "head"),
            P("batch", "head"),
            P("batch", "head"),
            P("batch", "head"),
            P("head", "batch"),
            P("batch"),
            P("batch", "head"),
            P("batch", "head"),
            P("head", "batch"),
        ),
        check_vma=False,
    )
```

```python
import functools
import math

import jax
import jax.numpy as jnp
from jax import lax
from jax.experimental import pallas as pl
from jax.experimental.pallas import tpu as pltpu
from jax.sharding import PartitionSpec as P

EPSILON = 1e-06
MASKED = -1e30
DOCUMENTS = 7
BF = jnp.bfloat16
F32 = jnp.float32


MESH = pl.DeviceIdType.MESH
VMEM_LIMIT = 60 << 20


def ring_place(head, count):
    high, low = head // 2, head % 2
    return (1 - low) * high + low * (count - 1 - high)


def ring_head(place, count):
    low = place // (count // 2)
    high = (1 - low) * place + low * (count - 1 - place)
    return 2 * high + low


def ring_setup(count):
    batch = lax.axis_index("batch")
    place = ring_place(lax.axis_index("head"), count)
    right = (batch, ring_head(lax.rem(place + 1, count), count))
    left = (batch, ring_head(lax.rem(place + count - 1, count), count))
    return place, right, left


def greet(devices):
    barrier = pltpu.get_barrier_semaphore()
    for device in devices:
        pl.semaphore_signal(barrier, inc=1, device_id=device, device_id_type=MESH)
    pl.semaphore_wait(barrier, len(devices))


def send(source, target, sems, slot, device):
    copy = pltpu.make_async_remote_copy(
        src_ref=source,
        dst_ref=target,
        send_sem=sems[0].at[slot],
        recv_sem=sems[1].at[slot],
        device_id=device,
        device_id_type=MESH,
    )
    copy.start()
    return copy


def half_of(extent, flow):
    if extent[1] % 256:
        return (pl.ds(flow * (extent[0] // 2), extent[0] // 2), slice(None))
    return (slice(None), pl.ds(flow * (extent[1] // 2), extent[1] // 2))


def place_of(whole, own, chunk, form):
    rows, wide = own.shape[-2:]
    if form == "lead":
        return whole.at[chunk]
    if form == "rows":
        return whole.at[pl.ds(pl.multiple_of(chunk * rows, rows), rows)]
    return whole.at[:, pl.ds(pl.multiple_of(chunk * wide, wide), wide)]


def spread_kernel(count, batches, plans, *refs):
    steps = count // 2
    arrays = len(plans)
    own_refs, all_refs = list(refs[:arrays]), refs[arrays : 2 * arrays]
    for index, (_, form) in enumerate(plans):
        if form == "low":
            half = own_refs[index].shape[0] // 2
            own_refs[index] = own_refs[index].at[pl.ds(half, half)]
    send_sem, recv_sem, local_sem = refs[2 * arrays :]
    place, right, left = ring_setup(count)
    head = lax.axis_index("head")
    batch = lax.axis_index("batch")
    across, core = batch // 2, lax.rem(batch, 2)
    others = batches // 2
    twin = (across * 2 + 1 - core, head)
    peers = [(lax.rem(across + hop, others) * 2 + core, head) for hop in range(1, others)]
    ring = any(axis == "head" for axis, _ in plans)
    grid = any(axis == "batch" for axis, _ in plans)
    greet((right, left) * ring + (twin, *peers) * grid)
    sems = (send_sem, recv_sem)
    slot = 0
    waiting, arriving, local = [], [], []

    def go(source, target, device):
        nonlocal slot
        copy = send(source, target, sems, slot, device)
        slot += 1
        waiting.append(copy)
        return copy

    stages = []
    for index, (axis, form) in enumerate(plans):
        own, whole = own_refs[index], all_refs[index]
        spot = place if axis == "head" else batch
        copy = pltpu.make_async_copy(own, place_of(whole, own, spot, form), local_sem.at[index])
        copy.start()
        local.append(copy)
        if axis == "batch":
            stages.append(index)
    onward = []

    def stage():
        for copy, block in onward:
            copy.wait_recv()
            arriving.append(go(block, block, twin))
        onward.clear()
        if stages:
            index = stages.pop(0)
            own, whole, form = own_refs[index], all_refs[index], plans[index][1]
            mine = place_of(whole, own, batch, form)
            for hop, peer in enumerate(peers, 1):
                source = lax.rem(across + others - hop, others) * 2 + core
                onward.append((go(own, mine, peer), place_of(whole, own, source, form)))
            arriving.append(go(own, mine, twin))

    stage()
    copies = [None] * (2 * arrays)
    for step in range(steps):
        for index, (axis, form) in enumerate(plans):
            if axis != "head":
                continue
            own = own_refs[index]
            for flow, chunk, device in ((0, place - step, right), (1, place + step, left)):
                at = 2 * index + flow
                if step:
                    copies[at].wait_recv()
                chunk = lax.rem(chunk + count, count)
                target = place_of(all_refs[index], own, chunk, form)
                source = target if step else own
                if step == steps - 1:
                    part = half_of(own.shape, flow)
                    source = source.at[part]
                    target = target.at[part]
                copies[at] = go(source, target, device)
        if step == steps // 2:
            stage()
    while stages or onward:
        stage()
    for copy in copies:
        if copy is not None:
            arriving.append(copy)
    for copy in arriving:
        copy.wait_recv()
    for copy in waiting:
        copy.wait_send()
    for copy in local:
        copy.wait()


def spread(arrays, plans, collective_id):
    count = lax.axis_size("head")
    batches = lax.axis_size("batch")
    shapes = []
    slots = 0
    for array, (axis, form) in zip(arrays, plans):
        many = count if axis == "head" else batches
        slots += count if axis == "head" else batches - 1
        if form == "lead":
            shapes.append((many, *array.shape))
        elif form == "rows":
            shapes.append((many * array.shape[0], array.shape[1]))
        else:
            tall = array.shape[0] // (2 if form == "low" else 1)
            shapes.append((tall, many * array.shape[1]))
    hbm = pl.BlockSpec(memory_space=pl.ANY)
    return pl.pallas_call(
        functools.partial(spread_kernel, count, batches, plans),
        out_shape=[jax.ShapeDtypeStruct(shape, a.dtype) for shape, a in zip(shapes, arrays)],
        in_specs=[pl.BlockSpec(memory_space=pltpu.VMEM)] * len(arrays),
        out_specs=[hbm] * len(arrays),
        scratch_shapes=[
            pltpu.SemaphoreType.DMA((slots,)),
            pltpu.SemaphoreType.DMA((slots,)),
            pltpu.SemaphoreType.DMA((len(arrays),)),
        ],
        compiler_params=pltpu.CompilerParams(
            collective_id=collective_id, has_side_effects=True, vmem_limit_bytes=VMEM_LIMIT
        ),
        name=f"spread_{collective_id}",
    )(*arrays)


def mlp_kernel(
    count, x_hbm, a_hbm, dy_hbm, gain_ref, out_hbm, gate_hbm, up_hbm, top_hbm, low_hbm,
    mlp_hbm, dmlp_hbm, ddown_hbm, h1_ref, dh1_ref, low_ref, dgain_ref, da_ref, ahead_ref, behind_ref,
    x_s, a_s, mlp_s, h1_s, dy_all, n2_all, hid_all, grad_all, dmlp_s, ddown_s, da_part,
    mlp_far, mlp_next, mlp_got, right_part, left_part, right_got, left_got,
    out_w, gate_w, up_w, down_w, in_sem, out_sem, grad_sem, weight_sem,
    send_sem, recv_sem, da_send, da_recv, far_send, far_recv,
):
    steps = count // 2
    rows = x_hbm.shape[0] // count
    width = x_hbm.shape[1]
    hidden = gate_w.shape[1]
    middle = hidden // 2
    weights = [
        pltpu.make_async_copy(source, target, weight_sem.at[index])
        for index, (source, target) in enumerate(
            (
                (out_hbm, out_w), (gate_hbm, gate_w), (up_hbm, up_w),
                (top_hbm, down_w.at[pl.ds(0, middle)]), (low_hbm, down_w.at[pl.ds(middle, middle)]),
            )
        )
    ]
    side = width // 2
    tile = 256
    broad = 1024
    inner = 256 if hidden % 256 == 0 else 128
    size = da_ref.shape[1]
    place, right, left = ring_setup(count)

    def member(hop):
        spot = lax.rem(place + hop, count)
        return spot, (lax.axis_index("batch"), ring_head(spot, count))

    def owners(group):
        first = jnp.where(group == 0, 1, 0)
        one = lax.rem(place + steps - group, count)
        two = lax.rem(place - steps + group + first * steps + count, count)
        return one, two

    def span(owner):
        return pl.ds(pl.multiple_of(owner * rows, rows), rows)

    def tile_of(at, extent=tile):
        return pl.ds(pl.multiple_of(at * extent, extent), extent)

    def loads(group, slot):
        return [
            pltpu.make_async_copy(
                source.at[span(owner)],
                target.at[pl.ds(at * rows, rows)],
                in_sem.at[slot, 2 * index + at],
            )
            for index, (source, target) in enumerate(
                ((x_hbm, x_s.at[slot]), (a_hbm, a_s.at[slot]), (dy_hbm, dy_all.at[group]))
            )
            for at, owner in enumerate(owners(group))
        ]

    def stores(group, slot):
        return [
            pltpu.make_async_copy(
                mlp_s.at[slot, pl.ds(at * rows, rows)], mlp_hbm.at[span(owner)], out_sem.at[slot, at]
            )
            for at, owner in enumerate(owners(group))
        ]

    def passing(source, target, sems, slot, device):
        return pltpu.make_async_remote_copy(
            src_ref=source,
            dst_ref=target,
            send_sem=sems[0].at[slot],
            recv_sem=sems[1].at[slot],
            device_id=device,
            device_id_type=MESH,
        )

    ring_sems, far_sems = (send_sem, recv_sem), (far_send, far_recv)
    ahead, behind = pl.ds(0, side), pl.ds(side, side)

    def first_copies():
        return (
            passing(right_part.at[0, :, ahead], right_got.at[0, :, ahead], ring_sems, 0, right),
            passing(right_part.at[0, :, behind], left_got.at[0, :, behind], ring_sems, steps, left),
        )

    def later_copies(step):
        return (
            passing(right_got.at[step - 1], right_got.at[step], ring_sems, step, right),
            passing(left_got.at[step - 1], left_got.at[step], ring_sems, steps + step, left),
        )

    for copy in (*loads(0, 0), *weights):
        copy.start()
    greet([member(hop)[1] for hop in range(1, count)])
    weights[0].wait()

    @pl.loop(0, steps)
    def _(group):
        slot = lax.rem(group, 2)
        for copy in loads(group, slot):
            copy.wait()

        @pl.when(group + 1 < steps)
        def _():
            for copy in loads(group + 1, 1 - slot):
                copy.start()

        @pl.when(group >= 2)
        def _():
            for copy in stores(group - 2, slot):
                copy.wait()

        mixed = a_s[slot]

        def residual(at, total):
            cols = tile_of(at, broad)
            values = x_s[slot, :, cols].astype(F32) + matmul(mixed, out_w[:, cols])
            h1_s[:, cols] = values
            return total + jnp.sum(values * values, axis=1, keepdims=True)

        total = lax.fori_loop(0, width // broad, residual, jnp.zeros((2 * rows, 1), F32))
        scale = lax.rsqrt(total / width + EPSILON)

        @pl.when(group == 0)
        def _():
            h1_ref[...] = h1_s[pl.ds(rows, rows)]
            for copy in weights[1:]:
                copy.wait()

        @pl.loop(0, width // tile)
        def _(at):
            cols = tile_of(at)
            n2_all[group, :, cols] = (h1_s[:, cols] * scale * gain_ref[:, cols]).astype(BF)

        normed = n2_all[group]
        dy = dy_all[group]

        @pl.loop(0, hidden // inner)
        def _(at):
            cols = tile_of(at, inner)
            cols_up = pl.ds(pl.multiple_of(hidden + at * inner, inner), inner)
            gate = matmul(normed, gate_w[:, cols])
            up = matmul(normed, up_w[:, cols])
            d_hidden = cols_inner(dy, down_w[cols])
            sig = jax.nn.sigmoid(gate)
            silu = gate * sig
            hid_all[group, :, cols] = (silu * up).astype(BF)
            grad_all[group, :, cols] = (d_hidden * up * sig * (1.0 + gate * (1.0 - sig))).astype(BF)
            grad_all[group, :, cols_up] = (d_hidden * silu).astype(BF)

        hid = hid_all[group]
        d_gate = grad_all[group, :, :hidden]
        d_up = grad_all[group, :, hidden:]
        half = jnp.minimum(group, 1)

        @pl.loop(0, width // broad)
        def _(at):
            cols = tile_of(at, broad)
            part = (cols_inner(d_gate, gate_w[cols]) + cols_inner(d_up, up_w[cols])).astype(BF)
            right_part[half, :, cols] = part[:rows]
            left_part[half, :, cols] = part[rows:]

        @pl.when(group == 0)
        def _():
            for copy in first_copies():
                copy.start()

        @pl.when(group == 1)
        def _():
            one, two = first_copies()
            one.wait_recv()
            right_got[0, :, ahead] = add_low(right_part[1, :, ahead], right_got[0, :, ahead])
            right_got[0, :, behind] = right_part[1, :, behind]
            two.wait_recv()
            left_got[0, :, behind] = add_low(left_part[1, :, behind], left_got[0, :, behind])
            left_got[0, :, ahead] = left_part[1, :, ahead]

        @pl.when(group >= 2)
        def _():
            one, two = later_copies(group - 1)
            one.wait_recv()
            right_got[group - 1] = add_low(right_part[1], right_got[group - 1])
            two.wait_recv()
            left_got[group - 1] = add_low(left_part[1], left_got[group - 1])

        @pl.when(group >= 1)
        def _():
            for copy in later_copies(group):
                copy.start()

        @pl.loop(0, width // broad)
        def _(at):
            cols = tile_of(at, broad)
            mlp_s[slot, :, cols] = matmul(hid, down_w[:, cols]).astype(BF)

        for copy in stores(group, slot):
            copy.start()

        @pl.when(group == 0)
        def _():
            mlp_far[...] = mlp_s[slot, pl.ds(0, rows)]

        @pl.when(group == 1)
        def _():
            mlp_next[0] = mlp_s[slot, pl.ds(0, rows)]
            mlp_next[1] = mlp_s[slot, pl.ds(rows, rows)]

        @pl.when(group == 2)
        def _():
            ahead_ref[...] = mlp_s[slot, pl.ds(0, rows)]
            behind_ref[...] = mlp_s[slot, pl.ds(rows, rows)]

    far_copies = [
        passing(mlp_far.at[:, ahead], mlp_got.at[0, :, ahead], far_sems, 0, right),
        passing(mlp_far.at[:, behind], mlp_got.at[1, :, behind], far_sems, 1, left),
    ]
    for copy in far_copies:
        copy.start()

    every = steps * 2 * rows

    def dmlp_copy(at, slot):
        return pltpu.make_async_copy(
            dmlp_s.at[slot], dmlp_hbm.at[tile_of(at // 2), tile_of(lax.rem(at, 2), hidden)], grad_sem.at[slot]
        )

    mlp_tiles = 2 * (width // tile)

    @pl.loop(0, mlp_tiles)
    def _(at):
        slot = lax.rem(at, 2)

        @pl.when(at >= 2)
        def _():
            dmlp_copy(at - 2, slot).wait()

        normed = n2_all[:, :, tile_of(at // 2)].reshape(every, tile)
        grads = grad_all[:, :, tile_of(lax.rem(at, 2), hidden)].reshape(every, hidden)
        dmlp_s[slot] = rows_inner(normed, grads).astype(BF)
        dmlp_copy(at, slot).start()

    wide = 512
    across = width // wide

    def ddown_copy(at, slot):
        return pltpu.make_async_copy(
            ddown_s.at[slot],
            ddown_hbm.at[tile_of(at // across, inner), tile_of(lax.rem(at, across), wide)],
            grad_sem.at[2 + slot],
        )

    down_tiles = across * (hidden // inner)

    @pl.loop(0, down_tiles)
    def _(at):
        slot = lax.rem(at, 2)

        @pl.when(at >= 2)
        def _():
            ddown_copy(at - 2, slot).wait()

        hid = hid_all[:, :, tile_of(at // across, inner)].reshape(every, inner)
        dy = dy_all[:, :, tile_of(lax.rem(at, across), wide)].reshape(every, wide)
        ddown_s[slot] = rows_inner(hid, dy).astype(BF)
        ddown_copy(at, slot).start()

    for copy in later_copies(steps - 1):
        copy.wait_recv()
    for flow, have, lack in ((0, ahead, behind), (1, behind, ahead)):
        far_copies[flow].wait_recv()
        mlp_got[flow, :, have] = add_low(mlp_got[flow, :, have], mlp_next[flow, :, have])
        mlp_got[flow, :, lack] = mlp_next[flow, :, lack]
    next_copies = [
        passing(mlp_got.at[0], mlp_got.at[2], far_sems, 2, right),
        passing(mlp_got.at[1], mlp_got.at[3], far_sems, 3, left),
    ]
    for copy in next_copies:
        copy.start()

    def collect(at, state):
        squares, mean = state
        cols = tile_of(at)
        dn2 = (
            left_part[0, :, cols].astype(F32)
            + right_got[steps - 1, :, cols].astype(F32)
            + left_got[steps - 1, :, cols].astype(F32)
        )
        dh1_ref[:, cols] = dn2
        h1 = h1_ref[:, cols]
        squares = squares + jnp.sum(h1 * h1, axis=1, keepdims=True)
        return squares, mean + jnp.sum(gain_ref[:, cols] * dn2 * h1, axis=1, keepdims=True)

    zero = jnp.zeros((rows, 1), F32)
    squares, mean = lax.fori_loop(0, width // tile, collect, (zero, zero))
    scale_own = lax.rsqrt(squares / width + EPSILON)
    pull = scale_own * scale_own * scale_own * (mean / width)

    @pl.loop(0, width // tile)
    def _(at):
        cols = tile_of(at)
        dn2, h1 = dh1_ref[:, cols], h1_ref[:, cols]
        dgain_ref[:, cols] = jnp.sum(dn2 * h1 * scale_own, axis=0, keepdims=True)
        dy = dy_all[0, pl.ds(rows, rows), cols].astype(F32)
        d_resid = dy + scale_own * (gain_ref[:, cols] * dn2) - h1 * pull
        dh1_ref[:, cols] = d_resid
        low_ref[:, cols] = d_resid.astype(BF)

    def da_copy(hop):
        return passing(
            da_part.at[hop], da_ref.at[span(place)], (da_send, da_recv), hop, member(hop)[1]
        )

    low = low_ref[...]

    @pl.loop(1, count)
    def _(hop):
        spot = member(hop)[0]
        da_part[hop] = cols_inner(low, out_w[tile_of(spot, size)]).astype(BF)
        da_copy(hop).start()

    da_ref[span(place)] = cols_inner(low, out_w[tile_of(place, size)]).astype(BF)

    @pl.loop(1, count)
    def _(hop):
        da_copy(hop).wait_recv()
        da_copy(hop).wait_send()

    for flow, held in ((0, ahead_ref), (1, behind_ref)):
        next_copies[flow].wait_recv()
        held[...] = add_low(held[...], mlp_got[2 + flow])
    for copy in (*far_copies, *next_copies, *first_copies()):
        copy.wait_send()
    for step in range(1, steps):
        for copy in later_copies(step):
            copy.wait_send()
    for group in range(steps - 2, steps):
        for copy in stores(group, group % 2):
            copy.wait()
    for at in range(2):
        dmlp_copy(mlp_tiles - 2 + at, (mlp_tiles + at) % 2).wait()
        ddown_copy(down_tiles - 2 + at, (down_tiles + at) % 2).wait()


def mlp_back(tokens, mixed, dy, gain, out_w, gate_w, up_w, down_top, down_low, collective_id):
    count = lax.axis_size("head")
    total, width = tokens.shape
    hidden = gate_w.shape[1]
    rows, steps = total // count, count // 2
    size = mixed.shape[1] // count
    inner = 256 if hidden % 256 == 0 else 128
    vmem = pl.BlockSpec(memory_space=pltpu.VMEM)
    hbm = pl.BlockSpec(memory_space=pl.ANY)

    def slots(many, tall, wide, dtype=BF):
        return pltpu.VMEM((many, tall, wide), dtype)

    def shape(*extent, dtype=BF):
        return jax.ShapeDtypeStruct(extent, dtype)

    dma = pltpu.SemaphoreType.DMA
    flops = 2 * total * width * (mixed.shape[1] + 9 * hidden)
    return pl.pallas_call(
        functools.partial(mlp_kernel, count),
        out_shape=[
            shape(total, width), shape(width, 2 * hidden), shape(hidden, width),
            shape(rows, width, dtype=F32), shape(rows, width, dtype=F32), shape(rows, width),
            shape(1, width, dtype=F32), shape(total, size), shape(rows, width), shape(rows, width),
        ],
        in_specs=[hbm] * 3 + [vmem] + [hbm] * 5,
        out_specs=[hbm] * 3 + [vmem] * 7,
        scratch_shapes=[
            slots(2, 2 * rows, width), slots(2, 2 * rows, mixed.shape[1]), slots(2, 2 * rows, width),
            pltpu.VMEM((2 * rows, width), F32),
            slots(steps, 2 * rows, width), slots(steps, 2 * rows, width),
            slots(steps, 2 * rows, hidden), slots(steps, 2 * rows, 2 * hidden),
            slots(2, 256, hidden), slots(2, inner, 512), slots(count, rows, size),
            pltpu.VMEM((rows, width), BF), slots(2, rows, width), slots(4, rows, width),
            slots(2, rows, width), slots(2, rows, width),
            slots(steps, rows, width), slots(steps, rows, width),
            *[pltpu.VMEM(weight.shape, BF) for weight in (out_w, gate_w, up_w)],
            pltpu.VMEM((hidden, width), BF),
            dma((2, 6)), dma((2, 2)), dma((4,)), dma((5,)), dma((count,)), dma((count,)),
            dma((count,)), dma((count,)), dma((4,)), dma((4,)),
        ],
        compiler_params=pltpu.CompilerParams(
            collective_id=collective_id, has_side_effects=True, vmem_limit_bytes=VMEM_LIMIT
        ),
        cost_estimate=pl.CostEstimate(flops=flops, bytes_accessed=40 << 20, transcendentals=0),
        name="mlp_back",
    )(tokens, mixed, dy, gain, out_w, gate_w, up_w, down_top, down_low)


def entry_kernel(
    count, batches, x_ref, w_ref, out_ref, gain_ref, seg_ref, down_ref,
    n1_hbm, q_ref, logit_ref, kv_ref, w_all, out_all, gain_all, seg_all, down_all,
    x_s, n1_ref, send_sem, recv_sem, local_sem, x_sem, n1_sem,
):
    steps = count // 2
    others = batches // 2
    rows, width = x_ref.shape
    depth = w_ref.shape[0]
    size, wide = out_ref.shape
    block = 256
    blocks = rows // block

    def x_copy(at):
        here = pl.ds(pl.multiple_of(at * block, block), block)
        return pltpu.make_async_copy(x_ref.at[here], x_s.at[here], x_sem.at[at])

    def n1_copy(at):
        here = pl.ds(pl.multiple_of(at * block, block), block)
        return pltpu.make_async_copy(n1_ref.at[here], n1_hbm.at[here], n1_sem.at[at])

    for at in range(blocks):
        x_copy(at).start()
    place, right, left = ring_setup(count)
    head = lax.axis_index("head")
    batch = lax.axis_index("batch")
    across, core, low = batch // 2, lax.rem(batch, 2), lax.rem(head, 2)
    twin = (across * 2 + 1 - core, head)
    mate = (batch, head + 1 - 2 * low)
    spots = [lax.rem(across + hop, others) for hop in range(others)]
    backs = [lax.rem(across + others - hop, others) for hop in range(others)]
    peers = [(spot * 2 + core, head) for spot in spots]
    far_peers = [(spot * 2 + 1 - core, head) for spot in spots]
    greet((twin, mate, right, left, *peers[1:], *far_peers[1:]))
    sems = (send_sem, recv_sem)
    slot = 0
    copies = []

    def go(source, target, device):
        nonlocal slot
        copy = send(source, target, sems, slot, device)
        slot += 1
        copies.append(copy)
        return copy

    def part(at, extent):
        return pl.ds(pl.multiple_of(at * extent, extent), extent)

    def both(view, own):
        out = [go(own, view(batch), peers[hop]) for hop in range(1, others)]
        return out, [go(own, view(batch), twin)]

    def pass_on(view, arrived):
        out = []
        for hop in range(1, others):
            arrived[hop - 1].wait_recv()
            there = view(backs[hop] * 2 + core)
            out.append(go(there, there, twin))
        return out

    local = []

    def stay(source, target):
        copy = pltpu.make_async_copy(source, target, local_sem.at[len(local)])
        copy.start()
        local.append(copy)

    def main_view(at):
        return w_all.at[part(at, depth), pl.ds(0, 3 * size)]

    def mate_view(at):
        return w_all.at[part(at, depth), pl.ds(3 * size, size)]

    def out_view(chunk, at):
        return out_all.at[part(chunk, size), part(at, wide)]

    small = []
    for own, whole in ((gain_ref, gain_all), (seg_ref, seg_all)):
        for device in (twin, *peers[1:], *far_peers[1:]):
            small.append(go(own, whole.at[batch], device))
        stay(own, whole.at[batch])
    from_mate = go(w_ref.at[:, pl.ds(2 * size, size)], mate_view(batch), mate)
    main_out, main_twin = both(main_view, w_ref)
    stay(w_ref, main_view(batch))
    out_peers = [go(out_ref, out_view(place, batch), peers[hop]) for hop in range(1, others)]
    stay(out_ref, out_view(place, batch))
    flows = [[None, None] for _ in range(others)]

    def ring(step):
        for hop in range(others):
            lane = spots[0] if hop == 0 else backs[hop]
            at = lane * 2 + core
            if step == 0 and hop:
                out_peers[hop - 1].wait_recv()
            for flow, chunk, device in ((0, place - step, right), (1, place + step, left)):
                if step:
                    flows[hop][flow].wait_recv()
                target = out_view(lax.rem(chunk + count, count), at)
                source = out_ref if step == 0 and hop == 0 else target
                if step == steps - 1:
                    cut = (pl.ds(flow * (size // 2), size // 2), slice(None))
                    source, target = source.at[cut], target.at[cut]
                flows[hop][flow] = go(source, target, device)

    for copy in small:
        copy.wait_recv()
    for copy in local[:2]:
        copy.wait()

    def normalize(at):
        here = part(at, block)
        x_copy(at).wait()

        def squares(tile, total):
            values = x_s[here, part(tile, 256)].astype(F32)
            return total + jnp.sum(values * values, axis=1, keepdims=True)

        total = lax.fori_loop(0, width // 256, squares, jnp.zeros((block, 1), F32))
        scale = lax.rsqrt(total / width + EPSILON)

        @pl.loop(0, batches)
        def _(owner):
            for tile in range(depth // 128):
                cols = pl.ds(pl.multiple_of(owner * depth + tile * 128, 128), 128)
                values = x_s[here, cols].astype(F32) * scale
                n1_ref[here, cols] = (values * gain_all[owner, pl.ds(tile, 1)]).astype(BF)

        n1_copy(at).start()

    middle = blocks // 2

    @pl.loop(0, middle)
    def _(at):
        normalize(at)

    from_mate.wait_recv()
    mate_out, mate_twin = both(mate_view, mate_view(batch))
    ring(0)

    def down_view(at):
        return down_all.at[:, part(at, down_ref.shape[1])]

    down_own = down_ref.at[pl.ds(0, down_ref.shape[0] // 2)]
    down_out, down_twin = both(down_view, down_own)
    stay(down_own, down_view(batch))

    @pl.loop(middle, blocks)
    def _(at):
        normalize(at)

    main_passed = pass_on(main_view, main_out)
    mate_passed = pass_on(mate_view, mate_out)
    for copy in (*main_twin, *mate_twin, *main_passed, *mate_passed):
        copy.wait_recv()
    for copy in local[2:]:
        copy.wait()

    def kv_view(at):
        return kv_ref.at[part(at, rows)]

    @pl.loop(0, blocks)
    def _(at):
        here = part(at, block)
        values = matmul(n1_ref[here], w_all[:, pl.ds(2 * size, 2 * size)])
        one, two = values[:, :size], values[:, size:]
        first = jnp.where(low == 0, one, two).astype(BF)
        second = jnp.where(low == 0, two, one).astype(BF)
        half = size // 2
        there = pl.ds(pl.multiple_of(batch * rows + at * block, block), block)
        kv_ref[there, pl.ds(0, size)] = jnp.concatenate([first[:, :half], second[:, :half]], 1)
        kv_ref[there, pl.ds(size, size)] = jnp.concatenate([first[:, half:], second[:, half:]], 1)

    kv_out, kv_twin = both(kv_view, kv_view(batch))
    ring(1)

    @pl.loop(0, blocks)
    def _(at):
        here = part(at, block)
        values = matmul(n1_ref[here], w_all[:, pl.ds(0, 2 * size)])
        q_ref[here] = values[:, :size].astype(BF)
        logit_ref[here] = values[:, size:]

    for step in range(2, steps):
        ring(step)
    down_passed = pass_on(down_view, down_out)
    kv_passed = pass_on(kv_view, kv_out)
    for pair in flows:
        for copy in pair:
            copy.wait_recv()
    swaps = []
    for hop in range(others):
        there = out_all.at[:, part(spots[hop] * 2 + core, wide)]
        swaps.append(go(there, there, twin))
    for copy in (*kv_twin, *kv_passed, *swaps, *down_twin, *down_passed):
        copy.wait_recv()
    for copy in copies:
        copy.wait_send()
    for at in range(blocks):
        n1_copy(at).wait()


def entry(tokens, w_shard, w_out, gains, segments, w_down, collective_id):
    count = lax.axis_size("head")
    batches = lax.axis_size("batch")
    others = batches // 2
    rows, width = tokens.shape
    size, wide = w_out.shape
    vmem = pl.BlockSpec(memory_space=pltpu.VMEM)
    hbm = pl.BlockSpec(memory_space=pl.ANY)
    slots = 6 * batches + others * (count + 3)
    sems = pltpu.SemaphoreType.DMA((slots,))
    return pl.pallas_call(
        functools.partial(entry_kernel, count, batches),
        out_shape=[
            jax.ShapeDtypeStruct((rows, width), BF),
            jax.ShapeDtypeStruct((rows, size), BF),
            jax.ShapeDtypeStruct((rows, size), F32),
            jax.ShapeDtypeStruct((batches * rows, 2 * size), BF),
            jax.ShapeDtypeStruct((width, 4 * size), BF),
            jax.ShapeDtypeStruct((count * size, batches * wide), BF),
            jax.ShapeDtypeStruct((batches, *gains.shape), F32),
            jax.ShapeDtypeStruct((batches, *segments.shape), jnp.int32),
            jax.ShapeDtypeStruct((w_down.shape[0] // 2, batches * w_down.shape[1]), BF),
        ],
        in_specs=[hbm] + [vmem] * 5,
        out_specs=[hbm] + [vmem] * 4 + [hbm] + [vmem] * 2 + [hbm],
        scratch_shapes=[
            pltpu.VMEM((rows, width), BF), pltpu.VMEM((rows, width), BF),
            sems, sems, pltpu.SemaphoreType.DMA((5,)),
            pltpu.SemaphoreType.DMA((rows // 256,)), pltpu.SemaphoreType.DMA((rows // 256,)),
        ],
        compiler_params=pltpu.CompilerParams(
            collective_id=collective_id, has_side_effects=True, vmem_limit_bytes=VMEM_LIMIT
        ),
        name="entry",
    )(tokens, w_shard, w_out, gains, segments, w_down)


KEY_BLOCK = 512
QUERY_BLOCK = 640


def key_range(start_ref, base, query_block):
    first = query_block * QUERY_BLOCK
    lowest = start_ref[first]
    highest = start_ref[first + QUERY_BLOCK - 1]
    begin = lowest // KEY_BLOCK
    end = (base + first + QUERY_BLOCK - 1) // KEY_BLOCK + 1
    full_begin = jnp.minimum((highest + KEY_BLOCK - 1) // KEY_BLOCK, end)
    full_end = jnp.maximum((base + first + 1) // KEY_BLOCK, full_begin)
    return begin, full_begin, full_end, end


def allowed_pairs(key_block, start_row, base_row):
    shape = (KEY_BLOCK, QUERY_BLOCK)
    key_pos = key_block * KEY_BLOCK + lax.broadcasted_iota(jnp.int32, shape, 0)
    query_pos = base_row + lax.broadcasted_iota(jnp.int32, shape, 1)
    return (key_pos >= start_row) & (key_pos <= query_pos)


def attend_kernel(
    scale, start_sm, base_sm, q_ref, kv_ref, start_ref, logit_ref, o_ref, a_ref, lse_ref
):
    base = base_sm[0]
    size = q_ref.shape[1]
    factor = scale * math.log2(math.e)

    @pl.loop(0, q_ref.shape[0] // QUERY_BLOCK)
    def _(block):
        rows = pl.ds(pl.multiple_of(block * QUERY_BLOCK, QUERY_BLOCK), QUERY_BLOCK)
        queries = q_ref[rows]
        start_row = start_ref[:, rows]
        begin, full_begin, full_end, end = key_range(start_sm, base, block)

        def step(masked, at, state):
            old_max, old_sum, total = state
            keys = pl.ds(pl.multiple_of(at * KEY_BLOCK, KEY_BLOCK), KEY_BLOCK)
            scores = cols_inner(kv_ref[keys, :size], queries)
            if masked:
                allowed = allowed_pairs(at, start_row, base + block * QUERY_BLOCK)
                scores = jnp.where(allowed, scores, MASKED)
            new_max = jnp.maximum(old_max, jnp.max(scores, axis=0, keepdims=True))
            keep = jnp.exp2((old_max - new_max) * factor)
            weights = jnp.exp2(scores * factor - new_max * factor)
            new_sum = old_sum * keep + jnp.sum(weights, axis=0, keepdims=True)
            total = total * keep + rows_inner(kv_ref[keys, size:], weights.astype(BF))
            return new_max, new_sum, total

        state = (
            jnp.full((1, QUERY_BLOCK), MASKED, F32),
            jnp.zeros((1, QUERY_BLOCK), F32),
            jnp.zeros((size, QUERY_BLOCK), F32),
        )
        state = lax.fori_loop(begin, full_begin, functools.partial(step, True), state)
        state = lax.fori_loop(full_begin, full_end, functools.partial(step, False), state)
        state = lax.fori_loop(full_end, end, functools.partial(step, True), state)
        run_max, run_sum, total = state
        lse_ref[:, rows] = run_max * factor + jnp.log2(run_sum)
        attended = (total / run_sum).T
        o_ref[rows] = attended
        a_ref[rows] = (attended * jax.nn.sigmoid(logit_ref[rows])).astype(BF)


def attend_back_kernel(
    scale, start_sm, base_sm, q_ref, kv_ref, start_ref, logit_ref, o_ref, da_ref, lse_ref,
    dq_ref, dg_ref, dkv_ref, dk_acc, dv_acc,
):
    base = base_sm[0]
    size = q_ref.shape[1]
    factor = scale * math.log2(math.e)
    dk_acc[...] = jnp.zeros_like(dk_acc)
    dv_acc[...] = jnp.zeros_like(dv_acc)

    @pl.loop(0, q_ref.shape[0] // QUERY_BLOCK)
    def _(block):
        rows = pl.ds(pl.multiple_of(block * QUERY_BLOCK, QUERY_BLOCK), QUERY_BLOCK)
        queries = q_ref[rows]
        start_row = start_ref[:, rows]
        lse = lse_ref[:, rows]
        gate = jax.nn.sigmoid(logit_ref[rows])
        attended = o_ref[rows]
        d_mixed = da_ref[rows].astype(F32)
        d_attended = (d_mixed * gate).astype(BF)
        dg_ref[rows] = (d_mixed * attended * gate * (1.0 - gate)).astype(BF)
        delta = jnp.sum((d_attended.astype(F32) * attended).T, axis=0, keepdims=True)
        begin, full_begin, full_end, end = key_range(start_sm, base, block)

        def step(masked, at, d_queries):
            keys = pl.ds(pl.multiple_of(at * KEY_BLOCK, KEY_BLOCK), KEY_BLOCK)
            key_block = kv_ref[keys, :size]
            probs = jnp.exp2(cols_inner(key_block, queries) * factor - lse)
            if masked:
                allowed = allowed_pairs(at, start_row, base + block * QUERY_BLOCK)
                probs = jnp.where(allowed, probs, 0.0)
            d_probs = cols_inner(kv_ref[keys, size:], d_attended)
            d_scores = (probs * (d_probs - delta) * scale).astype(BF)
            dv_acc[keys] += matmul(probs.astype(BF), d_attended)
            dk_acc[keys] += matmul(d_scores, queries)
            return d_queries + rows_inner(key_block, d_scores)

        d_queries = jnp.zeros((size, QUERY_BLOCK), F32)
        d_queries = lax.fori_loop(begin, full_begin, functools.partial(step, True), d_queries)
        d_queries = lax.fori_loop(full_begin, full_end, functools.partial(step, False), d_queries)
        d_queries = lax.fori_loop(full_end, end, functools.partial(step, True), d_queries)
        dq_ref[rows] = d_queries.T.astype(BF)

    @pl.loop(0, kv_ref.shape[0] // KEY_BLOCK)
    def _(at):
        keys = pl.ds(pl.multiple_of(at * KEY_BLOCK, KEY_BLOCK), KEY_BLOCK)
        dk, dv = dk_acc[keys].astype(BF), dv_acc[keys].astype(BF)
        half = size // 2
        dkv_ref[keys, :size] = jnp.concatenate([dk[:, :half], dv[:, :half]], axis=1)
        dkv_ref[keys, size:] = jnp.concatenate([dk[:, half:], dv[:, half:]], axis=1)


def tail_kernel(
    count, batches, dq_ref, dg_ref, dkv_ref, w_ref, gain_ref, dh1_ref, second_ref,
    low_ref, h1_ref, ahead_ref, behind_ref, n1_ref, x_hbm, mixed_hbm, mlp_hbm,
    out_all, tok_all, gains_ref, wout_own, din_ref, key_ref, value_ref,
    part_ref, tok_ref, got, wout_got, gain_own, gain_got, gain_mid, gain_heads,
    din_s, din_got, din_x, wout_s, wout_twin, wout_x,
    cat_ref, out_s, out_got, core_got, x_first, x_second, y_first, y_second, held, n1_s,
    x_ref, mixed_ref, mlp_ref, mlp_next, send_sem, recv_sem, local_sem,
):
    steps = count // 2
    rows, width = x_ref.shape
    depth = cat_ref.shape[1]
    tall, size = dq_ref.shape
    tile = 256
    place, right, left = ring_setup(count)
    batch, head = lax.axis_index("batch"), lax.axis_index("head")
    others = [lax.rem(batch + hop, batches) for hop in range(1, batches)]
    members = [(batch, ring_head(lax.rem(place + hop, count), count)) for hop in range(1, count)]
    greet((*members, *[(other, head) for other in others]))
    sems = (send_sem, recv_sem)
    slot = 0
    copies = []

    def go(source, target, device):
        nonlocal slot
        copy = send(source, target, sems, slot, device)
        slot += 1
        copies.append(copy)
        return copy

    across, core = batch // 2, lax.rem(batch, 2)
    spots = [lax.rem(across + hop, batches // 2) for hop in range(batches // 2)]
    order = list(range(1, batches // 2)) + [0]
    twin = (across * 2 + 1 - core, head)

    def scatter_swap(view, held):
        return [go(view(2 * spots[hop] + 1 - core), held.at[spots[hop]], twin) for hop in order]

    def add_tiles(target, one, other):
        @pl.loop(0, target.shape[0] // 128)
        def _(at):
            lines = pl.ds(pl.multiple_of(at * 128, 128), 128)
            total = one[lines].astype(F32) + other[lines].astype(F32)
            target[lines] = total.astype(target.dtype)

    def scatter_cross(view, held, crossed, arriving):
        out = []
        for copy, hop in zip(arriving, order):
            copy.wait_recv()
            spot = spots[hop]
            add_tiles(held.at[spot], held.at[spot], view(2 * spot + core))
            if hop:
                out.append(go(held.at[spot], crossed.at[hop - 1], (spot * 2 + core, head)))
        return out

    def scatter_end(held, crossed, arriving, target):
        for hop, copy in enumerate(arriving):
            copy.wait_recv()
            last = hop == len(arriving) - 1
            add_tiles(target if last else held.at[across], held.at[across], crossed.at[hop])

    def wout_view(at):
        wide = width // batches
        return wout_s.at[:, pl.ds(pl.multiple_of(at * wide, wide), wide)]

    def din_view(at):
        tall = din_ref.shape[0]
        return din_s.at[pl.ds(pl.multiple_of(at * tall, tall), tall)]

    def span(owner, extent):
        return pl.ds(pl.multiple_of(lax.rem(owner + count, count) * extent, extent), extent)

    def compute(owner):
        here = span(owner, rows)
        values = cat_ref[here]

        @pl.loop(0, width // tile)
        def _(at):
            cols = pl.ds(pl.multiple_of(at * tile, tile), tile)
            part_ref[here, cols] = cols_inner(values, w_ref[cols, pl.ds(0, depth)]).astype(BF)

    def gather(own, whole, step, last):
        out = []
        for flow, chunk, device in ((0, place - step, right), (1, place + step, left)):
            if last:
                last[flow].wait_recv()
            target = whole.at[lax.rem(chunk + count, count)]
            source = target if step else own
            if step == steps - 1:
                cut = (slice(None), pl.ds(flow * (width // 2), width // 2))
                source, target = source.at[cut], target.at[cut]
            out.append(go(source, target, device))
        return out

    def reduce(parts, held, step, last):
        extent, side = held.shape[2], held.shape[3] // 2
        out = []
        for flow, owner, device in (
            (0, place + steps - step, right),
            (1, place - steps + step, left),
        ):
            have = pl.ds(flow * side, side)
            lack = pl.ds((1 - flow) * side, side)
            mine = parts.at[span(owner, extent)]
            if step == 0:
                out.append(go(mine.at[:, have], held.at[flow, 0, :, have], device))
                continue
            last[flow].wait_recv()
            if step == 1:
                held[flow, 0, :, have] = add_low(held[flow, 0, :, have], mine[:, have])
                held[flow, 0, :, lack] = mine[:, lack]
            else:
                held[flow, step - 1] = add_low(held[flow, step - 1], mine[...])
            out.append(go(held.at[flow, step - 1], held.at[flow, step], device))
        return out

    low = lax.rem(head, 2)
    mate = (batch, head + 1 - 2 * low)
    peers = [(spot * 2 + core, head) for spot in spots]
    mine = pl.ds(pl.multiple_of(low * size, size), size)
    given = pl.ds(pl.multiple_of((1 - low) * size, size), size)
    top, bottom = pl.ds(0, tall // 2), pl.ds(tall // 2, tall // 2)
    fresh = pl.ds(2 * size, size)

    def keys_of(at):
        return dkv_ref.at[pl.ds(pl.multiple_of(at * tall, tall), tall)]

    def normed_copy(at, slot):
        cols = pl.ds(pl.multiple_of(at * tile, tile), tile)
        return pltpu.make_async_copy(n1_ref.at[:, cols], n1_s.at[slot], local_sem.at[2 + slot])

    own_rows = pl.ds(pl.multiple_of(place * rows, rows), rows)
    fetches = [
        pltpu.make_async_copy(source.at[own_rows], target, local_sem.at[4 + index])
        for index, (source, target) in enumerate(
            ((mixed_hbm, mixed_ref), (mlp_hbm, mlp_ref), (x_hbm, x_ref))
        )
    ]
    nexts = [
        pltpu.make_async_copy(mlp_hbm.at[span(place + shift, rows)], mlp_next.at[at], local_sem.at[7 + at])
        for at, shift in enumerate((1, -1))
    ]
    for copy in (*nexts, *fetches):
        copy.start()
    for at in range(2):
        normed_copy(at, at).start()
    swaps = scatter_swap(keys_of, core_got)
    last_sums = []
    for at, (held_part, device) in enumerate(((ahead_ref, right), (behind_ref, left))):
        nexts[at].wait()
        mlp_next[at] = add_low(mlp_next[at], held_part[...])
        last_sums.append(go(mlp_next.at[at], out_got.at[at], device))
    cat_ref[:, pl.ds(0, size)] = dq_ref[...]
    cat_ref[:, pl.ds(size, size)] = dg_ref[...]
    for copy in fetches:
        copy.wait()

    @pl.loop(0, width // tile)
    def _(at):
        cols = pl.ds(pl.multiple_of(at * tile, tile), tile)
        wout_s[:, cols] = rows_inner(mixed_ref[...], low_ref[:, cols]).astype(BF)

    tops, bottoms = [], []
    for copy, hop in zip(swaps, order):
        copy.wait_recv()
        spot = spots[hop]
        add_tiles(core_got.at[spot], core_got.at[spot], keys_of(2 * spot + core))
        bottoms.append(go(core_got.at[spot, bottom, given], y_first.at[spot], mate))
        if hop:
            tops.append(go(core_got.at[spot, top], x_first.at[hop - 1], peers[hop]))
    wouts = scatter_swap(wout_view, wout_twin)
    for copy in last_sums:
        copy.wait_recv()
    out_s[...] = (
        h1_ref[...] + mlp_ref[...].astype(F32) + out_got[0].astype(F32) + out_got[1].astype(F32)
    ).astype(BF)
    keep_out = pltpu.make_async_copy(out_s, out_all.at[place], local_sem.at[0])
    keep_out.start()
    outs = gather(out_s, out_all, 0, None)
    total = core_got[across, top].astype(F32)
    for hop, copy in enumerate(tops):
        copy.wait_recv()
        total = total + x_first[hop].astype(F32)
    held[...] = total.astype(BF)
    last = go(held.at[:, given], y_second, mate)
    ends = []
    for copy, hop in zip(bottoms, order):
        copy.wait_recv()
        spot = spots[hop]
        y_first[spot] = add_low(y_first[spot], core_got[spot, bottom, mine])
        if hop:
            ends.append(go(y_first.at[spot], x_second.at[hop - 1], peers[hop]))
    last.wait_recv()
    cat_ref[top, fresh] = add_low(held[:, mine], y_second[...])
    total = y_first[across].astype(F32)
    for hop, copy in enumerate(ends):
        copy.wait_recv()
        total = total + x_second[hop].astype(F32)
    cat_ref[bottom, fresh] = total.astype(BF)

    compute(place + steps)
    sums = reduce(part_ref, got, 0, None)
    outs = gather(out_s, out_all, 1, outs)

    @pl.loop(1, count)
    def _(hop):
        compute(place + steps + hop)

    @pl.loop(0, width // tile)
    def _(at):
        slot = lax.rem(at, 2)
        normed_copy(at, slot).wait()
        cols = pl.ds(pl.multiple_of(at * tile, tile), tile)
        din_s[cols] = rows_inner(n1_s[slot], cat_ref[...]).astype(BF)

        @pl.when(at + 2 < width // tile)
        def _():
            normed_copy(at + 2, slot).start()

    dins = scatter_swap(din_view, din_got)
    for step in range(1, steps):
        sums = reduce(part_ref, got, step, sums)
        if 2 <= step < steps - 1:
            outs = gather(out_s, out_all, step, outs)
        if step == 1:
            wouts = scatter_cross(wout_view, wout_twin, wout_x, wouts)
            dins = scatter_cross(din_view, din_got, din_x, dins)
    for copy in sums:
        copy.wait_recv()

    def tile_of(at):
        return pl.ds(pl.multiple_of(at * tile, tile), tile)

    def total(cols):
        return (
            part_ref[span(place, rows), cols].astype(F32)
            + got[0, steps - 1, :, cols].astype(F32)
            + got[1, steps - 1, :, cols].astype(F32)
        )

    def collect(at, state):
        squares, mean = state
        cols = tile_of(at)
        x = x_ref[:, cols].astype(F32)
        squares = squares + jnp.sum(x * x, axis=1, keepdims=True)
        return squares, mean + jnp.sum(gain_ref[:, cols] * total(cols) * x, axis=1, keepdims=True)

    zero = jnp.zeros((rows, 1), F32)
    squares, mean = lax.fori_loop(0, width // tile, collect, (zero, zero))
    scale = lax.rsqrt(squares / width + EPSILON)
    pull = scale * scale * scale * (mean / width)

    @pl.loop(0, width // tile)
    def _(at):
        cols = tile_of(at)
        x, dn1 = x_ref[:, cols].astype(F32), total(cols)
        gain_own[pl.ds(0, 1), cols] = jnp.sum(dn1 * x * scale, axis=0, keepdims=True)
        gain_own[pl.ds(1, 1), cols] = second_ref[:, cols]
        tok_ref[:, cols] = (dh1_ref[:, cols] + scale * (gain_ref[:, cols] * dn1) - x * pull).astype(BF)

    keep_tok = pltpu.make_async_copy(tok_ref, tok_all.at[place], local_sem.at[1])
    keep_tok.start()
    toks = gather(tok_ref, tok_all, 0, None)
    outs = gather(out_s, out_all, steps - 1, outs)
    wout_part = wout_twin.at[across]
    scatter_end(wout_twin, wout_x, wouts, wout_part)
    wsums = reduce(wout_part, wout_got, 0, None)
    scatter_end(din_got, din_x, dins, din_ref)
    narrow = din_ref[:, pl.ds(2 * size, size)].T
    key_ref[...] = narrow[: size // 2]
    value_ref[...] = narrow[size // 2 :]
    wide = width // batches

    def slice_of(at):
        return pl.ds(pl.multiple_of(at * wide, wide), wide)

    gains = [
        go(gain_own.at[:, slice_of(other)], gain_got.at[hop], (other, head))
        for hop, other in enumerate(others)
    ]
    toks = gather(tok_ref, tok_all, 1, toks)
    wsums = reduce(wout_part, wout_got, 1, wsums)
    middle = gain_own[:, slice_of(batch)]
    for hop, copy in enumerate(gains):
        copy.wait_recv()
        middle = middle + gain_got[hop]
    gain_mid[...] = middle
    gain_heads[place] = middle
    gains = [go(gain_mid, gain_heads.at[place], member) for member in members]
    for step in range(2, steps):
        toks = gather(tok_ref, tok_all, step, toks)
        wsums = reduce(wout_part, wout_got, step, wsums)
    for copy in gains:
        copy.wait_recv()
    middle = gain_heads[0]
    for at in range(1, count):
        middle = middle + gain_heads[at]
    gains_ref[...] = middle
    for copy in (*wsums, *outs):
        copy.wait_recv()
    wout_own[...] = (
        wout_part[span(place, wout_own.shape[0])].astype(F32)
        + wout_got[0, steps - 1].astype(F32)
        + wout_got[1, steps - 1].astype(F32)
    )
    for copy in toks:
        copy.wait_recv()
    for copy in copies:
        copy.wait_send()
    keep_out.wait()
    keep_tok.wait()


def tail(arrays, collective_id):
    d_queries, tokens, mixed = arrays[0], arrays[-3], arrays[-2]
    count = lax.axis_size("head")
    batches = lax.axis_size("batch")
    steps = count // 2
    rows, width = tokens.shape[0] // count, tokens.shape[1]
    others = batches // 2
    size, wide = mixed.shape[1] // count, width // batches
    tall, head_size = d_queries.shape
    depth = 3 * head_size
    vmem = pl.BlockSpec(memory_space=pltpu.VMEM)
    hbm = pl.BlockSpec(memory_space=pl.ANY)
    whole = (count, rows, width)
    sems = pltpu.SemaphoreType.DMA((6 * count + 6 * batches,))
    gains = (2, width // batches)
    return pl.pallas_call(
        functools.partial(tail_kernel, count, batches),
        out_shape=[
            jax.ShapeDtypeStruct(whole, BF),
            jax.ShapeDtypeStruct(whole, BF),
            jax.ShapeDtypeStruct(gains, F32),
            jax.ShapeDtypeStruct((size, wide), F32),
            jax.ShapeDtypeStruct((wide, depth), F32),
            jax.ShapeDtypeStruct((size // 2, wide), F32),
            jax.ShapeDtypeStruct((size // 2, wide), F32),
        ],
        in_specs=[vmem] * 11 + [hbm] * 4,
        out_specs=[hbm] * 2 + [vmem] * 5,
        scratch_shapes=[
            pltpu.VMEM((count * rows, width), BF),
            pltpu.VMEM((rows, width), BF),
            pltpu.VMEM((2, steps, rows, width), BF),
            pltpu.VMEM((2, steps, size, wide), BF),
            pltpu.VMEM((2, width), F32),
            pltpu.VMEM((batches - 1, *gains), F32),
            pltpu.VMEM(gains, F32),
            pltpu.VMEM((count, *gains), F32),
            pltpu.VMEM((width, depth), BF),
            pltpu.VMEM((others, wide, depth), BF),
            pltpu.VMEM((others - 1, wide, depth), BF),
            pltpu.VMEM((count * size, width), BF),
            pltpu.VMEM((others, count * size, wide), BF),
            pltpu.VMEM((others - 1, count * size, wide), BF),
            pltpu.VMEM((tall, depth), BF),
            pltpu.VMEM((rows, width), BF),
            pltpu.VMEM((2, rows, width), BF),
            pltpu.VMEM((others, tall, 2 * head_size), BF),
            pltpu.VMEM((others - 1, tall // 2, 2 * head_size), BF),
            pltpu.VMEM((others - 1, tall // 2, head_size), BF),
            pltpu.VMEM((others, tall // 2, head_size), BF),
            pltpu.VMEM((tall // 2, head_size), BF),
            pltpu.VMEM((tall // 2, 2 * head_size), BF),
            pltpu.VMEM((2, tall, 256), BF),
            pltpu.VMEM((rows, width), BF),
            pltpu.VMEM((rows, mixed.shape[1]), BF),
            pltpu.VMEM((rows, width), BF),
            pltpu.VMEM((2, rows, width), BF),
            sems,
            sems,
            pltpu.SemaphoreType.DMA((9,)),
        ],
        compiler_params=pltpu.CompilerParams(
            collective_id=collective_id, has_side_effects=True, vmem_limit_bytes=VMEM_LIMIT
        ),
        cost_estimate=pl.CostEstimate(
            flops=4 * count * rows * width * depth, bytes_accessed=400 << 20, transcendentals=0
        ),
        name="tail",
    )(*arrays)


def finish_kernel(
    out_hbm, tok_hbm, mlp_hbm, down_hbm, in_ref, gains_ref, key_ref, value_ref, wout_ref,
    output, d_tokens, mgate_hbm, mup_hbm, d_down_hbm, query, gate, first, second, key, value, wout,
    held, mlp_ref, down_ref, mgate, mup, down, load_sem, store_sem, grad_sem,
):
    count, rows = out_hbm.shape[:2]
    loads, stores = [], []
    for index, (source, target) in enumerate(((out_hbm, output), (tok_hbm, d_tokens))):
        for at in range(count):
            slot = index * count + at
            loads.append(pltpu.make_async_copy(source.at[at], held.at[slot], load_sem.at[slot]))
            stores.append(
                pltpu.make_async_copy(
                    held.at[slot], target.at[pl.ds(at * rows, rows)], store_sem.at[slot]
                )
            )
    grads = [
        pltpu.make_async_copy(source, target, grad_sem.at[index])
        for index, (source, target) in enumerate(
            (
                (mlp_hbm, mlp_ref), (down_hbm, down_ref),
                (mgate, mgate_hbm), (mup, mup_hbm), (down, d_down_hbm),
            )
        )
    ]
    for copy in (*grads[:2], *loads):
        copy.start()
    hidden = mgate.shape[1]
    size = query.shape[1]

    def convert(target, source, start):
        tall = 32

        @pl.loop(0, target.shape[0] // tall)
        def _(at):
            lines = pl.ds(pl.multiple_of(at * tall, tall), tall)
            target[lines] = source[lines, pl.ds(start, target.shape[1])].astype(target.dtype)

    grads[0].wait()
    convert(mgate, mlp_ref, 0)
    grads[2].start()
    convert(mup, mlp_ref, hidden)
    grads[3].start()
    for load, store in zip(loads, stores):
        load.wait()
        store.start()
    grads[1].wait()
    convert(down, down_ref, 0)
    grads[4].start()
    convert(query, in_ref, 0)
    convert(gate, in_ref, size)
    key[...] = key_ref[...]
    value[...] = value_ref[...]
    wout[...] = wout_ref[...]
    first[...] = gains_ref[pl.ds(0, 1)]
    second[...] = gains_ref[pl.ds(1, 1)]
    for copy in (*stores, *grads[2:]):
        copy.wait()


def finish(output, d_tokens, d_mlp, d_down, d_in, gains, *rest):
    count, rows, width = output.shape
    tall, hidden = d_mlp.shape[0], d_mlp.shape[1] // 2
    down_rows, wide = d_down.shape
    size = d_in.shape[1] // 3
    vmem = pl.BlockSpec(memory_space=pltpu.VMEM)
    hbm = pl.BlockSpec(memory_space=pl.ANY)

    def shape(*extent, dtype=F32):
        return jax.ShapeDtypeStruct(extent, dtype)

    return pl.pallas_call(
        finish_kernel,
        out_shape=[
            shape(count * rows, width, dtype=BF), shape(count * rows, width, dtype=BF),
            shape(tall, hidden), shape(tall, hidden), shape(down_rows, wide),
            shape(tall, size), shape(tall, size),
            shape(1, wide), shape(1, wide), *[shape(*a.shape) for a in rest],
        ],
        in_specs=[hbm] * 4 + [vmem] * 5,
        out_specs=[hbm] * 5 + [vmem] * 7,
        scratch_shapes=[
            pltpu.VMEM((2 * count, rows, width), BF),
            pltpu.VMEM(d_mlp.shape, BF), pltpu.VMEM(d_down.shape, BF),
            pltpu.VMEM((tall, hidden), F32), pltpu.VMEM((tall, hidden), F32),
            pltpu.VMEM(d_down.shape, F32),
            pltpu.SemaphoreType.DMA((2 * count,)),
            pltpu.SemaphoreType.DMA((2 * count,)),
            pltpu.SemaphoreType.DMA((5,)),
        ],
        compiler_params=pltpu.CompilerParams(vmem_limit_bytes=VMEM_LIMIT),
        name="finish",
    )(output, d_tokens, d_mlp, d_down, d_in, gains, *rest)


def local_call(kernel, scalars, arrays, outs, scratch, flops, name):
    vmem = pl.BlockSpec(memory_space=pltpu.VMEM)
    smem = pl.BlockSpec(memory_space=pltpu.SMEM)
    return pl.pallas_call(
        kernel,
        out_shape=outs,
        in_specs=[smem] * len(scalars) + [vmem] * len(arrays),
        out_specs=[vmem] * len(outs),
        scratch_shapes=scratch,
        compiler_params=pltpu.CompilerParams(vmem_limit_bytes=VMEM_LIMIT),
        cost_estimate=pl.CostEstimate(flops=flops, bytes_accessed=8 << 20, transcendentals=0),
        name=name,
    )(*scalars, *arrays)


def ring_routes(count):
    spots = [ring_head(at, count) for at in range(count)]
    right = [(spots[at], spots[(at + 1) % count]) for at in range(count)]
    left = [(spots[at], spots[at - 1]) for at in range(count)]
    return right, left


def add_low(one, other):
    return (one.astype(F32) + other.astype(F32)).astype(BF)


def flow_steps(part, going, coming):
    count = lax.axis_size("head")
    place = ring_place(lax.axis_index("head"), count)
    right, left = ring_routes(count)
    rows = part.shape[0] // count
    steps = count // 2

    def mine(owner):
        return lax.dynamic_slice_in_dim(part, lax.rem(owner + count, count) * rows, rows, 0)

    for step in range(2, steps - 1):
        going = lax.ppermute(going, "head", right)
        coming = lax.ppermute(coming, "head", left)
        if step < steps - 2:
            going = add_low(going, mine(place + steps - 1 - step))
            coming = add_low(coming, mine(place - steps + 1 + step))
    return going, coming


def matmul(left, right):
    return jnp.dot(left, right, preferred_element_type=F32)


def rows_inner(left, right):
    return lax.dot_general(left, right, (((0,), (0,)), ((), ())), preferred_element_type=F32)


def cols_inner(left, right):
    return lax.dot_general(left, right, (((1,), (1,)), ((), ())), preferred_element_type=F32)


def rms_scale(values):
    return lax.rsqrt(jnp.mean(values * values, axis=1, keepdims=True) + EPSILON)


def per_device(
    tokens,
    segment_ids,
    norm1_gain,
    w_query,
    w_key,
    w_value,
    w_gate,
    w_out,
    norm2_gain,
    w_mlp_gate,
    w_mlp_up,
    w_down,
    out_grad,
):
    heads = lax.axis_size("head")
    batches = lax.axis_size("batch")
    row_count, width = tokens.shape
    head_size = w_query.shape[1]
    half = w_key.shape[1]
    chunk = row_count // heads
    me = ring_place(lax.axis_index("head"), heads)
    scale_factor = 1.0 / math.sqrt(head_size)

    w_shard = jnp.concatenate([w_query, w_gate, w_key, w_value], axis=1)
    gains = jnp.concatenate([norm1_gain, norm2_gain]).reshape(-1, 128).astype(F32)
    normed_one, queries, gate_logit, kv_all, w_in, out_full, gains, seg_all, down_top = entry(
        tokens, w_shard, w_out, gains, segment_ids.reshape(-1, 128), w_down, 1
    )
    gains, w_mlp_gate = lax.optimization_barrier((gains, w_mlp_gate))
    seg_all = seg_all.reshape(-1)
    gains = gains.reshape(batches, 2, -1).transpose(1, 0, 2).reshape(2, width)
    gain_one, gain_two = gains[0], gains[1]
    mgate_full = lax.all_gather(w_mlp_gate, "batch", axis=0, tiled=True)

    base = lax.axis_index("batch") * row_count
    ids = jnp.arange(DOCUMENTS, dtype=jnp.int32)
    below = jnp.sum((seg_all[None, :] < ids[:, None]).astype(jnp.int32), axis=1)
    starts = jnp.sum(jnp.where(segment_ids[None, :] == ids[:, None], below[:, None], 0), axis=0)
    scalars = (starts, base.reshape(1))
    pair_flops = 4 * row_count * kv_all.shape[0] * head_size
    attended, mixed, lse = local_call(
        functools.partial(attend_kernel, scale_factor),
        scalars,
        (queries, kv_all, starts[None], gate_logit),
        [
            jax.ShapeDtypeStruct((row_count, head_size), F32),
            jax.ShapeDtypeStruct((row_count, head_size), BF),
            jax.ShapeDtypeStruct((1, row_count), F32),
        ],
        [],
        pair_flops,
        "attend",
    )
    mixed_all, down_low, mup_full = spread(
        [mixed, w_down, w_mlp_up], (("head", "cols"), ("batch", "low"), ("batch", "rows")), 2
    )
    (
        mlp_part, d_mlp, d_down, resid_own, d_resid, d_resid_low, d_gain_two, d_mixed, going, coming,
    ) = mlp_back(
        tokens, mixed_all, out_grad, gain_two[None], out_full, mgate_full, mup_full, down_top, down_low, 3
    )
    hold = lax.optimization_barrier
    state = flow_steps(mlp_part, going, coming)

    d_queries, d_gate_logit, d_kv_all = local_call(
        functools.partial(attend_back_kernel, scale_factor),
        scalars,
        (queries, kv_all, starts[None], gate_logit, attended, d_mixed, lse),
        [
            jax.ShapeDtypeStruct((row_count, head_size), BF),
            jax.ShapeDtypeStruct((row_count, head_size), BF),
            jax.ShapeDtypeStruct(kv_all.shape, BF),
        ],
        [pltpu.VMEM((kv_all.shape[0], head_size), F32)] * 2,
        5 * pair_flops // 2,
        "attend_back",
    )
    d_down = lax.psum_scatter(d_down, "batch", scatter_dimension=1, tiled=True)
    d_mlp = lax.psum_scatter(d_mlp, "batch", scatter_dimension=0, tiled=True)
    output, d_tokens, d_gains, d_out, d_in, d_key, d_value = tail(
        (
            d_queries, d_gate_logit, d_kv_all, w_in, gain_one[None], d_resid, d_gain_two,
            d_resid_low, resid_own, *state, normed_one, tokens, mixed_all, mlp_part,
        ),
        5,
    )
    (
        output, d_tokens, d_mgate, d_mup, d_down, d_query, d_gate, d_one, d_two,
        d_key, d_value, d_out,
    ) = finish(output, d_tokens, d_mlp, d_down, d_in, d_gains, d_key, d_value, d_out)
    return (
        output,
        d_tokens,
        d_one.reshape(-1),
        d_query,
        d_key.T,
        d_value.T,
        d_gate,
        d_out,
        d_two.reshape(-1),
        d_mgate,
        d_mup,
        d_down,
    )


def solution(mesh):
    return jax.shard_map(
        per_device,
        mesh=mesh,
        in_specs=(
            P("batch", None),
            P("batch"),
            P("batch"),
            P("batch", "head"),
            P("batch", "head"),
            P("batch", "head"),
            P("batch", "head"),
            P("head", "batch"),
            P("batch"),
            P("batch", "head"),
            P("batch", "head"),
            P("head", "batch"),
            P("batch", None),
        ),
        out_specs=(
            P("batch", None),
            P("batch", None),
            P("batch"),
            P("batch", "head"),
            P("batch", "head"),
            P("batch", "head"),
            P("batch", "head"),
            P("head", "batch"),
            P("batch"),
            P("batch", "head"),
            P("batch", "head"),
            P("head", "batch"),
        ),
        check_vma=False,
    )
```
